32 devices in a mesh: dp: 8 (over z, y), tensor: 4 (over x, core).
Axes of the slice: x: 2, y: 2, z: 4, core: 2. Of those that a mesh axis runs over, the one named last changes fastest.
Arguments:
- tokens: bfloat16 [16384, 768], P(('dp', 'tensor')), may hold values from -6 to 6
- thoughts: bfloat16 [512, 768], P(('dp', 'tensor')), may hold values from -6 to 6
- positions: int32 [512], P(('dp', 'tensor')), may hold values from 0 to 511, as said below
- lengths: int32 [8, 4], P('dp'), may hold values from 1 to 1024, 2048 in all within a row
- attn_norm_gain: bfloat16 [768], P(('dp', 'tensor')), may hold values from 0.5 to 1.5
- attn_norm_shift: bfloat16 [768], P(('dp', 'tensor')), may hold values from -1.1953125 to 1.1953125
- qkv_weight: bfloat16 [768, 2304], P('dp', 'tensor'), may hold values from -0.21875 to 0.21875
- qv_bias: bfloat16 [2, 768], P(None, ('dp', 'tensor')), may hold values from -0.1796875 to 0.1796875
- attn_out_weight: bfloat16 [768, 768], P('tensor', 'dp'), may hold values from -3.5 to 3.5
- attn_out_bias: bfloat16 [768], P(('dp', 'tensor')), may hold values from -1.1953125 to 1.1953125
- mlp_norm_gain: bfloat16 [768], P(('dp', 'tensor')), may hold values from 0.5 to 1.5
- mlp_norm_shift: bfloat16 [768], P(('dp', 'tensor')), may hold values from -1.1953125 to 1.1953125
- fc_weight: bfloat16 [768, 3072], P('dp', 'tensor'), may hold values from -0.21875 to 0.21875
- fc_bias: bfloat16 [3072], P(('dp', 'tensor')), may hold values from -1.1953125 to 1.1953125
- proj_weight: bfloat16 [3072, 768], P('tensor', 'dp'), may hold values from -0.21875 to 0.21875
- proj_bias: bfloat16 [768], P(('dp', 'tensor')), may hold values from -1.1953125 to 1.1953125
- cotangent: bfloat16 [16384, 768], P(('dp', 'tensor')), may hold values from -6 to 6
Outputs:
- block_out: bfloat16 [16384, 768], P(('dp', 'tensor'))
- grad_tokens: float32 [16384, 768], P(('dp', 'tensor'))
- grad_thoughts: float32 [512, 768], P(('dp', 'tensor'))
- grad_attn_norm_gain: float32 [768], P(('dp', 'tensor'))
- grad_attn_norm_shift: float32 [768], P(('dp', 'tensor'))
- grad_qkv_weight: float32 [768, 2304], P('dp', 'tensor')
- grad_qv_bias: float32 [2, 768], P(None, ('dp', 'tensor'))
- grad_attn_out_weight: float32 [768, 768], P('tensor', 'dp')
- grad_attn_out_bias: float32 [768], P(('dp', 'tensor'))
- grad_mlp_norm_gain: float32 [768], P(('dp', 'tensor'))
- grad_mlp_norm_shift: float32 [768], P(('dp', 'tensor'))
- grad_fc_weight: float32 [768, 3072], P('dp', 'tensor')
- grad_fc_bias: float32 [3072], P(('dp', 'tensor'))
- grad_proj_weight: float32 [3072, 768], P('tensor', 'dp')
- grad_proj_bias: float32 [768], P(('dp', 'tensor'))
The draws below stay inside these ranges and needn't reach their ends.
Inputs may be any that keep to these rules, and one draw needn't show every extreme that they name: Row i lists the lengths of the 3 sequences packed from the first slot of group i, in order, and last the number of padded slots after them; each row sums to 2048 and its largest entry is 1024. `positions`: entry j lies in the window of 32 slots starting at (j mod 16) * 32, so the entries of one block are distinct.
All inputs are finite; a program needn't handle non-finite values.
Results may differ from the reference program's by a relative error of at most 0.024.
Values may be sent and summed in bfloat16 or wider, within the bound.
A program may use at most 128 MiB of HBM per device.

```python
import math
import jax
import jax.numpy as jnp
import numpy as np
from jax import lax

D = 768
H = 12
HD = 64
FF = 3072
TOK_DEV = 2048
SEQ_DEV = 3
LAT_DEV = 16
MAXLEN = 1024
BQ = 512
ROWS = 512
TOKENS = 16384
THOUGHTS = 512
N_DP = 8
N_TENSOR = 4


def draw_positions(key, part):
    stride_rows = TOK_DEV // N_TENSOR // LAT_DEV
    offsets = jax.random.randint(key, (N_DP * N_TENSOR, LAT_DEV), 0, stride_rows, dtype=jnp.int32)
    window_starts = jnp.arange(LAT_DEV, dtype=jnp.int32) * stride_rows
    placed = offsets + window_starts[None, :]
    placed = placed.at[0, 0].set(0)
    placed = placed.at[0, LAT_DEV - 1].set(TOK_DEV // N_TENSOR - 1)
    return placed.reshape(N_DP * N_TENSOR * LAT_DEV).astype(jnp.int32)


def shard_levels(rng, extent, pieces, least, top_value):
    def one(position, blocks):
        draws = jax.random.uniform(jax.random.fold_in(jax.random.fold_in(rng, 6), position), (blocks,), jnp.float32, least / len(pieces), top_value / len(pieces))
        return jnp.repeat(jnp.exp(draws), extent[position] // blocks).reshape((-1,) + (1,) * (len(extent) - position - 1))

    factor_of = one(*pieces[0])
    for cut in pieces[1:]:
        factor_of = factor_of * one(*cut)
    return factor_of


def profile(count, total, limit, slope):
    portions = [(1 << 20) // math.isqrt(grade ** slope) + 1 for grade in range(2, count + 1)]
    rest, counts = total - limit - (count - 1), [1] * (count - 1)
    while rest > 0:
        candidates = [i for i in range(count - 1) if counts[i] < limit]
        whole, remaining = sum([portions[i] for i in candidates]), rest
        for i in candidates:
            addition = min(limit - counts[i], max(1, remaining * portions[i] // whole), rest)
            counts[i] = counts[i] + addition
            rest = rest - addition
    return np.array([limit] + counts)


def ragged(key, number_of, total, limit, skew):
    if number_of == 2:
        one = jax.random.randint(key, (), max(1, total - limit), min(limit, total - 1) + 1)
        return jnp.stack([one, total - one])
    tallies = jnp.asarray(profile(number_of, total, limit, skew), jnp.int32)
    couples = (number_of - 1) // 2
    source_of, sink = tallies[1:1 + 2 * couples:2], tallies[2:2 + 2 * couples:2]
    margin = jnp.minimum(source_of - 1, limit - sink)
    moved = jax.random.randint(jax.random.fold_in(key, 1), (couples,), 0, 1 << 20) % (margin + 1)
    tallies = tallies.at[1:1 + 2 * couples:2].set(source_of - moved).at[2:2 + 2 * couples:2].set(sink + moved)
    return tallies[jax.random.permutation(jax.random.fold_in(key, 2), number_of)]


def bell_draw(key, extent, scale, limit, shards=(), kind=jnp.bfloat16):
    entries = jax.random.normal(key, extent, jnp.float32) * scale
    if len(shards) > 0:
        entries = shard_levels(key, extent, shards, -0.22, 0.18) * entries
    return jnp.clip(entries, min=-limit, max=limit).astype(kind)


def setup_inputs(seed: int = 0) -> dict:
    arg_keys = jax.random.split(jax.random.key(seed), 18)
    tokens = bell_draw(arg_keys[0], (TOKENS, D), 1.0, 6.0, ((0, 32),))
    thoughts = bell_draw(arg_keys[1], (THOUGHTS, D), 1.0, 6.0, ((0, 32),))
    positions = draw_positions(jax.random.fold_in(arg_keys[17], 71), 0)
    lengths = jax.vmap(lambda own: ragged(own, SEQ_DEV + 1, TOK_DEV, MAXLEN, 2))(jax.random.split(arg_keys[3], N_DP)).reshape((N_DP, SEQ_DEV + 1)).astype(jnp.int32)
    attn_norm_gain = jnp.clip(1.0 + 0.1 * jax.random.normal(arg_keys[4], (D,), jnp.float32), 0.5, 1.5).astype(jnp.bfloat16)
    attn_norm_shift = bell_draw(arg_keys[5], (D,), 0.2, 1.1953125, ((0, 32),))
    qkv_weight = bell_draw(arg_keys[6], (D, 3 * D), D ** -0.5, 0.21875, ((0, 8), (1, 4)))
    qv_bias = bell_draw(arg_keys[7], (2, D), 0.03, 0.1796875, ((1, 32),))
    attn_out_weight = bell_draw(arg_keys[8], (D, D), (max(1, D * 8 // TOK_DEV)) ** -0.5, 3.5, ((0, 4), (1, 8)))
    attn_out_bias = bell_draw(arg_keys[9], (D,), 0.2, 1.1953125, ((0, 32),))
    mlp_norm_gain = jnp.clip(1.0 + 0.1 * jax.random.normal(arg_keys[10], (D,), jnp.float32), 0.5, 1.5).astype(jnp.bfloat16)
    mlp_norm_shift = bell_draw(arg_keys[11], (D,), 0.2, 1.1953125, ((0, 32),))
    fc_weight = bell_draw(arg_keys[12], (D, FF), D ** -0.5, 0.21875, ((0, 8), (1, 4)))
    fc_bias = bell_draw(arg_keys[13], (FF,), 0.2, 1.1953125, ((0, 32),))
    proj_weight = bell_draw(arg_keys[14], (FF, D), (FF // 4) ** -0.5, 0.21875, ((0, 4), (1, 8)))
    proj_bias = bell_draw(arg_keys[15], (D,), 0.2, 1.1953125, ((0, 32),))
    cotangent = bell_draw(arg_keys[16], (TOKENS, D), 1.0, 6.0, ((0, 32),))
    return {"tokens": tokens, "thoughts": thoughts, "positions": positions, "lengths": lengths, "attn_norm_gain": attn_norm_gain, "attn_norm_shift": attn_norm_shift, "qkv_weight": qkv_weight, "qv_bias": qv_bias, "attn_out_weight": attn_out_weight, "attn_out_bias": attn_out_bias, "mlp_norm_gain": mlp_norm_gain, "mlp_norm_shift": mlp_norm_shift, "fc_weight": fc_weight, "fc_bias": fc_bias, "proj_weight": proj_weight, "proj_bias": proj_bias, "cotangent": cotangent}


@jax.custom_vjp
def low(v):
    return lax.optimization_barrier(v.astype(jnp.bfloat16)).astype(jnp.float32)

@jax.custom_vjp
def low_back(v):
    return v

def low_keep(v):
    return (low(v), None)

def low_pass(kept, grad):
    return (grad,)

def back_keep(v):
    return (v, None)

def back_low(kept, grad):
    return (low(grad),)
low.defvjp(low_keep, low_pass)
low_back.defvjp(back_keep, back_low)
HIGHEST_PRECISION = lax.Precision.HIGHEST
EPSILON = 1e-05
MASKED = -1e+30

def layer_norm(values, gain_row, shift_row):
    center = lax.optimization_barrier(jnp.mean(values, axis=-1, keepdims=True))
    offset = values - center
    spread = lax.optimization_barrier(jnp.mean(offset * offset, axis=-1, keepdims=True))
    return offset * lax.rsqrt(spread + EPSILON) * gain_row + shift_row

def matmul(left_side, right_side):
    return jnp.dot(left_side, right_side, precision=HIGHEST_PRECISION, preferred_element_type=jnp.float32)

def group_forward(hidden, lens_row, params):
    attn_norm_gain, attn_norm_shift, qkv_weight, qv_bias, attn_out_weight, attn_out_bias, mlp_norm_gain, mlp_norm_shift, fc_weight, fc_bias, proj_weight, proj_bias = params
    slot_ids = jnp.arange(TOK_DEV, dtype=jnp.int32)
    seq_ends = jnp.cumsum(lens_row).astype(jnp.int32)
    segment = lax.optimization_barrier(jnp.sum((slot_ids[:, None] >= seq_ends[None, :]).astype(jnp.int32), axis=1)).astype(jnp.int32)
    live_rows = (segment < SEQ_DEV).astype(jnp.float32)
    normed_one = low(layer_norm(hidden, attn_norm_gain, attn_norm_shift))
    zero_bias = jnp.zeros((D,), jnp.float32)
    bias_three = jnp.stack([qv_bias[0], zero_bias, qv_bias[1]], axis=0).reshape(3, H, HD).transpose(1, 0, 2)
    mixed_qkv = matmul(normed_one, qkv_weight).reshape(TOK_DEV, H, 3, HD) + bias_three[None]
    mixed_qkv = low(low_back(mixed_qkv))
    queries = mixed_qkv[:, :, 0, :]
    key_rows = mixed_qkv[:, :, 1, :]
    values = mixed_qkv[:, :, 2, :]
    score_scale = HD ** (-0.5)

    def attend(block_index):
        first_row = block_index * BQ
        query_block = lax.dynamic_slice_in_dim(queries, first_row, BQ, 0)
        segment_block = lax.dynamic_slice_in_dim(segment, first_row, BQ, 0)
        slot_block = first_row + jnp.arange(BQ, dtype=jnp.int32)
        scores = jnp.einsum('qhe,khe->hqk', query_block, key_rows, precision=HIGHEST_PRECISION) * score_scale
        allowed = (segment_block[:, None] == segment[None, :]) & (slot_block[:, None] >= slot_ids[None, :])
        scores = low_back(jnp.where(allowed[None], scores, MASKED))
        attn_probs = low(jax.nn.softmax(scores, axis=-1))
        return jnp.einsum('hqk,khe->qhe', attn_probs, values, precision=HIGHEST_PRECISION)
    attended = lax.map(jax.checkpoint(attend), jnp.arange(TOK_DEV // BQ, dtype=jnp.int32))
    attended = low(low_back(attended.reshape(TOK_DEV, D)))
    middle = hidden + low_back(matmul(attended, attn_out_weight)) + attn_out_bias
    normed_two = low(layer_norm(middle, mlp_norm_gain, mlp_norm_shift))
    inner_rows = low_back(matmul(normed_two, fc_weight) + fc_bias)
    activated = low(jax.nn.gelu(inner_rows, approximate=True))
    final_rows = middle + low_back(matmul(activated, proj_weight)) + proj_bias
    return final_rows * live_rows[:, None]

def reference(tokens, thoughts, positions, lengths, attn_norm_gain, attn_norm_shift, qkv_weight, qv_bias, attn_out_weight, attn_out_bias, mlp_norm_gain, mlp_norm_shift, fc_weight, fc_bias, proj_weight, proj_bias, cotangent):
    params = tuple((weight_arg.astype(jnp.float32) for weight_arg in (attn_norm_gain, attn_norm_shift, qkv_weight, qv_bias, attn_out_weight, attn_out_bias, mlp_norm_gain, mlp_norm_shift, fc_weight, fc_bias, proj_weight, proj_bias)))
    slot_index = jnp.arange(THOUGHTS, dtype=jnp.int32) // LAT_DEV * ROWS + positions.astype(jnp.int32)
    group_fn = jax.checkpoint(group_forward)

    def forward(token_values, thought_values, weight_values):
        hidden = token_values.at[slot_index].set(thought_values)
        groups = hidden.reshape(N_DP, TOK_DEV, D)

        def group_step(carried, group_pair):
            return (carried, group_fn(group_pair[0], group_pair[1], weight_values))
        _, finals = lax.scan(group_step, jnp.zeros((), jnp.float32), (groups, lengths))
        return finals.reshape(TOKENS, D)
    final_rows, pullback = jax.vjp(forward, tokens.astype(jnp.float32), thoughts.astype(jnp.float32), params)
    grad_tokens, grad_thoughts, grad_params = pullback(cotangent.astype(jnp.float32))
    return (final_rows.astype(jnp.bfloat16), grad_tokens, grad_thoughts, grad_params[0], grad_params[1], grad_params[2], grad_params[3], grad_params[4], grad_params[5], grad_params[6], grad_params[7], grad_params[8], grad_params[9], grad_params[10], grad_params[11])
```

```python
import jax
import jax.numpy as jnp
from jax import lax
from jax.experimental import pallas as pl
from jax.experimental.pallas import tpu as pltpu
from jax.sharding import PartitionSpec as P

H = 12
HD = 64
FF = 3072
SEQ_DEV = 3
EPSILON = 1e-05
MASKED = -1e30
NH = 3
SLABS = 2
WIDE = SLABS * 128
BQ = 512
BK = 512
VEC_ROWS = 16
MESH = pl.DeviceIdType.MESH
ANY = pl.BlockSpec(memory_space=pl.ANY)
VM = pl.BlockSpec(memory_space=pltpu.VMEM)
LOW = jnp.bfloat16
F32 = jnp.float32


def nn(a, b):
    return lax.dot_general(a, b, (((1,), (0,)), ((), ())), preferred_element_type=jnp.float32)


def head_rows(slab, head):
    half = slab[(head % 2) * HD : (head % 2 + 1) * HD]
    zero = jnp.zeros_like(half)
    return jnp.concatenate([half, zero] if head % 2 == 0 else [zero, half], axis=0)


def attend_kernel(bounds_ref, mixed_ref, start_ref, out_ref, stat_ref, qt_ref, vt_ref):
    tokens = mixed_ref.shape[0]
    for first in range(0, tokens, BQ):
        rows = pl.ds(first, BQ)
        for slab in range(SLABS):
            lanes = slab * 128
            qt_ref[lanes : lanes + 128, rows] = (
                mixed_ref[rows, lanes : lanes + 128] * HD ** (-0.5)
            ).T
            vt_ref[lanes : lanes + 128, rows] = mixed_ref[
                rows, 2 * WIDE + lanes : 2 * WIDE + lanes + 128
            ].T

    def query_block(block, carry):
        first = pl.multiple_of(block * BQ, BQ)
        columns = pl.ds(first, BQ)
        start = start_ref[:, columns]
        query_ids = first + lax.broadcasted_iota(jnp.int32, (BK, BQ), 1)
        queries = [
            head_rows(qt_ref[(h // 2) * 128 : (h // 2 + 1) * 128, columns], h) for h in range(NH)
        ]

        def key_block(key, state):
            base = pl.multiple_of(key * BK, BK)
            rows = pl.ds(base, BK)
            key_ids = base + lax.broadcasted_iota(jnp.int32, (BK, BQ), 0)
            allowed = (key_ids <= query_ids) & (key_ids >= start)
            result = []
            for h in range(NH):
                peak, total, acc = state[h]
                slab = h // 2
                scores = nn(mixed_ref[rows, WIDE + slab * 128 : WIDE + slab * 128 + 128], queries[h])
                scores = jnp.where(allowed, scores, MASKED)
                fresh = jnp.maximum(peak, jnp.max(scores, axis=0, keepdims=True))
                weight = jnp.exp(scores - fresh)
                decay = jnp.exp(peak - fresh)
                total = total * decay + jnp.sum(weight, axis=0, keepdims=True)
                values = vt_ref[h * HD : (h + 1) * HD, rows]
                acc = acc * decay + nn(values, weight.astype(jnp.bfloat16))
                result.append((fresh, total, acc))
            return tuple(result)

        empty = tuple(
            (
                jnp.full((1, BQ), MASKED, jnp.float32),
                jnp.zeros((1, BQ), jnp.float32),
                jnp.zeros((HD, BQ), jnp.float32),
            )
            for _ in range(NH)
        )
        state = lax.fori_loop(bounds_ref[block], (block + 1) * (BQ // BK), key_block, empty)
        for h in range(NH):
            peak, total, acc = state[h]
            out_ref[h * HD : (h + 1) * HD, columns] = (acc / total).astype(jnp.bfloat16)
            stat_ref[h : h + 1, columns] = peak + jnp.log(total)
        return carry

    lax.fori_loop(0, tokens // BQ, query_block, 0)


def attend(bounds, mixed, start):
    tokens = mixed.shape[0]
    vm = pl.BlockSpec(memory_space=pltpu.VMEM)
    return pl.pallas_call(
        attend_kernel,
        out_shape=(
            jax.ShapeDtypeStruct((NH * HD, tokens), jnp.bfloat16),
            jax.ShapeDtypeStruct((8, tokens), jnp.float32),
        ),
        in_specs=[pl.BlockSpec(memory_space=pltpu.SMEM), vm, vm],
        out_specs=(vm, vm),
        scratch_shapes=[pltpu.VMEM((WIDE, tokens), jnp.bfloat16)] * 2,
        compiler_params=pltpu.CompilerParams(vmem_limit_bytes=40 << 20),
        name="attend",
    )(bounds, mixed, start)


def attend_back_kernel(
    bounds_ref, mixed_ref, start_ref, out_ref, stat_ref, gradt_ref,
    gmixed_ref, qt_ref, kt_ref, grad_ref, delta_ref, dqt_ref
):
    tokens = mixed_ref.shape[0]
    for first in range(0, tokens, BQ):
        rows = pl.ds(first, BQ)
        for slab in range(SLABS):
            lanes = slab * 128
            qt_ref[lanes : lanes + 128, rows] = (
                mixed_ref[rows, lanes : lanes + 128] * HD ** (-0.5)
            ).T
            kt_ref[lanes : lanes + 128, rows] = mixed_ref[rows, WIDE + lanes : WIDE + lanes + 128].T
        grad_ref[rows, 0:128] = gradt_ref[0:128, rows].T
        grad_ref[rows, 128:256] = jnp.concatenate(
            [gradt_ref[128:192, rows], jnp.zeros((64, BQ), jnp.bfloat16)], axis=0
        ).T
        for h in range(NH):
            product = gradt_ref[h * HD : (h + 1) * HD, rows].astype(jnp.float32) * out_ref[
                h * HD : (h + 1) * HD, rows
            ].astype(jnp.float32)
            delta_ref[h : h + 1, rows] = jnp.sum(product, axis=0, keepdims=True)
    dqt_ref[...] = jnp.zeros_like(dqt_ref)
    lane = lax.broadcasted_iota(jnp.int32, (BQ, 128), 1)

    def key_block(key, carry):
        base = pl.multiple_of(key * BK, BK)
        rows = pl.ds(base, BK)
        key_ids = base + lax.broadcasted_iota(jnp.int32, (BK, BQ), 0)

        def query_block(block, state):
            first = pl.multiple_of(block * BQ, BQ)
            columns = pl.ds(first, BQ)
            start = start_ref[:, columns]
            query_ids = first + lax.broadcasted_iota(jnp.int32, (BK, BQ), 1)
            allowed = (key_ids <= query_ids) & (key_ids >= start)
            grad_keys = list(state[:SLABS])
            grad_values = list(state[SLABS:])
            for h in range(NH):
                slab = h // 2
                low, high = slab * 128, slab * 128 + 128
                queries = head_rows(qt_ref[low:high, columns], h)
                scores = nn(mixed_ref[rows, WIDE + low : WIDE + high], queries)
                probs = jnp.where(allowed, jnp.exp(scores - stat_ref[h : h + 1, columns]), 0.0)
                keep = (lane // HD) == (h % 2)
                grads = jnp.where(keep, grad_ref[columns, low:high], 0.0)
                grad_values[slab] += nn(probs.astype(jnp.bfloat16), grads)
                if h == NH - 1 and NH % 2 == 1:
                    grad_rows = jnp.concatenate(
                        [gradt_ref[h * HD : (h + 1) * HD, columns], jnp.zeros((HD, BQ), jnp.bfloat16)],
                        axis=0,
                    )
                else:
                    grad_rows = head_rows(gradt_ref[low:high, columns], h)
                grad_probs = nn(mixed_ref[rows, 2 * WIDE + low : 2 * WIDE + high], grad_rows)
                grad_scores = (probs * (grad_probs - delta_ref[h : h + 1, columns])).astype(
                    jnp.bfloat16
                )
                natural = mixed_ref[columns, low:high]
                grad_keys[slab] += nn(grad_scores, jnp.where(keep, natural, 0.0))
                dqt_ref[h * HD : (h + 1) * HD, columns] += nn(
                    kt_ref[h * HD : (h + 1) * HD, rows], grad_scores
                )
            return tuple(grad_keys) + tuple(grad_values)

        empty = (jnp.zeros((BK, 128), jnp.float32),) * (2 * SLABS)
        state = lax.fori_loop(key * BK // BQ, bounds_ref[key], query_block, empty)
        for slab in range(SLABS):
            low = slab * 128
            gmixed_ref[rows, WIDE + low : WIDE + low + 128] = (
                state[slab] * HD ** (-0.5)
            ).astype(jnp.bfloat16)
            gmixed_ref[rows, 2 * WIDE + low : 2 * WIDE + low + 128] = state[SLABS + slab].astype(
                jnp.bfloat16
            )
        return carry

    lax.fori_loop(0, tokens // BK, key_block, 0)
    for first in range(0, tokens, BQ):
        rows = pl.ds(first, BQ)
        for slab in range(SLABS):
            low = slab * 128
            gmixed_ref[rows, low : low + 128] = (
                (dqt_ref[low : low + 128, rows] * HD ** (-0.5)).T.astype(jnp.bfloat16)
            )


def attend_back(bounds, mixed, start, out, stat, gradt):
    tokens = mixed.shape[0]
    vm = pl.BlockSpec(memory_space=pltpu.VMEM)
    return pl.pallas_call(
        attend_back_kernel,
        out_shape=jax.ShapeDtypeStruct((tokens, 3 * WIDE), jnp.bfloat16),
        in_specs=[pl.BlockSpec(memory_space=pltpu.SMEM)] + [vm] * 5,
        out_specs=vm,
        scratch_shapes=[
            pltpu.VMEM((WIDE, tokens), jnp.bfloat16),
            pltpu.VMEM((WIDE, tokens), jnp.bfloat16),
            pltpu.VMEM((tokens, WIDE), jnp.bfloat16),
            pltpu.VMEM((8, tokens), jnp.float32),
            pltpu.VMEM((WIDE, tokens), jnp.float32),
        ],
        compiler_params=pltpu.CompilerParams(vmem_limit_bytes=50 << 20),
        name="attend_back",
    )(bounds, mixed, start, out, stat, gradt)


def segment_tables(lengths_row, tokens):
    ends = jnp.cumsum(lengths_row)
    slots = jnp.arange(tokens, dtype=jnp.int32)
    passed = slots[:, None] >= ends[None, :]
    start = jnp.max(jnp.where(passed, ends[None, :], 0), axis=1)
    stop = jnp.min(jnp.where(passed, tokens, ends[None, :]), axis=1)
    first_key = start[::BQ] // BK
    last_query = (stop[BK - 1 :: BK] - 1) // BQ + 1
    return start.astype(jnp.int32), first_key.astype(jnp.int32), last_query.astype(jnp.int32)


class Copies:
    def __init__(self, send, recv):
        self.send, self.recv, self.made = send, recv, []

    def start(self, source, target, device):
        index = len(self.made)
        copy = pltpu.make_async_remote_copy(
            src_ref=source,
            dst_ref=target,
            send_sem=self.send.at[index],
            recv_sem=self.recv.at[index],
            device_id=device,
            device_id_type=MESH,
        )
        copy.start()
        self.made.append(copy)
        return copy

    def finish(self):
        for copy in self.made:
            copy.wait_send()


def greet(devices):
    barrier = pltpu.get_barrier_semaphore()
    for device in devices:
        pl.semaphore_signal(barrier, inc=1, device_id=device, device_id_type=MESH)
    pl.semaphore_wait(barrier, len(devices))


def place(ring):
    dp = lax.axis_index("dp")
    tensor = lax.axis_index("tensor")
    spot, side = dp // 2, dp % 2
    return {
        "dp": dp,
        "tensor": tensor,
        "spot": spot,
        "side": side,
        "chip": tensor // 2,
        "core": tensor % 2,
        "up": ((spot + 1) % ring * 2 + side, tensor),
        "down": ((spot + ring - 1) % ring * 2 + side, tensor),
        "across": (spot * 2 + 1 - side, tensor),
        "mate": (dp, tensor + 1 - 2 * (tensor % 2)),
        "far": (dp, (tensor + 2) % 4),
        "corner": (dp, 3 - tensor),
    }


def comm_call(kernel, name, outputs, inputs, in_specs, out_specs, copies, cid, scratch=(), local=1):
    return pl.pallas_call(
        kernel,
        out_shape=outputs,
        in_specs=in_specs,
        out_specs=out_specs,
        scratch_shapes=list(scratch)
        + [
            pltpu.SemaphoreType.DMA((copies,)),
            pltpu.SemaphoreType.DMA((copies,)),
            pltpu.SemaphoreType.DMA((local,)),
        ],
        compiler_params=pltpu.CompilerParams(
            collective_id=cid, has_side_effects=True, vmem_limit_bytes=50 << 20
        ),
        name=name,
    )(*inputs)


def gather_inputs(hidden, cotangent, weights, vectors, n_dp):
    ring = n_dp // 2
    rows, width = hidden.shape
    half_rows, half = rows // 2, width // 2
    count = len(weights)

    def kernel(*refs):
        hidden_ref, cot_ref = refs[0], refs[1]
        share = refs[2 : 2 + count]
        vec_ref = refs[2 + count]
        hidden_out, cot_out = refs[3 + count], refs[4 + count]
        full = refs[5 + count : 5 + 2 * count]
        vec_out = refs[5 + 2 * count]
        send, recv, local = refs[6 + 2 * count :]
        at = place(ring)
        dp, tensor, spot, side = at["dp"], at["tensor"], at["spot"], at["side"]
        far_row = (tensor + 2) % 4
        greet([at[k] for k in ("up", "down", "across", "mate", "far", "corner")])
        copies = Copies(send, recv)

        def hop_weights(stream, hop):
            row = side if stream == 0 else 1 - side
            above = (spot + ring - (hop - 1)) % ring * 2 + row
            below = (spot + hop - 1) % ring * 2 + row
            made = []
            for i in range(count):
                fresh = stream == 0 and hop == 1
                up_from = share[i] if fresh else full[i].at[above]
                down_from = share[i] if fresh else full[i].at[below]
                made.append(
                    copies.start(
                        up_from.at[:, 0:half], full[i].at[above, :, 0:half], at["up"]
                    )
                )
                made.append(
                    copies.start(
                        down_from.at[:, half:width], full[i].at[below, :, half:width], at["down"]
                    )
                )
            return made

        def hop_vectors(stream, hop):
            row = side if stream == 0 else 1 - side
            above = (spot + ring - (hop - 1)) % ring * 2 + row
            below = (spot + hop - 1) % ring * 2 + row
            return [
                copies.start(vec_out.at[above, 0:2], vec_out.at[above, 0:2], at["up"]),
                copies.start(vec_out.at[below, 2:4], vec_out.at[below, 2:4], at["down"]),
            ]

        def wait(made):
            for copy in made:
                copy.wait_recv()

        first_half, second_half = pl.ds(0, half_rows), pl.ds(half_rows, half_rows)
        vec_made = [copies.start(vec_ref, vec_out.at[dp, tensor], at[k]) for k in ("mate", "far", "corner")]
        far_made = [
            copies.start(hidden_ref.at[part], hidden_out.at[tensor, part], at["far"])
            for part in (first_half, second_half)
        ]
        own = hop_weights(0, 1)
        across = [
            copies.start(share[i], full[i].at[dp], at["across"]) for i in range(count)
        ]
        mate_made = [
            copies.start(hidden_ref, hidden_out.at[tensor], at["mate"]),
            copies.start(cot_ref, cot_out.at[1], at["mate"]),
        ]
        stays = [
            pltpu.make_async_copy(vec_ref, vec_out.at[dp, tensor], local.at[0]),
            pltpu.make_async_copy(hidden_ref, hidden_out.at[tensor], local.at[1]),
            pltpu.make_async_copy(cot_ref, cot_out.at[0], local.at[2]),
        ] + [
            pltpu.make_async_copy(share[i], full[i].at[dp], local.at[3 + i]) for i in range(count)
        ]
        for copy in stays:
            copy.start()
        wait(vec_made)
        stays[0].wait()
        own_vec = hop_vectors(0, 1)
        across.append(copies.start(vec_out.at[dp], vec_out.at[dp], at["across"]))
        relayed = []

        def relay(part, made):
            made.wait_recv()
            relayed.append(
                copies.start(
                    hidden_out.at[far_row, part], hidden_out.at[far_row, part], at["mate"]
                )
            )

        other = other_vec = None
        for hop in range(1, ring):
            wait(own)
            wait(own_vec)
            if hop < ring - 1:
                own = hop_weights(0, hop + 1)
                own_vec = hop_vectors(0, hop + 1)
            if hop == 1:
                relay(first_half, far_made[0])
                wait(across)
            else:
                wait(other)
                wait(other_vec)
            other = hop_weights(1, hop)
            other_vec = hop_vectors(1, hop)
            if hop == min(2, ring - 1):
                relay(second_half, far_made[1])
        wait(other)
        wait(other_vec)
        wait(mate_made)
        wait(relayed)
        copies.finish()
        for copy in stays[1:]:
            copy.wait()

    outputs = (
        (
            jax.ShapeDtypeStruct((4, rows, width), LOW),
            jax.ShapeDtypeStruct((2, rows, width), LOW),
        )
        + tuple(jax.ShapeDtypeStruct((n_dp,) + w.shape, LOW) for w in weights)
        + (jax.ShapeDtypeStruct((n_dp, 4) + vectors.shape, LOW),)
    )
    copy_count = 3 + 2 + 2 + 2 + count + 1 + 2 * (ring - 1) * (2 * count + 2)
    return comm_call(
        kernel,
        "gather_inputs",
        outputs,
        (hidden, cotangent, *weights, vectors),
        [VM] * (3 + count),
        tuple([ANY] * len(outputs)),
        copy_count,
        0,
        local=3 + count,
    )


def mate_rows(rows_here, n_dp, cid):
    def kernel(in_ref, out_ref, send, recv, local):
        at = place(n_dp // 2)
        greet([at["mate"]])
        copies = Copies(send, recv)
        copy = copies.start(in_ref, out_ref.at[1], at["mate"])
        stay = pltpu.make_async_copy(in_ref, out_ref.at[0], local.at[0])
        stay.start()
        stay.wait()
        copy.wait()

    return comm_call(
        kernel,
        f"mate_rows_{cid}",
        jax.ShapeDtypeStruct((2,) + rows_here.shape, rows_here.dtype),
        (rows_here,),
        [VM],
        ANY,
        1,
        cid,
    )


def mate_sum_part(parts, n_dp, cid):
    def kernel(in_ref, out_ref, send, recv, local):
        at = place(n_dp // 2)
        greet([at["mate"]])
        copies = Copies(send, recv)
        copies.start(in_ref.at[1], out_ref, at["mate"]).wait()

    return comm_call(
        kernel,
        f"mate_sum_part_{cid}",
        jax.ShapeDtypeStruct(parts.shape[1:], parts.dtype),
        (parts,),
        [ANY],
        ANY,
        1,
        cid,
    )


def heads_to_rows(attended, n_dp, cid):
    head_rows_here, slots = attended.shape
    block = slots // 4

    def kernel(in_ref, out_ref, send, recv, local):
        at = place(n_dp // 2)
        greet([at["far"]])
        copies = Copies(send, recv)
        made, stays = [], []
        for i in range(2):
            core = at["core"] if i == 0 else 1 - at["core"]
            theirs = ((1 - at["chip"]) * 2 + core) * block
            ours = (at["chip"] * 2 + core) * block
            made.append(
                copies.start(
                    in_ref.at[:, pl.ds(pl.multiple_of(theirs, block), block)],
                    out_ref.at[1, :, i * block : (i + 1) * block],
                    at["far"],
                )
            )
            stays.append(
                pltpu.make_async_copy(
                    in_ref.at[:, pl.ds(pl.multiple_of(ours, block), block)],
                    out_ref.at[0, :, i * block : (i + 1) * block],
                    local.at[i],
                )
            )
            stays[-1].start()
        for copy in stays + made:
            copy.wait()

    return comm_call(
        kernel,
        "heads_to_rows",
        jax.ShapeDtypeStruct((2, head_rows_here, slots // 2), attended.dtype),
        (attended,),
        [VM],
        ANY,
        2,
        cid,
        local=2,
    )


def rows_to_heads(grads, n_dp, cid):
    _, head_rows_here, slots = grads.shape
    block = slots // 2

    def kernel(in_ref, out_ref, send, recv, local):
        at = place(n_dp // 2)
        greet([at["far"]])
        copies = Copies(send, recv)
        made, stays = [], []
        for i in range(2):
            core = at["core"] if i == 0 else 1 - at["core"]
            ours = pl.ds(pl.multiple_of((at["chip"] * 2 + core) * block, block), block)
            made.append(
                copies.start(
                    in_ref.at[1, :, i * block : (i + 1) * block], out_ref.at[:, ours], at["far"]
                )
            )
            stays.append(
                pltpu.make_async_copy(
                    in_ref.at[0, :, i * block : (i + 1) * block], out_ref.at[:, ours], local.at[i]
                )
            )
            stays[-1].start()
        for copy in stays + made:
            copy.wait()

    return comm_call(
        kernel,
        "rows_to_heads",
        jax.ShapeDtypeStruct((head_rows_here, 2 * slots), grads.dtype),
        (grads,),
        [VM],
        ANY,
        2,
        cid,
        local=2,
    )


def reduce_grads(weight_grads, row_parts, vector_parts, n_dp, cid):
    ring = n_dp // 2
    count = len(weight_grads)
    shard, width = weight_grads[0].shape[1:]
    half = width // 2
    rows = row_parts.shape[1]
    half_rows = rows // 2
    hops = ring - 1
    grads = [g.reshape(ring, 2, shard, width) for g in weight_grads]
    vectors = vector_parts.reshape(4, ring, 2, VEC_ROWS, 128)

    def kernel(*refs):
        grad = refs[:count]
        part, vec = refs[count], refs[count + 1]
        out = refs[count + 2 : 2 * count + 2]
        part_out, vec_out = refs[2 * count + 2], refs[2 * count + 3]
        (
            land, sums, side_send, side_land, own_sum,
            mate_land, far_send, far_land,
            vec_land, vec_sum, vec_ring_land, vec_ring_send, vec_side_land, vec_side_send,
            send, recv, local,
        ) = refs[2 * count + 4 :]
        at = place(ring)
        tensor, spot, side = at["tensor"], at["spot"], at["side"]
        mate_row, far_row, corner_row = at["mate"][1], at["far"][1], at["corner"][1]
        greet([at[k] for k in ("up", "down", "across", "mate", "far", "corner")])
        copies = Copies(send, recv)
        lanes = (pl.ds(0, half), pl.ds(half, half))
        tile_rows = (pl.ds(0, 8), pl.ds(8, 8))
        way = ("up", "down")

        def target(direction, hop):
            if direction == 0:
                return (spot + 2 * ring - 1 - hop) % ring
            return (spot + 1 + hop) % ring

        mate_far = copies.start(part.at[corner_row], mate_land.at[1], at["mate"])
        vec_made = [
            copies.start(vec.at[row], vec_land.at[i], at[k])
            for i, (k, row) in enumerate(
                (("mate", mate_row), ("far", far_row), ("corner", corner_row))
            )
        ]
        moving = {}
        for i in range(count):
            for direction in range(2):
                moving[i, direction] = copies.start(
                    grad[i].at[target(direction, 0), :, :, lanes[direction]],
                    land.at[i, direction, 0],
                    at[way[direction]],
                )
        mate_own = copies.start(part.at[mate_row], mate_land.at[0], at["mate"])
        mate_far.wait_recv()
        far_made = []
        for i in range(2):
            span = pl.ds(i * half_rows, half_rows)
            far_send[span] = (
                mate_land[1, span].astype(F32) + part[far_row, span].astype(F32)
            ).astype(LOW)
            far_made.append(copies.start(far_send.at[span], far_land.at[span], at["far"]))
        for copy in vec_made:
            copy.wait_recv()
        vec_sum[...] = vec[tensor] + vec_land[0] + vec_land[1] + vec_land[2]
        vec_moving = [
            copies.start(
                vec_sum.at[target(direction, 0), :, tile_rows[direction]],
                vec_ring_land.at[direction, 0],
                at[way[direction]],
            )
            for direction in range(2)
        ]
        side_moving = []
        for hop in range(1, ring):
            for i in range(count):
                for direction in range(2):
                    moving[i, direction].wait_recv()
                    position = target(direction, hop)
                    total = land[i, direction, hop - 1].astype(F32) + grad[i][
                        position, :, :, lanes[direction]
                    ].astype(F32)
                    if hop < hops:
                        sums[i, direction, hop - 1] = total.astype(LOW)
                        moving[i, direction] = copies.start(
                            sums.at[i, direction, hop - 1],
                            land.at[i, direction, hop],
                            at[way[direction]],
                        )
                    else:
                        own_sum[i, :, :, lanes[direction]] = total
                        side_send[i, :, :, lanes[direction]] = total.astype(LOW)
                if hop == hops:
                    side_moving.append(
                        copies.start(
                            side_send.at[i, 1 - side], side_land.at[i], at["across"]
                        )
                    )
            for direction in range(2):
                vec_moving[direction].wait_recv()
                position = target(direction, hop)
                total = (
                    vec_ring_land[direction, hop - 1] + vec_sum[position, :, tile_rows[direction]]
                )
                if hop < hops:
                    vec_ring_send[direction, hop - 1] = total
                    vec_moving[direction] = copies.start(
                        vec_ring_send.at[direction, hop - 1],
                        vec_ring_land.at[direction, hop],
                        at[way[direction]],
                    )
                else:
                    vec_side_send[:, tile_rows[direction]] = total
        vec_side = copies.start(vec_side_send.at[1 - side], vec_side_land, at["across"])
        mate_own.wait_recv()
        for i in range(2):
            span = pl.ds(i * half_rows, half_rows)
            far_made[i].wait_recv()
            part_out[span] = (
                part[tensor, span].astype(F32)
                + mate_land[0, span].astype(F32)
                + far_land[span].astype(F32)
            )
        for i in range(count):
            side_moving[i].wait_recv()
            out[i][...] = own_sum[i, side] + side_land[i].astype(F32)
        vec_side.wait_recv()
        vec_out[...] = vec_side_send[side] + vec_side_land[...]
        copies.finish()

    outputs = (
        (jax.ShapeDtypeStruct((shard, width), F32),) * count
        + (
            jax.ShapeDtypeStruct((rows, width), F32),
            jax.ShapeDtypeStruct((VEC_ROWS, 128), F32),
        )
    )
    later = max(hops - 1, 1)
    scratch = [
        pltpu.VMEM((count, 2, hops, 2, shard, half), LOW),
        pltpu.VMEM((count, 2, later, 2, shard, half), LOW),
        pltpu.VMEM((count, 2, shard, width), LOW),
        pltpu.VMEM((count, shard, width), LOW),
        pltpu.VMEM((count, 2, shard, width), F32),
        pltpu.VMEM((2, rows, width), LOW),
        pltpu.VMEM((rows, width), LOW),
        pltpu.VMEM((rows, width), LOW),
        pltpu.VMEM((3, ring, 2, VEC_ROWS, 128), F32),
        pltpu.VMEM((ring, 2, VEC_ROWS, 128), F32),
        pltpu.VMEM((2, hops, 2, 8, 128), F32),
        pltpu.VMEM((2, later, 2, 8, 128), F32),
        pltpu.VMEM((VEC_ROWS, 128), F32),
        pltpu.VMEM((2, VEC_ROWS, 128), F32),
    ]
    copy_count = 2 + 3 + 2 + 2 * hops * (count + 1) + count + 1
    return comm_call(
        kernel,
        "reduce_grads",
        outputs,
        (*grads, row_parts, vectors),
        [VM] * (count + 2),
        (VM,) * len(outputs),
        copy_count,
        cid,
        scratch=scratch,
    )


def normalize(values):
    center = jnp.mean(values, axis=-1, keepdims=True)
    offset = values - center
    spread = jnp.mean(offset * offset, axis=-1, keepdims=True)
    inverse = lax.rsqrt(spread + EPSILON)
    return offset * inverse, inverse


def norm_back(normed, inverse, grad, gain):
    scaled = grad * gain
    center = jnp.mean(scaled, axis=-1, keepdims=True)
    along = jnp.mean(scaled * normed, axis=-1, keepdims=True)
    return inverse * (scaled - center - normed * along)


def gelu_tanh(values):
    return jax.nn.gelu(values, approximate=True)


def product(equation, left, right):
    return jnp.einsum(equation, left, right, preferred_element_type=F32)


def pack_three(qkv, out_turned):
    depth = qkv.shape[0]
    parts = jnp.transpose(qkv.reshape(depth, NH, 3, HD), (0, 2, 1, 3))
    extra = out_turned.reshape(depth, 3, 1, HD)
    return jnp.concatenate([parts, extra], axis=2).reshape(depth, 3 * WIDE)


def unpack_three(packed):
    depth = packed.shape[0]
    split = packed.reshape(depth, 3, NH + 1, HD)
    qkv = jnp.transpose(split[:, :, :NH], (0, 2, 1, 3)).reshape(depth, 3 * NH * HD)
    return qkv, split[:, :, NH].reshape(depth, NH * HD)


def per_device(
    tokens,
    thoughts,
    positions,
    lengths,
    attn_norm_gain,
    attn_norm_shift,
    qkv_weight,
    qv_bias,
    attn_out_weight,
    attn_out_bias,
    mlp_norm_gain,
    mlp_norm_shift,
    fc_weight,
    fc_bias,
    proj_weight,
    proj_bias,
    cotangent,
):
    n_dp = lax.axis_size("dp")
    n_tensor = lax.axis_size("tensor")
    tensor = lax.axis_index("tensor")
    rows, width = tokens.shape
    slots = rows * n_tensor
    head_width = NH * HD
    units = FF // n_tensor
    far = (tensor + 2) % n_tensor
    swap_far = [(i, (i + 2) % n_tensor) for i in range(n_tensor)]

    window = rows // thoughts.shape[0]
    starts = jnp.arange(thoughts.shape[0], dtype=jnp.int32) * window
    placed = (
        jnp.arange(window, dtype=jnp.int32)[None, :] == (positions - starts)[:, None]
    )[:, :, None]
    tokens_low = jnp.where(
        placed, thoughts[:, None, :], tokens.reshape(-1, window, width)
    ).reshape(rows, width)

    start, first_key, last_query = segment_tables(lengths[0], slots)
    live_slots = jnp.sum(lengths[0][:SEQ_DEV])
    own_slots = tensor * rows + jnp.arange(rows, dtype=jnp.int32)
    live = (own_slots < live_slots)[:, None]
    grad_final_low = jnp.where(live, cotangent, jnp.zeros_like(cotangent))

    share = width // (n_dp * n_tensor)
    small = [
        attn_norm_gain, attn_norm_shift, qv_bias[0], qv_bias[1], attn_out_bias,
        mlp_norm_gain, mlp_norm_shift, proj_bias, fc_bias,
    ]
    vectors = jnp.stack([jnp.pad(v, (0, 128 - v.shape[0])) for v in small])
    vectors = jnp.pad(vectors, ((0, VEC_ROWS - len(small)), (0, 0)))

    shares = (fc_weight, proj_weight.T, pack_three(qkv_weight, attn_out_weight.T))
    gathered = gather_inputs(tokens_low, grad_final_low, shares, vectors, n_dp)
    group_rows, grad_rows, fc_all, proj_all, mix_all, vec_all = gathered
    fc_own, proj_own, mix_own = [w.reshape(width, -1) for w in (fc_all, proj_all, mix_all)]
    out_own = mix_own.reshape(width, 3, NH + 1, HD)[:, :, NH].reshape(width, head_width)
    out_far = lax.ppermute(out_own, "tensor", swap_far)
    fc_far = lax.ppermute(fc_own, "tensor", swap_far)
    proj_far = lax.ppermute(proj_own, "tensor", swap_far)

    def whole(row, size):
        return vec_all[:, :, row, :size].reshape(-1).astype(F32)

    gain_one, shift_one, query_bias, value_bias, out_bias, gain_two, shift_two, last_bias = [
        whole(i, share) for i in range(8)
    ]
    hidden_bias = whole(8, fc_bias.shape[0])

    def own_part(vector, index, size):
        return lax.dynamic_slice_in_dim(vector, index * size, size, 0)

    pad = jnp.zeros((WIDE - head_width,), F32)
    bias_three = jnp.concatenate(
        [
            own_part(query_bias, tensor, head_width), pad,
            jnp.zeros((WIDE,), F32),
            own_part(value_bias, tensor, head_width), pad,
        ]
    )
    group_hidden = group_rows.reshape(slots, width).astype(F32)
    group_normed, _ = normalize(group_hidden)
    normed_one = (group_normed * gain_one + shift_one).astype(LOW)
    mixed = (product("td,dc->tc", normed_one, mix_own) + bias_three).astype(LOW)
    start_row = start[None, :]
    attended, stats = attend(first_key, mixed, start_row)
    both = heads_to_rows(attended, n_dp, 1)
    mid_part = product("et,de->td", both[0], out_own) + product("et,de->td", both[1], out_far)
    mid_low = mid_part.astype(LOW).reshape(2, rows, width)
    mid_mate = mate_sum_part(mid_low, n_dp, 2)
    hidden = tokens_low.astype(F32)
    middle = hidden + mid_low[0].astype(F32) + mid_mate.astype(F32) + out_bias
    normed_mid, inverse_mid = normalize(middle)
    normed_two = (normed_mid * gain_two + shift_two).astype(LOW)
    chip_two = mate_rows(normed_two, n_dp, 3).reshape(2 * rows, width)
    chip_grad = grad_rows.reshape(2 * rows, width)

    last_part, grad_two_part, unit_grads = 0.0, 0.0, []
    for fc, proj, index in ((fc_own, proj_own, tensor), (fc_far, proj_far, far)):
        inner = product("td,df->tf", chip_two, fc) + own_part(hidden_bias, index, units)
        activated, gelu_back = jax.vjp(gelu_tanh, inner)
        activated = activated.astype(LOW)
        last_part += product("tf,df->td", activated, proj)
        grad_activated = product("td,df->tf", chip_grad, proj)
        grad_inner = gelu_back(grad_activated)[0].astype(LOW)
        grad_two_part += product("tf,df->td", grad_inner, fc)
        unit_grads.append(
            (
                product("td,tf->df", chip_two, grad_inner),
                product("td,tf->df", chip_grad, activated),
                jnp.sum(grad_inner, axis=0, dtype=F32),
            )
        )
    (grad_fc, grad_proj, grad_fc_bias), (far_fc, far_proj, far_fc_bias) = unit_grads
    far_fc = lax.ppermute(far_fc.astype(LOW), "tensor", swap_far)
    far_proj = lax.ppermute(far_proj.astype(LOW), "tensor", swap_far)
    two_low = grad_two_part.astype(LOW).reshape(2, rows, width)
    two_mate = mate_sum_part(two_low, n_dp, 4)
    grad_two = two_low[0].astype(F32) + two_mate.astype(F32)
    grad_final = grad_final_low.astype(F32)
    grad_middle = grad_final + norm_back(normed_mid, inverse_mid, grad_two, gain_two)
    grad_gain_two = jnp.sum(normed_mid * grad_two, axis=0)
    grad_shift_two = jnp.sum(grad_two, axis=0)
    chip_mid = mate_rows(grad_middle.astype(LOW), n_dp, 5).reshape(2 * rows, width)
    grad_attended = jnp.stack(
        [product("de,td->et", w, chip_mid).astype(LOW) for w in (out_own, out_far)]
    )
    grad_out, far_out = [product("td,et->de", chip_mid, both[i]) for i in range(2)]
    grad_heads = rows_to_heads(grad_attended, n_dp, 6)
    last_low = last_part.astype(LOW).reshape(2, rows, width)
    last_mate = mate_sum_part(last_low, n_dp, 7)
    final = middle + last_low[0].astype(F32) + last_mate.astype(F32) + last_bias
    block_out = jnp.where(live, final, 0.0).astype(LOW)
    far_out = lax.ppermute(far_out.astype(LOW), "tensor", swap_far)

    grad_mixed = attend_back(last_query, mixed, start_row, attended, stats, grad_heads)
    one_part = product("tc,dc->td", grad_mixed, mix_own)
    grad_mix = product("td,tc->dc", normed_one, grad_mixed)
    grad_gain_one = jnp.sum(group_normed * one_part, axis=0)
    grad_shift_one = jnp.sum(one_part, axis=0)
    mix_sums = jnp.sum(grad_mixed, axis=0, dtype=F32)
    out_total = (grad_out + far_out.astype(F32)).reshape(width, 3, 1, HD)
    mix_total = grad_mix + jnp.pad(out_total, ((0, 0), (0, 0), (NH, 0), (0, 0))).reshape(
        width, 3 * WIDE
    )
    totals = [
        (grad_fc + far_fc.astype(F32)).astype(LOW),
        (grad_proj + far_proj.astype(F32)).astype(LOW),
        mix_total.astype(LOW),
    ]

    def spread(vector, index, size, length):
        return lax.dynamic_update_slice_in_dim(jnp.zeros((length,), F32), vector, index * size, 0)

    def tiles(vector):
        cut = vector.reshape(n_dp, n_tensor, -1)
        return jnp.pad(cut, ((0, 0), (0, 0), (0, 128 - cut.shape[2])))

    fc_bias_part = lax.dynamic_update_slice_in_dim(
        spread(grad_fc_bias, tensor, units, FF), far_fc_bias, far * units, 0
    )
    vector_rows = [
        grad_gain_one, grad_shift_one,
        spread(mix_sums[:head_width], tensor, head_width, width),
        spread(mix_sums[2 * WIDE : 2 * WIDE + head_width], tensor, head_width, width),
        jnp.sum(grad_middle, axis=0), grad_gain_two, grad_shift_two,
        jnp.sum(grad_final, axis=0), fc_bias_part,
    ]
    vector_parts = jnp.stack([tiles(v) for v in vector_rows], axis=2)
    vector_parts = jnp.pad(
        vector_parts, ((0, 0), (0, 0), (0, VEC_ROWS - len(vector_rows)), (0, 0))
    )
    vector_parts = jnp.transpose(vector_parts, (1, 0, 2, 3))
    reduced = reduce_grads(
        [g.reshape(n_dp, -1, width) for g in totals],
        one_part.astype(LOW).reshape(n_tensor, rows, width),
        vector_parts,
        n_dp,
        8,
    )
    fc_grad, proj_grad, mix_grad, grad_one, vec = reduced
    qkv_grad, out_grad = unpack_three(mix_grad)
    normed_hid, inverse_hid = normalize(hidden)
    grad_hidden = grad_middle + norm_back(normed_hid, inverse_hid, grad_one, gain_one)
    windows = grad_hidden.reshape(-1, window, width)
    grad_thoughts = jnp.sum(jnp.where(placed, windows, 0.0), axis=1)
    grad_tokens = jnp.where(placed, 0.0, windows).reshape(rows, width)
    return (
        block_out,
        grad_tokens,
        grad_thoughts,
        vec[0, :share],
        vec[1, :share],
        qkv_grad,
        vec[2:4, :share],
        out_grad.T,
        vec[4, :share],
        vec[5, :share],
        vec[6, :share],
        fc_grad,
        vec[8, : fc_bias.shape[0]],
        proj_grad.T,
        vec[7, :share],
    )


def solution(mesh):
    rows = P(("dp", "tensor"), None)
    line = P(("dp", "tensor"))
    in_specs = (
        rows, rows, line, P("dp", None), line, line, P("dp", "tensor"),
        P(None, ("dp", "tensor")), P("tensor", "dp"), line, line, line,
        P("dp", "tensor"), line, P("tensor", "dp"), line, rows,
    )
    out_specs = (
        rows, rows, rows, line, line, P("dp", "tensor"), P(None, ("dp", "tensor")),
        P("tensor", "dp"), line, line, line, P("dp", "tensor"), line, P("tensor", "dp"), line,
    )
    return jax.shard_map(
        per_device, mesh=mesh, in_specs=in_specs, out_specs=out_specs, check_vma=False
    )
```

```python
import functools
import math

import jax
import jax.numpy as jnp
from jax import lax
from jax.experimental import pallas as pl
from jax.experimental.pallas import tpu as pltpu
from jax.sharding import PartitionSpec as P

H = 12
HD = 64
FF = 3072
SEQ_DEV = 3
EPSILON = 1e-05
MASKED = -1e30
NH = 3
SLABS = 2
WIDE = SLABS * 128
BQ = 512
BK = 512
VEC_ROWS = 16
ROW_TILE = 256
GELU_SCALE = math.sqrt(2.0 / math.pi)
GELU_CUBE = 0.044715
MESH = pl.DeviceIdType.MESH
ANY = pl.BlockSpec(memory_space=pl.ANY)
VM = pl.BlockSpec(memory_space=pltpu.VMEM)
LOW = jnp.bfloat16
F32 = jnp.float32


def nn(a, b):
    return lax.dot_general(a, b, (((1,), (0,)), ((), ())), preferred_element_type=jnp.float32)


def nt(a, b):
    return lax.dot_general(a, b, (((1,), (1,)), ((), ())), preferred_element_type=jnp.float32)


def tn(a, b):
    return lax.dot_general(a, b, (((0,), (0,)), ((), ())), preferred_element_type=jnp.float32)


def head_rows(slab, head):
    half = slab[(head % 2) * HD : (head % 2 + 1) * HD]
    zero = jnp.zeros_like(half)
    return jnp.concatenate([half, zero] if head % 2 == 0 else [zero, half], axis=0)


def attend_kernel(bounds_ref, mixed_ref, start_ref, out_ref, stat_ref, qt_ref, vt_ref):
    tokens = mixed_ref.shape[0]
    for first in range(0, tokens, BQ):
        rows = pl.ds(first, BQ)
        for slab in range(SLABS):
            lanes = slab * 128
            qt_ref[lanes : lanes + 128, rows] = (
                mixed_ref[rows, lanes : lanes + 128] * HD ** (-0.5)
            ).T
            vt_ref[lanes : lanes + 128, rows] = mixed_ref[
                rows, 2 * WIDE + lanes : 2 * WIDE + lanes + 128
            ].T

    def query_block(block, carry):
        first = pl.multiple_of(block * BQ, BQ)
        columns = pl.ds(first, BQ)
        start = start_ref[:, columns]
        query_ids = first + lax.broadcasted_iota(jnp.int32, (BK, BQ), 1)
        queries = [
            head_rows(qt_ref[(h // 2) * 128 : (h // 2 + 1) * 128, columns], h) for h in range(NH)
        ]

        def key_block(key, state):
            base = pl.multiple_of(key * BK, BK)
            rows = pl.ds(base, BK)
            key_ids = base + lax.broadcasted_iota(jnp.int32, (BK, BQ), 0)
            allowed = (key_ids <= query_ids) & (key_ids >= start)
            result = []
            for h in range(NH):
                peak, total, acc = state[h]
                slab = h // 2
                scores = nn(mixed_ref[rows, WIDE + slab * 128 : WIDE + slab * 128 + 128], queries[h])
                scores = jnp.where(allowed, scores, MASKED)
                fresh = jnp.maximum(peak, jnp.max(scores, axis=0, keepdims=True))
                weight = jnp.exp(scores - fresh)
                decay = jnp.exp(peak - fresh)
                total = total * decay + jnp.sum(weight, axis=0, keepdims=True)
                values = vt_ref[h * HD : (h + 1) * HD, rows]
                acc = acc * decay + nn(values, weight.astype(jnp.bfloat16))
                result.append((fresh, total, acc))
            return tuple(result)

        empty = tuple(
            (
                jnp.full((1, BQ), MASKED, jnp.float32),
                jnp.zeros((1, BQ), jnp.float32),
                jnp.zeros((HD, BQ), jnp.float32),
            )
            for _ in range(NH)
        )
        state = lax.fori_loop(bounds_ref[block], (block + 1) * (BQ // BK), key_block, empty)
        for h in range(NH):
            peak, total, acc = state[h]
            out_ref[h * HD : (h + 1) * HD, columns] = (acc / total).astype(jnp.bfloat16)
            stat_ref[h : h + 1, columns] = peak + jnp.log(total)
        return carry

    lax.fori_loop(0, tokens // BQ, query_block, 0)


def attend(bounds, mixed, start):
    tokens = mixed.shape[0]
    vm = pl.BlockSpec(memory_space=pltpu.VMEM)
    return pl.pallas_call(
        attend_kernel,
        out_shape=(
            jax.ShapeDtypeStruct((NH * HD, tokens), jnp.bfloat16),
            jax.ShapeDtypeStruct((8, tokens), jnp.float32),
        ),
        in_specs=[pl.BlockSpec(memory_space=pltpu.SMEM), vm, vm],
        out_specs=(vm, vm),
        scratch_shapes=[pltpu.VMEM((WIDE, tokens), jnp.bfloat16)] * 2,
        compiler_params=pltpu.CompilerParams(vmem_limit_bytes=40 << 20),
        cost_estimate=pl.CostEstimate(
            flops=8 * tokens * tokens * NH * HD,
            bytes_accessed=16 * tokens * WIDE,
            transcendentals=tokens * tokens,
        ),
        name="attend",
    )(bounds, mixed, start)


def attend_back_kernel(
    bounds_ref, mixed_ref, start_ref, out_ref, stat_ref, gradt_ref,
    gmixed_ref, qt_ref, kt_ref, grad_ref, delta_ref, dqt_ref
):
    tokens = mixed_ref.shape[0]
    for first in range(0, tokens, BQ):
        rows = pl.ds(first, BQ)
        for slab in range(SLABS):
            lanes = slab * 128
            qt_ref[lanes : lanes + 128, rows] = (
                mixed_ref[rows, lanes : lanes + 128] * HD ** (-0.5)
            ).T
            kt_ref[lanes : lanes + 128, rows] = mixed_ref[rows, WIDE + lanes : WIDE + lanes + 128].T
        grad_ref[rows, 0:128] = gradt_ref[0:128, rows].T
        grad_ref[rows, 128:256] = jnp.concatenate(
            [gradt_ref[128:192, rows], jnp.zeros((64, BQ), jnp.bfloat16)], axis=0
        ).T
        for h in range(NH):
            product = gradt_ref[h * HD : (h + 1) * HD, rows].astype(jnp.float32) * out_ref[
                h * HD : (h + 1) * HD, rows
            ].astype(jnp.float32)
            delta_ref[h : h + 1, rows] = jnp.sum(product, axis=0, keepdims=True)
    dqt_ref[...] = jnp.zeros_like(dqt_ref)
    lane = lax.broadcasted_iota(jnp.int32, (BQ, 128), 1)

    def key_block(key, carry):
        base = pl.multiple_of(key * BK, BK)
        rows = pl.ds(base, BK)
        key_ids = base + lax.broadcasted_iota(jnp.int32, (BK, BQ), 0)

        def query_block(block, state):
            first = pl.multiple_of(block * BQ, BQ)
            columns = pl.ds(first, BQ)
            start = start_ref[:, columns]
            query_ids = first + lax.broadcasted_iota(jnp.int32, (BK, BQ), 1)
            allowed = (key_ids <= query_ids) & (key_ids >= start)
            grad_keys = list(state[:SLABS])
            grad_values = list(state[SLABS:])
            for h in range(NH):
                slab = h // 2
                low, high = slab * 128, slab * 128 + 128
                queries = head_rows(qt_ref[low:high, columns], h)
                scores = nn(mixed_ref[rows, WIDE + low : WIDE + high], queries)
                probs = jnp.where(allowed, jnp.exp(scores - stat_ref[h : h + 1, columns]), 0.0)
                keep = (lane // HD) == (h % 2)
                grads = jnp.where(keep, grad_ref[columns, low:high], 0.0)
                grad_values[slab] += nn(probs.astype(jnp.bfloat16), grads)
                if h == NH - 1 and NH % 2 == 1:
                    grad_rows = jnp.concatenate(
                        [gradt_ref[h * HD : (h + 1) * HD, columns], jnp.zeros((HD, BQ), jnp.bfloat16)],
                        axis=0,
                    )
                else:
                    grad_rows = head_rows(gradt_ref[low:high, columns], h)
                grad_probs = nn(mixed_ref[rows, 2 * WIDE + low : 2 * WIDE + high], grad_rows)
                grad_scores = (probs * (grad_probs - delta_ref[h : h + 1, columns])).astype(
                    jnp.bfloat16
                )
                natural = mixed_ref[columns, low:high]
                grad_keys[slab] += nn(grad_scores, jnp.where(keep, natural, 0.0))
                dqt_ref[h * HD : (h + 1) * HD, columns] += nn(
                    kt_ref[h * HD : (h + 1) * HD, rows], grad_scores
                )
            return tuple(grad_keys) + tuple(grad_values)

        empty = (jnp.zeros((BK, 128), jnp.float32),) * (2 * SLABS)
        state = lax.fori_loop(key * BK // BQ, bounds_ref[key], query_block, empty)
        for slab in range(SLABS):
            low = slab * 128
            gmixed_ref[rows, WIDE + low : WIDE + low + 128] = (
                state[slab] * HD ** (-0.5)
            ).astype(jnp.bfloat16)
            gmixed_ref[rows, 2 * WIDE + low : 2 * WIDE + low + 128] = state[SLABS + slab].astype(
                jnp.bfloat16
            )
        return carry

    lax.fori_loop(0, tokens // BK, key_block, 0)
    for first in range(0, tokens, BQ):
        rows = pl.ds(first, BQ)
        for slab in range(SLABS):
            low = slab * 128
            gmixed_ref[rows, low : low + 128] = (
                (dqt_ref[low : low + 128, rows] * HD ** (-0.5)).T.astype(jnp.bfloat16)
            )


def attend_back(bounds, mixed, start, out, stat, gradt):
    tokens = mixed.shape[0]
    vm = pl.BlockSpec(memory_space=pltpu.VMEM)
    return pl.pallas_call(
        attend_back_kernel,
        out_shape=jax.ShapeDtypeStruct((tokens, 3 * WIDE), jnp.bfloat16),
        in_specs=[pl.BlockSpec(memory_space=pltpu.SMEM)] + [vm] * 5,
        out_specs=vm,
        scratch_shapes=[
            pltpu.VMEM((WIDE, tokens), jnp.bfloat16),
            pltpu.VMEM((WIDE, tokens), jnp.bfloat16),
            pltpu.VMEM((tokens, WIDE), jnp.bfloat16),
            pltpu.VMEM((8, tokens), jnp.float32),
            pltpu.VMEM((WIDE, tokens), jnp.float32),
        ],
        compiler_params=pltpu.CompilerParams(vmem_limit_bytes=50 << 20),
        cost_estimate=pl.CostEstimate(
            flops=20 * tokens * tokens * NH * HD,
            bytes_accessed=32 * tokens * WIDE,
            transcendentals=tokens * tokens,
        ),
        name="attend_back",
    )(bounds, mixed, start, out, stat, gradt)


def segment_tables(lengths_row, tokens):
    ends = jnp.cumsum(lengths_row)
    slots = jnp.arange(tokens, dtype=jnp.int32)
    passed = slots[:, None] >= ends[None, :]
    start = jnp.max(jnp.where(passed, ends[None, :], 0), axis=1)
    stop = jnp.min(jnp.where(passed, tokens, ends[None, :]), axis=1)
    first_key = start[::BQ] // BK
    last_query = (stop[BK - 1 :: BK] - 1) // BQ + 1
    return start.astype(jnp.int32), first_key.astype(jnp.int32), last_query.astype(jnp.int32)


class Copies:
    def __init__(self, send, recv):
        self.send, self.recv, self.made, self.started = send, recv, 0, []

    def plan(self, source, target, device):
        index = self.made
        self.made += 1
        return pltpu.make_async_remote_copy(
            src_ref=source,
            dst_ref=target,
            send_sem=self.send.at[index],
            recv_sem=self.recv.at[index],
            device_id=device,
            device_id_type=MESH,
        )

    def begin(self, copy, condition=None):
        self.started.append((copy, condition))
        when(condition, copy.start)

    def start(self, source, target, device):
        copy = self.plan(source, target, device)
        self.begin(copy)
        return copy

    def finish(self):
        for copy, condition in self.started:
            when(condition, copy.wait_send)


def when(condition, action):
    if condition is None:
        action()
    else:
        pl.when(condition)(action)


def greet(devices):
    barrier = pltpu.get_barrier_semaphore()
    for device, condition in devices:
        when(
            condition,
            lambda device=device: pl.semaphore_signal(
                barrier, inc=1, device_id=device, device_id_type=MESH
            ),
        )
    present = [1 if condition is None else condition.astype(jnp.int32) for _, condition in devices]
    pl.semaphore_wait(barrier, sum(present))


class Place:
    def __init__(self, line):
        self.dp = dp = lax.axis_index("dp")
        self.tensor = tensor = lax.axis_index("tensor")
        self.spot, self.side = spot, side = dp // 2, dp % 2
        self.chip, self.core = tensor // 2, tensor % 2
        self.has_up, self.has_down = spot + 1 < line, spot > 0
        self.up = (jnp.minimum(spot + 1, line - 1) * 2 + side, tensor)
        self.down = (jnp.maximum(spot - 1, 0) * 2 + side, tensor)
        self.across = (spot * 2 + 1 - side, tensor)
        self.mate = (dp, tensor + 1 - 2 * (tensor % 2))
        self.far = (dp, (tensor + 2) % 4)
        self.corner = (dp, 3 - tensor)

    def everyone(self):
        return [
            (self.mate, None), (self.far, None), (self.corner, None), (self.across, None),
            (self.up, self.has_up), (self.down, self.has_down),
        ]


def comm_call(kernel, name, outputs, inputs, in_specs, out_specs, copies, cid, scratch=(), local=1):
    return pl.pallas_call(
        kernel,
        out_shape=outputs,
        in_specs=in_specs,
        out_specs=out_specs,
        scratch_shapes=list(scratch)
        + [
            pltpu.SemaphoreType.DMA((copies,)),
            pltpu.SemaphoreType.DMA((copies,)),
            pltpu.SemaphoreType.DMA((local,)),
        ],
        compiler_params=pltpu.CompilerParams(
            collective_id=cid, has_side_effects=True, vmem_limit_bytes=50 << 20
        ),
        name=name,
    )(*inputs)


def gather_inputs(hidden, cotangent, weights, vectors, n_dp):
    line = n_dp // 2
    rows, width = hidden.shape
    half_rows = rows // 2
    count = len(weights)

    def kernel(*refs):
        hidden_ref, cot_ref = refs[0], refs[1]
        share = list(refs[2 : 2 + count])
        vec_ref = refs[2 + count]
        hidden_out, cot_out = refs[3 + count], refs[4 + count]
        full = list(refs[5 + count : 6 + 2 * count])
        vec_out = refs[5 + 2 * count]
        send, recv, local = refs[6 + 2 * count :]
        at = Place(line)
        dp, tensor, spot, side = at.dp, at.tensor, at.spot, at.side
        far_row = (tensor + 2) % 4
        greet(at.everyone())
        copies = Copies(send, recv)
        share.append(vec_out.at[dp])
        upward, downward, up_side, down_side = [], [], [], []
        for hop in range(line - 1):
            lists = ([], [], [], [])
            above = jnp.maximum(spot - hop, 0) * 2 + side
            below = jnp.minimum(spot + hop, line - 1) * 2 + side
            came_up = jnp.maximum(spot - 1 - hop, 0) * 2 + side
            came_down = jnp.minimum(spot + 1 + hop, line - 1) * 2 + side
            for i in range(count + 1):
                source = share[i] if hop == 0 else full[i].at[above]
                lists[0].append(copies.plan(source, full[i].at[above], at.up))
                source = share[i] if hop == 0 else full[i].at[below]
                lists[1].append(copies.plan(source, full[i].at[below], at.down))
                lists[2].append(copies.plan(full[i].at[came_up], full[i].at[came_up], at.across))
                lists[3].append(
                    copies.plan(full[i].at[came_down], full[i].at[came_down], at.across)
                )
            for made, group in zip((upward, downward, up_side, down_side), lists):
                made.append(group)

        vec_made = [
            copies.start(vec_ref, vec_out.at[dp, tensor], device)
            for device in (at.mate, at.far, at.corner)
        ]
        parts = [pl.ds(0, half_rows), pl.ds(half_rows, half_rows)]
        far_made = [
            copies.start(hidden_ref.at[part], hidden_out.at[tensor, part], at.far)
            for part in parts
        ]
        own_side = []
        for i in range(count):
            copies.begin(upward[0][i], at.has_up)
            copies.begin(downward[0][i], at.has_down)
            own_side.append(copies.start(share[i], full[i].at[dp], at.across))
        mate_made = [
            copies.start(hidden_ref, hidden_out.at[tensor], at.mate),
            copies.start(cot_ref, cot_out.at[1], at.mate),
        ]
        stays = [
            pltpu.make_async_copy(vec_ref, vec_out.at[dp, tensor], local.at[0]),
            pltpu.make_async_copy(hidden_ref, hidden_out.at[tensor], local.at[1]),
            pltpu.make_async_copy(cot_ref, cot_out.at[0], local.at[2]),
        ] + [
            pltpu.make_async_copy(share[i], full[i].at[dp], local.at[3 + i]) for i in range(count)
        ]
        for copy in stays:
            copy.start()
        for copy in vec_made:
            copy.wait_recv()
        stays[0].wait()
        copies.begin(upward[0][count], at.has_up)
        copies.begin(downward[0][count], at.has_down)
        own_side.append(copies.start(vec_out.at[dp], vec_out.at[dp], at.across))
        relayed = []
        for hop in range(line - 1):
            from_below, from_above = spot - 1 - hop >= 0, spot + 1 + hop < line
            for i in range(count + 1):
                when(from_below, upward[hop][i].wait_recv)
                copies.begin(up_side[hop][i], from_below)
                if hop + 1 < line - 1:
                    copies.begin(upward[hop + 1][i], from_below & at.has_up)
                when(from_above, downward[hop][i].wait_recv)
                copies.begin(down_side[hop][i], from_above)
                if hop + 1 < line - 1:
                    copies.begin(downward[hop + 1][i], from_above & at.has_down)
            if hop < 2:
                far_made[hop].wait_recv()
                relayed.append(
                    copies.start(
                        hidden_out.at[far_row, parts[hop]],
                        hidden_out.at[far_row, parts[hop]],
                        at.mate,
                    )
                )
        for copy in own_side + mate_made + relayed:
            copy.wait_recv()
        for hop in range(line - 1):
            from_below, from_above = spot - 1 - hop >= 0, spot + 1 + hop < line
            for i in range(count + 1):
                when(from_below, up_side[hop][i].wait_recv)
                when(from_above, down_side[hop][i].wait_recv)
        copies.finish()
        for copy in stays[1:]:
            copy.wait()

    outputs = (
        (
            jax.ShapeDtypeStruct((4, rows, width), LOW),
            jax.ShapeDtypeStruct((2, rows, width), LOW),
        )
        + tuple(jax.ShapeDtypeStruct((n_dp,) + w.shape, LOW) for w in weights)
        + (jax.ShapeDtypeStruct((n_dp, 4) + vectors.shape, LOW),)
    )
    copy_count = 3 + 2 + 2 + 2 + (count + 1) + 4 * (line - 1) * (count + 1)
    return comm_call(
        kernel,
        "gather_inputs",
        outputs,
        (hidden, cotangent, *weights, vectors),
        [VM] * (3 + count),
        tuple([ANY] * len(outputs)),
        copy_count,
        0,
        local=3 + count,
    )


def mate_rows(rows_here, n_dp, cid):
    def kernel(in_ref, out_ref, send, recv, local):
        at = Place(n_dp // 2)
        greet([(at.mate, None)])
        copies = Copies(send, recv)
        copy = copies.start(in_ref, out_ref.at[1], at.mate)
        stay = pltpu.make_async_copy(in_ref, out_ref.at[0], local.at[0])
        stay.start()
        stay.wait()
        copy.wait()

    return comm_call(
        kernel,
        f"mate_rows_{cid}",
        jax.ShapeDtypeStruct((2,) + rows_here.shape, rows_here.dtype),
        (rows_here,),
        [VM],
        ANY,
        1,
        cid,
    )


def mate_sum_part(parts, n_dp, cid):
    def kernel(in_ref, out_ref, send, recv, local):
        at = Place(n_dp // 2)
        greet([(at.mate, None)])
        copies = Copies(send, recv)
        copies.start(in_ref.at[1], out_ref, at.mate).wait()

    return comm_call(
        kernel,
        f"mate_sum_part_{cid}",
        jax.ShapeDtypeStruct(parts.shape[1:], parts.dtype),
        (parts,),
        [ANY],
        ANY,
        1,
        cid,
    )


def heads_to_rows(attended, n_dp, cid):
    head_rows_here, slots = attended.shape
    block = slots // 4

    def kernel(in_ref, out_ref, send, recv, local):
        at = Place(n_dp // 2)
        greet([(at.far, None)])
        copies = Copies(send, recv)
        made, stays = [], []
        for i in range(2):
            core = at.core if i == 0 else 1 - at.core
            theirs = ((1 - at.chip) * 2 + core) * block
            ours = (at.chip * 2 + core) * block
            made.append(
                copies.start(
                    in_ref.at[:, pl.ds(pl.multiple_of(theirs, block), block)],
                    out_ref.at[1, :, i * block : (i + 1) * block],
                    at.far,
                )
            )
            stays.append(
                pltpu.make_async_copy(
                    in_ref.at[:, pl.ds(pl.multiple_of(ours, block), block)],
                    out_ref.at[0, :, i * block : (i + 1) * block],
                    local.at[i],
                )
            )
            stays[-1].start()
        for copy in stays + made:
            copy.wait()

    return comm_call(
        kernel,
        "heads_to_rows",
        jax.ShapeDtypeStruct((2, head_rows_here, slots // 2), attended.dtype),
        (attended,),
        [VM],
        ANY,
        2,
        cid,
        local=2,
    )


def rows_to_heads(grads, n_dp, cid):
    _, head_rows_here, slots = grads.shape
    block = slots // 2

    def kernel(in_ref, out_ref, send, recv, local):
        at = Place(n_dp // 2)
        greet([(at.far, None)])
        copies = Copies(send, recv)
        made, stays = [], []
        for i in range(2):
            core = at.core if i == 0 else 1 - at.core
            ours = pl.ds(pl.multiple_of((at.chip * 2 + core) * block, block), block)
            made.append(
                copies.start(
                    in_ref.at[1, :, i * block : (i + 1) * block], out_ref.at[:, ours], at.far
                )
            )
            stays.append(
                pltpu.make_async_copy(
                    in_ref.at[0, :, i * block : (i + 1) * block], out_ref.at[:, ours], local.at[i]
                )
            )
            stays[-1].start()
        for copy in stays + made:
            copy.wait()

    return comm_call(
        kernel,
        "rows_to_heads",
        jax.ShapeDtypeStruct((head_rows_here, 2 * slots), grads.dtype),
        (grads,),
        [VM],
        ANY,
        2,
        cid,
        local=2,
    )


def reduce_grads(weight_grads, row_parts, vector_parts, n_dp, cid):
    line = n_dp // 2
    count = len(weight_grads)
    shard, width = weight_grads[0].shape[1:]
    rows = row_parts.shape[1]
    half_rows = rows // 2
    grads = [g.reshape(line, 2, shard, width) for g in weight_grads]
    vectors = vector_parts.reshape(4, line, 2, VEC_ROWS, 128)
    slots = [(distance, way) for distance in range(line - 1, 0, -1) for way in (0, 1)] + [(0, 0)]

    def kernel(*refs):
        refs = list(refs)

        def take(number):
            taken = refs[:number]
            del refs[:number]
            return taken

        grad = take(count)
        part, vec = take(2)
        out = take(count)
        part_out, vec_out = take(2)
        side_land, hop_send, hop_land = take(count + 1), take(count + 1), take(count + 1)
        mate_land, far_send, far_land, vec_land, vec_sum, send, recv, local = refs
        grad.append(vec_sum)
        out.append(vec_out)
        at = Place(line)
        tensor, spot, side = at.tensor, at.spot, at.side
        greet(at.everyone())
        copies = Copies(send, recv)
        mate_row, far_row, corner_row = at.mate[1], at.far[1], at.corner[1]

        def block_of(slot):
            distance, way = slots[slot]
            if way == 0:
                return jnp.minimum(spot + distance, line - 1), spot + distance < line
            return jnp.maximum(spot - distance, 0), spot - distance >= 0

        sides, hops = [], []
        for slot in range(len(slots)):
            block, inside = block_of(slot)
            way = slots[slot][1]
            sides.append(
                [
                    copies.plan(grad[i].at[block, 1 - side], side_land[i].at[slot], at.across)
                    for i in range(count + 1)
                ]
            )
            if slots[slot][0] > 0:
                hops.append(
                    [
                        copies.plan(
                            hop_send[i].at[slot], hop_land[i].at[slot], (at.up, at.down)[way]
                        )
                        for i in range(count + 1)
                    ]
                )

        mate_far = copies.start(part.at[corner_row], mate_land.at[1], at.mate)
        vec_made = [
            copies.start(vec.at[row], vec_land.at[i], device)
            for i, (device, row) in enumerate(
                ((at.mate, mate_row), (at.far, far_row), (at.corner, corner_row))
            )
        ]

        def cross(distance, items):
            for slot in range(len(slots)):
                if slots[slot][0] == distance:
                    for i in items:
                        copies.begin(sides[slot][i], block_of(slot)[1])

        cross(line - 1, range(count))
        cross(line - 2, range(count))
        mate_own = copies.start(part.at[mate_row], mate_land.at[0], at.mate)
        mate_far.wait_recv()
        far_made = []
        for i in range(2):
            span = pl.ds(i * half_rows, half_rows)
            far_send[span] = (
                mate_land[1, span].astype(F32) + part[far_row, span].astype(F32)
            ).astype(LOW)
            far_made.append(copies.start(far_send.at[span], far_land.at[span], at.far))
        for copy in vec_made:
            copy.wait_recv()
        vec_sum[...] = vec[tensor] + vec_land[0] + vec_land[1] + vec_land[2]
        cross(line - 1, [count])
        cross(line - 2, [count])

        def handle(slot, i):
            block, inside = block_of(slot)
            way = slots[slot][1]
            behind = (at.has_down, at.has_up)[way]
            outer = slot - 2

            def work():
                sides[slot][i].wait_recv()
                total = grad[i][block, side].astype(F32) + side_land[i][slot].astype(F32)
                if outer < 0:
                    hop_send[i][slot] = total.astype(hop_send[i].dtype)
                    return

                @pl.when(behind)
                def _():
                    hops[outer][i].wait_recv()
                    hop_send[i][slot] = (total + hop_land[i][outer].astype(F32)).astype(
                        hop_send[i].dtype
                    )

                @pl.when(jnp.logical_not(behind))
                def _():
                    hop_send[i][slot] = total.astype(hop_send[i].dtype)

            when(inside, work)
            copies.begin(hops[slot][i], inside)

        for slot in range(len(slots) - 1):
            for i in range(count + 1):
                handle(slot, i)
            if slots[slot][1] == 1 and slots[slot][0] >= 2:
                cross(slots[slot][0] - 2, range(count + 1))
        mate_own.wait_recv()
        for i in range(2):
            span = pl.ds(i * half_rows, half_rows)
            far_made[i].wait_recv()
            part_out[span] = (
                part[tensor, span].astype(F32)
                + mate_land[0, span].astype(F32)
                + far_land[span].astype(F32)
            )
        last = len(slots) - 1
        for i in range(count + 1):
            sides[last][i].wait_recv()
            out[i][...] = grad[i][spot, side].astype(F32) + side_land[i][last].astype(F32)
            for way, behind in enumerate((at.has_down, at.has_up)):

                def add(way=way, i=i):
                    hops[last - 2 + way][i].wait_recv()
                    out[i][...] += hop_land[i][last - 2 + way].astype(F32)

                when(behind, add)
        copies.finish()

    outputs = (
        (jax.ShapeDtypeStruct((shard, width), F32),) * count
        + (
            jax.ShapeDtypeStruct((rows, width), F32),
            jax.ShapeDtypeStruct((VEC_ROWS, 128), F32),
        )
    )
    moved = len(slots) - 1
    scratch = []
    for number in (moved + 1, moved, moved):
        scratch += [pltpu.VMEM((number, shard, width), LOW)] * count
        scratch.append(pltpu.VMEM((number, VEC_ROWS, 128), F32))
    scratch += [
        pltpu.VMEM((2, rows, width), LOW),
        pltpu.VMEM((rows, width), LOW),
        pltpu.VMEM((rows, width), LOW),
        pltpu.VMEM((3, line, 2, VEC_ROWS, 128), F32),
        pltpu.VMEM((line, 2, VEC_ROWS, 128), F32),
    ]
    copy_count = 2 + 3 + 2 + (2 * moved + 1) * (count + 1)
    return comm_call(
        kernel,
        "reduce_grads",
        outputs,
        (*grads, row_parts, vectors),
        [VM] * (count + 2),
        (VM,) * len(outputs),
        copy_count,
        cid,
        scratch=scratch,
    )


def unit_kernel(add, *refs):
    refs = list(refs)
    rows_ref, grad_ref, fc_ref, proj_ref, bias_ref = refs[:5]
    refs = refs[5:]
    if add:
        last_in, two_in = refs[:2]
        refs = refs[2:]
    last_ref, two_ref, fc_grad_ref, proj_grad_ref, bias_grad_ref = refs[:5]
    fc_sum, proj_sum = refs[5:]
    step = pl.program_id(0)

    @pl.when(step == 0)
    def _():
        fc_sum[...] = jnp.zeros_like(fc_sum)
        proj_sum[...] = jnp.zeros_like(proj_sum)
        bias_grad_ref[...] = jnp.zeros_like(bias_grad_ref)

    rows, grad = rows_ref[...], grad_ref[...]
    inner = nn(rows, fc_ref[...]) + bias_ref[...]
    square = inner * inner
    bend = jnp.tanh(GELU_SCALE * inner * (1.0 + GELU_CUBE * square))
    half = 0.5 * (1.0 + bend)
    activated = (inner * half).astype(LOW)
    slope = half + 0.5 * inner * (1.0 - bend * bend) * GELU_SCALE * (1.0 + 3.0 * GELU_CUBE * square)
    grad_inner = (nn(grad, proj_ref[...]) * slope).astype(LOW)
    last = nt(activated, proj_ref[...])
    two = nt(grad_inner, fc_ref[...])
    if add:
        last, two = last + last_in[...], two + two_in[...]
    last_ref[...] = last.astype(last_ref.dtype)
    two_ref[...] = two.astype(two_ref.dtype)
    fc_sum[...] += tn(rows, grad_inner)
    proj_sum[...] += tn(grad, activated)
    bias_grad_ref[...] += jnp.sum(grad_inner.astype(F32), axis=0, keepdims=True)

    @pl.when(step == pl.num_programs(0) - 1)
    def _():
        fc_grad_ref[...] = fc_sum[...].astype(fc_grad_ref.dtype)
        proj_grad_ref[...] = proj_sum[...].astype(proj_grad_ref.dtype)


def units_both_ways(rows, grad, fc, proj, bias, before, grad_type):
    count, width = rows.shape
    units = fc.shape[1]
    tile = pl.BlockSpec((ROW_TILE, width), lambda i: (i, 0))
    fixed = lambda shape: pl.BlockSpec(shape, lambda i: (0, 0))
    add = before is not None
    kind = LOW if add else F32
    return pl.pallas_call(
        functools.partial(unit_kernel, add),
        grid=(count // ROW_TILE,),
        out_shape=(
            jax.ShapeDtypeStruct((count, width), kind),
            jax.ShapeDtypeStruct((count, width), kind),
            jax.ShapeDtypeStruct((width, units), grad_type),
            jax.ShapeDtypeStruct((width, units), grad_type),
            jax.ShapeDtypeStruct((1, units), F32),
        ),
        in_specs=[tile, tile, fixed((width, units)), fixed((width, units)), fixed((1, units))]
        + [tile] * (2 if add else 0),
        out_specs=(tile, tile, fixed((width, units)), fixed((width, units)), fixed((1, units))),
        scratch_shapes=[pltpu.VMEM((width, units), F32)] * 2,
        compiler_params=pltpu.CompilerParams(
            dimension_semantics=("arbitrary",), vmem_limit_bytes=50 << 20
        ),
        cost_estimate=pl.CostEstimate(
            flops=12 * count * width * units,
            bytes_accessed=24 * count * width,
            transcendentals=count * units,
        ),
        name="units_far" if add else "units_own",
    )(rows, grad, fc, proj, bias, *(before or ()))


def normalize(values):
    center = jnp.mean(values, axis=-1, keepdims=True)
    offset = values - center
    spread = jnp.mean(offset * offset, axis=-1, keepdims=True)
    inverse = lax.rsqrt(spread + EPSILON)
    return offset * inverse, inverse


def norm_back(normed, inverse, grad, gain):
    scaled = grad * gain
    center = jnp.mean(scaled, axis=-1, keepdims=True)
    along = jnp.mean(scaled * normed, axis=-1, keepdims=True)
    return inverse * (scaled - center - normed * along)


def product(equation, left, right):
    return jnp.einsum(equation, left, right, preferred_element_type=F32)


def pack_three(qkv, out_turned):
    depth = qkv.shape[0]
    parts = jnp.transpose(qkv.reshape(depth, NH, 3, HD), (0, 2, 1, 3))
    extra = out_turned.reshape(depth, 3, 1, HD)
    return jnp.concatenate([parts, extra], axis=2).reshape(depth, 3 * WIDE)


def unpack_three(packed):
    depth = packed.shape[0]
    split = packed.reshape(depth, 3, NH + 1, HD)
    qkv = jnp.transpose(split[:, :, :NH], (0, 2, 1, 3)).reshape(depth, 3 * NH * HD)
    return qkv, split[:, :, NH].reshape(depth, NH * HD)


def per_device(
    tokens,
    thoughts,
    positions,
    lengths,
    attn_norm_gain,
    attn_norm_shift,
    qkv_weight,
    qv_bias,
    attn_out_weight,
    attn_out_bias,
    mlp_norm_gain,
    mlp_norm_shift,
    fc_weight,
    fc_bias,
    proj_weight,
    proj_bias,
    cotangent,
):
    n_dp = lax.axis_size("dp")
    n_tensor = lax.axis_size("tensor")
    tensor = lax.axis_index("tensor")
    rows, width = tokens.shape
    slots = rows * n_tensor
    head_width = NH * HD
    units = FF // n_tensor
    far = (tensor + 2) % n_tensor
    swap_far = [(i, (i + 2) % n_tensor) for i in range(n_tensor)]

    window = rows // thoughts.shape[0]
    starts = jnp.arange(thoughts.shape[0], dtype=jnp.int32) * window
    placed = (
        jnp.arange(window, dtype=jnp.int32)[None, :] == (positions - starts)[:, None]
    )[:, :, None]
    tokens_low = jnp.where(
        placed, thoughts[:, None, :], tokens.reshape(-1, window, width)
    ).reshape(rows, width)

    start, first_key, last_query = segment_tables(lengths[0], slots)
    live_slots = jnp.sum(lengths[0][:SEQ_DEV])
    own_slots = tensor * rows + jnp.arange(rows, dtype=jnp.int32)
    live = (own_slots < live_slots)[:, None]
    grad_final_low = jnp.where(live, cotangent, jnp.zeros_like(cotangent))

    share = width // (n_dp * n_tensor)
    small = [
        attn_norm_gain, attn_norm_shift, qv_bias[0], qv_bias[1], attn_out_bias,
        mlp_norm_gain, mlp_norm_shift, proj_bias, fc_bias,
    ]
    vectors = jnp.stack([jnp.pad(v, (0, 128 - v.shape[0])) for v in small])
    vectors = jnp.pad(vectors, ((0, VEC_ROWS - len(small)), (0, 0)))

    shares = (fc_weight, proj_weight.T, pack_three(qkv_weight, attn_out_weight.T))
    gathered = gather_inputs(tokens_low, grad_final_low, shares, vectors, n_dp)
    group_rows, grad_rows, fc_all, proj_all, mix_all, vec_all = gathered
    fc_own, proj_own, mix_own = [w.reshape(width, -1) for w in (fc_all, proj_all, mix_all)]
    out_own = mix_own.reshape(width, 3, NH + 1, HD)[:, :, NH].reshape(width, head_width)
    out_far = lax.ppermute(out_own, "tensor", swap_far)
    fc_far = lax.ppermute(fc_own, "tensor", swap_far)

    def whole(row, size):
        return vec_all[:, :, row, :size].reshape(-1).astype(F32)

    gain_one, shift_one, query_bias, value_bias, out_bias, gain_two, shift_two, last_bias = [
        whole(i, share) for i in range(8)
    ]
    hidden_bias = whole(8, fc_bias.shape[0])

    def own_part(vector, index, size):
        return lax.dynamic_slice_in_dim(vector, index * size, size, 0)

    pad = jnp.zeros((WIDE - head_width,), F32)
    bias_three = jnp.concatenate(
        [
            own_part(query_bias, tensor, head_width), pad,
            jnp.zeros((WIDE,), F32),
            own_part(value_bias, tensor, head_width), pad,
        ]
    )
    group_hidden = group_rows.reshape(slots, width).astype(F32)
    group_normed, _ = normalize(group_hidden)
    normed_one = (group_normed * gain_one + shift_one).astype(LOW)
    mixed = (product("td,dc->tc", normed_one, mix_own) + bias_three).astype(LOW)
    start_row = start[None, :]
    attended, stats = attend(first_key, mixed, start_row)
    sent, out_far, fc_far = lax.optimization_barrier((attended, out_far, fc_far))
    both = heads_to_rows(sent, n_dp, 1)
    both, proj_own_sent = lax.optimization_barrier((both, proj_own))
    proj_far = lax.ppermute(proj_own_sent, "tensor", swap_far)
    mid_part = product("et,de->td", both[0], out_own) + product("et,de->td", both[1], out_far)
    mid_low = mid_part.astype(LOW).reshape(2, rows, width)
    mid_mate = mate_sum_part(mid_low, n_dp, 2)
    hidden = tokens_low.astype(F32)
    middle = hidden + mid_low[0].astype(F32) + mid_mate.astype(F32) + out_bias
    normed_mid, inverse_mid = normalize(middle)
    normed_two = (normed_mid * gain_two + shift_two).astype(LOW)
    chip_two = mate_rows(normed_two, n_dp, 3).reshape(2 * rows, width)
    chip_grad = grad_rows.reshape(2 * rows, width)

    def bias_row(index):
        return own_part(hidden_bias, index, units)[None]

    last_own, two_own, grad_fc, grad_proj, grad_fc_bias = units_both_ways(
        chip_two, chip_grad, fc_own, proj_own, bias_row(tensor), None, F32
    )
    last_part, grad_two_part, far_fc, far_proj, far_fc_bias = units_both_ways(
        chip_two, chip_grad, fc_far, proj_far, bias_row(far), (last_own, two_own), LOW
    )
    grad_fc_bias, far_fc_bias = grad_fc_bias[0], far_fc_bias[0]
    split = width // 2
    proj_head = lax.ppermute(far_proj[:split], "tensor", swap_far)
    two_low = grad_two_part.reshape(2, rows, width)
    two_mate = mate_sum_part(two_low, n_dp, 4)
    grad_two = two_low[0].astype(F32) + two_mate.astype(F32)
    grad_final = grad_final_low.astype(F32)
    grad_middle = grad_final + norm_back(normed_mid, inverse_mid, grad_two, gain_two)
    grad_gain_two = jnp.sum(normed_mid * grad_two, axis=0)
    grad_shift_two = jnp.sum(grad_two, axis=0)
    chip_mid = mate_rows(grad_middle.astype(LOW), n_dp, 5).reshape(2 * rows, width)
    grad_attended = jnp.stack(
        [product("de,td->et", w, chip_mid).astype(LOW) for w in (out_own, out_far)]
    )
    grad_out, far_out = [product("td,et->de", chip_mid, both[i]) for i in range(2)]
    grad_attended, proj_head = lax.optimization_barrier((grad_attended, proj_head))
    grad_heads = rows_to_heads(grad_attended, n_dp, 6)
    grad_heads, rest, far_fc, far_out = lax.optimization_barrier(
        (grad_heads, far_proj[split:], far_fc, far_out.astype(LOW))
    )
    proj_tail = lax.ppermute(rest, "tensor", swap_far)
    far_fc = lax.ppermute(far_fc, "tensor", swap_far)
    far_out = lax.ppermute(far_out, "tensor", swap_far)
    last_low = last_part.reshape(2, rows, width)
    last_mate = mate_sum_part(last_low, n_dp, 7)
    final = middle + last_low[0].astype(F32) + last_mate.astype(F32) + last_bias
    block_out = jnp.where(live, final, 0.0).astype(LOW)

    grad_mixed = attend_back(last_query, mixed, start_row, attended, stats, grad_heads)
    grad_mixed, proj_tail = lax.optimization_barrier((grad_mixed, proj_tail))
    one_part = product("tc,dc->td", grad_mixed, mix_own)
    grad_mix = product("td,tc->dc", normed_one, grad_mixed)
    grad_gain_one = jnp.sum(group_normed * one_part, axis=0)
    grad_shift_one = jnp.sum(one_part, axis=0)
    mix_sums = jnp.sum(grad_mixed, axis=0, dtype=F32)
    out_total = (grad_out + far_out.astype(F32)).reshape(width, 3, 1, HD)
    mix_total = grad_mix + jnp.pad(out_total, ((0, 0), (0, 0), (NH, 0), (0, 0))).reshape(
        width, 3 * WIDE
    )
    totals = [
        (grad_fc + far_fc.astype(F32)).astype(LOW),
        (grad_proj + jnp.concatenate([proj_head, proj_tail]).astype(F32)).astype(LOW),
        mix_total.astype(LOW),
    ]

    def spread(vector, index, size, length):
        return lax.dynamic_update_slice_in_dim(jnp.zeros((length,), F32), vector, index * size, 0)

    def tiles(vector):
        cut = vector.reshape(n_dp, n_tensor, -1)
        return jnp.pad(cut, ((0, 0), (0, 0), (0, 128 - cut.shape[2])))

    fc_bias_part = lax.dynamic_update_slice_in_dim(
        spread(grad_fc_bias, tensor, units, FF), far_fc_bias, far * units, 0
    )
    vector_rows = [
        grad_gain_one, grad_shift_one,
        spread(mix_sums[:head_width], tensor, head_width, width),
        spread(mix_sums[2 * WIDE : 2 * WIDE + head_width], tensor, head_width, width),
        jnp.sum(grad_middle, axis=0), grad_gain_two, grad_shift_two,
        jnp.sum(grad_final, axis=0), fc_bias_part,
    ]
    vector_parts = jnp.stack([tiles(v) for v in vector_rows], axis=2)
    vector_parts = jnp.pad(
        vector_parts, ((0, 0), (0, 0), (0, VEC_ROWS - len(vector_rows)), (0, 0))
    )
    vector_parts = jnp.transpose(vector_parts, (1, 0, 2, 3))
    reduced = reduce_grads(
        [g.reshape(n_dp, -1, width) for g in totals],
        one_part.astype(LOW).reshape(n_tensor, rows, width),
        vector_parts,
        n_dp,
        8,
    )
    fc_grad, proj_grad, mix_grad, grad_one, vec = reduced
    qkv_grad, out_grad = unpack_three(mix_grad)
    normed_hid, inverse_hid = normalize(hidden)
    grad_hidden = grad_middle + norm_back(normed_hid, inverse_hid, grad_one, gain_one)
    windows = grad_hidden.reshape(-1, window, width)
    grad_thoughts = jnp.sum(jnp.where(placed, windows, 0.0), axis=1)
    grad_tokens = jnp.where(placed, 0.0, windows).reshape(rows, width)
    return (
        block_out,
        grad_tokens,
        grad_thoughts,
        vec[0, :share],
        vec[1, :share],
        qkv_grad,
        vec[2:4, :share],
        out_grad.T,
        vec[4, :share],
        vec[5, :share],
        vec[6, :share],
        fc_grad,
        vec[8, : fc_bias.shape[0]],
        proj_grad.T,
        vec[7, :share],
    )


def solution(mesh):
    rows = P(("dp", "tensor"), None)
    line = P(("dp", "tensor"))
    in_specs = (
        rows, rows, line, P("dp", None), line, line, P("dp", "tensor"),
        P(None, ("dp", "tensor")), P("tensor", "dp"), line, line, line,
        P("dp", "tensor"), line, P("tensor", "dp"), line, rows,
    )
    out_specs = (
        rows, rows, rows, line, line, P("dp", "tensor"), P(None, ("dp", "tensor")),
        P("tensor", "dp"), line, line, line, P("dp", "tensor"), line, P("tensor", "dp"), line,
    )
    return jax.shard_map(
        per_device, mesh=mesh, in_specs=in_specs, out_specs=out_specs, check_vma=False
    )
```

```python
import functools
import math

import jax
import jax.numpy as jnp
from jax import lax
from jax.experimental import pallas as pl
from jax.experimental.pallas import tpu as pltpu
from jax.sharding import PartitionSpec as P

H = 12
HD = 64
FF = 3072
SEQ_DEV = 3
EPSILON = 1e-05
MASKED = -1e30
NH = 3
SLABS = 2
WIDE = SLABS * 128
BQ = 512
BK = 512
VEC_ROWS = 16
ROW_TILE = 256
GELU_SCALE = math.sqrt(2.0 / math.pi)
GELU_CUBE = 0.044715
MESH = pl.DeviceIdType.MESH
ANY = pl.BlockSpec(memory_space=pl.ANY)
VM = pl.BlockSpec(memory_space=pltpu.VMEM)
LOW = jnp.bfloat16
F32 = jnp.float32


def nn(a, b):
    return lax.dot_general(a, b, (((1,), (0,)), ((), ())), preferred_element_type=jnp.float32)


def nt(a, b):
    return lax.dot_general(a, b, (((1,), (1,)), ((), ())), preferred_element_type=jnp.float32)


def tn(a, b):
    return lax.dot_general(a, b, (((0,), (0,)), ((), ())), preferred_element_type=jnp.float32)


def head_rows(slab, head):
    half = slab[(head % 2) * HD : (head % 2 + 1) * HD]
    zero = jnp.zeros_like(half)
    return jnp.concatenate([half, zero] if head % 2 == 0 else [zero, half], axis=0)


def segment_start(ends_ref, slots):
    start = jnp.zeros_like(slots)
    for i in range(SEQ_DEV):
        start = jnp.where(slots >= ends_ref[i], ends_ref[i], start)
    return start


def segment_stop(ends_ref, slot, slots):
    stop = slots
    for i in reversed(range(SEQ_DEV)):
        stop = jnp.where(slot < ends_ref[i], ends_ref[i], stop)
    return stop


def attend_kernel(ends_ref, mixed_ref, out_ref, stat_ref, qt_ref, vt_ref):
    tokens = mixed_ref.shape[0]
    for first in range(0, tokens, BQ):
        rows = pl.ds(first, BQ)
        for slab in range(SLABS):
            lanes = slab * 128
            qt_ref[lanes : lanes + 128, rows] = (
                mixed_ref[rows, lanes : lanes + 128] * HD ** (-0.5)
            ).T
            vt_ref[lanes : lanes + 128, rows] = mixed_ref[
                rows, 2 * WIDE + lanes : 2 * WIDE + lanes + 128
            ].T

    def query_block(block, carry):
        first = pl.multiple_of(block * BQ, BQ)
        columns = pl.ds(first, BQ)
        start = segment_start(ends_ref, first + lax.broadcasted_iota(jnp.int32, (1, BQ), 1))
        query_ids = first + lax.broadcasted_iota(jnp.int32, (BK, BQ), 1)
        queries = [
            head_rows(qt_ref[(h // 2) * 128 : (h // 2 + 1) * 128, columns], h) for h in range(NH)
        ]

        def key_block(key, state):
            base = pl.multiple_of(key * BK, BK)
            rows = pl.ds(base, BK)
            key_ids = base + lax.broadcasted_iota(jnp.int32, (BK, BQ), 0)
            allowed = (key_ids <= query_ids) & (key_ids >= start)
            result = []
            for h in range(NH):
                peak, total, acc = state[h]
                slab = h // 2
                scores = nn(mixed_ref[rows, WIDE + slab * 128 : WIDE + slab * 128 + 128], queries[h])
                scores = jnp.where(allowed, scores, MASKED)
                fresh = jnp.maximum(peak, jnp.max(scores, axis=0, keepdims=True))
                weight = jnp.exp(scores - fresh)
                decay = jnp.exp(peak - fresh)
                total = total * decay + jnp.sum(weight, axis=0, keepdims=True)
                values = vt_ref[h * HD : (h + 1) * HD, rows]
                acc = acc * decay + nn(values, weight.astype(jnp.bfloat16))
                result.append((fresh, total, acc))
            return tuple(result)

        empty = tuple(
            (
                jnp.full((1, BQ), MASKED, jnp.float32),
                jnp.zeros((1, BQ), jnp.float32),
                jnp.zeros((HD, BQ), jnp.float32),
            )
            for _ in range(NH)
        )
        state = lax.fori_loop(segment_start(ends_ref, first) // BK, (block + 1) * (BQ // BK), key_block, empty)
        for h in range(NH):
            peak, total, acc = state[h]
            out_ref[h * HD : (h + 1) * HD, columns] = (acc / total).astype(jnp.bfloat16)
            stat_ref[h : h + 1, columns] = peak + jnp.log(total)
        return carry

    lax.fori_loop(0, tokens // BQ, query_block, 0)


def attend(ends, mixed):
    tokens = mixed.shape[0]
    vm = pl.BlockSpec(memory_space=pltpu.VMEM)
    return pl.pallas_call(
        attend_kernel,
        out_shape=(
            jax.ShapeDtypeStruct((NH * HD, tokens), jnp.bfloat16),
            jax.ShapeDtypeStruct((8, tokens), jnp.float32),
        ),
        in_specs=[pl.BlockSpec(memory_space=pltpu.SMEM), vm],
        out_specs=(vm, vm),
        scratch_shapes=[pltpu.VMEM((WIDE, tokens), jnp.bfloat16)] * 2,
        compiler_params=pltpu.CompilerParams(vmem_limit_bytes=40 << 20),
        cost_estimate=pl.CostEstimate(
            flops=8 * tokens * tokens * NH * HD,
            bytes_accessed=16 * tokens * WIDE,
            transcendentals=tokens * tokens,
        ),
        name="attend",
    )(ends, mixed)


def attend_back_kernel(
    ends_ref, mixed_ref, out_ref, stat_ref, gradt_ref,
    gmixed_ref, qt_ref, kt_ref, grad_ref, delta_ref, dqt_ref
):
    tokens = mixed_ref.shape[0]
    for first in range(0, tokens, BQ):
        rows = pl.ds(first, BQ)
        for slab in range(SLABS):
            lanes = slab * 128
            qt_ref[lanes : lanes + 128, rows] = (
                mixed_ref[rows, lanes : lanes + 128] * HD ** (-0.5)
            ).T
            kt_ref[lanes : lanes + 128, rows] = mixed_ref[rows, WIDE + lanes : WIDE + lanes + 128].T
        grad_ref[rows, 0:128] = gradt_ref[0:128, rows].T
        grad_ref[rows, 128:256] = jnp.concatenate(
            [gradt_ref[128:192, rows], jnp.zeros((64, BQ), jnp.bfloat16)], axis=0
        ).T
        for h in range(NH):
            product = gradt_ref[h * HD : (h + 1) * HD, rows].astype(jnp.float32) * out_ref[
                h * HD : (h + 1) * HD, rows
            ].astype(jnp.float32)
            delta_ref[h : h + 1, rows] = jnp.sum(product, axis=0, keepdims=True)
    dqt_ref[...] = jnp.zeros_like(dqt_ref)
    lane = lax.broadcasted_iota(jnp.int32, (BQ, 128), 1)

    def key_block(key, carry):
        base = pl.multiple_of(key * BK, BK)
        rows = pl.ds(base, BK)
        key_ids = base + lax.broadcasted_iota(jnp.int32, (BK, BQ), 0)

        def query_block(block, state):
            first = pl.multiple_of(block * BQ, BQ)
            columns = pl.ds(first, BQ)
            start = segment_start(ends_ref, first + lax.broadcasted_iota(jnp.int32, (1, BQ), 1))
            query_ids = first + lax.broadcasted_iota(jnp.int32, (BK, BQ), 1)
            allowed = (key_ids <= query_ids) & (key_ids >= start)
            grad_keys = list(state[:SLABS])
            grad_values = list(state[SLABS:])
            for h in range(NH):
                slab = h // 2
                low, high = slab * 128, slab * 128 + 128
                queries = head_rows(qt_ref[low:high, columns], h)
                scores = nn(mixed_ref[rows, WIDE + low : WIDE + high], queries)
                probs = jnp.where(allowed, jnp.exp(scores - stat_ref[h : h + 1, columns]), 0.0)
                keep = (lane // HD) == (h % 2)
                grads = jnp.where(keep, grad_ref[columns, low:high], 0.0)
                grad_values[slab] += nn(probs.astype(jnp.bfloat16), grads)
                if h == NH - 1 and NH % 2 == 1:
                    grad_rows = jnp.concatenate(
                        [gradt_ref[h * HD : (h + 1) * HD, columns], jnp.zeros((HD, BQ), jnp.bfloat16)],
                        axis=0,
                    )
                else:
                    grad_rows = head_rows(gradt_ref[low:high, columns], h)
                grad_probs = nn(mixed_ref[rows, 2 * WIDE + low : 2 * WIDE + high], grad_rows)
                grad_scores = (probs * (grad_probs - delta_ref[h : h + 1, columns])).astype(
                    jnp.bfloat16
                )
                natural = mixed_ref[columns, low:high]
                grad_keys[slab] += nn(grad_scores, jnp.where(keep, natural, 0.0))
                dqt_ref[h * HD : (h + 1) * HD, columns] += nn(
                    kt_ref[h * HD : (h + 1) * HD, rows], grad_scores
                )
            return tuple(grad_keys) + tuple(grad_values)

        empty = (jnp.zeros((BK, 128), jnp.float32),) * (2 * SLABS)
        stop = segment_stop(ends_ref, base + BK - 1, tokens)
        state = lax.fori_loop(key * BK // BQ, (stop - 1) // BQ + 1, query_block, empty)
        for slab in range(SLABS):
            low = slab * 128
            gmixed_ref[rows, WIDE + low : WIDE + low + 128] = (
                state[slab] * HD ** (-0.5)
            ).astype(jnp.bfloat16)
            gmixed_ref[rows, 2 * WIDE + low : 2 * WIDE + low + 128] = state[SLABS + slab].astype(
                jnp.bfloat16
            )
        return carry

    lax.fori_loop(0, tokens // BK, key_block, 0)
    for first in range(0, tokens, BQ):
        rows = pl.ds(first, BQ)
        for slab in range(SLABS):
            low = slab * 128
            gmixed_ref[rows, low : low + 128] = (
                (dqt_ref[low : low + 128, rows] * HD ** (-0.5)).T.astype(jnp.bfloat16)
            )


def attend_back(ends, mixed, out, stat, gradt):
    tokens = mixed.shape[0]
    vm = pl.BlockSpec(memory_space=pltpu.VMEM)
    return pl.pallas_call(
        attend_back_kernel,
        out_shape=jax.ShapeDtypeStruct((tokens, 3 * WIDE), jnp.bfloat16),
        in_specs=[pl.BlockSpec(memory_space=pltpu.SMEM)] + [vm] * 4,
        out_specs=vm,
        scratch_shapes=[
            pltpu.VMEM((WIDE, tokens), jnp.bfloat16),
            pltpu.VMEM((WIDE, tokens), jnp.bfloat16),
            pltpu.VMEM((tokens, WIDE), jnp.bfloat16),
            pltpu.VMEM((8, tokens), jnp.float32),
            pltpu.VMEM((WIDE, tokens), jnp.float32),
        ],
        compiler_params=pltpu.CompilerParams(vmem_limit_bytes=50 << 20),
        cost_estimate=pl.CostEstimate(
            flops=20 * tokens * tokens * NH * HD,
            bytes_accessed=32 * tokens * WIDE,
            transcendentals=tokens * tokens,
        ),
        name="attend_back",
    )(ends, mixed, out, stat, gradt)


class Copies:
    def __init__(self, send, recv):
        self.send, self.recv, self.made, self.started = send, recv, 0, []

    def plan(self, source, target, device):
        index = self.made
        self.made += 1
        return pltpu.make_async_remote_copy(
            src_ref=source,
            dst_ref=target,
            send_sem=self.send.at[index],
            recv_sem=self.recv.at[index],
            device_id=device,
            device_id_type=MESH,
        )

    def begin(self, copy, condition=None):
        self.started.append((copy, condition))
        when(condition, copy.start)

    def start(self, source, target, device):
        copy = self.plan(source, target, device)
        self.begin(copy)
        return copy

    def finish(self):
        for copy, condition in self.started:
            when(condition, copy.wait_send)


def when(condition, action):
    if condition is None:
        action()
    else:
        pl.when(condition)(action)


def greet(devices):
    barrier = pltpu.get_barrier_semaphore()
    for device, condition in devices:
        when(
            condition,
            lambda device=device: pl.semaphore_signal(
                barrier, inc=1, device_id=device, device_id_type=MESH
            ),
        )
    present = [1 if condition is None else condition.astype(jnp.int32) for _, condition in devices]
    pl.semaphore_wait(barrier, sum(present))


class Place:
    def __init__(self, line):
        self.dp = dp = lax.axis_index("dp")
        self.tensor = tensor = lax.axis_index("tensor")
        self.spot, self.side = spot, side = dp // 2, dp % 2
        self.chip, self.core = tensor // 2, tensor % 2
        self.has_up, self.has_down = spot + 1 < line, spot > 0
        self.up = (jnp.minimum(spot + 1, line - 1) * 2 + side, tensor)
        self.down = (jnp.maximum(spot - 1, 0) * 2 + side, tensor)
        self.across = (spot * 2 + 1 - side, tensor)
        self.mate = (dp, tensor + 1 - 2 * (tensor % 2))
        self.far = (dp, (tensor + 2) % 4)
        self.corner = (dp, 3 - tensor)

    def everyone(self):
        return [
            (self.mate, None), (self.far, None), (self.corner, None), (self.across, None),
            (self.up, self.has_up), (self.down, self.has_down),
        ]


def comm_call(kernel, name, outputs, inputs, in_specs, out_specs, copies, cid, scratch=(), local=1):
    return pl.pallas_call(
        kernel,
        out_shape=outputs,
        in_specs=in_specs,
        out_specs=out_specs,
        scratch_shapes=list(scratch)
        + [
            pltpu.SemaphoreType.DMA((copies,)),
            pltpu.SemaphoreType.DMA((copies,)),
            pltpu.SemaphoreType.DMA((local,)),
        ],
        compiler_params=pltpu.CompilerParams(
            collective_id=cid, has_side_effects=True, vmem_limit_bytes=50 << 20
        ),
        name=name,
    )(*inputs)


def one_hot(rows, columns, shift, limit):
    lane = lax.broadcasted_iota(jnp.int32, (rows, columns), 0)
    spot = lax.broadcasted_iota(jnp.int32, (rows, columns), 1)
    return ((spot == lane + shift) & (lane < limit)).astype(LOW)


def gather_inputs(hidden, cotangent, fc, proj, mix, vectors, n_dp):
    line = n_dp // 2
    hops = line - 1
    rows, width = hidden.shape
    shard = fc.shape[0]
    half_rows = rows // 2
    share = width // (n_dp * 4)

    def kernel(
        hidden_ref, cot_ref, fc_ref, proj_ref, mix_ref, vec_ref,
        normed_out, mixed_out, mix_out, fc_near, fc_side, fc_far, proj_near, cot_out, out_out,
        vec_out,
        land, mix_land, tiles, tile_land, normed, mixed, out_turned, send, recv, local,
    ):
        at = Place(line)
        dp, tensor, spot, side = at.dp, at.tensor, at.spot, at.side
        mate_row, far_row, corner_row = at.mate[1], at.far[1], at.corner[1]
        greet(at.everyone())
        copies = Copies(send, recv)
        MIX, FC, PROJ, VEC = range(4)
        own = [mix_ref, fc_ref, proj_ref, tiles.at[dp]]

        def seat(item, position):
            if item == MIX:
                return mix_land.at[position * 2 + side]
            if item == FC:
                return fc_near.at[position]
            if item == PROJ:
                return proj_near.at[position]
            return tiles.at[position * 2 + side]

        def plan(item, hop):
            above, below = jnp.maximum(spot - hop, 0), jnp.minimum(spot + hop, line - 1)
            came_up = jnp.maximum(spot - 1 - hop, 0)
            came_down = jnp.minimum(spot + 1 + hop, line - 1)
            made = {
                "up": copies.plan(
                    own[item] if hop == 0 else seat(item, above), seat(item, above), at.up
                ),
                "down": copies.plan(
                    own[item] if hop == 0 else seat(item, below), seat(item, below), at.down
                ),
                "onward": [],
            }
            for position in (came_up, came_down):
                onward = []
                if item in (MIX, VEC):
                    onward.append(copies.plan(seat(item, position), seat(item, position), at.across))
                if item == FC:
                    onward.append(copies.plan(fc_near.at[position], fc_side.at[position], at.across))
                    onward.append(copies.plan(fc_near.at[position], fc_far.at[position], at.far))
                made["onward"].append(onward)
            return made

        plans = [[plan(item, hop) for hop in range(hops)] for item in range(4)]

        def launch(item):
            copies.begin(plans[item][0]["up"], at.has_up)
            copies.begin(plans[item][0]["down"], at.has_down)

        def handle(item, hop):
            made = plans[item][hop]
            for way, key, comes, goes in (
                (0, "up", spot - 1 - hop >= 0, at.has_up),
                (1, "down", spot + 1 + hop < line, at.has_down),
            ):
                when(comes, made[key].wait_recv)
                if hop + 1 < hops:
                    copies.begin(plans[item][hop + 1][key], comes & goes)
                for copy in made["onward"][way]:
                    copies.begin(copy, comes)

        def settle(item):
            for hop in range(hops):
                for way, comes in ((0, spot - 1 - hop >= 0), (1, spot + 1 + hop < line)):
                    for copy in plans[item][hop]["onward"][way]:
                        when(comes, copy.wait_recv)

        stays = []

        def stay(source, target):
            copy = pltpu.make_async_copy(source, target, local.at[len(stays)])
            copy.start()
            stays.append(copy)
            return copy

        vec_made = [
            copies.start(vec_ref, tile_land.at[i], device)
            for i, device in enumerate((at.mate, at.far, at.corner))
        ]
        parts = [pl.ds(0, half_rows), pl.ds(half_rows, half_rows)]
        launch(MIX)
        far_made = [
            copies.start(hidden_ref.at[part], land.at[far_row_here, part], at.far)
            for far_row_here in (2,)
            for part in parts
        ]
        mix_side = copies.start(mix_ref, mix_land.at[dp], at.across)
        launch(FC)
        fc_sides = [
            copies.start(fc_ref, fc_side.at[spot], at.across),
            copies.start(fc_ref, fc_far.at[spot], at.far),
        ]
        mate_made = copies.start(hidden_ref, land.at[1], at.mate)
        cot_made = copies.start(cot_ref, cot_out.at[1], at.mate)
        stay(cot_ref, cot_out.at[0])
        stay(fc_ref, fc_near.at[spot])
        stay(proj_ref, proj_near.at[spot])
        mix_land[dp] = mix_ref[...]
        for copy in vec_made:
            copy.wait_recv()
        merged = jnp.zeros((VEC_ROWS, 128), F32)
        bias_rows = jnp.zeros((VEC_ROWS, 128), F32)
        row_ids = lax.broadcasted_iota(jnp.int32, (VEC_ROWS, 128), 0)
        for i, index in enumerate((tensor, mate_row, far_row, corner_row)):
            tile = vec_ref[...] if i == 0 else tile_land[i - 1]
            merged += nn(tile, one_hot(128, 128, index * share, share))
            bias_rows = jnp.where(row_ids == 8 + index, tile[8:9].astype(F32), bias_rows)
        tiles[dp] = jnp.where(row_ids < 8, merged, bias_rows).astype(LOW)
        launch(VEC)
        vec_side = copies.start(tiles.at[dp], tiles.at[dp], at.across)

        def norm_rows(source, index):
            @pl.loop(0, rows // 128)
            def _(i):
                span = pl.ds(pl.multiple_of(i * 128, 128), 128)
                normed[index, span] = normalize(source[span].astype(F32))[0].astype(LOW)

            stay(normed.at[index], normed_out.at[index])

        def relay(i):
            far_made[i].wait_recv()
            return copies.start(land.at[2, parts[i]], land.at[3, parts[i]], at.mate)

        def mix_rows(index):
            @pl.loop(0, rows // 256)
            def _(i):
                span = pl.ds(pl.multiple_of(i * 256, 256), 256)
                turned = normed[index, span].astype(F32) * whole[0:1] + whole[1:2]
                weight = mix_land[...].reshape(width, width)
                mixed[index, span] = (nn(turned.astype(LOW), weight) + bias).astype(LOW)

            stay(mixed.at[index], mixed_out.at[index])

        norm_rows(hidden_ref, tensor)
        relayed = []
        for step in range(hops + 2):
            for item, hop in ((MIX, step), (VEC, step), (FC, step - 1), (PROJ, step - 2)):
                if 0 <= hop < hops:
                    handle(item, hop)
            if step == 0:
                launch(PROJ)
                mate_made.wait_recv()
                norm_rows(land.at[1], mate_row)
                relayed.append(relay(0))
            if step == 1:
                relayed.append(relay(1))
                norm_rows(land.at[2], far_row)
            if step == hops - 1:
                for copy in relayed:
                    copy.wait_recv()
                norm_rows(land.at[3], corner_row)
            if step == hops:
                mix_side.wait_recv()
                vec_side.wait_recv()
                settle(MIX)
                settle(VEC)
                whole = jnp.zeros((VEC_ROWS, width), F32)
                for i in range(n_dp):
                    whole += nn(tiles[i], one_hot(128, width, i * shard, shard))
                vec_out[...] = whole
                lane = lax.broadcasted_iota(jnp.int32, (width, WIDE), 0)
                column = lax.broadcasted_iota(jnp.int32, (width, WIDE), 1)
                pick = (lane == column + tensor * (NH * HD)) & (column < NH * HD)
                picked = nn(whole.astype(LOW), pick.astype(LOW))
                bias = jnp.concatenate(
                    [picked[2:3], jnp.zeros((1, WIDE), F32), picked[3:4]], axis=1
                )
                mix_rows(tensor)
                mix_rows(mate_row)
        mix_rows(far_row)
        mix_rows(corner_row)
        stay(mix_land, mix_out)
        weight = mix_land[...].reshape(width, width)
        for part in range(3):
            low = part * WIDE + WIDE - 128
            turned = weight[:, low : low + 128].T
            out_turned[part * HD : (part + 1) * HD] = turned[128 - HD :]
        stay(out_turned, out_out)
        settle(FC)
        for copy in fc_sides:
            copy.wait_recv()
        cot_made.wait_recv()
        copies.finish()
        for copy in stays:
            copy.wait()

    low = lambda *shape: jax.ShapeDtypeStruct(shape, LOW)
    outputs = (
        low(4, rows, width), low(4, rows, width), low(n_dp, shard, width),
        low(line, shard, width), low(line, shard, width), low(line, shard, width),
        low(line, shard, width), low(2, rows, width), low(NH * HD, width),
        jax.ShapeDtypeStruct((VEC_ROWS, width), F32),
    )
    scratch = [
        pltpu.VMEM((4, rows, width), LOW),
        pltpu.VMEM((n_dp, shard, width), LOW),
        pltpu.VMEM((n_dp, VEC_ROWS, 128), LOW),
        pltpu.VMEM((3, VEC_ROWS, 128), LOW),
        pltpu.VMEM((4, rows, width), LOW),
        pltpu.VMEM((4, rows, width), LOW),
        pltpu.VMEM((NH * HD, width), LOW),
    ]
    return comm_call(
        kernel,
        "gather_inputs",
        outputs,
        (hidden, cotangent, fc, proj, mix, vectors),
        [VM] * 6,
        tuple([ANY] * (len(outputs) - 1)) + (VM,),
        3 + 2 + 1 + 2 + 2 + 1 + 2 + hops * (2 * 4 + 2 * 4),
        0,
        scratch=scratch,
        local=3 + 8 + 2,
    )


def mate_rows(rows_here, n_dp, cid):
    def kernel(in_ref, out_ref, send, recv, local):
        at = Place(n_dp // 2)
        greet([(at.mate, None)])
        copies = Copies(send, recv)
        copy = copies.start(in_ref, out_ref.at[1], at.mate)
        stay = pltpu.make_async_copy(in_ref, out_ref.at[0], local.at[0])
        stay.start()
        stay.wait()
        copy.wait()

    return comm_call(
        kernel,
        f"mate_rows_{cid}",
        jax.ShapeDtypeStruct((2,) + rows_here.shape, rows_here.dtype),
        (rows_here,),
        [VM],
        ANY,
        1,
        cid,
    )


def mate_sum_part(parts, n_dp, cid):
    def kernel(in_ref, out_ref, send, recv, local):
        at = Place(n_dp // 2)
        greet([(at.mate, None)])
        copies = Copies(send, recv)
        copies.start(in_ref.at[1], out_ref, at.mate).wait()

    return comm_call(
        kernel,
        f"mate_sum_part_{cid}",
        jax.ShapeDtypeStruct(parts.shape[1:], parts.dtype),
        (parts,),
        [ANY],
        ANY,
        1,
        cid,
    )


def heads_to_rows(attended, n_dp, cid):
    head_rows_here, slots = attended.shape
    block = slots // 4

    def kernel(in_ref, out_ref, send, recv, local):
        at = Place(n_dp // 2)
        greet([(at.far, None)])
        copies = Copies(send, recv)
        made, stays = [], []
        for i in range(2):
            core = at.core if i == 0 else 1 - at.core
            theirs = ((1 - at.chip) * 2 + core) * block
            ours = (at.chip * 2 + core) * block
            made.append(
                copies.start(
                    in_ref.at[:, pl.ds(pl.multiple_of(theirs, block), block)],
                    out_ref.at[1, :, i * block : (i + 1) * block],
                    at.far,
                )
            )
            stays.append(
                pltpu.make_async_copy(
                    in_ref.at[:, pl.ds(pl.multiple_of(ours, block), block)],
                    out_ref.at[0, :, i * block : (i + 1) * block],
                    local.at[i],
                )
            )
            stays[-1].start()
        for copy in stays + made:
            copy.wait()

    return comm_call(
        kernel,
        "heads_to_rows",
        jax.ShapeDtypeStruct((2, head_rows_here, slots // 2), attended.dtype),
        (attended,),
        [VM],
        ANY,
        2,
        cid,
        local=2,
    )


def rows_to_heads(grads, n_dp, cid):
    _, head_rows_here, slots = grads.shape
    block = slots // 2

    def kernel(in_ref, out_ref, send, recv, local):
        at = Place(n_dp // 2)
        greet([(at.far, None)])
        copies = Copies(send, recv)
        made, stays = [], []
        for i in range(2):
            core = at.core if i == 0 else 1 - at.core
            ours = pl.ds(pl.multiple_of((at.chip * 2 + core) * block, block), block)
            made.append(
                copies.start(
                    in_ref.at[1, :, i * block : (i + 1) * block], out_ref.at[:, ours], at.far
                )
            )
            stays.append(
                pltpu.make_async_copy(
                    in_ref.at[0, :, i * block : (i + 1) * block], out_ref.at[:, ours], local.at[i]
                )
            )
            stays[-1].start()
        for copy in stays + made:
            copy.wait()

    return comm_call(
        kernel,
        "rows_to_heads",
        jax.ShapeDtypeStruct((head_rows_here, 2 * slots), grads.dtype),
        (grads,),
        [VM],
        ANY,
        2,
        cid,
        local=2,
    )


def reduce_grads(weight_grads, row_parts, vector_parts, n_dp, cid):
    line = n_dp // 2
    count = len(weight_grads)
    shard, width = weight_grads[0].shape[1:]
    rows = row_parts.shape[1]
    half_rows = rows // 2
    grads = [g.reshape(line, 2, shard, width) for g in weight_grads]
    vectors = vector_parts.reshape(4, line, 2, VEC_ROWS, 128)
    slots = [(distance, way) for distance in range(line - 1, 0, -1) for way in (0, 1)] + [(0, 0)]

    def kernel(*refs):
        refs = list(refs)

        def take(number):
            taken = refs[:number]
            del refs[:number]
            return taken

        grad = take(count)
        part, vec = take(2)
        out = take(count)
        part_out, vec_out = take(2)
        side_land, hop_send, hop_land = take(count + 1), take(count + 1), take(count + 1)
        mate_land, far_send, far_land, vec_land, vec_sum, send, recv, local = refs
        grad.append(vec_sum)
        out.append(vec_out)
        at = Place(line)
        tensor, spot, side = at.tensor, at.spot, at.side
        greet(at.everyone())
        copies = Copies(send, recv)
        mate_row, far_row, corner_row = at.mate[1], at.far[1], at.corner[1]

        def block_of(slot):
            distance, way = slots[slot]
            if way == 0:
                return jnp.minimum(spot + distance, line - 1), spot + distance < line
            return jnp.maximum(spot - distance, 0), spot - distance >= 0

        sides, hops = [], []
        for slot in range(len(slots)):
            block, inside = block_of(slot)
            way = slots[slot][1]
            sides.append(
                [
                    copies.plan(grad[i].at[block, 1 - side], side_land[i].at[slot], at.across)
                    for i in range(count + 1)
                ]
            )
            if slots[slot][0] > 0:
                hops.append(
                    [
                        copies.plan(
                            hop_send[i].at[slot], hop_land[i].at[slot], (at.up, at.down)[way]
                        )
                        for i in range(count + 1)
                    ]
                )

        mate_far = copies.start(part.at[corner_row], mate_land.at[1], at.mate)
        vec_made = [
            copies.start(vec.at[row], vec_land.at[i], device)
            for i, (device, row) in enumerate(
                ((at.mate, mate_row), (at.far, far_row), (at.corner, corner_row))
            )
        ]

        def cross(distance, items):
            for slot in range(len(slots)):
                if slots[slot][0] == distance:
                    for i in items:
                        copies.begin(sides[slot][i], block_of(slot)[1])

        cross(line - 1, range(count))
        cross(line - 2, range(count))
        mate_own = copies.start(part.at[mate_row], mate_land.at[0], at.mate)
        mate_far.wait_recv()
        far_made = []
        for i in range(2):
            span = pl.ds(i * half_rows, half_rows)
            far_send[span] = (
                mate_land[1, span].astype(F32) + part[far_row, span].astype(F32)
            ).astype(LOW)
            far_made.append(copies.start(far_send.at[span], far_land.at[span], at.far))
        for copy in vec_made:
            copy.wait_recv()
        vec_sum[...] = vec[tensor] + vec_land[0] + vec_land[1] + vec_land[2]
        cross(line - 1, [count])
        cross(line - 2, [count])

        def handle(slot, i):
            block, inside = block_of(slot)
            way = slots[slot][1]
            behind = (at.has_down, at.has_up)[way]
            outer = slot - 2

            def work():
                sides[slot][i].wait_recv()
                total = grad[i][block, side].astype(F32) + side_land[i][slot].astype(F32)
                if outer < 0:
                    hop_send[i][slot] = total.astype(hop_send[i].dtype)
                    return

                @pl.when(behind)
                def _():
                    hops[outer][i].wait_recv()
                    hop_send[i][slot] = (total + hop_land[i][outer].astype(F32)).astype(
                        hop_send[i].dtype
                    )

                @pl.when(jnp.logical_not(behind))
                def _():
                    hop_send[i][slot] = total.astype(hop_send[i].dtype)

            when(inside, work)
            copies.begin(hops[slot][i], inside)

        for slot in range(len(slots) - 1):
            for i in range(count + 1):
                handle(slot, i)
            if slots[slot][1] == 1 and slots[slot][0] >= 2:
                cross(slots[slot][0] - 2, range(count + 1))
        mate_own.wait_recv()
        for i in range(2):
            span = pl.ds(i * half_rows, half_rows)
            far_made[i].wait_recv()
            part_out[span] = (
                part[tensor, span].astype(F32)
                + mate_land[0, span].astype(F32)
                + far_land[span].astype(F32)
            )
        last = len(slots) - 1
        for i in range(count + 1):
            sides[last][i].wait_recv()
            out[i][...] = grad[i][spot, side].astype(F32) + side_land[i][last].astype(F32)
            for way, behind in enumerate((at.has_down, at.has_up)):

                def add(way=way, i=i):
                    hops[last - 2 + way][i].wait_recv()
                    out[i][...] += hop_land[i][last - 2 + way].astype(F32)

                when(behind, add)
        copies.finish()

    outputs = (
        (jax.ShapeDtypeStruct((shard, width), F32),) * count
        + (
            jax.ShapeDtypeStruct((rows, width), F32),
            jax.ShapeDtypeStruct((VEC_ROWS, 128), F32),
        )
    )
    moved = len(slots) - 1
    scratch = []
    for number in (moved + 1, moved, moved):
        scratch += [pltpu.VMEM((number, shard, width), LOW)] * count
        scratch.append(pltpu.VMEM((number, VEC_ROWS, 128), F32))
    scratch += [
        pltpu.VMEM((2, rows, width), LOW),
        pltpu.VMEM((rows, width), LOW),
        pltpu.VMEM((rows, width), LOW),
        pltpu.VMEM((3, line, 2, VEC_ROWS, 128), F32),
        pltpu.VMEM((line, 2, VEC_ROWS, 128), F32),
    ]
    copy_count = 2 + 3 + 2 + (2 * moved + 1) * (count + 1)
    return comm_call(
        kernel,
        "reduce_grads",
        outputs,
        (*grads, row_parts, vectors),
        [VM] * (count + 2),
        (VM,) * len(outputs),
        copy_count,
        cid,
        scratch=scratch,
    )


def unit_kernel(add, line, live_ref, *refs):
    refs = list(refs)
    rows_ref, grad_in = refs[:2]
    pieces, bias_ref = refs[2:6], refs[6]
    refs = refs[7:]
    if add:
        last_in, two_in = refs[:2]
        refs = refs[2:]
    last_ref, two_ref, fc_grad_ref, proj_grad_ref, bias_grad_ref = refs[:5]
    fc_all, proj_all, fc_sum, proj_sum = refs[5:]
    step = pl.program_id(0)
    side, tensor, live = live_ref[0], live_ref[1], live_ref[2]

    @pl.when(step == 0)
    def _():
        for full, near, across in ((fc_all, *pieces[:2]), (proj_all, *pieces[2:])):
            for i in range(line):
                full[2 * i + side] = near[i]
                full[2 * i + 1 - side] = across[i]
        fc_sum[...] = jnp.zeros_like(fc_sum)
        proj_sum[...] = jnp.zeros_like(proj_sum)
        bias_grad_ref[...] = jnp.zeros_like(bias_grad_ref)

    count, width = rows_ref.shape
    half = pl.num_programs(0) // 2
    block = jnp.where(step < half, tensor, tensor + 1 - 2 * (tensor % 2))
    first = block * (half * count) + (step % half) * count
    alive = first + lax.broadcasted_iota(jnp.int32, (count, 1), 0) < live
    rows = rows_ref[...]
    grad = jnp.where(alive, grad_in[...], jnp.zeros_like(grad_in))
    fc = fc_all[...].reshape(width, -1)
    proj = proj_all[...].reshape(width, -1)
    inner = nn(rows, fc) + bias_ref[...]
    square = inner * inner
    bend = jnp.tanh(GELU_SCALE * inner * (1.0 + GELU_CUBE * square))
    half = 0.5 * (1.0 + bend)
    activated = (inner * half).astype(LOW)
    slope = half + 0.5 * inner * (1.0 - bend * bend) * GELU_SCALE * (1.0 + 3.0 * GELU_CUBE * square)
    grad_inner = (nn(grad, proj) * slope).astype(LOW)
    last = nt(activated, proj)
    two = nt(grad_inner, fc)
    if add:
        last, two = last + last_in[...], two + two_in[...]
    last_ref[...] = last.astype(last_ref.dtype)
    two_ref[...] = two.astype(two_ref.dtype)
    fc_sum[...] += tn(rows, grad_inner)
    proj_sum[...] += tn(grad, activated)
    bias_grad_ref[...] += jnp.sum(grad_inner.astype(F32), axis=0, keepdims=True)

    @pl.when(step == pl.num_programs(0) - 1)
    def _():
        fc_grad_ref[...] = fc_sum[...].astype(fc_grad_ref.dtype)
        proj_grad_ref[...] = proj_sum[...].astype(proj_grad_ref.dtype)


def units_both_ways(scalars, rows, grad, pieces, bias, before, grad_type):
    count, width = rows.shape
    line, shard, units = pieces[0].shape
    tile = pl.BlockSpec((ROW_TILE, width), lambda i: (i, 0))
    fixed = lambda shape: pl.BlockSpec(shape, lambda i: (0,) * len(shape))
    add = before is not None
    kind = LOW if add else F32
    return pl.pallas_call(
        functools.partial(unit_kernel, add, line),
        grid=(count // ROW_TILE,),
        out_shape=(
            jax.ShapeDtypeStruct((count, width), kind),
            jax.ShapeDtypeStruct((count, width), kind),
            jax.ShapeDtypeStruct((width, units), grad_type),
            jax.ShapeDtypeStruct((width, units), grad_type),
            jax.ShapeDtypeStruct((1, units), F32),
        ),
        in_specs=[pl.BlockSpec(memory_space=pltpu.SMEM), tile, tile]
        + [fixed((line, shard, units))] * 4
        + [fixed((1, units))]
        + [tile] * (2 if add else 0),
        out_specs=(tile, tile, fixed((width, units)), fixed((width, units)), fixed((1, units))),
        scratch_shapes=[pltpu.VMEM((2 * line, shard, units), LOW)] * 2
        + [pltpu.VMEM((width, units), F32)] * 2,
        compiler_params=pltpu.CompilerParams(
            dimension_semantics=("arbitrary",), vmem_limit_bytes=56 << 20
        ),
        cost_estimate=pl.CostEstimate(
            flops=12 * count * width * units,
            bytes_accessed=24 * count * width,
            transcendentals=count * units,
        ),
        name="units_far" if add else "units_own",
    )(scalars, rows, grad, *pieces, bias, *(before or ()))


def normalize(values):
    center = jnp.mean(values, axis=-1, keepdims=True)
    offset = values - center
    spread = jnp.mean(offset * offset, axis=-1, keepdims=True)
    inverse = lax.rsqrt(spread + EPSILON)
    return offset * inverse, inverse


def norm_back(normed, inverse, grad, gain):
    scaled = grad * gain
    center = jnp.mean(scaled, axis=-1, keepdims=True)
    along = jnp.mean(scaled * normed, axis=-1, keepdims=True)
    return inverse * (scaled - center - normed * along)


def product(equation, left, right):
    return jnp.einsum(equation, left, right, preferred_element_type=F32)


def pack_three(qkv, out_turned):
    depth = qkv.shape[0]
    parts = jnp.transpose(qkv.reshape(depth, NH, 3, HD), (0, 2, 1, 3))
    extra = out_turned.reshape(depth, 3, 1, HD)
    return jnp.concatenate([parts, extra], axis=2).reshape(depth, 3 * WIDE)


def unpack_three(packed):
    depth = packed.shape[0]
    split = packed.reshape(depth, 3, NH + 1, HD)
    qkv = jnp.transpose(split[:, :, :NH], (0, 2, 1, 3)).reshape(depth, 3 * NH * HD)
    return qkv, split[:, :, NH].reshape(depth, NH * HD)


def per_device(
    tokens,
    thoughts,
    positions,
    lengths,
    attn_norm_gain,
    attn_norm_shift,
    qkv_weight,
    qv_bias,
    attn_out_weight,
    attn_out_bias,
    mlp_norm_gain,
    mlp_norm_shift,
    fc_weight,
    fc_bias,
    proj_weight,
    proj_bias,
    cotangent,
):
    n_dp = lax.axis_size("dp")
    n_tensor = lax.axis_size("tensor")
    tensor = lax.axis_index("tensor")
    rows, width = tokens.shape
    slots = rows * n_tensor
    head_width = NH * HD
    units = FF // n_tensor
    far = (tensor + 2) % n_tensor
    swap_far = [(i, (i + 2) % n_tensor) for i in range(n_tensor)]

    window = rows // thoughts.shape[0]
    starts = jnp.arange(thoughts.shape[0], dtype=jnp.int32) * window
    placed = (
        jnp.arange(window, dtype=jnp.int32)[None, :] == (positions - starts)[:, None]
    )[:, :, None]
    tokens_low = jnp.where(
        placed, thoughts[:, None, :], tokens.reshape(-1, window, width)
    ).reshape(rows, width)

    ends = [lengths[0, 0]]
    for i in range(1, SEQ_DEV):
        ends.append(ends[-1] + lengths[0, i])
    segment_ends = jnp.stack(ends)
    live_slots = ends[-1]
    own_slots = tensor * rows + jnp.arange(rows, dtype=jnp.int32)
    live = (own_slots < live_slots)[:, None]

    share = width // (n_dp * n_tensor)
    small = [
        attn_norm_gain, attn_norm_shift, qv_bias[0], qv_bias[1], attn_out_bias,
        mlp_norm_gain, mlp_norm_shift, proj_bias, fc_bias,
    ]
    vectors = jnp.concatenate([jnp.pad(v[None], ((0, 0), (0, 128 - v.shape[0]))) for v in small])
    vectors = jnp.pad(vectors, ((0, VEC_ROWS - len(small)), (0, 0)))

    (
        group_low, mixed, mix_all, fc_near, fc_side, fc_far_near, proj_near, grad_rows, out_own,
        vec_all,
    ) = gather_inputs(
        tokens_low, cotangent, fc_weight, proj_weight.T,
        pack_three(qkv_weight, attn_out_weight.T), vectors, n_dp,
    )
    mix_own = mix_all.reshape(width, -1)
    group_low = group_low.reshape(slots, width)
    mixed = mixed.reshape(slots, -1)
    swap_side = [(i, i + 1 - 2 * (i % 2)) for i in range(n_dp)]
    out_far = lax.ppermute(out_own, "tensor", swap_far)
    proj_far_near = lax.ppermute(proj_near, "tensor", swap_far)
    fc_far_side = lax.ppermute(fc_far_near, "dp", swap_side)
    proj_side = lax.ppermute(proj_near, "dp", swap_side)
    gain_one, shift_one, out_bias, gain_two, shift_two, last_bias = [
        vec_all[i] for i in (0, 1, 4, 5, 6, 7)
    ]
    hidden_bias = jnp.transpose(
        vec_all[8 : 8 + n_tensor].reshape(n_tensor, n_dp, -1), (1, 0, 2)
    ).reshape(n_tensor, units)

    attended, stats = attend(segment_ends, mixed)
    sent, out_far, proj_far_near = lax.optimization_barrier((attended, out_far, proj_far_near))
    both = heads_to_rows(sent, n_dp, 1)
    proj_far_side = lax.ppermute(proj_far_near, "dp", swap_side)
    mid_part = product("et,ed->td", both[0], out_own) + product("et,ed->td", both[1], out_far)
    mid_low = mid_part.astype(LOW).reshape(2, rows, width)
    mid_mate = mate_sum_part(mid_low, n_dp, 2)
    hidden = tokens_low.astype(F32)
    middle = hidden + mid_low[0].astype(F32) + mid_mate.astype(F32) + out_bias
    normed_mid, inverse_mid = normalize(middle)
    normed_two = (normed_mid * gain_two + shift_two).astype(LOW)
    chip_two = mate_rows(normed_two, n_dp, 3).reshape(2 * rows, width)
    chip_grad = grad_rows.reshape(2 * rows, width)

    def bias_row(index):
        return lax.dynamic_slice_in_dim(hidden_bias, index, 1, 0)

    scalars = jnp.stack([lax.axis_index("dp") % 2, tensor, live_slots]).astype(jnp.int32)
    last_own, two_own, grad_fc, grad_proj, grad_fc_bias = units_both_ways(
        scalars, chip_two, chip_grad, (fc_near, fc_side, proj_near, proj_side), bias_row(tensor),
        None, F32,
    )
    last_part, grad_two_part, far_fc, far_proj, far_fc_bias = units_both_ways(
        scalars, chip_two, chip_grad,
        (fc_far_near, fc_far_side, proj_far_near, proj_far_side), bias_row(far),
        (last_own, two_own), LOW,
    )
    grad_fc_bias, far_fc_bias = grad_fc_bias[0], far_fc_bias[0]
    split = width // 2
    proj_head = lax.ppermute(far_proj[:split], "tensor", swap_far)
    two_low = grad_two_part.reshape(2, rows, width)
    two_mate = mate_sum_part(two_low, n_dp, 4)
    grad_two = two_low[0].astype(F32) + two_mate.astype(F32)
    grad_final = jnp.where(live, cotangent, jnp.zeros_like(cotangent)).astype(F32)
    grad_middle = grad_final + norm_back(normed_mid, inverse_mid, grad_two, gain_two)
    grad_gain_two = jnp.sum(normed_mid * grad_two, axis=0)
    grad_shift_two = jnp.sum(grad_two, axis=0)
    chip_mid = mate_rows(grad_middle.astype(LOW), n_dp, 5).reshape(2 * rows, width)
    grad_attended = jnp.stack(
        [product("ed,td->et", w, chip_mid).astype(LOW) for w in (out_own, out_far)]
    )
    grad_out, far_out = [product("td,et->de", chip_mid, both[i]) for i in range(2)]
    grad_attended, proj_head = lax.optimization_barrier((grad_attended, proj_head))
    grad_heads = rows_to_heads(grad_attended, n_dp, 6)
    grad_heads, rest, far_fc, far_out = lax.optimization_barrier(
        (grad_heads, far_proj[split:], far_fc, far_out.astype(LOW))
    )
    proj_tail = lax.ppermute(rest, "tensor", swap_far)
    far_fc = lax.ppermute(far_fc, "tensor", swap_far)
    far_out = lax.ppermute(far_out, "tensor", swap_far)
    last_low = last_part.reshape(2, rows, width)
    last_mate = mate_sum_part(last_low, n_dp, 7)
    final = middle + last_low[0].astype(F32) + last_mate.astype(F32) + last_bias
    block_out = jnp.where(live, final, 0.0).astype(LOW)

    grad_mixed = attend_back(segment_ends, mixed, attended, stats, grad_heads)
    grad_mixed, proj_tail = lax.optimization_barrier((grad_mixed, proj_tail))
    one_part = product("tc,dc->td", grad_mixed, mix_own)
    mix_sums = jnp.sum(grad_mixed, axis=0, dtype=F32)
    plain_mix = product("td,tc->dc", group_low, grad_mixed)
    grad_mix = plain_mix * gain_one[:, None] + shift_one[:, None] * mix_sums
    grad_gain_one = jnp.sum(plain_mix * mix_own.astype(F32), axis=1)
    grad_shift_one = jnp.sum(mix_own.astype(F32) * mix_sums, axis=1)
    out_total = (grad_out + far_out.astype(F32)).reshape(width, 3, 1, HD)
    mix_total = grad_mix + jnp.pad(out_total, ((0, 0), (0, 0), (NH, 0), (0, 0))).reshape(
        width, 3 * WIDE
    )
    totals = [
        (grad_fc + far_fc.astype(F32)).astype(LOW),
        (grad_proj + jnp.concatenate([proj_head, proj_tail]).astype(F32)).astype(LOW),
        mix_total.astype(LOW),
    ]

    def spread(vector, index, size, length):
        return lax.dynamic_update_slice_in_dim(jnp.zeros((length,), F32), vector, index * size, 0)

    def tiles(vector):
        cut = vector.reshape(n_dp, n_tensor, -1)
        return jnp.pad(cut, ((0, 0), (0, 0), (0, 128 - cut.shape[2])))

    fc_bias_part = lax.dynamic_update_slice_in_dim(
        spread(grad_fc_bias, tensor, units, FF), far_fc_bias, far * units, 0
    )
    vector_rows = [
        grad_gain_one, grad_shift_one,
        spread(mix_sums[:head_width], tensor, head_width, width),
        spread(mix_sums[2 * WIDE : 2 * WIDE + head_width], tensor, head_width, width),
        jnp.sum(grad_middle, axis=0), grad_gain_two, grad_shift_two,
        jnp.sum(grad_final, axis=0), fc_bias_part,
    ]
    vector_parts = jnp.stack([tiles(v) for v in vector_rows], axis=2)
    vector_parts = jnp.pad(
        vector_parts, ((0, 0), (0, 0), (0, VEC_ROWS - len(vector_rows)), (0, 0))
    )
    vector_parts = jnp.transpose(vector_parts, (1, 0, 2, 3))
    reduced = reduce_grads(
        [g.reshape(n_dp, -1, width) for g in totals],
        one_part.astype(LOW).reshape(n_tensor, rows, width),
        vector_parts,
        n_dp,
        8,
    )
    fc_grad, proj_grad, mix_grad, grad_one, vec = reduced
    qkv_grad, out_grad = unpack_three(mix_grad)
    normed_hid, inverse_hid = normalize(hidden)
    grad_hidden = grad_middle + norm_back(normed_hid, inverse_hid, grad_one, gain_one)
    windows = grad_hidden.reshape(-1, window, width)
    grad_thoughts = jnp.sum(jnp.where(placed, windows, 0.0), axis=1)
    grad_tokens = jnp.where(placed, 0.0, windows).reshape(rows, width)
    return (
        block_out,
        grad_tokens,
        grad_thoughts,
        vec[0, :share],
        vec[1, :share],
        qkv_grad,
        vec[2:4, :share],
        out_grad.T,
        vec[4, :share],
        vec[5, :share],
        vec[6, :share],
        fc_grad,
        vec[8, : fc_bias.shape[0]],
        proj_grad.T,
        vec[7, :share],
    )


def solution(mesh):
    rows = P(("dp", "tensor"), None)
    line = P(("dp", "tensor"))
    in_specs = (
        rows, rows, line, P("dp", None), line, line, P("dp", "tensor"),
        P(None, ("dp", "tensor")), P("tensor", "dp"), line, line, line,
        P("dp", "tensor"), line, P("tensor", "dp"), line, rows,
    )
    out_specs = (
        rows, rows, rows, line, line, P("dp", "tensor"), P(None, ("dp", "tensor")),
        P("tensor", "dp"), line, line, line, P("dp", "tensor"), line, P("tensor", "dp"), line,
    )
    return jax.shard_map(
        per_device, mesh=mesh, in_specs=in_specs, out_specs=out_specs, check_vma=False
    )
```

```python
import functools
import math

import jax
import jax.numpy as jnp
from jax import lax
from jax.experimental import pallas as pl
from jax.experimental.pallas import tpu as pltpu
from jax.sharding import PartitionSpec as P

H = 12
HD = 64
FF = 3072
SEQ_DEV = 3
EPSILON = 1e-05
MASKED = -1e30
NH = 3
SLABS = 2
WIDE = SLABS * 128
BQ = 512
BK = 512
VEC_ROWS = 16
ROW_TILE = 256
GELU_SCALE = math.sqrt(2.0 / math.pi)
GELU_CUBE = 0.044715
MESH = pl.DeviceIdType.MESH
ANY = pl.BlockSpec(memory_space=pl.ANY)
VM = pl.BlockSpec(memory_space=pltpu.VMEM)
LOW = jnp.bfloat16
F32 = jnp.float32


def nn(a, b):
    return lax.dot_general(a, b, (((1,), (0,)), ((), ())), preferred_element_type=jnp.float32)


def nt(a, b):
    return lax.dot_general(a, b, (((1,), (1,)), ((), ())), preferred_element_type=jnp.float32)


def tn(a, b):
    return lax.dot_general(a, b, (((0,), (0,)), ((), ())), preferred_element_type=jnp.float32)


def head_rows(slab, head):
    half = slab[(head % 2) * HD : (head % 2 + 1) * HD]
    zero = jnp.zeros_like(half)
    return jnp.concatenate([half, zero] if head % 2 == 0 else [zero, half], axis=0)


def segment_start(ends_ref, slots):
    start = jnp.zeros_like(slots)
    for i in range(SEQ_DEV):
        start = jnp.where(slots >= ends_ref[i], ends_ref[i], start)
    return start


def segment_stop(ends_ref, slot, slots):
    stop = slots
    for i in reversed(range(SEQ_DEV)):
        stop = jnp.where(slot < ends_ref[i], ends_ref[i], stop)
    return stop


def attend_kernel(ends_ref, mixed_ref, out_ref, stat_ref, qt_ref, vt_ref):
    tokens = mixed_ref.shape[0]
    for first in range(0, tokens, BQ):
        rows = pl.ds(first, BQ)
        for slab in range(SLABS):
            lanes = slab * 128
            qt_ref[lanes : lanes + 128, rows] = (
                mixed_ref[rows, lanes : lanes + 128] * HD ** (-0.5)
            ).T
            vt_ref[lanes : lanes + 128, rows] = mixed_ref[
                rows, 2 * WIDE + lanes : 2 * WIDE + lanes + 128
            ].T

    def query_block(block, carry):
        first = pl.multiple_of(block * BQ, BQ)
        columns = pl.ds(first, BQ)
        start = segment_start(ends_ref, first + lax.broadcasted_iota(jnp.int32, (1, BQ), 1))
        query_ids = first + lax.broadcasted_iota(jnp.int32, (BK, BQ), 1)
        queries = [
            head_rows(qt_ref[(h // 2) * 128 : (h // 2 + 1) * 128, columns], h) for h in range(NH)
        ]

        def key_block(key, state):
            base = pl.multiple_of(key * BK, BK)
            rows = pl.ds(base, BK)
            key_ids = base + lax.broadcasted_iota(jnp.int32, (BK, BQ), 0)
            allowed = (key_ids <= query_ids) & (key_ids >= start)
            result = []
            for h in range(NH):
                peak, total, acc = state[h]
                slab = h // 2
                scores = nn(mixed_ref[rows, WIDE + slab * 128 : WIDE + slab * 128 + 128], queries[h])
                scores = jnp.where(allowed, scores, MASKED)
                fresh = jnp.maximum(peak, jnp.max(scores, axis=0, keepdims=True))
                weight = jnp.exp(scores - fresh)
                decay = jnp.exp(peak - fresh)
                total = total * decay + jnp.sum(weight, axis=0, keepdims=True)
                values = vt_ref[h * HD : (h + 1) * HD, rows]
                acc = acc * decay + nn(values, weight.astype(jnp.bfloat16))
                result.append((fresh, total, acc))
            return tuple(result)

        empty = tuple(
            (
                jnp.full((1, BQ), MASKED, jnp.float32),
                jnp.zeros((1, BQ), jnp.float32),
                jnp.zeros((HD, BQ), jnp.float32),
            )
            for _ in range(NH)
        )
        state = lax.fori_loop(segment_start(ends_ref, first) // BK, (block + 1) * (BQ // BK), key_block, empty)
        for h in range(NH):
            peak, total, acc = state[h]
            out_ref[h * HD : (h + 1) * HD, columns] = (acc / total).astype(jnp.bfloat16)
            stat_ref[h : h + 1, columns] = peak + jnp.log(total)
        return carry

    lax.fori_loop(0, tokens // BQ, query_block, 0)


def attend(ends, mixed):
    tokens = mixed.shape[0]
    vm = pl.BlockSpec(memory_space=pltpu.VMEM)
    return pl.pallas_call(
        attend_kernel,
        out_shape=(
            jax.ShapeDtypeStruct((NH * HD, tokens), jnp.bfloat16),
            jax.ShapeDtypeStruct((8, tokens), jnp.float32),
        ),
        in_specs=[pl.BlockSpec(memory_space=pltpu.SMEM), vm],
        out_specs=(vm, vm),
        scratch_shapes=[pltpu.VMEM((WIDE, tokens), jnp.bfloat16)] * 2,
        compiler_params=pltpu.CompilerParams(vmem_limit_bytes=40 << 20),
        cost_estimate=pl.CostEstimate(
            flops=8 * tokens * tokens * NH * HD,
            bytes_accessed=16 * tokens * WIDE,
            transcendentals=tokens * tokens,
        ),
        name="attend",
    )(ends, mixed)


def attend_back_kernel(
    ends_ref, mixed_ref, out_ref, stat_ref, gradt_ref,
    gmixed_ref, qt_ref, kt_ref, grad_ref, delta_ref, dqt_ref
):
    tokens = mixed_ref.shape[0]
    for first in range(0, tokens, BQ):
        rows = pl.ds(first, BQ)
        for slab in range(SLABS):
            lanes = slab * 128
            qt_ref[lanes : lanes + 128, rows] = (
                mixed_ref[rows, lanes : lanes + 128] * HD ** (-0.5)
            ).T
            kt_ref[lanes : lanes + 128, rows] = mixed_ref[rows, WIDE + lanes : WIDE + lanes + 128].T
        grad_ref[rows, 0:128] = gradt_ref[0:128, rows].T
        grad_ref[rows, 128:256] = jnp.concatenate(
            [gradt_ref[128:192, rows], jnp.zeros((64, BQ), jnp.bfloat16)], axis=0
        ).T
        for h in range(NH):
            product = gradt_ref[h * HD : (h + 1) * HD, rows].astype(jnp.float32) * out_ref[
                h * HD : (h + 1) * HD, rows
            ].astype(jnp.float32)
            delta_ref[h : h + 1, rows] = jnp.sum(product, axis=0, keepdims=True)
    dqt_ref[...] = jnp.zeros_like(dqt_ref)
    lane = lax.broadcasted_iota(jnp.int32, (BQ, 128), 1)

    def key_block(key, carry):
        base = pl.multiple_of(key * BK, BK)
        rows = pl.ds(base, BK)
        key_ids = base + lax.broadcasted_iota(jnp.int32, (BK, BQ), 0)

        def query_block(block, state):
            first = pl.multiple_of(block * BQ, BQ)
            columns = pl.ds(first, BQ)
            start = segment_start(ends_ref, first + lax.broadcasted_iota(jnp.int32, (1, BQ), 1))
            query_ids = first + lax.broadcasted_iota(jnp.int32, (BK, BQ), 1)
            allowed = (key_ids <= query_ids) & (key_ids >= start)
            grad_keys = list(state[:SLABS])
            grad_values = list(state[SLABS:])
            for h in range(NH):
                slab = h // 2
                low, high = slab * 128, slab * 128 + 128
                queries = head_rows(qt_ref[low:high, columns], h)
                scores = nn(mixed_ref[rows, WIDE + low : WIDE + high], queries)
                probs = jnp.where(allowed, jnp.exp(scores - stat_ref[h : h + 1, columns]), 0.0)
                keep = (lane // HD) == (h % 2)
                grads = jnp.where(keep, grad_ref[columns, low:high], 0.0)
                grad_values[slab] += nn(probs.astype(jnp.bfloat16), grads)
                if h == NH - 1 and NH % 2 == 1:
                    grad_rows = jnp.concatenate(
                        [gradt_ref[h * HD : (h + 1) * HD, columns], jnp.zeros((HD, BQ), jnp.bfloat16)],
                        axis=0,
                    )
                else:
                    grad_rows = head_rows(gradt_ref[low:high, columns], h)
                grad_probs = nn(mixed_ref[rows, 2 * WIDE + low : 2 * WIDE + high], grad_rows)
                grad_scores = (probs * (grad_probs - delta_ref[h : h + 1, columns])).astype(
                    jnp.bfloat16
                )
                natural = mixed_ref[columns, low:high]
                grad_keys[slab] += nn(grad_scores, jnp.where(keep, natural, 0.0))
                dqt_ref[h * HD : (h + 1) * HD, columns] += nn(
                    kt_ref[h * HD : (h + 1) * HD, rows], grad_scores
                )
            return tuple(grad_keys) + tuple(grad_values)

        empty = (jnp.zeros((BK, 128), jnp.float32),) * (2 * SLABS)
        stop = segment_stop(ends_ref, base + BK - 1, tokens)
        state = lax.fori_loop(key * BK // BQ, (stop - 1) // BQ + 1, query_block, empty)
        for slab in range(SLABS):
            low = slab * 128
            gmixed_ref[rows, WIDE + low : WIDE + low + 128] = (
                state[slab] * HD ** (-0.5)
            ).astype(jnp.bfloat16)
            gmixed_ref[rows, 2 * WIDE + low : 2 * WIDE + low + 128] = state[SLABS + slab].astype(
                jnp.bfloat16
            )
        return carry

    lax.fori_loop(0, tokens // BK, key_block, 0)
    for first in range(0, tokens, BQ):
        rows = pl.ds(first, BQ)
        for slab in range(SLABS):
            low = slab * 128
            gmixed_ref[rows, low : low + 128] = (
                (dqt_ref[low : low + 128, rows] * HD ** (-0.5)).T.astype(jnp.bfloat16)
            )


def attend_back(ends, mixed, out, stat, gradt):
    tokens = mixed.shape[0]
    vm = pl.BlockSpec(memory_space=pltpu.VMEM)
    return pl.pallas_call(
        attend_back_kernel,
        out_shape=jax.ShapeDtypeStruct((tokens, 3 * WIDE), jnp.bfloat16),
        in_specs=[pl.BlockSpec(memory_space=pltpu.SMEM)] + [vm] * 4,
        out_specs=vm,
        scratch_shapes=[
            pltpu.VMEM((WIDE, tokens), jnp.bfloat16),
            pltpu.VMEM((WIDE, tokens), jnp.bfloat16),
            pltpu.VMEM((tokens, WIDE), jnp.bfloat16),
            pltpu.VMEM((8, tokens), jnp.float32),
            pltpu.VMEM((WIDE, tokens), jnp.float32),
        ],
        compiler_params=pltpu.CompilerParams(vmem_limit_bytes=50 << 20),
        cost_estimate=pl.CostEstimate(
            flops=20 * tokens * tokens * NH * HD,
            bytes_accessed=32 * tokens * WIDE,
            transcendentals=tokens * tokens,
        ),
        name="attend_back",
    )(ends, mixed, out, stat, gradt)


class Copies:
    def __init__(self, send, recv):
        self.send, self.recv, self.made, self.started = send, recv, 0, []

    def plan(self, source, target, device):
        index = self.made
        self.made += 1
        return pltpu.make_async_remote_copy(
            src_ref=source,
            dst_ref=target,
            send_sem=self.send.at[index],
            recv_sem=self.recv.at[index],
            device_id=device,
            device_id_type=MESH,
        )

    def begin(self, copy, condition=None):
        self.started.append((copy, condition))
        when(condition, copy.start)

    def start(self, source, target, device):
        copy = self.plan(source, target, device)
        self.begin(copy)
        return copy

    def finish(self):
        for copy, condition in self.started:
            when(condition, copy.wait_send)


def when(condition, action):
    if condition is None:
        action()
    else:
        pl.when(condition)(action)


def greet(devices):
    barrier = pltpu.get_barrier_semaphore()
    for device, condition in devices:
        when(
            condition,
            lambda device=device: pl.semaphore_signal(
                barrier, inc=1, device_id=device, device_id_type=MESH
            ),
        )
    present = [1 if condition is None else condition.astype(jnp.int32) for _, condition in devices]
    pl.semaphore_wait(barrier, sum(present))


class Place:
    def __init__(self, line):
        self.dp = dp = lax.axis_index("dp")
        self.tensor = tensor = lax.axis_index("tensor")
        self.spot, self.side = spot, side = dp // 2, dp % 2
        self.chip, self.core = tensor // 2, tensor % 2
        self.has_up, self.has_down = spot + 1 < line, spot > 0
        self.up = (jnp.minimum(spot + 1, line - 1) * 2 + side, tensor)
        self.down = (jnp.maximum(spot - 1, 0) * 2 + side, tensor)
        self.across = (spot * 2 + 1 - side, tensor)
        self.mate = (dp, tensor + 1 - 2 * (tensor % 2))
        self.far = (dp, (tensor + 2) % 4)
        self.corner = (dp, 3 - tensor)

    def everyone(self):
        return [
            (self.mate, None), (self.far, None), (self.corner, None), (self.across, None),
            (self.up, self.has_up), (self.down, self.has_down),
        ]


def comm_call(kernel, name, outputs, inputs, in_specs, out_specs, copies, cid, scratch=(), local=1, limit=50 << 20):
    return pl.pallas_call(
        kernel,
        out_shape=outputs,
        in_specs=in_specs,
        out_specs=out_specs,
        scratch_shapes=list(scratch)
        + [
            pltpu.SemaphoreType.DMA((copies,)),
            pltpu.SemaphoreType.DMA((copies,)),
            pltpu.SemaphoreType.DMA((local,)),
        ],
        compiler_params=pltpu.CompilerParams(
            collective_id=cid, has_side_effects=True, vmem_limit_bytes=limit
        ),
        name=name,
    )(*inputs)


def one_hot(rows, columns, shift, limit):
    lane = lax.broadcasted_iota(jnp.int32, (rows, columns), 0)
    spot = lax.broadcasted_iota(jnp.int32, (rows, columns), 1)
    return ((spot == lane + shift) & (lane < limit)).astype(LOW)


def gather_inputs(hidden, cotangent, fc, proj, mix, vectors, n_dp):
    line = n_dp // 2
    hops = line - 1
    rows, width = hidden.shape
    shard = fc.shape[0]
    half_rows = rows // 2
    share = width // (n_dp * 4)

    def kernel(
        hidden_ref, cot_ref, fc_ref, proj_ref, mix_ref, vec_ref,
        normed_out, mixed_out, mix_out, fc_near, fc_side, fc_far, proj_near, cot_out, out_out,
        vec_out,
        land, mix_land, tiles, tile_land, normed, mixed, out_turned, send, recv, local,
    ):
        at = Place(line)
        dp, tensor, spot, side = at.dp, at.tensor, at.spot, at.side
        mate_row, far_row, corner_row = at.mate[1], at.far[1], at.corner[1]
        greet(at.everyone())
        copies = Copies(send, recv)
        MIX, FC, PROJ, VEC = range(4)
        own = [mix_ref, fc_ref, proj_ref, tiles.at[dp]]

        def seat(item, position):
            if item == MIX:
                return mix_land.at[position * 2 + side]
            if item == FC:
                return fc_near.at[position]
            if item == PROJ:
                return proj_near.at[position]
            return tiles.at[position * 2 + side]

        def plan(item, hop):
            above, below = jnp.maximum(spot - hop, 0), jnp.minimum(spot + hop, line - 1)
            came_up = jnp.maximum(spot - 1 - hop, 0)
            came_down = jnp.minimum(spot + 1 + hop, line - 1)
            made = {
                "up": copies.plan(
                    own[item] if hop == 0 else seat(item, above), seat(item, above), at.up
                ),
                "down": copies.plan(
                    own[item] if hop == 0 else seat(item, below), seat(item, below), at.down
                ),
                "onward": [],
            }
            for position in (came_up, came_down):
                onward = []
                if item in (MIX, VEC):
                    onward.append(copies.plan(seat(item, position), seat(item, position), at.across))
                if item == FC:
                    onward.append(copies.plan(fc_near.at[position], fc_side.at[position], at.across))
                    onward.append(copies.plan(fc_near.at[position], fc_far.at[position], at.far))
                made["onward"].append(onward)
            return made

        plans = [[plan(item, hop) for hop in range(hops)] for item in range(4)]

        def launch(item):
            copies.begin(plans[item][0]["up"], at.has_up)
            copies.begin(plans[item][0]["down"], at.has_down)

        def handle(item, hop):
            made = plans[item][hop]
            for way, key, comes, goes in (
                (0, "up", spot - 1 - hop >= 0, at.has_up),
                (1, "down", spot + 1 + hop < line, at.has_down),
            ):
                when(comes, made[key].wait_recv)
                if hop + 1 < hops:
                    copies.begin(plans[item][hop + 1][key], comes & goes)
                for copy in made["onward"][way]:
                    copies.begin(copy, comes)

        def settle(item):
            for hop in range(hops):
                for way, comes in ((0, spot - 1 - hop >= 0), (1, spot + 1 + hop < line)):
                    for copy in plans[item][hop]["onward"][way]:
                        when(comes, copy.wait_recv)

        stays = []

        def stay(source, target):
            copy = pltpu.make_async_copy(source, target, local.at[len(stays)])
            copy.start()
            stays.append(copy)
            return copy

        vec_made = [
            copies.start(vec_ref, tile_land.at[i], device)
            for i, device in enumerate((at.mate, at.far, at.corner))
        ]
        parts = [pl.ds(0, half_rows), pl.ds(half_rows, half_rows)]
        launch(MIX)
        far_made = [
            copies.start(hidden_ref.at[part], land.at[far_row_here, part], at.far)
            for far_row_here in (2,)
            for part in parts
        ]
        mix_side = copies.start(mix_ref, mix_land.at[dp], at.across)
        launch(FC)
        fc_sides = [
            copies.start(fc_ref, fc_side.at[spot], at.across),
            copies.start(fc_ref, fc_far.at[spot], at.far),
        ]
        mate_made = copies.start(hidden_ref, land.at[1], at.mate)
        cot_made = copies.start(cot_ref, cot_out.at[1], at.mate)
        stay(cot_ref, cot_out.at[0])
        stay(fc_ref, fc_near.at[spot])
        stay(proj_ref, proj_near.at[spot])
        mix_land[dp] = mix_ref[...]
        for copy in vec_made:
            copy.wait_recv()
        merged = jnp.zeros((VEC_ROWS, 128), F32)
        bias_rows = jnp.zeros((VEC_ROWS, 128), F32)
        row_ids = lax.broadcasted_iota(jnp.int32, (VEC_ROWS, 128), 0)
        for i, index in enumerate((tensor, mate_row, far_row, corner_row)):
            tile = vec_ref[...] if i == 0 else tile_land[i - 1]
            merged += nn(tile, one_hot(128, 128, index * share, share))
            bias_rows = jnp.where(row_ids == 8 + index, tile[8:9].astype(F32), bias_rows)
        tiles[dp] = jnp.where(row_ids < 8, merged, bias_rows).astype(LOW)
        launch(VEC)
        vec_side = copies.start(tiles.at[dp], tiles.at[dp], at.across)

        def norm_rows(source, index):
            @pl.loop(0, rows // 128)
            def _(i):
                span = pl.ds(pl.multiple_of(i * 128, 128), 128)
                normed[index, span] = normalize(source[span].astype(F32))[0].astype(LOW)

            stay(normed.at[index], normed_out.at[index])

        def relay(i):
            far_made[i].wait_recv()
            return copies.start(land.at[2, parts[i]], land.at[3, parts[i]], at.mate)

        def mix_rows(index):
            @pl.loop(0, rows // 256)
            def _(i):
                span = pl.ds(pl.multiple_of(i * 256, 256), 256)
                turned = normed[index, span].astype(F32) * whole[0:1] + whole[1:2]
                weight = mix_land[...].reshape(width, width)
                mixed[index, span] = (nn(turned.astype(LOW), weight) + bias).astype(LOW)

            stay(mixed.at[index], mixed_out.at[index])

        norm_rows(hidden_ref, tensor)
        relayed = []
        for step in range(hops + 2):
            for item, hop in ((MIX, step), (VEC, step), (FC, step - 1), (PROJ, step - 2)):
                if 0 <= hop < hops:
                    handle(item, hop)
            if step == 0:
                launch(PROJ)
                mate_made.wait_recv()
                norm_rows(land.at[1], mate_row)
                relayed.append(relay(0))
            if step == 1:
                relayed.append(relay(1))
                norm_rows(land.at[2], far_row)
            if step == hops - 1:
                for copy in relayed:
                    copy.wait_recv()
                norm_rows(land.at[3], corner_row)
            if step == hops:
                mix_side.wait_recv()
                vec_side.wait_recv()
                settle(MIX)
                settle(VEC)
                whole = jnp.zeros((VEC_ROWS, width), F32)
                for i in range(n_dp):
                    whole += nn(tiles[i], one_hot(128, width, i * shard, shard))
                vec_out[...] = whole
                lane = lax.broadcasted_iota(jnp.int32, (width, WIDE), 0)
                column = lax.broadcasted_iota(jnp.int32, (width, WIDE), 1)
                pick = (lane == column + tensor * (NH * HD)) & (column < NH * HD)
                picked = nn(whole.astype(LOW), pick.astype(LOW))
                bias = jnp.concatenate(
                    [picked[2:3], jnp.zeros((1, WIDE), F32), picked[3:4]], axis=1
                )
                mix_rows(tensor)
                mix_rows(mate_row)
        mix_rows(far_row)
        mix_rows(corner_row)
        stay(mix_land, mix_out)
        weight = mix_land[...].reshape(width, width)
        for part in range(3):
            low = part * WIDE + WIDE - 128
            turned = weight[:, low : low + 128].T
            out_turned[part * HD : (part + 1) * HD] = turned[128 - HD :]
        stay(out_turned, out_out)
        settle(FC)
        for copy in fc_sides:
            copy.wait_recv()
        cot_made.wait_recv()
        copies.finish()
        for copy in stays:
            copy.wait()

    low = lambda *shape: jax.ShapeDtypeStruct(shape, LOW)
    outputs = (
        low(4, rows, width), low(4, rows, width), low(n_dp, shard, width),
        low(line, shard, width), low(line, shard, width), low(line, shard, width),
        low(line, shard, width), low(2, rows, width), low(NH * HD, width),
        jax.ShapeDtypeStruct((VEC_ROWS, width), F32),
    )
    scratch = [
        pltpu.VMEM((4, rows, width), LOW),
        pltpu.VMEM((n_dp, shard, width), LOW),
        pltpu.VMEM((n_dp, VEC_ROWS, 128), LOW),
        pltpu.VMEM((3, VEC_ROWS, 128), LOW),
        pltpu.VMEM((4, rows, width), LOW),
        pltpu.VMEM((4, rows, width), LOW),
        pltpu.VMEM((NH * HD, width), LOW),
    ]
    return comm_call(
        kernel,
        "gather_inputs",
        outputs,
        (hidden, cotangent, fc, proj, mix, vectors),
        [VM] * 6,
        tuple([ANY] * (len(outputs) - 1)) + (VM,),
        3 + 2 + 1 + 2 + 2 + 1 + 2 + hops * (2 * 4 + 2 * 4),
        0,
        scratch=scratch,
        local=3 + 8 + 2,
    )


def mate_rows(rows_here, n_dp, cid):
    def kernel(in_ref, out_ref, send, recv, local):
        at = Place(n_dp // 2)
        greet([(at.mate, None)])
        copies = Copies(send, recv)
        copy = copies.start(in_ref, out_ref.at[1], at.mate)
        stay = pltpu.make_async_copy(in_ref, out_ref.at[0], local.at[0])
        stay.start()
        stay.wait()
        copy.wait()

    return comm_call(
        kernel,
        f"mate_rows_{cid}",
        jax.ShapeDtypeStruct((2,) + rows_here.shape, rows_here.dtype),
        (rows_here,),
        [VM],
        ANY,
        1,
        cid,
    )


def mate_sum_part(parts, n_dp, cid):
    def kernel(in_ref, out_ref, send, recv, local):
        at = Place(n_dp // 2)
        greet([(at.mate, None)])
        copies = Copies(send, recv)
        copies.start(in_ref.at[1], out_ref, at.mate).wait()

    return comm_call(
        kernel,
        f"mate_sum_part_{cid}",
        jax.ShapeDtypeStruct(parts.shape[1:], parts.dtype),
        (parts,),
        [ANY],
        ANY,
        1,
        cid,
    )


def heads_to_rows(attended, n_dp, cid):
    head_rows_here, slots = attended.shape
    block = slots // 4

    def kernel(in_ref, out_ref, send, recv, local):
        at = Place(n_dp // 2)
        greet([(at.far, None)])
        copies = Copies(send, recv)
        made, stays = [], []
        for i in range(2):
            core = at.core if i == 0 else 1 - at.core
            theirs = ((1 - at.chip) * 2 + core) * block
            ours = (at.chip * 2 + core) * block
            made.append(
                copies.start(
                    in_ref.at[:, pl.ds(pl.multiple_of(theirs, block), block)],
                    out_ref.at[1, :, i * block : (i + 1) * block],
                    at.far,
                )
            )
            stays.append(
                pltpu.make_async_copy(
                    in_ref.at[:, pl.ds(pl.multiple_of(ours, block), block)],
                    out_ref.at[0, :, i * block : (i + 1) * block],
                    local.at[i],
                )
            )
            stays[-1].start()
        for copy in stays + made:
            copy.wait()

    return comm_call(
        kernel,
        "heads_to_rows",
        jax.ShapeDtypeStruct((2, head_rows_here, slots // 2), attended.dtype),
        (attended,),
        [VM],
        ANY,
        2,
        cid,
        local=2,
    )


def rows_to_heads(grads, n_dp, cid):
    _, head_rows_here, slots = grads.shape
    block = slots // 2

    def kernel(in_ref, out_ref, send, recv, local):
        at = Place(n_dp // 2)
        greet([(at.far, None)])
        copies = Copies(send, recv)
        made, stays = [], []
        for i in range(2):
            core = at.core if i == 0 else 1 - at.core
            ours = pl.ds(pl.multiple_of((at.chip * 2 + core) * block, block), block)
            made.append(
                copies.start(
                    in_ref.at[1, :, i * block : (i + 1) * block], out_ref.at[:, ours], at.far
                )
            )
            stays.append(
                pltpu.make_async_copy(
                    in_ref.at[0, :, i * block : (i + 1) * block], out_ref.at[:, ours], local.at[i]
                )
            )
            stays[-1].start()
        for copy in stays + made:
            copy.wait()

    return comm_call(
        kernel,
        "rows_to_heads",
        jax.ShapeDtypeStruct((head_rows_here, 2 * slots), grads.dtype),
        (grads,),
        [VM],
        ANY,
        2,
        cid,
        local=2,
    )


def finish_grads(scalars, arrays, n_dp, cid):
    names = list(arrays)
    line = n_dp // 2
    shard = arrays["mix"].shape[1]
    rows, width = arrays["hidden"].shape
    half_rows = rows // 2
    group = 4 * rows
    latents = arrays["positions"].shape[0]
    window = rows // latents
    far_end = line - 1
    slots = [(distance, way) for distance in range(far_end, 0, -1) for way in (0, 1)] + [(0, 0)]
    last = len(slots) - 1
    share = width // (n_dp * 4)
    FC, PROJ, MIX, VEC = range(4)

    def kernel(scalar_ref, *refs):
        refs = list(refs)

        def take(number):
            taken = refs[:number]
            del refs[:number]
            return taken

        source = dict(zip(names, take(len(names))))
        fc_out, proj_out, mix_out, vec_out, tokens_out, thoughts_out, block_out = take(7)
        held = dict(zip(names, take(len(names))))
        cross_send, cross_land = take(4), take(4)
        hop_send, hop_land = take(4), take(4)
        (
            part, mate_land, far_send, far_land, last_land, total, vec_mine, vec_land, vec_near,
            send, recv, local,
        ) = refs
        out = [fc_out, proj_out, mix_out, None]
        at = Place(line)
        tensor, spot, side = at.tensor, at.spot, at.side
        mate_row, far_row, corner_row = at.mate[1], at.far[1], at.corner[1]
        copies = Copies(send, recv)
        loads = {}
        for i, name in enumerate(names):
            loads[name] = pltpu.make_async_copy(source[name], held[name], local.at[i])
            loads[name].start()
        greet(at.everyone())
        peers = [at.far, at.across, at.across, at.across]

        def block_of(slot):
            distance, way = slots[slot]
            if way == 0:
                return jnp.minimum(spot + distance, far_end), spot + distance < line
            return jnp.maximum(spot - distance, 0), spot - distance >= 0

        crosses, hops = [], []
        for slot in range(len(slots)):
            block, _ = block_of(slot)
            crosses.append(
                [
                    copies.plan(cross_send[i].at[block], cross_land[i].at[block], peers[i])
                    for i in range(4)
                ]
            )
            if slot < last:
                hops.append(
                    [
                        copies.plan(
                            hop_send[i].at[slot],
                            hop_land[i].at[slot],
                            (at.up, at.down)[slots[slot][1]],
                        )
                        for i in range(4)
                    ]
                )

        def cross(distance, items):
            for slot in range(len(slots)):
                if slots[slot][0] == distance:
                    for i in items:
                        copies.begin(crosses[slot][i], block_of(slot)[1])

        def own_term(i, block):
            if i == FC:
                return held["fc_near"][block].astype(F32) + held["fc_near_side"][block].astype(F32)
            if i == PROJ:
                return held["proj_near"][block].astype(F32) + held["proj_near_far"][
                    block
                ].astype(F32)
            if i == MIX:
                return total[block * 2 + side].astype(F32)
            return vec_near[block * 2 + side]

        def handle(slot, i):
            block, inside = block_of(slot)
            behind = (at.has_down, at.has_up)[slots[slot][1]]
            outer = slot - 2

            def work():
                crosses[slot][i].wait_recv()
                value = own_term(i, block) + cross_land[i][block].astype(F32)
                if outer < 0:
                    hop_send[i][slot] = value.astype(hop_send[i].dtype)
                    return

                @pl.when(behind)
                def _():
                    hops[outer][i].wait_recv()
                    hop_send[i][slot] = (value + hop_land[i][outer].astype(F32)).astype(
                        hop_send[i].dtype
                    )

                @pl.when(jnp.logical_not(behind))
                def _():
                    hop_send[i][slot] = value.astype(hop_send[i].dtype)

            when(inside, work)
            copies.begin(hops[slot][i], inside)

        def handle_all(distance, items):
            for slot in range(last):
                if slots[slot][0] == distance:
                    for i in items:
                        handle(slot, i)

        def close(i, target):
            crosses[last][i].wait_recv()
            target[...] = own_term(i, spot) + cross_land[i][spot].astype(F32)
            for way, behind in enumerate((at.has_down, at.has_up)):

                def add(way=way):
                    hops[last - 2 + way][i].wait_recv()
                    target[...] += hop_land[i][last - 2 + way].astype(F32)

                when(behind, add)

        for i, one, two in ((FC, "fc_far", "fc_far_side"), (PROJ, "proj_side", "proj_side_far")):
            loads[one].wait()
            loads[two].wait()
            for block in range(line):
                cross_send[i][block] = (
                    held[one][block].astype(F32) + held[two][block].astype(F32)
                ).astype(LOW)
            cross(far_end, [i])
            cross(far_end - 1, [i])
        loads["last"].wait()
        last_copy = copies.start(held["last"].at[1], last_land, at.mate)
        loads["grad_mixed"].wait()
        loads["mix"].wait()

        def row_part(index):
            @pl.loop(0, rows // 256)
            def _(i):
                span = pl.ds(pl.multiple_of(i * 256, 256), 256)
                weight = held["mix"][...].reshape(width, width)
                part[index, span] = nt(held["grad_mixed"][index, span], weight).astype(LOW)

        row_part(corner_row)
        mate_far = copies.start(part.at[corner_row], mate_land.at[1], at.mate)
        row_part(mate_row)
        mate_own = copies.start(part.at[mate_row], mate_land.at[0], at.mate)
        for name in ("fc_near", "fc_near_side", "proj_near", "proj_near_far"):
            loads[name].wait()
        handle_all(far_end, (FC, PROJ))
        row_part(far_row)
        mate_far.wait_recv()
        far_made = []
        for i in range(2):
            span = pl.ds(i * half_rows, half_rows)
            far_send[span] = (
                mate_land[1, span].astype(F32) + part[far_row, span].astype(F32)
            ).astype(LOW)
            far_made.append(copies.start(far_send.at[span], far_land.at[span], at.far))
        row_part(tensor)
        if far_end > 1:
            handle_all(far_end - 1, (FC, PROJ))
        for distance in range(far_end - 2, -1, -1):
            cross(distance, (FC, PROJ))

        for name in ("group", "out_own", "out_far", "vec_all", "vec_part"):
            loads[name].wait()

        def outer_product(i, carry):
            sums, columns = carry
            block, start = i // (rows // 256), (i % (rows // 256)) * 256
            span = pl.ds(pl.multiple_of(start, 256), 256)
            grad = held["grad_mixed"][block, span]
            sums = sums + tn(held["group"][block, span], grad)
            return sums, columns + jnp.sum(grad.astype(F32), axis=0, keepdims=True)

        plain = jnp.zeros((width, width), F32)
        columns = jnp.zeros((1, width), F32)
        plain, columns = lax.fori_loop(0, group // 256, outer_product, (plain, columns))
        turned = held["vec_all"][...].T
        weight = held["mix"][...].reshape(width, width).astype(F32)
        gain_grad = jnp.sum(plain * weight, axis=1, keepdims=True)
        shift_grad = jnp.sum(weight * columns, axis=1, keepdims=True)
        scaled = plain * turned[:, 0:1] + turned[:, 1:2] * columns
        extras = []
        out_sum = held["out_own"][...].astype(F32) + held["out_far"][...].astype(F32)
        for p in range(3):
            piece = out_sum[p * HD : (p + 1) * HD]
            extras.append(jnp.zeros((width, WIDE - 128), F32))
            extras.append(jnp.concatenate([jnp.zeros((128 - HD, width), F32), piece], axis=0).T)
        scaled = scaled + jnp.concatenate(extras, axis=1)
        for k in range(n_dp):
            total[k] = scaled[k * shard : (k + 1) * shard].astype(LOW)
        for block in range(line):
            cross_send[MIX][block] = total[block * 2 + 1 - side]
        cross(far_end, [MIX])
        cross(far_end - 1, [MIX])
        vec_mine[...] = held["vec_part"][...]
        flat = jnp.concatenate(
            [gain_grad, shift_grad, jnp.zeros((width, 6), F32)], axis=1
        ).T
        vec_mine[0:2] = flat[0:2]
        vec_lane = lax.broadcasted_iota(jnp.int32, (1, width), 1)
        in_part = (vec_lane >= tensor * (NH * HD)) & (vec_lane < (tensor + 1) * (NH * HD))
        for row, low in ((2, 0), (3, 2 * WIDE)):
            line_up = jnp.concatenate([columns[:, low : low + WIDE]] + [columns[:, 0:WIDE]] * 2, axis=1)
            placed = jnp.zeros((1, width), F32)
            for t in range(4):
                shifted = pltpu.roll(line_up, t * NH * HD, 1)
                placed = jnp.where(tensor == t, shifted, placed)
            vec_mine[row : row + 1] = jnp.where(in_part, placed, 0.0)
        vec_made = [
            copies.start(vec_mine, vec_land.at[i], device)
            for i, device in enumerate((at.mate, at.far, at.corner))
        ]
        for distance in range(far_end - 2, 0, -1):
            handle_all(distance, (FC, PROJ))
        for copy in vec_made:
            copy.wait_recv()
        vec_sum = vec_mine[...] + vec_land[0] + vec_land[1] + vec_land[2]
        for k in range(n_dp):
            vec_near[k] = pltpu.roll(vec_sum, (width - k * shard) % width, 1)[:, 0:128]
        for block in range(line):
            cross_send[VEC][block] = vec_near[block * 2 + 1 - side]
        cross(far_end, [VEC])
        cross(far_end - 1, [VEC])
        for distance in range(far_end, 0, -1):
            handle_all(distance, (MIX, VEC))
            if distance >= 2:
                cross(distance - 2, (MIX, VEC))

        for name in ("hidden", "grad_middle", "middle", "positions"):
            loads[name].wait()
        last_copy.wait_recv()
        first_row = tensor * rows
        last_bias = held["vec_all"][7:8]
        gain = held["vec_all"][0:1]
        mate_own.wait_recv()
        for copy in far_made:
            copy.wait_recv()
        tile = 4 * window

        @pl.loop(0, rows // tile)
        def _(i):
            start = pl.multiple_of(i * tile, tile)
            span = pl.ds(start, tile)
            ids = first_row + start + lax.broadcasted_iota(jnp.int32, (tile, 1), 0)
            final = (
                held["middle"][span]
                + held["last"][0, span].astype(F32)
                + last_land[span].astype(F32)
                + last_bias
            )
            block_out[span] = jnp.where(ids < scalar_ref[2], final, 0.0).astype(LOW)
            grad = (
                part[tensor, span].astype(F32)
                + mate_land[0, span].astype(F32)
                + far_land[span].astype(F32)
            )
            normed, inverse = normalize(held["hidden"][span].astype(F32))
            grad = held["grad_middle"][span] + norm_back(normed, inverse, grad, gain)
            for w in range(4):
                spot_row = held["positions"][pl.ds(i * 4 + w, 1)][:, 0:1] - (i * 4 + w) * window
                here = lax.broadcasted_iota(jnp.int32, (window, 1), 0) == spot_row
                piece = grad[w * window : (w + 1) * window]
                tokens_out[pl.ds(pl.multiple_of(start + w * window, window), window)] = jnp.where(
                    here, 0.0, piece
                )
                thoughts_out[pl.ds(i * 4 + w, 1)] = jnp.sum(
                    jnp.where(here, piece, 0.0), axis=0, keepdims=True
                )

        for i in (FC, PROJ, MIX):
            close(i, out[i])
        close(VEC, vec_out)
        copies.finish()

    f32 = lambda *shape: jax.ShapeDtypeStruct(shape, F32)
    outputs = (
        f32(shard, width), f32(shard, width), f32(shard, width), f32(VEC_ROWS, 128),
        f32(rows, width), f32(latents, width), jax.ShapeDtypeStruct((rows, width), LOW),
    )
    scratch = [pltpu.VMEM(arrays[name].shape, arrays[name].dtype) for name in names]
    for number in (line, line, last, last):
        scratch += [pltpu.VMEM((number, shard, width), LOW)] * 3
        scratch.append(pltpu.VMEM((number, VEC_ROWS, 128), F32))
    scratch += [
        pltpu.VMEM((4, rows, width), LOW),
        pltpu.VMEM((2, rows, width), LOW),
        pltpu.VMEM((rows, width), LOW),
        pltpu.VMEM((rows, width), LOW),
        pltpu.VMEM((rows, width), LOW),
        pltpu.VMEM((n_dp, shard, width), LOW),
        pltpu.VMEM((VEC_ROWS, width), F32),
        pltpu.VMEM((3, VEC_ROWS, width), F32),
        pltpu.VMEM((n_dp, VEC_ROWS, 128), F32),
    ]
    return comm_call(
        kernel,
        "finish_grads",
        outputs,
        (scalars, *arrays.values()),
        [pl.BlockSpec(memory_space=pltpu.SMEM)] + [ANY] * len(names),
        (VM,) * len(outputs),
        (2 * last + 1) * 4 + 1 + 2 + 2 + 3,
        cid,
        scratch=scratch,
        local=len(names),
        limit=63 << 20,
    )


def unit_kernel(add, line, live_ref, *refs):
    refs = list(refs)
    rows_ref, grad_in = refs[:2]
    pieces, bias_ref = refs[2:6], refs[6]
    refs = refs[7:]
    if add:
        last_in, two_in = refs[:2]
        refs = refs[2:]
    last_ref, two_ref, fc_near, fc_side, proj_near, proj_side, bias_grad_ref = refs[:7]
    fc_all, proj_all, fc_sum, proj_sum = refs[7:]
    step = pl.program_id(0)
    side, tensor, live = live_ref[0], live_ref[1], live_ref[2]

    @pl.when(step == 0)
    def _():
        for full, near, across in ((fc_all, *pieces[:2]), (proj_all, *pieces[2:])):
            for i in range(line):
                full[2 * i + side] = near[i]
                full[2 * i + 1 - side] = across[i]
        fc_sum[...] = jnp.zeros_like(fc_sum)
        proj_sum[...] = jnp.zeros_like(proj_sum)
        bias_grad_ref[...] = jnp.zeros_like(bias_grad_ref)

    count, width = rows_ref.shape
    half = pl.num_programs(0) // 2
    block = jnp.where(step < half, tensor, tensor + 1 - 2 * (tensor % 2))
    first = block * (half * count) + (step % half) * count
    alive = first + lax.broadcasted_iota(jnp.int32, (count, 1), 0) < live
    rows = rows_ref[...]
    grad = jnp.where(alive, grad_in[...], jnp.zeros_like(grad_in))
    fc = fc_all[...].reshape(width, -1)
    proj = proj_all[...].reshape(width, -1)
    inner = nn(rows, fc) + bias_ref[...]
    square = inner * inner
    bend = jnp.tanh(GELU_SCALE * inner * (1.0 + GELU_CUBE * square))
    half = 0.5 * (1.0 + bend)
    activated = (inner * half).astype(LOW)
    slope = half + 0.5 * inner * (1.0 - bend * bend) * GELU_SCALE * (1.0 + 3.0 * GELU_CUBE * square)
    grad_inner = (nn(grad, proj) * slope).astype(LOW)
    last = nt(activated, proj)
    two = nt(grad_inner, fc)
    if add:
        last, two = last + last_in[...], two + two_in[...]
    last_ref[...] = last.astype(last_ref.dtype)
    two_ref[...] = two.astype(two_ref.dtype)
    fc_sum[...] += tn(rows, grad_inner)
    proj_sum[...] += tn(grad, activated)
    bias_grad_ref[...] += jnp.sum(grad_inner.astype(F32), axis=0, keepdims=True)

    @pl.when(step == pl.num_programs(0) - 1)
    def _():
        shard = fc_near.shape[1]
        for sums, near, across in ((fc_sum, fc_near, fc_side), (proj_sum, proj_near, proj_side)):
            for i in range(line):
                even = sums[2 * i * shard : (2 * i + 1) * shard].astype(LOW)
                odd = sums[(2 * i + 1) * shard : (2 * i + 2) * shard].astype(LOW)
                near[i] = jnp.where(side == 0, even, odd)
                across[i] = jnp.where(side == 0, odd, even)


def units_both_ways(scalars, rows, grad, pieces, bias, before):
    count, width = rows.shape
    line, shard, units = pieces[0].shape
    tile = pl.BlockSpec((ROW_TILE, width), lambda i: (i, 0))
    fixed = lambda shape: pl.BlockSpec(shape, lambda i: (0,) * len(shape))
    add = before is not None
    kind = LOW if add else F32
    return pl.pallas_call(
        functools.partial(unit_kernel, add, line),
        grid=(count // ROW_TILE,),
        out_shape=(
            jax.ShapeDtypeStruct((count, width), kind),
            jax.ShapeDtypeStruct((count, width), kind),
        )
        + (jax.ShapeDtypeStruct((line, shard, units), LOW),) * 4
        + (jax.ShapeDtypeStruct((1, units), F32),        ),
        in_specs=[pl.BlockSpec(memory_space=pltpu.SMEM), tile, tile]
        + [fixed((line, shard, units))] * 4
        + [fixed((1, units))]
        + [tile] * (2 if add else 0),
        out_specs=(tile, tile) + (fixed((line, shard, units)),) * 4 + (fixed((1, units)),),
        scratch_shapes=[pltpu.VMEM((2 * line, shard, units), LOW)] * 2
        + [pltpu.VMEM((width, units), F32)] * 2,
        compiler_params=pltpu.CompilerParams(
            dimension_semantics=("arbitrary",), vmem_limit_bytes=56 << 20
        ),
        cost_estimate=pl.CostEstimate(
            flops=12 * count * width * units,
            bytes_accessed=24 * count * width,
            transcendentals=count * units,
        ),
        name="units_second" if add else "units_first",
    )(scalars, rows, grad, *pieces, bias, *(before or ()))


def normalize(values):
    center = jnp.mean(values, axis=-1, keepdims=True)
    offset = values - center
    spread = jnp.mean(offset * offset, axis=-1, keepdims=True)
    inverse = lax.rsqrt(spread + EPSILON)
    return offset * inverse, inverse


def norm_back(normed, inverse, grad, gain):
    scaled = grad * gain
    center = jnp.mean(scaled, axis=-1, keepdims=True)
    along = jnp.mean(scaled * normed, axis=-1, keepdims=True)
    return inverse * (scaled - center - normed * along)


def product(equation, left, right):
    return jnp.einsum(equation, left, right, preferred_element_type=F32)


def pack_three(qkv, out_turned):
    depth = qkv.shape[0]
    parts = jnp.transpose(qkv.reshape(depth, NH, 3, HD), (0, 2, 1, 3))
    extra = out_turned.reshape(depth, 3, 1, HD)
    return jnp.concatenate([parts, extra], axis=2).reshape(depth, 3 * WIDE)


def unpack_three(packed):
    depth = packed.shape[0]
    split = packed.reshape(depth, 3, NH + 1, HD)
    qkv = jnp.transpose(split[:, :, :NH], (0, 2, 1, 3)).reshape(depth, 3 * NH * HD)
    return qkv, split[:, :, NH].reshape(depth, NH * HD)


def per_device(
    tokens,
    thoughts,
    positions,
    lengths,
    attn_norm_gain,
    attn_norm_shift,
    qkv_weight,
    qv_bias,
    attn_out_weight,
    attn_out_bias,
    mlp_norm_gain,
    mlp_norm_shift,
    fc_weight,
    fc_bias,
    proj_weight,
    proj_bias,
    cotangent,
):
    n_dp = lax.axis_size("dp")
    n_tensor = lax.axis_size("tensor")
    tensor = lax.axis_index("tensor")
    rows, width = tokens.shape
    slots = rows * n_tensor
    head_width = NH * HD
    units = FF // n_tensor
    far = (tensor + 2) % n_tensor
    swap_far = [(i, (i + 2) % n_tensor) for i in range(n_tensor)]

    window = rows // thoughts.shape[0]
    starts = jnp.arange(thoughts.shape[0], dtype=jnp.int32) * window
    placed = (
        jnp.arange(window, dtype=jnp.int32)[None, :] == (positions - starts)[:, None]
    )[:, :, None]
    tokens_low = jnp.where(
        placed, thoughts[:, None, :], tokens.reshape(-1, window, width)
    ).reshape(rows, width)

    ends = [lengths[0, 0]]
    for i in range(1, SEQ_DEV):
        ends.append(ends[-1] + lengths[0, i])
    segment_ends = jnp.stack(ends)
    live_slots = ends[-1]
    own_slots = tensor * rows + jnp.arange(rows, dtype=jnp.int32)
    live = (own_slots < live_slots)[:, None]

    share = width // (n_dp * n_tensor)
    small = [
        attn_norm_gain, attn_norm_shift, qv_bias[0], qv_bias[1], attn_out_bias,
        mlp_norm_gain, mlp_norm_shift, proj_bias, fc_bias,
    ]
    vectors = jnp.concatenate([jnp.pad(v[None], ((0, 0), (0, 128 - v.shape[0]))) for v in small])
    vectors = jnp.pad(vectors, ((0, VEC_ROWS - len(small)), (0, 0)))

    (
        group_low, mixed, mix_all, fc_near, fc_side, fc_far_near, proj_near, grad_rows, out_own,
        vec_all,
    ) = gather_inputs(
        tokens_low, cotangent, fc_weight, proj_weight.T,
        pack_three(qkv_weight, attn_out_weight.T), vectors, n_dp,
    )
    mix_own = mix_all.reshape(width, -1)
    group_low = group_low.reshape(slots, width)
    mixed = mixed.reshape(slots, -1)
    swap_side = [(i, i + 1 - 2 * (i % 2)) for i in range(n_dp)]
    out_far = lax.ppermute(out_own, "tensor", swap_far)
    proj_far_near = lax.ppermute(proj_near, "tensor", swap_far)
    fc_far_side = lax.ppermute(fc_far_near, "dp", swap_side)
    proj_side = lax.ppermute(proj_near, "dp", swap_side)
    gain_one, shift_one, out_bias, gain_two, shift_two, last_bias = [
        vec_all[i] for i in (0, 1, 4, 5, 6, 7)
    ]
    hidden_bias = jnp.transpose(
        vec_all[8 : 8 + n_tensor].reshape(n_tensor, n_dp, -1), (1, 0, 2)
    ).reshape(n_tensor, units)

    attended, stats = attend(segment_ends, mixed)
    sent, out_far, proj_far_near = lax.optimization_barrier((attended, out_far, proj_far_near))
    both = heads_to_rows(sent, n_dp, 1)
    proj_far_side = lax.ppermute(proj_far_near, "dp", swap_side)
    mid_part = product("et,ed->td", both[0], out_own) + product("et,ed->td", both[1], out_far)
    mid_low = mid_part.astype(LOW).reshape(2, rows, width)
    mid_mate = mate_sum_part(mid_low, n_dp, 2)
    hidden = tokens_low.astype(F32)
    middle = hidden + mid_low[0].astype(F32) + mid_mate.astype(F32) + out_bias
    normed_mid, inverse_mid = normalize(middle)
    normed_two = (normed_mid * gain_two + shift_two).astype(LOW)
    chip_two = mate_rows(normed_two, n_dp, 3).reshape(2 * rows, width)
    chip_grad = grad_rows.reshape(2 * rows, width)

    def bias_row(index):
        return lax.dynamic_slice_in_dim(hidden_bias, index, 1, 0)

    scalars = jnp.stack([lax.axis_index("dp") % 2, tensor, live_slots]).astype(jnp.int32)
    first = units_both_ways(
        scalars, chip_two, chip_grad,
        (fc_far_near, fc_far_side, proj_far_near, proj_far_side), bias_row(far), None,
    )
    far_fc_near, far_fc_side, far_proj_near, far_proj_side, far_fc_bias = first[2:]
    proj_near_far = lax.ppermute(far_proj_near, "tensor", swap_far)
    proj_side_far = lax.ppermute(far_proj_side, "tensor", swap_far)
    fc_far_side_in = lax.ppermute(far_fc_side, "dp", swap_side)
    second = units_both_ways(
        scalars, chip_two, chip_grad, (fc_near, fc_side, proj_near, proj_side), bias_row(tensor),
        first[:2],
    )
    last_part, grad_two_part, fc_near_grad, fc_side_grad, proj_near_grad, proj_side_grad = second[:6]
    fc_near_side_in = lax.ppermute(fc_side_grad, "dp", swap_side)
    grad_fc_bias, far_fc_bias = second[6][0], far_fc_bias[0]
    two_low = grad_two_part.reshape(2, rows, width)
    two_mate = mate_sum_part(two_low, n_dp, 4)
    grad_two = two_low[0].astype(F32) + two_mate.astype(F32)
    grad_final = jnp.where(live, cotangent, jnp.zeros_like(cotangent)).astype(F32)
    grad_middle = grad_final + norm_back(normed_mid, inverse_mid, grad_two, gain_two)
    grad_gain_two = jnp.sum(normed_mid * grad_two, axis=0)
    grad_shift_two = jnp.sum(grad_two, axis=0)
    chip_mid = mate_rows(grad_middle.astype(LOW), n_dp, 5).reshape(2 * rows, width)
    grad_attended = jnp.stack(
        [product("ed,td->et", w, chip_mid).astype(LOW) for w in (out_own, out_far)]
    )
    grad_out, far_out = [product("et,td->ed", both[i], chip_mid).astype(LOW) for i in range(2)]
    grad_attended, proj_near_far, proj_side_far = lax.optimization_barrier(
        (grad_attended, proj_near_far, proj_side_far)
    )
    grad_heads = rows_to_heads(grad_attended, n_dp, 6)
    grad_heads, far_out = lax.optimization_barrier((grad_heads, far_out))
    far_out = lax.ppermute(far_out, "tensor", swap_far)
    last_low = last_part.reshape(2, rows, width)

    grad_mixed = attend_back(segment_ends, mixed, attended, stats, grad_heads)
    bias_part = jnp.zeros((n_tensor, units), F32)
    bias_part = lax.dynamic_update_slice_in_dim(bias_part, grad_fc_bias[None], tensor, 0)
    bias_part = lax.dynamic_update_slice_in_dim(bias_part, far_fc_bias[None], far, 0)
    bias_part = jnp.transpose(bias_part.reshape(n_dp, n_tensor, -1), (1, 0, 2))
    zero_row = jnp.zeros((width,), F32)
    vec_part = jnp.concatenate(
        [
            jnp.stack(
                [
                    zero_row, zero_row, zero_row, zero_row, jnp.sum(grad_middle, axis=0),
                    grad_gain_two, grad_shift_two, jnp.sum(grad_final, axis=0),
                ]
            ),
            bias_part.reshape(n_tensor, width),
            jnp.zeros((VEC_ROWS - 8 - n_tensor, width), F32),
        ]
    )
    arrays = {
        "fc_far": far_fc_near, "fc_far_side": fc_far_side_in,
        "proj_side": proj_side_grad, "proj_side_far": proj_side_far,
        "grad_mixed": grad_mixed.reshape(n_tensor, rows, width), "mix": mix_all,
        "fc_near": fc_near_grad, "fc_near_side": fc_near_side_in,
        "proj_near": proj_near_grad, "proj_near_far": proj_near_far,
        "last": last_low,
        "group": group_low.reshape(n_tensor, rows, width),
        "out_own": grad_out, "out_far": far_out,
        "vec_all": vec_all, "vec_part": vec_part,
        "hidden": tokens_low, "grad_middle": grad_middle, "middle": middle,
        "positions": jnp.broadcast_to(positions[:, None], (positions.shape[0], 128)),
    }
    fc_grad, proj_grad, mix_grad, vec, grad_tokens, grad_thoughts, block_out = finish_grads(
        scalars, arrays, n_dp, 8
    )
    qkv_grad, out_grad = unpack_three(mix_grad)
    small_grads = lax.dynamic_slice_in_dim(vec[:8], tensor * share, share, 1)
    fc_bias_grad = lax.dynamic_slice_in_dim(vec, 8 + tensor, 1, 0)[0, : fc_bias.shape[0]]
    return (
        block_out,
        grad_tokens,
        grad_thoughts,
        small_grads[0],
        small_grads[1],
        qkv_grad,
        small_grads[2:4],
        out_grad.T,
        small_grads[4],
        small_grads[5],
        small_grads[6],
        fc_grad,
        fc_bias_grad,
        proj_grad.T,
        small_grads[7],
    )


def solution(mesh):
    rows = P(("dp", "tensor"), None)
    line = P(("dp", "tensor"))
    in_specs = (
        rows, rows, line, P("dp", None), line, line, P("dp", "tensor"),
        P(None, ("dp", "tensor")), P("tensor", "dp"), line, line, line,
        P("dp", "tensor"), line, P("tensor", "dp"), line, rows,
    )
    out_specs = (
        rows, rows, rows, line, line, P("dp", "tensor"), P(None, ("dp", "tensor")),
        P("tensor", "dp"), line, line, line, P("dp", "tensor"), line, P("tensor", "dp"), line,
    )
    return jax.shard_map(
        per_device, mesh=mesh, in_specs=in_specs, out_specs=out_specs, check_vma=False
    )
```

```python
import functools
import math

import jax
import jax.numpy as jnp
from jax import lax
from jax.experimental import pallas as pl
from jax.experimental.pallas import tpu as pltpu
from jax.sharding import PartitionSpec as P

H = 12
HD = 64
FF = 3072
SEQ_DEV = 3
EPSILON = 1e-05
MASKED = -1e30
NH = 3
SLABS = 2
WIDE = SLABS * 128
BQ = 512
BK = 512
VEC_ROWS = 16
ROW_TILE = 256
GELU_SCALE = math.sqrt(2.0 / math.pi)
GELU_CUBE = 0.044715
MESH = pl.DeviceIdType.MESH
ANY = pl.BlockSpec(memory_space=pl.ANY)
VM = pl.BlockSpec(memory_space=pltpu.VMEM)
LOW = jnp.bfloat16
F32 = jnp.float32


def nn(a, b):
    return lax.dot_general(a, b, (((1,), (0,)), ((), ())), preferred_element_type=jnp.float32)


def nt(a, b):
    return lax.dot_general(a, b, (((1,), (1,)), ((), ())), preferred_element_type=jnp.float32)


def tn(a, b):
    return lax.dot_general(a, b, (((0,), (0,)), ((), ())), preferred_element_type=jnp.float32)


def head_rows(slab, head):
    half = slab[(head % 2) * HD : (head % 2 + 1) * HD]
    zero = jnp.zeros_like(half)
    return jnp.concatenate([half, zero] if head % 2 == 0 else [zero, half], axis=0)


def segment_start(ends_ref, slots):
    start = jnp.zeros_like(slots)
    for i in range(SEQ_DEV):
        start = jnp.where(slots >= ends_ref[i], ends_ref[i], start)
    return start


def segment_stop(ends_ref, slot, slots):
    stop = slots
    for i in reversed(range(SEQ_DEV)):
        stop = jnp.where(slot < ends_ref[i], ends_ref[i], stop)
    return stop


def attend_kernel(ends_ref, mixed_ref, out_ref, stat_ref, qt_ref, vt_ref):
    tokens = mixed_ref.shape[0]
    for first in range(0, tokens, BQ):
        rows = pl.ds(first, BQ)
        for slab in range(SLABS):
            lanes = slab * 128
            qt_ref[lanes : lanes + 128, rows] = (
                mixed_ref[rows, lanes : lanes + 128] * HD ** (-0.5)
            ).T
            vt_ref[lanes : lanes + 128, rows] = mixed_ref[
                rows, 2 * WIDE + lanes : 2 * WIDE + lanes + 128
            ].T

    def query_block(block, carry):
        first = pl.multiple_of(block * BQ, BQ)
        columns = pl.ds(first, BQ)
        start = segment_start(ends_ref, first + lax.broadcasted_iota(jnp.int32, (1, BQ), 1))
        query_ids = first + lax.broadcasted_iota(jnp.int32, (BK, BQ), 1)
        queries = [
            head_rows(qt_ref[(h // 2) * 128 : (h // 2 + 1) * 128, columns], h) for h in range(NH)
        ]

        def key_block(key, state):
            base = pl.multiple_of(key * BK, BK)
            rows = pl.ds(base, BK)
            key_ids = base + lax.broadcasted_iota(jnp.int32, (BK, BQ), 0)
            allowed = (key_ids <= query_ids) & (key_ids >= start)
            result = []
            for h in range(NH):
                peak, total, acc = state[h]
                slab = h // 2
                scores = nn(mixed_ref[rows, WIDE + slab * 128 : WIDE + slab * 128 + 128], queries[h])
                scores = jnp.where(allowed, scores, MASKED)
                fresh = jnp.maximum(peak, jnp.max(scores, axis=0, keepdims=True))
                weight = jnp.exp(scores - fresh)
                decay = jnp.exp(peak - fresh)
                total = total * decay + jnp.sum(weight, axis=0, keepdims=True)
                values = vt_ref[h * HD : (h + 1) * HD, rows]
                acc = acc * decay + nn(values, weight.astype(jnp.bfloat16))
                result.append((fresh, total, acc))
            return tuple(result)

        empty = tuple(
            (
                jnp.full((1, BQ), MASKED, jnp.float32),
                jnp.zeros((1, BQ), jnp.float32),
                jnp.zeros((HD, BQ), jnp.float32),
            )
            for _ in range(NH)
        )
        state = lax.fori_loop(segment_start(ends_ref, first) // BK, (block + 1) * (BQ // BK), key_block, empty)
        for h in range(NH):
            peak, total, acc = state[h]
            out_ref[h * HD : (h + 1) * HD, columns] = (acc / total).astype(jnp.bfloat16)
            stat_ref[h : h + 1, columns] = peak + jnp.log(total)
        return carry

    lax.fori_loop(0, tokens // BQ, query_block, 0)


def attend(ends, mixed):
    tokens = mixed.shape[0]
    vm = pl.BlockSpec(memory_space=pltpu.VMEM)
    return pl.pallas_call(
        attend_kernel,
        out_shape=(
            jax.ShapeDtypeStruct((NH * HD, tokens), jnp.bfloat16),
            jax.ShapeDtypeStruct((8, tokens), jnp.float32),
        ),
        in_specs=[pl.BlockSpec(memory_space=pltpu.SMEM), vm],
        out_specs=(vm, vm),
        scratch_shapes=[pltpu.VMEM((WIDE, tokens), jnp.bfloat16)] * 2,
        compiler_params=pltpu.CompilerParams(vmem_limit_bytes=40 << 20),
        cost_estimate=pl.CostEstimate(
            flops=8 * tokens * tokens * NH * HD,
            bytes_accessed=16 * tokens * WIDE,
            transcendentals=tokens * tokens,
        ),
        name="attend",
    )(ends, mixed)


def attend_back_kernel(
    ends_ref, mixed_ref, out_ref, stat_ref, gradt_ref,
    gmixed_ref, qt_ref, kt_ref, grad_ref, delta_ref, dqt_ref
):
    tokens = mixed_ref.shape[0]
    for first in range(0, tokens, BQ):
        rows = pl.ds(first, BQ)
        for slab in range(SLABS):
            lanes = slab * 128
            qt_ref[lanes : lanes + 128, rows] = (
                mixed_ref[rows, lanes : lanes + 128] * HD ** (-0.5)
            ).T
            kt_ref[lanes : lanes + 128, rows] = mixed_ref[rows, WIDE + lanes : WIDE + lanes + 128].T
        grad_ref[rows, 0:128] = gradt_ref[0:128, rows].T
        grad_ref[rows, 128:256] = jnp.concatenate(
            [gradt_ref[128:192, rows], jnp.zeros((64, BQ), jnp.bfloat16)], axis=0
        ).T
        for h in range(NH):
            product = gradt_ref[h * HD : (h + 1) * HD, rows].astype(jnp.float32) * out_ref[
                h * HD : (h + 1) * HD, rows
            ].astype(jnp.float32)
            delta_ref[h : h + 1, rows] = jnp.sum(product, axis=0, keepdims=True)
    dqt_ref[...] = jnp.zeros_like(dqt_ref)
    lane = lax.broadcasted_iota(jnp.int32, (BQ, 128), 1)

    def key_block(key, carry):
        base = pl.multiple_of(key * BK, BK)
        rows = pl.ds(base, BK)
        key_ids = base + lax.broadcasted_iota(jnp.int32, (BK, BQ), 0)

        def query_block(block, state):
            first = pl.multiple_of(block * BQ, BQ)
            columns = pl.ds(first, BQ)
            start = segment_start(ends_ref, first + lax.broadcasted_iota(jnp.int32, (1, BQ), 1))
            query_ids = first + lax.broadcasted_iota(jnp.int32, (BK, BQ), 1)
            allowed = (key_ids <= query_ids) & (key_ids >= start)
            grad_keys = list(state[:SLABS])
            grad_values = list(state[SLABS:])
            for h in range(NH):
                slab = h // 2
                low, high = slab * 128, slab * 128 + 128
                queries = head_rows(qt_ref[low:high, columns], h)
                scores = nn(mixed_ref[rows, WIDE + low : WIDE + high], queries)
                probs = jnp.where(allowed, jnp.exp(scores - stat_ref[h : h + 1, columns]), 0.0)
                keep = (lane // HD) == (h % 2)
                grads = jnp.where(keep, grad_ref[columns, low:high], 0.0)
                grad_values[slab] += nn(probs.astype(jnp.bfloat16), grads)
                if h == NH - 1 and NH % 2 == 1:
                    grad_rows = jnp.concatenate(
                        [gradt_ref[h * HD : (h + 1) * HD, columns], jnp.zeros((HD, BQ), jnp.bfloat16)],
                        axis=0,
                    )
                else:
                    grad_rows = head_rows(gradt_ref[low:high, columns], h)
                grad_probs = nn(mixed_ref[rows, 2 * WIDE + low : 2 * WIDE + high], grad_rows)
                grad_scores = (probs * (grad_probs - delta_ref[h : h + 1, columns])).astype(
                    jnp.bfloat16
                )
                natural = mixed_ref[columns, low:high]
                grad_keys[slab] += nn(grad_scores, jnp.where(keep, natural, 0.0))
                dqt_ref[h * HD : (h + 1) * HD, columns] += nn(
                    kt_ref[h * HD : (h + 1) * HD, rows], grad_scores
                )
            return tuple(grad_keys) + tuple(grad_values)

        empty = (jnp.zeros((BK, 128), jnp.float32),) * (2 * SLABS)
        stop = segment_stop(ends_ref, base + BK - 1, tokens)
        state = lax.fori_loop(key * BK // BQ, (stop - 1) // BQ + 1, query_block, empty)
        for slab in range(SLABS):
            low = slab * 128
            gmixed_ref[rows, WIDE + low : WIDE + low + 128] = (
                state[slab] * HD ** (-0.5)
            ).astype(jnp.bfloat16)
            gmixed_ref[rows, 2 * WIDE + low : 2 * WIDE + low + 128] = state[SLABS + slab].astype(
                jnp.bfloat16
            )
        return carry

    lax.fori_loop(0, tokens // BK, key_block, 0)
    for first in range(0, tokens, BQ):
        rows = pl.ds(first, BQ)
        for slab in range(SLABS):
            low = slab * 128
            gmixed_ref[rows, low : low + 128] = (
                (dqt_ref[low : low + 128, rows] * HD ** (-0.5)).T.astype(jnp.bfloat16)
            )


def attend_back(ends, mixed, out, stat, gradt):
    tokens = mixed.shape[0]
    vm = pl.BlockSpec(memory_space=pltpu.VMEM)
    return pl.pallas_call(
        attend_back_kernel,
        out_shape=jax.ShapeDtypeStruct((tokens, 3 * WIDE), jnp.bfloat16),
        in_specs=[pl.BlockSpec(memory_space=pltpu.SMEM)] + [vm] * 4,
        out_specs=vm,
        scratch_shapes=[
            pltpu.VMEM((WIDE, tokens), jnp.bfloat16),
            pltpu.VMEM((WIDE, tokens), jnp.bfloat16),
            pltpu.VMEM((tokens, WIDE), jnp.bfloat16),
            pltpu.VMEM((8, tokens), jnp.float32),
            pltpu.VMEM((WIDE, tokens), jnp.float32),
        ],
        compiler_params=pltpu.CompilerParams(vmem_limit_bytes=50 << 20),
        cost_estimate=pl.CostEstimate(
            flops=20 * tokens * tokens * NH * HD,
            bytes_accessed=32 * tokens * WIDE,
            transcendentals=tokens * tokens,
        ),
        name="attend_back",
    )(ends, mixed, out, stat, gradt)


class Copies:
    def __init__(self, send, recv):
        self.send, self.recv, self.made, self.started = send, recv, 0, []

    def plan(self, source, target, device):
        index = self.made
        self.made += 1
        return pltpu.make_async_remote_copy(
            src_ref=source,
            dst_ref=target,
            send_sem=self.send.at[index],
            recv_sem=self.recv.at[index],
            device_id=device,
            device_id_type=MESH,
        )

    def begin(self, copy, condition=None):
        self.started.append((copy, condition))
        when(condition, copy.start)

    def start(self, source, target, device):
        copy = self.plan(source, target, device)
        self.begin(copy)
        return copy

    def finish(self):
        for copy, condition in self.started:
            when(condition, copy.wait_send)


def when(condition, action):
    if condition is None:
        action()
    else:
        pl.when(condition)(action)


def greet(devices):
    barrier = pltpu.get_barrier_semaphore()
    for device, condition in devices:
        when(
            condition,
            lambda device=device: pl.semaphore_signal(
                barrier, inc=1, device_id=device, device_id_type=MESH
            ),
        )
    present = [1 if condition is None else condition.astype(jnp.int32) for _, condition in devices]
    pl.semaphore_wait(barrier, sum(present))


class Place:
    def __init__(self, line):
        self.dp = dp = lax.axis_index("dp")
        self.tensor = tensor = lax.axis_index("tensor")
        self.spot, self.side = spot, side = dp // 2, dp % 2
        self.chip, self.core = tensor // 2, tensor % 2
        self.has_up, self.has_down = spot + 1 < line, spot > 0
        self.up = (jnp.minimum(spot + 1, line - 1) * 2 + side, tensor)
        self.down = (jnp.maximum(spot - 1, 0) * 2 + side, tensor)
        self.across = (spot * 2 + 1 - side, tensor)
        self.mate = (dp, tensor + 1 - 2 * (tensor % 2))
        self.far = (dp, (tensor + 2) % 4)
        self.corner = (dp, 3 - tensor)

    def everyone(self):
        return [
            (self.mate, None), (self.far, None), (self.corner, None), (self.across, None),
            (self.up, self.has_up), (self.down, self.has_down),
        ]


def comm_call(kernel, name, outputs, inputs, in_specs, out_specs, copies, cid, scratch=(), local=1, limit=50 << 20):
    return pl.pallas_call(
        kernel,
        out_shape=outputs,
        in_specs=in_specs,
        out_specs=out_specs,
        scratch_shapes=list(scratch)
        + [
            pltpu.SemaphoreType.DMA((copies,)),
            pltpu.SemaphoreType.DMA((copies,)),
            pltpu.SemaphoreType.DMA((local,)),
        ],
        compiler_params=pltpu.CompilerParams(
            collective_id=cid, has_side_effects=True, vmem_limit_bytes=limit
        ),
        name=name,
    )(*inputs)


def one_hot(rows, columns, shift, limit):
    lane = lax.broadcasted_iota(jnp.int32, (rows, columns), 0)
    spot = lax.broadcasted_iota(jnp.int32, (rows, columns), 1)
    return ((spot == lane + shift) & (lane < limit)).astype(LOW)


def gather_inputs(hidden, cotangent, fc, proj, mix, vectors, n_dp):
    line = n_dp // 2
    hops = line - 1
    rows, width = hidden.shape
    shard = fc.shape[0]
    half_rows = rows // 2
    share = width // (n_dp * 4)

    def kernel(
        hidden_ref, cot_ref, fc_ref, proj_ref, mix_ref, vec_ref,
        normed_out, mixed_out, mix_out, fc_near, fc_side, fc_far, proj_near, cot_out, out_out,
        vec_out,
        land, mix_land, tiles, tile_land, normed, mixed, out_turned, send, recv, local,
    ):
        at = Place(line)
        dp, tensor, spot, side = at.dp, at.tensor, at.spot, at.side
        mate_row, far_row, corner_row = at.mate[1], at.far[1], at.corner[1]
        greet(at.everyone())
        copies = Copies(send, recv)
        MIX, FC, PROJ, VEC = range(4)
        own = [mix_ref, fc_ref, proj_ref, tiles.at[dp]]

        def seat(item, position):
            if item == MIX:
                return mix_land.at[position * 2 + side]
            if item == FC:
                return fc_near.at[position]
            if item == PROJ:
                return proj_near.at[position]
            return tiles.at[position * 2 + side]

        def plan(item, hop):
            above, below = jnp.maximum(spot - hop, 0), jnp.minimum(spot + hop, line - 1)
            came_up = jnp.maximum(spot - 1 - hop, 0)
            came_down = jnp.minimum(spot + 1 + hop, line - 1)
            made = {
                "up": copies.plan(
                    own[item] if hop == 0 else seat(item, above), seat(item, above), at.up
                ),
                "down": copies.plan(
                    own[item] if hop == 0 else seat(item, below), seat(item, below), at.down
                ),
                "onward": [],
            }
            for position in (came_up, came_down):
                onward = []
                if item in (MIX, VEC):
                    onward.append(copies.plan(seat(item, position), seat(item, position), at.across))
                if item == FC:
                    onward.append(copies.plan(fc_near.at[position], fc_side.at[position], at.across))
                    onward.append(copies.plan(fc_near.at[position], fc_far.at[position], at.far))
                made["onward"].append(onward)
            return made

        plans = [[plan(item, hop) for hop in range(hops)] for item in range(4)]

        def launch(item):
            copies.begin(plans[item][0]["up"], at.has_up)
            copies.begin(plans[item][0]["down"], at.has_down)

        def handle(item, hop):
            made = plans[item][hop]
            for way, key, comes, goes in (
                (0, "up", spot - 1 - hop >= 0, at.has_up),
                (1, "down", spot + 1 + hop < line, at.has_down),
            ):
                when(comes, made[key].wait_recv)
                if hop + 1 < hops:
                    copies.begin(plans[item][hop + 1][key], comes & goes)
                for copy in made["onward"][way]:
                    copies.begin(copy, comes)

        def settle(item):
            for hop in range(hops):
                for way, comes in ((0, spot - 1 - hop >= 0), (1, spot + 1 + hop < line)):
                    for copy in plans[item][hop]["onward"][way]:
                        when(comes, copy.wait_recv)

        stays = []

        def stay(source, target):
            copy = pltpu.make_async_copy(source, target, local.at[len(stays)])
            copy.start()
            stays.append(copy)
            return copy

        vec_made = [
            copies.start(vec_ref, tile_land.at[i], device)
            for i, device in enumerate((at.mate, at.far, at.corner))
        ]
        parts = [pl.ds(0, half_rows), pl.ds(half_rows, half_rows)]
        launch(MIX)
        far_made = [
            copies.start(hidden_ref.at[part], land.at[far_row_here, part], at.far)
            for far_row_here in (2,)
            for part in parts
        ]
        mix_side = copies.start(mix_ref, mix_land.at[dp], at.across)
        launch(FC)
        fc_sides = [
            copies.start(fc_ref, fc_side.at[spot], at.across),
            copies.start(fc_ref, fc_far.at[spot], at.far),
        ]
        mate_made = copies.start(hidden_ref, land.at[1], at.mate)
        cot_made = copies.start(cot_ref, cot_out.at[1], at.mate)
        stay(cot_ref, cot_out.at[0])
        stay(fc_ref, fc_near.at[spot])
        stay(proj_ref, proj_near.at[spot])
        mix_land[dp] = mix_ref[...]
        for copy in vec_made:
            copy.wait_recv()
        merged = jnp.zeros((VEC_ROWS, 128), F32)
        bias_rows = jnp.zeros((VEC_ROWS, 128), F32)
        row_ids = lax.broadcasted_iota(jnp.int32, (VEC_ROWS, 128), 0)
        for i, index in enumerate((tensor, mate_row, far_row, corner_row)):
            tile = vec_ref[...] if i == 0 else tile_land[i - 1]
            merged += nn(tile, one_hot(128, 128, index * share, share))
            bias_rows = jnp.where(row_ids == 8 + index, tile[8:9].astype(F32), bias_rows)
        tiles[dp] = jnp.where(row_ids < 8, merged, bias_rows).astype(LOW)
        launch(VEC)
        vec_side = copies.start(tiles.at[dp], tiles.at[dp], at.across)

        def norm_rows(source, index):
            @pl.loop(0, rows // 128)
            def _(i):
                span = pl.ds(pl.multiple_of(i * 128, 128), 128)
                normed[index, span] = normalize(source[span].astype(F32))[0].astype(LOW)

            stay(normed.at[index], normed_out.at[index])

        def relay(i):
            far_made[i].wait_recv()
            return copies.start(land.at[2, parts[i]], land.at[3, parts[i]], at.mate)

        def mix_rows(index):
            @pl.loop(0, rows // 256)
            def _(i):
                span = pl.ds(pl.multiple_of(i * 256, 256), 256)
                turned = normed[index, span].astype(F32) * whole[0:1] + whole[1:2]
                weight = mix_land[...].reshape(width, width)
                mixed[index, span] = (nn(turned.astype(LOW), weight) + bias).astype(LOW)

            stay(mixed.at[index], mixed_out.at[index])

        norm_rows(hidden_ref, tensor)
        relayed = []
        for step in range(hops + 2):
            for item, hop in ((MIX, step), (VEC, step), (FC, step - 1), (PROJ, step - 2)):
                if 0 <= hop < hops:
                    handle(item, hop)
            if step == 0:
                launch(PROJ)
                mate_made.wait_recv()
                norm_rows(land.at[1], mate_row)
                relayed.append(relay(0))
            if step == 1:
                relayed.append(relay(1))
                norm_rows(land.at[2], far_row)
            if step == hops - 1:
                for copy in relayed:
                    copy.wait_recv()
                norm_rows(land.at[3], corner_row)
            if step == hops:
                mix_side.wait_recv()
                vec_side.wait_recv()
                settle(MIX)
                settle(VEC)
                whole = jnp.zeros((VEC_ROWS, width), F32)
                for i in range(n_dp):
                    whole += nn(tiles[i], one_hot(128, width, i * shard, shard))
                vec_out[...] = whole
                lane = lax.broadcasted_iota(jnp.int32, (width, WIDE), 0)
                column = lax.broadcasted_iota(jnp.int32, (width, WIDE), 1)
                pick = (lane == column + tensor * (NH * HD)) & (column < NH * HD)
                picked = nn(whole.astype(LOW), pick.astype(LOW))
                bias = jnp.concatenate(
                    [picked[2:3], jnp.zeros((1, WIDE), F32), picked[3:4]], axis=1
                )
                mix_rows(tensor)
                mix_rows(mate_row)
        mix_rows(far_row)
        mix_rows(corner_row)
        stay(mix_land, mix_out)
        weight = mix_land[...].reshape(width, width)
        for part in range(3):
            low = part * WIDE + WIDE - 128
            turned = weight[:, low : low + 128].T
            out_turned[part * HD : (part + 1) * HD] = turned[128 - HD :]
        stay(out_turned, out_out)
        settle(FC)
        for copy in fc_sides:
            copy.wait_recv()
        cot_made.wait_recv()
        copies.finish()
        for copy in stays:
            copy.wait()

    low = lambda *shape: jax.ShapeDtypeStruct(shape, LOW)
    outputs = (
        low(4, rows, width), low(4, rows, width), low(n_dp, shard, width),
        low(line, shard, width), low(line, shard, width), low(line, shard, width),
        low(line, shard, width), low(2, rows, width), low(NH * HD, width),
        jax.ShapeDtypeStruct((VEC_ROWS, width), F32),
    )
    scratch = [
        pltpu.VMEM((4, rows, width), LOW),
        pltpu.VMEM((n_dp, shard, width), LOW),
        pltpu.VMEM((n_dp, VEC_ROWS, 128), LOW),
        pltpu.VMEM((3, VEC_ROWS, 128), LOW),
        pltpu.VMEM((4, rows, width), LOW),
        pltpu.VMEM((4, rows, width), LOW),
        pltpu.VMEM((NH * HD, width), LOW),
    ]
    return comm_call(
        kernel,
        "gather_inputs",
        outputs,
        (hidden, cotangent, fc, proj, mix, vectors),
        [VM] * 6,
        tuple([ANY] * (len(outputs) - 1)) + (VM,),
        3 + 2 + 1 + 2 + 2 + 1 + 2 + hops * (2 * 4 + 2 * 4),
        0,
        scratch=scratch,
        local=3 + 8 + 2,
    )


def after_attention(attended, out_own, out_far, hidden, vec_all, n_dp, cid):
    head_width, slots = attended.shape
    rows, width = hidden.shape
    half_rows = rows // 2

    def kernel(
        heads_ref, own_ref, far_ref, hidden_ref, vec_ref,
        both_out, middle_out, two_out,
        land, part, part_low, part_land, two, send, recv, local,
    ):
        at = Place(n_dp // 2)
        greet([(at.far, None), (at.mate, None)])
        copies = Copies(send, recv)
        cores = (at.core, 1 - at.core)
        made = [None, None]
        for i in (1, 0):
            theirs = pl.multiple_of(((1 - at.chip) * 2 + cores[i]) * rows, rows)
            made[i] = copies.start(heads_ref.at[:, pl.ds(theirs, rows)], land.at[i], at.far)
        stays = []

        def stay(source, target):
            stays.append(pltpu.make_async_copy(source, target, local.at[len(stays)]))
            stays[-1].start()

        spans = []
        for i in range(2):
            ours = pl.multiple_of((at.chip * 2 + cores[i]) * rows, rows)
            spans.append(pl.ds(ours, rows))
            stay(heads_ref.at[:, spans[i]], both_out.at[0, :, i * rows : (i + 1) * rows])
            part[i] = tn(heads_ref[:, spans[i]], own_ref[...])
        sums = None
        for i in (1, 0):
            made[i].wait_recv()
            stay(land.at[i], both_out.at[1, :, i * rows : (i + 1) * rows])
            part[i] += tn(land[i], far_ref[...])
            if i == 1:
                part_low[...] = part[1].astype(LOW)
                sums = copies.start(part_low, part_land, at.mate)
        sums.wait_recv()
        mated = []
        for piece in range(2):

            @pl.loop(0, half_rows // 128)
            def _(i):
                span = pl.ds(pl.multiple_of(piece * half_rows + i * 128, 128), 128)
                middle = (
                    hidden_ref[span].astype(F32)
                    + part[0, span]
                    + part_land[span].astype(F32)
                    + vec_ref[4:5]
                )
                middle_out[span] = middle
                two[span] = (normalize(middle)[0] * vec_ref[5:6] + vec_ref[6:7]).astype(LOW)

            span = pl.ds(piece * half_rows, half_rows)
            mated.append(copies.start(two.at[span], two_out.at[1, span], at.mate))
        stay(two, two_out.at[0])
        for copy in mated:
            copy.wait_recv()
        copies.finish()
        for copy in stays:
            copy.wait()

    return comm_call(
        kernel,
        "after_attention",
        (
            jax.ShapeDtypeStruct((2, head_width, 2 * rows), LOW),
            jax.ShapeDtypeStruct((rows, width), F32),
            jax.ShapeDtypeStruct((2, rows, width), LOW),
        ),
        (attended, out_own, out_far, hidden, vec_all),
        [VM] * 5,
        (ANY, VM, ANY),
        5,
        cid,
        scratch=[
            pltpu.VMEM((2, head_width, rows), LOW),
            pltpu.VMEM((2, rows, width), F32),
            pltpu.VMEM((rows, width), LOW),
            pltpu.VMEM((rows, width), LOW),
            pltpu.VMEM((rows, width), LOW),
        ],
        local=5,
    )


def before_attention_back(scalars, two, middle, cotangent, both, out_own, out_far, vec_all, n_dp, cid):
    _, rows, width = two.shape
    head_width = out_own.shape[0]
    half_rows = rows // 2

    def kernel(
        scalar_ref, two_ref, middle_ref, cot_ref, both_ref, own_ref, far_ref, vec_ref,
        heads_out, grad_out, own_out, far_out, vec_out,
        two_land, mid, stay_heads, sent_heads, send, recv, local,
    ):
        at = Place(n_dp // 2)
        greet([(at.far, None), (at.mate, None)])
        copies = Copies(send, recv)
        halves = [pl.ds(0, half_rows), pl.ds(half_rows, half_rows)]
        sums = [copies.start(two_ref.at[1, span], two_land.at[span], at.mate) for span in halves]
        vec_out[...] = jnp.zeros_like(vec_out)
        first_row = at.tensor * rows
        mated = []
        for piece in range(2):
            sums[piece].wait_recv()

            @pl.loop(0, half_rows // 128)
            def _(i):
                start = pl.multiple_of(piece * half_rows + i * 128, 128)
                span = pl.ds(start, 128)
                grad = two_ref[0, span].astype(F32) + two_land[span].astype(F32)
                normed, inverse = normalize(middle_ref[span])
                ids = first_row + start + lax.broadcasted_iota(jnp.int32, (128, 1), 0)
                final = jnp.where(ids < scalar_ref[2], cot_ref[span].astype(F32), 0.0)
                total = final + norm_back(normed, inverse, grad, vec_ref[5:6])
                grad_out[span] = total
                mid[0, span] = total.astype(LOW)
                for row, term in ((4, total), (5, normed * grad), (6, grad), (7, final)):
                    vec_out[row : row + 1] += jnp.sum(term, axis=0, keepdims=True)

            mated.append(copies.start(mid.at[0, halves[piece]], mid.at[1, halves[piece]], at.mate))
        cores = (at.core, 1 - at.core)
        made, stays = [], []
        for i in range(2):
            if i == 1:
                for copy in mated:
                    copy.wait_recv()
            ours = pl.ds(pl.multiple_of((at.chip * 2 + cores[i]) * rows, rows), rows)
            sent_heads[i] = nt(far_ref[...], mid[i]).astype(LOW)
            made.append(copies.start(sent_heads.at[i], heads_out.at[:, ours], at.far))
            stay_heads[i] = nt(own_ref[...], mid[i]).astype(LOW)
            stays.append(
                pltpu.make_async_copy(stay_heads.at[i], heads_out.at[:, ours], local.at[i])
            )
            stays[-1].start()
        grads = mid[...].reshape(2 * rows, width)
        own_out[...] = nn(both_ref[0], grads).astype(LOW)
        far_out[...] = nn(both_ref[1], grads).astype(LOW)
        for copy in made:
            copy.wait_recv()
        copies.finish()
        for copy in stays:
            copy.wait()

    return comm_call(
        kernel,
        "before_attention_back",
        (
            jax.ShapeDtypeStruct((head_width, 4 * rows), LOW),
            jax.ShapeDtypeStruct((rows, width), F32),
            jax.ShapeDtypeStruct((head_width, width), LOW),
            jax.ShapeDtypeStruct((head_width, width), LOW),
            jax.ShapeDtypeStruct((VEC_ROWS, width), F32),
        ),
        (scalars, two, middle, cotangent, both, out_own, out_far, vec_all),
        [pl.BlockSpec(memory_space=pltpu.SMEM)] + [VM] * 7,
        (ANY,) + (VM,) * 4,
        6,
        cid,
        scratch=[
            pltpu.VMEM((rows, width), LOW),
            pltpu.VMEM((2, rows, width), LOW),
            pltpu.VMEM((2, head_width, rows), LOW),
            pltpu.VMEM((2, head_width, rows), LOW),
        ],
        local=2,
    )


def finish_grads(scalars, arrays, n_dp, cid):
    names = list(arrays)
    line = n_dp // 2
    shard = arrays["mix"].shape[1]
    rows, width = arrays["hidden"].shape
    half_rows = rows // 2
    group = 4 * rows
    latents = arrays["positions"].shape[0]
    window = rows // latents
    far_end = line - 1
    slots = [(distance, way) for distance in range(far_end, 0, -1) for way in (0, 1)] + [(0, 0)]
    last = len(slots) - 1
    share = width // (n_dp * 4)
    FC, PROJ, MIX, VEC = range(4)

    def kernel(scalar_ref, *refs):
        refs = list(refs)

        def take(number):
            taken = refs[:number]
            del refs[:number]
            return taken

        source = dict(zip(names, take(len(names))))
        fc_out, proj_out, mix_out, vec_out, tokens_out, thoughts_out, block_out = take(7)
        held = dict(zip(names, take(len(names))))
        cross_send, cross_land = take(4), take(4)
        hop_send, hop_land = take(4), take(4)
        (
            part, mate_land, far_send, far_land, last_land, total, vec_mine, vec_land, vec_near,
            send, recv, local,
        ) = refs
        out = [fc_out, proj_out, mix_out, None]
        at = Place(line)
        tensor, spot, side = at.tensor, at.spot, at.side
        mate_row, far_row, corner_row = at.mate[1], at.far[1], at.corner[1]
        copies = Copies(send, recv)
        loads = {}
        for i, name in enumerate(names):
            loads[name] = pltpu.make_async_copy(source[name], held[name], local.at[i])
            loads[name].start()
        greet(at.everyone())
        peers = [at.far, at.across, at.across, at.across]

        def block_of(slot):
            distance, way = slots[slot]
            if way == 0:
                return jnp.minimum(spot + distance, far_end), spot + distance < line
            return jnp.maximum(spot - distance, 0), spot - distance >= 0

        crosses, hops = [], []
        for slot in range(len(slots)):
            block, _ = block_of(slot)
            crosses.append(
                [
                    copies.plan(cross_send[i].at[block], cross_land[i].at[block], peers[i])
                    for i in range(4)
                ]
            )
            if slot < last:
                hops.append(
                    [
                        copies.plan(
                            hop_send[i].at[slot],
                            hop_land[i].at[slot],
                            (at.up, at.down)[slots[slot][1]],
                        )
                        for i in range(4)
                    ]
                )

        def cross(distance, items):
            for slot in range(len(slots)):
                if slots[slot][0] == distance:
                    for i in items:
                        copies.begin(crosses[slot][i], block_of(slot)[1])

        def own_term(i, block):
            if i == FC:
                return held["fc_near"][block].astype(F32) + held["fc_near_side"][block].astype(F32)
            if i == PROJ:
                return held["proj_near"][block].astype(F32) + held["proj_near_far"][
                    block
                ].astype(F32)
            if i == MIX:
                return total[block * 2 + side].astype(F32)
            return vec_near[block * 2 + side]

        def handle(slot, i):
            block, inside = block_of(slot)
            behind = (at.has_down, at.has_up)[slots[slot][1]]
            outer = slot - 2

            def work():
                crosses[slot][i].wait_recv()
                value = own_term(i, block) + cross_land[i][block].astype(F32)
                if outer < 0:
                    hop_send[i][slot] = value.astype(hop_send[i].dtype)
                    return

                @pl.when(behind)
                def _():
                    hops[outer][i].wait_recv()
                    hop_send[i][slot] = (value + hop_land[i][outer].astype(F32)).astype(
                        hop_send[i].dtype
                    )

                @pl.when(jnp.logical_not(behind))
                def _():
                    hop_send[i][slot] = value.astype(hop_send[i].dtype)

            when(inside, work)
            copies.begin(hops[slot][i], inside)

        def handle_all(distance, items):
            for slot in range(last):
                if slots[slot][0] == distance:
                    for i in items:
                        handle(slot, i)

        def close(i, target):
            crosses[last][i].wait_recv()
            target[...] = own_term(i, spot) + cross_land[i][spot].astype(F32)
            for way, behind in enumerate((at.has_down, at.has_up)):

                def add(way=way):
                    hops[last - 2 + way][i].wait_recv()
                    target[...] += hop_land[i][last - 2 + way].astype(F32)

                when(behind, add)

        for i, one, two in ((FC, "fc_far", "fc_far_side"), (PROJ, "proj_side", "proj_side_far")):
            loads[one].wait()
            loads[two].wait()
            for block in range(line):
                cross_send[i][block] = (
                    held[one][block].astype(F32) + held[two][block].astype(F32)
                ).astype(LOW)
            cross(far_end, [i])
            cross(far_end - 1, [i])
        loads["last"].wait()
        last_copy = copies.start(held["last"].at[1], last_land, at.mate)
        loads["grad_mixed"].wait()
        loads["mix"].wait()

        def row_part(index):
            @pl.loop(0, rows // 256)
            def _(i):
                span = pl.ds(pl.multiple_of(i * 256, 256), 256)
                weight = held["mix"][...].reshape(width, width)
                part[index, span] = nt(held["grad_mixed"][index, span], weight).astype(LOW)

        row_part(corner_row)
        mate_far = copies.start(part.at[corner_row], mate_land.at[1], at.mate)
        row_part(mate_row)
        mate_own = copies.start(part.at[mate_row], mate_land.at[0], at.mate)
        for name in ("fc_near", "fc_near_side", "proj_near", "proj_near_far"):
            loads[name].wait()
        handle_all(far_end, (FC, PROJ))
        row_part(far_row)
        mate_far.wait_recv()
        far_made = []
        for i in range(2):
            span = pl.ds(i * half_rows, half_rows)
            far_send[span] = (
                mate_land[1, span].astype(F32) + part[far_row, span].astype(F32)
            ).astype(LOW)
            far_made.append(copies.start(far_send.at[span], far_land.at[span], at.far))
        row_part(tensor)
        if far_end > 1:
            handle_all(far_end - 1, (FC, PROJ))
        for distance in range(far_end - 2, -1, -1):
            cross(distance, (FC, PROJ))

        for name in ("group", "out_own", "out_far", "vec_all", "vec_part"):
            loads[name].wait()

        def outer_product(i, carry):
            sums, columns = carry
            block, start = i // (rows // 256), (i % (rows // 256)) * 256
            span = pl.ds(pl.multiple_of(start, 256), 256)
            grad = held["grad_mixed"][block, span]
            sums = sums + tn(held["group"][block, span], grad)
            return sums, columns + jnp.sum(grad.astype(F32), axis=0, keepdims=True)

        plain = jnp.zeros((width, width), F32)
        columns = jnp.zeros((1, width), F32)
        plain, columns = lax.fori_loop(0, group // 256, outer_product, (plain, columns))
        turned = held["vec_all"][...].T
        weight = held["mix"][...].reshape(width, width).astype(F32)
        gain_grad = jnp.sum(plain * weight, axis=1, keepdims=True)
        shift_grad = jnp.sum(weight * columns, axis=1, keepdims=True)
        scaled = plain * turned[:, 0:1] + turned[:, 1:2] * columns
        extras = []
        out_sum = held["out_own"][...].astype(F32) + held["out_far"][...].astype(F32)
        for p in range(3):
            piece = out_sum[p * HD : (p + 1) * HD]
            extras.append(jnp.zeros((width, WIDE - 128), F32))
            extras.append(jnp.concatenate([jnp.zeros((128 - HD, width), F32), piece], axis=0).T)
        scaled = scaled + jnp.concatenate(extras, axis=1)
        for k in range(n_dp):
            total[k] = scaled[k * shard : (k + 1) * shard].astype(LOW)
        for block in range(line):
            cross_send[MIX][block] = total[block * 2 + 1 - side]
        cross(far_end, [MIX])
        cross(far_end - 1, [MIX])
        vec_mine[...] = held["vec_part"][...]
        flat = jnp.concatenate(
            [gain_grad, shift_grad, jnp.zeros((width, 6), F32)], axis=1
        ).T
        vec_mine[0:2] = flat[0:2]
        vec_lane = lax.broadcasted_iota(jnp.int32, (1, width), 1)
        in_part = (vec_lane >= tensor * (NH * HD)) & (vec_lane < (tensor + 1) * (NH * HD))
        for row, low in ((2, 0), (3, 2 * WIDE)):
            line_up = jnp.concatenate([columns[:, low : low + WIDE]] + [columns[:, 0:WIDE]] * 2, axis=1)
            placed = jnp.zeros((1, width), F32)
            for t in range(4):
                shifted = pltpu.roll(line_up, t * NH * HD, 1)
                placed = jnp.where(tensor == t, shifted, placed)
            vec_mine[row : row + 1] = jnp.where(in_part, placed, 0.0)
        vec_made = [
            copies.start(vec_mine, vec_land.at[i], device)
            for i, device in enumerate((at.mate, at.far, at.corner))
        ]
        for distance in range(far_end - 2, 0, -1):
            handle_all(distance, (FC, PROJ))
        for copy in vec_made:
            copy.wait_recv()
        vec_sum = vec_mine[...] + vec_land[0] + vec_land[1] + vec_land[2]
        for k in range(n_dp):
            vec_near[k] = pltpu.roll(vec_sum, (width - k * shard) % width, 1)[:, 0:128]
        for block in range(line):
            cross_send[VEC][block] = vec_near[block * 2 + 1 - side]
        cross(far_end, [VEC])
        cross(far_end - 1, [VEC])
        for distance in range(far_end, 0, -1):
            handle_all(distance, (MIX, VEC))
            if distance >= 2:
                cross(distance - 2, (MIX, VEC))

        for name in ("hidden", "grad_middle", "middle", "positions"):
            loads[name].wait()
        last_copy.wait_recv()
        first_row = tensor * rows
        last_bias = held["vec_all"][7:8]
        gain = held["vec_all"][0:1]
        mate_own.wait_recv()
        for copy in far_made:
            copy.wait_recv()
        tile = 4 * window

        @pl.loop(0, rows // tile)
        def _(i):
            start = pl.multiple_of(i * tile, tile)
            span = pl.ds(start, tile)
            ids = first_row + start + lax.broadcasted_iota(jnp.int32, (tile, 1), 0)
            final = (
                held["middle"][span]
                + held["last"][0, span].astype(F32)
                + last_land[span].astype(F32)
                + last_bias
            )
            block_out[span] = jnp.where(ids < scalar_ref[2], final, 0.0).astype(LOW)
            grad = (
                part[tensor, span].astype(F32)
                + mate_land[0, span].astype(F32)
                + far_land[span].astype(F32)
            )
            normed, inverse = normalize(held["hidden"][span].astype(F32))
            grad = held["grad_middle"][span] + norm_back(normed, inverse, grad, gain)
            for w in range(4):
                spot_row = held["positions"][pl.ds(i * 4 + w, 1)][:, 0:1] - (i * 4 + w) * window
                here = lax.broadcasted_iota(jnp.int32, (window, 1), 0) == spot_row
                piece = grad[w * window : (w + 1) * window]
                tokens_out[pl.ds(pl.multiple_of(start + w * window, window), window)] = jnp.where(
                    here, 0.0, piece
                )
                thoughts_out[pl.ds(i * 4 + w, 1)] = jnp.sum(
                    jnp.where(here, piece, 0.0), axis=0, keepdims=True
                )

        for i in (FC, PROJ, MIX):
            close(i, out[i])
        close(VEC, vec_out)
        copies.finish()

    f32 = lambda *shape: jax.ShapeDtypeStruct(shape, F32)
    outputs = (
        f32(shard, width), f32(shard, width), f32(shard, width), f32(VEC_ROWS, 128),
        f32(rows, width), f32(latents, width), jax.ShapeDtypeStruct((rows, width), LOW),
    )
    scratch = [pltpu.VMEM(arrays[name].shape, arrays[name].dtype) for name in names]
    for number in (line, line, last, last):
        scratch += [pltpu.VMEM((number, shard, width), LOW)] * 3
        scratch.append(pltpu.VMEM((number, VEC_ROWS, 128), F32))
    scratch += [
        pltpu.VMEM((4, rows, width), LOW),
        pltpu.VMEM((2, rows, width), LOW),
        pltpu.VMEM((rows, width), LOW),
        pltpu.VMEM((rows, width), LOW),
        pltpu.VMEM((rows, width), LOW),
        pltpu.VMEM((n_dp, shard, width), LOW),
        pltpu.VMEM((VEC_ROWS, width), F32),
        pltpu.VMEM((3, VEC_ROWS, width), F32),
        pltpu.VMEM((n_dp, VEC_ROWS, 128), F32),
    ]
    return comm_call(
        kernel,
        "finish_grads",
        outputs,
        (scalars, *arrays.values()),
        [pl.BlockSpec(memory_space=pltpu.SMEM)] + [ANY] * len(names),
        (VM,) * len(outputs),
        (2 * last + 1) * 4 + 1 + 2 + 2 + 3,
        cid,
        scratch=scratch,
        local=len(names),
        limit=63 << 20,
    )


def unit_kernel(add, line, live_ref, *refs):
    refs = list(refs)
    rows_ref, grad_in = refs[:2]
    pieces, bias_ref = refs[2:6], refs[6]
    refs = refs[7:]
    if add:
        last_in, two_in = refs[:2]
        refs = refs[2:]
    last_ref, two_ref, fc_near, fc_side, proj_near, proj_side, bias_grad_ref = refs[:7]
    fc_all, proj_all, fc_sum, proj_sum = refs[7:]
    step = pl.program_id(0)
    side, tensor, live = live_ref[0], live_ref[1], live_ref[2]

    @pl.when(step == 0)
    def _():
        for full, near, across in ((fc_all, *pieces[:2]), (proj_all, *pieces[2:])):
            for i in range(line):
                full[2 * i + side] = near[i]
                full[2 * i + 1 - side] = across[i]
        fc_sum[...] = jnp.zeros_like(fc_sum)
        proj_sum[...] = jnp.zeros_like(proj_sum)
        bias_grad_ref[...] = jnp.zeros_like(bias_grad_ref)

    count, width = rows_ref.shape
    half = pl.num_programs(0) // 2
    block = jnp.where(step < half, tensor, tensor + 1 - 2 * (tensor % 2))
    first = block * (half * count) + (step % half) * count
    alive = first + lax.broadcasted_iota(jnp.int32, (count, 1), 0) < live
    rows = rows_ref[...]
    grad = jnp.where(alive, grad_in[...], jnp.zeros_like(grad_in))
    fc = fc_all[...].reshape(width, -1)
    proj = proj_all[...].reshape(width, -1)
    inner = nn(rows, fc) + bias_ref[...]
    square = inner * inner
    bend = jnp.tanh(GELU_SCALE * inner * (1.0 + GELU_CUBE * square))
    half = 0.5 * (1.0 + bend)
    activated = (inner * half).astype(LOW)
    slope = half + 0.5 * inner * (1.0 - bend * bend) * GELU_SCALE * (1.0 + 3.0 * GELU_CUBE * square)
    grad_inner = (nn(grad, proj) * slope).astype(LOW)
    last = nt(activated, proj)
    two = nt(grad_inner, fc)
    if add:
        last, two = last + last_in[...], two + two_in[...]
    last_ref[...] = last.astype(last_ref.dtype)
    two_ref[...] = two.astype(two_ref.dtype)
    fc_sum[...] += tn(rows, grad_inner)
    proj_sum[...] += tn(grad, activated)
    bias_grad_ref[...] += jnp.sum(grad_inner.astype(F32), axis=0, keepdims=True)

    @pl.when(step == pl.num_programs(0) - 1)
    def _():
        shard = fc_near.shape[1]
        for sums, near, across in ((fc_sum, fc_near, fc_side), (proj_sum, proj_near, proj_side)):
            for i in range(line):
                even = sums[2 * i * shard : (2 * i + 1) * shard].astype(LOW)
                odd = sums[(2 * i + 1) * shard : (2 * i + 2) * shard].astype(LOW)
                near[i] = jnp.where(side == 0, even, odd)
                across[i] = jnp.where(side == 0, odd, even)


def units_both_ways(scalars, rows, grad, pieces, bias, before):
    count, width = rows.shape
    line, shard, units = pieces[0].shape
    tile = pl.BlockSpec((ROW_TILE, width), lambda i: (i, 0))
    fixed = lambda shape: pl.BlockSpec(shape, lambda i: (0,) * len(shape))
    add = before is not None
    kind = LOW if add else F32
    return pl.pallas_call(
        functools.partial(unit_kernel, add, line),
        grid=(count // ROW_TILE,),
        out_shape=(
            jax.ShapeDtypeStruct((count, width), kind),
            jax.ShapeDtypeStruct((count, width), kind),
        )
        + (jax.ShapeDtypeStruct((line, shard, units), LOW),) * 4
        + (jax.ShapeDtypeStruct((1, units), F32),        ),
        in_specs=[pl.BlockSpec(memory_space=pltpu.SMEM), tile, tile]
        + [fixed((line, shard, units))] * 4
        + [fixed((1, units))]
        + [tile] * (2 if add else 0),
        out_specs=(tile, tile) + (fixed((line, shard, units)),) * 4 + (fixed((1, units)),),
        scratch_shapes=[pltpu.VMEM((2 * line, shard, units), LOW)] * 2
        + [pltpu.VMEM((width, units), F32)] * 2,
        compiler_params=pltpu.CompilerParams(
            dimension_semantics=("arbitrary",), vmem_limit_bytes=56 << 20
        ),
        cost_estimate=pl.CostEstimate(
            flops=12 * count * width * units,
            bytes_accessed=24 * count * width,
            transcendentals=count * units,
        ),
        name="units_second" if add else "units_first",
    )(scalars, rows, grad, *pieces, bias, *(before or ()))


def normalize(values):
    center = jnp.mean(values, axis=-1, keepdims=True)
    offset = values - center
    spread = jnp.mean(offset * offset, axis=-1, keepdims=True)
    inverse = lax.rsqrt(spread + EPSILON)
    return offset * inverse, inverse


def norm_back(normed, inverse, grad, gain):
    scaled = grad * gain
    center = jnp.mean(scaled, axis=-1, keepdims=True)
    along = jnp.mean(scaled * normed, axis=-1, keepdims=True)
    return inverse * (scaled - center - normed * along)


def product(equation, left, right):
    return jnp.einsum(equation, left, right, preferred_element_type=F32)


def pack_three(qkv, out_turned):
    depth = qkv.shape[0]
    parts = jnp.transpose(qkv.reshape(depth, NH, 3, HD), (0, 2, 1, 3))
    extra = out_turned.reshape(depth, 3, 1, HD)
    return jnp.concatenate([parts, extra], axis=2).reshape(depth, 3 * WIDE)


def unpack_three(packed):
    depth = packed.shape[0]
    split = packed.reshape(depth, 3, NH + 1, HD)
    qkv = jnp.transpose(split[:, :, :NH], (0, 2, 1, 3)).reshape(depth, 3 * NH * HD)
    return qkv, split[:, :, NH].reshape(depth, NH * HD)


def per_device(
    tokens,
    thoughts,
    positions,
    lengths,
    attn_norm_gain,
    attn_norm_shift,
    qkv_weight,
    qv_bias,
    attn_out_weight,
    attn_out_bias,
    mlp_norm_gain,
    mlp_norm_shift,
    fc_weight,
    fc_bias,
    proj_weight,
    proj_bias,
    cotangent,
):
    n_dp = lax.axis_size("dp")
    n_tensor = lax.axis_size("tensor")
    tensor = lax.axis_index("tensor")
    rows, width = tokens.shape
    slots = rows * n_tensor
    units = FF // n_tensor
    far = (tensor + 2) % n_tensor
    swap_far = [(i, (i + 2) % n_tensor) for i in range(n_tensor)]

    window = rows // thoughts.shape[0]
    starts = jnp.arange(thoughts.shape[0], dtype=jnp.int32) * window
    placed = (
        jnp.arange(window, dtype=jnp.int32)[None, :] == (positions - starts)[:, None]
    )[:, :, None]
    tokens_low = jnp.where(
        placed, thoughts[:, None, :], tokens.reshape(-1, window, width)
    ).reshape(rows, width)

    ends = [lengths[0, 0]]
    for i in range(1, SEQ_DEV):
        ends.append(ends[-1] + lengths[0, i])
    segment_ends = jnp.stack(ends)
    live_slots = ends[-1]

    share = width // (n_dp * n_tensor)
    small = [
        attn_norm_gain, attn_norm_shift, qv_bias[0], qv_bias[1], attn_out_bias,
        mlp_norm_gain, mlp_norm_shift, proj_bias, fc_bias,
    ]
    vectors = jnp.concatenate([jnp.pad(v[None], ((0, 0), (0, 128 - v.shape[0]))) for v in small])
    vectors = jnp.pad(vectors, ((0, VEC_ROWS - len(small)), (0, 0)))

    (
        group_low, mixed, mix_all, fc_near, fc_side, fc_far_near, proj_near, grad_rows, out_own,
        vec_all,
    ) = gather_inputs(
        tokens_low, cotangent, fc_weight, proj_weight.T,
        pack_three(qkv_weight, attn_out_weight.T), vectors, n_dp,
    )
    mix_own = mix_all.reshape(width, -1)
    group_low = group_low.reshape(slots, width)
    mixed = mixed.reshape(slots, -1)
    swap_side = [(i, i + 1 - 2 * (i % 2)) for i in range(n_dp)]
    out_far = lax.ppermute(out_own, "tensor", swap_far)
    proj_far_near = lax.ppermute(proj_near, "tensor", swap_far)
    fc_far_side = lax.ppermute(fc_far_near, "dp", swap_side)
    proj_side = lax.ppermute(proj_near, "dp", swap_side)
    hidden_bias = jnp.transpose(
        vec_all[8 : 8 + n_tensor].reshape(n_tensor, n_dp, -1), (1, 0, 2)
    ).reshape(n_tensor, units)

    attended, stats = attend(segment_ends, mixed)
    sent, out_far, proj_far_near = lax.optimization_barrier((attended, out_far, proj_far_near))
    proj_far_side = lax.ppermute(proj_far_near, "dp", swap_side)
    both, middle, chip_two = after_attention(
        sent, out_own, out_far, tokens_low, vec_all, n_dp, 1
    )
    chip_two, proj_far_side = lax.optimization_barrier((chip_two, proj_far_side))
    chip_two = chip_two.reshape(2 * rows, width)
    chip_grad = grad_rows.reshape(2 * rows, width)

    def bias_row(index):
        return lax.dynamic_slice_in_dim(hidden_bias, index, 1, 0)

    scalars = jnp.stack([lax.axis_index("dp") % 2, tensor, live_slots]).astype(jnp.int32)
    first = units_both_ways(
        scalars, chip_two, chip_grad,
        (fc_far_near, fc_far_side, proj_far_near, proj_far_side), bias_row(far), None,
    )
    far_fc_near, far_fc_side, far_proj_near, far_proj_side, far_fc_bias = first[2:]
    proj_near_far = lax.ppermute(far_proj_near, "tensor", swap_far)
    proj_side_far = lax.ppermute(far_proj_side, "tensor", swap_far)
    fc_far_side_in = lax.ppermute(far_fc_side, "dp", swap_side)
    second = units_both_ways(
        scalars, chip_two, chip_grad, (fc_near, fc_side, proj_near, proj_side), bias_row(tensor),
        first[:2],
    )
    last_part, grad_two_part, fc_near_grad, fc_side_grad, proj_near_grad, proj_side_grad = second[:6]
    fc_near_side_in = lax.ppermute(fc_side_grad, "dp", swap_side)
    grad_fc_bias, far_fc_bias = second[6][0], far_fc_bias[0]
    grad_heads, grad_middle, grad_out, far_out, vec_part = before_attention_back(
        scalars, grad_two_part.reshape(2, rows, width), middle, cotangent, both, out_own, out_far,
        vec_all, n_dp, 2,
    )
    grad_heads, proj_near_far, fc_far_side_in, far_out = lax.optimization_barrier(
        (grad_heads, proj_near_far, fc_far_side_in, far_out)
    )
    far_out = lax.ppermute(far_out, "tensor", swap_far)
    last_low = last_part.reshape(2, rows, width)

    grad_mixed = attend_back(segment_ends, mixed, attended, stats, grad_heads)
    bias_part = jnp.zeros((n_tensor, units), F32)
    bias_part = lax.dynamic_update_slice_in_dim(bias_part, grad_fc_bias[None], tensor, 0)
    bias_part = lax.dynamic_update_slice_in_dim(bias_part, far_fc_bias[None], far, 0)
    bias_part = jnp.transpose(bias_part.reshape(n_dp, n_tensor, -1), (1, 0, 2))
    vec_part += jnp.pad(
        bias_part.reshape(n_tensor, width), ((8, VEC_ROWS - 8 - n_tensor), (0, 0))
    )
    arrays = {
        "fc_far": far_fc_near, "fc_far_side": fc_far_side_in,
        "proj_side": proj_side_grad, "proj_side_far": proj_side_far,
        "grad_mixed": grad_mixed.reshape(n_tensor, rows, width), "mix": mix_all,
        "fc_near": fc_near_grad, "fc_near_side": fc_near_side_in,
        "proj_near": proj_near_grad, "proj_near_far": proj_near_far,
        "last": last_low,
        "group": group_low.reshape(n_tensor, rows, width),
        "out_own": grad_out, "out_far": far_out,
        "vec_all": vec_all, "vec_part": vec_part,
        "hidden": tokens_low, "grad_middle": grad_middle, "middle": middle,
        "positions": jnp.broadcast_to(positions[:, None], (positions.shape[0], 128)),
    }
    fc_grad, proj_grad, mix_grad, vec, grad_tokens, grad_thoughts, block_out = finish_grads(
        scalars, arrays, n_dp, 8
    )
    qkv_grad, out_grad = unpack_three(mix_grad)
    small_grads = lax.dynamic_slice_in_dim(vec[:8], tensor * share, share, 1)
    fc_bias_grad = lax.dynamic_slice_in_dim(vec, 8 + tensor, 1, 0)[0, : fc_bias.shape[0]]
    return (
        block_out,
        grad_tokens,
        grad_thoughts,
        small_grads[0],
        small_grads[1],
        qkv_grad,
        small_grads[2:4],
        out_grad.T,
        small_grads[4],
        small_grads[5],
        small_grads[6],
        fc_grad,
        fc_bias_grad,
        proj_grad.T,
        small_grads[7],
    )


def solution(mesh):
    rows = P(("dp", "tensor"), None)
    line = P(("dp", "tensor"))
    in_specs = (
        rows, rows, line, P("dp", None), line, line, P("dp", "tensor"),
        P(None, ("dp", "tensor")), P("tensor", "dp"), line, line, line,
        P("dp", "tensor"), line, P("tensor", "dp"), line, rows,
    )
    out_specs = (
        rows, rows, rows, line, line, P("dp", "tensor"), P(None, ("dp", "tensor")),
        P("tensor", "dp"), line, line, line, P("dp", "tensor"), line, P("tensor", "dp"), line,
    )
    return jax.shard_map(
        per_device, mesh=mesh, in_specs=in_specs, out_specs=out_specs, check_vma=False
    )
```

```python
import functools
import math

import jax
import jax.numpy as jnp
from jax import lax
from jax.experimental import pallas as pl
from jax.experimental.pallas import tpu as pltpu
from jax.sharding import PartitionSpec as P

H = 12
HD = 64
FF = 3072
SEQ_DEV = 3
EPSILON = 1e-05
MASKED = -1e30
NH = 3
SLABS = 2
WIDE = SLABS * 128
BQ = 512
BK = 512
VEC_ROWS = 16
ROW_TILE = 256
GELU_SCALE = math.sqrt(2.0 / math.pi)
GELU_CUBE = 0.044715
MESH = pl.DeviceIdType.MESH
ANY = pl.BlockSpec(memory_space=pl.ANY)
VM = pl.BlockSpec(memory_space=pltpu.VMEM)
LOW = jnp.bfloat16
F32 = jnp.float32


def nn(a, b):
    return lax.dot_general(a, b, (((1,), (0,)), ((), ())), preferred_element_type=jnp.float32)


def nt(a, b):
    return lax.dot_general(a, b, (((1,), (1,)), ((), ())), preferred_element_type=jnp.float32)


def tn(a, b):
    return lax.dot_general(a, b, (((0,), (0,)), ((), ())), preferred_element_type=jnp.float32)


def head_rows(slab, head):
    half = slab[(head % 2) * HD : (head % 2 + 1) * HD]
    zero = jnp.zeros_like(half)
    return jnp.concatenate([half, zero] if head % 2 == 0 else [zero, half], axis=0)


def ends_of(lengths_ref):
    ends = [lengths_ref[0, 0]]
    for i in range(1, SEQ_DEV):
        ends.append(ends[-1] + lengths_ref[0, i])
    return ends


def segment_start(ends, slots):
    start = jnp.zeros_like(slots)
    for i in range(SEQ_DEV):
        start = jnp.where(slots >= ends[i], ends[i], start)
    return start


def segment_stop(ends, slot, slots):
    stop = slots
    for i in reversed(range(SEQ_DEV)):
        stop = jnp.where(slot < ends[i], ends[i], stop)
    return stop


def attend_kernel(lengths_ref, mixed_ref, out_ref, stat_ref, qt_ref, vt_ref):
    tokens = mixed_ref.shape[0]
    ends = ends_of(lengths_ref)
    for first in range(0, tokens, BQ):
        rows = pl.ds(first, BQ)
        for slab in range(SLABS):
            lanes = slab * 128
            qt_ref[lanes : lanes + 128, rows] = (
                mixed_ref[rows, lanes : lanes + 128] * HD ** (-0.5)
            ).T
            vt_ref[lanes : lanes + 128, rows] = mixed_ref[
                rows, 2 * WIDE + lanes : 2 * WIDE + lanes + 128
            ].T

    def query_block(block, carry):
        first = pl.multiple_of(block * BQ, BQ)
        columns = pl.ds(first, BQ)
        start = segment_start(ends, first + lax.broadcasted_iota(jnp.int32, (1, BQ), 1))
        query_ids = first + lax.broadcasted_iota(jnp.int32, (BK, BQ), 1)
        queries = [
            head_rows(qt_ref[(h // 2) * 128 : (h // 2 + 1) * 128, columns], h) for h in range(NH)
        ]

        def key_block(key, state):
            base = pl.multiple_of(key * BK, BK)
            rows = pl.ds(base, BK)
            key_ids = base + lax.broadcasted_iota(jnp.int32, (BK, BQ), 0)
            allowed = (key_ids <= query_ids) & (key_ids >= start)
            result = []
            for h in range(NH):
                peak, total, acc = state[h]
                slab = h // 2
                scores = nn(mixed_ref[rows, WIDE + slab * 128 : WIDE + slab * 128 + 128], queries[h])
                scores = jnp.where(allowed, scores, MASKED)
                fresh = jnp.maximum(peak, jnp.max(scores, axis=0, keepdims=True))
                weight = jnp.exp(scores - fresh)
                decay = jnp.exp(peak - fresh)
                total = total * decay + jnp.sum(weight, axis=0, keepdims=True)
                values = vt_ref[h * HD : (h + 1) * HD, rows]
                acc = acc * decay + nn(values, weight.astype(jnp.bfloat16))
                result.append((fresh, total, acc))
            return tuple(result)

        empty = tuple(
            (
                jnp.full((1, BQ), MASKED, jnp.float32),
                jnp.zeros((1, BQ), jnp.float32),
                jnp.zeros((HD, BQ), jnp.float32),
            )
            for _ in range(NH)
        )
        state = lax.fori_loop(segment_start(ends, first) // BK, (block + 1) * (BQ // BK), key_block, empty)
        for h in range(NH):
            peak, total, acc = state[h]
            out_ref[h * HD : (h + 1) * HD, columns] = (acc / total).astype(jnp.bfloat16)
            stat_ref[h : h + 1, columns] = peak + jnp.log(total)
        return carry

    lax.fori_loop(0, tokens // BQ, query_block, 0)


def attend(lengths, mixed):
    tokens = mixed.shape[0]
    vm = pl.BlockSpec(memory_space=pltpu.VMEM)
    return pl.pallas_call(
        attend_kernel,
        out_shape=(
            jax.ShapeDtypeStruct((NH * HD, tokens), jnp.bfloat16),
            jax.ShapeDtypeStruct((8, tokens), jnp.float32),
        ),
        in_specs=[pl.BlockSpec(memory_space=pltpu.SMEM), vm],
        out_specs=(vm, vm),
        scratch_shapes=[pltpu.VMEM((WIDE, tokens), jnp.bfloat16)] * 2,
        compiler_params=pltpu.CompilerParams(vmem_limit_bytes=40 << 20),
        cost_estimate=pl.CostEstimate(
            flops=8 * tokens * tokens * NH * HD,
            bytes_accessed=16 * tokens * WIDE,
            transcendentals=tokens * tokens,
        ),
        name="attend",
    )(lengths, mixed)


def attend_back_kernel(
    lengths_ref, mixed_ref, out_ref, stat_ref, gradt_ref,
    gmixed_ref, qt_ref, kt_ref, grad_ref, delta_ref, dqt_ref
):
    tokens = mixed_ref.shape[0]
    ends = ends_of(lengths_ref)
    for first in range(0, tokens, BQ):
        rows = pl.ds(first, BQ)
        for slab in range(SLABS):
            lanes = slab * 128
            qt_ref[lanes : lanes + 128, rows] = (
                mixed_ref[rows, lanes : lanes + 128] * HD ** (-0.5)
            ).T
            kt_ref[lanes : lanes + 128, rows] = mixed_ref[rows, WIDE + lanes : WIDE + lanes + 128].T
        grad_ref[rows, 0:128] = gradt_ref[0:128, rows].T
        grad_ref[rows, 128:256] = jnp.concatenate(
            [gradt_ref[128:192, rows], jnp.zeros((64, BQ), jnp.bfloat16)], axis=0
        ).T
        for h in range(NH):
            product = gradt_ref[h * HD : (h + 1) * HD, rows].astype(jnp.float32) * out_ref[
                h * HD : (h + 1) * HD, rows
            ].astype(jnp.float32)
            delta_ref[h : h + 1, rows] = jnp.sum(product, axis=0, keepdims=True)
    dqt_ref[...] = jnp.zeros_like(dqt_ref)
    lane = lax.broadcasted_iota(jnp.int32, (BQ, 128), 1)

    def key_block(key, carry):
        base = pl.multiple_of(key * BK, BK)
        rows = pl.ds(base, BK)
        key_ids = base + lax.broadcasted_iota(jnp.int32, (BK, BQ), 0)

        def query_block(block, state):
            first = pl.multiple_of(block * BQ, BQ)
            columns = pl.ds(first, BQ)
            start = segment_start(ends, first + lax.broadcasted_iota(jnp.int32, (1, BQ), 1))
            query_ids = first + lax.broadcasted_iota(jnp.int32, (BK, BQ), 1)
            allowed = (key_ids <= query_ids) & (key_ids >= start)
            grad_keys = list(state[:SLABS])
            grad_values = list(state[SLABS:])
            for h in range(NH):
                slab = h // 2
                low, high = slab * 128, slab * 128 + 128
                queries = head_rows(qt_ref[low:high, columns], h)
                scores = nn(mixed_ref[rows, WIDE + low : WIDE + high], queries)
                probs = jnp.where(allowed, jnp.exp(scores - stat_ref[h : h + 1, columns]), 0.0)
                keep = (lane // HD) == (h % 2)
                grads = jnp.where(keep, grad_ref[columns, low:high], 0.0)
                grad_values[slab] += nn(probs.astype(jnp.bfloat16), grads)
                if h == NH - 1 and NH % 2 == 1:
                    grad_rows = jnp.concatenate(
                        [gradt_ref[h * HD : (h + 1) * HD, columns], jnp.zeros((HD, BQ), jnp.bfloat16)],
                        axis=0,
                    )
                else:
                    grad_rows = head_rows(gradt_ref[low:high, columns], h)
                grad_probs = nn(mixed_ref[rows, 2 * WIDE + low : 2 * WIDE + high], grad_rows)
                grad_scores = (probs * (grad_probs - delta_ref[h : h + 1, columns])).astype(
                    jnp.bfloat16
                )
                natural = mixed_ref[columns, low:high]
                grad_keys[slab] += nn(grad_scores, jnp.where(keep, natural, 0.0))
                dqt_ref[h * HD : (h + 1) * HD, columns] += nn(
                    kt_ref[h * HD : (h + 1) * HD, rows], grad_scores
                )
            return tuple(grad_keys) + tuple(grad_values)

        empty = (jnp.zeros((BK, 128), jnp.float32),) * (2 * SLABS)
        stop = segment_stop(ends, base + BK - 1, tokens)
        state = lax.fori_loop(key * BK // BQ, (stop - 1) // BQ + 1, query_block, empty)
        for slab in range(SLABS):
            low = slab * 128
            gmixed_ref[rows, WIDE + low : WIDE + low + 128] = (
                state[slab] * HD ** (-0.5)
            ).astype(jnp.bfloat16)
            gmixed_ref[rows, 2 * WIDE + low : 2 * WIDE + low + 128] = state[SLABS + slab].astype(
                jnp.bfloat16
            )
        return carry

    lax.fori_loop(0, tokens // BK, key_block, 0)
    for first in range(0, tokens, BQ):
        rows = pl.ds(first, BQ)
        for slab in range(SLABS):
            low = slab * 128
            gmixed_ref[rows, low : low + 128] = (
                (dqt_ref[low : low + 128, rows] * HD ** (-0.5)).T.astype(jnp.bfloat16)
            )


def attend_back(lengths, mixed, out, stat, gradt):
    tokens = mixed.shape[0]
    vm = pl.BlockSpec(memory_space=pltpu.VMEM)
    return pl.pallas_call(
        attend_back_kernel,
        out_shape=jax.ShapeDtypeStruct((tokens, 3 * WIDE), jnp.bfloat16),
        in_specs=[pl.BlockSpec(memory_space=pltpu.SMEM)] + [vm] * 4,
        out_specs=vm,
        scratch_shapes=[
            pltpu.VMEM((WIDE, tokens), jnp.bfloat16),
            pltpu.VMEM((WIDE, tokens), jnp.bfloat16),
            pltpu.VMEM((tokens, WIDE), jnp.bfloat16),
            pltpu.VMEM((8, tokens), jnp.float32),
            pltpu.VMEM((WIDE, tokens), jnp.float32),
        ],
        compiler_params=pltpu.CompilerParams(vmem_limit_bytes=50 << 20),
        cost_estimate=pl.CostEstimate(
            flops=20 * tokens * tokens * NH * HD,
            bytes_accessed=32 * tokens * WIDE,
            transcendentals=tokens * tokens,
        ),
        name="attend_back",
    )(lengths, mixed, out, stat, gradt)


class Copies:
    def __init__(self, send, recv):
        self.send, self.recv, self.made, self.started = send, recv, 0, []

    def plan(self, source, target, device):
        index = self.made
        self.made += 1
        return pltpu.make_async_remote_copy(
            src_ref=source,
            dst_ref=target,
            send_sem=self.send.at[index],
            recv_sem=self.recv.at[index],
            device_id=device,
            device_id_type=MESH,
        )

    def begin(self, copy, condition=None):
        self.started.append((copy, condition))
        when(condition, copy.start)

    def start(self, source, target, device):
        copy = self.plan(source, target, device)
        self.begin(copy)
        return copy

    def finish(self):
        for copy, condition in self.started:
            when(condition, copy.wait_send)


def when(condition, action):
    if condition is None:
        action()
    else:
        pl.when(condition)(action)


def greet(devices):
    barrier = pltpu.get_barrier_semaphore()
    for device, condition in devices:
        when(
            condition,
            lambda device=device: pl.semaphore_signal(
                barrier, inc=1, device_id=device, device_id_type=MESH
            ),
        )
    present = [1 if condition is None else condition.astype(jnp.int32) for _, condition in devices]
    pl.semaphore_wait(barrier, sum(present))


class Place:
    def __init__(self, line):
        self.dp = dp = lax.axis_index("dp")
        self.tensor = tensor = lax.axis_index("tensor")
        self.spot, self.side = spot, side = dp // 2, dp % 2
        self.chip, self.core = tensor // 2, tensor % 2
        self.has_up, self.has_down = spot + 1 < line, spot > 0
        self.up = (jnp.minimum(spot + 1, line - 1) * 2 + side, tensor)
        self.down = (jnp.maximum(spot - 1, 0) * 2 + side, tensor)
        self.across = (spot * 2 + 1 - side, tensor)
        self.mate = (dp, tensor + 1 - 2 * (tensor % 2))
        self.far = (dp, (tensor + 2) % 4)
        self.corner = (dp, 3 - tensor)

    def everyone(self):
        return [
            (self.mate, None), (self.far, None), (self.corner, None), (self.across, None),
            (self.up, self.has_up), (self.down, self.has_down),
        ]


def comm_call(kernel, name, outputs, inputs, in_specs, out_specs, copies, cid, scratch=(), local=1, limit=50 << 20):
    return pl.pallas_call(
        kernel,
        out_shape=outputs,
        in_specs=in_specs,
        out_specs=out_specs,
        scratch_shapes=list(scratch)
        + [
            pltpu.SemaphoreType.DMA((copies,)),
            pltpu.SemaphoreType.DMA((copies,)),
            pltpu.SemaphoreType.DMA((local,)),
        ],
        compiler_params=pltpu.CompilerParams(
            collective_id=cid, has_side_effects=True, vmem_limit_bytes=limit
        ),
        name=name,
    )(*inputs)


def one_hot(rows, columns, shift, limit):
    lane = lax.broadcasted_iota(jnp.int32, (rows, columns), 0)
    spot = lax.broadcasted_iota(jnp.int32, (rows, columns), 1)
    return ((spot == lane + shift) & (lane < limit)).astype(LOW)


def gather_inputs(hidden, cotangent, fc, proj, mix, vectors, n_dp):
    line = n_dp // 2
    hops = line - 1
    rows, width = hidden.shape
    shard = fc.shape[0]
    half_rows = rows // 2
    share = width // (n_dp * 4)

    def kernel(
        hidden_ref, cot_ref, fc_ref, proj_ref, mix_ref, vec_ref,
        normed_out, mixed_out, mix_out, fc_near, fc_side, fc_far, proj_near, cot_out, out_out,
        vec_out,
        land, mix_land, tiles, tile_land, normed, mixed, out_turned, send, recv, local,
    ):
        at = Place(line)
        dp, tensor, spot, side = at.dp, at.tensor, at.spot, at.side
        mate_row, far_row, corner_row = at.mate[1], at.far[1], at.corner[1]
        greet(at.everyone())
        copies = Copies(send, recv)
        MIX, FC, PROJ, VEC = range(4)
        own = [mix_ref, fc_ref, proj_ref, tiles.at[dp]]

        def seat(item, position):
            if item == MIX:
                return mix_land.at[position * 2 + side]
            if item == FC:
                return fc_near.at[position]
            if item == PROJ:
                return proj_near.at[position]
            return tiles.at[position * 2 + side]

        def plan(item, hop):
            above, below = jnp.maximum(spot - hop, 0), jnp.minimum(spot + hop, line - 1)
            came_up = jnp.maximum(spot - 1 - hop, 0)
            came_down = jnp.minimum(spot + 1 + hop, line - 1)
            made = {
                "up": copies.plan(
                    own[item] if hop == 0 else seat(item, above), seat(item, above), at.up
                ),
                "down": copies.plan(
                    own[item] if hop == 0 else seat(item, below), seat(item, below), at.down
                ),
                "onward": [],
            }
            for position in (came_up, came_down):
                onward = []
                if item in (MIX, VEC):
                    onward.append(copies.plan(seat(item, position), seat(item, position), at.across))
                if item == FC:
                    onward.append(copies.plan(fc_near.at[position], fc_side.at[position], at.across))
                    onward.append(copies.plan(fc_near.at[position], fc_far.at[position], at.far))
                made["onward"].append(onward)
            return made

        plans = [[plan(item, hop) for hop in range(hops)] for item in range(4)]

        def launch(item):
            copies.begin(plans[item][0]["up"], at.has_up)
            copies.begin(plans[item][0]["down"], at.has_down)

        def handle(item, hop):
            made = plans[item][hop]
            for way, key, comes, goes in (
                (0, "up", spot - 1 - hop >= 0, at.has_up),
                (1, "down", spot + 1 + hop < line, at.has_down),
            ):
                when(comes, made[key].wait_recv)
                if hop + 1 < hops:
                    copies.begin(plans[item][hop + 1][key], comes & goes)
                for copy in made["onward"][way]:
                    copies.begin(copy, comes)

        def settle(item):
            for hop in range(hops):
                for way, comes in ((0, spot - 1 - hop >= 0), (1, spot + 1 + hop < line)):
                    for copy in plans[item][hop]["onward"][way]:
                        when(comes, copy.wait_recv)

        stays = []

        def stay(source, target):
            copy = pltpu.make_async_copy(source, target, local.at[len(stays)])
            copy.start()
            stays.append(copy)
            return copy

        vec_made = [
            copies.start(vec_ref, tile_land.at[i], device)
            for i, device in enumerate((at.mate, at.far, at.corner))
        ]
        parts = [pl.ds(0, half_rows), pl.ds(half_rows, half_rows)]
        launch(MIX)
        far_made = [
            copies.start(hidden_ref.at[part], land.at[far_row_here, part], at.far)
            for far_row_here in (2,)
            for part in parts
        ]
        mix_side = copies.start(mix_ref, mix_land.at[dp], at.across)
        launch(FC)
        fc_sides = [
            copies.start(fc_ref, fc_side.at[spot], at.across),
            copies.start(fc_ref, fc_far.at[spot], at.far),
        ]
        mate_made = copies.start(hidden_ref, land.at[1], at.mate)
        cot_made = copies.start(cot_ref, cot_out.at[1], at.mate)
        stay(cot_ref, cot_out.at[0])
        stay(fc_ref, fc_near.at[spot])
        stay(proj_ref, proj_near.at[spot])
        mix_land[dp] = mix_ref[...]
        for copy in vec_made:
            copy.wait_recv()
        merged = jnp.zeros((VEC_ROWS, 128), F32)
        bias_rows = jnp.zeros((VEC_ROWS, 128), F32)
        row_ids = lax.broadcasted_iota(jnp.int32, (VEC_ROWS, 128), 0)
        for i, index in enumerate((tensor, mate_row, far_row, corner_row)):
            tile = vec_ref[...] if i == 0 else tile_land[i - 1]
            merged += nn(tile, one_hot(128, 128, index * share, share))
            bias_rows = jnp.where(row_ids == 8 + index, tile[8:9].astype(F32), bias_rows)
        tiles[dp] = jnp.where(row_ids < 8, merged, bias_rows).astype(LOW)
        launch(VEC)
        vec_side = copies.start(tiles.at[dp], tiles.at[dp], at.across)

        def norm_rows(source, index):
            @pl.loop(0, rows // 128)
            def _(i):
                span = pl.ds(pl.multiple_of(i * 128, 128), 128)
                normed[index, span] = normalize(source[span].astype(F32))[0].astype(LOW)

            stay(normed.at[index], normed_out.at[index])

        def relay(i):
            far_made[i].wait_recv()
            return copies.start(land.at[2, parts[i]], land.at[3, parts[i]], at.mate)

        def mix_rows(index):
            @pl.loop(0, rows // 256)
            def _(i):
                span = pl.ds(pl.multiple_of(i * 256, 256), 256)
                turned = normed[index, span].astype(F32) * whole[0:1] + whole[1:2]
                weight = mix_land[...].reshape(width, width)
                mixed[index, span] = (nn(turned.astype(LOW), weight) + bias).astype(LOW)

            stay(mixed.at[index], mixed_out.at[index])

        norm_rows(hidden_ref, tensor)
        relayed = []
        for step in range(hops + 2):
            for item, hop in ((MIX, step), (VEC, step), (FC, step - 1), (PROJ, step - 2)):
                if 0 <= hop < hops:
                    handle(item, hop)
            if step == 0:
                launch(PROJ)
                mate_made.wait_recv()
                norm_rows(land.at[1], mate_row)
                relayed.append(relay(0))
            if step == 1:
                relayed.append(relay(1))
                norm_rows(land.at[2], far_row)
            if step == hops - 1:
                for copy in relayed:
                    copy.wait_recv()
                norm_rows(land.at[3], corner_row)
            if step == hops:
                mix_side.wait_recv()
                vec_side.wait_recv()
                settle(MIX)
                settle(VEC)
                whole = jnp.zeros((VEC_ROWS, width), F32)
                for i in range(n_dp):
                    whole += nn(tiles[i], one_hot(128, width, i * shard, shard))
                vec_out[...] = whole
                for i, block in enumerate((tensor, far_row)):
                    vec_out[12 + i : 13 + i] = units_row(whole[8:12], block, n_dp)
                lane = lax.broadcasted_iota(jnp.int32, (width, WIDE), 0)
                column = lax.broadcasted_iota(jnp.int32, (width, WIDE), 1)
                pick = (lane == column + tensor * (NH * HD)) & (column < NH * HD)
                picked = nn(whole.astype(LOW), pick.astype(LOW))
                bias = jnp.concatenate(
                    [picked[2:3], jnp.zeros((1, WIDE), F32), picked[3:4]], axis=1
                )
                mix_rows(tensor)
                mix_rows(mate_row)
        mix_rows(far_row)
        mix_rows(corner_row)
        stay(mix_land, mix_out)
        weight = mix_land[...].reshape(width, width)
        for part in range(3):
            low = part * WIDE + WIDE - 128
            turned = weight[:, low : low + 128].T
            out_turned[part * HD : (part + 1) * HD] = turned[128 - HD :]
        stay(out_turned, out_out)
        settle(FC)
        for copy in fc_sides:
            copy.wait_recv()
        cot_made.wait_recv()
        copies.finish()
        for copy in stays:
            copy.wait()

    low = lambda *shape: jax.ShapeDtypeStruct(shape, LOW)
    outputs = (
        low(4, rows, width), low(4, rows, width), low(n_dp, shard, width),
        low(line, shard, width), low(line, shard, width), low(line, shard, width),
        low(line, shard, width), low(2, rows, width), low(NH * HD, width),
        jax.ShapeDtypeStruct((VEC_ROWS, width), F32),
    )
    scratch = [
        pltpu.VMEM((4, rows, width), LOW),
        pltpu.VMEM((n_dp, shard, width), LOW),
        pltpu.VMEM((n_dp, VEC_ROWS, 128), LOW),
        pltpu.VMEM((3, VEC_ROWS, 128), LOW),
        pltpu.VMEM((4, rows, width), LOW),
        pltpu.VMEM((4, rows, width), LOW),
        pltpu.VMEM((NH * HD, width), LOW),
    ]
    return comm_call(
        kernel,
        "gather_inputs",
        outputs,
        (hidden, cotangent, fc, proj, mix, vectors),
        [VM] * 6,
        tuple([ANY] * (len(outputs) - 1)) + (VM,),
        3 + 2 + 1 + 2 + 2 + 1 + 2 + hops * (2 * 4 + 2 * 4),
        0,
        scratch=scratch,
        local=3 + 8 + 2,
    )


def after_attention(attended, out_own, out_far, hidden, vec_all, n_dp, cid):
    head_width, slots = attended.shape
    rows, width = hidden.shape
    half_rows = rows // 2

    def kernel(
        heads_ref, own_ref, far_ref, hidden_ref, vec_ref,
        both_out, middle_out, two_out,
        land, part, part_low, part_land, two, send, recv, local,
    ):
        at = Place(n_dp // 2)
        greet([(at.far, None), (at.mate, None)])
        copies = Copies(send, recv)
        cores = (at.core, 1 - at.core)
        made = [None, None]
        for i in (1, 0):
            theirs = pl.multiple_of(((1 - at.chip) * 2 + cores[i]) * rows, rows)
            made[i] = copies.start(heads_ref.at[:, pl.ds(theirs, rows)], land.at[i], at.far)
        stays = []

        def stay(source, target):
            stays.append(pltpu.make_async_copy(source, target, local.at[len(stays)]))
            stays[-1].start()

        spans = []
        for i in range(2):
            ours = pl.multiple_of((at.chip * 2 + cores[i]) * rows, rows)
            spans.append(pl.ds(ours, rows))
            stay(heads_ref.at[:, spans[i]], both_out.at[0, :, i * rows : (i + 1) * rows])
            part[i] = tn(heads_ref[:, spans[i]], own_ref[...])
        sums = None
        for i in (1, 0):
            made[i].wait_recv()
            stay(land.at[i], both_out.at[1, :, i * rows : (i + 1) * rows])
            part[i] += tn(land[i], far_ref[...])
            if i == 1:
                part_low[...] = part[1].astype(LOW)
                sums = copies.start(part_low, part_land, at.mate)
        sums.wait_recv()
        mated = []
        for piece in range(2):

            @pl.loop(0, half_rows // 128)
            def _(i):
                span = pl.ds(pl.multiple_of(piece * half_rows + i * 128, 128), 128)
                middle = (
                    hidden_ref[span].astype(F32)
                    + part[0, span]
                    + part_land[span].astype(F32)
                    + vec_ref[4:5]
                )
                middle_out[span] = middle
                two[span] = (normalize(middle)[0] * vec_ref[5:6] + vec_ref[6:7]).astype(LOW)

            span = pl.ds(piece * half_rows, half_rows)
            mated.append(copies.start(two.at[span], two_out.at[1, span], at.mate))
        stay(two, two_out.at[0])
        for copy in mated:
            copy.wait_recv()
        copies.finish()
        for copy in stays:
            copy.wait()

    return comm_call(
        kernel,
        "after_attention",
        (
            jax.ShapeDtypeStruct((2, head_width, 2 * rows), LOW),
            jax.ShapeDtypeStruct((rows, width), F32),
            jax.ShapeDtypeStruct((2, rows, width), LOW),
        ),
        (attended, out_own, out_far, hidden, vec_all),
        [VM] * 5,
        (ANY, VM, ANY),
        5,
        cid,
        scratch=[
            pltpu.VMEM((2, head_width, rows), LOW),
            pltpu.VMEM((2, rows, width), F32),
            pltpu.VMEM((rows, width), LOW),
            pltpu.VMEM((rows, width), LOW),
            pltpu.VMEM((rows, width), LOW),
        ],
        local=5,
    )


def before_attention_back(lengths, two, middle, cotangent, both, out_own, out_far, vec_all, n_dp, cid):
    _, rows, width = two.shape
    head_width = out_own.shape[0]
    half_rows = rows // 2

    def kernel(
        lengths_ref, two_ref, middle_ref, cot_ref, both_ref, own_ref, far_ref, vec_ref,
        heads_out, grad_out, own_out, far_out, vec_out,
        two_land, mid, stay_heads, sent_heads, send, recv, local,
    ):
        at = Place(n_dp // 2)
        greet([(at.far, None), (at.mate, None)])
        copies = Copies(send, recv)
        halves = [pl.ds(0, half_rows), pl.ds(half_rows, half_rows)]
        sums = [copies.start(two_ref.at[1, span], two_land.at[span], at.mate) for span in halves]
        vec_out[...] = jnp.zeros_like(vec_out)
        first_row = at.tensor * rows
        live = ends_of(lengths_ref)[-1]
        mated = []
        for piece in range(2):
            sums[piece].wait_recv()

            @pl.loop(0, half_rows // 128)
            def _(i):
                start = pl.multiple_of(piece * half_rows + i * 128, 128)
                span = pl.ds(start, 128)
                grad = two_ref[0, span].astype(F32) + two_land[span].astype(F32)
                normed, inverse = normalize(middle_ref[span])
                ids = first_row + start + lax.broadcasted_iota(jnp.int32, (128, 1), 0)
                final = jnp.where(ids < live, cot_ref[span].astype(F32), 0.0)
                total = final + norm_back(normed, inverse, grad, vec_ref[5:6])
                grad_out[span] = total
                mid[0, span] = total.astype(LOW)
                for row, term in ((4, total), (5, normed * grad), (6, grad), (7, final)):
                    vec_out[row : row + 1] += jnp.sum(term, axis=0, keepdims=True)

            mated.append(copies.start(mid.at[0, halves[piece]], mid.at[1, halves[piece]], at.mate))
        cores = (at.core, 1 - at.core)
        made, stays = [], []
        for i in range(2):
            if i == 1:
                for copy in mated:
                    copy.wait_recv()
            ours = pl.ds(pl.multiple_of((at.chip * 2 + cores[i]) * rows, rows), rows)
            sent_heads[i] = nt(far_ref[...], mid[i]).astype(LOW)
            made.append(copies.start(sent_heads.at[i], heads_out.at[:, ours], at.far))
            stay_heads[i] = nt(own_ref[...], mid[i]).astype(LOW)
            stays.append(
                pltpu.make_async_copy(stay_heads.at[i], heads_out.at[:, ours], local.at[i])
            )
            stays[-1].start()
        grads = mid[...].reshape(2 * rows, width)
        own_out[...] = nn(both_ref[0], grads).astype(LOW)
        far_out[...] = nn(both_ref[1], grads).astype(LOW)
        for copy in made:
            copy.wait_recv()
        copies.finish()
        for copy in stays:
            copy.wait()

    return comm_call(
        kernel,
        "before_attention_back",
        (
            jax.ShapeDtypeStruct((head_width, 4 * rows), LOW),
            jax.ShapeDtypeStruct((rows, width), F32),
            jax.ShapeDtypeStruct((head_width, width), LOW),
            jax.ShapeDtypeStruct((head_width, width), LOW),
            jax.ShapeDtypeStruct((VEC_ROWS, width), F32),
        ),
        (lengths, two, middle, cotangent, both, out_own, out_far, vec_all),
        [pl.BlockSpec(memory_space=pltpu.SMEM)] + [VM] * 7,
        (ANY,) + (VM,) * 4,
        6,
        cid,
        scratch=[
            pltpu.VMEM((rows, width), LOW),
            pltpu.VMEM((2, rows, width), LOW),
            pltpu.VMEM((2, head_width, rows), LOW),
            pltpu.VMEM((2, head_width, rows), LOW),
        ],
        local=2,
    )


def finish_grads(lengths, arrays, n_dp, cid):
    names = list(arrays)
    line = n_dp // 2
    shard = arrays["mix"].shape[1]
    rows, width = arrays["hidden"].shape
    half_rows = rows // 2
    group = 4 * rows
    latents = arrays["positions"].shape[0]
    window = rows // latents
    far_end = line - 1
    slots = [(distance, way) for distance in range(far_end, 0, -1) for way in (0, 1)] + [(0, 0)]
    last = len(slots) - 1
    share = width // (n_dp * 4)
    FC, PROJ, MIX, VEC = range(4)

    def kernel(lengths_ref, *refs):
        refs = list(refs)

        def take(number):
            taken = refs[:number]
            del refs[:number]
            return taken

        source = dict(zip(names, take(len(names))))
        fc_out, proj_out, mix_out, vec_out, tokens_out, thoughts_out, block_out = take(7)
        held = dict(zip(names, take(len(names))))
        cross_send, cross_land = [None, None] + take(2), [None, None] + take(2)
        hop_send, hop_land = take(4), take(4)
        (
            part, mate_land, far_send, far_land, last_land, total, vec_mine, vec_land, vec_near,
            plain_sum, column_sum, send, recv, local,
        ) = refs
        out = [fc_out, proj_out, mix_out, None]
        at = Place(line)
        tensor, spot, side = at.tensor, at.spot, at.side
        mate_row, far_row, corner_row = at.mate[1], at.far[1], at.corner[1]
        copies = Copies(send, recv)
        loads = {}
        for i, name in enumerate(names):
            loads[name] = pltpu.make_async_copy(source[name], held[name], local.at[i])

        def load(*group):
            for name in group:
                loads[name].start()

        load("fc_near", "fc_near_side", "fc_cross", "proj_near", "proj_near_far", "proj_cross")
        load("grad_mixed", "mix")
        greet(at.everyone())

        def block_of(slot):
            distance, way = slots[slot]
            if way == 0:
                return jnp.minimum(spot + distance, far_end), spot + distance < line
            return jnp.maximum(spot - distance, 0), spot - distance >= 0

        crosses, hops = [], []
        for slot in range(len(slots)):
            block, _ = block_of(slot)
            crosses.append(
                {
                    i: copies.plan(cross_send[i].at[block], cross_land[i].at[block], at.across)
                    for i in (MIX, VEC)
                }
            )
            if slot < last:
                hops.append(
                    [
                        copies.plan(
                            hop_send[i].at[slot],
                            hop_land[i].at[slot],
                            (at.up, at.down)[slots[slot][1]],
                        )
                        for i in range(4)
                    ]
                )

        def cross(distance, items):
            for slot in range(len(slots)):
                if slots[slot][0] == distance:
                    for i in items:
                        copies.begin(crosses[slot][i], block_of(slot)[1])

        terms = (
            ("fc_near", "fc_near_side", "fc_cross"),
            ("proj_near", "proj_near_far", "proj_cross"),
        )

        def own_term(i, block):
            if i in (FC, PROJ):
                return sum(held[name][block].astype(F32) for name in terms[i])
            if i == MIX:
                return total[block * 2 + side].astype(F32)
            return vec_near[block * 2 + side]

        def handle(slot, i):
            block, inside = block_of(slot)
            behind = (at.has_down, at.has_up)[slots[slot][1]]
            outer = slot - 2

            def work():
                value = own_term(i, block)
                if i in (MIX, VEC):
                    crosses[slot][i].wait_recv()
                    value = value + cross_land[i][block].astype(F32)
                if outer < 0:
                    hop_send[i][slot] = value.astype(hop_send[i].dtype)
                    return

                @pl.when(behind)
                def _():
                    hops[outer][i].wait_recv()
                    hop_send[i][slot] = (value + hop_land[i][outer].astype(F32)).astype(
                        hop_send[i].dtype
                    )

                @pl.when(jnp.logical_not(behind))
                def _():
                    hop_send[i][slot] = value.astype(hop_send[i].dtype)

            when(inside, work)
            copies.begin(hops[slot][i], inside)

        def handle_all(distance, items):
            for slot in range(last):
                if slots[slot][0] == distance:
                    for i in items:
                        handle(slot, i)

        def close(i, target):
            value = own_term(i, spot)
            if i in (MIX, VEC):
                crosses[last][i].wait_recv()
                value = value + cross_land[i][spot].astype(F32)
            target[...] = value
            for way, behind in enumerate((at.has_down, at.has_up)):

                def add(way=way):
                    hops[last - 2 + way][i].wait_recv()
                    target[...] += hop_land[i][last - 2 + way].astype(F32)

                when(behind, add)

        for name in ("fc_near", "fc_near_side", "fc_cross", "proj_near", "proj_near_far", "proj_cross"):
            loads[name].wait()
        handle_all(far_end, (FC, PROJ))
        load("group", "out_own", "out_far", "vec_all", "vec_part", "bias_own", "bias_far")
        load("last", "hidden", "grad_middle", "middle", "positions")
        loads["grad_mixed"].wait()
        loads["mix"].wait()

        def row_part(index):
            @pl.loop(0, rows // 256)
            def _(i):
                span = pl.ds(pl.multiple_of(i * 256, 256), 256)
                weight = held["mix"][...].reshape(width, width)
                part[index, span] = nt(held["grad_mixed"][index, span], weight).astype(LOW)

        row_part(corner_row)
        mate_far = copies.start(part.at[corner_row], mate_land.at[1], at.mate)
        row_part(mate_row)
        mate_own = copies.start(part.at[mate_row], mate_land.at[0], at.mate)
        row_part(far_row)
        mate_far.wait_recv()
        far_made = []
        for i in range(2):
            span = pl.ds(i * half_rows, half_rows)
            far_send[span] = (
                mate_land[1, span].astype(F32) + part[far_row, span].astype(F32)
            ).astype(LOW)
            far_made.append(copies.start(far_send.at[span], far_land.at[span], at.far))
        row_part(tensor)
        if far_end > 1:
            handle_all(far_end - 1, (FC, PROJ))
        loads["last"].wait()
        last_copy = copies.start(held["last"].at[1], last_land, at.mate)
        for name in ("group", "out_own", "out_far", "vec_all", "vec_part", "bias_own", "bias_far"):
            loads[name].wait()

        plain_sum[...] = jnp.zeros_like(plain_sum)
        column_sum[...] = jnp.zeros_like(column_sum)

        @pl.loop(0, group // 256)
        def _(i):
            block, start = i // (rows // 256), (i % (rows // 256)) * 256
            span = pl.ds(pl.multiple_of(start, 256), 256)
            grad = held["grad_mixed"][block, span]
            plain_sum[...] += tn(held["group"][block, span], grad)
            column_sum[...] += jnp.sum(grad.astype(F32), axis=0, keepdims=True)

        plain, columns = plain_sum[...], column_sum[...]
        turned = held["vec_all"][...].T
        weight = held["mix"][...].reshape(width, width).astype(F32)
        gain_grad = jnp.sum(plain * weight, axis=1, keepdims=True)
        shift_grad = jnp.sum(weight * columns, axis=1, keepdims=True)
        scaled = plain * turned[:, 0:1] + turned[:, 1:2] * columns
        extras = []
        out_sum = held["out_own"][...].astype(F32) + held["out_far"][...].astype(F32)
        for p in range(3):
            piece = out_sum[p * HD : (p + 1) * HD]
            extras.append(jnp.zeros((width, WIDE - 128), F32))
            extras.append(jnp.concatenate([jnp.zeros((128 - HD, width), F32), piece], axis=0).T)
        scaled = scaled + jnp.concatenate(extras, axis=1)
        for k in range(n_dp):
            total[k] = scaled[k * shard : (k + 1) * shard].astype(LOW)
        for block in range(line):
            cross_send[MIX][block] = total[block * 2 + 1 - side]
        cross(far_end, [MIX])
        cross(far_end - 1, [MIX])
        vec_mine[...] = held["vec_part"][...]
        flat = jnp.concatenate(
            [gain_grad, shift_grad, jnp.zeros((width, 6), F32)], axis=1
        ).T
        vec_mine[0:2] = flat[0:2]
        vec_mine[8:12] = units_rows_back(held["bias_own"][...], tensor, n_dp) + units_rows_back(
            held["bias_far"][...], far_row, n_dp
        )
        vec_lane = lax.broadcasted_iota(jnp.int32, (1, width), 1)
        in_part = (vec_lane >= tensor * (NH * HD)) & (vec_lane < (tensor + 1) * (NH * HD))
        for row, low in ((2, 0), (3, 2 * WIDE)):
            line_up = jnp.concatenate([columns[:, low : low + WIDE]] + [columns[:, 0:WIDE]] * 2, axis=1)
            placed = jnp.zeros((1, width), F32)
            for t in range(4):
                shifted = pltpu.roll(line_up, t * NH * HD, 1)
                placed = jnp.where(tensor == t, shifted, placed)
            vec_mine[row : row + 1] = jnp.where(in_part, placed, 0.0)
        vec_made = [
            copies.start(vec_mine, vec_land.at[i], device)
            for i, device in enumerate((at.mate, at.far, at.corner))
        ]
        for distance in range(far_end - 2, 0, -1):
            handle_all(distance, (FC, PROJ))
        for copy in vec_made:
            copy.wait_recv()
        vec_sum = vec_mine[...] + vec_land[0] + vec_land[1] + vec_land[2]
        for k in range(n_dp):
            vec_near[k] = pltpu.roll(vec_sum, (width - k * shard) % width, 1)[:, 0:128]
        for block in range(line):
            cross_send[VEC][block] = vec_near[block * 2 + 1 - side]
        cross(far_end, [VEC])
        cross(far_end - 1, [VEC])
        for distance in range(far_end, 0, -1):
            handle_all(distance, (MIX, VEC))
            if distance >= 2:
                cross(distance - 2, (MIX, VEC))

        for name in ("hidden", "grad_middle", "middle", "positions"):
            loads[name].wait()
        last_copy.wait_recv()
        first_row = tensor * rows
        live = ends_of(lengths_ref)[-1]
        last_bias = held["vec_all"][7:8]
        gain = held["vec_all"][0:1]
        mate_own.wait_recv()
        for copy in far_made:
            copy.wait_recv()
        tile = 4 * window

        @pl.loop(0, rows // tile)
        def _(i):
            start = pl.multiple_of(i * tile, tile)
            span = pl.ds(start, tile)
            ids = first_row + start + lax.broadcasted_iota(jnp.int32, (tile, 1), 0)
            final = (
                held["middle"][span]
                + held["last"][0, span].astype(F32)
                + last_land[span].astype(F32)
                + last_bias
            )
            block_out[span] = jnp.where(ids < live, final, 0.0).astype(LOW)
            grad = (
                part[tensor, span].astype(F32)
                + mate_land[0, span].astype(F32)
                + far_land[span].astype(F32)
            )
            normed, inverse = normalize(held["hidden"][span].astype(F32))
            grad = held["grad_middle"][span] + norm_back(normed, inverse, grad, gain)
            for w in range(4):
                spot_row = held["positions"][pl.ds(i * 4 + w, 1)][:, 0:1] - (i * 4 + w) * window
                here = lax.broadcasted_iota(jnp.int32, (window, 1), 0) == spot_row
                piece = grad[w * window : (w + 1) * window]
                tokens_out[pl.ds(pl.multiple_of(start + w * window, window), window)] = jnp.where(
                    here, 0.0, piece
                )
                thoughts_out[pl.ds(i * 4 + w, 1)] = jnp.sum(
                    jnp.where(here, piece, 0.0), axis=0, keepdims=True
                )

        for i in (FC, PROJ, MIX):
            close(i, out[i])
        close(VEC, vec_out)
        copies.finish()

    f32 = lambda *shape: jax.ShapeDtypeStruct(shape, F32)
    outputs = (
        f32(shard, width), f32(shard, width), f32(shard, width), f32(VEC_ROWS, 128),
        f32(rows, width), f32(latents, width), jax.ShapeDtypeStruct((rows, width), LOW),
    )
    scratch = [pltpu.VMEM(arrays[name].shape, arrays[name].dtype) for name in names]
    for number, wide in ((line, 1), (line, 1), (last, 3), (last, 3)):
        scratch += [pltpu.VMEM((number, shard, width), LOW)] * wide
        scratch.append(pltpu.VMEM((number, VEC_ROWS, 128), F32))
    scratch += [
        pltpu.VMEM((4, rows, width), LOW),
        pltpu.VMEM((2, rows, width), LOW),
        pltpu.VMEM((rows, width), LOW),
        pltpu.VMEM((rows, width), LOW),
        pltpu.VMEM((rows, width), LOW),
        pltpu.VMEM((n_dp, shard, width), LOW),
        pltpu.VMEM((VEC_ROWS, width), F32),
        pltpu.VMEM((3, VEC_ROWS, width), F32),
        pltpu.VMEM((n_dp, VEC_ROWS, 128), F32),
        pltpu.VMEM((width, width), F32),
        pltpu.VMEM((1, width), F32),
    ]
    return comm_call(
        kernel,
        "finish_grads",
        outputs,
        (lengths, *arrays.values()),
        [pl.BlockSpec(memory_space=pltpu.SMEM)] + [ANY] * len(names),
        (VM,) * len(outputs),
        (last + 1) * 2 + last * 4 + 1 + 2 + 2 + 3,
        cid,
        scratch=scratch,
        local=len(names),
        limit=63 << 20,
    )


def unit_kernel(add, line, bias_row, lengths_ref, *refs):
    refs = list(refs)
    rows_ref, grad_in = refs[:2]
    pieces, vec_ref = refs[2:6], refs[6]
    refs = refs[7:]
    if add:
        last_in, two_in = refs[:2]
        refs = refs[2:]
    last_ref, two_ref, fc_near, fc_side, proj_near, proj_side, bias_grad_ref = refs[:7]
    fc_all, proj_all, fc_sum, proj_sum = refs[7:]
    step = pl.program_id(0)
    side, tensor = lax.axis_index("dp") % 2, lax.axis_index("tensor")
    live = ends_of(lengths_ref)[-1]

    @pl.when(step == 0)
    def _():
        for full, near, across in ((fc_all, *pieces[:2]), (proj_all, *pieces[2:])):
            for i in range(line):
                full[2 * i + side] = near[i]
                full[2 * i + 1 - side] = across[i]
        fc_sum[...] = jnp.zeros_like(fc_sum)
        proj_sum[...] = jnp.zeros_like(proj_sum)
        bias_grad_ref[...] = jnp.zeros_like(bias_grad_ref)

    count, width = rows_ref.shape
    half = pl.num_programs(0) // 2
    block = jnp.where(step < half, tensor, tensor + 1 - 2 * (tensor % 2))
    first = block * (half * count) + (step % half) * count
    alive = first + lax.broadcasted_iota(jnp.int32, (count, 1), 0) < live
    rows = rows_ref[...]
    grad = jnp.where(alive, grad_in[...], jnp.zeros_like(grad_in))
    fc = fc_all[...].reshape(width, -1)
    proj = proj_all[...].reshape(width, -1)
    inner = nn(rows, fc) + vec_ref[bias_row : bias_row + 1]
    square = inner * inner
    bend = jnp.tanh(GELU_SCALE * inner * (1.0 + GELU_CUBE * square))
    half = 0.5 * (1.0 + bend)
    activated = (inner * half).astype(LOW)
    slope = half + 0.5 * inner * (1.0 - bend * bend) * GELU_SCALE * (1.0 + 3.0 * GELU_CUBE * square)
    grad_inner = (nn(grad, proj) * slope).astype(LOW)
    last = nt(activated, proj)
    two = nt(grad_inner, fc)
    if add:
        last, two = last + last_in[...], two + two_in[...]
    last_ref[...] = last.astype(last_ref.dtype)
    two_ref[...] = two.astype(two_ref.dtype)
    fc_sum[...] += tn(rows, grad_inner)
    proj_sum[...] += tn(grad, activated)
    bias_grad_ref[...] += jnp.sum(grad_inner.astype(F32), axis=0, keepdims=True)

    @pl.when(step == pl.num_programs(0) - 1)
    def _():
        shard = fc_near.shape[1]
        for sums, near, across in ((fc_sum, fc_near, fc_side), (proj_sum, proj_near, proj_side)):
            for i in range(line):
                even = sums[2 * i * shard : (2 * i + 1) * shard].astype(LOW)
                odd = sums[(2 * i + 1) * shard : (2 * i + 2) * shard].astype(LOW)
                near[i] = jnp.where(side == 0, even, odd)
                across[i] = jnp.where(side == 0, odd, even)


def units_both_ways(lengths, rows, grad, pieces, vec_all, bias_row, before):
    count, width = rows.shape
    line, shard, units = pieces[0].shape
    tile = pl.BlockSpec((ROW_TILE, width), lambda i: (i, 0))
    fixed = lambda shape: pl.BlockSpec(shape, lambda i: (0,) * len(shape))
    add = before is not None
    kind = LOW if add else F32
    return pl.pallas_call(
        functools.partial(unit_kernel, add, line, bias_row),
        grid=(count // ROW_TILE,),
        out_shape=(
            jax.ShapeDtypeStruct((count, width), kind),
            jax.ShapeDtypeStruct((count, width), kind),
        )
        + (jax.ShapeDtypeStruct((line, shard, units), LOW),) * 4
        + (jax.ShapeDtypeStruct((1, units), F32),        ),
        in_specs=[pl.BlockSpec(memory_space=pltpu.SMEM), tile, tile]
        + [fixed((line, shard, units))] * 4
        + [fixed(vec_all.shape)]
        + [tile] * (2 if add else 0),
        out_specs=(tile, tile) + (fixed((line, shard, units)),) * 4 + (fixed((1, units)),),
        scratch_shapes=[pltpu.VMEM((2 * line, shard, units), LOW)] * 2
        + [pltpu.VMEM((width, units), F32)] * 2,
        compiler_params=pltpu.CompilerParams(
            dimension_semantics=("arbitrary",), vmem_limit_bytes=56 << 20
        ),
        cost_estimate=pl.CostEstimate(
            flops=12 * count * width * units,
            bytes_accessed=24 * count * width,
            transcendentals=count * units,
        ),
        name="units_second" if add else "units_first",
    )(lengths, rows, grad, *pieces, vec_all, *(before or ()))


SM = pl.BlockSpec(memory_space=pltpu.SMEM)


def prepare(tokens, thoughts, positions, qkv, out, proj, vectors):
    rows, width = tokens.shape
    latents = thoughts.shape[0]
    window = rows // latents
    shard = qkv.shape[0]

    def kernel(pos_ref, tokens_ref, thoughts_ref, qkv_ref, out_ref, proj_ref, *refs):
        vec_refs = refs[: len(vectors)]
        hidden_out, mix_out, turned_out, vec_out, pos_out, tile = refs[len(vectors) :]
        pos_row = lax.broadcasted_iota(jnp.int32, (latents, 128), 0)
        spread = jnp.zeros((latents, 128), jnp.int32)
        for w in range(latents):
            spread = jnp.where(pos_row == w, pos_ref[w], spread)
            span = pl.ds(w * window, window)
            here = lax.broadcasted_iota(jnp.int32, (window, 1), 0) == pos_ref[w] - w * window
            hidden_out[span] = jnp.where(
                here, thoughts_ref[w : w + 1].astype(F32), tokens_ref[span].astype(F32)
            ).astype(LOW)
        pos_out[...] = spread
        turned = qkv_ref[...].astype(F32).T
        extra = out_ref[...].astype(F32)
        pieces = []
        for part in range(3):
            for h in range(NH):
                low = (h * 3 + part) * HD
                pieces.append(turned[low : low + HD])
            pieces.append(extra[part * HD : (part + 1) * HD])
        mix_out[...] = jnp.concatenate(pieces, axis=0).T.astype(LOW)
        turned_out[...] = proj_ref[...].astype(F32).T.astype(LOW)
        tile[...] = jnp.zeros_like(tile)
        row = 0
        for ref in vec_refs:
            count, size = ref.shape
            tile[row : row + count, 0:size] = ref[...].astype(F32)
            row += count
        vec_out[...] = tile[...].astype(LOW)

    low = lambda *shape: jax.ShapeDtypeStruct(shape, LOW)
    return pl.pallas_call(
        kernel,
        out_shape=(
            low(rows, width), low(shard, 3 * WIDE), low(proj.shape[1], proj.shape[0]),
            low(VEC_ROWS, 128), jax.ShapeDtypeStruct((latents, 128), jnp.int32),
        ),
        in_specs=[SM] + [VM] * (5 + len(vectors)),
        out_specs=(VM,) * 5,
        scratch_shapes=[pltpu.VMEM((VEC_ROWS, 128), F32)],
        name="prepare",
    )(positions, tokens, thoughts, qkv, out, proj, *vectors)


def split_grads(mix_grad, proj_grad, vec, share):
    shard, width = mix_grad.shape
    head_width = NH * HD

    def kernel(mix_ref, proj_ref, vec_ref, qkv_out, out_out, proj_out, small_out, bias_out):
        tensor = lax.axis_index("tensor")
        turned = mix_ref[...].T
        pieces = []
        for h in range(NH):
            for part in range(3):
                low = part * WIDE + h * HD
                pieces.append(turned[low : low + HD])
        qkv_out[...] = jnp.concatenate(pieces, axis=0).T
        for part in range(3):
            low = part * WIDE + head_width
            out_out[part * HD : (part + 1) * HD] = turned[low : low + HD]
        proj_out[...] = proj_ref[...].T
        rows = vec_ref[0:8]
        moved = rows
        for i in range(1, 4):
            moved = jnp.where(tensor == i, pltpu.roll(rows, 128 - i * share, 1), moved)
        small_out[...] = moved
        bias_out[...] = vec_ref[pl.ds(8 + tensor, 1)]

    f32 = lambda *shape: jax.ShapeDtypeStruct(shape, F32)
    return pl.pallas_call(
        kernel,
        out_shape=(
            f32(shard, 3 * head_width), f32(head_width, shard), f32(width, shard),
            f32(8, 128), f32(1, 128),
        ),
        in_specs=[VM] * 3,
        out_specs=(VM,) * 5,
        name="split_grads",
    )(mix_grad, proj_grad, vec)


def by_tensor(row, step, index):
    moved = row
    for i in range(1, 4):
        moved = jnp.where(index == i, pltpu.roll(row, (i * step) % row.shape[1], 1), moved)
    return moved


def units_row(rows, block, n_dp):
    width = rows.shape[1]
    shard, step = width // n_dp, n_dp // 4
    lane = lax.broadcasted_iota(jnp.int32, (1, width), 1) // shard
    base = by_tensor(rows, width - step * shard, block)
    total = jnp.zeros((1, width), F32)
    for j in range(n_dp):
        moved = pltpu.roll(base[j % 4 : j % 4 + 1], (j - j // 4) * shard, 1)
        total = jnp.where(lane == j, moved, total)
    return total


def units_rows_back(row, block, n_dp):
    width = row.shape[1]
    shard, step = width // n_dp, n_dp // 4
    lane = lax.broadcasted_iota(jnp.int32, (1, width), 1) // shard
    rows = [jnp.zeros((1, width), F32) for _ in range(4)]
    for j in range(n_dp):
        moved = pltpu.roll(row, (width - (j - j // 4) * shard) % width, 1)
        rows[j % 4] = jnp.where(lane == j // 4, moved, rows[j % 4])
    return by_tensor(jnp.concatenate(rows, axis=0), step * shard, block)


def normalize(values):
    center = jnp.mean(values, axis=-1, keepdims=True)
    offset = values - center
    spread = jnp.mean(offset * offset, axis=-1, keepdims=True)
    inverse = lax.rsqrt(spread + EPSILON)
    return offset * inverse, inverse


def norm_back(normed, inverse, grad, gain):
    scaled = grad * gain
    center = jnp.mean(scaled, axis=-1, keepdims=True)
    along = jnp.mean(scaled * normed, axis=-1, keepdims=True)
    return inverse * (scaled - center - normed * along)


def product(equation, left, right):
    return jnp.einsum(equation, left, right, preferred_element_type=F32)


def per_device(
    tokens,
    thoughts,
    positions,
    lengths,
    attn_norm_gain,
    attn_norm_shift,
    qkv_weight,
    qv_bias,
    attn_out_weight,
    attn_out_bias,
    mlp_norm_gain,
    mlp_norm_shift,
    fc_weight,
    fc_bias,
    proj_weight,
    proj_bias,
    cotangent,
):
    n_dp = lax.axis_size("dp")
    n_tensor = lax.axis_size("tensor")
    rows, width = tokens.shape
    slots = rows * n_tensor
    swap_far = [(i, (i + 2) % n_tensor) for i in range(n_tensor)]

    share = width // (n_dp * n_tensor)
    small = [
        attn_norm_gain[None], attn_norm_shift[None], qv_bias, attn_out_bias[None],
        mlp_norm_gain[None], mlp_norm_shift[None], proj_bias[None], fc_bias[None],
    ]
    hidden, mix_share, proj_share, vectors, places = prepare(
        tokens, thoughts, positions, qkv_weight, attn_out_weight, proj_weight, small
    )
    (
        group_low, mixed, mix_all, fc_near, fc_side, fc_far_near, proj_near, grad_rows, out_own,
        vec_all,
    ) = gather_inputs(hidden, cotangent, fc_weight, proj_share, mix_share, vectors, n_dp)
    mixed = mixed.reshape(slots, -1)
    swap_side = [(i, i + 1 - 2 * (i % 2)) for i in range(n_dp)]
    out_far = lax.ppermute(out_own, "tensor", swap_far)
    proj_far_near = lax.ppermute(proj_near, "tensor", swap_far)
    fc_far_side = lax.ppermute(fc_far_near, "dp", swap_side)
    proj_side = lax.ppermute(proj_near, "dp", swap_side)
    attended, stats = attend(lengths, mixed)
    sent, out_far, proj_far_near, fc_far_side, proj_side = lax.optimization_barrier(
        (attended, out_far, proj_far_near, fc_far_side, proj_side)
    )
    proj_far_side = lax.ppermute(proj_far_near, "dp", swap_side)
    both, middle, chip_two = after_attention(
        sent, out_own, out_far, hidden, vec_all, n_dp, 1
    )
    chip_two, proj_far_side = lax.optimization_barrier((chip_two, proj_far_side))
    chip_two = chip_two.reshape(2 * rows, width)
    chip_grad = grad_rows.reshape(2 * rows, width)

    first = units_both_ways(
        lengths, chip_two, chip_grad,
        (fc_far_near, fc_far_side, proj_far_near, proj_far_side), vec_all, 13, None,
    )
    far_fc_near, far_fc_side, far_proj_near, far_proj_side, far_fc_bias = first[2:]
    proj_side_far = lax.ppermute(far_proj_side, "tensor", swap_far)
    fc_far_side_in = lax.ppermute(far_fc_side, "dp", swap_side)
    second = units_both_ways(
        lengths, chip_two, chip_grad, (fc_near, fc_side, proj_near, proj_side), vec_all, 12,
        first[:2],
    )
    last_part, grad_two_part, fc_near_grad, fc_side_grad, proj_near_grad, proj_side_grad = second[:6]
    fc_near_side_in = lax.ppermute(fc_side_grad, "dp", swap_side)
    grad_heads, grad_middle, grad_out, far_out, vec_part = before_attention_back(
        lengths, grad_two_part.reshape(2, rows, width), middle, cotangent, both, out_own, out_far,
        vec_all, n_dp, 2,
    )
    fc_cross = far_fc_near + fc_far_side_in
    proj_cross = proj_side_grad + proj_side_far
    grad_heads, fc_cross, proj_cross, far_out, far_proj_near = lax.optimization_barrier(
        (grad_heads, fc_cross, proj_cross, far_out, far_proj_near)
    )
    fc_cross = lax.ppermute(fc_cross, "tensor", swap_far)
    proj_cross = lax.ppermute(proj_cross, "dp", swap_side)
    far_out = lax.ppermute(far_out, "tensor", swap_far)
    proj_near_far = lax.ppermute(far_proj_near, "tensor", swap_far)
    last_low = last_part.reshape(2, rows, width)

    grad_mixed = attend_back(lengths, mixed, attended, stats, grad_heads)
    arrays = {
        "fc_near": fc_near_grad, "fc_near_side": fc_near_side_in, "fc_cross": fc_cross,
        "proj_near": proj_near_grad, "proj_near_far": proj_near_far, "proj_cross": proj_cross,
        "grad_mixed": grad_mixed.reshape(n_tensor, rows, width), "mix": mix_all,
        "last": last_low, "group": group_low,
        "out_own": grad_out, "out_far": far_out,
        "vec_all": vec_all, "vec_part": vec_part, "bias_own": second[6], "bias_far": far_fc_bias,
        "hidden": hidden, "grad_middle": grad_middle, "middle": middle, "positions": places,
    }
    fc_grad, proj_grad, mix_grad, vec, grad_tokens, grad_thoughts, block_out = finish_grads(
        lengths, arrays, n_dp, 8
    )
    qkv_grad, out_grad, proj_grad, small_grads, bias_grad = split_grads(
        mix_grad, proj_grad, vec, share
    )
    small_grads = small_grads[:, :share]
    return (
        block_out,
        grad_tokens,
        grad_thoughts,
        small_grads[0],
        small_grads[1],
        qkv_grad,
        small_grads[2:4],
        out_grad,
        small_grads[4],
        small_grads[5],
        small_grads[6],
        fc_grad,
        bias_grad[0, : fc_bias.shape[0]],
        proj_grad,
        small_grads[7],
    )


def solution(mesh):
    rows = P(("dp", "tensor"), None)
    line = P(("dp", "tensor"))
    in_specs = (
        rows, rows, line, P("dp", None), line, line, P("dp", "tensor"),
        P(None, ("dp", "tensor")), P("tensor", "dp"), line, line, line,
        P("dp", "tensor"), line, P("tensor", "dp"), line, rows,
    )
    out_specs = (
        rows, rows, rows, line, line, P("dp", "tensor"), P(None, ("dp", "tensor")),
        P("tensor", "dp"), line, line, line, P("dp", "tensor"), line, P("tensor", "dp"), line,
    )
    return jax.shard_map(
        per_device, mesh=mesh, in_specs=in_specs, out_specs=out_specs, check_vma=False
    )
```

```python
import functools
import math

import jax
import jax.numpy as jnp
from jax import lax
from jax.experimental import pallas as pl
from jax.experimental.pallas import tpu as pltpu
from jax.sharding import PartitionSpec as P

H = 12
HD = 64
FF = 3072
SEQ_DEV = 3
EPSILON = 1e-05
MASKED = -1e30
NH = 3
SLABS = 2
WIDE = SLABS * 128
BQ = 512
BK = 512
VEC_ROWS = 16
ROW_TILE = 256
GELU_SCALE = math.sqrt(2.0 / math.pi)
GELU_CUBE = 0.044715
MESH = pl.DeviceIdType.MESH
ANY = pl.BlockSpec(memory_space=pl.ANY)
VM = pl.BlockSpec(memory_space=pltpu.VMEM)
SM = pl.BlockSpec(memory_space=pltpu.SMEM)
LOW = jnp.bfloat16
F32 = jnp.float32


def nn(a, b):
    return lax.dot_general(a, b, (((1,), (0,)), ((), ())), preferred_element_type=jnp.float32)


def nt(a, b):
    return lax.dot_general(a, b, (((1,), (1,)), ((), ())), preferred_element_type=jnp.float32)


def tn(a, b):
    return lax.dot_general(a, b, (((0,), (0,)), ((), ())), preferred_element_type=jnp.float32)


def head_rows(slab, head):
    half = slab[(head % 2) * HD : (head % 2 + 1) * HD]
    zero = jnp.zeros_like(half)
    return jnp.concatenate([half, zero] if head % 2 == 0 else [zero, half], axis=0)


def ends_of(lengths_ref):
    ends = [lengths_ref[0, 0]]
    for i in range(1, SEQ_DEV):
        ends.append(ends[-1] + lengths_ref[0, i])
    return ends


def segment_start(ends, slots):
    start = jnp.zeros_like(slots)
    for i in range(SEQ_DEV):
        start = jnp.where(slots >= ends[i], ends[i], start)
    return start


def segment_stop(ends, slot, slots):
    stop = slots
    for i in reversed(range(SEQ_DEV)):
        stop = jnp.where(slot < ends[i], ends[i], stop)
    return stop


def attend_kernel(lengths_ref, mixed_ref, out_ref, stat_ref, qt_ref, vt_ref):
    tokens = mixed_ref.shape[0]
    ends = ends_of(lengths_ref)
    for first in range(0, tokens, BQ):
        rows = pl.ds(first, BQ)
        for slab in range(SLABS):
            lanes = slab * 128
            qt_ref[lanes : lanes + 128, rows] = (
                mixed_ref[rows, lanes : lanes + 128] * HD ** (-0.5)
            ).T
            vt_ref[lanes : lanes + 128, rows] = mixed_ref[
                rows, 2 * WIDE + lanes : 2 * WIDE + lanes + 128
            ].T

    def query_block(block, carry):
        first = pl.multiple_of(block * BQ, BQ)
        columns = pl.ds(first, BQ)
        start = segment_start(ends, first + lax.broadcasted_iota(jnp.int32, (1, BQ), 1))
        query_ids = first + lax.broadcasted_iota(jnp.int32, (BK, BQ), 1)
        queries = [
            head_rows(qt_ref[(h // 2) * 128 : (h // 2 + 1) * 128, columns], h) for h in range(NH)
        ]

        def key_block(key, state):
            base = pl.multiple_of(key * BK, BK)
            rows = pl.ds(base, BK)
            key_ids = base + lax.broadcasted_iota(jnp.int32, (BK, BQ), 0)
            allowed = (key_ids <= query_ids) & (key_ids >= start)
            result = []
            for h in range(NH):
                peak, total, acc = state[h]
                slab = h // 2
                scores = nn(mixed_ref[rows, WIDE + slab * 128 : WIDE + slab * 128 + 128], queries[h])
                scores = jnp.where(allowed, scores, MASKED)
                fresh = jnp.maximum(peak, jnp.max(scores, axis=0, keepdims=True))
                weight = jnp.exp(scores - fresh)
                decay = jnp.exp(peak - fresh)
                total = total * decay + jnp.sum(weight, axis=0, keepdims=True)
                values = vt_ref[h * HD : (h + 1) * HD, rows]
                acc = acc * decay + nn(values, weight.astype(jnp.bfloat16))
                result.append((fresh, total, acc))
            return tuple(result)

        empty = tuple(
            (
                jnp.full((1, BQ), MASKED, jnp.float32),
                jnp.zeros((1, BQ), jnp.float32),
                jnp.zeros((HD, BQ), jnp.float32),
            )
            for _ in range(NH)
        )
        state = lax.fori_loop(segment_start(ends, first) // BK, (block + 1) * (BQ // BK), key_block, empty)
        for h in range(NH):
            peak, total, acc = state[h]
            out_ref[h * HD : (h + 1) * HD, columns] = (acc / total).astype(jnp.bfloat16)
            stat_ref[h : h + 1, columns] = peak + jnp.log(total)
        return carry

    lax.fori_loop(0, tokens // BQ, query_block, 0)


def attend(lengths, mixed):
    tokens = mixed.shape[0]
    vm = pl.BlockSpec(memory_space=pltpu.VMEM)
    return pl.pallas_call(
        attend_kernel,
        out_shape=(
            jax.ShapeDtypeStruct((NH * HD, tokens), jnp.bfloat16),
            jax.ShapeDtypeStruct((8, tokens), jnp.float32),
        ),
        in_specs=[pl.BlockSpec(memory_space=pltpu.SMEM), vm],
        out_specs=(vm, vm),
        scratch_shapes=[pltpu.VMEM((WIDE, tokens), jnp.bfloat16)] * 2,
        compiler_params=pltpu.CompilerParams(vmem_limit_bytes=40 << 20),
        cost_estimate=pl.CostEstimate(
            flops=8 * tokens * tokens * NH * HD,
            bytes_accessed=16 * tokens * WIDE,
            transcendentals=tokens * tokens,
        ),
        name="attend",
    )(lengths, mixed)


def attend_back_kernel(
    lengths_ref, mixed_ref, out_ref, stat_ref, gradt_ref,
    gmixed_ref, qt_ref, kt_ref, grad_ref, delta_ref, dqt_ref
):
    tokens = mixed_ref.shape[0]
    ends = ends_of(lengths_ref)
    for first in range(0, tokens, BQ):
        rows = pl.ds(first, BQ)
        for slab in range(SLABS):
            lanes = slab * 128
            qt_ref[lanes : lanes + 128, rows] = (
                mixed_ref[rows, lanes : lanes + 128] * HD ** (-0.5)
            ).T
            kt_ref[lanes : lanes + 128, rows] = mixed_ref[rows, WIDE + lanes : WIDE + lanes + 128].T
        grad_ref[rows, 0:128] = gradt_ref[0:128, rows].T
        grad_ref[rows, 128:256] = jnp.concatenate(
            [gradt_ref[128:192, rows], jnp.zeros((64, BQ), jnp.bfloat16)], axis=0
        ).T
        for h in range(NH):
            product = gradt_ref[h * HD : (h + 1) * HD, rows].astype(jnp.float32) * out_ref[
                h * HD : (h + 1) * HD, rows
            ].astype(jnp.float32)
            delta_ref[h : h + 1, rows] = jnp.sum(product, axis=0, keepdims=True)
    dqt_ref[...] = jnp.zeros_like(dqt_ref)
    lane = lax.broadcasted_iota(jnp.int32, (BQ, 128), 1)

    def key_block(key, carry):
        base = pl.multiple_of(key * BK, BK)
        rows = pl.ds(base, BK)
        key_ids = base + lax.broadcasted_iota(jnp.int32, (BK, BQ), 0)

        def query_block(block, state):
            first = pl.multiple_of(block * BQ, BQ)
            columns = pl.ds(first, BQ)
            start = segment_start(ends, first + lax.broadcasted_iota(jnp.int32, (1, BQ), 1))
            query_ids = first + lax.broadcasted_iota(jnp.int32, (BK, BQ), 1)
            allowed = (key_ids <= query_ids) & (key_ids >= start)
            grad_keys = list(state[:SLABS])
            grad_values = list(state[SLABS:])
            for h in range(NH):
                slab = h // 2
                low, high = slab * 128, slab * 128 + 128
                queries = head_rows(qt_ref[low:high, columns], h)
                scores = nn(mixed_ref[rows, WIDE + low : WIDE + high], queries)
                probs = jnp.where(allowed, jnp.exp(scores - stat_ref[h : h + 1, columns]), 0.0)
                keep = (lane // HD) == (h % 2)
                grads = jnp.where(keep, grad_ref[columns, low:high], 0.0)
                grad_values[slab] += nn(probs.astype(jnp.bfloat16), grads)
                if h == NH - 1 and NH % 2 == 1:
                    grad_rows = jnp.concatenate(
                        [gradt_ref[h * HD : (h + 1) * HD, columns], jnp.zeros((HD, BQ), jnp.bfloat16)],
                        axis=0,
                    )
                else:
                    grad_rows = head_rows(gradt_ref[low:high, columns], h)
                grad_probs = nn(mixed_ref[rows, 2 * WIDE + low : 2 * WIDE + high], grad_rows)
                grad_scores = (probs * (grad_probs - delta_ref[h : h + 1, columns])).astype(
                    jnp.bfloat16
                )
                natural = mixed_ref[columns, low:high]
                grad_keys[slab] += nn(grad_scores, jnp.where(keep, natural, 0.0))
                dqt_ref[h * HD : (h + 1) * HD, columns] += nn(
                    kt_ref[h * HD : (h + 1) * HD, rows], grad_scores
                )
            return tuple(grad_keys) + tuple(grad_values)

        empty = (jnp.zeros((BK, 128), jnp.float32),) * (2 * SLABS)
        stop = segment_stop(ends, base + BK - 1, tokens)
        state = lax.fori_loop(key * BK // BQ, (stop - 1) // BQ + 1, query_block, empty)
        for slab in range(SLABS):
            low = slab * 128
            gmixed_ref[rows, WIDE + low : WIDE + low + 128] = (
                state[slab] * HD ** (-0.5)
            ).astype(jnp.bfloat16)
            gmixed_ref[rows, 2 * WIDE + low : 2 * WIDE + low + 128] = state[SLABS + slab].astype(
                jnp.bfloat16
            )
        return carry

    lax.fori_loop(0, tokens // BK, key_block, 0)
    for first in range(0, tokens, BQ):
        rows = pl.ds(first, BQ)
        for slab in range(SLABS):
            low = slab * 128
            gmixed_ref[rows, low : low + 128] = (
                (dqt_ref[low : low + 128, rows] * HD ** (-0.5)).T.astype(jnp.bfloat16)
            )


def attend_back(lengths, mixed, out, stat, gradt):
    tokens = mixed.shape[0]
    vm = pl.BlockSpec(memory_space=pltpu.VMEM)
    return pl.pallas_call(
        attend_back_kernel,
        out_shape=jax.ShapeDtypeStruct((tokens, 3 * WIDE), jnp.bfloat16),
        in_specs=[pl.BlockSpec(memory_space=pltpu.SMEM)] + [vm] * 4,
        out_specs=vm,
        scratch_shapes=[
            pltpu.VMEM((WIDE, tokens), jnp.bfloat16),
            pltpu.VMEM((WIDE, tokens), jnp.bfloat16),
            pltpu.VMEM((tokens, WIDE), jnp.bfloat16),
            pltpu.VMEM((8, tokens), jnp.float32),
            pltpu.VMEM((WIDE, tokens), jnp.float32),
        ],
        compiler_params=pltpu.CompilerParams(vmem_limit_bytes=50 << 20),
        cost_estimate=pl.CostEstimate(
            flops=20 * tokens * tokens * NH * HD,
            bytes_accessed=32 * tokens * WIDE,
            transcendentals=tokens * tokens,
        ),
        name="attend_back",
    )(lengths, mixed, out, stat, gradt)


class Copies:
    def __init__(self, send, recv):
        self.send, self.recv, self.made, self.started = send, recv, 0, []

    def plan(self, source, target, device):
        index = self.made
        self.made += 1
        return pltpu.make_async_remote_copy(
            src_ref=source,
            dst_ref=target,
            send_sem=self.send.at[index],
            recv_sem=self.recv.at[index],
            device_id=device,
            device_id_type=MESH,
        )

    def begin(self, copy, condition=None):
        self.started.append((copy, condition))
        when(condition, copy.start)

    def start(self, source, target, device):
        copy = self.plan(source, target, device)
        self.begin(copy)
        return copy

    def finish(self):
        for copy, condition in self.started:
            when(condition, copy.wait_send)


def when(condition, action):
    if condition is None:
        action()
    else:
        pl.when(condition)(action)


def greet(devices):
    barrier = pltpu.get_barrier_semaphore()
    for device, condition in devices:
        when(
            condition,
            lambda device=device: pl.semaphore_signal(
                barrier, inc=1, device_id=device, device_id_type=MESH
            ),
        )
    present = [1 if condition is None else condition.astype(jnp.int32) for _, condition in devices]
    pl.semaphore_wait(barrier, sum(present))


class Place:
    def __init__(self, line):
        self.dp = dp = lax.axis_index("dp")
        self.tensor = tensor = lax.axis_index("tensor")
        self.spot, self.side = spot, side = dp // 2, dp % 2
        self.chip, self.core = tensor // 2, tensor % 2
        self.has_up, self.has_down = spot + 1 < line, spot > 0
        self.up = (jnp.minimum(spot + 1, line - 1) * 2 + side, tensor)
        self.down = (jnp.maximum(spot - 1, 0) * 2 + side, tensor)
        self.across = (spot * 2 + 1 - side, tensor)
        self.mate = (dp, tensor + 1 - 2 * (tensor % 2))
        self.far = (dp, (tensor + 2) % 4)
        self.corner = (dp, 3 - tensor)

    def everyone(self):
        return [
            (self.mate, None), (self.far, None), (self.corner, None), (self.across, None),
            (self.up, self.has_up), (self.down, self.has_down),
        ]


def comm_call(kernel, name, outputs, inputs, in_specs, out_specs, copies, cid, scratch=(), local=1, limit=50 << 20):
    return pl.pallas_call(
        kernel,
        out_shape=outputs,
        in_specs=in_specs,
        out_specs=out_specs,
        scratch_shapes=list(scratch)
        + [
            pltpu.SemaphoreType.DMA((copies,)),
            pltpu.SemaphoreType.DMA((copies,)),
            pltpu.SemaphoreType.DMA((local,)),
        ],
        compiler_params=pltpu.CompilerParams(
            collective_id=cid, has_side_effects=True, vmem_limit_bytes=limit
        ),
        name=name,
    )(*inputs)


def one_hot(rows, columns, shift, limit):
    lane = lax.broadcasted_iota(jnp.int32, (rows, columns), 0)
    spot = lax.broadcasted_iota(jnp.int32, (rows, columns), 1)
    return ((spot == lane + shift) & (lane < limit)).astype(LOW)


def gather_inputs(tokens, thoughts, positions, cotangent, fc, proj, qkv, out, vectors, n_dp):
    line = n_dp // 2
    hops = line - 1
    rows, width = tokens.shape
    latents = thoughts.shape[0]
    window = rows // latents
    shard = fc.shape[0]
    half_rows = rows // 2
    share = width // (n_dp * 4)

    def kernel(
        pos_ref, tokens_ref, thoughts_ref, cot_ref, fc_ref, proj_ref, qkv_ref, out_ref, *refs
    ):
        vec_refs = refs[: len(vectors)]
        (
            normed_out, mixed_out, mix_out, fc_near, fc_side, fc_far, proj_near, cot_out, out_out,
            hidden_out, vec_out, pos_out,
            hidden_ref, mix_ref, vec_ref, tile,
            land, mix_land, tiles, tile_land, normed, mixed, out_turned, send, recv, local,
        ) = refs[len(vectors) :]
        pos_row = lax.broadcasted_iota(jnp.int32, (latents, 128), 0)
        places = jnp.zeros((latents, 128), jnp.int32)
        for w in range(latents):
            places = jnp.where(pos_row == w, pos_ref[w], places)
            span = pl.ds(w * window, window)
            here = lax.broadcasted_iota(jnp.int32, (window, 1), 0) == pos_ref[w] - w * window
            hidden_ref[span] = jnp.where(
                here, thoughts_ref[w : w + 1].astype(F32), tokens_ref[span].astype(F32)
            ).astype(LOW)
        pos_out[...] = places
        turned = qkv_ref[...].astype(F32).T
        extra = out_ref[...].astype(F32)
        pieces = []
        for p in range(3):
            for h in range(NH):
                low = (h * 3 + p) * HD
                pieces.append(turned[low : low + HD])
            pieces.append(extra[p * HD : (p + 1) * HD])
        mix_ref[...] = jnp.concatenate(pieces, axis=0).T.astype(LOW)
        tile[...] = jnp.zeros_like(tile)
        row = 0
        for ref in vec_refs:
            count, size = ref.shape
            tile[row : row + count, 0:size] = ref[...].astype(F32)
            row += count
        vec_ref[...] = tile[...].astype(LOW)
        at = Place(line)
        dp, tensor, spot, side = at.dp, at.tensor, at.spot, at.side
        mate_row, far_row, corner_row = at.mate[1], at.far[1], at.corner[1]
        greet(at.everyone())
        copies = Copies(send, recv)
        MIX, FC, PROJ, VEC = range(4)
        own = [mix_ref, fc_ref, proj_ref, tiles.at[dp]]

        def seat(item, position):
            if item == MIX:
                return mix_land.at[position * 2 + side]
            if item == FC:
                return fc_near.at[position]
            if item == PROJ:
                return proj_near.at[position]
            return tiles.at[position * 2 + side]

        def plan(item, hop):
            above, below = jnp.maximum(spot - hop, 0), jnp.minimum(spot + hop, line - 1)
            came_up = jnp.maximum(spot - 1 - hop, 0)
            came_down = jnp.minimum(spot + 1 + hop, line - 1)
            made = {
                "up": copies.plan(
                    own[item] if hop == 0 else seat(item, above), seat(item, above), at.up
                ),
                "down": copies.plan(
                    own[item] if hop == 0 else seat(item, below), seat(item, below), at.down
                ),
                "onward": [],
            }
            for position in (came_up, came_down):
                onward = []
                if item in (MIX, VEC):
                    onward.append(copies.plan(seat(item, position), seat(item, position), at.across))
                if item == FC:
                    onward.append(copies.plan(fc_near.at[position], fc_side.at[position], at.across))
                    onward.append(copies.plan(fc_near.at[position], fc_far.at[position], at.far))
                made["onward"].append(onward)
            return made

        plans = [[plan(item, hop) for hop in range(hops)] for item in range(4)]

        def launch(item):
            copies.begin(plans[item][0]["up"], at.has_up)
            copies.begin(plans[item][0]["down"], at.has_down)

        def handle(item, hop):
            made = plans[item][hop]
            for way, key, comes, goes in (
                (0, "up", spot - 1 - hop >= 0, at.has_up),
                (1, "down", spot + 1 + hop < line, at.has_down),
            ):
                when(comes, made[key].wait_recv)
                if hop + 1 < hops:
                    copies.begin(plans[item][hop + 1][key], comes & goes)
                for copy in made["onward"][way]:
                    copies.begin(copy, comes)

        def settle(item):
            for hop in range(hops):
                for way, comes in ((0, spot - 1 - hop >= 0), (1, spot + 1 + hop < line)):
                    for copy in plans[item][hop]["onward"][way]:
                        when(comes, copy.wait_recv)

        stays = []

        def stay(source, target):
            copy = pltpu.make_async_copy(source, target, local.at[len(stays)])
            copy.start()
            stays.append(copy)
            return copy

        vec_made = [
            copies.start(vec_ref, tile_land.at[i], device)
            for i, device in enumerate((at.mate, at.far, at.corner))
        ]
        parts = [pl.ds(0, half_rows), pl.ds(half_rows, half_rows)]
        launch(MIX)
        far_made = [
            copies.start(hidden_ref.at[part], land.at[far_row_here, part], at.far)
            for far_row_here in (2,)
            for part in parts
        ]
        mix_side = copies.start(mix_ref, mix_land.at[dp], at.across)
        launch(FC)
        fc_sides = [
            copies.start(fc_ref, fc_side.at[spot], at.across),
            copies.start(fc_ref, fc_far.at[spot], at.far),
        ]
        mate_made = copies.start(hidden_ref, land.at[1], at.mate)
        cot_made = copies.start(cot_ref, cot_out, at.mate)
        stay(hidden_ref, hidden_out)
        stay(fc_ref, fc_near.at[spot])
        stay(proj_ref, proj_near.at[spot])
        mix_land[dp] = mix_ref[...]
        for copy in vec_made:
            copy.wait_recv()
        merged = jnp.zeros((VEC_ROWS, 128), F32)
        bias_rows = jnp.zeros((VEC_ROWS, 128), F32)
        row_ids = lax.broadcasted_iota(jnp.int32, (VEC_ROWS, 128), 0)
        for i, index in enumerate((tensor, mate_row, far_row, corner_row)):
            tile = vec_ref[...] if i == 0 else tile_land[i - 1]
            merged += nn(tile, one_hot(128, 128, index * share, share))
            bias_rows = jnp.where(row_ids == 8 + index, tile[8:9].astype(F32), bias_rows)
        tiles[dp] = jnp.where(row_ids < 8, merged, bias_rows).astype(LOW)
        launch(VEC)
        vec_side = copies.start(tiles.at[dp], tiles.at[dp], at.across)

        def norm_rows(source, index):
            @pl.loop(0, rows // 128)
            def _(i):
                span = pl.ds(pl.multiple_of(i * 128, 128), 128)
                normed[index, span] = normalize(source[span].astype(F32))[0].astype(LOW)

            stay(normed.at[index], normed_out.at[index])

        def relay(i):
            far_made[i].wait_recv()
            return copies.start(land.at[2, parts[i]], land.at[3, parts[i]], at.mate)

        def mix_rows(index):
            @pl.loop(0, rows // 256)
            def _(i):
                span = pl.ds(pl.multiple_of(i * 256, 256), 256)
                turned = normed[index, span].astype(F32) * whole[0:1] + whole[1:2]
                weight = mix_land[...].reshape(width, width)
                mixed[index, span] = (nn(turned.astype(LOW), weight) + bias).astype(LOW)

            stay(mixed.at[index], mixed_out.at[index])

        norm_rows(hidden_ref, tensor)
        relayed = []
        for step in range(hops + 2):
            for item, hop in ((MIX, step), (VEC, step), (FC, step - 1), (PROJ, step - 2)):
                if 0 <= hop < hops:
                    handle(item, hop)
            if step == 0:
                launch(PROJ)
                mate_made.wait_recv()
                norm_rows(land.at[1], mate_row)
                relayed.append(relay(0))
            if step == 1:
                relayed.append(relay(1))
                norm_rows(land.at[2], far_row)
            if step == hops - 1:
                for copy in relayed:
                    copy.wait_recv()
                norm_rows(land.at[3], corner_row)
            if step == hops:
                mix_side.wait_recv()
                vec_side.wait_recv()
                settle(MIX)
                settle(VEC)
                whole = jnp.zeros((VEC_ROWS, width), F32)
                for i in range(n_dp):
                    whole += nn(tiles[i], one_hot(128, width, i * shard, shard))
                vec_out[...] = whole
                for i, block in enumerate((tensor, far_row)):
                    vec_out[12 + i : 13 + i] = units_row(whole[8:12], block, n_dp)
                lane = lax.broadcasted_iota(jnp.int32, (width, WIDE), 0)
                column = lax.broadcasted_iota(jnp.int32, (width, WIDE), 1)
                pick = (lane == column + tensor * (NH * HD)) & (column < NH * HD)
                picked = nn(whole.astype(LOW), pick.astype(LOW))
                bias = jnp.concatenate(
                    [picked[2:3], jnp.zeros((1, WIDE), F32), picked[3:4]], axis=1
                )
                mix_rows(tensor)
                mix_rows(mate_row)
        mix_rows(far_row)
        mix_rows(corner_row)
        stay(mix_land, mix_out)
        weight = mix_land[...].reshape(width, width)
        for part in range(3):
            low = part * WIDE + WIDE - 128
            turned = weight[:, low : low + 128].T
            out_turned[part * HD : (part + 1) * HD] = turned[128 - HD :]
        stay(out_turned, out_out)
        settle(FC)
        for copy in fc_sides:
            copy.wait_recv()
        cot_made.wait_recv()
        copies.finish()
        for copy in stays:
            copy.wait()

    low = lambda *shape: jax.ShapeDtypeStruct(shape, LOW)
    outputs = (
        low(4, rows, width), low(4, rows, width), low(n_dp, shard, width),
        low(line, shard, width), low(line, shard, width), low(line, shard, width),
        low(line, shard, width), low(rows, width), low(NH * HD, width), low(rows, width),
        jax.ShapeDtypeStruct((VEC_ROWS, width), F32),
        jax.ShapeDtypeStruct((latents, 128), jnp.int32),
    )
    scratch = [
        pltpu.VMEM((rows, width), LOW),
        pltpu.VMEM((shard, 3 * WIDE), LOW),
        pltpu.VMEM((VEC_ROWS, 128), LOW),
        pltpu.VMEM((VEC_ROWS, 128), F32),
        pltpu.VMEM((4, rows, width), LOW),
        pltpu.VMEM((n_dp, shard, width), LOW),
        pltpu.VMEM((n_dp, VEC_ROWS, 128), LOW),
        pltpu.VMEM((3, VEC_ROWS, 128), LOW),
        pltpu.VMEM((4, rows, width), LOW),
        pltpu.VMEM((4, rows, width), LOW),
        pltpu.VMEM((NH * HD, width), LOW),
    ]
    return comm_call(
        kernel,
        "gather_inputs",
        outputs,
        (positions, tokens, thoughts, cotangent, fc, proj, qkv, out, *vectors),
        [SM, VM, VM, ANY, ANY, ANY] + [VM] * (2 + len(vectors)),
        (ANY,) * 10 + (VM, VM),
        3 + 2 + 1 + 2 + 2 + 1 + 2 + hops * (2 * 4 + 2 * 4),
        0,
        scratch=scratch,
        local=3 + 8 + 2,
    )


def after_attention(attended, out_own, out_far, hidden, vec_all, n_dp, cid):
    head_width, slots = attended.shape
    rows, width = hidden.shape
    half_rows = rows // 2

    def kernel(
        heads_ref, own_ref, far_ref, hidden_ref, vec_ref,
        both_out, middle_out, two_out,
        land, part, part_low, part_land, two, send, recv, local,
    ):
        at = Place(n_dp // 2)
        greet([(at.far, None), (at.mate, None)])
        copies = Copies(send, recv)
        cores = (at.core, 1 - at.core)
        made = [None, None]
        for i in (1, 0):
            theirs = pl.multiple_of(((1 - at.chip) * 2 + cores[i]) * rows, rows)
            made[i] = copies.start(heads_ref.at[:, pl.ds(theirs, rows)], land.at[i], at.far)
        stays = []

        def stay(source, target):
            stays.append(pltpu.make_async_copy(source, target, local.at[len(stays)]))
            stays[-1].start()

        spans = []
        for i in range(2):
            ours = pl.multiple_of((at.chip * 2 + cores[i]) * rows, rows)
            spans.append(pl.ds(ours, rows))
            stay(heads_ref.at[:, spans[i]], both_out.at[0, :, i * rows : (i + 1) * rows])
            part[i] = tn(heads_ref[:, spans[i]], own_ref[...])
        sums = None
        for i in (1, 0):
            made[i].wait_recv()
            stay(land.at[i], both_out.at[1, :, i * rows : (i + 1) * rows])
            part[i] += tn(land[i], far_ref[...])
            if i == 1:
                part_low[...] = part[1].astype(LOW)
                sums = copies.start(part_low, part_land, at.mate)
        sums.wait_recv()
        mated = []
        for piece in range(2):

            @pl.loop(0, half_rows // 128)
            def _(i):
                span = pl.ds(pl.multiple_of(piece * half_rows + i * 128, 128), 128)
                middle = (
                    hidden_ref[span].astype(F32)
                    + part[0, span]
                    + part_land[span].astype(F32)
                    + vec_ref[4:5]
                )
                middle_out[span] = middle
                two[span] = (normalize(middle)[0] * vec_ref[5:6] + vec_ref[6:7]).astype(LOW)

            span = pl.ds(piece * half_rows, half_rows)
            mated.append(copies.start(two.at[span], two_out.at[1, span], at.mate))
        stay(two, two_out.at[0])
        for copy in mated:
            copy.wait_recv()
        copies.finish()
        for copy in stays:
            copy.wait()

    return comm_call(
        kernel,
        "after_attention",
        (
            jax.ShapeDtypeStruct((2, head_width, 2 * rows), LOW),
            jax.ShapeDtypeStruct((rows, width), F32),
            jax.ShapeDtypeStruct((2, rows, width), LOW),
        ),
        (attended, out_own, out_far, hidden, vec_all),
        [VM] * 5,
        (ANY, VM, ANY),
        5,
        cid,
        scratch=[
            pltpu.VMEM((2, head_width, rows), LOW),
            pltpu.VMEM((2, rows, width), F32),
            pltpu.VMEM((rows, width), LOW),
            pltpu.VMEM((rows, width), LOW),
            pltpu.VMEM((rows, width), LOW),
        ],
        local=5,
    )


def before_attention_back(lengths, two, middle, cotangent, both, out_own, out_far, vec_all, n_dp, cid):
    _, rows, width = two.shape
    head_width = out_own.shape[0]
    half_rows = rows // 2

    def kernel(
        lengths_ref, two_ref, middle_ref, cot_ref, both_ref, own_ref, far_ref, vec_ref,
        heads_out, grad_out, own_out, far_out, vec_out,
        two_land, mid, stay_heads, sent_heads, send, recv, local,
    ):
        at = Place(n_dp // 2)
        greet([(at.far, None), (at.mate, None)])
        copies = Copies(send, recv)
        halves = [pl.ds(0, half_rows), pl.ds(half_rows, half_rows)]
        sums = [copies.start(two_ref.at[1, span], two_land.at[span], at.mate) for span in halves]
        vec_out[...] = jnp.zeros_like(vec_out)
        first_row = at.tensor * rows
        live = ends_of(lengths_ref)[-1]
        mated = []
        for piece in range(2):
            sums[piece].wait_recv()

            @pl.loop(0, half_rows // 128)
            def _(i):
                start = pl.multiple_of(piece * half_rows + i * 128, 128)
                span = pl.ds(start, 128)
                grad = two_ref[0, span].astype(F32) + two_land[span].astype(F32)
                normed, inverse = normalize(middle_ref[span])
                ids = first_row + start + lax.broadcasted_iota(jnp.int32, (128, 1), 0)
                final = jnp.where(ids < live, cot_ref[span].astype(F32), 0.0)
                total = final + norm_back(normed, inverse, grad, vec_ref[5:6])
                grad_out[span] = total
                mid[0, span] = total.astype(LOW)
                for row, term in ((4, total), (5, normed * grad), (6, grad), (7, final)):
                    vec_out[row : row + 1] += jnp.sum(term, axis=0, keepdims=True)

            mated.append(copies.start(mid.at[0, halves[piece]], mid.at[1, halves[piece]], at.mate))
        cores = (at.core, 1 - at.core)
        made, stays = [], []
        for i in range(2):
            if i == 1:
                for copy in mated:
                    copy.wait_recv()
            ours = pl.ds(pl.multiple_of((at.chip * 2 + cores[i]) * rows, rows), rows)
            sent_heads[i] = nt(far_ref[...], mid[i]).astype(LOW)
            made.append(copies.start(sent_heads.at[i], heads_out.at[:, ours], at.far))
            stay_heads[i] = nt(own_ref[...], mid[i]).astype(LOW)
            stays.append(
                pltpu.make_async_copy(stay_heads.at[i], heads_out.at[:, ours], local.at[i])
            )
            stays[-1].start()
        grads = mid[...].reshape(2 * rows, width)
        own_out[...] = nn(both_ref[0], grads).astype(LOW)
        far_out[...] = nn(both_ref[1], grads).astype(LOW)
        for copy in made:
            copy.wait_recv()
        copies.finish()
        for copy in stays:
            copy.wait()

    return comm_call(
        kernel,
        "before_attention_back",
        (
            jax.ShapeDtypeStruct((head_width, 4 * rows), LOW),
            jax.ShapeDtypeStruct((rows, width), F32),
            jax.ShapeDtypeStruct((head_width, width), LOW),
            jax.ShapeDtypeStruct((head_width, width), LOW),
            jax.ShapeDtypeStruct((VEC_ROWS, width), F32),
        ),
        (lengths, two, middle, cotangent, both, out_own, out_far, vec_all),
        [pl.BlockSpec(memory_space=pltpu.SMEM)] + [VM] * 7,
        (ANY,) + (VM,) * 4,
        6,
        cid,
        scratch=[
            pltpu.VMEM((rows, width), LOW),
            pltpu.VMEM((2, rows, width), LOW),
            pltpu.VMEM((2, head_width, rows), LOW),
            pltpu.VMEM((2, head_width, rows), LOW),
        ],
        local=2,
    )


def finish_grads(lengths, arrays, n_dp, cid):
    part_rows = arrays["hidden"].shape[0] // 4
    names = list(arrays)
    kept = [name for name in names if name != "out_far"]
    line = n_dp // 2
    shard = arrays["mix"].shape[1]
    rows, width = arrays["hidden"].shape
    group = 4 * rows
    latents = arrays["positions"].shape[0]
    window = rows // latents
    far_end = line - 1
    slots = [(distance, way) for distance in range(far_end, 0, -1) for way in (0, 1)] + [(0, 0)]
    last = len(slots) - 1
    share = width // (n_dp * 4)
    FC, PROJ, MIX, VEC = range(4)

    def kernel(lengths_ref, *refs):
        refs = list(refs)

        def take(number):
            taken = refs[:number]
            del refs[:number]
            return taken

        source = dict(zip(names, take(len(names))))
        fc_out, proj_out, mix_out, vec_out, tokens_out, thoughts_out, block_out = take(7)
        held = dict(zip(kept, take(len(kept))))
        cross_send, cross_land = [None, None] + take(2), [None, None] + take(2)
        hop_send, hop_land = take(4), take(4)
        (
            part, mate_land, far_send, far_land, last_land, total, vec_mine, vec_land, vec_near,
            plain_sum, column_sum, out_land, send, recv, local,
        ) = refs
        out = [fc_out, proj_out, mix_out, None]
        at = Place(line)
        tensor, spot, side = at.tensor, at.spot, at.side
        mate_row, far_row, corner_row = at.mate[1], at.far[1], at.corner[1]
        copies = Copies(send, recv)
        loads = {}
        held["out_far"] = out_land
        for i, name in enumerate(kept):
            loads[name] = pltpu.make_async_copy(source[name], held[name], local.at[i])

        def load(*group):
            for name in group:
                loads[name].start()

        load("fc_near", "fc_near_side", "fc_cross", "proj_near", "proj_near_far", "proj_cross")
        load("grad_mixed", "mix")
        greet(at.everyone())

        def block_of(slot):
            distance, way = slots[slot]
            if way == 0:
                return jnp.minimum(spot + distance, far_end), spot + distance < line
            return jnp.maximum(spot - distance, 0), spot - distance >= 0

        crosses, hops = [], []
        for slot in range(len(slots)):
            block, _ = block_of(slot)
            crosses.append(
                {
                    i: copies.plan(cross_send[i].at[block], cross_land[i].at[block], at.across)
                    for i in (MIX, VEC)
                }
            )
            if slot < last:
                hops.append(
                    [
                        copies.plan(
                            hop_send[i].at[slot],
                            hop_land[i].at[slot],
                            (at.up, at.down)[slots[slot][1]],
                        )
                        for i in range(4)
                    ]
                )

        def cross(distance, items):
            for slot in range(len(slots)):
                if slots[slot][0] == distance:
                    for i in items:
                        copies.begin(crosses[slot][i], block_of(slot)[1])

        terms = (
            ("fc_near", "fc_near_side", "fc_cross"),
            ("proj_near", "proj_near_far", "proj_cross"),
        )

        def own_term(i, block):
            if i in (FC, PROJ):
                return sum(held[name][block].astype(F32) for name in terms[i])
            if i == MIX:
                return total[block * 2 + side].astype(F32)
            return vec_near[block * 2 + side]

        def handle(slot, i):
            block, inside = block_of(slot)
            behind = (at.has_down, at.has_up)[slots[slot][1]]
            outer = slot - 2

            def work():
                value = own_term(i, block)
                if i in (MIX, VEC):
                    crosses[slot][i].wait_recv()
                    value = value + cross_land[i][block].astype(F32)
                if outer < 0:
                    hop_send[i][slot] = value.astype(hop_send[i].dtype)
                    return

                @pl.when(behind)
                def _():
                    hops[outer][i].wait_recv()
                    hop_send[i][slot] = (value + hop_land[i][outer].astype(F32)).astype(
                        hop_send[i].dtype
                    )

                @pl.when(jnp.logical_not(behind))
                def _():
                    hop_send[i][slot] = value.astype(hop_send[i].dtype)

            when(inside, work)
            copies.begin(hops[slot][i], inside)

        def handle_all(distance, items):
            for slot in range(last):
                if slots[slot][0] == distance:
                    for i in items:
                        handle(slot, i)

        def close(i, target):
            value = own_term(i, spot)
            if i in (MIX, VEC):
                crosses[last][i].wait_recv()
                value = value + cross_land[i][spot].astype(F32)
            target[...] = value
            for way, behind in enumerate((at.has_down, at.has_up)):

                def add(way=way):
                    hops[last - 2 + way][i].wait_recv()
                    target[...] += hop_land[i][last - 2 + way].astype(F32)

                when(behind, add)

        for name in ("fc_near", "fc_near_side", "fc_cross", "proj_near", "proj_near_far", "proj_cross"):
            loads[name].wait()
        out_made = copies.start(source["out_far"], out_land, at.far)
        handle_all(far_end, (FC, PROJ))
        load("group", "out_own", "vec_all", "vec_part", "bias_own", "bias_far")
        load("last", "hidden", "grad_middle", "middle", "positions")
        loads["grad_mixed"].wait()
        loads["mix"].wait()

        def row_part(index):
            @pl.loop(0, rows // 256)
            def _(i):
                span = pl.ds(pl.multiple_of(i * 256, 256), 256)
                weight = held["mix"][...].reshape(width, width)
                part[index, span] = nt(held["grad_mixed"][index, span], weight).astype(LOW)

        row_part(corner_row)
        mate_far = copies.start(part.at[corner_row], mate_land.at[1], at.mate)
        row_part(mate_row)
        mate_own = copies.start(part.at[mate_row], mate_land.at[0], at.mate)
        row_part(far_row)
        mate_far.wait_recv()
        far_made = []

        def send_far(count):
            for i in range(len(far_made), len(far_made) + count):
                span = pl.ds(i * part_rows, part_rows)
                far_send[span] = (
                    mate_land[1, span].astype(F32) + part[far_row, span].astype(F32)
                ).astype(LOW)
                far_made.append(copies.start(far_send.at[span], far_land.at[span], at.far))

        send_far(1)
        row_part(tensor)
        send_far(1)
        if far_end > 1:
            handle_all(far_end - 1, (FC, PROJ))
        loads["last"].wait()
        last_copy = copies.start(held["last"].at[1], last_land, at.mate)
        for name in ("group", "out_own", "vec_all", "vec_part", "bias_own", "bias_far"):
            loads[name].wait()
        out_made.wait_recv()

        plain_sum[...] = jnp.zeros_like(plain_sum)
        column_sum[...] = jnp.zeros_like(column_sum)

        @pl.loop(0, group // 256)
        def _(i):
            block, start = i // (rows // 256), (i % (rows // 256)) * 256
            span = pl.ds(pl.multiple_of(start, 256), 256)
            grad = held["grad_mixed"][block, span]
            plain_sum[...] += tn(held["group"][block, span], grad)
            column_sum[...] += jnp.sum(grad.astype(F32), axis=0, keepdims=True)

        send_far(1)
        plain, columns = plain_sum[...], column_sum[...]
        turned = held["vec_all"][...].T
        weight = held["mix"][...].reshape(width, width).astype(F32)
        gain_grad = jnp.sum(plain * weight, axis=1, keepdims=True)
        shift_grad = jnp.sum(weight * columns, axis=1, keepdims=True)
        scaled = plain * turned[:, 0:1] + turned[:, 1:2] * columns
        extras = []
        out_sum = held["out_own"][...].astype(F32) + held["out_far"][...].astype(F32)
        for p in range(3):
            piece = out_sum[p * HD : (p + 1) * HD]
            extras.append(jnp.zeros((width, WIDE - 128), F32))
            extras.append(jnp.concatenate([jnp.zeros((128 - HD, width), F32), piece], axis=0).T)
        scaled = scaled + jnp.concatenate(extras, axis=1)
        for k in range(n_dp):
            total[k] = scaled[k * shard : (k + 1) * shard].astype(LOW)
        for block in range(line):
            cross_send[MIX][block] = total[block * 2 + 1 - side]
        cross(far_end, [MIX])
        cross(far_end - 1, [MIX])
        vec_mine[...] = held["vec_part"][...]
        flat = jnp.concatenate(
            [gain_grad, shift_grad, jnp.zeros((width, 6), F32)], axis=1
        ).T
        vec_mine[0:2] = flat[0:2]
        vec_mine[8:12] = units_rows_back(held["bias_own"][...], tensor, n_dp) + units_rows_back(
            held["bias_far"][...], far_row, n_dp
        )
        vec_lane = lax.broadcasted_iota(jnp.int32, (1, width), 1)
        in_part = (vec_lane >= tensor * (NH * HD)) & (vec_lane < (tensor + 1) * (NH * HD))
        for row, low in ((2, 0), (3, 2 * WIDE)):
            line_up = jnp.concatenate([columns[:, low : low + WIDE]] + [columns[:, 0:WIDE]] * 2, axis=1)
            placed = jnp.zeros((1, width), F32)
            for t in range(4):
                shifted = pltpu.roll(line_up, t * NH * HD, 1)
                placed = jnp.where(tensor == t, shifted, placed)
            vec_mine[row : row + 1] = jnp.where(in_part, placed, 0.0)
        vec_made = [
            copies.start(vec_mine, vec_land.at[i], device)
            for i, device in enumerate((at.mate, at.far, at.corner))
        ]
        for distance in range(far_end - 2, 0, -1):
            handle_all(distance, (FC, PROJ))
        send_far(1)
        for copy in vec_made:
            copy.wait_recv()
        vec_sum = vec_mine[...] + vec_land[0] + vec_land[1] + vec_land[2]
        for k in range(n_dp):
            vec_near[k] = pltpu.roll(vec_sum, (width - k * shard) % width, 1)[:, 0:128]
        for block in range(line):
            cross_send[VEC][block] = vec_near[block * 2 + 1 - side]
        cross(far_end, [VEC])
        cross(far_end - 1, [VEC])
        for distance in range(far_end, 0, -1):
            handle_all(distance, (MIX, VEC))
            if distance >= 2:
                cross(distance - 2, (MIX, VEC))

        for name in ("hidden", "grad_middle", "middle", "positions"):
            loads[name].wait()
        last_copy.wait_recv()
        first_row = tensor * rows
        live = ends_of(lengths_ref)[-1]
        last_bias = held["vec_all"][7:8]
        gain = held["vec_all"][0:1]
        mate_own.wait_recv()
        for copy in far_made:
            copy.wait_recv()
        tile = 4 * window

        @pl.loop(0, rows // tile)
        def _(i):
            start = pl.multiple_of(i * tile, tile)
            span = pl.ds(start, tile)
            ids = first_row + start + lax.broadcasted_iota(jnp.int32, (tile, 1), 0)
            final = (
                held["middle"][span]
                + held["last"][0, span].astype(F32)
                + last_land[span].astype(F32)
                + last_bias
            )
            block_out[span] = jnp.where(ids < live, final, 0.0).astype(LOW)
            grad = (
                part[tensor, span].astype(F32)
                + mate_land[0, span].astype(F32)
                + far_land[span].astype(F32)
            )
            normed, inverse = normalize(held["hidden"][span].astype(F32))
            grad = held["grad_middle"][span] + norm_back(normed, inverse, grad, gain)
            for w in range(4):
                spot_row = held["positions"][pl.ds(i * 4 + w, 1)][:, 0:1] - (i * 4 + w) * window
                here = lax.broadcasted_iota(jnp.int32, (window, 1), 0) == spot_row
                piece = grad[w * window : (w + 1) * window]
                tokens_out[pl.ds(pl.multiple_of(start + w * window, window), window)] = jnp.where(
                    here, 0.0, piece
                )
                thoughts_out[pl.ds(i * 4 + w, 1)] = jnp.sum(
                    jnp.where(here, piece, 0.0), axis=0, keepdims=True
                )

        for i in (FC, PROJ, MIX):
            close(i, out[i])
        close(VEC, vec_out)
        copies.finish()

    f32 = lambda *shape: jax.ShapeDtypeStruct(shape, F32)
    outputs = (
        f32(shard, width), f32(shard, width), f32(shard, width), f32(VEC_ROWS, 128),
        f32(rows, width), f32(latents, width), jax.ShapeDtypeStruct((rows, width), LOW),
    )
    scratch = [pltpu.VMEM(arrays[name].shape, arrays[name].dtype) for name in kept]
    for number, wide in ((line, 1), (line, 1), (last, 3), (last, 3)):
        scratch += [pltpu.VMEM((number, shard, width), LOW)] * wide
        scratch.append(pltpu.VMEM((number, VEC_ROWS, 128), F32))
    scratch += [
        pltpu.VMEM((4, rows, width), LOW),
        pltpu.VMEM((2, rows, width), LOW),
        pltpu.VMEM((rows, width), LOW),
        pltpu.VMEM((rows, width), LOW),
        pltpu.VMEM((rows, width), LOW),
        pltpu.VMEM((n_dp, shard, width), LOW),
        pltpu.VMEM((VEC_ROWS, width), F32),
        pltpu.VMEM((3, VEC_ROWS, width), F32),
        pltpu.VMEM((n_dp, VEC_ROWS, 128), F32),
        pltpu.VMEM((width, width), F32),
        pltpu.VMEM((1, width), F32),
        pltpu.VMEM(arrays["out_far"].shape, LOW),
    ]
    return comm_call(
        kernel,
        "finish_grads",
        outputs,
        (lengths, *arrays.values()),
        [pl.BlockSpec(memory_space=pltpu.SMEM)] + [ANY] * len(names),
        (VM,) * len(outputs),
        (last + 1) * 2 + last * 4 + 1 + 2 + 4 + 3 + 1,
        cid,
        scratch=scratch,
        local=len(kept),
        limit=63 << 20,
    )


def unit_kernel(add, line, bias_row, lengths_ref, *refs):
    refs = list(refs)
    rows_ref, grad_own, grad_mate = refs[:3]
    pieces, vec_ref = refs[3:7], refs[7]
    refs = refs[8:]
    if add:
        last_in, two_in = refs[:2]
        refs = refs[2:]
    last_ref, two_ref, fc_near, fc_side, proj_near, proj_side, bias_grad_ref = refs[:7]
    fc_all, proj_all, fc_sum, proj_sum = refs[7:]
    step = pl.program_id(0)
    side, tensor = lax.axis_index("dp") % 2, lax.axis_index("tensor")
    live = ends_of(lengths_ref)[-1]

    @pl.when(step == 0)
    def _():
        for full, near, across in ((fc_all, *pieces[:2]), (proj_all, *pieces[2:])):
            for i in range(line):
                full[2 * i + side] = near[i]
                full[2 * i + 1 - side] = across[i]
        fc_sum[...] = jnp.zeros_like(fc_sum)
        proj_sum[...] = jnp.zeros_like(proj_sum)
        bias_grad_ref[...] = jnp.zeros_like(bias_grad_ref)

    count, width = rows_ref.shape
    half = pl.num_programs(0) // 2
    block = jnp.where(step < half, tensor, tensor + 1 - 2 * (tensor % 2))
    first = block * (half * count) + (step % half) * count
    alive = first + lax.broadcasted_iota(jnp.int32, (count, 1), 0) < live
    rows = rows_ref[...]
    grad = jnp.where(step < half, grad_own[...], grad_mate[...])
    grad = jnp.where(alive, grad, jnp.zeros_like(grad))
    fc = fc_all[...].reshape(width, -1)
    proj = proj_all[...].reshape(width, -1)
    inner = nn(rows, fc) + vec_ref[bias_row : bias_row + 1]
    square = inner * inner
    bend = jnp.tanh(GELU_SCALE * inner * (1.0 + GELU_CUBE * square))
    half = 0.5 * (1.0 + bend)
    activated = (inner * half).astype(LOW)
    slope = half + 0.5 * inner * (1.0 - bend * bend) * GELU_SCALE * (1.0 + 3.0 * GELU_CUBE * square)
    grad_inner = (nn(grad, proj) * slope).astype(LOW)
    last = nt(activated, proj)
    two = nt(grad_inner, fc)
    if add:
        last, two = last + last_in[...], two + two_in[...]
    last_ref[...] = last.astype(last_ref.dtype)
    two_ref[...] = two.astype(two_ref.dtype)
    fc_sum[...] += tn(rows, grad_inner)
    proj_sum[...] += tn(grad, activated)
    bias_grad_ref[...] += jnp.sum(grad_inner.astype(F32), axis=0, keepdims=True)

    @pl.when(step == pl.num_programs(0) - 1)
    def _():
        shard = fc_near.shape[1]
        for sums, near, across in ((fc_sum, fc_near, fc_side), (proj_sum, proj_near, proj_side)):
            for i in range(line):
                even = sums[2 * i * shard : (2 * i + 1) * shard].astype(LOW)
                odd = sums[(2 * i + 1) * shard : (2 * i + 2) * shard].astype(LOW)
                near[i] = jnp.where(side == 0, even, odd)
                across[i] = jnp.where(side == 0, odd, even)


def units_both_ways(lengths, rows, grad, mate_grad, pieces, vec_all, bias_row, before):
    count, width = rows.shape
    line, shard, units = pieces[0].shape
    half = count // ROW_TILE // 2
    tile = pl.BlockSpec((ROW_TILE, width), lambda i: (i, 0))
    fixed = lambda shape: pl.BlockSpec(shape, lambda i: (0,) * len(shape))
    add = before is not None
    kind = LOW if add else F32
    return pl.pallas_call(
        functools.partial(unit_kernel, add, line, bias_row),
        grid=(count // ROW_TILE,),
        out_shape=(
            jax.ShapeDtypeStruct((count, width), kind),
            jax.ShapeDtypeStruct((count, width), kind),
        )
        + (jax.ShapeDtypeStruct((line, shard, units), LOW),) * 4
        + (jax.ShapeDtypeStruct((1, units), F32),        ),
        in_specs=[
            SM,
            tile,
            pl.BlockSpec((ROW_TILE, width), lambda i: (jnp.minimum(i, half - 1), 0)),
            pl.BlockSpec((ROW_TILE, width), lambda i: (jnp.maximum(i - half, 0), 0)),
        ]
        + [fixed((line, shard, units))] * 4
        + [fixed(vec_all.shape)]
        + [tile] * (2 if add else 0),
        out_specs=(tile, tile) + (fixed((line, shard, units)),) * 4 + (fixed((1, units)),),
        scratch_shapes=[pltpu.VMEM((2 * line, shard, units), LOW)] * 2
        + [pltpu.VMEM((width, units), F32)] * 2,
        compiler_params=pltpu.CompilerParams(
            dimension_semantics=("arbitrary",), vmem_limit_bytes=56 << 20
        ),
        cost_estimate=pl.CostEstimate(
            flops=12 * count * width * units,
            bytes_accessed=24 * count * width,
            transcendentals=count * units,
        ),
        name="units_second" if add else "units_first",
    )(lengths, rows, grad, mate_grad, *pieces, vec_all, *(before or ()))


def split_grads(mix_grad, vec, through, share):
    shard, width = mix_grad.shape
    head_width = NH * HD
    count = len(through)

    def kernel(mix_ref, vec_ref, *refs):
        given, (qkv_out, out_out), refs = refs[:count], refs[count : count + 2], refs[count + 2 :]
        small, passed, sems = refs[:8], refs[8 : 8 + count], refs[8 + count]
        copies = [
            pltpu.make_async_copy(given[i], passed[i], sems.at[i]) for i in range(count)
        ]
        for copy in copies:
            copy.start()
        tensor = lax.axis_index("tensor")
        turned = mix_ref[...].T
        pieces = []
        for h in range(NH):
            for part in range(3):
                low = part * WIDE + h * HD
                pieces.append(turned[low : low + HD])
        qkv_out[...] = jnp.concatenate(pieces, axis=0).T
        for part in range(3):
            low = part * WIDE + head_width
            out_out[part * HD : (part + 1) * HD] = turned[low : low + HD]
        rows = vec_ref[0:8]
        moved = rows
        for i in range(1, 4):
            moved = jnp.where(tensor == i, pltpu.roll(rows, 128 - i * share, 1), moved)
        for i, row in enumerate((0, 1, 4, 5, 6, 7)):
            small[i][...] = moved[row : row + 1, 0:share]
        small[6][...] = moved[2:4, 0:share]
        small[7][...] = vec_ref[pl.ds(8 + tensor, 1)][:, 0:shard]
        for copy in copies:
            copy.wait()

    f32 = lambda *shape: jax.ShapeDtypeStruct(shape, F32)
    return pl.pallas_call(
        kernel,
        out_shape=(f32(shard, 3 * head_width), f32(head_width, shard))
        + (f32(1, share),) * 6
        + (f32(2, share), f32(1, shard))
        + tuple(jax.ShapeDtypeStruct(x.shape, x.dtype) for x in through),
        in_specs=[VM] * (2 + count),
        out_specs=(VM,) * 10 + (ANY,) * count,
        scratch_shapes=[pltpu.SemaphoreType.DMA((count,))],
        name="split_grads",
    )(mix_grad, vec, *through)


def by_tensor(row, step, index):
    moved = row
    for i in range(1, 4):
        moved = jnp.where(index == i, pltpu.roll(row, (i * step) % row.shape[1], 1), moved)
    return moved


def units_row(rows, block, n_dp):
    width = rows.shape[1]
    shard, step = width // n_dp, n_dp // 4
    lane = lax.broadcasted_iota(jnp.int32, (1, width), 1) // shard
    base = by_tensor(rows, width - step * shard, block)
    total = jnp.zeros((1, width), F32)
    for j in range(n_dp):
        moved = pltpu.roll(base[j % 4 : j % 4 + 1], (j - j // 4) * shard, 1)
        total = jnp.where(lane == j, moved, total)
    return total


def units_rows_back(row, block, n_dp):
    width = row.shape[1]
    shard, step = width // n_dp, n_dp // 4
    lane = lax.broadcasted_iota(jnp.int32, (1, width), 1) // shard
    rows = [jnp.zeros((1, width), F32) for _ in range(4)]
    for j in range(n_dp):
        moved = pltpu.roll(row, (width - (j - j // 4) * shard) % width, 1)
        rows[j % 4] = jnp.where(lane == j // 4, moved, rows[j % 4])
    return by_tensor(jnp.concatenate(rows, axis=0), step * shard, block)


def normalize(values):
    center = jnp.mean(values, axis=-1, keepdims=True)
    offset = values - center
    spread = jnp.mean(offset * offset, axis=-1, keepdims=True)
    inverse = lax.rsqrt(spread + EPSILON)
    return offset * inverse, inverse


def norm_back(normed, inverse, grad, gain):
    scaled = grad * gain
    center = jnp.mean(scaled, axis=-1, keepdims=True)
    along = jnp.mean(scaled * normed, axis=-1, keepdims=True)
    return inverse * (scaled - center - normed * along)


def product(equation, left, right):
    return jnp.einsum(equation, left, right, preferred_element_type=F32)


def per_device(
    tokens,
    thoughts,
    positions,
    lengths,
    attn_norm_gain,
    attn_norm_shift,
    qkv_weight,
    qv_bias,
    attn_out_weight,
    attn_out_bias,
    mlp_norm_gain,
    mlp_norm_shift,
    fc_weight,
    fc_bias,
    proj_weight,
    proj_bias,
    cotangent,
):
    n_dp = lax.axis_size("dp")
    n_tensor = lax.axis_size("tensor")
    rows, width = tokens.shape
    slots = rows * n_tensor
    swap_far = [(i, (i + 2) % n_tensor) for i in range(n_tensor)]

    share = width // (n_dp * n_tensor)
    small = [
        attn_norm_gain[None], attn_norm_shift[None], qv_bias, attn_out_bias[None],
        mlp_norm_gain[None], mlp_norm_shift[None], proj_bias[None], fc_bias[None],
    ]
    (
        group_low, mixed, mix_all, fc_near, fc_side, fc_far_near, proj_near, mate_grad, out_own,
        hidden, vec_all, places,
    ) = gather_inputs(
        tokens, thoughts, positions, cotangent, fc_weight, proj_weight.T, qkv_weight,
        attn_out_weight, small, n_dp,
    )
    mixed = mixed.reshape(slots, -1)
    swap_side = [(i, i + 1 - 2 * (i % 2)) for i in range(n_dp)]
    out_far = lax.ppermute(out_own, "tensor", swap_far)
    proj_far_near = lax.ppermute(proj_near, "tensor", swap_far)
    fc_far_side = lax.ppermute(fc_far_near, "dp", swap_side)
    attended, stats = attend(lengths, mixed)
    sent, out_far, proj_far_near, fc_far_side = lax.optimization_barrier(
        (attended, out_far, proj_far_near, fc_far_side)
    )
    proj_far_side = lax.ppermute(proj_far_near, "dp", swap_side)
    both, middle, chip_two = after_attention(
        sent, out_own, out_far, hidden, vec_all, n_dp, 1
    )
    chip_two, proj_far_side, proj_sent = lax.optimization_barrier(
        (chip_two, proj_far_side, proj_near)
    )
    proj_side = lax.ppermute(proj_sent, "dp", swap_side)
    chip_two = chip_two.reshape(2 * rows, width)

    first = units_both_ways(
        lengths, chip_two, cotangent, mate_grad,
        (fc_far_near, fc_far_side, proj_far_near, proj_far_side), vec_all, 13, None,
    )
    far_fc_near, far_fc_side, far_proj_near, far_proj_side, far_fc_bias = first[2:]
    proj_side_far = lax.ppermute(far_proj_side, "tensor", swap_far)
    fc_far_side_in = lax.ppermute(far_fc_side, "dp", swap_side)
    second = units_both_ways(
        lengths, chip_two, cotangent, mate_grad, (fc_near, fc_side, proj_near, proj_side), vec_all, 12,
        first[:2],
    )
    last_part, grad_two_part, fc_near_grad, fc_side_grad, proj_near_grad, proj_side_grad = second[:6]
    fc_near_side_in = lax.ppermute(fc_side_grad, "dp", swap_side)
    grad_heads, grad_middle, grad_out, far_out, vec_part = before_attention_back(
        lengths, grad_two_part.reshape(2, rows, width), middle, cotangent, both, out_own, out_far,
        vec_all, n_dp, 2,
    )
    fc_cross = far_fc_near + fc_far_side_in
    proj_cross = proj_side_grad + proj_side_far
    grad_heads, fc_cross, proj_cross, far_proj_near = lax.optimization_barrier(
        (grad_heads, fc_cross, proj_cross, far_proj_near)
    )
    fc_cross = lax.ppermute(fc_cross, "tensor", swap_far)
    proj_cross = lax.ppermute(proj_cross, "dp", swap_side)
    proj_near_far = lax.ppermute(far_proj_near, "tensor", swap_far)
    last_low = last_part.reshape(2, rows, width)

    grad_mixed = attend_back(lengths, mixed, attended, stats, grad_heads)
    arrays = {
        "fc_near": fc_near_grad, "fc_near_side": fc_near_side_in, "fc_cross": fc_cross,
        "proj_near": proj_near_grad, "proj_near_far": proj_near_far, "proj_cross": proj_cross,
        "grad_mixed": grad_mixed.reshape(n_tensor, rows, width), "mix": mix_all,
        "last": last_low, "group": group_low,
        "out_own": grad_out, "out_far": far_out,
        "vec_all": vec_all, "vec_part": vec_part, "bias_own": second[6], "bias_far": far_fc_bias,
        "hidden": hidden, "grad_middle": grad_middle, "middle": middle, "positions": places,
    }
    fc_grad, proj_grad, mix_grad, vec, grad_tokens, grad_thoughts, block_out = finish_grads(
        lengths, arrays, n_dp, 8
    )
    parts = split_grads(
        mix_grad, vec, (fc_grad, proj_grad, grad_tokens, grad_thoughts, block_out), share
    )
    qkv_grad, out_grad = parts[:2]
    gain_one, shift_one, out_bias, gain_two, shift_two, last_bias = [p[0] for p in parts[2:8]]
    query_value, hidden_bias = parts[8], parts[9][0]
    fc_grad, proj_grad, grad_tokens, grad_thoughts, block_out = parts[10:]
    return (
        block_out,
        grad_tokens,
        grad_thoughts,
        gain_one,
        shift_one,
        qkv_grad,
        query_value,
        out_grad,
        out_bias,
        gain_two,
        shift_two,
        fc_grad,
        hidden_bias,
        proj_grad.T,
        last_bias,
    )


def solution(mesh):
    rows = P(("dp", "tensor"), None)
    line = P(("dp", "tensor"))
    in_specs = (
        rows, rows, line, P("dp", None), line, line, P("dp", "tensor"),
        P(None, ("dp", "tensor")), P("tensor", "dp"), line, line, line,
        P("dp", "tensor"), line, P("tensor", "dp"), line, rows,
    )
    out_specs = (
        rows, rows, rows, line, line, P("dp", "tensor"), P(None, ("dp", "tensor")),
        P("tensor", "dp"), line, line, line, P("dp", "tensor"), line, P("tensor", "dp"), line,
    )
    return jax.shard_map(
        per_device, mesh=mesh, in_specs=in_specs, out_specs=out_specs, check_vma=False
    )
```

```python
import functools
import math

import jax
import jax.numpy as jnp
from jax import lax
from jax.experimental import pallas as pl
from jax.experimental.pallas import tpu as pltpu
from jax.sharding import PartitionSpec as P

H = 12
HD = 64
FF = 3072
SEQ_DEV = 3
EPSILON = 1e-05
MASKED = -1e30
NH = 3
SLABS = 2
WIDE = SLABS * 128
BQ = 512
BK = 512
VEC_ROWS = 16
ROW_TILE = 256
GELU_SCALE = math.sqrt(2.0 / math.pi)
GELU_CUBE = 0.044715
MESH = pl.DeviceIdType.MESH
ANY = pl.BlockSpec(memory_space=pl.ANY)
VM = pl.BlockSpec(memory_space=pltpu.VMEM)
SM = pl.BlockSpec(memory_space=pltpu.SMEM)
LOW = jnp.bfloat16
F32 = jnp.float32


def nn(a, b):
    return lax.dot_general(a, b, (((1,), (0,)), ((), ())), preferred_element_type=jnp.float32)


def nt(a, b):
    return lax.dot_general(a, b, (((1,), (1,)), ((), ())), preferred_element_type=jnp.float32)


def tn(a, b):
    return lax.dot_general(a, b, (((0,), (0,)), ((), ())), preferred_element_type=jnp.float32)


def head_rows(slab, head):
    half = slab[(head % 2) * HD : (head % 2 + 1) * HD]
    zero = jnp.zeros_like(half)
    return jnp.concatenate([half, zero] if head % 2 == 0 else [zero, half], axis=0)


def ends_of(lengths_ref):
    ends = [lengths_ref[0, 0]]
    for i in range(1, SEQ_DEV):
        ends.append(ends[-1] + lengths_ref[0, i])
    return ends


def segment_start(ends, slots):
    start = jnp.zeros_like(slots)
    for i in range(SEQ_DEV):
        start = jnp.where(slots >= ends[i], ends[i], start)
    return start


def segment_stop(ends, slot, slots):
    stop = slots
    for i in reversed(range(SEQ_DEV)):
        stop = jnp.where(slot < ends[i], ends[i], stop)
    return stop


def attend_kernel(lengths_ref, mixed_in, out_ref, stat_ref, mixed_ref, qt_ref, vt_ref, sems):
    tokens = mixed_ref.shape[0]
    ends = ends_of(lengths_ref)
    loads = []
    for i in range(tokens // BQ):
        rows = pl.ds(i * BQ, BQ)
        loads.append(pltpu.make_async_copy(mixed_in.at[rows], mixed_ref.at[rows], sems.at[i]))
        loads[i].start()
    for first in range(0, tokens, BQ):
        rows = pl.ds(first, BQ)
        loads[first // BQ].wait()
        for slab in range(SLABS):
            lanes = slab * 128
            qt_ref[lanes : lanes + 128, rows] = (
                mixed_ref[rows, lanes : lanes + 128] * HD ** (-0.5)
            ).T
            vt_ref[lanes : lanes + 128, rows] = mixed_ref[
                rows, 2 * WIDE + lanes : 2 * WIDE + lanes + 128
            ].T

    def query_block(block, carry):
        first = pl.multiple_of(block * BQ, BQ)
        columns = pl.ds(first, BQ)
        start = segment_start(ends, first + lax.broadcasted_iota(jnp.int32, (1, BQ), 1))
        query_ids = first + lax.broadcasted_iota(jnp.int32, (BK, BQ), 1)
        queries = [
            head_rows(qt_ref[(h // 2) * 128 : (h // 2 + 1) * 128, columns], h) for h in range(NH)
        ]

        def key_block(key, state):
            base = pl.multiple_of(key * BK, BK)
            rows = pl.ds(base, BK)
            key_ids = base + lax.broadcasted_iota(jnp.int32, (BK, BQ), 0)
            allowed = (key_ids <= query_ids) & (key_ids >= start)
            result = []
            for h in range(NH):
                peak, total, acc = state[h]
                slab = h // 2
                scores = nn(mixed_ref[rows, WIDE + slab * 128 : WIDE + slab * 128 + 128], queries[h])
                scores = jnp.where(allowed, scores, MASKED)
                fresh = jnp.maximum(peak, jnp.max(scores, axis=0, keepdims=True))
                weight = jnp.exp(scores - fresh)
                decay = jnp.exp(peak - fresh)
                total = total * decay + jnp.sum(weight, axis=0, keepdims=True)
                values = vt_ref[h * HD : (h + 1) * HD, rows]
                acc = acc * decay + nn(values, weight.astype(jnp.bfloat16))
                result.append((fresh, total, acc))
            return tuple(result)

        empty = tuple(
            (
                jnp.full((1, BQ), MASKED, jnp.float32),
                jnp.zeros((1, BQ), jnp.float32),
                jnp.zeros((HD, BQ), jnp.float32),
            )
            for _ in range(NH)
        )
        state = lax.fori_loop(segment_start(ends, first) // BK, (block + 1) * (BQ // BK), key_block, empty)
        for h in range(NH):
            peak, total, acc = state[h]
            out_ref[h * HD : (h + 1) * HD, columns] = (acc / total).astype(jnp.bfloat16)
            stat_ref[h : h + 1, columns] = peak + jnp.log(total)
        return carry

    count = (ends[-1] + BQ - 1) // BQ
    lax.fori_loop(0, count, query_block, 0)

    def padded_block(block, carry):
        columns = pl.ds(pl.multiple_of(block * BQ, BQ), BQ)
        out_ref[:, columns] = jnp.zeros((out_ref.shape[0], BQ), jnp.bfloat16)
        return carry

    lax.fori_loop(count, tokens // BQ, padded_block, 0)


def attend(lengths, mixed):
    tokens = mixed.shape[0]
    vm = pl.BlockSpec(memory_space=pltpu.VMEM)
    return pl.pallas_call(
        attend_kernel,
        out_shape=(
            jax.ShapeDtypeStruct((NH * HD, tokens), jnp.bfloat16),
            jax.ShapeDtypeStruct((8, tokens), jnp.float32),
        ),
        in_specs=[pl.BlockSpec(memory_space=pltpu.SMEM), pl.BlockSpec(memory_space=pl.ANY)],
        out_specs=(vm, vm),
        scratch_shapes=[pltpu.VMEM(mixed.shape, mixed.dtype)]
        + [pltpu.VMEM((WIDE, tokens), jnp.bfloat16)] * 2
        + [pltpu.SemaphoreType.DMA((tokens // BQ,))],
        compiler_params=pltpu.CompilerParams(vmem_limit_bytes=40 << 20),
        cost_estimate=pl.CostEstimate(
            flops=8 * tokens * tokens * NH * HD,
            bytes_accessed=16 * tokens * WIDE,
            transcendentals=tokens * tokens,
        ),
        name="attend",
    )(lengths, mixed)


def attend_back_kernel(
    lengths_ref, mixed_ref, out_ref, stat_ref, gradt_ref,
    gmixed_ref, qt_ref, kt_ref, grad_ref, delta_ref, dqt_ref
):
    tokens = mixed_ref.shape[0]
    ends = ends_of(lengths_ref)
    for first in range(0, tokens, BQ):
        rows = pl.ds(first, BQ)
        for slab in range(SLABS):
            lanes = slab * 128
            qt_ref[lanes : lanes + 128, rows] = (
                mixed_ref[rows, lanes : lanes + 128] * HD ** (-0.5)
            ).T
            kt_ref[lanes : lanes + 128, rows] = mixed_ref[rows, WIDE + lanes : WIDE + lanes + 128].T
        grad_ref[rows, 0:128] = gradt_ref[0:128, rows].T
        grad_ref[rows, 128:256] = jnp.concatenate(
            [gradt_ref[128:192, rows], jnp.zeros((64, BQ), jnp.bfloat16)], axis=0
        ).T
        for h in range(NH):
            product = gradt_ref[h * HD : (h + 1) * HD, rows].astype(jnp.float32) * out_ref[
                h * HD : (h + 1) * HD, rows
            ].astype(jnp.float32)
            delta_ref[h : h + 1, rows] = jnp.sum(product, axis=0, keepdims=True)
    dqt_ref[...] = jnp.zeros_like(dqt_ref)
    lane = lax.broadcasted_iota(jnp.int32, (BQ, 128), 1)

    def key_block(key, carry):
        base = pl.multiple_of(key * BK, BK)
        rows = pl.ds(base, BK)
        key_ids = base + lax.broadcasted_iota(jnp.int32, (BK, BQ), 0)

        def query_block(block, state):
            first = pl.multiple_of(block * BQ, BQ)
            columns = pl.ds(first, BQ)
            start = segment_start(ends, first + lax.broadcasted_iota(jnp.int32, (1, BQ), 1))
            query_ids = first + lax.broadcasted_iota(jnp.int32, (BK, BQ), 1)
            allowed = (key_ids <= query_ids) & (key_ids >= start)
            grad_keys = list(state[:SLABS])
            grad_values = list(state[SLABS:])
            for h in range(NH):
                slab = h // 2
                low, high = slab * 128, slab * 128 + 128
                queries = head_rows(qt_ref[low:high, columns], h)
                scores = nn(mixed_ref[rows, WIDE + low : WIDE + high], queries)
                probs = jnp.where(allowed, jnp.exp(scores - stat_ref[h : h + 1, columns]), 0.0)
                keep = (lane // HD) == (h % 2)
                grads = jnp.where(keep, grad_ref[columns, low:high], 0.0)
                grad_values[slab] += nn(probs.astype(jnp.bfloat16), grads)
                if h == NH - 1 and NH % 2 == 1:
                    grad_rows = jnp.concatenate(
                        [gradt_ref[h * HD : (h + 1) * HD, columns], jnp.zeros((HD, BQ), jnp.bfloat16)],
                        axis=0,
                    )
                else:
                    grad_rows = head_rows(gradt_ref[low:high, columns], h)
                grad_probs = nn(mixed_ref[rows, 2 * WIDE + low : 2 * WIDE + high], grad_rows)
                grad_scores = (probs * (grad_probs - delta_ref[h : h + 1, columns])).astype(
                    jnp.bfloat16
                )
                natural = mixed_ref[columns, low:high]
                grad_keys[slab] += nn(grad_scores, jnp.where(keep, natural, 0.0))
                dqt_ref[h * HD : (h + 1) * HD, columns] += nn(
                    kt_ref[h * HD : (h + 1) * HD, rows], grad_scores
                )
            return tuple(grad_keys) + tuple(grad_values)

        empty = (jnp.zeros((BK, 128), jnp.float32),) * (2 * SLABS)
        stop = jnp.minimum(segment_stop(ends, base + BK - 1, tokens), ends[-1])
        state = lax.fori_loop(key * BK // BQ, (stop - 1) // BQ + 1, query_block, empty)
        for slab in range(SLABS):
            low = slab * 128
            gmixed_ref[rows, WIDE + low : WIDE + low + 128] = (
                state[slab] * HD ** (-0.5)
            ).astype(jnp.bfloat16)
            gmixed_ref[rows, 2 * WIDE + low : 2 * WIDE + low + 128] = state[SLABS + slab].astype(
                jnp.bfloat16
            )
        return carry

    count = (ends[-1] + BK - 1) // BK
    lax.fori_loop(0, count, key_block, 0)

    def padded_block(key, carry):
        rows = pl.ds(pl.multiple_of(key * BK, BK), BK)
        gmixed_ref[rows, WIDE:] = jnp.zeros((BK, 2 * WIDE), jnp.bfloat16)
        return carry

    lax.fori_loop(count, tokens // BK, padded_block, 0)
    for first in range(0, tokens, BQ):
        rows = pl.ds(first, BQ)
        for slab in range(SLABS):
            low = slab * 128
            gmixed_ref[rows, low : low + 128] = (
                (dqt_ref[low : low + 128, rows] * HD ** (-0.5)).T.astype(jnp.bfloat16)
            )


def attend_back(lengths, mixed, out, stat, gradt):
    tokens = mixed.shape[0]
    vm = pl.BlockSpec(memory_space=pltpu.VMEM)
    return pl.pallas_call(
        attend_back_kernel,
        out_shape=jax.ShapeDtypeStruct((tokens, 3 * WIDE), jnp.bfloat16),
        in_specs=[pl.BlockSpec(memory_space=pltpu.SMEM)] + [vm] * 4,
        out_specs=vm,
        scratch_shapes=[
            pltpu.VMEM((WIDE, tokens), jnp.bfloat16),
            pltpu.VMEM((WIDE, tokens), jnp.bfloat16),
            pltpu.VMEM((tokens, WIDE), jnp.bfloat16),
            pltpu.VMEM((8, tokens), jnp.float32),
            pltpu.VMEM((WIDE, tokens), jnp.float32),
        ],
        compiler_params=pltpu.CompilerParams(vmem_limit_bytes=50 << 20),
        cost_estimate=pl.CostEstimate(
            flops=20 * tokens * tokens * NH * HD,
            bytes_accessed=32 * tokens * WIDE,
            transcendentals=tokens * tokens,
        ),
        name="attend_back",
    )(lengths, mixed, out, stat, gradt)


class Copies:
    def __init__(self, send, recv):
        self.send, self.recv, self.made, self.started = send, recv, 0, []

    def plan(self, source, target, device):
        index = self.made
        self.made += 1
        return pltpu.make_async_remote_copy(
            src_ref=source,
            dst_ref=target,
            send_sem=self.send.at[index],
            recv_sem=self.recv.at[index],
            device_id=device,
            device_id_type=MESH,
        )

    def begin(self, copy, condition=None):
        self.started.append((copy, condition))
        when(condition, copy.start)

    def start(self, source, target, device):
        copy = self.plan(source, target, device)
        self.begin(copy)
        return copy

    def finish(self):
        for copy, condition in self.started:
            when(condition, copy.wait_send)


def when(condition, action):
    if condition is None:
        action()
    else:
        pl.when(condition)(action)


def greet(devices):
    barrier = pltpu.get_barrier_semaphore()
    for device, condition in devices:
        when(
            condition,
            lambda device=device: pl.semaphore_signal(
                barrier, inc=1, device_id=device, device_id_type=MESH
            ),
        )
    present = [1 if condition is None else condition.astype(jnp.int32) for _, condition in devices]
    pl.semaphore_wait(barrier, sum(present))


class Place:
    def __init__(self, line):
        self.dp = dp = lax.axis_index("dp")
        self.tensor = tensor = lax.axis_index("tensor")
        self.spot, self.side = spot, side = dp // 2, dp % 2
        self.chip, self.core = tensor // 2, tensor % 2
        self.has_up, self.has_down = spot + 1 < line, spot > 0
        self.up = (jnp.minimum(spot + 1, line - 1) * 2 + side, tensor)
        self.down = (jnp.maximum(spot - 1, 0) * 2 + side, tensor)
        self.across = (spot * 2 + 1 - side, tensor)
        self.mate = (dp, tensor + 1 - 2 * (tensor % 2))
        self.far = (dp, (tensor + 2) % 4)
        self.corner = (dp, 3 - tensor)

    def everyone(self):
        return [
            (self.mate, None), (self.far, None), (self.corner, None), (self.across, None),
            (self.up, self.has_up), (self.down, self.has_down),
        ]


def comm_call(kernel, name, outputs, inputs, in_specs, out_specs, copies, cid, scratch=(), local=1, limit=50 << 20):
    return pl.pallas_call(
        kernel,
        out_shape=outputs,
        in_specs=in_specs,
        out_specs=out_specs,
        scratch_shapes=list(scratch)
        + [
            pltpu.SemaphoreType.DMA((copies,)),
            pltpu.SemaphoreType.DMA((copies,)),
            pltpu.SemaphoreType.DMA((local,)),
        ],
        compiler_params=pltpu.CompilerParams(
            collective_id=cid, has_side_effects=True, vmem_limit_bytes=limit
        ),
        name=name,
    )(*inputs)


def one_hot(rows, columns, shift, limit):
    lane = lax.broadcasted_iota(jnp.int32, (rows, columns), 0)
    spot = lax.broadcasted_iota(jnp.int32, (rows, columns), 1)
    return ((spot == lane + shift) & (lane < limit)).astype(LOW)


def gather_inputs(tokens, thoughts, positions, cotangent, fc, proj, qkv, out, vectors, n_dp):
    line = n_dp // 2
    hops = line - 1
    rows, width = tokens.shape
    latents = thoughts.shape[0]
    window = rows // latents
    shard = fc.shape[0]
    half_rows = rows // 2
    share = width // (n_dp * 4)

    def kernel(
        pos_ref, tokens_in, thoughts_in, cot_ref, fc_ref, proj_ref, qkv_in, out_in, *refs
    ):
        given = (tokens_in, thoughts_in, qkv_in, out_in) + refs[: len(vectors)]
        (
            normed_out, mixed_out, mix_out, fc_near, fc_side, fc_far, proj_near, cot_out, out_out,
            hidden_out, vec_out, pos_out,
            hidden_ref, mix_ref, vec_ref, tile,
            land, mix_land, tiles, tile_land, normed, mixed, out_turned,
            *held, arrive, send, recv, local,
        ) = refs[len(vectors) :]
        arrivals = [
            pltpu.make_async_copy(given[i], held[i], arrive.at[i]) for i in range(len(given))
        ]
        for copy in arrivals:
            copy.start()
        tokens_ref, thoughts_ref, qkv_ref, out_ref = held[:4]
        vec_refs = held[4:]
        arrivals[0].wait()
        arrivals[1].wait()
        pos_row = lax.broadcasted_iota(jnp.int32, (latents, 128), 0)
        places = jnp.zeros((latents, 128), jnp.int32)
        for w in range(latents):
            places = jnp.where(pos_row == w, pos_ref[w], places)
            span = pl.ds(w * window, window)
            here = lax.broadcasted_iota(jnp.int32, (window, 1), 0) == pos_ref[w] - w * window
            hidden_ref[span] = jnp.where(
                here, thoughts_ref[w : w + 1].astype(F32), tokens_ref[span].astype(F32)
            ).astype(LOW)
        pos_out[...] = places
        for copy in arrivals[2:]:
            copy.wait()
        turned = qkv_ref[...].astype(F32).T
        extra = out_ref[...].astype(F32)
        pieces = []
        for p in range(3):
            for h in range(NH):
                low = (h * 3 + p) * HD
                pieces.append(turned[low : low + HD])
            pieces.append(extra[p * HD : (p + 1) * HD])
        mix_ref[...] = jnp.concatenate(pieces, axis=0).T.astype(LOW)
        tile[...] = jnp.zeros_like(tile)
        row = 0
        for ref in vec_refs:
            count, size = ref.shape
            tile[row : row + count, 0:size] = ref[...].astype(F32)
            row += count
        vec_ref[...] = tile[...].astype(LOW)
        at = Place(line)
        dp, tensor, spot, side = at.dp, at.tensor, at.spot, at.side
        mate_row, far_row, corner_row = at.mate[1], at.far[1], at.corner[1]
        greet(at.everyone())
        copies = Copies(send, recv)
        MIX, FC, PROJ, VEC = range(4)
        own = [mix_ref, fc_ref, proj_ref, tiles.at[dp]]

        def seat(item, position):
            if item == MIX:
                return mix_land.at[position * 2 + side]
            if item == FC:
                return fc_near.at[position]
            if item == PROJ:
                return proj_near.at[position]
            return tiles.at[position * 2 + side]

        def plan(item, hop):
            above, below = jnp.maximum(spot - hop, 0), jnp.minimum(spot + hop, line - 1)
            came_up = jnp.maximum(spot - 1 - hop, 0)
            came_down = jnp.minimum(spot + 1 + hop, line - 1)
            made = {
                "up": copies.plan(
                    own[item] if hop == 0 else seat(item, above), seat(item, above), at.up
                ),
                "down": copies.plan(
                    own[item] if hop == 0 else seat(item, below), seat(item, below), at.down
                ),
                "onward": [],
            }
            for position in (came_up, came_down):
                onward = []
                if item in (MIX, VEC):
                    onward.append(copies.plan(seat(item, position), seat(item, position), at.across))
                if item == FC:
                    onward.append(copies.plan(fc_near.at[position], fc_side.at[position], at.across))
                    onward.append(copies.plan(fc_near.at[position], fc_far.at[position], at.far))
                made["onward"].append(onward)
            return made

        plans = [[plan(item, hop) for hop in range(hops)] for item in range(4)]

        def launch(item):
            copies.begin(plans[item][0]["up"], at.has_up)
            copies.begin(plans[item][0]["down"], at.has_down)

        def handle(item, hop):
            made = plans[item][hop]
            for way, key, comes, goes in (
                (0, "up", spot - 1 - hop >= 0, at.has_up),
                (1, "down", spot + 1 + hop < line, at.has_down),
            ):
                when(comes, made[key].wait_recv)
                if hop + 1 < hops:
                    copies.begin(plans[item][hop + 1][key], comes & goes)
                for copy in made["onward"][way]:
                    copies.begin(copy, comes)

        def settle(item):
            for hop in range(hops):
                for way, comes in ((0, spot - 1 - hop >= 0), (1, spot + 1 + hop < line)):
                    for copy in plans[item][hop]["onward"][way]:
                        when(comes, copy.wait_recv)

        stays = []

        def stay(source, target):
            copy = pltpu.make_async_copy(source, target, local.at[len(stays)])
            copy.start()
            stays.append(copy)
            return copy

        vec_made = [
            copies.start(vec_ref, tile_land.at[i], device)
            for i, device in enumerate((at.mate, at.far, at.corner))
        ]
        parts = [pl.ds(0, half_rows), pl.ds(half_rows, half_rows)]
        launch(MIX)
        far_made = [
            copies.start(hidden_ref.at[part], land.at[far_row_here, part], at.far)
            for far_row_here in (2,)
            for part in parts
        ]
        mix_side = copies.start(mix_ref, mix_land.at[dp], at.across)
        launch(FC)
        fc_sides = [
            copies.start(fc_ref, fc_side.at[spot], at.across),
            copies.start(fc_ref, fc_far.at[spot], at.far),
        ]
        mate_made = copies.start(hidden_ref, land.at[1], at.mate)
        cot_made = copies.start(cot_ref, cot_out, at.mate)
        stay(hidden_ref, hidden_out)
        stay(fc_ref, fc_near.at[spot])
        stay(proj_ref, proj_near.at[spot])
        mix_land[dp] = mix_ref[...]
        for copy in vec_made:
            copy.wait_recv()
        merged = jnp.zeros((VEC_ROWS, 128), F32)
        bias_rows = jnp.zeros((VEC_ROWS, 128), F32)
        row_ids = lax.broadcasted_iota(jnp.int32, (VEC_ROWS, 128), 0)
        for i, index in enumerate((tensor, mate_row, far_row, corner_row)):
            tile = vec_ref[...] if i == 0 else tile_land[i - 1]
            merged += nn(tile, one_hot(128, 128, index * share, share))
            bias_rows = jnp.where(row_ids == 8 + index, tile[8:9].astype(F32), bias_rows)
        tiles[dp] = jnp.where(row_ids < 8, merged, bias_rows).astype(LOW)
        launch(VEC)
        vec_side = copies.start(tiles.at[dp], tiles.at[dp], at.across)

        def norm_rows(source, index):
            @pl.loop(0, rows // 128)
            def _(i):
                span = pl.ds(pl.multiple_of(i * 128, 128), 128)
                normed[index, span] = normalize(source[span].astype(F32))[0].astype(LOW)

            stay(normed.at[index], normed_out.at[index])

        def relay(i):
            far_made[i].wait_recv()
            return copies.start(land.at[2, parts[i]], land.at[3, parts[i]], at.mate)

        def mix_rows(index):
            @pl.loop(0, rows // 256)
            def _(i):
                span = pl.ds(pl.multiple_of(i * 256, 256), 256)
                turned = normed[index, span].astype(F32) * whole[0:1] + whole[1:2]
                weight = mix_land[...].reshape(width, width)
                mixed[index, span] = (nn(turned.astype(LOW), weight) + bias).astype(LOW)

            stay(mixed.at[index], mixed_out.at[index])

        norm_rows(hidden_ref, tensor)
        relayed = []
        for step in range(hops + 2):
            for item, hop in ((MIX, step), (VEC, step), (FC, step - 1), (PROJ, step - 2)):
                if 0 <= hop < hops:
                    handle(item, hop)
            if step == 0:
                launch(PROJ)
                mate_made.wait_recv()
                norm_rows(land.at[1], mate_row)
                relayed.append(relay(0))
            if step == 1:
                relayed.append(relay(1))
                norm_rows(land.at[2], far_row)
            if step == hops - 1:
                for copy in relayed:
                    copy.wait_recv()
                norm_rows(land.at[3], corner_row)
            if step == hops:
                mix_side.wait_recv()
                vec_side.wait_recv()
                settle(MIX)
                settle(VEC)
                whole = jnp.zeros((VEC_ROWS, width), F32)
                for i in range(n_dp):
                    whole += nn(tiles[i], one_hot(128, width, i * shard, shard))
                vec_out[...] = whole
                for i, block in enumerate((tensor, far_row)):
                    vec_out[12 + i : 13 + i] = units_row(whole[8:12], block, n_dp)
                lane = lax.broadcasted_iota(jnp.int32, (width, WIDE), 0)
                column = lax.broadcasted_iota(jnp.int32, (width, WIDE), 1)
                pick = (lane == column + tensor * (NH * HD)) & (column < NH * HD)
                picked = nn(whole.astype(LOW), pick.astype(LOW))
                bias = jnp.concatenate(
                    [picked[2:3], jnp.zeros((1, WIDE), F32), picked[3:4]], axis=1
                )
                mix_rows(tensor)
                mix_rows(mate_row)
        mix_rows(far_row)
        mix_rows(corner_row)
        stay(mix_land, mix_out)
        weight = mix_land[...].reshape(width, width)
        for part in range(3):
            low = part * WIDE + WIDE - 128
            turned = weight[:, low : low + 128].T
            out_turned[part * HD : (part + 1) * HD] = turned[128 - HD :]
        stay(out_turned, out_out)
        settle(FC)
        for copy in fc_sides:
            copy.wait_recv()
        cot_made.wait_recv()
        copies.finish()
        for copy in stays:
            copy.wait()

    low = lambda *shape: jax.ShapeDtypeStruct(shape, LOW)
    outputs = (
        low(4, rows, width), low(4, rows, width), low(n_dp, shard, width),
        low(line, shard, width), low(line, shard, width), low(line, shard, width),
        low(line, shard, width), low(rows, width), low(NH * HD, width), low(rows, width),
        jax.ShapeDtypeStruct((VEC_ROWS, width), F32),
        jax.ShapeDtypeStruct((latents, 128), jnp.int32),
    )
    scratch = [
        pltpu.VMEM((rows, width), LOW),
        pltpu.VMEM((shard, 3 * WIDE), LOW),
        pltpu.VMEM((VEC_ROWS, 128), LOW),
        pltpu.VMEM((VEC_ROWS, 128), F32),
        pltpu.VMEM((4, rows, width), LOW),
        pltpu.VMEM((n_dp, shard, width), LOW),
        pltpu.VMEM((n_dp, VEC_ROWS, 128), LOW),
        pltpu.VMEM((3, VEC_ROWS, 128), LOW),
        pltpu.VMEM((4, rows, width), LOW),
        pltpu.VMEM((4, rows, width), LOW),
        pltpu.VMEM((NH * HD, width), LOW),
    ]
    given = (tokens, thoughts, qkv, out, *vectors)
    scratch += [pltpu.VMEM(x.shape, x.dtype) for x in given]
    scratch.append(pltpu.SemaphoreType.DMA((len(given),)))
    return comm_call(
        kernel,
        "gather_inputs",
        outputs,
        (positions, tokens, thoughts, cotangent, fc, proj, qkv, out, *vectors),
        [SM] + [ANY] * (7 + len(vectors)),
        (ANY,) * 10 + (VM, VM),
        3 + 2 + 1 + 2 + 2 + 1 + 2 + hops * (2 * 4 + 2 * 4),
        0,
        scratch=scratch,
        local=3 + 8 + 2,
    )


def after_attention(attended, out_own, out_far, hidden, vec_all, n_dp, cid):
    head_width, slots = attended.shape
    rows, width = hidden.shape
    half_rows = rows // 2

    def kernel(
        heads_ref, own_ref, far_ref, hidden_ref, vec_ref,
        both_out, middle_out, two_out,
        land, part, part_low, part_land, two, send, recv, local,
    ):
        at = Place(n_dp // 2)
        greet([(at.far, None), (at.mate, None)])
        copies = Copies(send, recv)
        cores = (at.core, 1 - at.core)
        made = [None, None]
        for i in (1, 0):
            theirs = pl.multiple_of(((1 - at.chip) * 2 + cores[i]) * rows, rows)
            made[i] = copies.start(heads_ref.at[:, pl.ds(theirs, rows)], land.at[i], at.far)
        stays = []

        def stay(source, target):
            stays.append(pltpu.make_async_copy(source, target, local.at[len(stays)]))
            stays[-1].start()

        spans = []
        for i in range(2):
            ours = pl.multiple_of((at.chip * 2 + cores[i]) * rows, rows)
            spans.append(pl.ds(ours, rows))
            stay(heads_ref.at[:, spans[i]], both_out.at[0, :, i * rows : (i + 1) * rows])
            part[i] = tn(heads_ref[:, spans[i]], own_ref[...])
        sums = None
        for i in (1, 0):
            made[i].wait_recv()
            stay(land.at[i], both_out.at[1, :, i * rows : (i + 1) * rows])
            part[i] += tn(land[i], far_ref[...])
            if i == 1:
                part_low[...] = part[1].astype(LOW)
                sums = copies.start(part_low, part_land, at.mate)
        sums.wait_recv()
        mated = []
        for piece in range(2):

            @pl.loop(0, half_rows // 128)
            def _(i):
                span = pl.ds(pl.multiple_of(piece * half_rows + i * 128, 128), 128)
                middle = (
                    hidden_ref[span].astype(F32)
                    + part[0, span]
                    + part_land[span].astype(F32)
                    + vec_ref[4:5]
                )
                middle_out[span] = middle
                two[span] = (normalize(middle)[0] * vec_ref[5:6] + vec_ref[6:7]).astype(LOW)

            span = pl.ds(piece * half_rows, half_rows)
            mated.append(copies.start(two.at[span], two_out.at[1, span], at.mate))
        stay(two, two_out.at[0])
        for copy in mated:
            copy.wait_recv()
        copies.finish()
        for copy in stays:
            copy.wait()

    return comm_call(
        kernel,
        "after_attention",
        (
            jax.ShapeDtypeStruct((2, head_width, 2 * rows), LOW),
            jax.ShapeDtypeStruct((rows, width), F32),
            jax.ShapeDtypeStruct((2, rows, width), LOW),
        ),
        (attended, out_own, out_far, hidden, vec_all),
        [VM] * 5,
        (ANY, VM, ANY),
        5,
        cid,
        scratch=[
            pltpu.VMEM((2, head_width, rows), LOW),
            pltpu.VMEM((2, rows, width), F32),
            pltpu.VMEM((rows, width), LOW),
            pltpu.VMEM((rows, width), LOW),
            pltpu.VMEM((rows, width), LOW),
        ],
        local=5,
    )


def before_attention_back(lengths, two, middle, cotangent, both, out_own, out_far, vec_all, n_dp, cid):
    _, rows, width = two.shape
    head_width = out_own.shape[0]
    half_rows = rows // 2

    def kernel(
        lengths_ref, two_ref, middle_ref, cot_ref, both_ref, own_ref, far_ref, vec_ref,
        heads_out, grad_out, own_out, far_out, vec_out,
        two_land, mid, stay_heads, sent_heads, send, recv, local,
    ):
        at = Place(n_dp // 2)
        greet([(at.far, None), (at.mate, None)])
        copies = Copies(send, recv)
        halves = [pl.ds(0, half_rows), pl.ds(half_rows, half_rows)]
        sums = [copies.start(two_ref.at[1, span], two_land.at[span], at.mate) for span in halves]
        vec_out[...] = jnp.zeros_like(vec_out)
        first_row = at.tensor * rows
        live = ends_of(lengths_ref)[-1]
        mated = []
        for piece in range(2):
            sums[piece].wait_recv()

            @pl.loop(0, half_rows // 128)
            def _(i):
                start = pl.multiple_of(piece * half_rows + i * 128, 128)
                span = pl.ds(start, 128)
                grad = two_ref[0, span].astype(F32) + two_land[span].astype(F32)
                normed, inverse = normalize(middle_ref[span])
                ids = first_row + start + lax.broadcasted_iota(jnp.int32, (128, 1), 0)
                final = jnp.where(ids < live, cot_ref[span].astype(F32), 0.0)
                total = final + norm_back(normed, inverse, grad, vec_ref[5:6])
                grad_out[span] = total
                mid[0, span] = total.astype(LOW)
                for row, term in ((4, total), (5, normed * grad), (6, grad), (7, final)):
                    vec_out[row : row + 1] += jnp.sum(term, axis=0, keepdims=True)

            mated.append(copies.start(mid.at[0, halves[piece]], mid.at[1, halves[piece]], at.mate))
        cores = (at.core, 1 - at.core)
        made, stays = [], []
        for i in range(2):
            if i == 1:
                for copy in mated:
                    copy.wait_recv()
            ours = pl.ds(pl.multiple_of((at.chip * 2 + cores[i]) * rows, rows), rows)
            sent_heads[i] = nt(far_ref[...], mid[i]).astype(LOW)
            made.append(copies.start(sent_heads.at[i], heads_out.at[:, ours], at.far))
            stay_heads[i] = nt(own_ref[...], mid[i]).astype(LOW)
            stays.append(
                pltpu.make_async_copy(stay_heads.at[i], heads_out.at[:, ours], local.at[i])
            )
            stays[-1].start()
        grads = mid[...].reshape(2 * rows, width)
        own_out[...] = nn(both_ref[0], grads).astype(LOW)
        far_out[...] = nn(both_ref[1], grads).astype(LOW)
        for copy in made:
            copy.wait_recv()
        copies.finish()
        for copy in stays:
            copy.wait()

    return comm_call(
        kernel,
        "before_attention_back",
        (
            jax.ShapeDtypeStruct((head_width, 4 * rows), LOW),
            jax.ShapeDtypeStruct((rows, width), F32),
            jax.ShapeDtypeStruct((head_width, width), LOW),
            jax.ShapeDtypeStruct((head_width, width), LOW),
            jax.ShapeDtypeStruct((VEC_ROWS, width), F32),
        ),
        (lengths, two, middle, cotangent, both, out_own, out_far, vec_all),
        [pl.BlockSpec(memory_space=pltpu.SMEM)] + [VM] * 7,
        (ANY,) + (VM,) * 4,
        6,
        cid,
        scratch=[
            pltpu.VMEM((rows, width), LOW),
            pltpu.VMEM((2, rows, width), LOW),
            pltpu.VMEM((2, head_width, rows), LOW),
            pltpu.VMEM((2, head_width, rows), LOW),
        ],
        local=2,
    )


def finish_grads(lengths, arrays, n_dp, cid):
    part_rows = arrays["hidden"].shape[0] // 4
    names = list(arrays)
    kept = [name for name in names if name != "out_far"]
    line = n_dp // 2
    shard = arrays["mix"].shape[1]
    rows, width = arrays["hidden"].shape
    group = 4 * rows
    latents = arrays["positions"].shape[0]
    window = rows // latents
    far_end = line - 1
    slots = [(distance, way) for distance in range(far_end, 0, -1) for way in (0, 1)] + [(0, 0)]
    last = len(slots) - 1
    share = width // (n_dp * 4)
    FC, PROJ, MIX, VEC = range(4)

    def kernel(lengths_ref, *refs):
        refs = list(refs)

        def take(number):
            taken = refs[:number]
            del refs[:number]
            return taken

        source = dict(zip(names, take(len(names))))
        fc_out, proj_out, mix_out, vec_out, tokens_out, thoughts_out, block_out = take(7)
        held = dict(zip(kept, take(len(kept))))
        cross_send, cross_land = [None, None] + take(2), [None, None] + take(2)
        hop_send, hop_land = take(4), take(4)
        (
            part, mate_land, far_send, far_land, last_land, total, vec_mine, vec_land, vec_near,
            plain_sum, column_sum, out_land, tokens_kept, thoughts_kept, block_kept, send, recv,
            local,
        ) = refs
        out = [fc_out, proj_out, mix_out, None]
        at = Place(line)
        tensor, spot, side = at.tensor, at.spot, at.side
        mate_row, far_row, corner_row = at.mate[1], at.far[1], at.corner[1]
        copies = Copies(send, recv)
        loads = {}
        held["out_far"] = out_land
        for i, name in enumerate(kept):
            loads[name] = pltpu.make_async_copy(source[name], held[name], local.at[i])

        def load(*group):
            for name in group:
                loads[name].start()

        load("fc_near", "fc_near_side", "fc_cross", "proj_near", "proj_near_far", "proj_cross")
        load("grad_mixed", "mix")
        greet(at.everyone())

        def block_of(slot):
            distance, way = slots[slot]
            if way == 0:
                return jnp.minimum(spot + distance, far_end), spot + distance < line
            return jnp.maximum(spot - distance, 0), spot - distance >= 0

        crosses, hops = [], []
        for slot in range(len(slots)):
            block, _ = block_of(slot)
            crosses.append(
                {
                    i: copies.plan(cross_send[i].at[block], cross_land[i].at[block], at.across)
                    for i in (MIX, VEC)
                }
            )
            if slot < last:
                hops.append(
                    [
                        copies.plan(
                            hop_send[i].at[slot],
                            hop_land[i].at[slot],
                            (at.up, at.down)[slots[slot][1]],
                        )
                        for i in range(4)
                    ]
                )

        def cross(distance, items):
            for slot in range(len(slots)):
                if slots[slot][0] == distance:
                    for i in items:
                        copies.begin(crosses[slot][i], block_of(slot)[1])

        terms = (
            ("fc_near", "fc_near_side", "fc_cross"),
            ("proj_near", "proj_near_far", "proj_cross"),
        )

        def own_term(i, block):
            if i in (FC, PROJ):
                return sum(held[name][block].astype(F32) for name in terms[i])
            if i == MIX:
                return total[block * 2 + side].astype(F32)
            return vec_near[block * 2 + side]

        def handle(slot, i):
            block, inside = block_of(slot)
            behind = (at.has_down, at.has_up)[slots[slot][1]]
            outer = slot - 2

            def work():
                value = own_term(i, block)
                if i in (MIX, VEC):
                    crosses[slot][i].wait_recv()
                    value = value + cross_land[i][block].astype(F32)
                if outer < 0:
                    hop_send[i][slot] = value.astype(hop_send[i].dtype)
                    return

                @pl.when(behind)
                def _():
                    hops[outer][i].wait_recv()
                    hop_send[i][slot] = (value + hop_land[i][outer].astype(F32)).astype(
                        hop_send[i].dtype
                    )

                @pl.when(jnp.logical_not(behind))
                def _():
                    hop_send[i][slot] = value.astype(hop_send[i].dtype)

            when(inside, work)
            copies.begin(hops[slot][i], inside)

        def handle_all(distance, items):
            for slot in range(last):
                if slots[slot][0] == distance:
                    for i in items:
                        handle(slot, i)

        def close(i, target):
            value = own_term(i, spot)
            if i in (MIX, VEC):
                crosses[last][i].wait_recv()
                value = value + cross_land[i][spot].astype(F32)
            target[...] = value
            for way, behind in enumerate((at.has_down, at.has_up)):

                def add(way=way):
                    hops[last - 2 + way][i].wait_recv()
                    target[...] += hop_land[i][last - 2 + way].astype(F32)

                when(behind, add)

        for name in ("fc_near", "fc_near_side", "fc_cross", "proj_near", "proj_near_far", "proj_cross"):
            loads[name].wait()
        out_made = copies.start(source["out_far"], out_land, at.far)
        handle_all(far_end, (FC, PROJ))
        load("group", "out_own", "vec_all", "vec_part", "bias_own", "bias_far")
        load("last", "hidden", "grad_middle", "middle", "positions")
        loads["grad_mixed"].wait()
        loads["mix"].wait()

        def row_part(index):
            @pl.loop(0, rows // 256)
            def _(i):
                span = pl.ds(pl.multiple_of(i * 256, 256), 256)
                weight = held["mix"][...].reshape(width, width)
                part[index, span] = nt(held["grad_mixed"][index, span], weight).astype(LOW)

        row_part(corner_row)
        mate_far = copies.start(part.at[corner_row], mate_land.at[1], at.mate)
        row_part(mate_row)
        mate_own = copies.start(part.at[mate_row], mate_land.at[0], at.mate)
        row_part(far_row)
        mate_far.wait_recv()
        far_made = []

        def send_far(count):
            for i in range(len(far_made), len(far_made) + count):
                span = pl.ds(i * part_rows, part_rows)
                far_send[span] = (
                    mate_land[1, span].astype(F32) + part[far_row, span].astype(F32)
                ).astype(LOW)
                far_made.append(copies.start(far_send.at[span], far_land.at[span], at.far))

        send_far(4)
        row_part(tensor)
        if far_end > 1:
            handle_all(far_end - 1, (FC, PROJ))
        loads["last"].wait()
        last_copy = copies.start(held["last"].at[1], last_land, at.mate)
        for name in ("group", "out_own", "vec_all", "vec_part", "bias_own", "bias_far"):
            loads[name].wait()
        out_made.wait_recv()

        plain_sum[...] = jnp.zeros_like(plain_sum)
        column_sum[...] = jnp.zeros_like(column_sum)

        @pl.loop(0, group // 256)
        def _(i):
            block, start = i // (rows // 256), (i % (rows // 256)) * 256
            span = pl.ds(pl.multiple_of(start, 256), 256)
            grad = held["grad_mixed"][block, span]
            plain_sum[...] += tn(held["group"][block, span], grad)
            column_sum[...] += jnp.sum(grad.astype(F32), axis=0, keepdims=True)

        plain, columns = plain_sum[...], column_sum[...]
        turned = held["vec_all"][...].T
        weight = held["mix"][...].reshape(width, width).astype(F32)
        gain_grad = jnp.sum(plain * weight, axis=1, keepdims=True)
        shift_grad = jnp.sum(weight * columns, axis=1, keepdims=True)
        scaled = plain * turned[:, 0:1] + turned[:, 1:2] * columns
        extras = []
        out_sum = held["out_own"][...].astype(F32) + held["out_far"][...].astype(F32)
        for p in range(3):
            piece = out_sum[p * HD : (p + 1) * HD]
            extras.append(jnp.zeros((width, WIDE - 128), F32))
            extras.append(jnp.concatenate([jnp.zeros((128 - HD, width), F32), piece], axis=0).T)
        scaled = scaled + jnp.concatenate(extras, axis=1)
        for k in range(n_dp):
            total[k] = scaled[k * shard : (k + 1) * shard].astype(LOW)
        for block in range(line):
            cross_send[MIX][block] = total[block * 2 + 1 - side]
        cross(far_end, [MIX])
        cross(far_end - 1, [MIX])
        vec_mine[...] = held["vec_part"][...]
        flat = jnp.concatenate(
            [gain_grad, shift_grad, jnp.zeros((width, 6), F32)], axis=1
        ).T
        vec_mine[0:2] = flat[0:2]
        vec_mine[8:12] = units_rows_back(held["bias_own"][...], tensor, n_dp) + units_rows_back(
            held["bias_far"][...], far_row, n_dp
        )
        vec_lane = lax.broadcasted_iota(jnp.int32, (1, width), 1)
        in_part = (vec_lane >= tensor * (NH * HD)) & (vec_lane < (tensor + 1) * (NH * HD))
        for row, low in ((2, 0), (3, 2 * WIDE)):
            line_up = jnp.concatenate([columns[:, low : low + WIDE]] + [columns[:, 0:WIDE]] * 2, axis=1)
            placed = jnp.zeros((1, width), F32)
            for t in range(4):
                shifted = pltpu.roll(line_up, t * NH * HD, 1)
                placed = jnp.where(tensor == t, shifted, placed)
            vec_mine[row : row + 1] = jnp.where(in_part, placed, 0.0)
        vec_made = [
            copies.start(vec_mine, vec_land.at[i], device)
            for i, device in enumerate((at.mate, at.far, at.corner))
        ]
        for distance in range(far_end - 2, 0, -1):
            handle_all(distance, (FC, PROJ))
        for copy in vec_made:
            copy.wait_recv()
        vec_sum = vec_mine[...] + vec_land[0] + vec_land[1] + vec_land[2]
        for k in range(n_dp):
            vec_near[k] = pltpu.roll(vec_sum, (width - k * shard) % width, 1)[:, 0:128]
        for block in range(line):
            cross_send[VEC][block] = vec_near[block * 2 + 1 - side]
        cross(far_end, [VEC])
        cross(far_end - 1, [VEC])
        live = ends_of(lengths_ref)[-1]
        stays = []

        def close_rows(i):
            if i == 0:
                for name in ("hidden", "grad_middle", "middle", "positions"):
                    loads[name].wait()
                last_copy.wait_recv()
                mate_own.wait_recv()
            far_made[i].wait_recv()
            span = pl.ds(i * part_rows, part_rows)
            ids = tensor * rows + i * part_rows + lax.broadcasted_iota(
                jnp.int32, (part_rows, 1), 0
            )
            final = (
                held["middle"][span]
                + held["last"][0, span].astype(F32)
                + last_land[span].astype(F32)
                + held["vec_all"][7:8]
            )
            block_kept[span] = jnp.where(ids < live, final, 0.0).astype(LOW)
            grad = (
                part[tensor, span].astype(F32)
                + mate_land[0, span].astype(F32)
                + far_land[span].astype(F32)
            )
            normed, inverse = normalize(held["hidden"][span].astype(F32))
            grad = held["grad_middle"][span] + norm_back(
                normed, inverse, grad, held["vec_all"][0:1]
            )
            for w in range(part_rows // window):
                index = i * (part_rows // window) + w
                here = (
                    lax.broadcasted_iota(jnp.int32, (window, 1), 0)
                    == held["positions"][index : index + 1, 0:1] - index * window
                )
                piece = grad[w * window : (w + 1) * window]
                tokens_kept[pl.ds(index * window, window)] = jnp.where(here, 0.0, piece)
                thoughts_kept[index : index + 1] = jnp.sum(
                    jnp.where(here, piece, 0.0), axis=0, keepdims=True
                )
            moves = [(tokens_kept.at[span], tokens_out.at[span])]
            moves.append((block_kept.at[span], block_out.at[span]))
            if i == 3:
                moves.append((thoughts_kept, thoughts_out))
            for kept_ref, out_ref in moves:
                stays.append(
                    pltpu.make_async_copy(kept_ref, out_ref, local.at[len(kept) + len(stays)])
                )
                stays[-1].start()

        done = 0
        for distance in range(far_end, 0, -1):
            handle_all(distance, (MIX, VEC))
            if distance >= 2:
                cross(distance - 2, (MIX, VEC))
            if distance <= 3:
                close_rows(done)
                done += 1
        for i in range(done, 4):
            close_rows(i)
        for i in (FC, PROJ, MIX):
            close(i, out[i])
        close(VEC, vec_out)
        copies.finish()
        for copy in stays:
            copy.wait()

    f32 = lambda *shape: jax.ShapeDtypeStruct(shape, F32)
    outputs = (
        f32(shard, width), f32(shard, width), f32(shard, width), f32(VEC_ROWS, 128),
        f32(rows, width), f32(latents, width), jax.ShapeDtypeStruct((rows, width), LOW),
    )
    scratch = [pltpu.VMEM(arrays[name].shape, arrays[name].dtype) for name in kept]
    for number, wide in ((line, 1), (line, 1), (last, 3), (last, 3)):
        scratch += [pltpu.VMEM((number, shard, width), LOW)] * wide
        scratch.append(pltpu.VMEM((number, VEC_ROWS, 128), F32))
    scratch += [
        pltpu.VMEM((4, rows, width), LOW),
        pltpu.VMEM((2, rows, width), LOW),
        pltpu.VMEM((rows, width), LOW),
        pltpu.VMEM((rows, width), LOW),
        pltpu.VMEM((rows, width), LOW),
        pltpu.VMEM((n_dp, shard, width), LOW),
        pltpu.VMEM((VEC_ROWS, width), F32),
        pltpu.VMEM((3, VEC_ROWS, width), F32),
        pltpu.VMEM((n_dp, VEC_ROWS, 128), F32),
        pltpu.VMEM((width, width), F32),
        pltpu.VMEM((1, width), F32),
        pltpu.VMEM(arrays["out_far"].shape, LOW),
        pltpu.VMEM((rows, width), F32),
        pltpu.VMEM((latents, width), F32),
        pltpu.VMEM((rows, width), LOW),
    ]
    return comm_call(
        kernel,
        "finish_grads",
        outputs,
        (lengths, *arrays.values()),
        [SM] + [ANY] * len(names),
        (VM,) * 4 + (ANY,) * 3,
        (last + 1) * 2 + last * 4 + 1 + 2 + 4 + 3 + 1,
        cid,
        scratch=scratch,
        local=len(kept) + 9,
        limit=63 << 20,
    )


def unit_kernel(add, line, bias_row, lengths_ref, *refs):
    refs = list(refs)
    rows_ref, grad_own, grad_mate = refs[:3]
    pieces, vec_ref = refs[3:7], refs[7]
    refs = refs[8:]
    if add:
        last_in, two_in = refs[:2]
        refs = refs[2:]
    last_ref, two_ref, fc_near, fc_side, proj_near, proj_side, bias_grad_ref = refs[:7]
    fc_all, proj_all, fc_sum, proj_sum = refs[7:]
    step = pl.program_id(0)
    side, tensor = lax.axis_index("dp") % 2, lax.axis_index("tensor")
    live = ends_of(lengths_ref)[-1]

    @pl.when(step == 0)
    def _():
        for full, near, across in ((fc_all, *pieces[:2]), (proj_all, *pieces[2:])):
            for i in range(line):
                full[2 * i + side] = near[i]
                full[2 * i + 1 - side] = across[i]
        fc_sum[...] = jnp.zeros_like(fc_sum)
        proj_sum[...] = jnp.zeros_like(proj_sum)
        bias_grad_ref[...] = jnp.zeros_like(bias_grad_ref)

    count, width = rows_ref.shape
    half = pl.num_programs(0) // 2
    block = jnp.where(step < half, tensor, tensor + 1 - 2 * (tensor % 2))
    first = block * (half * count) + (step % half) * count
    alive = first + lax.broadcasted_iota(jnp.int32, (count, 1), 0) < live
    rows = rows_ref[...]
    grad = jnp.where(step < half, grad_own[...], grad_mate[...])
    grad = jnp.where(alive, grad, jnp.zeros_like(grad))
    fc = fc_all[...].reshape(width, -1)
    proj = proj_all[...].reshape(width, -1)
    inner = nn(rows, fc) + vec_ref[bias_row : bias_row + 1]
    square = inner * inner
    bend = jnp.tanh(GELU_SCALE * inner * (1.0 + GELU_CUBE * square))
    half = 0.5 * (1.0 + bend)
    activated = (inner * half).astype(LOW)
    slope = half + 0.5 * inner * (1.0 - bend * bend) * GELU_SCALE * (1.0 + 3.0 * GELU_CUBE * square)
    grad_inner = (nn(grad, proj) * slope).astype(LOW)
    last = nt(activated, proj)
    two = nt(grad_inner, fc)
    if add:
        last, two = last + last_in[...], two + two_in[...]
    last_ref[...] = last.astype(last_ref.dtype)
    two_ref[...] = two.astype(two_ref.dtype)
    fc_sum[...] += tn(rows, grad_inner)
    proj_sum[...] += tn(grad, activated)
    bias_grad_ref[...] += jnp.sum(grad_inner.astype(F32), axis=0, keepdims=True)

    @pl.when(step == pl.num_programs(0) - 1)
    def _():
        shard = fc_near.shape[1]
        for sums, near, across in ((fc_sum, fc_near, fc_side), (proj_sum, proj_near, proj_side)):
            for i in range(line):
                even = sums[2 * i * shard : (2 * i + 1) * shard].astype(LOW)
                odd = sums[(2 * i + 1) * shard : (2 * i + 2) * shard].astype(LOW)
                near[i] = jnp.where(side == 0, even, odd)
                across[i] = jnp.where(side == 0, odd, even)


def units_both_ways(lengths, rows, grad, mate_grad, pieces, vec_all, bias_row, before):
    count, width = rows.shape
    line, shard, units = pieces[0].shape
    half = count // ROW_TILE // 2
    tile = pl.BlockSpec((ROW_TILE, width), lambda i: (i, 0))
    fixed = lambda shape: pl.BlockSpec(shape, lambda i: (0,) * len(shape))
    add = before is not None
    kind = LOW if add else F32
    return pl.pallas_call(
        functools.partial(unit_kernel, add, line, bias_row),
        grid=(count // ROW_TILE,),
        out_shape=(
            jax.ShapeDtypeStruct((count, width), kind),
            jax.ShapeDtypeStruct((count, width), kind),
        )
        + (jax.ShapeDtypeStruct((line, shard, units), LOW),) * 4
        + (jax.ShapeDtypeStruct((1, units), F32),        ),
        in_specs=[
            SM,
            tile,
            pl.BlockSpec((ROW_TILE, width), lambda i: (jnp.minimum(i, half - 1), 0)),
            pl.BlockSpec((ROW_TILE, width), lambda i: (jnp.maximum(i - half, 0), 0)),
        ]
        + [fixed((line, shard, units))] * 4
        + [fixed(vec_all.shape)]
        + [tile] * (2 if add else 0),
        out_specs=(tile, tile) + (fixed((line, shard, units)),) * 4 + (fixed((1, units)),),
        scratch_shapes=[pltpu.VMEM((2 * line, shard, units), LOW)] * 2
        + [pltpu.VMEM((width, units), F32)] * 2,
        compiler_params=pltpu.CompilerParams(
            dimension_semantics=("arbitrary",), vmem_limit_bytes=56 << 20
        ),
        cost_estimate=pl.CostEstimate(
            flops=12 * count * width * units,
            bytes_accessed=24 * count * width,
            transcendentals=count * units,
        ),
        name="units_second" if add else "units_first",
    )(lengths, rows, grad, mate_grad, *pieces, vec_all, *(before or ()))


def split_grads(mix_grad, vec, through, share):
    shard, width = mix_grad.shape
    head_width = NH * HD
    count = len(through)

    def kernel(mix_ref, vec_ref, *refs):
        given, (qkv_out, out_out), refs = refs[:count], refs[count : count + 2], refs[count + 2 :]
        small, passed, held, sems = refs[:8], refs[8 : 8 + count], refs[8 + count : -1], refs[-1]
        ins = [pltpu.make_async_copy(given[i], held[i], sems.at[i]) for i in range(count)]
        outs = [
            pltpu.make_async_copy(held[i], passed[i], sems.at[count + i]) for i in range(count)
        ]
        for copy in ins:
            copy.start()
        for i in range(count):
            ins[i].wait()
            outs[i].start()
        tensor = lax.axis_index("tensor")
        turned = mix_ref[...].T
        pieces = []
        for h in range(NH):
            for part in range(3):
                low = part * WIDE + h * HD
                pieces.append(turned[low : low + HD])
        qkv_out[...] = jnp.concatenate(pieces, axis=0).T
        for part in range(3):
            low = part * WIDE + head_width
            out_out[part * HD : (part + 1) * HD] = turned[low : low + HD]
        rows = vec_ref[0:8]
        moved = rows
        for i in range(1, 4):
            moved = jnp.where(tensor == i, pltpu.roll(rows, 128 - i * share, 1), moved)
        for i, row in enumerate((0, 1, 4, 5, 6, 7)):
            small[i][...] = moved[row : row + 1, 0:share]
        small[6][...] = moved[2:4, 0:share]
        small[7][...] = vec_ref[pl.ds(8 + tensor, 1)][:, 0:shard]
        for copy in outs:
            copy.wait()

    f32 = lambda *shape: jax.ShapeDtypeStruct(shape, F32)
    return pl.pallas_call(
        kernel,
        out_shape=(f32(shard, 3 * head_width), f32(head_width, shard))
        + (f32(1, share),) * 6
        + (f32(2, share), f32(1, shard))
        + tuple(jax.ShapeDtypeStruct(x.shape, x.dtype) for x in through),
        in_specs=[VM] * 2 + [ANY] * count,
        out_specs=(VM,) * 10 + (ANY,) * count,
        scratch_shapes=[pltpu.VMEM(x.shape, x.dtype) for x in through]
        + [pltpu.SemaphoreType.DMA((2 * count,))],
        name="split_grads",
    )(mix_grad, vec, *through)


def by_tensor(row, step, index):
    moved = row
    for i in range(1, 4):
        moved = jnp.where(index == i, pltpu.roll(row, (i * step) % row.shape[1], 1), moved)
    return moved


def units_row(rows, block, n_dp):
    width = rows.shape[1]
    shard, step = width // n_dp, n_dp // 4
    lane = lax.broadcasted_iota(jnp.int32, (1, width), 1) // shard
    base = by_tensor(rows, width - step * shard, block)
    total = jnp.zeros((1, width), F32)
    for j in range(n_dp):
        moved = pltpu.roll(base[j % 4 : j % 4 + 1], (j - j // 4) * shard, 1)
        total = jnp.where(lane == j, moved, total)
    return total


def units_rows_back(row, block, n_dp):
    width = row.shape[1]
    shard, step = width // n_dp, n_dp // 4
    lane = lax.broadcasted_iota(jnp.int32, (1, width), 1) // shard
    rows = [jnp.zeros((1, width), F32) for _ in range(4)]
    for j in range(n_dp):
        moved = pltpu.roll(row, (width - (j - j // 4) * shard) % width, 1)
        rows[j % 4] = jnp.where(lane == j // 4, moved, rows[j % 4])
    return by_tensor(jnp.concatenate(rows, axis=0), step * shard, block)


def normalize(values):
    center = jnp.mean(values, axis=-1, keepdims=True)
    offset = values - center
    spread = jnp.mean(offset * offset, axis=-1, keepdims=True)
    inverse = lax.rsqrt(spread + EPSILON)
    return offset * inverse, inverse


def norm_back(normed, inverse, grad, gain):
    scaled = grad * gain
    center = jnp.mean(scaled, axis=-1, keepdims=True)
    along = jnp.mean(scaled * normed, axis=-1, keepdims=True)
    return inverse * (scaled - center - normed * along)


def product(equation, left, right):
    return jnp.einsum(equation, left, right, preferred_element_type=F32)


def per_device(
    tokens,
    thoughts,
    positions,
    lengths,
    attn_norm_gain,
    attn_norm_shift,
    qkv_weight,
    qv_bias,
    attn_out_weight,
    attn_out_bias,
    mlp_norm_gain,
    mlp_norm_shift,
    fc_weight,
    fc_bias,
    proj_weight,
    proj_bias,
    cotangent,
):
    n_dp = lax.axis_size("dp")
    n_tensor = lax.axis_size("tensor")
    rows, width = tokens.shape
    slots = rows * n_tensor
    swap_far = [(i, (i + 2) % n_tensor) for i in range(n_tensor)]

    share = width // (n_dp * n_tensor)
    small = [
        attn_norm_gain[None], attn_norm_shift[None], qv_bias, attn_out_bias[None],
        mlp_norm_gain[None], mlp_norm_shift[None], proj_bias[None], fc_bias[None],
    ]
    (
        group_low, mixed, mix_all, fc_near, fc_side, fc_far_near, proj_near, mate_grad, out_own,
        hidden, vec_all, places,
    ) = gather_inputs(
        tokens, thoughts, positions, cotangent, fc_weight, proj_weight.T, qkv_weight,
        attn_out_weight, small, n_dp,
    )
    mixed = mixed.reshape(slots, -1)
    swap_side = [(i, i + 1 - 2 * (i % 2)) for i in range(n_dp)]
    out_far = lax.ppermute(out_own, "tensor", swap_far)
    proj_far_near = lax.ppermute(proj_near, "tensor", swap_far)
    fc_far_side = lax.ppermute(fc_far_near, "dp", swap_side)
    attended, stats = attend(lengths, mixed)
    sent, out_far, proj_far_near, fc_far_side = lax.optimization_barrier(
        (attended, out_far, proj_far_near, fc_far_side)
    )
    proj_far_side = lax.ppermute(proj_far_near, "dp", swap_side)
    both, middle, chip_two = after_attention(
        sent, out_own, out_far, hidden, vec_all, n_dp, 1
    )
    chip_two, proj_far_side, proj_sent = lax.optimization_barrier(
        (chip_two, proj_far_side, proj_near)
    )
    proj_side = lax.ppermute(proj_sent, "dp", swap_side)
    chip_two = chip_two.reshape(2 * rows, width)

    first = units_both_ways(
        lengths, chip_two, cotangent, mate_grad,
        (fc_far_near, fc_far_side, proj_far_near, proj_far_side), vec_all, 13, None,
    )
    far_fc_near, far_fc_side, far_proj_near, far_proj_side, far_fc_bias = first[2:]
    proj_side_far = lax.ppermute(far_proj_side, "tensor", swap_far)
    fc_far_side_in = lax.ppermute(far_fc_side, "dp", swap_side)
    second = units_both_ways(
        lengths, chip_two, cotangent, mate_grad, (fc_near, fc_side, proj_near, proj_side), vec_all, 12,
        first[:2],
    )
    last_part, grad_two_part, fc_near_grad, fc_side_grad, proj_near_grad, proj_side_grad = second[:6]
    fc_near_side_in = lax.ppermute(fc_side_grad, "dp", swap_side)
    grad_heads, grad_middle, grad_out, far_out, vec_part = before_attention_back(
        lengths, grad_two_part.reshape(2, rows, width), middle, cotangent, both, out_own, out_far,
        vec_all, n_dp, 2,
    )
    fc_cross = far_fc_near + fc_far_side_in
    proj_cross = proj_side_grad + proj_side_far
    grad_heads, fc_cross, proj_cross, far_proj_near = lax.optimization_barrier(
        (grad_heads, fc_cross, proj_cross, far_proj_near)
    )
    fc_cross = lax.ppermute(fc_cross, "tensor", swap_far)
    proj_cross = lax.ppermute(proj_cross, "dp", swap_side)
    proj_near_far = lax.ppermute(far_proj_near, "tensor", swap_far)
    last_low = last_part.reshape(2, rows, width)

    grad_mixed = attend_back(lengths, mixed, attended, stats, grad_heads)
    arrays = {
        "fc_near": fc_near_grad, "fc_near_side": fc_near_side_in, "fc_cross": fc_cross,
        "proj_near": proj_near_grad, "proj_near_far": proj_near_far, "proj_cross": proj_cross,
        "grad_mixed": grad_mixed.reshape(n_tensor, rows, width), "mix": mix_all,
        "last": last_low, "group": group_low,
        "out_own": grad_out, "out_far": far_out,
        "vec_all": vec_all, "vec_part": vec_part, "bias_own": second[6], "bias_far": far_fc_bias,
        "hidden": hidden, "grad_middle": grad_middle, "middle": middle, "positions": places,
    }
    fc_grad, proj_grad, mix_grad, vec, grad_tokens, grad_thoughts, block_out = finish_grads(
        lengths, arrays, n_dp, 8
    )
    parts = split_grads(
        mix_grad, vec, (fc_grad, proj_grad, grad_tokens, grad_thoughts, block_out), share
    )
    qkv_grad, out_grad = parts[:2]
    gain_one, shift_one, out_bias, gain_two, shift_two, last_bias = [p[0] for p in parts[2:8]]
    query_value, hidden_bias = parts[8], parts[9][0]
    fc_grad, proj_grad, grad_tokens, grad_thoughts, block_out = parts[10:]
    return (
        block_out,
        grad_tokens,
        grad_thoughts,
        gain_one,
        shift_one,
        qkv_grad,
        query_value,
        out_grad,
        out_bias,
        gain_two,
        shift_two,
        fc_grad,
        hidden_bias,
        proj_grad.T,
        last_bias,
    )


def solution(mesh):
    rows = P(("dp", "tensor"), None)
    line = P(("dp", "tensor"))
    in_specs = (
        rows, rows, line, P("dp", None), line, line, P("dp", "tensor"),
        P(None, ("dp", "tensor")), P("tensor", "dp"), line, line, line,
        P("dp", "tensor"), line, P("tensor", "dp"), line, rows,
    )
    out_specs = (
        rows, rows, rows, line, line, P("dp", "tensor"), P(None, ("dp", "tensor")),
        P("tensor", "dp"), line, line, line, P("dp", "tensor"), line, P("tensor", "dp"), line,
    )
    return jax.shard_map(
        per_device, mesh=mesh, in_specs=in_specs, out_specs=out_specs, check_vma=False
    )
```

```python
import functools
import math

import jax
import jax.numpy as jnp
from jax import lax
from jax.experimental import pallas as pl
from jax.experimental.pallas import tpu as pltpu
from jax.sharding import PartitionSpec as P

H = 12
HD = 64
FF = 3072
SEQ_DEV = 3
EPSILON = 1e-05
MASKED = -1e30
NH = 3
SLABS = 2
WIDE = SLABS * 128
BQ = 512
BK = 512
VEC_ROWS = 16
ROW_TILE = 256
GELU_SCALE = math.sqrt(2.0 / math.pi)
GELU_CUBE = 0.044715
MESH = pl.DeviceIdType.MESH
ANY = pl.BlockSpec(memory_space=pltpu.HBM)
VM = pl.BlockSpec(memory_space=pltpu.VMEM)
SM = pl.BlockSpec(memory_space=pltpu.SMEM)
LOW = jnp.bfloat16
F32 = jnp.float32


def nn(a, b):
    return lax.dot_general(a, b, (((1,), (0,)), ((), ())), preferred_element_type=jnp.float32)


def nt(a, b):
    return lax.dot_general(a, b, (((1,), (1,)), ((), ())), preferred_element_type=jnp.float32)


def tn(a, b):
    return lax.dot_general(a, b, (((0,), (0,)), ((), ())), preferred_element_type=jnp.float32)


def head_rows(slab, head):
    half = slab[(head % 2) * HD : (head % 2 + 1) * HD]
    zero = jnp.zeros_like(half)
    return jnp.concatenate([half, zero] if head % 2 == 0 else [zero, half], axis=0)


def ends_of(lengths_ref):
    ends = [lengths_ref[0, 0]]
    for i in range(1, SEQ_DEV):
        ends.append(ends[-1] + lengths_ref[0, i])
    return ends


def segment_start(ends, slots):
    start = jnp.zeros_like(slots)
    for i in range(SEQ_DEV):
        start = jnp.where(slots >= ends[i], ends[i], start)
    return start


def segment_stop(ends, slot, slots):
    stop = slots
    for i in reversed(range(SEQ_DEV)):
        stop = jnp.where(slot < ends[i], ends[i], stop)
    return stop


def attend_kernel(lengths_ref, mixed_in, out_ref, stat_ref, mixed_ref, qt_ref, vt_ref, sems):
    tokens = mixed_ref.shape[0]
    ends = ends_of(lengths_ref)
    loads = []
    for i in range(tokens // BQ):
        rows = pl.ds(i * BQ, BQ)
        loads.append(pltpu.make_async_copy(mixed_in.at[rows], mixed_ref.at[rows], sems.at[i]))
        loads[i].start()
    for first in range(0, tokens, BQ):
        rows = pl.ds(first, BQ)
        loads[first // BQ].wait()
        for slab in range(SLABS):
            lanes = slab * 128
            qt_ref[lanes : lanes + 128, rows] = (
                mixed_ref[rows, lanes : lanes + 128] * HD ** (-0.5)
            ).T
            vt_ref[lanes : lanes + 128, rows] = mixed_ref[
                rows, 2 * WIDE + lanes : 2 * WIDE + lanes + 128
            ].T

    def query_block(block, carry):
        first = pl.multiple_of(block * BQ, BQ)
        columns = pl.ds(first, BQ)
        start = segment_start(ends, first + lax.broadcasted_iota(jnp.int32, (1, BQ), 1))
        query_ids = first + lax.broadcasted_iota(jnp.int32, (BK, BQ), 1)
        queries = [
            head_rows(qt_ref[(h // 2) * 128 : (h // 2 + 1) * 128, columns], h) for h in range(NH)
        ]

        def key_block(key, state):
            base = pl.multiple_of(key * BK, BK)
            rows = pl.ds(base, BK)
            key_ids = base + lax.broadcasted_iota(jnp.int32, (BK, BQ), 0)
            allowed = (key_ids <= query_ids) & (key_ids >= start)
            result = []
            for h in range(NH):
                peak, total, acc = state[h]
                slab = h // 2
                scores = nn(mixed_ref[rows, WIDE + slab * 128 : WIDE + slab * 128 + 128], queries[h])
                scores = jnp.where(allowed, scores, MASKED)
                fresh = jnp.maximum(peak, jnp.max(scores, axis=0, keepdims=True))
                weight = jnp.exp(scores - fresh)
                decay = jnp.exp(peak - fresh)
                total = total * decay + jnp.sum(weight, axis=0, keepdims=True)
                values = vt_ref[h * HD : (h + 1) * HD, rows]
                acc = acc * decay + nn(values, weight.astype(jnp.bfloat16))
                result.append((fresh, total, acc))
            return tuple(result)

        empty = tuple(
            (
                jnp.full((1, BQ), MASKED, jnp.float32),
                jnp.zeros((1, BQ), jnp.float32),
                jnp.zeros((HD, BQ), jnp.float32),
            )
            for _ in range(NH)
        )
        state = lax.fori_loop(segment_start(ends, first) // BK, (block + 1) * (BQ // BK), key_block, empty)
        for h in range(NH):
            peak, total, acc = state[h]
            out_ref[h * HD : (h + 1) * HD, columns] = (acc / total).astype(jnp.bfloat16)
            stat_ref[h : h + 1, columns] = peak + jnp.log(total)
        return carry

    count = (ends[-1] + BQ - 1) // BQ
    lax.fori_loop(0, count, query_block, 0)

    def padded_block(block, carry):
        columns = pl.ds(pl.multiple_of(block * BQ, BQ), BQ)
        out_ref[:, columns] = jnp.zeros((out_ref.shape[0], BQ), jnp.bfloat16)
        return carry

    lax.fori_loop(count, tokens // BQ, padded_block, 0)


def attend(lengths, mixed):
    tokens = mixed.shape[0]
    vm = pl.BlockSpec(memory_space=pltpu.VMEM)
    return pl.pallas_call(
        attend_kernel,
        out_shape=(
            jax.ShapeDtypeStruct((NH * HD, tokens), jnp.bfloat16),
            jax.ShapeDtypeStruct((8, tokens), jnp.float32),
        ),
        in_specs=[pl.BlockSpec(memory_space=pltpu.SMEM), pl.BlockSpec(memory_space=pltpu.HBM)],
        out_specs=(vm, vm),
        scratch_shapes=[pltpu.VMEM(mixed.shape, mixed.dtype)]
        + [pltpu.VMEM((WIDE, tokens), jnp.bfloat16)] * 2
        + [pltpu.SemaphoreType.DMA((tokens // BQ,))],
        compiler_params=pltpu.CompilerParams(vmem_limit_bytes=40 << 20),
        cost_estimate=pl.CostEstimate(
            flops=8 * tokens * tokens * NH * HD,
            bytes_accessed=16 * tokens * WIDE,
            transcendentals=tokens * tokens,
        ),
        name="attend",
    )(lengths, mixed)


def attend_back_kernel(
    lengths_ref, mixed_ref, out_ref, stat_ref, gradt_ref,
    gmixed_ref, qt_ref, kt_ref, grad_ref, delta_ref, dqt_ref
):
    tokens = mixed_ref.shape[0]
    ends = ends_of(lengths_ref)
    for first in range(0, tokens, BQ):
        rows = pl.ds(first, BQ)
        for slab in range(SLABS):
            lanes = slab * 128
            qt_ref[lanes : lanes + 128, rows] = (
                mixed_ref[rows, lanes : lanes + 128] * HD ** (-0.5)
            ).T
            kt_ref[lanes : lanes + 128, rows] = mixed_ref[rows, WIDE + lanes : WIDE + lanes + 128].T
        grad_ref[rows, 0:128] = gradt_ref[0:128, rows].T
        grad_ref[rows, 128:256] = jnp.concatenate(
            [gradt_ref[128:192, rows], jnp.zeros((64, BQ), jnp.bfloat16)], axis=0
        ).T
        for h in range(NH):
            product = gradt_ref[h * HD : (h + 1) * HD, rows].astype(jnp.float32) * out_ref[
                h * HD : (h + 1) * HD, rows
            ].astype(jnp.float32)
            delta_ref[h : h + 1, rows] = jnp.sum(product, axis=0, keepdims=True)
    dqt_ref[...] = jnp.zeros_like(dqt_ref)
    lane = lax.broadcasted_iota(jnp.int32, (BQ, 128), 1)

    def key_block(key, carry):
        base = pl.multiple_of(key * BK, BK)
        rows = pl.ds(base, BK)
        key_ids = base + lax.broadcasted_iota(jnp.int32, (BK, BQ), 0)

        def query_block(block, state):
            first = pl.multiple_of(block * BQ, BQ)
            columns = pl.ds(first, BQ)
            start = segment_start(ends, first + lax.broadcasted_iota(jnp.int32, (1, BQ), 1))
            query_ids = first + lax.broadcasted_iota(jnp.int32, (BK, BQ), 1)
            allowed = (key_ids <= query_ids) & (key_ids >= start)
            grad_keys = list(state[:SLABS])
            grad_values = list(state[SLABS:])
            for h in range(NH):
                slab = h // 2
                low, high = slab * 128, slab * 128 + 128
                queries = head_rows(qt_ref[low:high, columns], h)
                scores = nn(mixed_ref[rows, WIDE + low : WIDE + high], queries)
                probs = jnp.where(allowed, jnp.exp(scores - stat_ref[h : h + 1, columns]), 0.0)
                keep = (lane // HD) == (h % 2)
                grads = jnp.where(keep, grad_ref[columns, low:high], 0.0)
                grad_values[slab] += nn(probs.astype(jnp.bfloat16), grads)
                if h == NH - 1 and NH % 2 == 1:
                    grad_rows = jnp.concatenate(
                        [gradt_ref[h * HD : (h + 1) * HD, columns], jnp.zeros((HD, BQ), jnp.bfloat16)],
                        axis=0,
                    )
                else:
                    grad_rows = head_rows(gradt_ref[low:high, columns], h)
                grad_probs = nn(mixed_ref[rows, 2 * WIDE + low : 2 * WIDE + high], grad_rows)
                grad_scores = (probs * (grad_probs - delta_ref[h : h + 1, columns])).astype(
                    jnp.bfloat16
                )
                natural = mixed_ref[columns, low:high]
                grad_keys[slab] += nn(grad_scores, jnp.where(keep, natural, 0.0))
                dqt_ref[h * HD : (h + 1) * HD, columns] += nn(
                    kt_ref[h * HD : (h + 1) * HD, rows], grad_scores
                )
            return tuple(grad_keys) + tuple(grad_values)

        empty = (jnp.zeros((BK, 128), jnp.float32),) * (2 * SLABS)
        stop = jnp.minimum(segment_stop(ends, base + BK - 1, tokens), ends[-1])
        state = lax.fori_loop(key * BK // BQ, (stop - 1) // BQ + 1, query_block, empty)
        for slab in range(SLABS):
            low = slab * 128
            gmixed_ref[rows, WIDE + low : WIDE + low + 128] = (
                state[slab] * HD ** (-0.5)
            ).astype(jnp.bfloat16)
            gmixed_ref[rows, 2 * WIDE + low : 2 * WIDE + low + 128] = state[SLABS + slab].astype(
                jnp.bfloat16
            )
        return carry

    count = (ends[-1] + BK - 1) // BK
    lax.fori_loop(0, count, key_block, 0)

    def padded_block(key, carry):
        rows = pl.ds(pl.multiple_of(key * BK, BK), BK)
        gmixed_ref[rows, WIDE:] = jnp.zeros((BK, 2 * WIDE), jnp.bfloat16)
        return carry

    lax.fori_loop(count, tokens // BK, padded_block, 0)
    for first in range(0, tokens, BQ):
        rows = pl.ds(first, BQ)
        for slab in range(SLABS):
            low = slab * 128
            gmixed_ref[rows, low : low + 128] = (
                (dqt_ref[low : low + 128, rows] * HD ** (-0.5)).T.astype(jnp.bfloat16)
            )


def attend_back(lengths, mixed, out, stat, gradt):
    tokens = mixed.shape[0]
    vm = pl.BlockSpec(memory_space=pltpu.VMEM)
    return pl.pallas_call(
        attend_back_kernel,
        out_shape=jax.ShapeDtypeStruct((tokens, 3 * WIDE), jnp.bfloat16),
        in_specs=[pl.BlockSpec(memory_space=pltpu.SMEM)] + [vm] * 4,
        out_specs=vm,
        scratch_shapes=[
            pltpu.VMEM((WIDE, tokens), jnp.bfloat16),
            pltpu.VMEM((WIDE, tokens), jnp.bfloat16),
            pltpu.VMEM((tokens, WIDE), jnp.bfloat16),
            pltpu.VMEM((8, tokens), jnp.float32),
            pltpu.VMEM((WIDE, tokens), jnp.float32),
        ],
        compiler_params=pltpu.CompilerParams(vmem_limit_bytes=50 << 20),
        cost_estimate=pl.CostEstimate(
            flops=20 * tokens * tokens * NH * HD,
            bytes_accessed=32 * tokens * WIDE,
            transcendentals=tokens * tokens,
        ),
        name="attend_back",
    )(lengths, mixed, out, stat, gradt)


class Copies:
    def __init__(self, send, recv):
        self.send, self.recv, self.made, self.started = send, recv, 0, []

    def plan(self, source, target, device):
        index = self.made
        self.made += 1
        return pltpu.make_async_remote_copy(
            src_ref=source,
            dst_ref=target,
            send_sem=self.send.at[index],
            recv_sem=self.recv.at[index],
            device_id=device,
            device_id_type=MESH,
        )

    def begin(self, copy, condition=None):
        self.started.append((copy, condition))
        when(condition, copy.start)

    def start(self, source, target, device):
        copy = self.plan(source, target, device)
        self.begin(copy)
        return copy

    def finish(self):
        for copy, condition in self.started:
            when(condition, copy.wait_send)


def when(condition, action):
    if condition is None:
        action()
    else:
        pl.when(condition)(action)


def greet(devices):
    barrier = pltpu.get_barrier_semaphore()
    for device, condition in devices:
        when(
            condition,
            lambda device=device: pl.semaphore_signal(
                barrier, inc=1, device_id=device, device_id_type=MESH
            ),
        )
    present = [1 if condition is None else condition.astype(jnp.int32) for _, condition in devices]
    pl.semaphore_wait(barrier, sum(present))


class Place:
    def __init__(self, line):
        self.dp = dp = lax.axis_index("dp")
        self.tensor = tensor = lax.axis_index("tensor")
        self.spot, self.side = spot, side = dp // 2, dp % 2
        self.chip, self.core = tensor // 2, tensor % 2
        self.has_up, self.has_down = spot + 1 < line, spot > 0
        self.up = (jnp.minimum(spot + 1, line - 1) * 2 + side, tensor)
        self.down = (jnp.maximum(spot - 1, 0) * 2 + side, tensor)
        self.across = (spot * 2 + 1 - side, tensor)
        self.mate = (dp, tensor + 1 - 2 * (tensor % 2))
        self.far = (dp, (tensor + 2) % 4)
        self.corner = (dp, 3 - tensor)

    def everyone(self):
        return [
            (self.mate, None), (self.far, None), (self.corner, None), (self.across, None),
            (self.up, self.has_up), (self.down, self.has_down),
        ]


def comm_call(kernel, name, outputs, inputs, in_specs, out_specs, copies, cid, scratch=(), local=1, limit=50 << 20):
    return pl.pallas_call(
        kernel,
        out_shape=outputs,
        in_specs=in_specs,
        out_specs=out_specs,
        scratch_shapes=list(scratch)
        + [
            pltpu.SemaphoreType.DMA((copies,)),
            pltpu.SemaphoreType.DMA((copies,)),
            pltpu.SemaphoreType.DMA((local,)),
        ],
        compiler_params=pltpu.CompilerParams(
            collective_id=cid, has_side_effects=True, vmem_limit_bytes=limit
        ),
        name=name,
    )(*inputs)


def one_hot(rows, columns, shift, limit):
    lane = lax.broadcasted_iota(jnp.int32, (rows, columns), 0)
    spot = lax.broadcasted_iota(jnp.int32, (rows, columns), 1)
    return ((spot == lane + shift) & (lane < limit)).astype(LOW)


def gather_inputs(tokens, thoughts, positions, cotangent, fc, proj, qkv, out, vectors, n_dp):
    line = n_dp // 2
    hops = line - 1
    rows, width = tokens.shape
    latents = thoughts.shape[0]
    window = rows // latents
    shard = fc.shape[0]
    half_rows = rows // 2
    share = width // (n_dp * 4)

    def kernel(
        pos_ref, tokens_in, thoughts_in, cot_ref, fc_in, proj_in, qkv_in, out_in, *refs
    ):
        given = (fc_in, tokens_in, thoughts_in, proj_in, qkv_in, out_in) + refs[: len(vectors)]
        (
            normed_out, mixed_out, mix_out, fc_near, fc_side, fc_far, proj_near, cot_out, out_out,
            hidden_out, vec_out, pos_out,
            hidden_ref, mix_ref, vec_ref, tile,
            land, mix_land, tiles, tile_land, normed, mixed, out_turned,
            *held, arrive, send, recv, local,
        ) = refs[len(vectors) :]
        arrivals = [
            pltpu.make_async_copy(given[i], held[i], arrive.at[i]) for i in range(len(given))
        ]
        for copy in arrivals:
            copy.start()
        fc_ref, tokens_ref, thoughts_ref, proj_ref, qkv_ref, out_ref = held[:6]
        vec_refs = held[6:]
        at = Place(line)
        dp, tensor, spot, side = at.dp, at.tensor, at.spot, at.side
        mate_row, far_row, corner_row = at.mate[1], at.far[1], at.corner[1]
        greet(at.everyone())
        copies = Copies(send, recv)
        MIX, FC, PROJ, VEC = range(4)
        own = [mix_ref, fc_ref, proj_ref, tiles.at[dp]]

        def seat(item, position):
            if item == MIX:
                return mix_land.at[position * 2 + side]
            if item == FC:
                return fc_near.at[position]
            if item == PROJ:
                return proj_near.at[position]
            return tiles.at[position * 2 + side]

        def plan(item, hop):
            above, below = jnp.maximum(spot - hop, 0), jnp.minimum(spot + hop, line - 1)
            came_up = jnp.maximum(spot - 1 - hop, 0)
            came_down = jnp.minimum(spot + 1 + hop, line - 1)
            made = {
                "up": copies.plan(
                    own[item] if hop == 0 else seat(item, above), seat(item, above), at.up
                ),
                "down": copies.plan(
                    own[item] if hop == 0 else seat(item, below), seat(item, below), at.down
                ),
                "onward": [],
            }
            for position in (came_up, came_down):
                onward = []
                if item in (MIX, VEC):
                    onward.append(copies.plan(seat(item, position), seat(item, position), at.across))
                if item == FC:
                    onward.append(copies.plan(fc_near.at[position], fc_side.at[position], at.across))
                    onward.append(copies.plan(fc_near.at[position], fc_far.at[position], at.far))
                made["onward"].append(onward)
            return made

        plans = [[plan(item, hop) for hop in range(hops)] for item in range(4)]

        def launch(item):
            copies.begin(plans[item][0]["up"], at.has_up)
            copies.begin(plans[item][0]["down"], at.has_down)

        def handle(item, hop):
            made = plans[item][hop]
            for way, key, comes, goes in (
                (0, "up", spot - 1 - hop >= 0, at.has_up),
                (1, "down", spot + 1 + hop < line, at.has_down),
            ):
                when(comes, made[key].wait_recv)
                if hop + 1 < hops:
                    copies.begin(plans[item][hop + 1][key], comes & goes)
                for copy in made["onward"][way]:
                    copies.begin(copy, comes)

        def settle(item):
            for hop in range(hops):
                for way, comes in ((0, spot - 1 - hop >= 0), (1, spot + 1 + hop < line)):
                    for copy in plans[item][hop]["onward"][way]:
                        when(comes, copy.wait_recv)

        stays = []

        def stay(source, target):
            copy = pltpu.make_async_copy(source, target, local.at[len(stays)])
            copy.start()
            stays.append(copy)
            return copy

        parts = [pl.ds(0, half_rows), pl.ds(half_rows, half_rows)]
        arrivals[0].wait()
        launch(FC)
        fc_sides = [copies.start(fc_ref, fc_side.at[spot], at.across)]
        cot_made = copies.start(cot_ref, cot_out, at.mate)
        for copy in arrivals[6:]:
            copy.wait()
        tile[...] = jnp.zeros_like(tile)
        row = 0
        for ref in vec_refs:
            count, size = ref.shape
            tile[row : row + count, 0:size] = ref[...].astype(F32)
            row += count
        vec_ref[...] = tile[...].astype(LOW)
        vec_made = [
            copies.start(vec_ref, tile_land.at[i], device)
            for i, device in enumerate((at.mate, at.far, at.corner))
        ]
        arrivals[1].wait()
        arrivals[2].wait()
        pos_row = lax.broadcasted_iota(jnp.int32, (latents, 128), 0)
        places = jnp.zeros((latents, 128), jnp.int32)
        for w in range(latents):
            places = jnp.where(pos_row == w, pos_ref[w], places)
            span = pl.ds(w * window, window)
            here = lax.broadcasted_iota(jnp.int32, (window, 1), 0) == pos_ref[w] - w * window
            hidden_ref[span] = jnp.where(
                here, thoughts_ref[w : w + 1].astype(F32), tokens_ref[span].astype(F32)
            ).astype(LOW)
        pos_out[...] = places
        far_made = [
            copies.start(hidden_ref.at[part], land.at[2, part], at.far) for part in parts
        ]
        mate_made = copies.start(hidden_ref, land.at[1], at.mate)
        fc_sides.append(copies.start(fc_ref, fc_far.at[spot], at.far))
        for copy in arrivals[3:6]:
            copy.wait()
        turned = qkv_ref[...].astype(F32).T
        extra = out_ref[...].astype(F32)
        pieces = []
        for p in range(3):
            for h in range(NH):
                low = (h * 3 + p) * HD
                pieces.append(turned[low : low + HD])
            pieces.append(extra[p * HD : (p + 1) * HD])
        mix_ref[...] = jnp.concatenate(pieces, axis=0).T.astype(LOW)
        launch(MIX)
        mix_side = copies.start(mix_ref, mix_land.at[dp], at.across)
        stay(hidden_ref, hidden_out)
        stay(fc_ref, fc_near.at[spot])
        stay(proj_ref, proj_near.at[spot])
        mix_land[dp] = mix_ref[...]
        for copy in vec_made:
            copy.wait_recv()
        merged = jnp.zeros((VEC_ROWS, 128), F32)
        bias_rows = jnp.zeros((VEC_ROWS, 128), F32)
        row_ids = lax.broadcasted_iota(jnp.int32, (VEC_ROWS, 128), 0)
        for i, index in enumerate((tensor, mate_row, far_row, corner_row)):
            tile = vec_ref[...] if i == 0 else tile_land[i - 1]
            merged += nn(tile, one_hot(128, 128, index * share, share))
            bias_rows = jnp.where(row_ids == 8 + index, tile[8:9].astype(F32), bias_rows)
        tiles[dp] = jnp.where(row_ids < 8, merged, bias_rows).astype(LOW)
        launch(VEC)
        vec_side = copies.start(tiles.at[dp], tiles.at[dp], at.across)

        def norm_rows(source, index):
            @pl.loop(0, rows // 128)
            def _(i):
                span = pl.ds(pl.multiple_of(i * 128, 128), 128)
                normed[index, span] = normalize(source[span].astype(F32))[0].astype(LOW)

            stay(normed.at[index], normed_out.at[index])

        def relay(i):
            far_made[i].wait_recv()
            return copies.start(land.at[2, parts[i]], land.at[3, parts[i]], at.mate)

        def mix_rows(index):
            @pl.loop(0, rows // 256)
            def _(i):
                span = pl.ds(pl.multiple_of(i * 256, 256), 256)
                turned = normed[index, span].astype(F32) * whole[0:1] + whole[1:2]
                weight = mix_land[...].reshape(width, width)
                mixed[index, span] = (nn(turned.astype(LOW), weight) + bias).astype(LOW)

            stay(mixed.at[index], mixed_out.at[index])

        norm_rows(hidden_ref, tensor)
        relayed = []
        for step in range(hops + 2):
            for item, hop in ((MIX, step), (VEC, step), (FC, step - 1), (PROJ, step - 2)):
                if 0 <= hop < hops:
                    handle(item, hop)
            if step == 0:
                launch(PROJ)
                mate_made.wait_recv()
                norm_rows(land.at[1], mate_row)
                relayed.append(relay(0))
            if step == 1:
                relayed.append(relay(1))
                norm_rows(land.at[2], far_row)
            if step == hops:
                mix_side.wait_recv()
                vec_side.wait_recv()
                settle(MIX)
                settle(VEC)
                whole = jnp.zeros((VEC_ROWS, width), F32)
                for i in range(n_dp):
                    whole += nn(tiles[i], one_hot(128, width, i * shard, shard))
                vec_out[...] = whole
                for i, block in enumerate((tensor, far_row)):
                    vec_out[12 + i : 13 + i] = units_row(whole[8:12], block, n_dp)
                lane = lax.broadcasted_iota(jnp.int32, (width, WIDE), 0)
                column = lax.broadcasted_iota(jnp.int32, (width, WIDE), 1)
                pick = (lane == column + tensor * (NH * HD)) & (column < NH * HD)
                picked = nn(whole.astype(LOW), pick.astype(LOW))
                bias = jnp.concatenate(
                    [picked[2:3], jnp.zeros((1, WIDE), F32), picked[3:4]], axis=1
                )
                mix_rows(tensor)
                mix_rows(mate_row)
        mix_rows(far_row)
        for copy in relayed:
            copy.wait_recv()
        norm_rows(land.at[3], corner_row)
        mix_rows(corner_row)
        stay(mix_land, mix_out)
        weight = mix_land[...].reshape(width, width)
        for part in range(3):
            low = part * WIDE + WIDE - 128
            turned = weight[:, low : low + 128].T
            out_turned[part * HD : (part + 1) * HD] = turned[128 - HD :]
        stay(out_turned, out_out)
        settle(FC)
        for copy in fc_sides:
            copy.wait_recv()
        cot_made.wait_recv()
        copies.finish()
        for copy in stays:
            copy.wait()

    low = lambda *shape: jax.ShapeDtypeStruct(shape, LOW)
    outputs = (
        low(4, rows, width), low(4, rows, width), low(n_dp, shard, width),
        low(line, shard, width), low(line, shard, width), low(line, shard, width),
        low(line, shard, width), low(rows, width), low(NH * HD, width), low(rows, width),
        jax.ShapeDtypeStruct((VEC_ROWS, width), F32),
        jax.ShapeDtypeStruct((latents, 128), jnp.int32),
    )
    scratch = [
        pltpu.VMEM((rows, width), LOW),
        pltpu.VMEM((shard, 3 * WIDE), LOW),
        pltpu.VMEM((VEC_ROWS, 128), LOW),
        pltpu.VMEM((VEC_ROWS, 128), F32),
        pltpu.VMEM((4, rows, width), LOW),
        pltpu.VMEM((n_dp, shard, width), LOW),
        pltpu.VMEM((n_dp, VEC_ROWS, 128), LOW),
        pltpu.VMEM((3, VEC_ROWS, 128), LOW),
        pltpu.VMEM((4, rows, width), LOW),
        pltpu.VMEM((4, rows, width), LOW),
        pltpu.VMEM((NH * HD, width), LOW),
    ]
    given = (fc, tokens, thoughts, proj, qkv, out, *vectors)
    scratch += [pltpu.VMEM(x.shape, x.dtype) for x in given]
    scratch.append(pltpu.SemaphoreType.DMA((len(given),)))
    return comm_call(
        kernel,
        "gather_inputs",
        outputs,
        (positions, tokens, thoughts, cotangent, fc, proj, qkv, out, *vectors),
        [SM] + [ANY] * (7 + len(vectors)),
        (ANY,) * 10 + (VM, VM),
        3 + 2 + 1 + 2 + 2 + 1 + 2 + hops * (2 * 4 + 2 * 4),
        0,
        scratch=scratch,
        local=3 + 8 + 2,
    )


def after_attention(attended, out_own, out_far, hidden, vec_all, n_dp, cid):
    head_width, slots = attended.shape
    rows, width = hidden.shape
    half_rows = rows // 2

    def kernel(
        heads_ref, own_ref, far_ref, hidden_ref, vec_ref,
        both_out, middle_out, two_out,
        land, part, part_low, part_land, two, send, recv, local,
    ):
        at = Place(n_dp // 2)
        greet([(at.far, None), (at.mate, None)])
        copies = Copies(send, recv)
        cores = (at.core, 1 - at.core)
        made = [None, None]
        for i in (1, 0):
            theirs = pl.multiple_of(((1 - at.chip) * 2 + cores[i]) * rows, rows)
            made[i] = copies.start(heads_ref.at[:, pl.ds(theirs, rows)], land.at[i], at.far)
        stays = []

        def stay(source, target):
            stays.append(pltpu.make_async_copy(source, target, local.at[len(stays)]))
            stays[-1].start()

        spans = []
        for i in range(2):
            ours = pl.multiple_of((at.chip * 2 + cores[i]) * rows, rows)
            spans.append(pl.ds(ours, rows))
            stay(heads_ref.at[:, spans[i]], both_out.at[0, :, i * rows : (i + 1) * rows])
            part[i] = tn(heads_ref[:, spans[i]], own_ref[...])
        sums = None
        for i in (1, 0):
            made[i].wait_recv()
            stay(land.at[i], both_out.at[1, :, i * rows : (i + 1) * rows])
            part[i] += tn(land[i], far_ref[...])
            if i == 1:
                part_low[...] = part[1].astype(LOW)
                sums = copies.start(part_low, part_land, at.mate)
        sums.wait_recv()
        mated = []
        for piece in range(2):

            @pl.loop(0, half_rows // 128)
            def _(i):
                span = pl.ds(pl.multiple_of(piece * half_rows + i * 128, 128), 128)
                middle = (
                    hidden_ref[span].astype(F32)
                    + part[0, span]
                    + part_land[span].astype(F32)
                    + vec_ref[4:5]
                )
                middle_out[span] = middle
                two[span] = (normalize(middle)[0] * vec_ref[5:6] + vec_ref[6:7]).astype(LOW)

            span = pl.ds(piece * half_rows, half_rows)
            mated.append(copies.start(two.at[span], two_out.at[1, span], at.mate))
        stay(two, two_out.at[0])
        for copy in mated:
            copy.wait_recv()
        copies.finish()
        for copy in stays:
            copy.wait()

    return comm_call(
        kernel,
        "after_attention",
        (
            jax.ShapeDtypeStruct((2, head_width, 2 * rows), LOW),
            jax.ShapeDtypeStruct((rows, width), F32),
            jax.ShapeDtypeStruct((2, rows, width), LOW),
        ),
        (attended, out_own, out_far, hidden, vec_all),
        [VM] * 5,
        (ANY, VM, ANY),
        5,
        cid,
        scratch=[
            pltpu.VMEM((2, head_width, rows), LOW),
            pltpu.VMEM((2, rows, width), F32),
            pltpu.VMEM((rows, width), LOW),
            pltpu.VMEM((rows, width), LOW),
            pltpu.VMEM((rows, width), LOW),
        ],
        local=5,
    )


def before_attention_back(lengths, two, middle, cotangent, both, out_own, out_far, vec_all, n_dp, cid):
    _, rows, width = two.shape
    head_width = out_own.shape[0]
    half_rows = rows // 2

    def kernel(
        lengths_ref, two_ref, middle_ref, cot_ref, both_ref, own_ref, far_ref, vec_ref,
        heads_out, grad_out, own_out, far_out, vec_out,
        two_land, mid, stay_heads, sent_heads, send, recv, local,
    ):
        at = Place(n_dp // 2)
        greet([(at.far, None), (at.mate, None)])
        copies = Copies(send, recv)
        halves = [pl.ds(0, half_rows), pl.ds(half_rows, half_rows)]
        sums = [copies.start(two_ref.at[1, span], two_land.at[span], at.mate) for span in halves]
        vec_out[...] = jnp.zeros_like(vec_out)
        first_row = at.tensor * rows
        live = ends_of(lengths_ref)[-1]
        mated = []
        for piece in range(2):
            sums[piece].wait_recv()

            @pl.loop(0, half_rows // 128)
            def _(i):
                start = pl.multiple_of(piece * half_rows + i * 128, 128)
                span = pl.ds(start, 128)
                grad = two_ref[0, span].astype(F32) + two_land[span].astype(F32)
                normed, inverse = normalize(middle_ref[span])
                ids = first_row + start + lax.broadcasted_iota(jnp.int32, (128, 1), 0)
                final = jnp.where(ids < live, cot_ref[span].astype(F32), 0.0)
                total = final + norm_back(normed, inverse, grad, vec_ref[5:6])
                grad_out[span] = total
                mid[0, span] = total.astype(LOW)
                for row, term in ((4, total), (5, normed * grad), (6, grad), (7, final)):
                    vec_out[row : row + 1] += jnp.sum(term, axis=0, keepdims=True)

            mated.append(copies.start(mid.at[0, halves[piece]], mid.at[1, halves[piece]], at.mate))
        cores = (at.core, 1 - at.core)
        made, stays = [], []
        for i in range(2):
            if i == 1:
                for copy in mated:
                    copy.wait_recv()
            ours = pl.ds(pl.multiple_of((at.chip * 2 + cores[i]) * rows, rows), rows)
            sent_heads[i] = nt(far_ref[...], mid[i]).astype(LOW)
            made.append(copies.start(sent_heads.at[i], heads_out.at[:, ours], at.far))
            stay_heads[i] = nt(own_ref[...], mid[i]).astype(LOW)
            stays.append(
                pltpu.make_async_copy(stay_heads.at[i], heads_out.at[:, ours], local.at[i])
            )
            stays[-1].start()
        grads = mid[...].reshape(2 * rows, width)
        own_out[...] = nn(both_ref[0], grads).astype(LOW)
        far_out[...] = nn(both_ref[1], grads).astype(LOW)
        for copy in made:
            copy.wait_recv()
        copies.finish()
        for copy in stays:
            copy.wait()

    return comm_call(
        kernel,
        "before_attention_back",
        (
            jax.ShapeDtypeStruct((head_width, 4 * rows), LOW),
            jax.ShapeDtypeStruct((rows, width), F32),
            jax.ShapeDtypeStruct((head_width, width), LOW),
            jax.ShapeDtypeStruct((head_width, width), LOW),
            jax.ShapeDtypeStruct((VEC_ROWS, width), F32),
        ),
        (lengths, two, middle, cotangent, both, out_own, out_far, vec_all),
        [pl.BlockSpec(memory_space=pltpu.SMEM)] + [VM] * 7,
        (ANY,) + (VM,) * 4,
        6,
        cid,
        scratch=[
            pltpu.VMEM((rows, width), LOW),
            pltpu.VMEM((2, rows, width), LOW),
            pltpu.VMEM((2, head_width, rows), LOW),
            pltpu.VMEM((2, head_width, rows), LOW),
        ],
        local=2,
    )


def finish_grads(lengths, arrays, n_dp, cid):
    part_rows = arrays["hidden"].shape[0] // 4
    names = list(arrays)
    kept = [name for name in names if name != "out_far"]
    line = n_dp // 2
    shard = arrays["mix"].shape[1]
    rows, width = arrays["hidden"].shape
    group = 4 * rows
    latents = arrays["positions"].shape[0]
    window = rows // latents
    far_end = line - 1
    slots = [(distance, way) for distance in range(far_end, 0, -1) for way in (0, 1)] + [(0, 0)]
    last = len(slots) - 1
    share = width // (n_dp * 4)
    FC, PROJ, MIX, VEC = range(4)

    def kernel(lengths_ref, *refs):
        refs = list(refs)

        def take(number):
            taken = refs[:number]
            del refs[:number]
            return taken

        source = dict(zip(names, take(len(names))))
        fc_out, proj_out, mix_out, vec_out, tokens_out, thoughts_out, block_out = take(7)
        held = dict(zip(kept, take(len(kept))))
        cross_send, cross_land = [None, None] + take(2), [None, None] + take(2)
        hop_send, hop_land = take(4), take(4)
        (
            part, mate_land, far_send, far_land, last_land, total, vec_mine, vec_land, vec_near,
            plain_sum, column_sum, out_land, tokens_kept, thoughts_kept, block_kept, send, recv,
            local,
        ) = refs
        out = [fc_out, proj_out, mix_out, None]
        at = Place(line)
        tensor, spot, side = at.tensor, at.spot, at.side
        mate_row, far_row, corner_row = at.mate[1], at.far[1], at.corner[1]
        copies = Copies(send, recv)
        loads = {}
        held["out_far"] = out_land
        for i, name in enumerate(kept):
            loads[name] = pltpu.make_async_copy(source[name], held[name], local.at[i])

        def load(*group):
            for name in group:
                loads[name].start()

        load("fc_near", "fc_near_side", "fc_cross", "proj_near", "proj_near_far", "proj_cross")
        load("grad_mixed", "mix")
        greet(at.everyone())

        def block_of(slot):
            distance, way = slots[slot]
            if way == 0:
                return jnp.minimum(spot + distance, far_end), spot + distance < line
            return jnp.maximum(spot - distance, 0), spot - distance >= 0

        crosses, hops = [], []
        for slot in range(len(slots)):
            block, _ = block_of(slot)
            crosses.append(
                {
                    i: copies.plan(cross_send[i].at[block], cross_land[i].at[block], at.across)
                    for i in (MIX, VEC)
                }
            )
            if slot < last:
                hops.append(
                    [
                        copies.plan(
                            hop_send[i].at[slot],
                            hop_land[i].at[slot],
                            (at.up, at.down)[slots[slot][1]],
                        )
                        for i in range(4)
                    ]
                )

        def cross(distance, items):
            for slot in range(len(slots)):
                if slots[slot][0] == distance:
                    for i in items:
                        copies.begin(crosses[slot][i], block_of(slot)[1])

        terms = (
            ("fc_near", "fc_near_side", "fc_cross"),
            ("proj_near", "proj_near_far", "proj_cross"),
        )

        def own_term(i, block):
            if i in (FC, PROJ):
                return sum(held[name][block].astype(F32) for name in terms[i])
            if i == MIX:
                return total[block * 2 + side].astype(F32)
            return vec_near[block * 2 + side]

        def handle(slot, i):
            block, inside = block_of(slot)
            behind = (at.has_down, at.has_up)[slots[slot][1]]
            outer = slot - 2

            def work():
                value = own_term(i, block)
                if i in (MIX, VEC):
                    crosses[slot][i].wait_recv()
                    value = value + cross_land[i][block].astype(F32)
                if outer < 0:
                    hop_send[i][slot] = value.astype(hop_send[i].dtype)
                    return

                @pl.when(behind)
                def _():
                    hops[outer][i].wait_recv()
                    hop_send[i][slot] = (value + hop_land[i][outer].astype(F32)).astype(
                        hop_send[i].dtype
                    )

                @pl.when(jnp.logical_not(behind))
                def _():
                    hop_send[i][slot] = value.astype(hop_send[i].dtype)

            when(inside, work)
            copies.begin(hops[slot][i], inside)

        def handle_all(distance, items):
            for slot in range(last):
                if slots[slot][0] == distance:
                    for i in items:
                        handle(slot, i)

        def close(i, target):
            value = own_term(i, spot)
            if i in (MIX, VEC):
                crosses[last][i].wait_recv()
                value = value + cross_land[i][spot].astype(F32)
            target[...] = value
            for way, behind in enumerate((at.has_down, at.has_up)):

                def add(way=way):
                    hops[last - 2 + way][i].wait_recv()
                    target[...] += hop_land[i][last - 2 + way].astype(F32)

                when(behind, add)

        for name in ("fc_near", "fc_near_side", "fc_cross", "proj_near", "proj_near_far", "proj_cross"):
            loads[name].wait()
        out_made = copies.start(source["out_far"], out_land, at.far)
        handle_all(far_end, (FC, PROJ))
        load("group", "out_own", "vec_all", "vec_part", "bias_own", "bias_far")
        load("last", "hidden", "grad_middle", "middle", "positions")
        loads["grad_mixed"].wait()
        loads["mix"].wait()

        def row_part(index):
            @pl.loop(0, rows // 256)
            def _(i):
                span = pl.ds(pl.multiple_of(i * 256, 256), 256)
                weight = held["mix"][...].reshape(width, width)
                part[index, span] = nt(held["grad_mixed"][index, span], weight).astype(LOW)

        row_part(corner_row)
        mate_far = copies.start(part.at[corner_row], mate_land.at[1], at.mate)
        row_part(mate_row)
        mate_own = copies.start(part.at[mate_row], mate_land.at[0], at.mate)
        row_part(far_row)
        mate_far.wait_recv()
        far_made = []

        def send_far(count):
            for i in range(len(far_made), min(len(far_made) + count, 8)):
                span = pl.ds(i * (part_rows // 2), part_rows // 2)
                far_send[span] = (
                    mate_land[1, span].astype(F32) + part[far_row, span].astype(F32)
                ).astype(LOW)
                far_made.append(copies.start(far_send.at[span], far_land.at[span], at.far))

        send_far(2)
        row_part(tensor)
        send_far(1)
        if far_end > 1:
            handle_all(far_end - 1, (FC, PROJ))
        loads["last"].wait()
        last_copy = copies.start(held["last"].at[1], last_land, at.mate)
        for name in ("group", "out_own", "vec_all", "vec_part", "bias_own", "bias_far"):
            loads[name].wait()
        out_made.wait_recv()

        plain_sum[...] = jnp.zeros_like(plain_sum)
        column_sum[...] = jnp.zeros_like(column_sum)

        @pl.loop(0, group // 256)
        def _(i):
            block, start = i // (rows // 256), (i % (rows // 256)) * 256
            span = pl.ds(pl.multiple_of(start, 256), 256)
            grad = held["grad_mixed"][block, span]
            plain_sum[...] += tn(held["group"][block, span], grad)
            column_sum[...] += jnp.sum(grad.astype(F32), axis=0, keepdims=True)

        send_far(2)
        plain, columns = plain_sum[...], column_sum[...]
        turned = held["vec_all"][...].T
        weight = held["mix"][...].reshape(width, width).astype(F32)
        gain_grad = jnp.sum(plain * weight, axis=1, keepdims=True)
        shift_grad = jnp.sum(weight * columns, axis=1, keepdims=True)
        scaled = plain * turned[:, 0:1] + turned[:, 1:2] * columns
        extras = []
        out_sum = held["out_own"][...].astype(F32) + held["out_far"][...].astype(F32)
        for p in range(3):
            piece = out_sum[p * HD : (p + 1) * HD]
            extras.append(jnp.zeros((width, WIDE - 128), F32))
            extras.append(jnp.concatenate([jnp.zeros((128 - HD, width), F32), piece], axis=0).T)
        scaled = scaled + jnp.concatenate(extras, axis=1)
        for k in range(n_dp):
            total[k] = scaled[k * shard : (k + 1) * shard].astype(LOW)
        for block in range(line):
            cross_send[MIX][block] = total[block * 2 + 1 - side]
        cross(far_end, [MIX])
        cross(far_end - 1, [MIX])
        vec_mine[...] = held["vec_part"][...]
        flat = jnp.concatenate(
            [gain_grad, shift_grad, jnp.zeros((width, 6), F32)], axis=1
        ).T
        vec_mine[0:2] = flat[0:2]
        vec_mine[8:12] = units_rows_back(held["bias_own"][...], tensor, n_dp) + units_rows_back(
            held["bias_far"][...], far_row, n_dp
        )
        vec_lane = lax.broadcasted_iota(jnp.int32, (1, width), 1)
        in_part = (vec_lane >= tensor * (NH * HD)) & (vec_lane < (tensor + 1) * (NH * HD))
        for row, low in ((2, 0), (3, 2 * WIDE)):
            line_up = jnp.concatenate([columns[:, low : low + WIDE]] + [columns[:, 0:WIDE]] * 2, axis=1)
            placed = jnp.zeros((1, width), F32)
            for t in range(4):
                shifted = pltpu.roll(line_up, t * NH * HD, 1)
                placed = jnp.where(tensor == t, shifted, placed)
            vec_mine[row : row + 1] = jnp.where(in_part, placed, 0.0)
        vec_made = [
            copies.start(vec_mine, vec_land.at[i], device)
            for i, device in enumerate((at.mate, at.far, at.corner))
        ]
        for distance in range(far_end - 2, 0, -1):
            handle_all(distance, (FC, PROJ))
        send_far(1)
        for copy in vec_made:
            copy.wait_recv()
        send_far(1)
        vec_sum = vec_mine[...] + vec_land[0] + vec_land[1] + vec_land[2]
        for k in range(n_dp):
            vec_near[k] = pltpu.roll(vec_sum, (width - k * shard) % width, 1)[:, 0:128]
        for block in range(line):
            cross_send[VEC][block] = vec_near[block * 2 + 1 - side]
        cross(far_end, [VEC])
        cross(far_end - 1, [VEC])
        send_far(8)
        live = ends_of(lengths_ref)[-1]
        stays = []

        def close_rows(i):
            if i == 0:
                for name in ("hidden", "grad_middle", "middle", "positions"):
                    loads[name].wait()
                last_copy.wait_recv()
                mate_own.wait_recv()
            far_made[2 * i].wait_recv()
            far_made[2 * i + 1].wait_recv()
            span = pl.ds(i * part_rows, part_rows)
            ids = tensor * rows + i * part_rows + lax.broadcasted_iota(
                jnp.int32, (part_rows, 1), 0
            )
            final = (
                held["middle"][span]
                + held["last"][0, span].astype(F32)
                + last_land[span].astype(F32)
                + held["vec_all"][7:8]
            )
            block_kept[span] = jnp.where(ids < live, final, 0.0).astype(LOW)
            grad = (
                part[tensor, span].astype(F32)
                + mate_land[0, span].astype(F32)
                + far_land[span].astype(F32)
            )
            normed, inverse = normalize(held["hidden"][span].astype(F32))
            grad = held["grad_middle"][span] + norm_back(
                normed, inverse, grad, held["vec_all"][0:1]
            )
            for w in range(part_rows // window):
                index = i * (part_rows // window) + w
                here = (
                    lax.broadcasted_iota(jnp.int32, (window, 1), 0)
                    == held["positions"][index : index + 1, 0:1] - index * window
                )
                piece = grad[w * window : (w + 1) * window]
                tokens_kept[pl.ds(index * window, window)] = jnp.where(here, 0.0, piece)
                thoughts_kept[index : index + 1] = jnp.sum(
                    jnp.where(here, piece, 0.0), axis=0, keepdims=True
                )
            moves = [(tokens_kept.at[span], tokens_out.at[span])]
            moves.append((block_kept.at[span], block_out.at[span]))
            if i == 3:
                moves.append((thoughts_kept, thoughts_out))
            for kept_ref, out_ref in moves:
                stays.append(
                    pltpu.make_async_copy(kept_ref, out_ref, local.at[len(kept) + len(stays)])
                )
                stays[-1].start()

        done = 0
        for distance in range(far_end, 0, -1):
            handle_all(distance, (MIX, VEC))
            if distance >= 2:
                cross(distance - 2, (MIX, VEC))
            if distance <= 3:
                close_rows(done)
                done += 1
        for i in range(done, 4):
            close_rows(i)
        for i in (FC, PROJ, MIX):
            close(i, out[i])
        close(VEC, vec_out)
        copies.finish()
        for copy in stays:
            copy.wait()

    f32 = lambda *shape: jax.ShapeDtypeStruct(shape, F32)
    outputs = (
        f32(shard, width), f32(shard, width), f32(shard, width), f32(VEC_ROWS, 128),
        f32(rows, width), f32(latents, width), jax.ShapeDtypeStruct((rows, width), LOW),
    )
    scratch = [pltpu.VMEM(arrays[name].shape, arrays[name].dtype) for name in kept]
    for number, wide in ((line, 1), (line, 1), (last, 3), (last, 3)):
        scratch += [pltpu.VMEM((number, shard, width), LOW)] * wide
        scratch.append(pltpu.VMEM((number, VEC_ROWS, 128), F32))
    scratch += [
        pltpu.VMEM((4, rows, width), LOW),
        pltpu.VMEM((2, rows, width), LOW),
        pltpu.VMEM((rows, width), LOW),
        pltpu.VMEM((rows, width), LOW),
        pltpu.VMEM((rows, width), LOW),
        pltpu.VMEM((n_dp, shard, width), LOW),
        pltpu.VMEM((VEC_ROWS, width), F32),
        pltpu.VMEM((3, VEC_ROWS, width), F32),
        pltpu.VMEM((n_dp, VEC_ROWS, 128), F32),
        pltpu.VMEM((width, width), F32),
        pltpu.VMEM((1, width), F32),
        pltpu.VMEM(arrays["out_far"].shape, LOW),
        pltpu.VMEM((rows, width), F32),
        pltpu.VMEM((latents, width), F32),
        pltpu.VMEM((rows, width), LOW),
    ]
    return comm_call(
        kernel,
        "finish_grads",
        outputs,
        (lengths, *arrays.values()),
        [SM] + [ANY] * len(names),
        (VM,) * 4 + (ANY,) * 3,
        (last + 1) * 2 + last * 4 + 1 + 2 + 8 + 3 + 1,
        cid,
        scratch=scratch,
        local=len(kept) + 9,
        limit=63 << 20,
    )


def unit_kernel(add, line, bias_row, lengths_ref, *refs):
    refs = list(refs)
    rows_ref, grad_own, grad_mate = refs[:3]
    pieces, vec_ref = refs[3:7], refs[7]
    refs = refs[8:]
    if add:
        last_in, two_in = refs[:2]
        refs = refs[2:]
    last_ref, two_ref, fc_near, fc_side, proj_near, proj_side, bias_grad_ref = refs[:7]
    fc_all, proj_all, fc_sum, proj_sum = refs[7:]
    step = pl.program_id(0)
    side, tensor = lax.axis_index("dp") % 2, lax.axis_index("tensor")
    live = ends_of(lengths_ref)[-1]

    @pl.when(step == 0)
    def _():
        for full, near, across in ((fc_all, *pieces[:2]), (proj_all, *pieces[2:])):
            for i in range(line):
                full[2 * i + side] = near[i]
                full[2 * i + 1 - side] = across[i]
        fc_sum[...] = jnp.zeros_like(fc_sum)
        proj_sum[...] = jnp.zeros_like(proj_sum)
        bias_grad_ref[...] = jnp.zeros_like(bias_grad_ref)

    count, width = rows_ref.shape
    half = pl.num_programs(0) // 2
    block = jnp.where(step < half, tensor, tensor + 1 - 2 * (tensor % 2))
    first = block * (half * count) + (step % half) * count
    alive = first + lax.broadcasted_iota(jnp.int32, (count, 1), 0) < live
    rows = rows_ref[...]
    grad = jnp.where(step < half, grad_own[...], grad_mate[...])
    grad = jnp.where(alive, grad, jnp.zeros_like(grad))
    fc = fc_all[...].reshape(width, -1)
    proj = proj_all[...].reshape(width, -1)
    inner = nn(rows, fc) + vec_ref[bias_row : bias_row + 1]
    square = inner * inner
    bend = jnp.tanh(GELU_SCALE * inner * (1.0 + GELU_CUBE * square))
    half = 0.5 * (1.0 + bend)
    activated = (inner * half).astype(LOW)
    slope = half + 0.5 * inner * (1.0 - bend * bend) * GELU_SCALE * (1.0 + 3.0 * GELU_CUBE * square)
    grad_inner = (nn(grad, proj) * slope).astype(LOW)
    last = nt(activated, proj)
    two = nt(grad_inner, fc)
    if add:
        last, two = last + last_in[...], two + two_in[...]
    last_ref[...] = last.astype(last_ref.dtype)
    two_ref[...] = two.astype(two_ref.dtype)
    fc_sum[...] += tn(rows, grad_inner)
    proj_sum[...] += tn(grad, activated)
    bias_grad_ref[...] += jnp.sum(grad_inner.astype(F32), axis=0, keepdims=True)

    @pl.when(step == pl.num_programs(0) - 1)
    def _():
        shard = fc_near.shape[1]
        for sums, near, across in ((fc_sum, fc_near, fc_side), (proj_sum, proj_near, proj_side)):
            for i in range(line):
                even = sums[2 * i * shard : (2 * i + 1) * shard].astype(LOW)
                odd = sums[(2 * i + 1) * shard : (2 * i + 2) * shard].astype(LOW)
                near[i] = jnp.where(side == 0, even, odd)
                across[i] = jnp.where(side == 0, odd, even)


def units_both_ways(lengths, rows, grad, mate_grad, pieces, vec_all, bias_row, before):
    count, width = rows.shape
    line, shard, units = pieces[0].shape
    half = count // ROW_TILE // 2
    tile = pl.BlockSpec((ROW_TILE, width), lambda i: (i, 0))
    fixed = lambda shape: pl.BlockSpec(shape, lambda i: (0,) * len(shape))
    add = before is not None
    kind = LOW if add else F32
    return pl.pallas_call(
        functools.partial(unit_kernel, add, line, bias_row),
        grid=(count // ROW_TILE,),
        out_shape=(
            jax.ShapeDtypeStruct((count, width), kind),
            jax.ShapeDtypeStruct((count, width), kind),
        )
        + (jax.ShapeDtypeStruct((line, shard, units), LOW),) * 4
        + (jax.ShapeDtypeStruct((1, units), F32),        ),
        in_specs=[
            SM,
            tile,
            pl.BlockSpec((ROW_TILE, width), lambda i: (jnp.minimum(i, half - 1), 0)),
            pl.BlockSpec((ROW_TILE, width), lambda i: (jnp.maximum(i - half, 0), 0)),
        ]
        + [fixed((line, shard, units))] * 4
        + [fixed(vec_all.shape)]
        + [tile] * (2 if add else 0),
        out_specs=(tile, tile) + (fixed((line, shard, units)),) * 4 + (fixed((1, units)),),
        scratch_shapes=[pltpu.VMEM((2 * line, shard, units), LOW)] * 2
        + [pltpu.VMEM((width, units), F32)] * 2,
        compiler_params=pltpu.CompilerParams(
            dimension_semantics=("arbitrary",), vmem_limit_bytes=56 << 20
        ),
        cost_estimate=pl.CostEstimate(
            flops=12 * count * width * units,
            bytes_accessed=24 * count * width,
            transcendentals=count * units,
        ),
        name="units_second" if add else "units_first",
    )(lengths, rows, grad, mate_grad, *pieces, vec_all, *(before or ()))


def split_grads(mix_grad, vec, through, share):
    shard, width = mix_grad.shape
    head_width = NH * HD
    count = len(through)

    def kernel(mix_ref, vec_ref, *refs):
        given, (qkv_out, out_out), refs = refs[:count], refs[count : count + 2], refs[count + 2 :]
        small, passed, held, sems = refs[:8], refs[8 : 8 + count], refs[8 + count : -1], refs[-1]
        ins = [pltpu.make_async_copy(given[i], held[i], sems.at[i]) for i in range(count)]
        outs = [
            pltpu.make_async_copy(held[i], passed[i], sems.at[count + i]) for i in range(count)
        ]
        for copy in ins:
            copy.start()
        for i in range(count):
            ins[i].wait()
            outs[i].start()
        tensor = lax.axis_index("tensor")
        turned = mix_ref[...].T
        pieces = []
        for h in range(NH):
            for part in range(3):
                low = part * WIDE + h * HD
                pieces.append(turned[low : low + HD])
        qkv_out[...] = jnp.concatenate(pieces, axis=0).T
        for part in range(3):
            low = part * WIDE + head_width
            out_out[part * HD : (part + 1) * HD] = turned[low : low + HD]
        rows = vec_ref[0:8]
        moved = rows
        for i in range(1, 4):
            moved = jnp.where(tensor == i, pltpu.roll(rows, 128 - i * share, 1), moved)
        for i, row in enumerate((0, 1, 4, 5, 6, 7)):
            small[i][...] = moved[row : row + 1, 0:share]
        small[6][...] = moved[2:4, 0:share]
        small[7][...] = vec_ref[pl.ds(8 + tensor, 1)][:, 0:shard]
        for copy in outs:
            copy.wait()

    f32 = lambda *shape: jax.ShapeDtypeStruct(shape, F32)
    return pl.pallas_call(
        kernel,
        out_shape=(f32(shard, 3 * head_width), f32(head_width, shard))
        + (f32(1, share),) * 6
        + (f32(2, share), f32(1, shard))
        + tuple(jax.ShapeDtypeStruct(x.shape, x.dtype) for x in through),
        in_specs=[VM] * 2 + [ANY] * count,
        out_specs=(VM,) * 10 + (ANY,) * count,
        scratch_shapes=[pltpu.VMEM(x.shape, x.dtype) for x in through]
        + [pltpu.SemaphoreType.DMA((2 * count,))],
        name="split_grads",
    )(mix_grad, vec, *through)


def by_tensor(row, step, index):
    moved = row
    for i in range(1, 4):
        moved = jnp.where(index == i, pltpu.roll(row, (i * step) % row.shape[1], 1), moved)
    return moved


def units_row(rows, block, n_dp):
    width = rows.shape[1]
    shard, step = width // n_dp, n_dp // 4
    lane = lax.broadcasted_iota(jnp.int32, (1, width), 1) // shard
    base = by_tensor(rows, width - step * shard, block)
    total = jnp.zeros((1, width), F32)
    for j in range(n_dp):
        moved = pltpu.roll(base[j % 4 : j % 4 + 1], (j - j // 4) * shard, 1)
        total = jnp.where(lane == j, moved, total)
    return total


def units_rows_back(row, block, n_dp):
    width = row.shape[1]
    shard, step = width // n_dp, n_dp // 4
    lane = lax.broadcasted_iota(jnp.int32, (1, width), 1) // shard
    rows = [jnp.zeros((1, width), F32) for _ in range(4)]
    for j in range(n_dp):
        moved = pltpu.roll(row, (width - (j - j // 4) * shard) % width, 1)
        rows[j % 4] = jnp.where(lane == j // 4, moved, rows[j % 4])
    return by_tensor(jnp.concatenate(rows, axis=0), step * shard, block)


def normalize(values):
    center = jnp.mean(values, axis=-1, keepdims=True)
    offset = values - center
    spread = jnp.mean(offset * offset, axis=-1, keepdims=True)
    inverse = lax.rsqrt(spread + EPSILON)
    return offset * inverse, inverse


def norm_back(normed, inverse, grad, gain):
    scaled = grad * gain
    center = jnp.mean(scaled, axis=-1, keepdims=True)
    along = jnp.mean(scaled * normed, axis=-1, keepdims=True)
    return inverse * (scaled - center - normed * along)


def product(equation, left, right):
    return jnp.einsum(equation, left, right, preferred_element_type=F32)


def per_device(
    tokens,
    thoughts,
    positions,
    lengths,
    attn_norm_gain,
    attn_norm_shift,
    qkv_weight,
    qv_bias,
    attn_out_weight,
    attn_out_bias,
    mlp_norm_gain,
    mlp_norm_shift,
    fc_weight,
    fc_bias,
    proj_weight,
    proj_bias,
    cotangent,
):
    n_dp = lax.axis_size("dp")
    n_tensor = lax.axis_size("tensor")
    rows, width = tokens.shape
    slots = rows * n_tensor
    swap_far = [(i, (i + 2) % n_tensor) for i in range(n_tensor)]

    share = width // (n_dp * n_tensor)
    small = [
        attn_norm_gain[None], attn_norm_shift[None], qv_bias, attn_out_bias[None],
        mlp_norm_gain[None], mlp_norm_shift[None], proj_bias[None], fc_bias[None],
    ]
    (
        group_low, mixed, mix_all, fc_near, fc_side, fc_far_near, proj_near, mate_grad, out_own,
        hidden, vec_all, places,
    ) = gather_inputs(
        tokens, thoughts, positions, cotangent, fc_weight, proj_weight.T, qkv_weight,
        attn_out_weight, small, n_dp,
    )
    mixed = mixed.reshape(slots, -1)
    swap_side = [(i, i + 1 - 2 * (i % 2)) for i in range(n_dp)]
    out_far = lax.ppermute(out_own, "tensor", swap_far)
    proj_far_near = lax.ppermute(proj_near, "tensor", swap_far)
    fc_far_side = lax.ppermute(fc_far_near, "dp", swap_side)
    attended, stats = attend(lengths, mixed)
    sent, out_far, proj_far_near, fc_far_side = lax.optimization_barrier(
        (attended, out_far, proj_far_near, fc_far_side)
    )
    proj_far_side = lax.ppermute(proj_far_near, "dp", swap_side)
    both, middle, chip_two = after_attention(
        sent, out_own, out_far, hidden, vec_all, n_dp, 1
    )
    chip_two, proj_far_side, proj_sent = lax.optimization_barrier(
        (chip_two, proj_far_side, proj_near)
    )
    proj_side = lax.ppermute(proj_sent, "dp", swap_side)
    chip_two = chip_two.reshape(2 * rows, width)

    first = units_both_ways(
        lengths, chip_two, cotangent, mate_grad,
        (fc_far_near, fc_far_side, proj_far_near, proj_far_side), vec_all, 13, None,
    )
    far_fc_near, far_fc_side, far_proj_near, far_proj_side, far_fc_bias = first[2:]
    proj_side_far = lax.ppermute(far_proj_side, "tensor", swap_far)
    fc_far_side_in = lax.ppermute(far_fc_side, "dp", swap_side)
    second = units_both_ways(
        lengths, chip_two, cotangent, mate_grad, (fc_near, fc_side, proj_near, proj_side), vec_all, 12,
        first[:2],
    )
    last_part, grad_two_part, fc_near_grad, fc_side_grad, proj_near_grad, proj_side_grad = second[:6]
    fc_near_side_in = lax.ppermute(fc_side_grad, "dp", swap_side)
    grad_heads, grad_middle, grad_out, far_out, vec_part = before_attention_back(
        lengths, grad_two_part.reshape(2, rows, width), middle, cotangent, both, out_own, out_far,
        vec_all, n_dp, 2,
    )
    fc_cross = far_fc_near + fc_far_side_in
    proj_cross = proj_side_grad + proj_side_far
    grad_heads, fc_cross, proj_cross, far_proj_near = lax.optimization_barrier(
        (grad_heads, fc_cross, proj_cross, far_proj_near)
    )
    fc_cross = lax.ppermute(fc_cross, "tensor", swap_far)
    proj_cross = lax.ppermute(proj_cross, "dp", swap_side)
    proj_near_far = lax.ppermute(far_proj_near, "tensor", swap_far)
    last_low = last_part.reshape(2, rows, width)

    grad_mixed = attend_back(lengths, mixed, attended, stats, grad_heads)
    arrays = {
        "fc_near": fc_near_grad, "fc_near_side": fc_near_side_in, "fc_cross": fc_cross,
        "proj_near": proj_near_grad, "proj_near_far": proj_near_far, "proj_cross": proj_cross,
        "grad_mixed": grad_mixed.reshape(n_tensor, rows, width), "mix": mix_all,
        "last": last_low, "group": group_low,
        "out_own": grad_out, "out_far": far_out,
        "vec_all": vec_all, "vec_part": vec_part, "bias_own": second[6], "bias_far": far_fc_bias,
        "hidden": hidden, "grad_middle": grad_middle, "middle": middle, "positions": places,
    }
    fc_grad, proj_grad, mix_grad, vec, grad_tokens, grad_thoughts, block_out = finish_grads(
        lengths, arrays, n_dp, 8
    )
    parts = split_grads(
        mix_grad, vec, (fc_grad, proj_grad, grad_tokens, grad_thoughts, block_out), share
    )
    qkv_grad, out_grad = parts[:2]
    gain_one, shift_one, out_bias, gain_two, shift_two, last_bias = [p[0] for p in parts[2:8]]
    query_value, hidden_bias = parts[8], parts[9][0]
    fc_grad, proj_grad, grad_tokens, grad_thoughts, block_out = parts[10:]
    return (
        block_out,
        grad_tokens,
        grad_thoughts,
        gain_one,
        shift_one,
        qkv_grad,
        query_value,
        out_grad,
        out_bias,
        gain_two,
        shift_two,
        fc_grad,
        hidden_bias,
        proj_grad.T,
        last_bias,
    )


def solution(mesh):
    rows = P(("dp", "tensor"), None)
    line = P(("dp", "tensor"))
    in_specs = (
        rows, rows, line, P("dp", None), line, line, P("dp", "tensor"),
        P(None, ("dp", "tensor")), P("tensor", "dp"), line, line, line,
        P("dp", "tensor"), line, P("tensor", "dp"), line, rows,
    )
    out_specs = (
        rows, rows, rows, line, line, P("dp", "tensor"), P(None, ("dp", "tensor")),
        P("tensor", "dp"), line, line, line, P("dp", "tensor"), line, P("tensor", "dp"), line,
    )
    return jax.shard_map(
        per_device, mesh=mesh, in_specs=in_specs, out_specs=out_specs, check_vma=False
    )
```

```python
import functools
import math

import jax
import jax.numpy as jnp
from jax import lax
from jax.experimental import pallas as pl
from jax.experimental.pallas import tpu as pltpu
from jax.sharding import PartitionSpec as P

H = 12
HD = 64
FF = 3072
SEQ_DEV = 3
EPSILON = 1e-05
MASKED = -1e30
NH = 3
SLABS = 2
WIDE = SLABS * 128
BQ = 512
BK = 512
VEC_ROWS = 16
VMEM_LIMIT = 67043328
ROW_TILE = 256
GELU_SCALE = math.sqrt(2.0 / math.pi)
GELU_CUBE = 0.044715
MESH = pl.DeviceIdType.MESH
ANY = pl.BlockSpec(memory_space=pltpu.HBM)
VM = pl.BlockSpec(memory_space=pltpu.VMEM)
SM = pl.BlockSpec(memory_space=pltpu.SMEM)
LOW = jnp.bfloat16
F32 = jnp.float32


def nn(a, b):
    return lax.dot_general(a, b, (((1,), (0,)), ((), ())), preferred_element_type=jnp.float32)


def nt(a, b):
    return lax.dot_general(a, b, (((1,), (1,)), ((), ())), preferred_element_type=jnp.float32)


def tn(a, b):
    return lax.dot_general(a, b, (((0,), (0,)), ((), ())), preferred_element_type=jnp.float32)


def head_rows(slab, head):
    half = slab[(head % 2) * HD : (head % 2 + 1) * HD]
    zero = jnp.zeros_like(half)
    return jnp.concatenate([half, zero] if head % 2 == 0 else [zero, half], axis=0)


def ends_of(lengths_ref):
    ends = [lengths_ref[0, 0]]
    for i in range(1, SEQ_DEV):
        ends.append(ends[-1] + lengths_ref[0, i])
    return ends


def segment_start(ends, slots):
    start = jnp.zeros_like(slots)
    for i in range(SEQ_DEV):
        start = jnp.where(slots >= ends[i], ends[i], start)
    return start


def segment_stop(ends, slot, slots):
    stop = slots
    for i in reversed(range(SEQ_DEV)):
        stop = jnp.where(slot < ends[i], ends[i], stop)
    return stop


def attend_kernel(lengths_ref, mixed_in, out_ref, stat_ref, mixed_ref, qt_ref, vt_ref, sems):
    tokens = mixed_ref.shape[0]
    ends = ends_of(lengths_ref)
    loads = []
    for i in range(tokens // BQ):
        rows = pl.ds(i * BQ, BQ)
        loads.append(pltpu.make_async_copy(mixed_in.at[rows], mixed_ref.at[rows], sems.at[i]))
        loads[i].start()
    for first in range(0, tokens, BQ):
        rows = pl.ds(first, BQ)
        loads[first // BQ].wait()
        for slab in range(SLABS):
            lanes = slab * 128
            qt_ref[lanes : lanes + 128, rows] = (
                mixed_ref[rows, lanes : lanes + 128] * HD ** (-0.5)
            ).T
            vt_ref[lanes : lanes + 128, rows] = mixed_ref[
                rows, 2 * WIDE + lanes : 2 * WIDE + lanes + 128
            ].T

    def query_block(block, carry):
        first = pl.multiple_of(block * BQ, BQ)
        columns = pl.ds(first, BQ)
        start = segment_start(ends, first + lax.broadcasted_iota(jnp.int32, (1, BQ), 1))
        query_ids = first + lax.broadcasted_iota(jnp.int32, (BK, BQ), 1)
        queries = [
            head_rows(qt_ref[(h // 2) * 128 : (h // 2 + 1) * 128, columns], h) for h in range(NH)
        ]

        def key_block(key, state):
            base = pl.multiple_of(key * BK, BK)
            rows = pl.ds(base, BK)
            key_ids = base + lax.broadcasted_iota(jnp.int32, (BK, BQ), 0)
            allowed = (key_ids <= query_ids) & (key_ids >= start)
            result = []
            for h in range(NH):
                peak, total, acc = state[h]
                slab = h // 2
                scores = nn(mixed_ref[rows, WIDE + slab * 128 : WIDE + slab * 128 + 128], queries[h])
                scores = jnp.where(allowed, scores, MASKED)
                fresh = jnp.maximum(peak, jnp.max(scores, axis=0, keepdims=True))
                weight = jnp.exp(scores - fresh)
                decay = jnp.exp(peak - fresh)
                total = total * decay + jnp.sum(weight, axis=0, keepdims=True)
                values = vt_ref[h * HD : (h + 1) * HD, rows]
                acc = acc * decay + nn(values, weight.astype(jnp.bfloat16))
                result.append((fresh, total, acc))
            return tuple(result)

        empty = tuple(
            (
                jnp.full((1, BQ), MASKED, jnp.float32),
                jnp.zeros((1, BQ), jnp.float32),
                jnp.zeros((HD, BQ), jnp.float32),
            )
            for _ in range(NH)
        )
        state = lax.fori_loop(segment_start(ends, first) // BK, (block + 1) * (BQ // BK), key_block, empty)
        for h in range(NH):
            peak, total, acc = state[h]
            out_ref[h * HD : (h + 1) * HD, columns] = (acc / total).astype(jnp.bfloat16)
            stat_ref[h : h + 1, columns] = peak + jnp.log(total)
        return carry

    count = (ends[-1] + BQ - 1) // BQ
    lax.fori_loop(0, count, query_block, 0)

    def padded_block(block, carry):
        columns = pl.ds(pl.multiple_of(block * BQ, BQ), BQ)
        out_ref[:, columns] = jnp.zeros((out_ref.shape[0], BQ), jnp.bfloat16)
        return carry

    lax.fori_loop(count, tokens // BQ, padded_block, 0)


def attend(lengths, mixed):
    tokens = mixed.shape[0]
    vm = pl.BlockSpec(memory_space=pltpu.VMEM)
    return pl.pallas_call(
        attend_kernel,
        out_shape=(
            jax.ShapeDtypeStruct((NH * HD, tokens), jnp.bfloat16),
            jax.ShapeDtypeStruct((8, tokens), jnp.float32),
        ),
        in_specs=[pl.BlockSpec(memory_space=pltpu.SMEM), pl.BlockSpec(memory_space=pltpu.HBM)],
        out_specs=(vm, vm),
        scratch_shapes=[pltpu.VMEM(mixed.shape, mixed.dtype)]
        + [pltpu.VMEM((WIDE, tokens), jnp.bfloat16)] * 2
        + [pltpu.SemaphoreType.DMA((tokens // BQ,))],
        compiler_params=pltpu.CompilerParams(vmem_limit_bytes=VMEM_LIMIT),
        cost_estimate=pl.CostEstimate(
            flops=8 * tokens * tokens * NH * HD,
            bytes_accessed=16 * tokens * WIDE,
            transcendentals=tokens * tokens,
        ),
        name="attend",
    )(lengths, mixed)


def attend_back_kernel(
    lengths_ref, mixed_ref, out_ref, stat_ref, gradt_ref,
    gmixed_ref, qt_ref, kt_ref, grad_ref, delta_ref, dqt_ref
):
    tokens = mixed_ref.shape[0]
    ends = ends_of(lengths_ref)
    for first in range(0, tokens, BQ):
        rows = pl.ds(first, BQ)
        for slab in range(SLABS):
            lanes = slab * 128
            qt_ref[lanes : lanes + 128, rows] = (
                mixed_ref[rows, lanes : lanes + 128] * HD ** (-0.5)
            ).T
            kt_ref[lanes : lanes + 128, rows] = mixed_ref[rows, WIDE + lanes : WIDE + lanes + 128].T
        grad_ref[rows, 0:128] = gradt_ref[0:128, rows].T
        grad_ref[rows, 128:256] = jnp.concatenate(
            [gradt_ref[128:192, rows], jnp.zeros((64, BQ), jnp.bfloat16)], axis=0
        ).T
        for h in range(NH):
            product = gradt_ref[h * HD : (h + 1) * HD, rows].astype(jnp.float32) * out_ref[
                h * HD : (h + 1) * HD, rows
            ].astype(jnp.float32)
            delta_ref[h : h + 1, rows] = jnp.sum(product, axis=0, keepdims=True)
    dqt_ref[...] = jnp.zeros_like(dqt_ref)
    lane = lax.broadcasted_iota(jnp.int32, (BQ, 128), 1)

    def key_block(key, carry):
        base = pl.multiple_of(key * BK, BK)
        rows = pl.ds(base, BK)
        key_ids = base + lax.broadcasted_iota(jnp.int32, (BK, BQ), 0)

        def query_block(block, state):
            first = pl.multiple_of(block * BQ, BQ)
            columns = pl.ds(first, BQ)
            start = segment_start(ends, first + lax.broadcasted_iota(jnp.int32, (1, BQ), 1))
            query_ids = first + lax.broadcasted_iota(jnp.int32, (BK, BQ), 1)
            allowed = (key_ids <= query_ids) & (key_ids >= start)
            grad_keys = list(state[:SLABS])
            grad_values = list(state[SLABS:])
            for h in range(NH):
                slab = h // 2
                low, high = slab * 128, slab * 128 + 128
                queries = head_rows(qt_ref[low:high, columns], h)
                scores = nn(mixed_ref[rows, WIDE + low : WIDE + high], queries)
                probs = jnp.where(allowed, jnp.exp(scores - stat_ref[h : h + 1, columns]), 0.0)
                keep = (lane // HD) == (h % 2)
                grads = jnp.where(keep, grad_ref[columns, low:high], 0.0)
                grad_values[slab] += nn(probs.astype(jnp.bfloat16), grads)
                if h == NH - 1 and NH % 2 == 1:
                    grad_rows = jnp.concatenate(
                        [gradt_ref[h * HD : (h + 1) * HD, columns], jnp.zeros((HD, BQ), jnp.bfloat16)],
                        axis=0,
                    )
                else:
                    grad_rows = head_rows(gradt_ref[low:high, columns], h)
                grad_probs = nn(mixed_ref[rows, 2 * WIDE + low : 2 * WIDE + high], grad_rows)
                grad_scores = (probs * (grad_probs - delta_ref[h : h + 1, columns])).astype(
                    jnp.bfloat16
                )
                natural = mixed_ref[columns, low:high]
                grad_keys[slab] += nn(grad_scores, jnp.where(keep, natural, 0.0))
                dqt_ref[h * HD : (h + 1) * HD, columns] += nn(
                    kt_ref[h * HD : (h + 1) * HD, rows], grad_scores
                )
            return tuple(grad_keys) + tuple(grad_values)

        empty = (jnp.zeros((BK, 128), jnp.float32),) * (2 * SLABS)
        stop = jnp.minimum(segment_stop(ends, base + BK - 1, tokens), ends[-1])
        state = lax.fori_loop(key * BK // BQ, (stop - 1) // BQ + 1, query_block, empty)
        for slab in range(SLABS):
            low = slab * 128
            gmixed_ref[rows, WIDE + low : WIDE + low + 128] = (
                state[slab] * HD ** (-0.5)
            ).astype(jnp.bfloat16)
            gmixed_ref[rows, 2 * WIDE + low : 2 * WIDE + low + 128] = state[SLABS + slab].astype(
                jnp.bfloat16
            )
        return carry

    count = (ends[-1] + BK - 1) // BK
    lax.fori_loop(0, count, key_block, 0)

    def padded_block(key, carry):
        rows = pl.ds(pl.multiple_of(key * BK, BK), BK)
        gmixed_ref[rows, WIDE:] = jnp.zeros((BK, 2 * WIDE), jnp.bfloat16)
        return carry

    lax.fori_loop(count, tokens // BK, padded_block, 0)
    for first in range(0, tokens, BQ):
        rows = pl.ds(first, BQ)
        for slab in range(SLABS):
            low = slab * 128
            gmixed_ref[rows, low : low + 128] = (
                (dqt_ref[low : low + 128, rows] * HD ** (-0.5)).T.astype(jnp.bfloat16)
            )


def attend_back(lengths, mixed, out, stat, gradt):
    tokens = mixed.shape[0]
    vm = pl.BlockSpec(memory_space=pltpu.VMEM)
    return pl.pallas_call(
        attend_back_kernel,
        out_shape=jax.ShapeDtypeStruct((tokens, 3 * WIDE), jnp.bfloat16),
        in_specs=[pl.BlockSpec(memory_space=pltpu.SMEM)] + [vm] * 4,
        out_specs=vm,
        scratch_shapes=[
            pltpu.VMEM((WIDE, tokens), jnp.bfloat16),
            pltpu.VMEM((WIDE, tokens), jnp.bfloat16),
            pltpu.VMEM((tokens, WIDE), jnp.bfloat16),
            pltpu.VMEM((8, tokens), jnp.float32),
            pltpu.VMEM((WIDE, tokens), jnp.float32),
        ],
        compiler_params=pltpu.CompilerParams(vmem_limit_bytes=VMEM_LIMIT),
        cost_estimate=pl.CostEstimate(
            flops=20 * tokens * tokens * NH * HD,
            bytes_accessed=32 * tokens * WIDE,
            transcendentals=tokens * tokens,
        ),
        name="attend_back",
    )(lengths, mixed, out, stat, gradt)


class Copies:
    def __init__(self, send, recv):
        self.send, self.recv, self.made, self.started = send, recv, 0, []

    def plan(self, source, target, device):
        index = self.made
        self.made += 1
        return pltpu.make_async_remote_copy(
            src_ref=source,
            dst_ref=target,
            send_sem=self.send.at[index],
            recv_sem=self.recv.at[index],
            device_id=device,
            device_id_type=MESH,
        )

    def begin(self, copy, condition=None):
        self.started.append((copy, condition))
        when(condition, copy.start)

    def start(self, source, target, device):
        copy = self.plan(source, target, device)
        self.begin(copy)
        return copy

    def finish(self):
        for copy, condition in self.started:
            when(condition, copy.wait_send)


def when(condition, action):
    if condition is None:
        action()
    else:
        pl.when(condition)(action)


def greet(devices):
    barrier = pltpu.get_barrier_semaphore()
    for device, condition in devices:
        when(
            condition,
            lambda device=device: pl.semaphore_signal(
                barrier, inc=1, device_id=device, device_id_type=MESH
            ),
        )
    present = [1 if condition is None else condition.astype(jnp.int32) for _, condition in devices]
    pl.semaphore_wait(barrier, sum(present))


class Place:
    def __init__(self, line):
        self.dp = dp = lax.axis_index("dp")
        self.tensor = tensor = lax.axis_index("tensor")
        self.spot, self.side = spot, side = dp // 2, dp % 2
        self.chip, self.core = tensor // 2, tensor % 2
        self.has_up, self.has_down = spot + 1 < line, spot > 0
        self.up = (jnp.minimum(spot + 1, line - 1) * 2 + side, tensor)
        self.down = (jnp.maximum(spot - 1, 0) * 2 + side, tensor)
        self.across = (spot * 2 + 1 - side, tensor)
        self.mate = (dp, tensor + 1 - 2 * (tensor % 2))
        self.far = (dp, (tensor + 2) % 4)
        self.corner = (dp, 3 - tensor)

    def everyone(self):
        return [
            (self.mate, None), (self.far, None), (self.corner, None), (self.across, None),
            (self.up, self.has_up), (self.down, self.has_down),
        ]


def comm_call(kernel, name, outputs, inputs, in_specs, out_specs, copies, cid, scratch=(), local=1, limit=VMEM_LIMIT):
    return pl.pallas_call(
        kernel,
        out_shape=outputs,
        in_specs=in_specs,
        out_specs=out_specs,
        scratch_shapes=list(scratch)
        + [
            pltpu.SemaphoreType.DMA((copies,)),
            pltpu.SemaphoreType.DMA((copies,)),
            pltpu.SemaphoreType.DMA((local,)),
        ],
        compiler_params=pltpu.CompilerParams(
            collective_id=cid, has_side_effects=True, vmem_limit_bytes=limit
        ),
        name=name,
    )(*inputs)


def one_hot(rows, columns, shift, limit):
    lane = lax.broadcasted_iota(jnp.int32, (rows, columns), 0)
    spot = lax.broadcasted_iota(jnp.int32, (rows, columns), 1)
    return ((spot == lane + shift) & (lane < limit)).astype(LOW)


def gather_inputs(tokens, thoughts, positions, cotangent, fc, proj, qkv, out, vectors, n_dp):
    line = n_dp // 2
    hops = line - 1
    rows, width = tokens.shape
    latents = thoughts.shape[0]
    window = rows // latents
    shard = fc.shape[0]
    half_rows = rows // 2
    share = width // (n_dp * 4)

    def kernel(
        pos_ref, tokens_in, thoughts_in, cot_ref, fc_in, proj_in, qkv_in, out_in, *refs
    ):
        given = (fc_in, tokens_in, thoughts_in, proj_in, qkv_in, out_in) + refs[: len(vectors)]
        (
            normed_out, mixed_out, mix_out, fc_near, fc_side, fc_far, proj_near, cot_out, out_out,
            hidden_out, vec_out, pos_out,
            hidden_ref, mix_ref, vec_ref, tile,
            land, mix_land, tiles, tile_land, normed, mixed, out_turned,
            *held, arrive, send, recv, local,
        ) = refs[len(vectors) :]
        arrivals = [
            pltpu.make_async_copy(given[i], held[i], arrive.at[i]) for i in range(len(given))
        ]
        for copy in arrivals:
            copy.start()
        fc_ref, tokens_ref, thoughts_ref, proj_ref, qkv_ref, out_ref = held[:6]
        vec_refs = held[6:]
        at = Place(line)
        dp, tensor, spot, side = at.dp, at.tensor, at.spot, at.side
        mate_row, far_row, corner_row = at.mate[1], at.far[1], at.corner[1]
        greet(at.everyone())
        copies = Copies(send, recv)
        MIX, FC, PROJ, VEC = range(4)
        own = [mix_ref, fc_ref, proj_ref, tiles.at[dp]]

        def seat(item, position):
            if item == MIX:
                return mix_land.at[position * 2 + side]
            if item == FC:
                return fc_near.at[position]
            if item == PROJ:
                return proj_near.at[position]
            return tiles.at[position * 2 + side]

        def plan(item, hop):
            above, below = jnp.maximum(spot - hop, 0), jnp.minimum(spot + hop, line - 1)
            came_up = jnp.maximum(spot - 1 - hop, 0)
            came_down = jnp.minimum(spot + 1 + hop, line - 1)
            made = {
                "up": copies.plan(
                    own[item] if hop == 0 else seat(item, above), seat(item, above), at.up
                ),
                "down": copies.plan(
                    own[item] if hop == 0 else seat(item, below), seat(item, below), at.down
                ),
                "onward": [],
            }
            for position in (came_up, came_down):
                onward = []
                if item in (MIX, VEC):
                    onward.append(copies.plan(seat(item, position), seat(item, position), at.across))
                if item == FC:
                    onward.append(copies.plan(fc_near.at[position], fc_side.at[position], at.across))
                    onward.append(copies.plan(fc_near.at[position], fc_far.at[position], at.far))
                made["onward"].append(onward)
            return made

        plans = [[plan(item, hop) for hop in range(hops)] for item in range(4)]

        def launch(item):
            copies.begin(plans[item][0]["up"], at.has_up)
            copies.begin(plans[item][0]["down"], at.has_down)

        def handle(item, hop):
            made = plans[item][hop]
            for way, key, comes, goes in (
                (0, "up", spot - 1 - hop >= 0, at.has_up),
                (1, "down", spot + 1 + hop < line, at.has_down),
            ):
                when(comes, made[key].wait_recv)
                if hop + 1 < hops:
                    copies.begin(plans[item][hop + 1][key], comes & goes)
                for copy in made["onward"][way]:
                    copies.begin(copy, comes)

        def settle(item):
            for hop in range(hops):
                for way, comes in ((0, spot - 1 - hop >= 0), (1, spot + 1 + hop < line)):
                    for copy in plans[item][hop]["onward"][way]:
                        when(comes, copy.wait_recv)

        stays = []

        def stay(source, target):
            copy = pltpu.make_async_copy(source, target, local.at[len(stays)])
            copy.start()
            stays.append(copy)
            return copy

        parts = [pl.ds(0, half_rows), pl.ds(half_rows, half_rows)]
        arrivals[0].wait()
        launch(FC)
        fc_sides = [copies.start(fc_ref, fc_side.at[spot], at.across)]
        cot_made = copies.start(cot_ref, cot_out, at.mate)
        for copy in arrivals[6:]:
            copy.wait()
        tile[...] = jnp.zeros_like(tile)
        row = 0
        for ref in vec_refs:
            count, size = ref.shape
            tile[row : row + count, 0:size] = ref[...].astype(F32)
            row += count
        vec_ref[...] = tile[...].astype(LOW)
        vec_made = [
            copies.start(vec_ref, tile_land.at[i], device)
            for i, device in enumerate((at.mate, at.far, at.corner))
        ]
        arrivals[1].wait()
        arrivals[2].wait()
        pos_row = lax.broadcasted_iota(jnp.int32, (latents, 128), 0)
        places = jnp.zeros((latents, 128), jnp.int32)
        for w in range(latents):
            places = jnp.where(pos_row == w, pos_ref[w], places)
            span = pl.ds(w * window, window)
            here = lax.broadcasted_iota(jnp.int32, (window, 1), 0) == pos_ref[w] - w * window
            hidden_ref[span] = jnp.where(
                here, thoughts_ref[w : w + 1].astype(F32), tokens_ref[span].astype(F32)
            ).astype(LOW)
        pos_out[...] = places
        far_made = [
            copies.start(hidden_ref.at[part], land.at[2, part], at.far) for part in parts
        ]
        mate_made = copies.start(hidden_ref, land.at[1], at.mate)
        fc_sides.append(copies.start(fc_ref, fc_far.at[spot], at.far))
        for copy in arrivals[3:6]:
            copy.wait()
        turned = qkv_ref[...].astype(F32).T
        extra = out_ref[...].astype(F32)
        pieces = []
        for p in range(3):
            for h in range(NH):
                low = (h * 3 + p) * HD
                pieces.append(turned[low : low + HD])
            pieces.append(extra[p * HD : (p + 1) * HD])
        mix_ref[...] = jnp.concatenate(pieces, axis=0).T.astype(LOW)
        launch(MIX)
        mix_side = copies.start(mix_ref, mix_land.at[dp], at.across)
        stay(hidden_ref, hidden_out)
        stay(fc_ref, fc_near.at[spot])
        stay(proj_ref, proj_near.at[spot])
        mix_land[dp] = mix_ref[...]
        for copy in vec_made:
            copy.wait_recv()
        merged = jnp.zeros((VEC_ROWS, 128), F32)
        bias_rows = jnp.zeros((VEC_ROWS, 128), F32)
        row_ids = lax.broadcasted_iota(jnp.int32, (VEC_ROWS, 128), 0)
        for i, index in enumerate((tensor, mate_row, far_row, corner_row)):
            tile = vec_ref[...] if i == 0 else tile_land[i - 1]
            merged += nn(tile, one_hot(128, 128, index * share, share))
            bias_rows = jnp.where(row_ids == 8 + index, tile[8:9].astype(F32), bias_rows)
        tiles[dp] = jnp.where(row_ids < 8, merged, bias_rows).astype(LOW)
        launch(VEC)
        vec_side = copies.start(tiles.at[dp], tiles.at[dp], at.across)

        def norm_rows(source, index):
            @pl.loop(0, rows // 128)
            def _(i):
                span = pl.ds(pl.multiple_of(i * 128, 128), 128)
                normed[index, span] = normalize(source[span].astype(F32))[0].astype(LOW)

            stay(normed.at[index], normed_out.at[index])

        def relay(i):
            far_made[i].wait_recv()
            return copies.start(land.at[2, parts[i]], land.at[3, parts[i]], at.mate)

        def mix_rows(index):
            @pl.loop(0, rows // 256)
            def _(i):
                span = pl.ds(pl.multiple_of(i * 256, 256), 256)
                turned = normed[index, span].astype(F32) * whole[0:1] + whole[1:2]
                weight = mix_land[...].reshape(width, width)
                mixed[index, span] = (nn(turned.astype(LOW), weight) + bias).astype(LOW)

            stay(mixed.at[index], mixed_out.at[index])

        norm_rows(hidden_ref, tensor)
        relayed = []
        for step in range(hops + 2):
            for item, hop in ((MIX, step), (VEC, step), (FC, step - 1), (PROJ, step - 2)):
                if 0 <= hop < hops:
                    handle(item, hop)
            if step == 0:
                launch(PROJ)
                mate_made.wait_recv()
                norm_rows(land.at[1], mate_row)
                relayed.append(relay(0))
            if step == 1:
                relayed.append(relay(1))
                norm_rows(land.at[2], far_row)
            if step == hops:
                mix_side.wait_recv()
                vec_side.wait_recv()
                settle(MIX)
                settle(VEC)
                whole = jnp.zeros((VEC_ROWS, width), F32)
                for i in range(n_dp):
                    whole += nn(tiles[i], one_hot(128, width, i * shard, shard))
                vec_out[...] = whole
                for i, block in enumerate((tensor, far_row)):
                    vec_out[12 + i : 13 + i] = units_row(whole[8:12], block, n_dp)
                lane = lax.broadcasted_iota(jnp.int32, (width, WIDE), 0)
                column = lax.broadcasted_iota(jnp.int32, (width, WIDE), 1)
                pick = (lane == column + tensor * (NH * HD)) & (column < NH * HD)
                picked = nn(whole.astype(LOW), pick.astype(LOW))
                bias = jnp.concatenate(
                    [picked[2:3], jnp.zeros((1, WIDE), F32), picked[3:4]], axis=1
                )
                mix_rows(tensor)
                mix_rows(mate_row)
        mix_rows(far_row)
        for copy in relayed:
            copy.wait_recv()
        norm_rows(land.at[3], corner_row)
        mix_rows(corner_row)
        stay(mix_land, mix_out)
        weight = mix_land[...].reshape(width, width)
        for part in range(3):
            low = part * WIDE + WIDE - 128
            turned = weight[:, low : low + 128].T
            out_turned[part * HD : (part + 1) * HD] = turned[128 - HD :]
        stay(out_turned, out_out)
        settle(FC)
        for copy in fc_sides:
            copy.wait_recv()
        cot_made.wait_recv()
        copies.finish()
        for copy in stays:
            copy.wait()

    low = lambda *shape: jax.ShapeDtypeStruct(shape, LOW)
    outputs = (
        low(4, rows, width), low(4, rows, width), low(n_dp, shard, width),
        low(line, shard, width), low(line, shard, width), low(line, shard, width),
        low(line, shard, width), low(rows, width), low(NH * HD, width), low(rows, width),
        jax.ShapeDtypeStruct((VEC_ROWS, width), F32),
        jax.ShapeDtypeStruct((latents, 128), jnp.int32),
    )
    scratch = [
        pltpu.VMEM((rows, width), LOW),
        pltpu.VMEM((shard, 3 * WIDE), LOW),
        pltpu.VMEM((VEC_ROWS, 128), LOW),
        pltpu.VMEM((VEC_ROWS, 128), F32),
        pltpu.VMEM((4, rows, width), LOW),
        pltpu.VMEM((n_dp, shard, width), LOW),
        pltpu.VMEM((n_dp, VEC_ROWS, 128), LOW),
        pltpu.VMEM((3, VEC_ROWS, 128), LOW),
        pltpu.VMEM((4, rows, width), LOW),
        pltpu.VMEM((4, rows, width), LOW),
        pltpu.VMEM((NH * HD, width), LOW),
    ]
    given = (fc, tokens, thoughts, proj, qkv, out, *vectors)
    scratch += [pltpu.VMEM(x.shape, x.dtype) for x in given]
    scratch.append(pltpu.SemaphoreType.DMA((len(given),)))
    return comm_call(
        kernel,
        "gather_inputs",
        outputs,
        (positions, tokens, thoughts, cotangent, fc, proj, qkv, out, *vectors),
        [SM] + [ANY] * (7 + len(vectors)),
        (ANY,) * 10 + (VM, VM),
        3 + 2 + 1 + 2 + 2 + 1 + 2 + hops * (2 * 4 + 2 * 4),
        0,
        scratch=scratch,
        local=3 + 8 + 2,
    )


def after_attention(attended, out_own, out_far, hidden, vec_all, n_dp, cid):
    head_width, slots = attended.shape
    rows, width = hidden.shape
    half_rows = rows // 2

    def kernel(
        heads_ref, own_ref, far_ref, hidden_ref, vec_ref,
        both_out, middle_out, two_out,
        land, part, part_low, part_land, two, send, recv, local,
    ):
        at = Place(n_dp // 2)
        greet([(at.far, None), (at.mate, None)])
        copies = Copies(send, recv)
        cores = (at.core, 1 - at.core)
        made = [None, None]
        for i in (1, 0):
            theirs = pl.multiple_of(((1 - at.chip) * 2 + cores[i]) * rows, rows)
            made[i] = copies.start(heads_ref.at[:, pl.ds(theirs, rows)], land.at[i], at.far)
        stays = []

        def stay(source, target):
            stays.append(pltpu.make_async_copy(source, target, local.at[len(stays)]))
            stays[-1].start()

        spans = []
        for i in range(2):
            ours = pl.multiple_of((at.chip * 2 + cores[i]) * rows, rows)
            spans.append(pl.ds(ours, rows))
            stay(heads_ref.at[:, spans[i]], both_out.at[0, :, i * rows : (i + 1) * rows])
            part[i] = tn(heads_ref[:, spans[i]], own_ref[...])
        sums = None
        for i in (1, 0):
            made[i].wait_recv()
            stay(land.at[i], both_out.at[1, :, i * rows : (i + 1) * rows])
            part[i] += tn(land[i], far_ref[...])
            if i == 1:
                part_low[...] = part[1].astype(LOW)
                sums = copies.start(part_low, part_land, at.mate)
        sums.wait_recv()
        mated = []
        for piece in range(2):

            @pl.loop(0, half_rows // 128)
            def _(i):
                span = pl.ds(pl.multiple_of(piece * half_rows + i * 128, 128), 128)
                middle = (
                    hidden_ref[span].astype(F32)
                    + part[0, span]
                    + part_land[span].astype(F32)
                    + vec_ref[4:5]
                )
                middle_out[span] = middle
                two[span] = (normalize(middle)[0] * vec_ref[5:6] + vec_ref[6:7]).astype(LOW)

            span = pl.ds(piece * half_rows, half_rows)
            mated.append(copies.start(two.at[span], two_out.at[1, span], at.mate))
        stay(two, two_out.at[0])
        for copy in mated:
            copy.wait_recv()
        copies.finish()
        for copy in stays:
            copy.wait()

    return comm_call(
        kernel,
        "after_attention",
        (
            jax.ShapeDtypeStruct((2, head_width, 2 * rows), LOW),
            jax.ShapeDtypeStruct((rows, width), F32),
            jax.ShapeDtypeStruct((2, rows, width), LOW),
        ),
        (attended, out_own, out_far, hidden, vec_all),
        [VM] * 5,
        (ANY, VM, ANY),
        5,
        cid,
        scratch=[
            pltpu.VMEM((2, head_width, rows), LOW),
            pltpu.VMEM((2, rows, width), F32),
            pltpu.VMEM((rows, width), LOW),
            pltpu.VMEM((rows, width), LOW),
            pltpu.VMEM((rows, width), LOW),
        ],
        local=5,
    )


def before_attention_back(lengths, two, middle, cotangent, both, out_own, out_far, vec_all, n_dp, cid):
    _, rows, width = two.shape
    head_width = out_own.shape[0]
    half_rows = rows // 2

    def kernel(
        lengths_ref, two_ref, middle_ref, cot_ref, both_ref, own_ref, far_ref, vec_ref,
        heads_out, grad_out, own_out, far_out, vec_out,
        two_land, mid, stay_heads, sent_heads, send, recv, local,
    ):
        at = Place(n_dp // 2)
        greet([(at.far, None), (at.mate, None)])
        copies = Copies(send, recv)
        halves = [pl.ds(0, half_rows), pl.ds(half_rows, half_rows)]
        sums = [copies.start(two_ref.at[1, span], two_land.at[span], at.mate) for span in halves]
        vec_out[...] = jnp.zeros_like(vec_out)
        first_row = at.tensor * rows
        live = ends_of(lengths_ref)[-1]
        mated = []
        for piece in range(2):
            sums[piece].wait_recv()

            @pl.loop(0, half_rows // 128)
            def _(i):
                start = pl.multiple_of(piece * half_rows + i * 128, 128)
                span = pl.ds(start, 128)
                grad = two_ref[0, span].astype(F32) + two_land[span].astype(F32)
                normed, inverse = normalize(middle_ref[span])
                ids = first_row + start + lax.broadcasted_iota(jnp.int32, (128, 1), 0)
                final = jnp.where(ids < live, cot_ref[span].astype(F32), 0.0)
                total = final + norm_back(normed, inverse, grad, vec_ref[5:6])
                grad_out[span] = total
                mid[0, span] = total.astype(LOW)
                for row, term in ((4, total), (5, normed * grad), (6, grad), (7, final)):
                    vec_out[row : row + 1] += jnp.sum(term, axis=0, keepdims=True)

            mated.append(copies.start(mid.at[0, halves[piece]], mid.at[1, halves[piece]], at.mate))
        cores = (at.core, 1 - at.core)
        made, stays = [], []
        for i in range(2):
            if i == 1:
                for copy in mated:
                    copy.wait_recv()
            ours = pl.ds(pl.multiple_of((at.chip * 2 + cores[i]) * rows, rows), rows)
            sent_heads[i] = nt(far_ref[...], mid[i]).astype(LOW)
            made.append(copies.start(sent_heads.at[i], heads_out.at[:, ours], at.far))
            stay_heads[i] = nt(own_ref[...], mid[i]).astype(LOW)
            stays.append(
                pltpu.make_async_copy(stay_heads.at[i], heads_out.at[:, ours], local.at[i])
            )
            stays[-1].start()
        grads = mid[...].reshape(2 * rows, width)
        own_out[...] = nn(both_ref[0], grads).astype(LOW)
        far_out[...] = nn(both_ref[1], grads).astype(LOW)
        for copy in made:
            copy.wait_recv()
        copies.finish()
        for copy in stays:
            copy.wait()

    return comm_call(
        kernel,
        "before_attention_back",
        (
            jax.ShapeDtypeStruct((head_width, 4 * rows), LOW),
            jax.ShapeDtypeStruct((rows, width), F32),
            jax.ShapeDtypeStruct((head_width, width), LOW),
            jax.ShapeDtypeStruct((head_width, width), LOW),
            jax.ShapeDtypeStruct((VEC_ROWS, width), F32),
        ),
        (lengths, two, middle, cotangent, both, out_own, out_far, vec_all),
        [pl.BlockSpec(memory_space=pltpu.SMEM)] + [VM] * 7,
        (ANY,) + (VM,) * 4,
        6,
        cid,
        scratch=[
            pltpu.VMEM((rows, width), LOW),
            pltpu.VMEM((2, rows, width), LOW),
            pltpu.VMEM((2, head_width, rows), LOW),
            pltpu.VMEM((2, head_width, rows), LOW),
        ],
        local=2,
    )


def finish_grads(lengths, arrays, n_dp, cid):
    part_rows = arrays["hidden"].shape[0] // 4
    names = list(arrays)
    kept = [name for name in names if name != "out_far"]
    line = n_dp // 2
    shard = arrays["mix"].shape[1]
    rows, width = arrays["hidden"].shape
    group = 4 * rows
    latents = arrays["positions"].shape[0]
    window = rows // latents
    far_end = line - 1
    slots = [(distance, way) for distance in range(far_end, 0, -1) for way in (0, 1)] + [(0, 0)]
    last = len(slots) - 1
    share = width // (n_dp * 4)
    FC, PROJ, MIX, VEC = range(4)

    def kernel(lengths_ref, *refs):
        refs = list(refs)

        def take(number):
            taken = refs[:number]
            del refs[:number]
            return taken

        source = dict(zip(names, take(len(names))))
        fc_out, proj_out, mix_out, vec_out, tokens_out, thoughts_out, block_out = take(7)
        held = dict(zip(kept, take(len(kept))))
        cross_send, cross_land = [None, None] + take(2), [None, None] + take(2)
        hop_send, hop_land = take(4), take(4)
        (
            part, mate_land, far_send, far_land, last_land, total, vec_mine, vec_land, vec_near,
            plain_sum, column_sum, out_land, tokens_kept, thoughts_kept, block_kept, send, recv,
            local,
        ) = refs
        out = [fc_out, proj_out, mix_out, None]
        at = Place(line)
        tensor, spot, side = at.tensor, at.spot, at.side
        mate_row, far_row, corner_row = at.mate[1], at.far[1], at.corner[1]
        copies = Copies(send, recv)
        loads = {}
        held["out_far"] = out_land
        for i, name in enumerate(kept):
            loads[name] = pltpu.make_async_copy(source[name], held[name], local.at[i])

        def load(*group):
            for name in group:
                loads[name].start()

        load("fc_near", "fc_near_side", "fc_cross", "proj_near", "proj_near_far", "proj_cross")
        load("grad_mixed", "mix")
        greet(at.everyone())

        def block_of(slot):
            distance, way = slots[slot]
            if way == 0:
                return jnp.minimum(spot + distance, far_end), spot + distance < line
            return jnp.maximum(spot - distance, 0), spot - distance >= 0

        crosses, hops = [], []
        for slot in range(len(slots)):
            block, _ = block_of(slot)
            crosses.append(
                {
                    i: copies.plan(cross_send[i].at[block], cross_land[i].at[block], at.across)
                    for i in (MIX, VEC)
                }
            )
            if slot < last:
                hops.append(
                    [
                        copies.plan(
                            hop_send[i].at[slot],
                            hop_land[i].at[slot],
                            (at.up, at.down)[slots[slot][1]],
                        )
                        for i in range(4)
                    ]
                )

        def cross(distance, items):
            for slot in range(len(slots)):
                if slots[slot][0] == distance:
                    for i in items:
                        copies.begin(crosses[slot][i], block_of(slot)[1])

        terms = (
            ("fc_near", "fc_near_side", "fc_cross"),
            ("proj_near", "proj_near_far", "proj_cross"),
        )

        def own_term(i, block):
            if i in (FC, PROJ):
                return sum(held[name][block].astype(F32) for name in terms[i])
            if i == MIX:
                return total[block * 2 + side].astype(F32)
            return vec_near[block * 2 + side]

        def handle(slot, i):
            block, inside = block_of(slot)
            behind = (at.has_down, at.has_up)[slots[slot][1]]
            outer = slot - 2

            def work():
                value = own_term(i, block)
                if i in (MIX, VEC):
                    crosses[slot][i].wait_recv()
                    value = value + cross_land[i][block].astype(F32)
                if outer < 0:
                    hop_send[i][slot] = value.astype(hop_send[i].dtype)
                    return

                @pl.when(behind)
                def _():
                    hops[outer][i].wait_recv()
                    hop_send[i][slot] = (value + hop_land[i][outer].astype(F32)).astype(
                        hop_send[i].dtype
                    )

                @pl.when(jnp.logical_not(behind))
                def _():
                    hop_send[i][slot] = value.astype(hop_send[i].dtype)

            when(inside, work)
            copies.begin(hops[slot][i], inside)

        def handle_all(distance, items):
            for slot in range(last):
                if slots[slot][0] == distance:
                    for i in items:
                        handle(slot, i)

        def close(i, target):
            value = own_term(i, spot)
            if i in (MIX, VEC):
                crosses[last][i].wait_recv()
                value = value + cross_land[i][spot].astype(F32)
            target[...] = value
            for way, behind in enumerate((at.has_down, at.has_up)):

                def add(way=way):
                    hops[last - 2 + way][i].wait_recv()
                    target[...] += hop_land[i][last - 2 + way].astype(F32)

                when(behind, add)

        for name in ("fc_near", "fc_near_side", "fc_cross", "proj_near", "proj_near_far", "proj_cross"):
            loads[name].wait()
        out_made = copies.start(source["out_far"], out_land, at.far)
        handle_all(far_end, (FC, PROJ))
        load("group", "out_own", "vec_all", "vec_part", "bias_own", "bias_far")
        load("last", "hidden", "grad_middle", "middle", "positions")
        loads["grad_mixed"].wait()
        loads["mix"].wait()

        def row_part(index):
            @pl.loop(0, rows // 256)
            def _(i):
                span = pl.ds(pl.multiple_of(i * 256, 256), 256)
                weight = held["mix"][...].reshape(width, width)
                part[index, span] = nt(held["grad_mixed"][index, span], weight).astype(LOW)

        row_part(corner_row)
        mate_far = copies.start(part.at[corner_row], mate_land.at[1], at.mate)
        row_part(mate_row)
        mate_own = copies.start(part.at[mate_row], mate_land.at[0], at.mate)
        row_part(far_row)
        mate_far.wait_recv()
        far_made = []

        def send_far(count):
            for i in range(len(far_made), min(len(far_made) + count, 8)):
                span = pl.ds(i * (part_rows // 2), part_rows // 2)
                far_send[span] = (
                    mate_land[1, span].astype(F32) + part[far_row, span].astype(F32)
                ).astype(LOW)
                far_made.append(copies.start(far_send.at[span], far_land.at[span], at.far))

        send_far(2)
        row_part(tensor)
        send_far(1)
        if far_end > 1:
            handle_all(far_end - 1, (FC, PROJ))
        loads["last"].wait()
        last_copy = copies.start(held["last"].at[1], last_land, at.mate)
        for name in ("group", "out_own", "vec_all", "vec_part", "bias_own", "bias_far"):
            loads[name].wait()
        out_made.wait_recv()

        plain_sum[...] = jnp.zeros_like(plain_sum)
        column_sum[...] = jnp.zeros_like(column_sum)

        @pl.loop(0, group // 256)
        def _(i):
            block, start = i // (rows // 256), (i % (rows // 256)) * 256
            span = pl.ds(pl.multiple_of(start, 256), 256)
            grad = held["grad_mixed"][block, span]
            plain_sum[...] += tn(held["group"][block, span], grad)
            column_sum[...] += jnp.sum(grad.astype(F32), axis=0, keepdims=True)

        send_far(2)
        plain, columns = plain_sum[...], column_sum[...]
        turned = held["vec_all"][...].T
        weight = held["mix"][...].reshape(width, width).astype(F32)
        gain_grad = jnp.sum(plain * weight, axis=1, keepdims=True)
        shift_grad = jnp.sum(weight * columns, axis=1, keepdims=True)
        scaled = plain * turned[:, 0:1] + turned[:, 1:2] * columns
        extras = []
        out_sum = held["out_own"][...].astype(F32) + held["out_far"][...].astype(F32)
        for p in range(3):
            piece = out_sum[p * HD : (p + 1) * HD]
            extras.append(jnp.zeros((width, WIDE - 128), F32))
            extras.append(jnp.concatenate([jnp.zeros((128 - HD, width), F32), piece], axis=0).T)
        scaled = scaled + jnp.concatenate(extras, axis=1)
        for k in range(n_dp):
            total[k] = scaled[k * shard : (k + 1) * shard].astype(LOW)
        for block in range(line):
            cross_send[MIX][block] = total[block * 2 + 1 - side]
        cross(far_end, [MIX])
        cross(far_end - 1, [MIX])
        vec_mine[...] = held["vec_part"][...]
        flat = jnp.concatenate(
            [gain_grad, shift_grad, jnp.zeros((width, 6), F32)], axis=1
        ).T
        vec_mine[0:2] = flat[0:2]
        vec_mine[8:12] = units_rows_back(held["bias_own"][...], tensor, n_dp) + units_rows_back(
            held["bias_far"][...], far_row, n_dp
        )
        vec_lane = lax.broadcasted_iota(jnp.int32, (1, width), 1)
        in_part = (vec_lane >= tensor * (NH * HD)) & (vec_lane < (tensor + 1) * (NH * HD))
        for row, low in ((2, 0), (3, 2 * WIDE)):
            line_up = jnp.concatenate([columns[:, low : low + WIDE]] + [columns[:, 0:WIDE]] * 2, axis=1)
            placed = jnp.zeros((1, width), F32)
            for t in range(4):
                shifted = pltpu.roll(line_up, t * NH * HD, 1)
                placed = jnp.where(tensor == t, shifted, placed)
            vec_mine[row : row + 1] = jnp.where(in_part, placed, 0.0)
        vec_made = [
            copies.start(vec_mine, vec_land.at[i], device)
            for i, device in enumerate((at.mate, at.far, at.corner))
        ]
        for distance in range(far_end - 2, 0, -1):
            handle_all(distance, (FC, PROJ))
        send_far(1)
        for copy in vec_made:
            copy.wait_recv()
        send_far(1)
        vec_sum = vec_mine[...] + vec_land[0] + vec_land[1] + vec_land[2]
        for k in range(n_dp):
            vec_near[k] = pltpu.roll(vec_sum, (width - k * shard) % width, 1)[:, 0:128]
        for block in range(line):
            cross_send[VEC][block] = vec_near[block * 2 + 1 - side]
        cross(far_end, [VEC])
        cross(far_end - 1, [VEC])
        send_far(8)
        live = ends_of(lengths_ref)[-1]
        stays = []

        def close_rows(i):
            if i == 0:
                for name in ("hidden", "grad_middle", "middle", "positions"):
                    loads[name].wait()
                last_copy.wait_recv()
                mate_own.wait_recv()
            far_made[2 * i].wait_recv()
            far_made[2 * i + 1].wait_recv()
            span = pl.ds(i * part_rows, part_rows)
            ids = tensor * rows + i * part_rows + lax.broadcasted_iota(
                jnp.int32, (part_rows, 1), 0
            )
            final = (
                held["middle"][span]
                + held["last"][0, span].astype(F32)
                + last_land[span].astype(F32)
                + held["vec_all"][7:8]
            )
            block_kept[span] = jnp.where(ids < live, final, 0.0).astype(LOW)
            grad = (
                part[tensor, span].astype(F32)
                + mate_land[0, span].astype(F32)
                + far_land[span].astype(F32)
            )
            normed, inverse = normalize(held["hidden"][span].astype(F32))
            grad = held["grad_middle"][span] + norm_back(
                normed, inverse, grad, held["vec_all"][0:1]
            )
            for w in range(part_rows // window):
                index = i * (part_rows // window) + w
                here = (
                    lax.broadcasted_iota(jnp.int32, (window, 1), 0)
                    == held["positions"][index : index + 1, 0:1] - index * window
                )
                piece = grad[w * window : (w + 1) * window]
                tokens_kept[pl.ds(index * window, window)] = jnp.where(here, 0.0, piece)
                thoughts_kept[index : index + 1] = jnp.sum(
                    jnp.where(here, piece, 0.0), axis=0, keepdims=True
                )
            moves = [(tokens_kept.at[span], tokens_out.at[span])]
            moves.append((block_kept.at[span], block_out.at[span]))
            if i == 3:
                moves.append((thoughts_kept, thoughts_out))
            for kept_ref, out_ref in moves:
                stays.append(
                    pltpu.make_async_copy(kept_ref, out_ref, local.at[len(kept) + len(stays)])
                )
                stays[-1].start()

        done = 0
        for distance in range(far_end, 0, -1):
            handle_all(distance, (MIX, VEC))
            if distance >= 2:
                cross(distance - 2, (MIX, VEC))
            if distance <= 3:
                close_rows(done)
                done += 1
        for i in range(done, 4):
            close_rows(i)
        for i in (FC, PROJ, MIX):
            close(i, out[i])
        close(VEC, vec_out)
        copies.finish()
        for copy in stays:
            copy.wait()

    f32 = lambda *shape: jax.ShapeDtypeStruct(shape, F32)
    outputs = (
        f32(shard, width), f32(shard, width), f32(shard, width), f32(VEC_ROWS, 128),
        f32(rows, width), f32(latents, width), jax.ShapeDtypeStruct((rows, width), LOW),
    )
    scratch = [pltpu.VMEM(arrays[name].shape, arrays[name].dtype) for name in kept]
    for number, wide in ((line, 1), (line, 1), (last, 3), (last, 3)):
        scratch += [pltpu.VMEM((number, shard, width), LOW)] * wide
        scratch.append(pltpu.VMEM((number, VEC_ROWS, 128), F32))
    scratch += [
        pltpu.VMEM((4, rows, width), LOW),
        pltpu.VMEM((2, rows, width), LOW),
        pltpu.VMEM((rows, width), LOW),
        pltpu.VMEM((rows, width), LOW),
        pltpu.VMEM((rows, width), LOW),
        pltpu.VMEM((n_dp, shard, width), LOW),
        pltpu.VMEM((VEC_ROWS, width), F32),
        pltpu.VMEM((3, VEC_ROWS, width), F32),
        pltpu.VMEM((n_dp, VEC_ROWS, 128), F32),
        pltpu.VMEM((width, width), F32),
        pltpu.VMEM((1, width), F32),
        pltpu.VMEM(arrays["out_far"].shape, LOW),
        pltpu.VMEM((rows, width), F32),
        pltpu.VMEM((latents, width), F32),
        pltpu.VMEM((rows, width), LOW),
    ]
    return comm_call(
        kernel,
        "finish_grads",
        outputs,
        (lengths, *arrays.values()),
        [SM] + [ANY] * len(names),
        (VM,) * 4 + (ANY,) * 3,
        (last + 1) * 2 + last * 4 + 1 + 2 + 8 + 3 + 1,
        cid,
        scratch=scratch,
        local=len(kept) + 9,
    )


def unit_kernel(add, line, bias_row, lengths_ref, *refs):
    refs = list(refs)
    rows_ref, grad_own, grad_mate = refs[:3]
    pieces, vec_ref = refs[3:7], refs[7]
    refs = refs[8:]
    if add:
        last_in, two_in = refs[:2]
        refs = refs[2:]
    last_ref, two_ref, fc_near, fc_side, proj_near, proj_side, bias_grad_ref = refs[:7]
    fc_all, proj_all, fc_sum, proj_sum = refs[7:]
    step = pl.program_id(0)
    side, tensor = lax.axis_index("dp") % 2, lax.axis_index("tensor")
    live = ends_of(lengths_ref)[-1]

    @pl.when(step == 0)
    def _():
        for full, near, across in ((fc_all, *pieces[:2]), (proj_all, *pieces[2:])):
            for i in range(line):
                full[2 * i + side] = near[i]
                full[2 * i + 1 - side] = across[i]
        fc_sum[...] = jnp.zeros_like(fc_sum)
        proj_sum[...] = jnp.zeros_like(proj_sum)
        bias_grad_ref[...] = jnp.zeros_like(bias_grad_ref)

    count, width = rows_ref.shape
    half = pl.num_programs(0) // 2
    block = jnp.where(step < half, tensor, tensor + 1 - 2 * (tensor % 2))
    first = block * (half * count) + (step % half) * count
    alive = first + lax.broadcasted_iota(jnp.int32, (count, 1), 0) < live
    rows = rows_ref[...]
    grad = jnp.where(step < half, grad_own[...], grad_mate[...])
    grad = jnp.where(alive, grad, jnp.zeros_like(grad))
    fc = fc_all[...].reshape(width, -1)
    proj = proj_all[...].reshape(width, -1)
    inner = nn(rows, fc) + vec_ref[bias_row : bias_row + 1]
    square = inner * inner
    bend = jnp.tanh(GELU_SCALE * inner * (1.0 + GELU_CUBE * square))
    half = 0.5 * (1.0 + bend)
    activated = (inner * half).astype(LOW)
    slope = half + 0.5 * inner * (1.0 - bend * bend) * GELU_SCALE * (1.0 + 3.0 * GELU_CUBE * square)
    grad_inner = (nn(grad, proj) * slope).astype(LOW)
    last = nt(activated, proj)
    two = nt(grad_inner, fc)
    if add:
        last, two = last + last_in[...], two + two_in[...]
    last_ref[...] = last.astype(last_ref.dtype)
    two_ref[...] = two.astype(two_ref.dtype)
    fc_sum[...] += tn(rows, grad_inner)
    proj_sum[...] += tn(grad, activated)
    bias_grad_ref[...] += jnp.sum(grad_inner.astype(F32), axis=0, keepdims=True)

    @pl.when(step == pl.num_programs(0) - 1)
    def _():
        shard = fc_near.shape[1]
        for sums, near, across in ((fc_sum, fc_near, fc_side), (proj_sum, proj_near, proj_side)):
            for i in range(line):
                even = sums[2 * i * shard : (2 * i + 1) * shard].astype(LOW)
                odd = sums[(2 * i + 1) * shard : (2 * i + 2) * shard].astype(LOW)
                near[i] = jnp.where(side == 0, even, odd)
                across[i] = jnp.where(side == 0, odd, even)


def units_both_ways(lengths, rows, grad, mate_grad, pieces, vec_all, bias_row, before):
    count, width = rows.shape
    line, shard, units = pieces[0].shape
    half = count // ROW_TILE // 2
    tile = pl.BlockSpec((ROW_TILE, width), lambda i: (i, 0))
    fixed = lambda shape: pl.BlockSpec(shape, lambda i: (0,) * len(shape))
    add = before is not None
    kind = LOW if add else F32
    return pl.pallas_call(
        functools.partial(unit_kernel, add, line, bias_row),
        grid=(count // ROW_TILE,),
        out_shape=(
            jax.ShapeDtypeStruct((count, width), kind),
            jax.ShapeDtypeStruct((count, width), kind),
        )
        + (jax.ShapeDtypeStruct((line, shard, units), LOW),) * 4
        + (jax.ShapeDtypeStruct((1, units), F32),        ),
        in_specs=[
            SM,
            tile,
            pl.BlockSpec((ROW_TILE, width), lambda i: (jnp.minimum(i, half - 1), 0)),
            pl.BlockSpec((ROW_TILE, width), lambda i: (jnp.maximum(i - half, 0), 0)),
        ]
        + [fixed((line, shard, units))] * 4
        + [fixed(vec_all.shape)]
        + [tile] * (2 if add else 0),
        out_specs=(tile, tile) + (fixed((line, shard, units)),) * 4 + (fixed((1, units)),),
        scratch_shapes=[pltpu.VMEM((2 * line, shard, units), LOW)] * 2
        + [pltpu.VMEM((width, units), F32)] * 2,
        compiler_params=pltpu.CompilerParams(
            dimension_semantics=("arbitrary",), vmem_limit_bytes=VMEM_LIMIT
        ),
        cost_estimate=pl.CostEstimate(
            flops=12 * count * width * units,
            bytes_accessed=24 * count * width,
            transcendentals=count * units,
        ),
        name="units_second" if add else "units_first",
    )(lengths, rows, grad, mate_grad, *pieces, vec_all, *(before or ()))


def split_grads(mix_grad, vec, through, share):
    shard, width = mix_grad.shape
    head_width = NH * HD
    count = len(through)

    def kernel(mix_ref, vec_ref, *refs):
        given, (qkv_out, out_out), refs = refs[:count], refs[count : count + 2], refs[count + 2 :]
        small, passed, held, sems = refs[:8], refs[8 : 8 + count], refs[8 + count : -1], refs[-1]
        ins = [pltpu.make_async_copy(given[i], held[i], sems.at[i]) for i in range(count)]
        outs = [
            pltpu.make_async_copy(held[i], passed[i], sems.at[count + i]) for i in range(count)
        ]
        for copy in ins:
            copy.start()
        for i in range(count):
            ins[i].wait()
            outs[i].start()
        tensor = lax.axis_index("tensor")
        turned = mix_ref[...].T
        pieces = []
        for h in range(NH):
            for part in range(3):
                low = part * WIDE + h * HD
                pieces.append(turned[low : low + HD])
        qkv_out[...] = jnp.concatenate(pieces, axis=0).T
        for part in range(3):
            low = part * WIDE + head_width
            out_out[part * HD : (part + 1) * HD] = turned[low : low + HD]
        rows = vec_ref[0:8]
        moved = rows
        for i in range(1, 4):
            moved = jnp.where(tensor == i, pltpu.roll(rows, 128 - i * share, 1), moved)
        for i, row in enumerate((0, 1, 4, 5, 6, 7)):
            small[i][...] = moved[row : row + 1, 0:share]
        small[6][...] = moved[2:4, 0:share]
        small[7][...] = vec_ref[pl.ds(8 + tensor, 1)][:, 0:shard]
        for copy in outs:
            copy.wait()

    f32 = lambda *shape: jax.ShapeDtypeStruct(shape, F32)
    return pl.pallas_call(
        kernel,
        out_shape=(f32(shard, 3 * head_width), f32(head_width, shard))
        + (f32(1, share),) * 6
        + (f32(2, share), f32(1, shard))
        + tuple(jax.ShapeDtypeStruct(x.shape, x.dtype) for x in through),
        in_specs=[VM] * 2 + [ANY] * count,
        out_specs=(VM,) * 10 + (ANY,) * count,
        scratch_shapes=[pltpu.VMEM(x.shape, x.dtype) for x in through]
        + [pltpu.SemaphoreType.DMA((2 * count,))],
        compiler_params=pltpu.CompilerParams(vmem_limit_bytes=VMEM_LIMIT),
        name="split_grads",
    )(mix_grad, vec, *through)


def by_tensor(row, step, index):
    moved = row
    for i in range(1, 4):
        moved = jnp.where(index == i, pltpu.roll(row, (i * step) % row.shape[1], 1), moved)
    return moved


def units_row(rows, block, n_dp):
    width = rows.shape[1]
    shard, step = width // n_dp, n_dp // 4
    lane = lax.broadcasted_iota(jnp.int32, (1, width), 1) // shard
    base = by_tensor(rows, width - step * shard, block)
    total = jnp.zeros((1, width), F32)
    for j in range(n_dp):
        moved = pltpu.roll(base[j % 4 : j % 4 + 1], (j - j // 4) * shard, 1)
        total = jnp.where(lane == j, moved, total)
    return total


def units_rows_back(row, block, n_dp):
    width = row.shape[1]
    shard, step = width // n_dp, n_dp // 4
    lane = lax.broadcasted_iota(jnp.int32, (1, width), 1) // shard
    rows = [jnp.zeros((1, width), F32) for _ in range(4)]
    for j in range(n_dp):
        moved = pltpu.roll(row, (width - (j - j // 4) * shard) % width, 1)
        rows[j % 4] = jnp.where(lane == j // 4, moved, rows[j % 4])
    return by_tensor(jnp.concatenate(rows, axis=0), step * shard, block)


def normalize(values):
    center = jnp.mean(values, axis=-1, keepdims=True)
    offset = values - center
    spread = jnp.mean(offset * offset, axis=-1, keepdims=True)
    inverse = lax.rsqrt(spread + EPSILON)
    return offset * inverse, inverse


def norm_back(normed, inverse, grad, gain):
    scaled = grad * gain
    center = jnp.mean(scaled, axis=-1, keepdims=True)
    along = jnp.mean(scaled * normed, axis=-1, keepdims=True)
    return inverse * (scaled - center - normed * along)


def product(equation, left, right):
    return jnp.einsum(equation, left, right, preferred_element_type=F32)


def per_device(
    tokens,
    thoughts,
    positions,
    lengths,
    attn_norm_gain,
    attn_norm_shift,
    qkv_weight,
    qv_bias,
    attn_out_weight,
    attn_out_bias,
    mlp_norm_gain,
    mlp_norm_shift,
    fc_weight,
    fc_bias,
    proj_weight,
    proj_bias,
    cotangent,
):
    n_dp = lax.axis_size("dp")
    n_tensor = lax.axis_size("tensor")
    rows, width = tokens.shape
    slots = rows * n_tensor
    swap_far = [(i, (i + 2) % n_tensor) for i in range(n_tensor)]

    share = width // (n_dp * n_tensor)
    small = [
        attn_norm_gain[None], attn_norm_shift[None], qv_bias, attn_out_bias[None],
        mlp_norm_gain[None], mlp_norm_shift[None], proj_bias[None], fc_bias[None],
    ]
    (
        group_low, mixed, mix_all, fc_near, fc_side, fc_far_near, proj_near, mate_grad, out_own,
        hidden, vec_all, places,
    ) = gather_inputs(
        tokens, thoughts, positions, cotangent, fc_weight, proj_weight.T, qkv_weight,
        attn_out_weight, small, n_dp,
    )
    mixed = mixed.reshape(slots, -1)
    swap_side = [(i, i + 1 - 2 * (i % 2)) for i in range(n_dp)]
    out_far = lax.ppermute(out_own, "tensor", swap_far)
    proj_far_near = lax.ppermute(proj_near, "tensor", swap_far)
    fc_far_side = lax.ppermute(fc_far_near, "dp", swap_side)
    attended, stats = attend(lengths, mixed)
    sent, out_far, proj_far_near, fc_far_side = lax.optimization_barrier(
        (attended, out_far, proj_far_near, fc_far_side)
    )
    proj_far_side = lax.ppermute(proj_far_near, "dp", swap_side)
    both, middle, chip_two = after_attention(
        sent, out_own, out_far, hidden, vec_all, n_dp, 1
    )
    chip_two, proj_far_side, proj_sent = lax.optimization_barrier(
        (chip_two, proj_far_side, proj_near)
    )
    proj_side = lax.ppermute(proj_sent, "dp", swap_side)
    chip_two = chip_two.reshape(2 * rows, width)

    first = units_both_ways(
        lengths, chip_two, cotangent, mate_grad,
        (fc_far_near, fc_far_side, proj_far_near, proj_far_side), vec_all, 13, None,
    )
    far_fc_near, far_fc_side, far_proj_near, far_proj_side, far_fc_bias = first[2:]
    proj_side_far = lax.ppermute(far_proj_side, "tensor", swap_far)
    fc_far_side_in = lax.ppermute(far_fc_side, "dp", swap_side)
    second = units_both_ways(
        lengths, chip_two, cotangent, mate_grad, (fc_near, fc_side, proj_near, proj_side), vec_all, 12,
        first[:2],
    )
    last_part, grad_two_part, fc_near_grad, fc_side_grad, proj_near_grad, proj_side_grad = second[:6]
    fc_near_side_in = lax.ppermute(fc_side_grad, "dp", swap_side)
    grad_heads, grad_middle, grad_out, far_out, vec_part = before_attention_back(
        lengths, grad_two_part.reshape(2, rows, width), middle, cotangent, both, out_own, out_far,
        vec_all, n_dp, 2,
    )
    fc_cross = far_fc_near + fc_far_side_in
    proj_cross = proj_side_grad + proj_side_far
    grad_heads, fc_cross, proj_cross, far_proj_near = lax.optimization_barrier(
        (grad_heads, fc_cross, proj_cross, far_proj_near)
    )
    fc_cross = lax.ppermute(fc_cross, "tensor", swap_far)
    proj_cross = lax.ppermute(proj_cross, "dp", swap_side)
    proj_near_far = lax.ppermute(far_proj_near, "tensor", swap_far)
    last_low = last_part.reshape(2, rows, width)

    grad_mixed = attend_back(lengths, mixed, attended, stats, grad_heads)
    arrays = {
        "fc_near": fc_near_grad, "fc_near_side": fc_near_side_in, "fc_cross": fc_cross,
        "proj_near": proj_near_grad, "proj_near_far": proj_near_far, "proj_cross": proj_cross,
        "grad_mixed": grad_mixed.reshape(n_tensor, rows, width), "mix": mix_all,
        "last": last_low, "group": group_low,
        "out_own": grad_out, "out_far": far_out,
        "vec_all": vec_all, "vec_part": vec_part, "bias_own": second[6], "bias_far": far_fc_bias,
        "hidden": hidden, "grad_middle": grad_middle, "middle": middle, "positions": places,
    }
    fc_grad, proj_grad, mix_grad, vec, grad_tokens, grad_thoughts, block_out = finish_grads(
        lengths, arrays, n_dp, 8
    )
    parts = split_grads(
        mix_grad, vec, (fc_grad, proj_grad, grad_tokens, grad_thoughts, block_out), share
    )
    qkv_grad, out_grad = parts[:2]
    gain_one, shift_one, out_bias, gain_two, shift_two, last_bias = [p[0] for p in parts[2:8]]
    query_value, hidden_bias = parts[8], parts[9][0]
    fc_grad, proj_grad, grad_tokens, grad_thoughts, block_out = parts[10:]
    return (
        block_out,
        grad_tokens,
        grad_thoughts,
        gain_one,
        shift_one,
        qkv_grad,
        query_value,
        out_grad,
        out_bias,
        gain_two,
        shift_two,
        fc_grad,
        hidden_bias,
        proj_grad.T,
        last_bias,
    )


def solution(mesh):
    rows = P(("dp", "tensor"), None)
    line = P(("dp", "tensor"))
    in_specs = (
        rows, rows, line, P("dp", None), line, line, P("dp", "tensor"),
        P(None, ("dp", "tensor")), P("tensor", "dp"), line, line, line,
        P("dp", "tensor"), line, P("tensor", "dp"), line, rows,
    )
    out_specs = (
        rows, rows, rows, line, line, P("dp", "tensor"), P(None, ("dp", "tensor")),
        P("tensor", "dp"), line, line, line, P("dp", "tensor"), line, P("tensor", "dp"), line,
    )
    return jax.shard_map(
        per_device, mesh=mesh, in_specs=in_specs, out_specs=out_specs, check_vma=False
    )
```

```python
import functools
import math

import jax
import jax.numpy as jnp
from jax import lax
from jax.experimental import pallas as pl
from jax.experimental.pallas import tpu as pltpu
from jax.sharding import PartitionSpec as P

H = 12
HD = 64
FF = 3072
SEQ_DEV = 3
EPSILON = 1e-05
MASKED = -1e30
NH = 3
SLABS = 2
WIDE = SLABS * 128
BQ = 512
BK = 512
VEC_ROWS = 16
VMEM_LIMIT = 67043328
ROW_TILE = 256
GELU_SCALE = math.sqrt(2.0 / math.pi)
GELU_CUBE = 0.044715
MESH = pl.DeviceIdType.MESH
ANY = pl.BlockSpec(memory_space=pltpu.HBM)
VM = pl.BlockSpec(memory_space=pltpu.VMEM)
SM = pl.BlockSpec(memory_space=pltpu.SMEM)
LOW = jnp.bfloat16
F32 = jnp.float32


def nn(a, b):
    return lax.dot_general(a, b, (((1,), (0,)), ((), ())), preferred_element_type=jnp.float32)


def nt(a, b):
    return lax.dot_general(a, b, (((1,), (1,)), ((), ())), preferred_element_type=jnp.float32)


def tn(a, b):
    return lax.dot_general(a, b, (((0,), (0,)), ((), ())), preferred_element_type=jnp.float32)


def head_rows(slab, head):
    half = slab[(head % 2) * HD : (head % 2 + 1) * HD]
    zero = jnp.zeros_like(half)
    return jnp.concatenate([half, zero] if head % 2 == 0 else [zero, half], axis=0)


def ends_of(lengths_ref):
    ends = [lengths_ref[0, 0]]
    for i in range(1, SEQ_DEV):
        ends.append(ends[-1] + lengths_ref[0, i])
    return ends


def segment_start(ends, slots):
    start = jnp.zeros_like(slots)
    for i in range(SEQ_DEV):
        start = jnp.where(slots >= ends[i], ends[i], start)
    return start


def segment_stop(ends, slot, slots):
    stop = slots
    for i in reversed(range(SEQ_DEV)):
        stop = jnp.where(slot < ends[i], ends[i], stop)
    return stop


def attend_kernel(
    lengths_ref, mixed_in, out_ref, stat_ref, mixed_ref, qt_ref, vt_ref, sems
):
    tokens = mixed_ref.shape[0]
    ends = ends_of(lengths_ref)
    count = (ends[-1] + BQ - 1) // BQ
    half = BQ // 2

    def load(block):
        rows = pl.ds(pl.multiple_of(block * BQ, BQ), BQ)
        return pltpu.make_async_copy(mixed_in.at[rows], mixed_ref.at[rows], sems.at[block])

    for block in range(tokens // BQ):
        load(block).start()

    def step(rows, keys, columns, queries, first, causal, state):
        size = queries[0].shape[1]
        slots = first + lax.broadcasted_iota(jnp.int32, (1, size), 1)
        start = segment_start(ends, slots)
        key_ids = rows + lax.broadcasted_iota(jnp.int32, (keys, size), 0)
        allowed = key_ids >= start
        if causal:
            allowed = allowed & (key_ids <= slots)
        span = pl.ds(rows, keys)
        result = []
        for h in range(NH):
            peak, total, acc = state[h]
            low = WIDE + (h // 2) * 128
            scores = nn(mixed_ref[span, low : low + 128], queries[h])
            scores = jnp.where(allowed, scores, MASKED)
            fresh = jnp.maximum(peak, jnp.max(scores, axis=0, keepdims=True))
            weight = jnp.exp(scores - fresh)
            decay = jnp.exp(peak - fresh)
            total = total * decay + jnp.sum(weight, axis=0, keepdims=True)
            values = vt_ref[h * HD : (h + 1) * HD, span]
            acc = acc * decay + nn(values, weight.astype(jnp.bfloat16))
            result.append((fresh, total, acc))
        return tuple(result)

    def query_block(block, carry):
        first = pl.multiple_of(block * BQ, BQ)
        columns = pl.ds(first, BQ)
        load(block).wait()
        for slab in range(SLABS):
            low = slab * 128
            qt_ref[low : low + 128] = (mixed_ref[columns, low : low + 128] * HD ** (-0.5)).T
            vt_ref[low : low + 128, columns] = mixed_ref[
                columns, 2 * WIDE + low : 2 * WIDE + low + 128
            ].T
        queries = [head_rows(qt_ref[(h // 2) * 128 : (h // 2 + 1) * 128], h) for h in range(NH)]

        def key_block(key, state):
            return step(pl.multiple_of(key * BK, BK), BK, columns, queries, first, False, state)

        empty = tuple(
            (
                jnp.full((1, BQ), MASKED, jnp.float32),
                jnp.zeros((1, BQ), jnp.float32),
                jnp.zeros((HD, BQ), jnp.float32),
            )
            for _ in range(NH)
        )
        state = lax.fori_loop(segment_start(ends, first) // BK, block, key_block, empty)
        for side, keys in ((0, half), (1, BQ)):
            piece = slice(side * half, (side + 1) * half)
            final = step(
                first, keys, columns, [q[:, piece] for q in queries], first + side * half, True,
                tuple(tuple(x[:, piece] for x in one) for one in state),
            )
            for h in range(NH):
                peak, total, acc = final[h]
                place_here = pl.ds(pl.multiple_of(first + side * half, half), half)
                out_ref[h * HD : (h + 1) * HD, place_here] = (acc / total).astype(jnp.bfloat16)
                stat_ref[h : h + 1, place_here] = peak + jnp.log(total)
        return carry

    lax.fori_loop(0, count, query_block, 0)

    def padded_block(block, carry):
        load(block).wait()
        columns = pl.ds(pl.multiple_of(block * BQ, BQ), BQ)
        out_ref[:, columns] = jnp.zeros((out_ref.shape[0], BQ), jnp.bfloat16)
        return carry

    lax.fori_loop(count, tokens // BQ, padded_block, 0)


def attend(lengths, mixed):
    tokens = mixed.shape[0]
    vm = pl.BlockSpec(memory_space=pltpu.VMEM)
    return pl.pallas_call(
        attend_kernel,
        out_shape=(
            jax.ShapeDtypeStruct((NH * HD, tokens), jnp.bfloat16),
            jax.ShapeDtypeStruct((8, tokens), jnp.float32),
        ),
        in_specs=[pl.BlockSpec(memory_space=pltpu.SMEM), pl.BlockSpec(memory_space=pltpu.HBM)],
        out_specs=(vm, vm),
        scratch_shapes=[
            pltpu.VMEM(mixed.shape, mixed.dtype),
            pltpu.VMEM((WIDE, BQ), jnp.bfloat16),
            pltpu.VMEM((WIDE, tokens), jnp.bfloat16),
            pltpu.SemaphoreType.DMA((tokens // BQ,)),
        ],
        compiler_params=pltpu.CompilerParams(vmem_limit_bytes=VMEM_LIMIT),
        cost_estimate=pl.CostEstimate(
            flops=8 * tokens * tokens * NH * HD,
            bytes_accessed=16 * tokens * WIDE,
            transcendentals=tokens * tokens,
        ),
        name="attend",
    )(lengths, mixed)


def attend_back_kernel(
    lengths_ref, mixed_in, out_in, stat_ref, gradt_in,
    gmixed_out, mixed_ref, out_ref, gradt_ref, gmixed_ref, qt_ref, kt_ref, grad_ref, delta_ref,
    dqt_ref, sems, out_sems
):
    tokens = mixed_ref.shape[0]
    blocks = tokens // BQ
    ends = ends_of(lengths_ref)
    count = (ends[-1] + BK - 1) // BK
    half = BQ // 2

    def loads(block):
        rows = pl.ds(pl.multiple_of(block * BQ, BQ), BQ)
        return (
            pltpu.make_async_copy(mixed_in.at[rows], mixed_ref.at[rows], sems.at[0, block]),
            pltpu.make_async_copy(out_in.at[:, rows], out_ref.at[:, rows], sems.at[1, block]),
            pltpu.make_async_copy(gradt_in.at[:, rows], gradt_ref.at[:, rows], sems.at[2, block]),
        )

    def leave(block, part):
        rows = pl.ds(pl.multiple_of(block * BQ, BQ), BQ)
        lanes = pl.ds(0, WIDE) if part == 0 else pl.ds(WIDE, 2 * WIDE)
        return pltpu.make_async_copy(
            gmixed_ref.at[rows, lanes], gmixed_out.at[rows, lanes], out_sems.at[part, block]
        )

    for block in reversed(range(blocks)):
        for copy in loads(block):
            copy.start()
    dqt_ref[...] = jnp.zeros_like(dqt_ref)

    def prepare_block(block):
        rows = pl.ds(pl.multiple_of(block * BQ, BQ), BQ)
        for slab in range(SLABS):
            low = slab * 128
            qt_ref[low : low + 128, rows] = (
                mixed_ref[rows, low : low + 128] * HD ** (-0.5)
            ).T
            kt_ref[low : low + 128, rows] = mixed_ref[rows, WIDE + low : WIDE + low + 128].T
        grad_ref[rows, 0:128] = gradt_ref[0:128, rows].T
        grad_ref[rows, 128:256] = jnp.concatenate(
            [gradt_ref[128:192, rows], jnp.zeros((64, BQ), jnp.bfloat16)], axis=0
        ).T
        for h in range(NH):
            product = gradt_ref[h * HD : (h + 1) * HD, rows].astype(jnp.float32) * out_ref[
                h * HD : (h + 1) * HD, rows
            ].astype(jnp.float32)
            delta_ref[h : h + 1, rows] = jnp.sum(product, axis=0, keepdims=True)

    def terms(base, keys, first, size, causal):
        rows, columns = pl.ds(base, keys), pl.ds(first, size)
        slots = first + lax.broadcasted_iota(jnp.int32, (1, size), 1)
        key_ids = base + lax.broadcasted_iota(jnp.int32, (keys, size), 0)
        allowed = key_ids >= segment_start(ends, slots)
        if causal:
            allowed = allowed & (key_ids <= slots)
        lane = lax.broadcasted_iota(jnp.int32, (size, 128), 1)
        grad_keys, grad_values = [None] * SLABS, [None] * SLABS
        for h in range(NH):
            slab = h // 2
            low, high = slab * 128, slab * 128 + 128
            queries = head_rows(qt_ref[low:high, columns], h)
            scores = nn(mixed_ref[rows, WIDE + low : WIDE + high], queries)
            probs = jnp.where(allowed, jnp.exp(scores - stat_ref[h : h + 1, columns]), 0.0)
            keep = (lane // HD) == (h % 2)
            value = nn(probs.astype(jnp.bfloat16), jnp.where(keep, grad_ref[columns, low:high], 0.0))
            if h == NH - 1 and NH % 2 == 1:
                grad_rows = jnp.concatenate(
                    [gradt_ref[h * HD : (h + 1) * HD, columns], jnp.zeros((HD, size), jnp.bfloat16)],
                    axis=0,
                )
            else:
                grad_rows = head_rows(gradt_ref[low:high, columns], h)
            grad_probs = nn(mixed_ref[rows, 2 * WIDE + low : 2 * WIDE + high], grad_rows)
            grad_scores = (probs * (grad_probs - delta_ref[h : h + 1, columns])).astype(
                jnp.bfloat16
            )
            key_term = nn(grad_scores, jnp.where(keep, mixed_ref[columns, low:high], 0.0))
            grad_values[slab] = value if grad_values[slab] is None else grad_values[slab] + value
            grad_keys[slab] = key_term if grad_keys[slab] is None else grad_keys[slab] + key_term
            dqt_ref[h * HD : (h + 1) * HD, columns] += nn(
                kt_ref[h * HD : (h + 1) * HD, rows], grad_scores
            )
        return grad_keys + grad_values

    def key_block(turn, carry):
        key = count - 1 - turn
        for copy in loads(key):
            copy.wait()
        prepare_block(key)
        base = pl.multiple_of(key * BK, BK)
        rows = pl.ds(base, BK)
        upper = terms(base, half, base, BQ, True)
        lower = terms(pl.multiple_of(base + half, half), half, pl.multiple_of(base + half, half), half, True)
        state = tuple(jnp.concatenate([a, b], axis=0) for a, b in zip(upper, lower))

        def query_block(block, state):
            fresh = terms(base, BK, pl.multiple_of(block * BQ, BQ), BQ, False)
            return tuple(a + b for a, b in zip(state, fresh))

        stop = jnp.minimum(segment_stop(ends, base + BK - 1, tokens), ends[-1])
        state = lax.fori_loop(key + 1, (stop - 1) // BQ + 1, query_block, state)
        for slab in range(SLABS):
            low = slab * 128
            gmixed_ref[rows, WIDE + low : WIDE + low + 128] = (
                state[slab] * HD ** (-0.5)
            ).astype(jnp.bfloat16)
            gmixed_ref[rows, 2 * WIDE + low : 2 * WIDE + low + 128] = state[SLABS + slab].astype(
                jnp.bfloat16
            )
        leave(key, 1).start()
        return carry

    def padded_block(key, carry):
        for copy in loads(key):
            copy.wait()
        rows = pl.ds(pl.multiple_of(key * BK, BK), BK)
        gmixed_ref[rows, WIDE:] = jnp.zeros((BK, 2 * WIDE), jnp.bfloat16)
        leave(key, 1).start()
        return carry

    lax.fori_loop(count, blocks, padded_block, 0)
    lax.fori_loop(0, count, key_block, 0)
    for block in range(blocks):
        rows = pl.ds(block * BQ, BQ)
        for slab in range(SLABS):
            low = slab * 128
            gmixed_ref[rows, low : low + 128] = (
                (dqt_ref[low : low + 128, rows] * HD ** (-0.5)).T.astype(jnp.bfloat16)
            )
        leave(block, 0).start()
    for block in range(blocks):
        leave(block, 0).wait()
        leave(block, 1).wait()


def attend_back(lengths, mixed, out, stat, gradt):
    tokens = mixed.shape[0]
    vm = pl.BlockSpec(memory_space=pltpu.VMEM)
    hbm = pl.BlockSpec(memory_space=pltpu.HBM)
    return pl.pallas_call(
        attend_back_kernel,
        out_shape=jax.ShapeDtypeStruct((tokens, 3 * WIDE), jnp.bfloat16),
        in_specs=[pl.BlockSpec(memory_space=pltpu.SMEM), hbm, hbm, vm, hbm],
        out_specs=hbm,
        scratch_shapes=[
            pltpu.VMEM(mixed.shape, jnp.bfloat16),
            pltpu.VMEM(out.shape, jnp.bfloat16),
            pltpu.VMEM(gradt.shape, jnp.bfloat16),
            pltpu.VMEM(mixed.shape, jnp.bfloat16),
            pltpu.VMEM((WIDE, tokens), jnp.bfloat16),
            pltpu.VMEM((WIDE, tokens), jnp.bfloat16),
            pltpu.VMEM((tokens, WIDE), jnp.bfloat16),
            pltpu.VMEM((8, tokens), jnp.float32),
            pltpu.VMEM((WIDE, tokens), jnp.float32),
            pltpu.SemaphoreType.DMA((3, tokens // BQ)),
            pltpu.SemaphoreType.DMA((2, tokens // BQ)),
        ],
        compiler_params=pltpu.CompilerParams(vmem_limit_bytes=VMEM_LIMIT),
        cost_estimate=pl.CostEstimate(
            flops=20 * tokens * tokens * NH * HD,
            bytes_accessed=32 * tokens * WIDE,
            transcendentals=tokens * tokens,
        ),
        name="attend_back",
    )(lengths, mixed, out, stat, gradt)


class Copies:
    def __init__(self, send, recv):
        self.send, self.recv, self.made, self.started = send, recv, 0, []

    def plan(self, source, target, device):
        index = self.made
        self.made += 1
        return pltpu.make_async_remote_copy(
            src_ref=source,
            dst_ref=target,
            send_sem=self.send.at[index],
            recv_sem=self.recv.at[index],
            device_id=device,
            device_id_type=MESH,
        )

    def begin(self, copy, condition=None):
        self.started.append((copy, condition))
        when(condition, copy.start)

    def start(self, source, target, device):
        copy = self.plan(source, target, device)
        self.begin(copy)
        return copy

    def finish(self):
        for copy, condition in self.started:
            when(condition, copy.wait_send)


def when(condition, action):
    if condition is None:
        action()
    else:
        pl.when(condition)(action)


def greet(devices):
    barrier = pltpu.get_barrier_semaphore()
    for device, condition in devices:
        when(
            condition,
            lambda device=device: pl.semaphore_signal(
                barrier, inc=1, device_id=device, device_id_type=MESH
            ),
        )
    present = [1 if condition is None else condition.astype(jnp.int32) for _, condition in devices]
    pl.semaphore_wait(barrier, sum(present))


class Place:
    def __init__(self, line):
        self.dp = dp = lax.axis_index("dp")
        self.tensor = tensor = lax.axis_index("tensor")
        self.spot, self.side = spot, side = dp // 2, dp % 2
        self.chip, self.core = tensor // 2, tensor % 2
        self.has_up, self.has_down = spot + 1 < line, spot > 0
        self.up = (jnp.minimum(spot + 1, line - 1) * 2 + side, tensor)
        self.down = (jnp.maximum(spot - 1, 0) * 2 + side, tensor)
        self.across = (spot * 2 + 1 - side, tensor)
        self.mate = (dp, tensor + 1 - 2 * (tensor % 2))
        self.far = (dp, (tensor + 2) % 4)
        self.corner = (dp, 3 - tensor)

    def everyone(self):
        return [
            (self.mate, None), (self.far, None), (self.corner, None), (self.across, None),
            (self.up, self.has_up), (self.down, self.has_down),
        ]


def comm_call(kernel, name, outputs, inputs, in_specs, out_specs, copies, cid, scratch=(), local=1, limit=VMEM_LIMIT):
    return pl.pallas_call(
        kernel,
        out_shape=outputs,
        in_specs=in_specs,
        out_specs=out_specs,
        scratch_shapes=list(scratch)
        + [
            pltpu.SemaphoreType.DMA((copies,)),
            pltpu.SemaphoreType.DMA((copies,)),
            pltpu.SemaphoreType.DMA((local,)),
        ],
        compiler_params=pltpu.CompilerParams(
            collective_id=cid, has_side_effects=True, vmem_limit_bytes=limit
        ),
        name=name,
    )(*inputs)


def one_hot(rows, columns, shift, limit):
    lane = lax.broadcasted_iota(jnp.int32, (rows, columns), 0)
    spot = lax.broadcasted_iota(jnp.int32, (rows, columns), 1)
    return ((spot == lane + shift) & (lane < limit)).astype(LOW)


def gather_inputs(tokens, thoughts, positions, cotangent, fc, proj, qkv, out, vectors, n_dp):
    line = n_dp // 2
    hops = line - 1
    rows, width = tokens.shape
    latents = thoughts.shape[0]
    window = rows // latents
    shard = fc.shape[0]
    half_rows = rows // 2
    share = width // (n_dp * 4)

    def kernel(
        pos_ref, tokens_in, thoughts_in, cot_ref, fc_in, proj_in, qkv_in, out_in, *refs
    ):
        given = (fc_in, tokens_in, thoughts_in, proj_in, qkv_in, out_in) + refs[: len(vectors)]
        (
            normed_out, mixed_out, mix_out, fc_near, fc_side, fc_far, proj_near, cot_out, out_out,
            hidden_out, vec_out, pos_out,
            hidden_ref, mix_ref, vec_ref, tile,
            land, mix_land, tiles, tile_land, normed, mixed, out_turned,
            *held, arrive, send, recv, local,
        ) = refs[len(vectors) :]
        arrivals = [
            pltpu.make_async_copy(given[i], held[i], arrive.at[i]) for i in range(len(given))
        ]
        for copy in arrivals:
            copy.start()
        fc_ref, tokens_ref, thoughts_ref, proj_ref, qkv_ref, out_ref = held[:6]
        vec_refs = held[6:]
        at = Place(line)
        dp, tensor, spot, side = at.dp, at.tensor, at.spot, at.side
        mate_row, far_row, corner_row = at.mate[1], at.far[1], at.corner[1]
        greet(at.everyone())
        copies = Copies(send, recv)
        MIX, FC, PROJ, VEC = range(4)
        own = [mix_ref, fc_ref, proj_ref, tiles.at[dp]]

        def seat(item, position):
            if item == MIX:
                return mix_land.at[position * 2 + side]
            if item == FC:
                return fc_near.at[position]
            if item == PROJ:
                return proj_near.at[position]
            return tiles.at[position * 2 + side]

        def plan(item, hop):
            above, below = jnp.maximum(spot - hop, 0), jnp.minimum(spot + hop, line - 1)
            came_up = jnp.maximum(spot - 1 - hop, 0)
            came_down = jnp.minimum(spot + 1 + hop, line - 1)
            made = {
                "up": copies.plan(
                    own[item] if hop == 0 else seat(item, above), seat(item, above), at.up
                ),
                "down": copies.plan(
                    own[item] if hop == 0 else seat(item, below), seat(item, below), at.down
                ),
                "onward": [],
            }
            for position in (came_up, came_down):
                onward = []
                if item in (MIX, VEC):
                    onward.append(copies.plan(seat(item, position), seat(item, position), at.across))
                if item == FC:
                    onward.append(copies.plan(fc_near.at[position], fc_side.at[position], at.across))
                    onward.append(copies.plan(fc_near.at[position], fc_far.at[position], at.far))
                made["onward"].append(onward)
            return made

        plans = [[plan(item, hop) for hop in range(hops)] for item in range(4)]

        def launch(item):
            copies.begin(plans[item][0]["up"], at.has_up)
            copies.begin(plans[item][0]["down"], at.has_down)

        def handle(item, hop):
            made = plans[item][hop]
            for way, key, comes, goes in (
                (0, "up", spot - 1 - hop >= 0, at.has_up),
                (1, "down", spot + 1 + hop < line, at.has_down),
            ):
                when(comes, made[key].wait_recv)
                if hop + 1 < hops:
                    copies.begin(plans[item][hop + 1][key], comes & goes)
                for copy in made["onward"][way]:
                    copies.begin(copy, comes)

        def settle(item):
            for hop in range(hops):
                for way, comes in ((0, spot - 1 - hop >= 0), (1, spot + 1 + hop < line)):
                    for copy in plans[item][hop]["onward"][way]:
                        when(comes, copy.wait_recv)

        stays = []

        def stay(source, target):
            copy = pltpu.make_async_copy(source, target, local.at[len(stays)])
            copy.start()
            stays.append(copy)
            return copy

        parts = [pl.ds(0, half_rows), pl.ds(half_rows, half_rows)]
        arrivals[0].wait()
        launch(FC)
        fc_sides = [copies.start(fc_ref, fc_side.at[spot], at.across)]
        cot_made = copies.start(cot_ref, cot_out, at.mate)
        for copy in arrivals[6:]:
            copy.wait()
        tile[...] = jnp.zeros_like(tile)
        row = 0
        for ref in vec_refs:
            count, size = ref.shape
            tile[row : row + count, 0:size] = ref[...].astype(F32)
            row += count
        vec_ref[...] = tile[...].astype(LOW)
        vec_made = [
            copies.start(vec_ref, tile_land.at[i], device)
            for i, device in enumerate((at.mate, at.far, at.corner))
        ]
        arrivals[1].wait()
        arrivals[2].wait()
        pos_row = lax.broadcasted_iota(jnp.int32, (latents, 128), 0)
        places = jnp.zeros((latents, 128), jnp.int32)
        for w in range(latents):
            places = jnp.where(pos_row == w, pos_ref[w], places)
            span = pl.ds(w * window, window)
            here = lax.broadcasted_iota(jnp.int32, (window, 1), 0) == pos_ref[w] - w * window
            hidden_ref[span] = jnp.where(
                here, thoughts_ref[w : w + 1].astype(F32), tokens_ref[span].astype(F32)
            ).astype(LOW)
        pos_out[...] = places
        far_made = [
            copies.start(hidden_ref.at[part], land.at[2, part], at.far) for part in parts
        ]
        mate_made = copies.start(hidden_ref, land.at[1], at.mate)
        fc_sides.append(copies.start(fc_ref, fc_far.at[spot], at.far))
        for copy in arrivals[3:6]:
            copy.wait()
        turned = qkv_ref[...].astype(F32).T
        extra = out_ref[...].astype(F32)
        pieces = []
        for p in range(3):
            for h in range(NH):
                low = (h * 3 + p) * HD
                pieces.append(turned[low : low + HD])
            pieces.append(extra[p * HD : (p + 1) * HD])
        mix_ref[...] = jnp.concatenate(pieces, axis=0).T.astype(LOW)
        launch(MIX)
        mix_side = copies.start(mix_ref, mix_land.at[dp], at.across)
        stay(hidden_ref, hidden_out)
        stay(fc_ref, fc_near.at[spot])
        stay(proj_ref, proj_near.at[spot])
        mix_land[dp] = mix_ref[...]
        for copy in vec_made:
            copy.wait_recv()
        merged = jnp.zeros((VEC_ROWS, 128), F32)
        bias_rows = jnp.zeros((VEC_ROWS, 128), F32)
        row_ids = lax.broadcasted_iota(jnp.int32, (VEC_ROWS, 128), 0)
        for i, index in enumerate((tensor, mate_row, far_row, corner_row)):
            tile = vec_ref[...] if i == 0 else tile_land[i - 1]
            merged += nn(tile, one_hot(128, 128, index * share, share))
            bias_rows = jnp.where(row_ids == 8 + index, tile[8:9].astype(F32), bias_rows)
        tiles[dp] = jnp.where(row_ids < 8, merged, bias_rows).astype(LOW)
        launch(VEC)
        vec_side = copies.start(tiles.at[dp], tiles.at[dp], at.across)

        def norm_rows(source, index):
            @pl.loop(0, rows // 128)
            def _(i):
                span = pl.ds(pl.multiple_of(i * 128, 128), 128)
                normed[index, span] = normalize(source[span].astype(F32))[0].astype(LOW)

            stay(normed.at[index], normed_out.at[index])

        def relay(i):
            far_made[i].wait_recv()
            return copies.start(land.at[2, parts[i]], land.at[3, parts[i]], at.mate)

        def mix_rows(index):
            @pl.loop(0, rows // 256)
            def _(i):
                span = pl.ds(pl.multiple_of(i * 256, 256), 256)
                turned = normed[index, span].astype(F32) * whole[0:1] + whole[1:2]
                weight = mix_land[...].reshape(width, width)
                mixed[index, span] = (nn(turned.astype(LOW), weight) + bias).astype(LOW)

            stay(mixed.at[index], mixed_out.at[index])

        norm_rows(hidden_ref, tensor)
        relayed = []
        for step in range(hops + 2):
            for item, hop in ((MIX, step), (VEC, step), (FC, step - 1), (PROJ, step - 2)):
                if 0 <= hop < hops:
                    handle(item, hop)
            if step == 0:
                launch(PROJ)
                mate_made.wait_recv()
                norm_rows(land.at[1], mate_row)
                relayed.append(relay(0))
            if step == 1:
                relayed.append(relay(1))
                norm_rows(land.at[2], far_row)
            if step == hops:
                mix_side.wait_recv()
                vec_side.wait_recv()
                settle(MIX)
                settle(VEC)
                whole = jnp.zeros((VEC_ROWS, width), F32)
                for i in range(n_dp):
                    whole += nn(tiles[i], one_hot(128, width, i * shard, shard))
                vec_out[...] = whole
                for i, block in enumerate((tensor, far_row)):
                    vec_out[12 + i : 13 + i] = units_row(whole[8:12], block, n_dp)
                lane = lax.broadcasted_iota(jnp.int32, (width, WIDE), 0)
                column = lax.broadcasted_iota(jnp.int32, (width, WIDE), 1)
                pick = (lane == column + tensor * (NH * HD)) & (column < NH * HD)
                picked = nn(whole.astype(LOW), pick.astype(LOW))
                bias = jnp.concatenate(
                    [picked[2:3], jnp.zeros((1, WIDE), F32), picked[3:4]], axis=1
                )
                mix_rows(tensor)
                mix_rows(mate_row)
        mix_rows(far_row)
        for copy in relayed:
            copy.wait_recv()
        norm_rows(land.at[3], corner_row)
        mix_rows(corner_row)
        stay(mix_land, mix_out)
        weight = mix_land[...].reshape(width, width)
        for part in range(3):
            low = part * WIDE + WIDE - 128
            turned = weight[:, low : low + 128].T
            out_turned[part * HD : (part + 1) * HD] = turned[128 - HD :]
        stay(out_turned, out_out)
        settle(FC)
        for copy in fc_sides:
            copy.wait_recv()
        cot_made.wait_recv()
        copies.finish()
        for copy in stays:
            copy.wait()

    low = lambda *shape: jax.ShapeDtypeStruct(shape, LOW)
    outputs = (
        low(4, rows, width), low(4, rows, width), low(n_dp, shard, width),
        low(line, shard, width), low(line, shard, width), low(line, shard, width),
        low(line, shard, width), low(rows, width), low(NH * HD, width), low(rows, width),
        jax.ShapeDtypeStruct((VEC_ROWS, width), F32),
        jax.ShapeDtypeStruct((latents, 128), jnp.int32),
    )
    scratch = [
        pltpu.VMEM((rows, width), LOW),
        pltpu.VMEM((shard, 3 * WIDE), LOW),
        pltpu.VMEM((VEC_ROWS, 128), LOW),
        pltpu.VMEM((VEC_ROWS, 128), F32),
        pltpu.VMEM((4, rows, width), LOW),
        pltpu.VMEM((n_dp, shard, width), LOW),
        pltpu.VMEM((n_dp, VEC_ROWS, 128), LOW),
        pltpu.VMEM((3, VEC_ROWS, 128), LOW),
        pltpu.VMEM((4, rows, width), LOW),
        pltpu.VMEM((4, rows, width), LOW),
        pltpu.VMEM((NH * HD, width), LOW),
    ]
    given = (fc, tokens, thoughts, proj, qkv, out, *vectors)
    scratch += [pltpu.VMEM(x.shape, x.dtype) for x in given]
    scratch.append(pltpu.SemaphoreType.DMA((len(given),)))
    return comm_call(
        kernel,
        "gather_inputs",
        outputs,
        (positions, tokens, thoughts, cotangent, fc, proj, qkv, out, *vectors),
        [SM] + [ANY] * (7 + len(vectors)),
        (ANY,) * 10 + (VM, VM),
        3 + 2 + 1 + 2 + 2 + 1 + 2 + hops * (2 * 4 + 2 * 4),
        0,
        scratch=scratch,
        local=3 + 8 + 2,
    )


def after_attention(attended, out_own, out_far, hidden, vec_all, n_dp, cid):
    head_width, slots = attended.shape
    rows, width = hidden.shape
    half_rows = rows // 2

    def kernel(
        heads_ref, own_ref, far_ref, hidden_ref, vec_ref,
        both_out, middle_out, two_out,
        land, part, part_low, part_land, two, send, recv, local,
    ):
        at = Place(n_dp // 2)
        greet([(at.far, None), (at.mate, None)])
        copies = Copies(send, recv)
        cores = (at.core, 1 - at.core)
        made = [None, None]
        for i in (1, 0):
            theirs = pl.multiple_of(((1 - at.chip) * 2 + cores[i]) * rows, rows)
            made[i] = copies.start(heads_ref.at[:, pl.ds(theirs, rows)], land.at[i], at.far)
        stays = []

        def stay(source, target):
            stays.append(pltpu.make_async_copy(source, target, local.at[len(stays)]))
            stays[-1].start()

        spans = []
        for i in range(2):
            ours = pl.multiple_of((at.chip * 2 + cores[i]) * rows, rows)
            spans.append(pl.ds(ours, rows))
            stay(heads_ref.at[:, spans[i]], both_out.at[0, :, i * rows : (i + 1) * rows])
            part[i] = tn(heads_ref[:, spans[i]], own_ref[...])
        sums = None
        for i in (1, 0):
            made[i].wait_recv()
            stay(land.at[i], both_out.at[1, :, i * rows : (i + 1) * rows])
            part[i] += tn(land[i], far_ref[...])
            if i == 1:
                part_low[...] = part[1].astype(LOW)
                sums = copies.start(part_low, part_land, at.mate)
        sums.wait_recv()
        mated = []
        for piece in range(2):

            @pl.loop(0, half_rows // 128)
            def _(i):
                span = pl.ds(pl.multiple_of(piece * half_rows + i * 128, 128), 128)
                middle = (
                    hidden_ref[span].astype(F32)
                    + part[0, span]
                    + part_land[span].astype(F32)
                    + vec_ref[4:5]
                )
                middle_out[span] = middle
                two[span] = (normalize(middle)[0] * vec_ref[5:6] + vec_ref[6:7]).astype(LOW)

            span = pl.ds(piece * half_rows, half_rows)
            mated.append(copies.start(two.at[span], two_out.at[1, span], at.mate))
        stay(two, two_out.at[0])
        for copy in mated:
            copy.wait_recv()
        copies.finish()
        for copy in stays:
            copy.wait()

    return comm_call(
        kernel,
        "after_attention",
        (
            jax.ShapeDtypeStruct((2, head_width, 2 * rows), LOW),
            jax.ShapeDtypeStruct((rows, width), F32),
            jax.ShapeDtypeStruct((2, rows, width), LOW),
        ),
        (attended, out_own, out_far, hidden, vec_all),
        [VM] * 5,
        (ANY, VM, ANY),
        5,
        cid,
        scratch=[
            pltpu.VMEM((2, head_width, rows), LOW),
            pltpu.VMEM((2, rows, width), F32),
            pltpu.VMEM((rows, width), LOW),
            pltpu.VMEM((rows, width), LOW),
            pltpu.VMEM((rows, width), LOW),
        ],
        local=5,
    )


def before_attention_back(
    lengths, two, middle, cotangent, both, out_own, out_far, vec_all, pairs, n_dp, cid
):
    _, rows, width = two.shape
    head_width = out_own.shape[0]
    half_rows = rows // 2

    def kernel(
        lengths_ref, two_ref, middle_ref, cot_ref, both_ref, own_ref, far_ref, vec_ref,
        one_a, one_b, two_a, two_b,
        heads_out, grad_out, own_out, far_out, vec_out, sum_one, sum_two,
        two_land, mid, stay_heads, sent_heads, held, send, recv, local,
    ):
        at = Place(n_dp // 2)
        greet([(at.far, None), (at.mate, None)])
        copies = Copies(send, recv)
        halves = [pl.ds(0, half_rows), pl.ds(half_rows, half_rows)]
        loads = [
            pltpu.make_async_copy(ref, held.at[i], local.at[2 + i])
            for i, ref in enumerate((one_a, one_b, two_a, two_b))
        ]
        for copy in loads:
            copy.start()
        sums = [copies.start(two_ref.at[1, span], two_land.at[span], at.mate) for span in halves]
        vec_out[...] = jnp.zeros_like(vec_out)
        first_row = at.tensor * rows
        live = ends_of(lengths_ref)[-1]
        mated = []
        for piece in range(2):
            sums[piece].wait_recv()

            @pl.loop(0, half_rows // 128)
            def _(i):
                start = pl.multiple_of(piece * half_rows + i * 128, 128)
                span = pl.ds(start, 128)
                grad = two_ref[0, span].astype(F32) + two_land[span].astype(F32)
                normed, inverse = normalize(middle_ref[span])
                ids = first_row + start + lax.broadcasted_iota(jnp.int32, (128, 1), 0)
                final = jnp.where(ids < live, cot_ref[span].astype(F32), 0.0)
                total = final + norm_back(normed, inverse, grad, vec_ref[5:6])
                grad_out[span] = total
                mid[0, span] = total.astype(LOW)
                for row, term in ((4, total), (5, normed * grad), (6, grad), (7, final)):
                    vec_out[row : row + 1] += jnp.sum(term, axis=0, keepdims=True)

            mated.append(copies.start(mid.at[0, halves[piece]], mid.at[1, halves[piece]], at.mate))
        cores = (at.core, 1 - at.core)
        made, stays = [], []
        for i in range(2):
            if i == 1:
                for copy in mated:
                    copy.wait_recv()
            ours = pl.ds(pl.multiple_of((at.chip * 2 + cores[i]) * rows, rows), rows)
            sent_heads[i] = nt(far_ref[...], mid[i]).astype(LOW)
            made.append(copies.start(sent_heads.at[i], heads_out.at[:, ours], at.far))
            stay_heads[i] = nt(own_ref[...], mid[i]).astype(LOW)
            stays.append(
                pltpu.make_async_copy(stay_heads.at[i], heads_out.at[:, ours], local.at[i])
            )
            stays[-1].start()
        grads = mid[...].reshape(2 * rows, width)
        own_out[...] = nn(both_ref[0], grads).astype(LOW)
        far_out[...] = nn(both_ref[1], grads).astype(LOW)
        for copy in loads:
            copy.wait()
        sum_one[...] = (held[0].astype(F32) + held[1].astype(F32)).astype(LOW)
        sum_two[...] = (held[2].astype(F32) + held[3].astype(F32)).astype(LOW)
        for copy in made:
            copy.wait_recv()
        copies.finish()
        for copy in stays:
            copy.wait()

    return comm_call(
        kernel,
        "before_attention_back",
        (
            jax.ShapeDtypeStruct((head_width, 4 * rows), LOW),
            jax.ShapeDtypeStruct((rows, width), F32),
            jax.ShapeDtypeStruct((head_width, width), LOW),
            jax.ShapeDtypeStruct((head_width, width), LOW),
            jax.ShapeDtypeStruct((VEC_ROWS, width), F32),
            jax.ShapeDtypeStruct(pairs[0].shape, LOW),
            jax.ShapeDtypeStruct(pairs[0].shape, LOW),
        ),
        (lengths, two, middle, cotangent, both, out_own, out_far, vec_all, *pairs),
        [SM] + [VM] * 7 + [ANY] * 4,
        (ANY,) + (VM,) * 6,
        6,
        cid,
        scratch=[
            pltpu.VMEM((rows, width), LOW),
            pltpu.VMEM((2, rows, width), LOW),
            pltpu.VMEM((2, head_width, rows), LOW),
            pltpu.VMEM((2, head_width, rows), LOW),
            pltpu.VMEM((4,) + pairs[0].shape, LOW),
        ],
        local=6,
    )


def finish_grads(lengths, arrays, n_dp, cid):
    part_rows = arrays["hidden"].shape[0] // 4
    names = list(arrays)
    kept = [name for name in names if name != "out_far"]
    line = n_dp // 2
    shard = arrays["mix"].shape[1]
    rows, width = arrays["hidden"].shape
    group = 4 * rows
    latents = arrays["positions"].shape[0]
    window = rows // latents
    far_end = line - 1
    slots = [(distance, way) for distance in range(far_end, 0, -1) for way in (0, 1)] + [(0, 0)]
    last = len(slots) - 1
    share = width // (n_dp * 4)
    FC, PROJ, MIX, VEC = range(4)

    def kernel(lengths_ref, *refs):
        refs = list(refs)

        def take(number):
            taken = refs[:number]
            del refs[:number]
            return taken

        source = dict(zip(names, take(len(names))))
        fc_out, proj_out, mix_out, vec_out, tokens_out, thoughts_out, block_out = take(7)
        held = dict(zip(kept, take(len(kept))))
        cross_send, cross_land = [None, None] + take(2), [None, None] + take(2)
        hop_send, hop_land = take(4), take(4)
        (
            part, mate_land, far_send, far_land, last_land, total, vec_mine, vec_land, vec_near,
            plain_sum, column_sum, out_land, tokens_kept, thoughts_kept, block_kept, send, recv,
            local,
        ) = refs
        out = [fc_out, proj_out, mix_out, None]
        at = Place(line)
        tensor, spot, side = at.tensor, at.spot, at.side
        mate_row, far_row, corner_row = at.mate[1], at.far[1], at.corner[1]
        copies = Copies(send, recv)
        loads = {}
        held["out_far"] = out_land
        for i, name in enumerate(kept):
            loads[name] = pltpu.make_async_copy(source[name], held[name], local.at[i])

        def load(*group):
            for name in group:
                loads[name].start()

        load("fc_near", "fc_near_side", "fc_cross", "proj_near", "proj_near_far", "proj_cross")
        load("grad_mixed", "mix")
        greet(at.everyone())

        def block_of(slot):
            distance, way = slots[slot]
            if way == 0:
                return jnp.minimum(spot + distance, far_end), spot + distance < line
            return jnp.maximum(spot - distance, 0), spot - distance >= 0

        crosses, hops = [], []
        for slot in range(len(slots)):
            block, _ = block_of(slot)
            crosses.append(
                {
                    i: copies.plan(cross_send[i].at[block], cross_land[i].at[block], at.across)
                    for i in (MIX, VEC)
                }
            )
            if slot < last:
                hops.append(
                    [
                        copies.plan(
                            hop_send[i].at[slot],
                            hop_land[i].at[slot],
                            (at.up, at.down)[slots[slot][1]],
                        )
                        for i in range(4)
                    ]
                )

        def cross(distance, items):
            for slot in range(len(slots)):
                if slots[slot][0] == distance:
                    for i in items:
                        copies.begin(crosses[slot][i], block_of(slot)[1])

        terms = (
            ("fc_near", "fc_near_side", "fc_cross"),
            ("proj_near", "proj_near_far", "proj_cross"),
        )

        def own_term(i, block):
            if i in (FC, PROJ):
                return sum(held[name][block].astype(F32) for name in terms[i])
            if i == MIX:
                return total[block * 2 + side].astype(F32)
            return vec_near[block * 2 + side]

        def handle(slot, i):
            block, inside = block_of(slot)
            behind = (at.has_down, at.has_up)[slots[slot][1]]
            outer = slot - 2

            def work():
                value = own_term(i, block)
                if i in (MIX, VEC):
                    crosses[slot][i].wait_recv()
                    value = value + cross_land[i][block].astype(F32)
                if outer < 0:
                    hop_send[i][slot] = value.astype(hop_send[i].dtype)
                    return

                @pl.when(behind)
                def _():
                    hops[outer][i].wait_recv()
                    hop_send[i][slot] = (value + hop_land[i][outer].astype(F32)).astype(
                        hop_send[i].dtype
                    )

                @pl.when(jnp.logical_not(behind))
                def _():
                    hop_send[i][slot] = value.astype(hop_send[i].dtype)

            when(inside, work)
            copies.begin(hops[slot][i], inside)

        def handle_all(distance, items):
            for slot in range(last):
                if slots[slot][0] == distance:
                    for i in items:
                        handle(slot, i)

        def close(i, target):
            value = own_term(i, spot)
            if i in (MIX, VEC):
                crosses[last][i].wait_recv()
                value = value + cross_land[i][spot].astype(F32)
            target[...] = value
            for way, behind in enumerate((at.has_down, at.has_up)):

                def add(way=way):
                    hops[last - 2 + way][i].wait_recv()
                    target[...] += hop_land[i][last - 2 + way].astype(F32)

                when(behind, add)

        for name in ("fc_near", "fc_near_side", "fc_cross", "proj_near", "proj_near_far", "proj_cross"):
            loads[name].wait()
        out_made = copies.start(source["out_far"], out_land, at.far)
        handle_all(far_end, (FC, PROJ))
        load("group", "out_own", "vec_all", "vec_part", "bias_own", "bias_far")
        load("last", "hidden", "grad_middle", "middle", "positions")
        loads["grad_mixed"].wait()
        loads["mix"].wait()

        def row_part(index):
            @pl.loop(0, rows // 256)
            def _(i):
                span = pl.ds(pl.multiple_of(i * 256, 256), 256)
                weight = held["mix"][...].reshape(width, width)
                part[index, span] = nt(held["grad_mixed"][index, span], weight).astype(LOW)

        row_part(corner_row)
        mate_far = copies.start(part.at[corner_row], mate_land.at[1], at.mate)
        row_part(mate_row)
        mate_own = copies.start(part.at[mate_row], mate_land.at[0], at.mate)
        row_part(far_row)
        mate_far.wait_recv()
        far_made = []

        def send_far(count):
            for i in range(len(far_made), min(len(far_made) + count, 8)):
                span = pl.ds(i * (part_rows // 2), part_rows // 2)
                far_send[span] = (
                    mate_land[1, span].astype(F32) + part[far_row, span].astype(F32)
                ).astype(LOW)
                far_made.append(copies.start(far_send.at[span], far_land.at[span], at.far))

        send_far(2)
        row_part(tensor)
        send_far(1)
        if far_end > 1:
            handle_all(far_end - 1, (FC, PROJ))
        loads["last"].wait()
        last_copy = copies.start(held["last"].at[1], last_land, at.mate)
        for name in ("group", "out_own", "vec_all", "vec_part", "bias_own", "bias_far"):
            loads[name].wait()
        out_made.wait_recv()

        plain_sum[...] = jnp.zeros_like(plain_sum)
        column_sum[...] = jnp.zeros_like(column_sum)

        @pl.loop(0, group // 256)
        def _(i):
            block, start = i // (rows // 256), (i % (rows // 256)) * 256
            span = pl.ds(pl.multiple_of(start, 256), 256)
            grad = held["grad_mixed"][block, span]
            plain_sum[...] += tn(held["group"][block, span], grad)
            column_sum[...] += jnp.sum(grad.astype(F32), axis=0, keepdims=True)

        send_far(2)
        plain, columns = plain_sum[...], column_sum[...]
        turned = held["vec_all"][...].T
        weight = held["mix"][...].reshape(width, width).astype(F32)
        gain_grad = jnp.sum(plain * weight, axis=1, keepdims=True)
        shift_grad = jnp.sum(weight * columns, axis=1, keepdims=True)
        scaled = plain * turned[:, 0:1] + turned[:, 1:2] * columns
        extras = []
        out_sum = held["out_own"][...].astype(F32) + held["out_far"][...].astype(F32)
        for p in range(3):
            piece = out_sum[p * HD : (p + 1) * HD]
            extras.append(jnp.zeros((width, WIDE - 128), F32))
            extras.append(jnp.concatenate([jnp.zeros((128 - HD, width), F32), piece], axis=0).T)
        scaled = scaled + jnp.concatenate(extras, axis=1)
        for k in range(n_dp):
            total[k] = scaled[k * shard : (k + 1) * shard].astype(LOW)
        for block in range(line):
            cross_send[MIX][block] = total[block * 2 + 1 - side]
        cross(far_end, [MIX])
        cross(far_end - 1, [MIX])
        vec_mine[...] = held["vec_part"][...]
        flat = jnp.concatenate(
            [gain_grad, shift_grad, jnp.zeros((width, 6), F32)], axis=1
        ).T
        vec_mine[0:2] = flat[0:2]
        vec_mine[8:12] = units_rows_back(held["bias_own"][...], tensor, n_dp) + units_rows_back(
            held["bias_far"][...], far_row, n_dp
        )
        vec_lane = lax.broadcasted_iota(jnp.int32, (1, width), 1)
        in_part = (vec_lane >= tensor * (NH * HD)) & (vec_lane < (tensor + 1) * (NH * HD))
        for row, low in ((2, 0), (3, 2 * WIDE)):
            line_up = jnp.concatenate([columns[:, low : low + WIDE]] + [columns[:, 0:WIDE]] * 2, axis=1)
            placed = jnp.zeros((1, width), F32)
            for t in range(4):
                shifted = pltpu.roll(line_up, t * NH * HD, 1)
                placed = jnp.where(tensor == t, shifted, placed)
            vec_mine[row : row + 1] = jnp.where(in_part, placed, 0.0)
        vec_made = [
            copies.start(vec_mine, vec_land.at[i], device)
            for i, device in enumerate((at.mate, at.far, at.corner))
        ]
        for distance in range(far_end - 2, 0, -1):
            handle_all(distance, (FC, PROJ))
        send_far(1)
        for copy in vec_made:
            copy.wait_recv()
        send_far(1)
        vec_sum = vec_mine[...] + vec_land[0] + vec_land[1] + vec_land[2]
        for k in range(n_dp):
            vec_near[k] = pltpu.roll(vec_sum, (width - k * shard) % width, 1)[:, 0:128]
        for block in range(line):
            cross_send[VEC][block] = vec_near[block * 2 + 1 - side]
        cross(far_end, [VEC])
        cross(far_end - 1, [VEC])
        send_far(8)
        live = ends_of(lengths_ref)[-1]
        stays = []

        def close_rows(i):
            if i == 0:
                for name in ("hidden", "grad_middle", "middle", "positions"):
                    loads[name].wait()
                last_copy.wait_recv()
                mate_own.wait_recv()
            far_made[2 * i].wait_recv()
            far_made[2 * i + 1].wait_recv()
            span = pl.ds(i * part_rows, part_rows)
            ids = tensor * rows + i * part_rows + lax.broadcasted_iota(
                jnp.int32, (part_rows, 1), 0
            )
            final = (
                held["middle"][span]
                + held["last"][0, span].astype(F32)
                + last_land[span].astype(F32)
                + held["vec_all"][7:8]
            )
            block_kept[span] = jnp.where(ids < live, final, 0.0).astype(LOW)
            grad = (
                part[tensor, span].astype(F32)
                + mate_land[0, span].astype(F32)
                + far_land[span].astype(F32)
            )
            normed, inverse = normalize(held["hidden"][span].astype(F32))
            grad = held["grad_middle"][span] + norm_back(
                normed, inverse, grad, held["vec_all"][0:1]
            )
            for w in range(part_rows // window):
                index = i * (part_rows // window) + w
                here = (
                    lax.broadcasted_iota(jnp.int32, (window, 1), 0)
                    == held["positions"][index : index + 1, 0:1] - index * window
                )
                piece = grad[w * window : (w + 1) * window]
                tokens_kept[pl.ds(index * window, window)] = jnp.where(here, 0.0, piece)
                thoughts_kept[index : index + 1] = jnp.sum(
                    jnp.where(here, piece, 0.0), axis=0, keepdims=True
                )
            moves = [(tokens_kept.at[span], tokens_out.at[span])]
            moves.append((block_kept.at[span], block_out.at[span]))
            if i == 3:
                moves.append((thoughts_kept, thoughts_out))
            for kept_ref, out_ref in moves:
                stays.append(
                    pltpu.make_async_copy(kept_ref, out_ref, local.at[len(kept) + len(stays)])
                )
                stays[-1].start()

        done = 0
        for distance in range(far_end, 0, -1):
            handle_all(distance, (MIX, VEC))
            if distance >= 2:
                cross(distance - 2, (MIX, VEC))
            if distance <= 3:
                close_rows(done)
                done += 1
        for i in range(done, 4):
            close_rows(i)
        for i in (FC, PROJ, MIX):
            close(i, out[i])
        close(VEC, vec_out)
        copies.finish()
        for copy in stays:
            copy.wait()

    f32 = lambda *shape: jax.ShapeDtypeStruct(shape, F32)
    outputs = (
        f32(shard, width), f32(shard, width), f32(shard, width), f32(VEC_ROWS, 128),
        f32(rows, width), f32(latents, width), jax.ShapeDtypeStruct((rows, width), LOW),
    )
    scratch = [pltpu.VMEM(arrays[name].shape, arrays[name].dtype) for name in kept]
    for number, wide in ((line, 1), (line, 1), (last, 3), (last, 3)):
        scratch += [pltpu.VMEM((number, shard, width), LOW)] * wide
        scratch.append(pltpu.VMEM((number, VEC_ROWS, 128), F32))
    scratch += [
        pltpu.VMEM((4, rows, width), LOW),
        pltpu.VMEM((2, rows, width), LOW),
        pltpu.VMEM((rows, width), LOW),
        pltpu.VMEM((rows, width), LOW),
        pltpu.VMEM((rows, width), LOW),
        pltpu.VMEM((n_dp, shard, width), LOW),
        pltpu.VMEM((VEC_ROWS, width), F32),
        pltpu.VMEM((3, VEC_ROWS, width), F32),
        pltpu.VMEM((n_dp, VEC_ROWS, 128), F32),
        pltpu.VMEM((width, width), F32),
        pltpu.VMEM((1, width), F32),
        pltpu.VMEM(arrays["out_far"].shape, LOW),
        pltpu.VMEM((rows, width), F32),
        pltpu.VMEM((latents, width), F32),
        pltpu.VMEM((rows, width), LOW),
    ]
    return comm_call(
        kernel,
        "finish_grads",
        outputs,
        (lengths, *arrays.values()),
        [SM] + [ANY] * len(names),
        (VM,) * 4 + (ANY,) * 3,
        (last + 1) * 2 + last * 4 + 1 + 2 + 8 + 3 + 1,
        cid,
        scratch=scratch,
        local=len(kept) + 9,
    )


def unit_kernel(add, line, bias_row, lengths_ref, *refs):
    refs = list(refs)
    rows_ref, grad_own, grad_mate = refs[:3]
    pieces, vec_ref = refs[3:7], refs[7]
    refs = refs[8:]
    if add:
        last_in, two_in = refs[:2]
        refs = refs[2:]
    last_ref, two_ref, fc_near, fc_side, proj_near, proj_side, bias_grad_ref = refs[:7]
    fc_all, proj_all, fc_sum, proj_sum = refs[7:]
    step = pl.program_id(0)
    side, tensor = lax.axis_index("dp") % 2, lax.axis_index("tensor")
    live = ends_of(lengths_ref)[-1]

    @pl.when(step == 0)
    def _():
        for full, near, across in ((fc_all, *pieces[:2]), (proj_all, *pieces[2:])):
            for i in range(line):
                full[2 * i + side] = near[i]
                full[2 * i + 1 - side] = across[i]
        fc_sum[...] = jnp.zeros_like(fc_sum)
        proj_sum[...] = jnp.zeros_like(proj_sum)
        bias_grad_ref[...] = jnp.zeros_like(bias_grad_ref)

    count, width = rows_ref.shape
    half = pl.num_programs(0) // 2
    block = jnp.where(step < half, tensor, tensor + 1 - 2 * (tensor % 2))
    first = block * (half * count) + (step % half) * count
    alive = first + lax.broadcasted_iota(jnp.int32, (count, 1), 0) < live
    rows = rows_ref[...]
    grad = jnp.where(step < half, grad_own[...], grad_mate[...])
    grad = jnp.where(alive, grad, jnp.zeros_like(grad))
    fc = fc_all[...].reshape(width, -1)
    proj = proj_all[...].reshape(width, -1)
    inner = nn(rows, fc) + vec_ref[bias_row : bias_row + 1]
    square = inner * inner
    bend = jnp.tanh(GELU_SCALE * inner * (1.0 + GELU_CUBE * square))
    half = 0.5 * (1.0 + bend)
    activated = (inner * half).astype(LOW)
    slope = half + 0.5 * inner * (1.0 - bend * bend) * GELU_SCALE * (1.0 + 3.0 * GELU_CUBE * square)
    grad_inner = (nn(grad, proj) * slope).astype(LOW)
    last = nt(activated, proj)
    two = nt(grad_inner, fc)
    if add:
        last, two = last + last_in[...], two + two_in[...]
    last_ref[...] = last.astype(last_ref.dtype)
    two_ref[...] = two.astype(two_ref.dtype)
    fc_sum[...] += tn(rows, grad_inner)
    proj_sum[...] += tn(grad, activated)
    bias_grad_ref[...] += jnp.sum(grad_inner.astype(F32), axis=0, keepdims=True)

    @pl.when(step == pl.num_programs(0) - 1)
    def _():
        shard = fc_near.shape[1]
        for sums, near, across in ((fc_sum, fc_near, fc_side), (proj_sum, proj_near, proj_side)):
            for i in range(line):
                even = sums[2 * i * shard : (2 * i + 1) * shard].astype(LOW)
                odd = sums[(2 * i + 1) * shard : (2 * i + 2) * shard].astype(LOW)
                near[i] = jnp.where(side == 0, even, odd)
                across[i] = jnp.where(side == 0, odd, even)


def units_both_ways(lengths, rows, grad, mate_grad, pieces, vec_all, bias_row, before):
    count, width = rows.shape
    line, shard, units = pieces[0].shape
    half = count // ROW_TILE // 2
    tile = pl.BlockSpec((ROW_TILE, width), lambda i: (i, 0))
    fixed = lambda shape: pl.BlockSpec(shape, lambda i: (0,) * len(shape))
    add = before is not None
    kind = LOW if add else F32
    return pl.pallas_call(
        functools.partial(unit_kernel, add, line, bias_row),
        grid=(count // ROW_TILE,),
        out_shape=(
            jax.ShapeDtypeStruct((count, width), kind),
            jax.ShapeDtypeStruct((count, width), kind),
        )
        + (jax.ShapeDtypeStruct((line, shard, units), LOW),) * 4
        + (jax.ShapeDtypeStruct((1, units), F32),        ),
        in_specs=[
            SM,
            tile,
            pl.BlockSpec((ROW_TILE, width), lambda i: (jnp.minimum(i, half - 1), 0)),
            pl.BlockSpec((ROW_TILE, width), lambda i: (jnp.maximum(i - half, 0), 0)),
        ]
        + [fixed((line, shard, units))] * 4
        + [fixed(vec_all.shape)]
        + [tile] * (2 if add else 0),
        out_specs=(tile, tile) + (fixed((line, shard, units)),) * 4 + (fixed((1, units)),),
        scratch_shapes=[pltpu.VMEM((2 * line, shard, units), LOW)] * 2
        + [pltpu.VMEM((width, units), F32)] * 2,
        compiler_params=pltpu.CompilerParams(
            dimension_semantics=("arbitrary",), vmem_limit_bytes=VMEM_LIMIT
        ),
        cost_estimate=pl.CostEstimate(
            flops=12 * count * width * units,
            bytes_accessed=24 * count * width,
            transcendentals=count * units,
        ),
        name="units_second" if add else "units_first",
    )(lengths, rows, grad, mate_grad, *pieces, vec_all, *(before or ()))


def split_grads(mix_grad, vec, through, share):
    shard, width = mix_grad.shape
    head_width = NH * HD
    count = len(through)
    pieces_of = []
    for i, array in enumerate(through):
        size = 128 if array.shape[0] % 128 == 0 else array.shape[0]
        pieces_of += [(i, row, size) for row in range(0, array.shape[0], size)]

    def kernel(mix_ref, vec_ref, *refs):
        given, (qkv_out, out_out), refs = refs[:count], refs[count : count + 2], refs[count + 2 :]
        small, passed, held, sems = refs[:8], refs[8 : 8 + count], refs[8 + count : -1], refs[-1]
        ins, outs = [], []
        for i, row, size in pieces_of:
            span = pl.ds(row, size)
            ins.append(
                pltpu.make_async_copy(
                    given[i].at[span], held[i].at[span], sems.at[0, len(ins)]
                )
            )
            outs.append(
                pltpu.make_async_copy(
                    held[i].at[span], passed[i].at[span], sems.at[1, len(outs)]
                )
            )
        for copy in ins:
            copy.start()
        for i in range(len(ins)):
            ins[i].wait()
            outs[i].start()
        tensor = lax.axis_index("tensor")
        turned = mix_ref[...].T
        pieces = []
        for h in range(NH):
            for part in range(3):
                low = part * WIDE + h * HD
                pieces.append(turned[low : low + HD])
        qkv_out[...] = jnp.concatenate(pieces, axis=0).T
        for part in range(3):
            low = part * WIDE + head_width
            out_out[part * HD : (part + 1) * HD] = turned[low : low + HD]
        rows = vec_ref[0:8]
        moved = rows
        for i in range(1, 4):
            moved = jnp.where(tensor == i, pltpu.roll(rows, 128 - i * share, 1), moved)
        for i, row in enumerate((0, 1, 4, 5, 6, 7)):
            small[i][...] = moved[row : row + 1, 0:share]
        small[6][...] = moved[2:4, 0:share]
        small[7][...] = vec_ref[pl.ds(8 + tensor, 1)][:, 0:shard]
        for copy in outs:
            copy.wait()

    f32 = lambda *shape: jax.ShapeDtypeStruct(shape, F32)
    return pl.pallas_call(
        kernel,
        out_shape=(f32(shard, 3 * head_width), f32(head_width, shard))
        + (f32(1, share),) * 6
        + (f32(2, share), f32(1, shard))
        + tuple(jax.ShapeDtypeStruct(x.shape, x.dtype) for x in through),
        in_specs=[VM] * 2 + [ANY] * count,
        out_specs=(VM,) * 10 + (ANY,) * count,
        scratch_shapes=[pltpu.VMEM(x.shape, x.dtype) for x in through]
        + [pltpu.SemaphoreType.DMA((2, len(pieces_of)))],
        compiler_params=pltpu.CompilerParams(vmem_limit_bytes=VMEM_LIMIT),
        name="split_grads",
    )(mix_grad, vec, *through)


def by_tensor(row, step, index):
    moved = row
    for i in range(1, 4):
        moved = jnp.where(index == i, pltpu.roll(row, (i * step) % row.shape[1], 1), moved)
    return moved


def units_row(rows, block, n_dp):
    width = rows.shape[1]
    shard, step = width // n_dp, n_dp // 4
    lane = lax.broadcasted_iota(jnp.int32, (1, width), 1) // shard
    base = by_tensor(rows, width - step * shard, block)
    total = jnp.zeros((1, width), F32)
    for j in range(n_dp):
        moved = pltpu.roll(base[j % 4 : j % 4 + 1], (j - j // 4) * shard, 1)
        total = jnp.where(lane == j, moved, total)
    return total


def units_rows_back(row, block, n_dp):
    width = row.shape[1]
    shard, step = width // n_dp, n_dp // 4
    lane = lax.broadcasted_iota(jnp.int32, (1, width), 1) // shard
    rows = [jnp.zeros((1, width), F32) for _ in range(4)]
    for j in range(n_dp):
        moved = pltpu.roll(row, (width - (j - j // 4) * shard) % width, 1)
        rows[j % 4] = jnp.where(lane == j // 4, moved, rows[j % 4])
    return by_tensor(jnp.concatenate(rows, axis=0), step * shard, block)


def normalize(values):
    center = jnp.mean(values, axis=-1, keepdims=True)
    offset = values - center
    spread = jnp.mean(offset * offset, axis=-1, keepdims=True)
    inverse = lax.rsqrt(spread + EPSILON)
    return offset * inverse, inverse


def norm_back(normed, inverse, grad, gain):
    scaled = grad * gain
    center = jnp.mean(scaled, axis=-1, keepdims=True)
    along = jnp.mean(scaled * normed, axis=-1, keepdims=True)
    return inverse * (scaled - center - normed * along)


def product(equation, left, right):
    return jnp.einsum(equation, left, right, preferred_element_type=F32)


def per_device(
    tokens,
    thoughts,
    positions,
    lengths,
    attn_norm_gain,
    attn_norm_shift,
    qkv_weight,
    qv_bias,
    attn_out_weight,
    attn_out_bias,
    mlp_norm_gain,
    mlp_norm_shift,
    fc_weight,
    fc_bias,
    proj_weight,
    proj_bias,
    cotangent,
):
    n_dp = lax.axis_size("dp")
    n_tensor = lax.axis_size("tensor")
    rows, width = tokens.shape
    slots = rows * n_tensor
    swap_far = [(i, (i + 2) % n_tensor) for i in range(n_tensor)]

    share = width // (n_dp * n_tensor)
    small = [
        attn_norm_gain[None], attn_norm_shift[None], qv_bias, attn_out_bias[None],
        mlp_norm_gain[None], mlp_norm_shift[None], proj_bias[None], fc_bias[None],
    ]
    (
        group_low, mixed, mix_all, fc_near, fc_side, fc_far_near, proj_near, mate_grad, out_own,
        hidden, vec_all, places,
    ) = gather_inputs(
        tokens, thoughts, positions, cotangent, fc_weight, proj_weight.T, qkv_weight,
        attn_out_weight, small, n_dp,
    )
    mixed = mixed.reshape(slots, -1)
    swap_side = [(i, i + 1 - 2 * (i % 2)) for i in range(n_dp)]
    out_far = lax.ppermute(out_own, "tensor", swap_far)
    proj_far_near = lax.ppermute(proj_near, "tensor", swap_far)
    fc_far_side = lax.ppermute(fc_far_near, "dp", swap_side)
    attended, stats = attend(lengths, mixed)
    sent, out_far, proj_far_near, fc_far_side = lax.optimization_barrier(
        (attended, out_far, proj_far_near, fc_far_side)
    )
    proj_far_side = lax.ppermute(proj_far_near, "dp", swap_side)
    both, middle, chip_two = after_attention(
        sent, out_own, out_far, hidden, vec_all, n_dp, 1
    )
    chip_two, proj_far_side, proj_sent = lax.optimization_barrier(
        (chip_two, proj_far_side, proj_near)
    )
    proj_side = lax.ppermute(proj_sent, "dp", swap_side)
    chip_two = chip_two.reshape(2 * rows, width)

    first = units_both_ways(
        lengths, chip_two, cotangent, mate_grad,
        (fc_far_near, fc_far_side, proj_far_near, proj_far_side), vec_all, 13, None,
    )
    far_fc_near, far_fc_side, far_proj_near, far_proj_side, far_fc_bias = first[2:]
    proj_side_far = lax.ppermute(far_proj_side, "tensor", swap_far)
    fc_far_side_in = lax.ppermute(far_fc_side, "dp", swap_side)
    second = units_both_ways(
        lengths, chip_two, cotangent, mate_grad, (fc_near, fc_side, proj_near, proj_side), vec_all, 12,
        first[:2],
    )
    last_part, grad_two_part, fc_near_grad, fc_side_grad, proj_near_grad, proj_side_grad = second[:6]
    fc_near_side_in = lax.ppermute(fc_side_grad, "dp", swap_side)
    grad_heads, grad_middle, grad_out, far_out, vec_part, fc_cross, proj_cross = before_attention_back(
        lengths, grad_two_part.reshape(2, rows, width), middle, cotangent, both, out_own, out_far,
        vec_all, (far_fc_near, fc_far_side_in, proj_side_grad, proj_side_far), n_dp, 2,
    )
    grad_heads, fc_cross, proj_cross, far_proj_near = lax.optimization_barrier(
        (grad_heads, fc_cross, proj_cross, far_proj_near)
    )
    fc_cross = lax.ppermute(fc_cross, "tensor", swap_far)
    proj_cross = lax.ppermute(proj_cross, "dp", swap_side)
    proj_near_far = lax.ppermute(far_proj_near, "tensor", swap_far)
    last_low = last_part.reshape(2, rows, width)

    grad_mixed = attend_back(lengths, mixed, attended, stats, grad_heads)
    arrays = {
        "fc_near": fc_near_grad, "fc_near_side": fc_near_side_in, "fc_cross": fc_cross,
        "proj_near": proj_near_grad, "proj_near_far": proj_near_far, "proj_cross": proj_cross,
        "grad_mixed": grad_mixed.reshape(n_tensor, rows, width), "mix": mix_all,
        "last": last_low, "group": group_low,
        "out_own": grad_out, "out_far": far_out,
        "vec_all": vec_all, "vec_part": vec_part, "bias_own": second[6], "bias_far": far_fc_bias,
        "hidden": hidden, "grad_middle": grad_middle, "middle": middle, "positions": places,
    }
    fc_grad, proj_grad, mix_grad, vec, grad_tokens, grad_thoughts, block_out = finish_grads(
        lengths, arrays, n_dp, 8
    )
    parts = split_grads(
        mix_grad, vec, (fc_grad, proj_grad, grad_tokens, grad_thoughts, block_out), share
    )
    qkv_grad, out_grad = parts[:2]
    gain_one, shift_one, out_bias, gain_two, shift_two, last_bias = [p[0] for p in parts[2:8]]
    query_value, hidden_bias = parts[8], parts[9][0]
    fc_grad, proj_grad, grad_tokens, grad_thoughts, block_out = parts[10:]
    return (
        block_out,
        grad_tokens,
        grad_thoughts,
        gain_one,
        shift_one,
        qkv_grad,
        query_value,
        out_grad,
        out_bias,
        gain_two,
        shift_two,
        fc_grad,
        hidden_bias,
        proj_grad.T,
        last_bias,
    )


def solution(mesh):
    rows = P(("dp", "tensor"), None)
    line = P(("dp", "tensor"))
    in_specs = (
        rows, rows, line, P("dp", None), line, line, P("dp", "tensor"),
        P(None, ("dp", "tensor")), P("tensor", "dp"), line, line, line,
        P("dp", "tensor"), line, P("tensor", "dp"), line, rows,
    )
    out_specs = (
        rows, rows, rows, line, line, P("dp", "tensor"), P(None, ("dp", "tensor")),
        P("tensor", "dp"), line, line, line, P("dp", "tensor"), line, P("tensor", "dp"), line,
    )
    return jax.shard_map(
        per_device, mesh=mesh, in_specs=in_specs, out_specs=out_specs, check_vma=False
    )
```

```python
import functools
import math

import jax
import jax.numpy as jnp
from jax import lax
from jax.experimental import pallas as pl
from jax.experimental.pallas import tpu as pltpu
from jax.sharding import PartitionSpec as P

H = 12
HD = 64
FF = 3072
SEQ_DEV = 3
EPSILON = 1e-05
MASKED = -1e30
NH = 3
SLABS = 2
WIDE = SLABS * 128
BQ = 512
BK = 512
VEC_ROWS = 16
VMEM_LIMIT = 67043328
ROW_TILE = 256
GELU_SCALE = math.sqrt(2.0 / math.pi)
GELU_CUBE = 0.044715
MESH = pl.DeviceIdType.MESH
ANY = pl.BlockSpec(memory_space=pltpu.HBM)
VM = pl.BlockSpec(memory_space=pltpu.VMEM)
SM = pl.BlockSpec(memory_space=pltpu.SMEM)
LOW = jnp.bfloat16
F32 = jnp.float32


def nn(a, b):
    return lax.dot_general(a, b, (((1,), (0,)), ((), ())), preferred_element_type=jnp.float32)


def nt(a, b):
    return lax.dot_general(a, b, (((1,), (1,)), ((), ())), preferred_element_type=jnp.float32)


def tn(a, b):
    return lax.dot_general(a, b, (((0,), (0,)), ((), ())), preferred_element_type=jnp.float32)


def head_rows(slab, head):
    half = slab[(head % 2) * HD : (head % 2 + 1) * HD]
    zero = jnp.zeros_like(half)
    return jnp.concatenate([half, zero] if head % 2 == 0 else [zero, half], axis=0)


def ends_of(lengths_ref):
    ends = [lengths_ref[0, 0]]
    for i in range(1, SEQ_DEV):
        ends.append(ends[-1] + lengths_ref[0, i])
    return ends


def segment_start(ends, slots):
    start = jnp.zeros_like(slots)
    for i in range(SEQ_DEV):
        start = jnp.where(slots >= ends[i], ends[i], start)
    return start


def segment_stop(ends, slot, slots):
    stop = slots
    for i in reversed(range(SEQ_DEV)):
        stop = jnp.where(slot < ends[i], ends[i], stop)
    return stop


def attend_kernel(
    lengths_ref, mixed_in, out_ref, stat_ref, mixed_ref, qt_ref, vt_ref, sems
):
    tokens = mixed_ref.shape[0]
    ends = ends_of(lengths_ref)
    count = (ends[-1] + BQ - 1) // BQ
    half = BQ // 2

    def load(block):
        rows = pl.ds(pl.multiple_of(block * BQ, BQ), BQ)
        return pltpu.make_async_copy(mixed_in.at[rows], mixed_ref.at[rows], sems.at[block])

    for block in range(tokens // BQ):
        load(block).start()

    def step(rows, keys, columns, queries, first, causal, state):
        size = queries[0].shape[1]
        slots = first + lax.broadcasted_iota(jnp.int32, (1, size), 1)
        start = segment_start(ends, slots)
        key_ids = rows + lax.broadcasted_iota(jnp.int32, (keys, size), 0)
        allowed = key_ids >= start
        if causal:
            allowed = allowed & (key_ids <= slots)
        span = pl.ds(rows, keys)
        result = []
        for h in range(NH):
            peak, total, acc = state[h]
            low = WIDE + (h // 2) * 128
            scores = nn(mixed_ref[span, low : low + 128], queries[h])
            scores = jnp.where(allowed, scores, MASKED)
            fresh = jnp.maximum(peak, jnp.max(scores, axis=0, keepdims=True))
            weight = jnp.exp(scores - fresh)
            decay = jnp.exp(peak - fresh)
            total = total * decay + jnp.sum(weight, axis=0, keepdims=True)
            values = vt_ref[h * HD : (h + 1) * HD, span]
            acc = acc * decay + nn(values, weight.astype(jnp.bfloat16))
            result.append((fresh, total, acc))
        return tuple(result)

    def query_block(block, carry):
        first = pl.multiple_of(block * BQ, BQ)
        columns = pl.ds(first, BQ)
        load(block).wait()
        for slab in range(SLABS):
            low = slab * 128
            qt_ref[low : low + 128] = (mixed_ref[columns, low : low + 128] * HD ** (-0.5)).T
            vt_ref[low : low + 128, columns] = mixed_ref[
                columns, 2 * WIDE + low : 2 * WIDE + low + 128
            ].T
        queries = [head_rows(qt_ref[(h // 2) * 128 : (h // 2 + 1) * 128], h) for h in range(NH)]

        def key_block(key, state):
            return step(pl.multiple_of(key * BK, BK), BK, columns, queries, first, False, state)

        empty = tuple(
            (
                jnp.full((1, BQ), MASKED, jnp.float32),
                jnp.zeros((1, BQ), jnp.float32),
                jnp.zeros((HD, BQ), jnp.float32),
            )
            for _ in range(NH)
        )
        state = lax.fori_loop(segment_start(ends, first) // BK, block, key_block, empty)
        for side, keys in ((0, half), (1, BQ)):
            piece = slice(side * half, (side + 1) * half)
            final = step(
                first, keys, columns, [q[:, piece] for q in queries], first + side * half, True,
                tuple(tuple(x[:, piece] for x in one) for one in state),
            )
            for h in range(NH):
                peak, total, acc = final[h]
                place_here = pl.ds(pl.multiple_of(first + side * half, half), half)
                out_ref[h * HD : (h + 1) * HD, place_here] = (acc / total).astype(jnp.bfloat16)
                stat_ref[h : h + 1, place_here] = peak + jnp.log(total)
        return carry

    lax.fori_loop(0, count, query_block, 0)

    def padded_block(block, carry):
        load(block).wait()
        columns = pl.ds(pl.multiple_of(block * BQ, BQ), BQ)
        out_ref[:, columns] = jnp.zeros((out_ref.shape[0], BQ), jnp.bfloat16)
        return carry

    lax.fori_loop(count, tokens // BQ, padded_block, 0)


def attend(lengths, mixed):
    tokens = mixed.shape[0]
    vm = pl.BlockSpec(memory_space=pltpu.VMEM)
    return pl.pallas_call(
        attend_kernel,
        out_shape=(
            jax.ShapeDtypeStruct((NH * HD, tokens), jnp.bfloat16),
            jax.ShapeDtypeStruct((8, tokens), jnp.float32),
        ),
        in_specs=[pl.BlockSpec(memory_space=pltpu.SMEM), pl.BlockSpec(memory_space=pltpu.HBM)],
        out_specs=(vm, vm),
        scratch_shapes=[
            pltpu.VMEM(mixed.shape, mixed.dtype),
            pltpu.VMEM((WIDE, BQ), jnp.bfloat16),
            pltpu.VMEM((WIDE, tokens), jnp.bfloat16),
            pltpu.SemaphoreType.DMA((tokens // BQ,)),
        ],
        compiler_params=pltpu.CompilerParams(vmem_limit_bytes=VMEM_LIMIT),
        cost_estimate=pl.CostEstimate(
            flops=8 * tokens * tokens * NH * HD,
            bytes_accessed=16 * tokens * WIDE,
            transcendentals=tokens * tokens,
        ),
        name="attend",
    )(lengths, mixed)


def attend_back_kernel(
    lengths_ref, mixed_in, out_in, stat_ref, gradt_in,
    gmixed_out, mixed_ref, out_ref, gradt_ref, gmixed_ref, qt_ref, kt_ref, grad_ref, delta_ref,
    dqt_ref, sems, out_sems
):
    tokens = mixed_ref.shape[0]
    blocks = tokens // BQ
    ends = ends_of(lengths_ref)
    count = (ends[-1] + BK - 1) // BK
    half = BQ // 2

    def loads(block):
        rows = pl.ds(pl.multiple_of(block * BQ, BQ), BQ)
        return (
            pltpu.make_async_copy(mixed_in.at[rows], mixed_ref.at[rows], sems.at[0, block]),
            pltpu.make_async_copy(out_in.at[:, rows], out_ref.at[:, rows], sems.at[1, block]),
            pltpu.make_async_copy(gradt_in.at[:, rows], gradt_ref.at[:, rows], sems.at[2, block]),
        )

    def leave(block, part):
        rows = pl.ds(pl.multiple_of(block * BQ, BQ), BQ)
        lanes = pl.ds(0, WIDE) if part == 0 else pl.ds(WIDE, 2 * WIDE)
        return pltpu.make_async_copy(
            gmixed_ref.at[rows, lanes], gmixed_out.at[rows, lanes], out_sems.at[part, block]
        )

    for block in reversed(range(blocks)):
        for copy in loads(block):
            copy.start()
    dqt_ref[...] = jnp.zeros_like(dqt_ref)

    def prepare_block(block):
        rows = pl.ds(pl.multiple_of(block * BQ, BQ), BQ)
        for slab in range(SLABS):
            low = slab * 128
            qt_ref[low : low + 128, rows] = (
                mixed_ref[rows, low : low + 128] * HD ** (-0.5)
            ).T
            kt_ref[low : low + 128, rows] = mixed_ref[rows, WIDE + low : WIDE + low + 128].T
        grad_ref[rows, 0:128] = gradt_ref[0:128, rows].T
        grad_ref[rows, 128:256] = jnp.concatenate(
            [gradt_ref[128:192, rows], jnp.zeros((64, BQ), jnp.bfloat16)], axis=0
        ).T
        for h in range(NH):
            product = gradt_ref[h * HD : (h + 1) * HD, rows].astype(jnp.float32) * out_ref[
                h * HD : (h + 1) * HD, rows
            ].astype(jnp.float32)
            delta_ref[h : h + 1, rows] = jnp.sum(product, axis=0, keepdims=True)

    def terms(base, keys, first, size, causal):
        rows, columns = pl.ds(base, keys), pl.ds(first, size)
        slots = first + lax.broadcasted_iota(jnp.int32, (1, size), 1)
        key_ids = base + lax.broadcasted_iota(jnp.int32, (keys, size), 0)
        allowed = key_ids >= segment_start(ends, slots)
        if causal:
            allowed = allowed & (key_ids <= slots)
        lane = lax.broadcasted_iota(jnp.int32, (size, 128), 1)
        grad_keys, grad_values = [None] * SLABS, [None] * SLABS
        for h in range(NH):
            slab = h // 2
            low, high = slab * 128, slab * 128 + 128
            queries = head_rows(qt_ref[low:high, columns], h)
            scores = nn(mixed_ref[rows, WIDE + low : WIDE + high], queries)
            probs = jnp.where(allowed, jnp.exp(scores - stat_ref[h : h + 1, columns]), 0.0)
            keep = (lane // HD) == (h % 2)
            value = nn(probs.astype(jnp.bfloat16), jnp.where(keep, grad_ref[columns, low:high], 0.0))
            if h == NH - 1 and NH % 2 == 1:
                grad_rows = jnp.concatenate(
                    [gradt_ref[h * HD : (h + 1) * HD, columns], jnp.zeros((HD, size), jnp.bfloat16)],
                    axis=0,
                )
            else:
                grad_rows = head_rows(gradt_ref[low:high, columns], h)
            grad_probs = nn(mixed_ref[rows, 2 * WIDE + low : 2 * WIDE + high], grad_rows)
            grad_scores = (probs * (grad_probs - delta_ref[h : h + 1, columns])).astype(
                jnp.bfloat16
            )
            key_term = nn(grad_scores, jnp.where(keep, mixed_ref[columns, low:high], 0.0))
            grad_values[slab] = value if grad_values[slab] is None else grad_values[slab] + value
            grad_keys[slab] = key_term if grad_keys[slab] is None else grad_keys[slab] + key_term
            dqt_ref[h * HD : (h + 1) * HD, columns] += nn(
                kt_ref[h * HD : (h + 1) * HD, rows], grad_scores
            )
        return grad_keys + grad_values

    def key_block(turn, carry):
        key = count - 1 - turn
        for copy in loads(key):
            copy.wait()
        prepare_block(key)
        base = pl.multiple_of(key * BK, BK)
        rows = pl.ds(base, BK)
        upper = terms(base, half, base, BQ, True)
        lower = terms(pl.multiple_of(base + half, half), half, pl.multiple_of(base + half, half), half, True)
        state = tuple(jnp.concatenate([a, b], axis=0) for a, b in zip(upper, lower))

        def query_block(block, state):
            fresh = terms(base, BK, pl.multiple_of(block * BQ, BQ), BQ, False)
            return tuple(a + b for a, b in zip(state, fresh))

        stop = jnp.minimum(segment_stop(ends, base + BK - 1, tokens), ends[-1])
        state = lax.fori_loop(key + 1, (stop - 1) // BQ + 1, query_block, state)
        for slab in range(SLABS):
            low = slab * 128
            gmixed_ref[rows, WIDE + low : WIDE + low + 128] = (
                state[slab] * HD ** (-0.5)
            ).astype(jnp.bfloat16)
            gmixed_ref[rows, 2 * WIDE + low : 2 * WIDE + low + 128] = state[SLABS + slab].astype(
                jnp.bfloat16
            )
        leave(key, 1).start()
        return carry

    def padded_block(key, carry):
        for copy in loads(key):
            copy.wait()
        rows = pl.ds(pl.multiple_of(key * BK, BK), BK)
        gmixed_ref[rows, WIDE:] = jnp.zeros((BK, 2 * WIDE), jnp.bfloat16)
        leave(key, 1).start()
        return carry

    lax.fori_loop(count, blocks, padded_block, 0)
    lax.fori_loop(0, count, key_block, 0)
    for block in range(blocks):
        rows = pl.ds(block * BQ, BQ)
        for slab in range(SLABS):
            low = slab * 128
            gmixed_ref[rows, low : low + 128] = (
                (dqt_ref[low : low + 128, rows] * HD ** (-0.5)).T.astype(jnp.bfloat16)
            )
        leave(block, 0).start()
    for block in range(blocks):
        leave(block, 0).wait()
        leave(block, 1).wait()


def attend_back(lengths, mixed, out, stat, gradt):
    tokens = mixed.shape[0]
    vm = pl.BlockSpec(memory_space=pltpu.VMEM)
    hbm = pl.BlockSpec(memory_space=pltpu.HBM)
    return pl.pallas_call(
        attend_back_kernel,
        out_shape=jax.ShapeDtypeStruct((tokens, 3 * WIDE), jnp.bfloat16),
        in_specs=[pl.BlockSpec(memory_space=pltpu.SMEM), hbm, hbm, vm, hbm],
        out_specs=hbm,
        scratch_shapes=[
            pltpu.VMEM(mixed.shape, jnp.bfloat16),
            pltpu.VMEM(out.shape, jnp.bfloat16),
            pltpu.VMEM(gradt.shape, jnp.bfloat16),
            pltpu.VMEM(mixed.shape, jnp.bfloat16),
            pltpu.VMEM((WIDE, tokens), jnp.bfloat16),
            pltpu.VMEM((WIDE, tokens), jnp.bfloat16),
            pltpu.VMEM((tokens, WIDE), jnp.bfloat16),
            pltpu.VMEM((8, tokens), jnp.float32),
            pltpu.VMEM((WIDE, tokens), jnp.float32),
            pltpu.SemaphoreType.DMA((3, tokens // BQ)),
            pltpu.SemaphoreType.DMA((2, tokens // BQ)),
        ],
        compiler_params=pltpu.CompilerParams(vmem_limit_bytes=VMEM_LIMIT),
        cost_estimate=pl.CostEstimate(
            flops=20 * tokens * tokens * NH * HD,
            bytes_accessed=32 * tokens * WIDE,
            transcendentals=tokens * tokens,
        ),
        name="attend_back",
    )(lengths, mixed, out, stat, gradt)


class Copies:
    def __init__(self, send, recv):
        self.send, self.recv, self.made, self.started = send, recv, 0, []

    def plan(self, source, target, device):
        index = self.made
        self.made += 1
        return pltpu.make_async_remote_copy(
            src_ref=source,
            dst_ref=target,
            send_sem=self.send.at[index],
            recv_sem=self.recv.at[index],
            device_id=device,
            device_id_type=MESH,
        )

    def begin(self, copy, condition=None):
        self.started.append((copy, condition))
        when(condition, copy.start)

    def start(self, source, target, device):
        copy = self.plan(source, target, device)
        self.begin(copy)
        return copy

    def finish(self):
        for copy, condition in self.started:
            when(condition, copy.wait_send)


def when(condition, action):
    if condition is None:
        action()
    else:
        pl.when(condition)(action)


def greet(devices):
    barrier = pltpu.get_barrier_semaphore()
    for device, condition in devices:
        when(
            condition,
            lambda device=device: pl.semaphore_signal(
                barrier, inc=1, device_id=device, device_id_type=MESH
            ),
        )
    present = [1 if condition is None else condition.astype(jnp.int32) for _, condition in devices]
    pl.semaphore_wait(barrier, sum(present))


class Place:
    def __init__(self, line):
        self.dp = dp = lax.axis_index("dp")
        self.tensor = tensor = lax.axis_index("tensor")
        self.spot, self.side = spot, side = dp // 2, dp % 2
        self.chip, self.core = tensor // 2, tensor % 2
        self.has_up, self.has_down = spot + 1 < line, spot > 0
        self.up = (jnp.minimum(spot + 1, line - 1) * 2 + side, tensor)
        self.down = (jnp.maximum(spot - 1, 0) * 2 + side, tensor)
        self.across = (spot * 2 + 1 - side, tensor)
        self.mate = (dp, tensor + 1 - 2 * (tensor % 2))
        self.far = (dp, (tensor + 2) % 4)
        self.corner = (dp, 3 - tensor)

    def everyone(self):
        return [
            (self.mate, None), (self.far, None), (self.corner, None), (self.across, None),
            (self.up, self.has_up), (self.down, self.has_down),
        ]


def comm_call(kernel, name, outputs, inputs, in_specs, out_specs, copies, cid, scratch=(), local=1, limit=VMEM_LIMIT):
    return pl.pallas_call(
        kernel,
        out_shape=outputs,
        in_specs=in_specs,
        out_specs=out_specs,
        scratch_shapes=list(scratch)
        + [
            pltpu.SemaphoreType.DMA((copies,)),
            pltpu.SemaphoreType.DMA((copies,)),
            pltpu.SemaphoreType.DMA((local,)),
        ],
        compiler_params=pltpu.CompilerParams(
            collective_id=cid, has_side_effects=True, vmem_limit_bytes=limit
        ),
        name=name,
    )(*inputs)


def one_hot(rows, columns, shift, limit):
    lane = lax.broadcasted_iota(jnp.int32, (rows, columns), 0)
    spot = lax.broadcasted_iota(jnp.int32, (rows, columns), 1)
    return ((spot == lane + shift) & (lane < limit)).astype(LOW)


def gather_inputs(tokens, thoughts, positions, cotangent, fc, proj, qkv, out, vectors, n_dp):
    line = n_dp // 2
    hops = line - 1
    rows, width = tokens.shape
    latents = thoughts.shape[0]
    window = rows // latents
    shard = fc.shape[0]
    half_rows = rows // 2
    share = width // (n_dp * 4)

    def kernel(
        pos_ref, tokens_in, thoughts_in, cot_ref, fc_in, proj_in, qkv_in, out_in, *refs
    ):
        given = (fc_in, tokens_in, thoughts_in, proj_in, qkv_in, out_in) + refs[: len(vectors)]
        (
            normed_out, mixed_out, mix_out, fc_near, fc_side, fc_far, proj_near, cot_out, out_out,
            hidden_out, vec_out, pos_out,
            hidden_ref, mix_ref, vec_ref, tile,
            land, mix_land, tiles, tile_land, normed, mixed, out_turned,
            *held, arrive, send, recv, local,
        ) = refs[len(vectors) :]
        arrivals = [
            pltpu.make_async_copy(given[i], held[i], arrive.at[i]) for i in range(len(given))
        ]
        for copy in arrivals:
            copy.start()
        fc_ref, tokens_ref, thoughts_ref, proj_ref, qkv_ref, out_ref = held[:6]
        vec_refs = held[6:]
        at = Place(line)
        dp, tensor, spot, side = at.dp, at.tensor, at.spot, at.side
        mate_row, far_row, corner_row = at.mate[1], at.far[1], at.corner[1]
        greet(at.everyone())
        copies = Copies(send, recv)
        MIX, FC, PROJ, VEC = range(4)
        own = [mix_ref, fc_ref, proj_ref, tiles.at[dp]]

        def seat(item, position):
            if item == MIX:
                return mix_land.at[position * 2 + side]
            if item == FC:
                return fc_near.at[position]
            if item == PROJ:
                return proj_near.at[position]
            return tiles.at[position * 2 + side]

        def plan(item, hop):
            above, below = jnp.maximum(spot - hop, 0), jnp.minimum(spot + hop, line - 1)
            came_up = jnp.maximum(spot - 1 - hop, 0)
            came_down = jnp.minimum(spot + 1 + hop, line - 1)
            made = {
                "up": copies.plan(
                    own[item] if hop == 0 else seat(item, above), seat(item, above), at.up
                ),
                "down": copies.plan(
                    own[item] if hop == 0 else seat(item, below), seat(item, below), at.down
                ),
                "onward": [],
            }
            for position in (came_up, came_down):
                onward = []
                if item in (MIX, VEC):
                    onward.append(copies.plan(seat(item, position), seat(item, position), at.across))
                if item == FC:
                    onward.append(copies.plan(fc_near.at[position], fc_side.at[position], at.across))
                    onward.append(copies.plan(fc_near.at[position], fc_far.at[position], at.far))
                made["onward"].append(onward)
            return made

        plans = [[plan(item, hop) for hop in range(hops)] for item in range(4)]

        def launch(item):
            copies.begin(plans[item][0]["up"], at.has_up)
            copies.begin(plans[item][0]["down"], at.has_down)

        def handle(item, hop):
            made = plans[item][hop]
            for way, key, comes, goes in (
                (0, "up", spot - 1 - hop >= 0, at.has_up),
                (1, "down", spot + 1 + hop < line, at.has_down),
            ):
                when(comes, made[key].wait_recv)
                if hop + 1 < hops:
                    copies.begin(plans[item][hop + 1][key], comes & goes)
                for copy in made["onward"][way]:
                    copies.begin(copy, comes)

        def settle(item):
            for hop in range(hops):
                for way, comes in ((0, spot - 1 - hop >= 0), (1, spot + 1 + hop < line)):
                    for copy in plans[item][hop]["onward"][way]:
                        when(comes, copy.wait_recv)

        stays = []

        def stay(source, target):
            copy = pltpu.make_async_copy(source, target, local.at[len(stays)])
            copy.start()
            stays.append(copy)
            return copy

        parts = [pl.ds(0, half_rows), pl.ds(half_rows, half_rows)]
        arrivals[0].wait()
        launch(FC)
        fc_sides = [copies.start(fc_ref, fc_side.at[spot], at.across)]
        cot_made = copies.start(cot_ref, cot_out, at.mate)
        for copy in arrivals[6:]:
            copy.wait()
        tile[...] = jnp.zeros_like(tile)
        row = 0
        for ref in vec_refs:
            count, size = ref.shape
            tile[row : row + count, 0:size] = ref[...].astype(F32)
            row += count
        vec_ref[...] = tile[...].astype(LOW)
        vec_made = [
            copies.start(vec_ref, tile_land.at[i], device)
            for i, device in enumerate((at.mate, at.far, at.corner))
        ]
        arrivals[1].wait()
        arrivals[2].wait()
        pos_row = lax.broadcasted_iota(jnp.int32, (latents, 128), 0)
        places = jnp.zeros((latents, 128), jnp.int32)
        for w in range(latents):
            places = jnp.where(pos_row == w, pos_ref[w], places)
            span = pl.ds(w * window, window)
            here = lax.broadcasted_iota(jnp.int32, (window, 1), 0) == pos_ref[w] - w * window
            hidden_ref[span] = jnp.where(
                here, thoughts_ref[w : w + 1].astype(F32), tokens_ref[span].astype(F32)
            ).astype(LOW)
        pos_out[...] = places
        far_made = [
            copies.start(hidden_ref.at[part], land.at[2, part], at.far) for part in parts
        ]
        mate_made = copies.start(hidden_ref, land.at[1], at.mate)
        fc_sides.append(copies.start(fc_ref, fc_far.at[spot], at.far))
        for copy in arrivals[3:6]:
            copy.wait()
        turned = qkv_ref[...].astype(F32).T
        extra = out_ref[...].astype(F32)
        pieces = []
        for p in range(3):
            for h in range(NH):
                low = (h * 3 + p) * HD
                pieces.append(turned[low : low + HD])
            pieces.append(extra[p * HD : (p + 1) * HD])
        mix_ref[...] = jnp.concatenate(pieces, axis=0).T.astype(LOW)
        launch(MIX)
        mix_side = copies.start(mix_ref, mix_land.at[dp], at.across)
        stay(hidden_ref, hidden_out)
        stay(fc_ref, fc_near.at[spot])
        stay(proj_ref, proj_near.at[spot])
        mix_land[dp] = mix_ref[...]
        for copy in vec_made:
            copy.wait_recv()
        merged = jnp.zeros((VEC_ROWS, 128), F32)
        bias_rows = jnp.zeros((VEC_ROWS, 128), F32)
        row_ids = lax.broadcasted_iota(jnp.int32, (VEC_ROWS, 128), 0)
        for i, index in enumerate((tensor, mate_row, far_row, corner_row)):
            tile = vec_ref[...] if i == 0 else tile_land[i - 1]
            merged += nn(tile, one_hot(128, 128, index * share, share))
            bias_rows = jnp.where(row_ids == 8 + index, tile[8:9].astype(F32), bias_rows)
        tiles[dp] = jnp.where(row_ids < 8, merged, bias_rows).astype(LOW)
        launch(VEC)
        vec_side = copies.start(tiles.at[dp], tiles.at[dp], at.across)

        def norm_rows(source, index):
            @pl.loop(0, rows // 128)
            def _(i):
                span = pl.ds(pl.multiple_of(i * 128, 128), 128)
                normed[index, span] = normalize(source[span].astype(F32))[0].astype(LOW)

            stay(normed.at[index], normed_out.at[index])

        def relay(i):
            far_made[i].wait_recv()
            return copies.start(land.at[2, parts[i]], land.at[3, parts[i]], at.mate)

        def mix_rows(index):
            @pl.loop(0, rows // 256)
            def _(i):
                span = pl.ds(pl.multiple_of(i * 256, 256), 256)
                turned = normed[index, span].astype(F32) * whole[0:1] + whole[1:2]
                weight = mix_land[...].reshape(width, width)
                mixed[index, span] = (nn(turned.astype(LOW), weight) + bias).astype(LOW)

            stay(mixed.at[index], mixed_out.at[index])

        norm_rows(hidden_ref, tensor)
        relayed = []
        for step in range(hops + 2):
            for item, hop in ((MIX, step), (VEC, step), (FC, step - 1), (PROJ, step - 2)):
                if 0 <= hop < hops:
                    handle(item, hop)
            if step == 0:
                launch(PROJ)
                mate_made.wait_recv()
                norm_rows(land.at[1], mate_row)
                relayed.append(relay(0))
            if step == 1:
                relayed.append(relay(1))
                norm_rows(land.at[2], far_row)
            if step == hops:
                mix_side.wait_recv()
                vec_side.wait_recv()
                settle(MIX)
                settle(VEC)
                whole = jnp.zeros((VEC_ROWS, width), F32)
                for i in range(n_dp):
                    whole += nn(tiles[i], one_hot(128, width, i * shard, shard))
                vec_out[...] = whole
                for i, block in enumerate((tensor, far_row)):
                    vec_out[12 + i : 13 + i] = units_row(whole[8:12], block, n_dp)
                lane = lax.broadcasted_iota(jnp.int32, (width, WIDE), 0)
                column = lax.broadcasted_iota(jnp.int32, (width, WIDE), 1)
                pick = (lane == column + tensor * (NH * HD)) & (column < NH * HD)
                picked = nn(whole.astype(LOW), pick.astype(LOW))
                bias = jnp.concatenate(
                    [picked[2:3], jnp.zeros((1, WIDE), F32), picked[3:4]], axis=1
                )
                mix_rows(tensor)
                mix_rows(mate_row)
        mix_rows(far_row)
        for copy in relayed:
            copy.wait_recv()
        norm_rows(land.at[3], corner_row)
        mix_rows(corner_row)
        stay(mix_land, mix_out)
        weight = mix_land[...].reshape(width, width)
        for part in range(3):
            low = part * WIDE + WIDE - 128
            turned = weight[:, low : low + 128].T
            out_turned[part * HD : (part + 1) * HD] = turned[128 - HD :]
        stay(out_turned, out_out)
        settle(FC)
        for copy in fc_sides:
            copy.wait_recv()
        cot_made.wait_recv()
        copies.finish()
        for copy in stays:
            copy.wait()

    low = lambda *shape: jax.ShapeDtypeStruct(shape, LOW)
    outputs = (
        low(4, rows, width), low(4, rows, width), low(n_dp, shard, width),
        low(line, shard, width), low(line, shard, width), low(line, shard, width),
        low(line, shard, width), low(rows, width), low(NH * HD, width), low(rows, width),
        jax.ShapeDtypeStruct((VEC_ROWS, width), F32),
        jax.ShapeDtypeStruct((latents, 128), jnp.int32),
    )
    scratch = [
        pltpu.VMEM((rows, width), LOW),
        pltpu.VMEM((shard, 3 * WIDE), LOW),
        pltpu.VMEM((VEC_ROWS, 128), LOW),
        pltpu.VMEM((VEC_ROWS, 128), F32),
        pltpu.VMEM((4, rows, width), LOW),
        pltpu.VMEM((n_dp, shard, width), LOW),
        pltpu.VMEM((n_dp, VEC_ROWS, 128), LOW),
        pltpu.VMEM((3, VEC_ROWS, 128), LOW),
        pltpu.VMEM((4, rows, width), LOW),
        pltpu.VMEM((4, rows, width), LOW),
        pltpu.VMEM((NH * HD, width), LOW),
    ]
    given = (fc, tokens, thoughts, proj, qkv, out, *vectors)
    scratch += [pltpu.VMEM(x.shape, x.dtype) for x in given]
    scratch.append(pltpu.SemaphoreType.DMA((len(given),)))
    return comm_call(
        kernel,
        "gather_inputs",
        outputs,
        (positions, tokens, thoughts, cotangent, fc, proj, qkv, out, *vectors),
        [SM] + [ANY] * (7 + len(vectors)),
        (ANY,) * 10 + (VM, VM),
        3 + 2 + 1 + 2 + 2 + 1 + 2 + hops * (2 * 4 + 2 * 4),
        0,
        scratch=scratch,
        local=3 + 8 + 2,
    )


def after_attention(attended, out_own, out_far, hidden, vec_all, n_dp, cid):
    head_width, slots = attended.shape
    rows, width = hidden.shape
    half_rows = rows // 2

    def kernel(
        heads_in, own_in, far_in, hidden_in, vec_ref,
        both_out, middle_out, two_out,
        heads_ref, own_ref, far_ref, hidden_ref,
        land, part, part_low, part_land, two, send, recv, local,
    ):
        loads = [
            pltpu.make_async_copy(source, target, local.at[5 + i])
            for i, (source, target) in enumerate(
                (
                    (heads_in, heads_ref), (own_in, own_ref), (far_in, far_ref),
                    (hidden_in, hidden_ref),
                )
            )
        ]
        for copy in loads:
            copy.start()
        at = Place(n_dp // 2)
        greet([(at.far, None), (at.mate, None)])
        copies = Copies(send, recv)
        cores = (at.core, 1 - at.core)
        made = [None, None]
        for i in (1, 0):
            theirs = pl.multiple_of(((1 - at.chip) * 2 + cores[i]) * rows, rows)
            made[i] = copies.start(heads_in.at[:, pl.ds(theirs, rows)], land.at[i], at.far)
        stays = []

        def stay(source, target):
            stays.append(pltpu.make_async_copy(source, target, local.at[len(stays)]))
            stays[-1].start()

        spans = []
        for copy in loads:
            copy.wait()
        for i in range(2):
            ours = pl.multiple_of((at.chip * 2 + cores[i]) * rows, rows)
            spans.append(pl.ds(ours, rows))
            stay(heads_ref.at[:, spans[i]], both_out.at[0, :, i * rows : (i + 1) * rows])
            part[i] = tn(heads_ref[:, spans[i]], own_ref[...])
        sums = None
        for i in (1, 0):
            made[i].wait_recv()
            stay(land.at[i], both_out.at[1, :, i * rows : (i + 1) * rows])
            part[i] += tn(land[i], far_ref[...])
            if i == 1:
                part_low[...] = part[1].astype(LOW)
                sums = copies.start(part_low, part_land, at.mate)
        sums.wait_recv()
        mated = []
        for piece in range(2):

            @pl.loop(0, half_rows // 128)
            def _(i):
                span = pl.ds(pl.multiple_of(piece * half_rows + i * 128, 128), 128)
                middle = (
                    hidden_ref[span].astype(F32)
                    + part[0, span]
                    + part_land[span].astype(F32)
                    + vec_ref[4:5]
                )
                middle_out[span] = middle
                two[span] = (normalize(middle)[0] * vec_ref[5:6] + vec_ref[6:7]).astype(LOW)

            span = pl.ds(piece * half_rows, half_rows)
            mated.append(copies.start(two.at[span], two_out.at[1, span], at.mate))
        stay(two, two_out.at[0])
        for copy in mated:
            copy.wait_recv()
        copies.finish()
        for copy in stays:
            copy.wait()

    return comm_call(
        kernel,
        "after_attention",
        (
            jax.ShapeDtypeStruct((2, head_width, 2 * rows), LOW),
            jax.ShapeDtypeStruct((rows, width), F32),
            jax.ShapeDtypeStruct((2, rows, width), LOW),
        ),
        (attended, out_own, out_far, hidden, vec_all),
        [ANY] * 4 + [VM],
        (ANY, VM, ANY),
        5,
        cid,
        scratch=[pltpu.VMEM(x.shape, x.dtype) for x in (attended, out_own, out_far, hidden)]
        + [
            pltpu.VMEM((2, head_width, rows), LOW),
            pltpu.VMEM((2, rows, width), F32),
            pltpu.VMEM((rows, width), LOW),
            pltpu.VMEM((rows, width), LOW),
            pltpu.VMEM((rows, width), LOW),
        ],
        local=9,
    )


def before_attention_back(
    lengths, two, middle, cotangent, both, out_own, out_far, vec_all, pairs, n_dp, cid
):
    _, rows, width = two.shape
    head_width = out_own.shape[0]
    half_rows = rows // 2

    def kernel(
        lengths_ref, two_in, middle_in, cot_in, both_in, own_in, far_in, vec_ref,
        one_a, one_b, two_a, two_b,
        heads_out, grad_out, own_out, far_out, vec_out, sum_one, sum_two,
        two_ref, middle_ref, cot_ref, both_ref, own_ref, far_ref,
        two_land, mid, stay_heads, sent_heads, held, send, recv, local,
    ):
        at = Place(n_dp // 2)
        greet([(at.far, None), (at.mate, None)])
        copies = Copies(send, recv)
        halves = [pl.ds(0, half_rows), pl.ds(half_rows, half_rows)]
        loads = [
            pltpu.make_async_copy(ref, held.at[i], local.at[2 + i])
            for i, ref in enumerate((one_a, one_b, two_a, two_b))
        ]
        early = [
            pltpu.make_async_copy(source, target, local.at[6 + i])
            for i, (source, target) in enumerate(
                (
                    (two_in.at[0], two_ref), (middle_in, middle_ref), (cot_in, cot_ref),
                    (far_in, far_ref), (own_in, own_ref), (both_in, both_ref),
                )
            )
        ]
        sums = [copies.start(two_in.at[1, span], two_land.at[span], at.mate) for span in halves]
        for copy in early + loads:
            copy.start()
        vec_out[...] = jnp.zeros_like(vec_out)
        first_row = at.tensor * rows
        live = ends_of(lengths_ref)[-1]
        mated = []
        for copy in early:
            copy.wait()
        for piece in range(2):
            sums[piece].wait_recv()

            @pl.loop(0, half_rows // 128)
            def _(i):
                start = pl.multiple_of(piece * half_rows + i * 128, 128)
                span = pl.ds(start, 128)
                grad = two_ref[span].astype(F32) + two_land[span].astype(F32)
                normed, inverse = normalize(middle_ref[span])
                ids = first_row + start + lax.broadcasted_iota(jnp.int32, (128, 1), 0)
                final = jnp.where(ids < live, cot_ref[span].astype(F32), 0.0)
                total = final + norm_back(normed, inverse, grad, vec_ref[5:6])
                grad_out[span] = total
                mid[0, span] = total.astype(LOW)
                for row, term in ((4, total), (5, normed * grad), (6, grad), (7, final)):
                    vec_out[row : row + 1] += jnp.sum(term, axis=0, keepdims=True)

            mated.append(copies.start(mid.at[0, halves[piece]], mid.at[1, halves[piece]], at.mate))
        cores = (at.core, 1 - at.core)
        made, stays = [], []
        for i in range(2):
            if i == 1:
                for copy in mated:
                    copy.wait_recv()
            ours = pl.ds(pl.multiple_of((at.chip * 2 + cores[i]) * rows, rows), rows)
            sent_heads[i] = nt(far_ref[...], mid[i]).astype(LOW)
            made.append(copies.start(sent_heads.at[i], heads_out.at[:, ours], at.far))
            stay_heads[i] = nt(own_ref[...], mid[i]).astype(LOW)
            stays.append(
                pltpu.make_async_copy(stay_heads.at[i], heads_out.at[:, ours], local.at[i])
            )
            stays[-1].start()
        grads = mid[...].reshape(2 * rows, width)
        own_out[...] = nn(both_ref[0], grads).astype(LOW)
        far_out[...] = nn(both_ref[1], grads).astype(LOW)
        for copy in loads:
            copy.wait()
        sum_one[...] = (held[0].astype(F32) + held[1].astype(F32)).astype(LOW)
        sum_two[...] = (held[2].astype(F32) + held[3].astype(F32)).astype(LOW)
        for copy in made:
            copy.wait_recv()
        copies.finish()
        for copy in stays:
            copy.wait()

    return comm_call(
        kernel,
        "before_attention_back",
        (
            jax.ShapeDtypeStruct((head_width, 4 * rows), LOW),
            jax.ShapeDtypeStruct((rows, width), F32),
            jax.ShapeDtypeStruct((head_width, width), LOW),
            jax.ShapeDtypeStruct((head_width, width), LOW),
            jax.ShapeDtypeStruct((VEC_ROWS, width), F32),
            jax.ShapeDtypeStruct(pairs[0].shape, LOW),
            jax.ShapeDtypeStruct(pairs[0].shape, LOW),
        ),
        (lengths, two, middle, cotangent, both, out_own, out_far, vec_all, *pairs),
        [SM] + [ANY] * 6 + [VM] + [ANY] * 4,
        (ANY,) + (VM,) * 6,
        6,
        cid,
        scratch=[pltpu.VMEM((rows, width), LOW)]
        + [pltpu.VMEM(x.shape, x.dtype) for x in (middle, cotangent, both, out_own, out_far)]
        + [
            pltpu.VMEM((rows, width), LOW),
            pltpu.VMEM((2, rows, width), LOW),
            pltpu.VMEM((2, head_width, rows), LOW),
            pltpu.VMEM((2, head_width, rows), LOW),
            pltpu.VMEM((4,) + pairs[0].shape, LOW),
        ],
        local=12,
    )


def finish_grads(lengths, arrays, n_dp, cid):
    part_rows = arrays["hidden"].shape[0] // 4
    names = list(arrays)
    kept = [name for name in names if name != "out_far"]
    line = n_dp // 2
    shard = arrays["mix"].shape[1]
    rows, width = arrays["hidden"].shape
    group = 4 * rows
    latents = arrays["positions"].shape[0]
    window = rows // latents
    far_end = line - 1
    slots = [(distance, way) for distance in range(far_end, 0, -1) for way in (0, 1)] + [(0, 0)]
    last = len(slots) - 1
    share = width // (n_dp * 4)
    FC, PROJ, MIX, VEC = range(4)

    def kernel(lengths_ref, *refs):
        refs = list(refs)

        def take(number):
            taken = refs[:number]
            del refs[:number]
            return taken

        source = dict(zip(names, take(len(names))))
        fc_out, proj_out, mix_out, vec_out, tokens_out, thoughts_out, block_out = take(7)
        held = dict(zip(kept, take(len(kept))))
        cross_send, cross_land = [None, None] + take(2), [None, None] + take(2)
        hop_send, hop_land = take(4), take(4)
        (
            part, mate_land, far_send, far_land, last_land, total, vec_mine, vec_land, vec_near,
            plain_sum, column_sum, out_land, tokens_kept, thoughts_kept, block_kept, send, recv,
            local,
        ) = refs
        out = [fc_out, proj_out, mix_out, None]
        at = Place(line)
        tensor, spot, side = at.tensor, at.spot, at.side
        mate_row, far_row, corner_row = at.mate[1], at.far[1], at.corner[1]
        copies = Copies(send, recv)
        loads = {}
        held["out_far"] = out_land
        for i, name in enumerate(kept):
            loads[name] = pltpu.make_async_copy(source[name], held[name], local.at[i])

        def load(*group):
            for name in group:
                loads[name].start()

        load("fc_near", "fc_near_side", "fc_cross", "proj_near", "proj_near_far", "proj_cross")
        load("grad_mixed", "mix")
        greet(at.everyone())

        def block_of(slot):
            distance, way = slots[slot]
            if way == 0:
                return jnp.minimum(spot + distance, far_end), spot + distance < line
            return jnp.maximum(spot - distance, 0), spot - distance >= 0

        crosses, hops = [], []
        for slot in range(len(slots)):
            block, _ = block_of(slot)
            crosses.append(
                {
                    i: copies.plan(cross_send[i].at[block], cross_land[i].at[block], at.across)
                    for i in (MIX, VEC)
                }
            )
            if slot < last:
                hops.append(
                    [
                        copies.plan(
                            hop_send[i].at[slot],
                            hop_land[i].at[slot],
                            (at.up, at.down)[slots[slot][1]],
                        )
                        for i in range(4)
                    ]
                )

        def cross(distance, items):
            for slot in range(len(slots)):
                if slots[slot][0] == distance:
                    for i in items:
                        copies.begin(crosses[slot][i], block_of(slot)[1])

        terms = (
            ("fc_near", "fc_near_side", "fc_cross"),
            ("proj_near", "proj_near_far", "proj_cross"),
        )

        def own_term(i, block):
            if i in (FC, PROJ):
                return sum(held[name][block].astype(F32) for name in terms[i])
            if i == MIX:
                return total[block * 2 + side].astype(F32)
            return vec_near[block * 2 + side]

        def handle(slot, i):
            block, inside = block_of(slot)
            behind = (at.has_down, at.has_up)[slots[slot][1]]
            outer = slot - 2

            def work():
                value = own_term(i, block)
                if i in (MIX, VEC):
                    crosses[slot][i].wait_recv()
                    value = value + cross_land[i][block].astype(F32)
                if outer < 0:
                    hop_send[i][slot] = value.astype(hop_send[i].dtype)
                    return

                @pl.when(behind)
                def _():
                    hops[outer][i].wait_recv()
                    hop_send[i][slot] = (value + hop_land[i][outer].astype(F32)).astype(
                        hop_send[i].dtype
                    )

                @pl.when(jnp.logical_not(behind))
                def _():
                    hop_send[i][slot] = value.astype(hop_send[i].dtype)

            when(inside, work)
            copies.begin(hops[slot][i], inside)

        def handle_all(distance, items):
            for slot in range(last):
                if slots[slot][0] == distance:
                    for i in items:
                        handle(slot, i)

        def close(i, target):
            value = own_term(i, spot)
            if i in (MIX, VEC):
                crosses[last][i].wait_recv()
                value = value + cross_land[i][spot].astype(F32)
            target[...] = value
            for way, behind in enumerate((at.has_down, at.has_up)):

                def add(way=way):
                    hops[last - 2 + way][i].wait_recv()
                    target[...] += hop_land[i][last - 2 + way].astype(F32)

                when(behind, add)

        for name in ("fc_near", "fc_near_side", "fc_cross", "proj_near", "proj_near_far", "proj_cross"):
            loads[name].wait()
        out_made = copies.start(source["out_far"], out_land, at.far)
        handle_all(far_end, (FC, PROJ))
        load("group", "out_own", "vec_all", "vec_part", "bias_own", "bias_far")
        load("last", "hidden", "grad_middle", "middle", "positions")
        loads["grad_mixed"].wait()
        loads["mix"].wait()

        def row_part(index):
            @pl.loop(0, rows // 256)
            def _(i):
                span = pl.ds(pl.multiple_of(i * 256, 256), 256)
                weight = held["mix"][...].reshape(width, width)
                part[index, span] = nt(held["grad_mixed"][index, span], weight).astype(LOW)

        for name in ("group", "out_own", "vec_all", "vec_part", "bias_own", "bias_far"):
            loads[name].wait()

        plain_sum[...] = jnp.zeros_like(plain_sum)
        column_sum[...] = jnp.zeros_like(column_sum)

        @pl.loop(0, group // 256)
        def _(i):
            block, start = i // (rows // 256), (i % (rows // 256)) * 256
            span = pl.ds(pl.multiple_of(start, 256), 256)
            grad = held["grad_mixed"][block, span]
            plain_sum[...] += tn(held["group"][block, span], grad)
            column_sum[...] += jnp.sum(grad.astype(F32), axis=0, keepdims=True)

        row_part(corner_row)
        mate_far = copies.start(part.at[corner_row], mate_land.at[1], at.mate)
        row_part(mate_row)
        mate_own = copies.start(part.at[mate_row], mate_land.at[0], at.mate)
        if far_end > 1:
            handle_all(far_end - 1, (FC, PROJ))
        out_made.wait_recv()
        plain, columns = plain_sum[...], column_sum[...]
        turned = held["vec_all"][...].T
        weight = held["mix"][...].reshape(width, width).astype(F32)
        gain_grad = jnp.sum(plain * weight, axis=1, keepdims=True)
        shift_grad = jnp.sum(weight * columns, axis=1, keepdims=True)
        scaled = plain * turned[:, 0:1] + turned[:, 1:2] * columns
        extras = []
        out_sum = held["out_own"][...].astype(F32) + held["out_far"][...].astype(F32)
        for p in range(3):
            piece = out_sum[p * HD : (p + 1) * HD]
            extras.append(jnp.zeros((width, WIDE - 128), F32))
            extras.append(jnp.concatenate([jnp.zeros((128 - HD, width), F32), piece], axis=0).T)
        scaled = scaled + jnp.concatenate(extras, axis=1)
        for k in range(n_dp):
            total[k] = scaled[k * shard : (k + 1) * shard].astype(LOW)
        for block in range(line):
            cross_send[MIX][block] = total[block * 2 + 1 - side]
        cross(far_end, [MIX])
        cross(far_end - 1, [MIX])
        row_part(far_row)
        mate_far.wait_recv()
        far_made = []

        def send_far(count):
            for i in range(len(far_made), min(len(far_made) + count, 8)):
                span = pl.ds(i * (part_rows // 2), part_rows // 2)
                far_send[span] = (
                    mate_land[1, span].astype(F32) + part[far_row, span].astype(F32)
                ).astype(LOW)
                far_made.append(copies.start(far_send.at[span], far_land.at[span], at.far))

        send_far(2)
        row_part(tensor)
        send_far(1)
        loads["last"].wait()
        last_copy = copies.start(held["last"].at[1], last_land, at.mate)
        vec_mine[...] = held["vec_part"][...]
        flat = jnp.concatenate(
            [gain_grad, shift_grad, jnp.zeros((width, 6), F32)], axis=1
        ).T
        vec_mine[0:2] = flat[0:2]
        vec_mine[8:12] = units_rows_back(held["bias_own"][...], tensor, n_dp) + units_rows_back(
            held["bias_far"][...], far_row, n_dp
        )
        vec_lane = lax.broadcasted_iota(jnp.int32, (1, width), 1)
        in_part = (vec_lane >= tensor * (NH * HD)) & (vec_lane < (tensor + 1) * (NH * HD))
        for row, low in ((2, 0), (3, 2 * WIDE)):
            line_up = jnp.concatenate([columns[:, low : low + WIDE]] + [columns[:, 0:WIDE]] * 2, axis=1)
            placed = jnp.zeros((1, width), F32)
            for t in range(4):
                shifted = pltpu.roll(line_up, t * NH * HD, 1)
                placed = jnp.where(tensor == t, shifted, placed)
            vec_mine[row : row + 1] = jnp.where(in_part, placed, 0.0)
        vec_made = [
            copies.start(vec_mine, vec_land.at[i], device)
            for i, device in enumerate((at.mate, at.far, at.corner))
        ]
        handle_all(far_end, [MIX])
        if far_end >= 2:
            cross(far_end - 2, [MIX])
        send_far(2)
        for distance in range(far_end - 2, 0, -1):
            handle_all(distance, (FC, PROJ))
        send_far(1)
        for copy in vec_made:
            copy.wait_recv()
        send_far(1)
        vec_sum = vec_mine[...] + vec_land[0] + vec_land[1] + vec_land[2]
        for k in range(n_dp):
            vec_near[k] = pltpu.roll(vec_sum, (width - k * shard) % width, 1)[:, 0:128]
        for block in range(line):
            cross_send[VEC][block] = vec_near[block * 2 + 1 - side]
        cross(far_end, [VEC])
        cross(far_end - 1, [VEC])
        send_far(8)
        live = ends_of(lengths_ref)[-1]
        stays = []

        def close_rows(i):
            if i == 0:
                for name in ("hidden", "grad_middle", "middle", "positions"):
                    loads[name].wait()
                last_copy.wait_recv()
                mate_own.wait_recv()
            far_made[2 * i].wait_recv()
            far_made[2 * i + 1].wait_recv()
            span = pl.ds(i * part_rows, part_rows)
            ids = tensor * rows + i * part_rows + lax.broadcasted_iota(
                jnp.int32, (part_rows, 1), 0
            )
            final = (
                held["middle"][span]
                + held["last"][0, span].astype(F32)
                + last_land[span].astype(F32)
                + held["vec_all"][7:8]
            )
            block_kept[span] = jnp.where(ids < live, final, 0.0).astype(LOW)
            grad = (
                part[tensor, span].astype(F32)
                + mate_land[0, span].astype(F32)
                + far_land[span].astype(F32)
            )
            normed, inverse = normalize(held["hidden"][span].astype(F32))
            grad = held["grad_middle"][span] + norm_back(
                normed, inverse, grad, held["vec_all"][0:1]
            )
            for w in range(part_rows // window):
                index = i * (part_rows // window) + w
                here = (
                    lax.broadcasted_iota(jnp.int32, (window, 1), 0)
                    == held["positions"][index : index + 1, 0:1] - index * window
                )
                piece = grad[w * window : (w + 1) * window]
                tokens_kept[pl.ds(index * window, window)] = jnp.where(here, 0.0, piece)
                thoughts_kept[index : index + 1] = jnp.sum(
                    jnp.where(here, piece, 0.0), axis=0, keepdims=True
                )
            moves = [(tokens_kept.at[span], tokens_out.at[span])]
            moves.append((block_kept.at[span], block_out.at[span]))
            if i == 3:
                moves.append((thoughts_kept, thoughts_out))
            for kept_ref, out_ref in moves:
                stays.append(
                    pltpu.make_async_copy(kept_ref, out_ref, local.at[len(kept) + len(stays)])
                )
                stays[-1].start()

        done = 0
        for distance in range(far_end, 0, -1):
            items = (MIX, VEC) if distance < far_end else (VEC,)
            handle_all(distance, items)
            if distance >= 2:
                cross(distance - 2, items)
            if distance <= 3:
                close_rows(done)
                done += 1
        for i in range(done, 4):
            close_rows(i)
        for i in (FC, PROJ, MIX):
            close(i, out[i])
        close(VEC, vec_out)
        copies.finish()
        for copy in stays:
            copy.wait()

    f32 = lambda *shape: jax.ShapeDtypeStruct(shape, F32)
    outputs = (
        f32(shard, width), f32(shard, width), f32(shard, width), f32(VEC_ROWS, 128),
        f32(rows, width), f32(latents, width), jax.ShapeDtypeStruct((rows, width), LOW),
    )
    scratch = [pltpu.VMEM(arrays[name].shape, arrays[name].dtype) for name in kept]
    for number, wide in ((line, 1), (line, 1), (last, 3), (last, 3)):
        scratch += [pltpu.VMEM((number, shard, width), LOW)] * wide
        scratch.append(pltpu.VMEM((number, VEC_ROWS, 128), F32))
    scratch += [
        pltpu.VMEM((4, rows, width), LOW),
        pltpu.VMEM((2, rows, width), LOW),
        pltpu.VMEM((rows, width), LOW),
        pltpu.VMEM((rows, width), LOW),
        pltpu.VMEM((rows, width), LOW),
        pltpu.VMEM((n_dp, shard, width), LOW),
        pltpu.VMEM((VEC_ROWS, width), F32),
        pltpu.VMEM((3, VEC_ROWS, width), F32),
        pltpu.VMEM((n_dp, VEC_ROWS, 128), F32),
        pltpu.VMEM((width, width), F32),
        pltpu.VMEM((1, width), F32),
        pltpu.VMEM(arrays["out_far"].shape, LOW),
        pltpu.VMEM((rows, width), F32),
        pltpu.VMEM((latents, width), F32),
        pltpu.VMEM((rows, width), LOW),
    ]
    return comm_call(
        kernel,
        "finish_grads",
        outputs,
        (lengths, *arrays.values()),
        [SM] + [ANY] * len(names),
        (VM,) * 4 + (ANY,) * 3,
        (last + 1) * 2 + last * 4 + 1 + 2 + 8 + 3 + 1,
        cid,
        scratch=scratch,
        local=len(kept) + 9,
    )


def unit_kernel(add, line, bias_row, lengths_ref, *refs):
    refs = list(refs)
    rows_ref, grad_own, grad_mate = refs[:3]
    pieces, vec_ref = refs[3:7], refs[7]
    refs = refs[8:]
    if add:
        last_in, two_in = refs[:2]
        refs = refs[2:]
    last_ref, two_ref, fc_near, fc_side, proj_near, proj_side, bias_grad_ref = refs[:7]
    fc_all, proj_all, fc_sum, proj_sum = refs[7:]
    step = pl.program_id(0)
    side, tensor = lax.axis_index("dp") % 2, lax.axis_index("tensor")
    live = ends_of(lengths_ref)[-1]

    @pl.when(step == 0)
    def _():
        for full, near, across in ((fc_all, *pieces[:2]), (proj_all, *pieces[2:])):
            for i in range(line):
                full[2 * i + side] = near[i]
                full[2 * i + 1 - side] = across[i]
        fc_sum[...] = jnp.zeros_like(fc_sum)
        proj_sum[...] = jnp.zeros_like(proj_sum)
        bias_grad_ref[...] = jnp.zeros_like(bias_grad_ref)

    count, width = rows_ref.shape
    half = pl.num_programs(0) // 2
    block = jnp.where(step < half, tensor, tensor + 1 - 2 * (tensor % 2))
    first = block * (half * count) + (step % half) * count
    alive = first + lax.broadcasted_iota(jnp.int32, (count, 1), 0) < live
    rows = rows_ref[...]
    grad = jnp.where(step < half, grad_own[...], grad_mate[...])
    grad = jnp.where(alive, grad, jnp.zeros_like(grad))
    fc = fc_all[...].reshape(width, -1)
    proj = proj_all[...].reshape(width, -1)
    inner = nn(rows, fc) + vec_ref[bias_row : bias_row + 1]
    square = inner * inner
    bend = jnp.tanh(GELU_SCALE * inner * (1.0 + GELU_CUBE * square))
    half = 0.5 * (1.0 + bend)
    activated = (inner * half).astype(LOW)
    slope = half + 0.5 * inner * (1.0 - bend * bend) * GELU_SCALE * (1.0 + 3.0 * GELU_CUBE * square)
    grad_inner = (nn(grad, proj) * slope).astype(LOW)
    last = nt(activated, proj)
    two = nt(grad_inner, fc)
    if add:
        last, two = last + last_in[...], two + two_in[...]
    last_ref[...] = last.astype(last_ref.dtype)
    two_ref[...] = two.astype(two_ref.dtype)
    fc_sum[...] += tn(rows, grad_inner)
    proj_sum[...] += tn(grad, activated)
    bias_grad_ref[...] += jnp.sum(grad_inner.astype(F32), axis=0, keepdims=True)

    @pl.when(step == pl.num_programs(0) - 1)
    def _():
        shard = fc_near.shape[1]
        for sums, near, across in ((fc_sum, fc_near, fc_side), (proj_sum, proj_near, proj_side)):
            for i in range(line):
                even = sums[2 * i * shard : (2 * i + 1) * shard].astype(LOW)
                odd = sums[(2 * i + 1) * shard : (2 * i + 2) * shard].astype(LOW)
                near[i] = jnp.where(side == 0, even, odd)
                across[i] = jnp.where(side == 0, odd, even)


def units_both_ways(lengths, rows, grad, mate_grad, pieces, vec_all, bias_row, before):
    count, width = rows.shape
    line, shard, units = pieces[0].shape
    half = count // ROW_TILE // 2
    tile = pl.BlockSpec((ROW_TILE, width), lambda i: (i, 0))
    fixed = lambda shape: pl.BlockSpec(shape, lambda i: (0,) * len(shape))
    add = before is not None
    kind = LOW if add else F32
    return pl.pallas_call(
        functools.partial(unit_kernel, add, line, bias_row),
        grid=(count // ROW_TILE,),
        out_shape=(
            jax.ShapeDtypeStruct((count, width), kind),
            jax.ShapeDtypeStruct((count, width), kind),
        )
        + (jax.ShapeDtypeStruct((line, shard, units), LOW),) * 4
        + (jax.ShapeDtypeStruct((1, units), F32),        ),
        in_specs=[
            SM,
            tile,
            pl.BlockSpec((ROW_TILE, width), lambda i: (jnp.minimum(i, half - 1), 0)),
            pl.BlockSpec((ROW_TILE, width), lambda i: (jnp.maximum(i - half, 0), 0)),
        ]
        + [fixed((line, shard, units))] * 4
        + [fixed(vec_all.shape)]
        + [tile] * (2 if add else 0),
        out_specs=(tile, tile) + (fixed((line, shard, units)),) * 4 + (fixed((1, units)),),
        scratch_shapes=[pltpu.VMEM((2 * line, shard, units), LOW)] * 2
        + [pltpu.VMEM((width, units), F32)] * 2,
        compiler_params=pltpu.CompilerParams(
            dimension_semantics=("arbitrary",), vmem_limit_bytes=VMEM_LIMIT
        ),
        cost_estimate=pl.CostEstimate(
            flops=12 * count * width * units,
            bytes_accessed=24 * count * width,
            transcendentals=count * units,
        ),
        name="units_second" if add else "units_first",
    )(lengths, rows, grad, mate_grad, *pieces, vec_all, *(before or ()))


def split_grads(mix_grad, vec, through, share):
    shard, width = mix_grad.shape
    head_width = NH * HD
    count = len(through)
    pieces_of = []
    for i, array in enumerate(through):
        size = 128 if array.shape[0] % 128 == 0 else array.shape[0]
        pieces_of += [(i, row, size) for row in range(0, array.shape[0], size)]

    def kernel(mix_ref, vec_ref, *refs):
        given, (qkv_out, out_out), refs = refs[:count], refs[count : count + 2], refs[count + 2 :]
        small, passed, held, sems = refs[:8], refs[8 : 8 + count], refs[8 + count : -1], refs[-1]
        ins, outs = [], []
        for i, row, size in pieces_of:
            span = pl.ds(row, size)
            ins.append(
                pltpu.make_async_copy(
                    given[i].at[span], held[i].at[span], sems.at[0, len(ins)]
                )
            )
            outs.append(
                pltpu.make_async_copy(
                    held[i].at[span], passed[i].at[span], sems.at[1, len(outs)]
                )
            )
        for copy in ins:
            copy.start()
        for i in range(len(ins)):
            ins[i].wait()
            outs[i].start()
        tensor = lax.axis_index("tensor")
        turned = mix_ref[...].T
        pieces = []
        for h in range(NH):
            for part in range(3):
                low = part * WIDE + h * HD
                pieces.append(turned[low : low + HD])
        qkv_out[...] = jnp.concatenate(pieces, axis=0).T
        for part in range(3):
            low = part * WIDE + head_width
            out_out[part * HD : (part + 1) * HD] = turned[low : low + HD]
        rows = vec_ref[0:8]
        moved = rows
        for i in range(1, 4):
            moved = jnp.where(tensor == i, pltpu.roll(rows, 128 - i * share, 1), moved)
        for i, row in enumerate((0, 1, 4, 5, 6, 7)):
            small[i][...] = moved[row : row + 1, 0:share]
        small[6][...] = moved[2:4, 0:share]
        small[7][...] = vec_ref[pl.ds(8 + tensor, 1)][:, 0:shard]
        for copy in outs:
            copy.wait()

    f32 = lambda *shape: jax.ShapeDtypeStruct(shape, F32)
    return pl.pallas_call(
        kernel,
        out_shape=(f32(shard, 3 * head_width), f32(head_width, shard))
        + (f32(1, share),) * 6
        + (f32(2, share), f32(1, shard))
        + tuple(jax.ShapeDtypeStruct(x.shape, x.dtype) for x in through),
        in_specs=[VM] * 2 + [ANY] * count,
        out_specs=(VM,) * 10 + (ANY,) * count,
        scratch_shapes=[pltpu.VMEM(x.shape, x.dtype) for x in through]
        + [pltpu.SemaphoreType.DMA((2, len(pieces_of)))],
        compiler_params=pltpu.CompilerParams(vmem_limit_bytes=VMEM_LIMIT),
        name="split_grads",
    )(mix_grad, vec, *through)


def by_tensor(row, step, index):
    moved = row
    for i in range(1, 4):
        moved = jnp.where(index == i, pltpu.roll(row, (i * step) % row.shape[1], 1), moved)
    return moved


def units_row(rows, block, n_dp):
    width = rows.shape[1]
    shard, step = width // n_dp, n_dp // 4
    lane = lax.broadcasted_iota(jnp.int32, (1, width), 1) // shard
    base = by_tensor(rows, width - step * shard, block)
    total = jnp.zeros((1, width), F32)
    for j in range(n_dp):
        moved = pltpu.roll(base[j % 4 : j % 4 + 1], (j - j // 4) * shard, 1)
        total = jnp.where(lane == j, moved, total)
    return total


def units_rows_back(row, block, n_dp):
    width = row.shape[1]
    shard, step = width // n_dp, n_dp // 4
    lane = lax.broadcasted_iota(jnp.int32, (1, width), 1) // shard
    rows = [jnp.zeros((1, width), F32) for _ in range(4)]
    for j in range(n_dp):
        moved = pltpu.roll(row, (width - (j - j // 4) * shard) % width, 1)
        rows[j % 4] = jnp.where(lane == j // 4, moved, rows[j % 4])
    return by_tensor(jnp.concatenate(rows, axis=0), step * shard, block)


def normalize(values):
    center = jnp.mean(values, axis=-1, keepdims=True)
    offset = values - center
    spread = jnp.mean(offset * offset, axis=-1, keepdims=True)
    inverse = lax.rsqrt(spread + EPSILON)
    return offset * inverse, inverse


def norm_back(normed, inverse, grad, gain):
    scaled = grad * gain
    center = jnp.mean(scaled, axis=-1, keepdims=True)
    along = jnp.mean(scaled * normed, axis=-1, keepdims=True)
    return inverse * (scaled - center - normed * along)


def product(equation, left, right):
    return jnp.einsum(equation, left, right, preferred_element_type=F32)


def per_device(
    tokens,
    thoughts,
    positions,
    lengths,
    attn_norm_gain,
    attn_norm_shift,
    qkv_weight,
    qv_bias,
    attn_out_weight,
    attn_out_bias,
    mlp_norm_gain,
    mlp_norm_shift,
    fc_weight,
    fc_bias,
    proj_weight,
    proj_bias,
    cotangent,
):
    n_dp = lax.axis_size("dp")
    n_tensor = lax.axis_size("tensor")
    rows, width = tokens.shape
    slots = rows * n_tensor
    swap_far = [(i, (i + 2) % n_tensor) for i in range(n_tensor)]

    share = width // (n_dp * n_tensor)
    small = [
        attn_norm_gain[None], attn_norm_shift[None], qv_bias, attn_out_bias[None],
        mlp_norm_gain[None], mlp_norm_shift[None], proj_bias[None], fc_bias[None],
    ]
    (
        group_low, mixed, mix_all, fc_near, fc_side, fc_far_near, proj_near, mate_grad, out_own,
        hidden, vec_all, places,
    ) = gather_inputs(
        tokens, thoughts, positions, cotangent, fc_weight, proj_weight.T, qkv_weight,
        attn_out_weight, small, n_dp,
    )
    mixed = mixed.reshape(slots, -1)
    swap_side = [(i, i + 1 - 2 * (i % 2)) for i in range(n_dp)]
    out_far = lax.ppermute(out_own, "tensor", swap_far)
    proj_far_near = lax.ppermute(proj_near, "tensor", swap_far)
    fc_far_side = lax.ppermute(fc_far_near, "dp", swap_side)
    attended, stats = attend(lengths, mixed)
    sent, out_far, proj_far_near, fc_far_side = lax.optimization_barrier(
        (attended, out_far, proj_far_near, fc_far_side)
    )
    proj_far_side = lax.ppermute(proj_far_near, "dp", swap_side)
    both, middle, chip_two = after_attention(
        sent, out_own, out_far, hidden, vec_all, n_dp, 1
    )
    chip_two, proj_far_side, proj_sent = lax.optimization_barrier(
        (chip_two, proj_far_side, proj_near)
    )
    proj_side = lax.ppermute(proj_sent, "dp", swap_side)
    chip_two = chip_two.reshape(2 * rows, width)

    first = units_both_ways(
        lengths, chip_two, cotangent, mate_grad,
        (fc_far_near, fc_far_side, proj_far_near, proj_far_side), vec_all, 13, None,
    )
    far_fc_near, far_fc_side, far_proj_near, far_proj_side, far_fc_bias = first[2:]
    proj_side_far = lax.ppermute(far_proj_side, "tensor", swap_far)
    fc_far_side_in = lax.ppermute(far_fc_side, "dp", swap_side)
    second = units_both_ways(
        lengths, chip_two, cotangent, mate_grad, (fc_near, fc_side, proj_near, proj_side), vec_all, 12,
        first[:2],
    )
    last_part, grad_two_part, fc_near_grad, fc_side_grad, proj_near_grad, proj_side_grad = second[:6]
    fc_near_side_in = lax.ppermute(fc_side_grad, "dp", swap_side)
    grad_heads, grad_middle, grad_out, far_out, vec_part, fc_cross, proj_cross = before_attention_back(
        lengths, grad_two_part.reshape(2, rows, width), middle, cotangent, both, out_own, out_far,
        vec_all, (far_fc_near, fc_far_side_in, proj_side_grad, proj_side_far), n_dp, 2,
    )
    grad_heads, fc_cross, proj_cross, far_proj_near = lax.optimization_barrier(
        (grad_heads, fc_cross, proj_cross, far_proj_near)
    )
    fc_cross = lax.ppermute(fc_cross, "tensor", swap_far)
    proj_cross = lax.ppermute(proj_cross, "dp", swap_side)
    proj_near_far = lax.ppermute(far_proj_near, "tensor", swap_far)
    last_low = last_part.reshape(2, rows, width)

    grad_mixed = attend_back(lengths, mixed, attended, stats, grad_heads)
    arrays = {
        "fc_near": fc_near_grad, "fc_near_side": fc_near_side_in, "fc_cross": fc_cross,
        "proj_near": proj_near_grad, "proj_near_far": proj_near_far, "proj_cross": proj_cross,
        "grad_mixed": grad_mixed.reshape(n_tensor, rows, width), "mix": mix_all,
        "last": last_low, "group": group_low,
        "out_own": grad_out, "out_far": far_out,
        "vec_all": vec_all, "vec_part": vec_part, "bias_own": second[6], "bias_far": far_fc_bias,
        "hidden": hidden, "grad_middle": grad_middle, "middle": middle, "positions": places,
    }
    fc_grad, proj_grad, mix_grad, vec, grad_tokens, grad_thoughts, block_out = finish_grads(
        lengths, arrays, n_dp, 8
    )
    parts = split_grads(
        mix_grad, vec, (fc_grad, proj_grad, grad_tokens, grad_thoughts, block_out), share
    )
    qkv_grad, out_grad = parts[:2]
    gain_one, shift_one, out_bias, gain_two, shift_two, last_bias = [p[0] for p in parts[2:8]]
    query_value, hidden_bias = parts[8], parts[9][0]
    fc_grad, proj_grad, grad_tokens, grad_thoughts, block_out = parts[10:]
    return (
        block_out,
        grad_tokens,
        grad_thoughts,
        gain_one,
        shift_one,
        qkv_grad,
        query_value,
        out_grad,
        out_bias,
        gain_two,
        shift_two,
        fc_grad,
        hidden_bias,
        proj_grad.T,
        last_bias,
    )


def solution(mesh):
    rows = P(("dp", "tensor"), None)
    line = P(("dp", "tensor"))
    in_specs = (
        rows, rows, line, P("dp", None), line, line, P("dp", "tensor"),
        P(None, ("dp", "tensor")), P("tensor", "dp"), line, line, line,
        P("dp", "tensor"), line, P("tensor", "dp"), line, rows,
    )
    out_specs = (
        rows, rows, rows, line, line, P("dp", "tensor"), P(None, ("dp", "tensor")),
        P("tensor", "dp"), line, line, line, P("dp", "tensor"), line, P("tensor", "dp"), line,
    )
    return jax.shard_map(
        per_device, mesh=mesh, in_specs=in_specs, out_specs=out_specs, check_vma=False
    )
```

```python
import functools
import math

import jax
import jax.numpy as jnp
from jax import lax
from jax.experimental import pallas as pl
from jax.experimental.pallas import tpu as pltpu
from jax.sharding import PartitionSpec as P

H = 12
HD = 64
FF = 3072
SEQ_DEV = 3
EPSILON = 1e-05
MASKED = -1e30
NH = 3
SLABS = 2
WIDE = SLABS * 128
BQ = 512
BK = 512
VEC_ROWS = 16
VMEM_LIMIT = 67043328
ROW_TILE = 256
GELU_SCALE = math.sqrt(2.0 / math.pi)
GELU_CUBE = 0.044715
MESH = pl.DeviceIdType.MESH
ANY = pl.BlockSpec(memory_space=pltpu.HBM)
VM = pl.BlockSpec(memory_space=pltpu.VMEM)
SM = pl.BlockSpec(memory_space=pltpu.SMEM)
LOW = jnp.bfloat16
F32 = jnp.float32


def nn(a, b):
    return lax.dot_general(a, b, (((1,), (0,)), ((), ())), preferred_element_type=jnp.float32)


def nt(a, b):
    return lax.dot_general(a, b, (((1,), (1,)), ((), ())), preferred_element_type=jnp.float32)


def tn(a, b):
    return lax.dot_general(a, b, (((0,), (0,)), ((), ())), preferred_element_type=jnp.float32)


def head_rows(slab, head):
    half = slab[(head % 2) * HD : (head % 2 + 1) * HD]
    zero = jnp.zeros_like(half)
    return jnp.concatenate([half, zero] if head % 2 == 0 else [zero, half], axis=0)


def ends_of(lengths_ref):
    ends = [lengths_ref[0, 0]]
    for i in range(1, SEQ_DEV):
        ends.append(ends[-1] + lengths_ref[0, i])
    return ends


def segment_start(ends, slots):
    start = jnp.zeros_like(slots)
    for i in range(SEQ_DEV):
        start = jnp.where(slots >= ends[i], ends[i], start)
    return start


def segment_stop(ends, slot, slots):
    stop = slots
    for i in reversed(range(SEQ_DEV)):
        stop = jnp.where(slot < ends[i], ends[i], stop)
    return stop


def attend_kernel(
    lengths_ref, mixed_in, out_ref, stat_ref, mixed_ref, qt_ref, vt_ref, sems
):
    tokens = mixed_ref.shape[0]
    ends = ends_of(lengths_ref)
    count = (ends[-1] + BQ - 1) // BQ
    half = BQ // 2

    def load(block):
        rows = pl.ds(pl.multiple_of(block * BQ, BQ), BQ)
        return pltpu.make_async_copy(mixed_in.at[rows], mixed_ref.at[rows], sems.at[block])

    for block in range(tokens // BQ):
        load(block).start()

    def step(rows, keys, columns, queries, first, causal, state):
        size = queries[0].shape[1]
        slots = first + lax.broadcasted_iota(jnp.int32, (1, size), 1)
        start = segment_start(ends, slots)
        key_ids = rows + lax.broadcasted_iota(jnp.int32, (keys, size), 0)
        allowed = key_ids >= start
        if causal:
            allowed = allowed & (key_ids <= slots)
        span = pl.ds(rows, keys)
        result = []
        for h in range(NH):
            peak, total, acc = state[h]
            low = WIDE + (h // 2) * 128
            scores = nn(mixed_ref[span, low : low + 128], queries[h])
            scores = jnp.where(allowed, scores, MASKED)
            fresh = jnp.maximum(peak, jnp.max(scores, axis=0, keepdims=True))
            weight = jnp.exp(scores - fresh)
            decay = jnp.exp(peak - fresh)
            total = total * decay + jnp.sum(weight, axis=0, keepdims=True)
            values = vt_ref[h * HD : (h + 1) * HD, span]
            acc = acc * decay + nn(values, weight.astype(jnp.bfloat16))
            result.append((fresh, total, acc))
        return tuple(result)

    def query_block(block, carry):
        first = pl.multiple_of(block * BQ, BQ)
        columns = pl.ds(first, BQ)
        load(block).wait()
        for slab in range(SLABS):
            low = slab * 128
            qt_ref[low : low + 128] = (mixed_ref[columns, low : low + 128] * HD ** (-0.5)).T
            vt_ref[low : low + 128, columns] = mixed_ref[
                columns, 2 * WIDE + low : 2 * WIDE + low + 128
            ].T
        queries = [head_rows(qt_ref[(h // 2) * 128 : (h // 2 + 1) * 128], h) for h in range(NH)]

        def key_block(key, state):
            return step(pl.multiple_of(key * BK, BK), BK, columns, queries, first, False, state)

        empty = tuple(
            (
                jnp.full((1, BQ), MASKED, jnp.float32),
                jnp.zeros((1, BQ), jnp.float32),
                jnp.zeros((HD, BQ), jnp.float32),
            )
            for _ in range(NH)
        )
        state = lax.fori_loop(segment_start(ends, first) // BK, block, key_block, empty)
        for side, keys in ((0, half), (1, BQ)):
            piece = slice(side * half, (side + 1) * half)
            final = step(
                first, keys, columns, [q[:, piece] for q in queries], first + side * half, True,
                tuple(tuple(x[:, piece] for x in one) for one in state),
            )
            for h in range(NH):
                peak, total, acc = final[h]
                place_here = pl.ds(pl.multiple_of(first + side * half, half), half)
                out_ref[h * HD : (h + 1) * HD, place_here] = (acc / total).astype(jnp.bfloat16)
                stat_ref[h : h + 1, place_here] = peak + jnp.log(total)
        return carry

    lax.fori_loop(0, count, query_block, 0)

    def padded_block(block, carry):
        load(block).wait()
        columns = pl.ds(pl.multiple_of(block * BQ, BQ), BQ)
        out_ref[:, columns] = jnp.zeros((out_ref.shape[0], BQ), jnp.bfloat16)
        return carry

    lax.fori_loop(count, tokens // BQ, padded_block, 0)


def attend(lengths, mixed):
    tokens = mixed.shape[0]
    vm = pl.BlockSpec(memory_space=pltpu.VMEM)
    return pl.pallas_call(
        attend_kernel,
        out_shape=(
            jax.ShapeDtypeStruct((NH * HD, tokens), jnp.bfloat16),
            jax.ShapeDtypeStruct((8, tokens), jnp.float32),
        ),
        in_specs=[pl.BlockSpec(memory_space=pltpu.SMEM), pl.BlockSpec(memory_space=pltpu.HBM)],
        out_specs=(vm, vm),
        scratch_shapes=[
            pltpu.VMEM(mixed.shape, mixed.dtype),
            pltpu.VMEM((WIDE, BQ), jnp.bfloat16),
            pltpu.VMEM((WIDE, tokens), jnp.bfloat16),
            pltpu.SemaphoreType.DMA((tokens // BQ,)),
        ],
        compiler_params=pltpu.CompilerParams(vmem_limit_bytes=VMEM_LIMIT),
        cost_estimate=pl.CostEstimate(
            flops=8 * tokens * tokens * NH * HD,
            bytes_accessed=16 * tokens * WIDE,
            transcendentals=tokens * tokens,
        ),
        name="attend",
    )(lengths, mixed)


def attend_back_kernel(
    lengths_ref, mixed_in, out_in, stat_ref, gradt_in,
    gmixed_out, mixed_ref, out_ref, gradt_ref, gmixed_ref, qt_ref, kt_ref, grad_ref, delta_ref,
    dqt_ref, sems, out_sems
):
    tokens = mixed_ref.shape[0]
    blocks = tokens // BQ
    ends = ends_of(lengths_ref)
    count = (ends[-1] + BK - 1) // BK
    half = BQ // 2

    def loads(block):
        rows = pl.ds(pl.multiple_of(block * BQ, BQ), BQ)
        return (
            pltpu.make_async_copy(mixed_in.at[rows], mixed_ref.at[rows], sems.at[0, block]),
            pltpu.make_async_copy(out_in.at[:, rows], out_ref.at[:, rows], sems.at[1, block]),
            pltpu.make_async_copy(gradt_in.at[:, rows], gradt_ref.at[:, rows], sems.at[2, block]),
        )

    def leave(block, part):
        rows = pl.ds(pl.multiple_of(block * BQ, BQ), BQ)
        lanes = pl.ds(0, WIDE) if part == 0 else pl.ds(WIDE, 2 * WIDE)
        return pltpu.make_async_copy(
            gmixed_ref.at[rows, lanes], gmixed_out.at[rows, lanes], out_sems.at[part, block]
        )

    for block in reversed(range(blocks)):
        for copy in loads(block):
            copy.start()
    dqt_ref[...] = jnp.zeros_like(dqt_ref)

    def prepare_block(block):
        rows = pl.ds(pl.multiple_of(block * BQ, BQ), BQ)
        for slab in range(SLABS):
            low = slab * 128
            qt_ref[low : low + 128, rows] = (
                mixed_ref[rows, low : low + 128] * HD ** (-0.5)
            ).T
            kt_ref[low : low + 128, rows] = mixed_ref[rows, WIDE + low : WIDE + low + 128].T
        grad_ref[rows, 0:128] = gradt_ref[0:128, rows].T
        grad_ref[rows, 128:256] = jnp.concatenate(
            [gradt_ref[128:192, rows], jnp.zeros((64, BQ), jnp.bfloat16)], axis=0
        ).T
        for h in range(NH):
            product = gradt_ref[h * HD : (h + 1) * HD, rows].astype(jnp.float32) * out_ref[
                h * HD : (h + 1) * HD, rows
            ].astype(jnp.float32)
            delta_ref[h : h + 1, rows] = jnp.sum(product, axis=0, keepdims=True)

    def terms(base, keys, first, size, causal):
        rows, columns = pl.ds(base, keys), pl.ds(first, size)
        slots = first + lax.broadcasted_iota(jnp.int32, (1, size), 1)
        key_ids = base + lax.broadcasted_iota(jnp.int32, (keys, size), 0)
        allowed = key_ids >= segment_start(ends, slots)
        if causal:
            allowed = allowed & (key_ids <= slots)
        lane = lax.broadcasted_iota(jnp.int32, (size, 128), 1)
        grad_keys, grad_values = [None] * SLABS, [None] * SLABS
        for h in range(NH):
            slab = h // 2
            low, high = slab * 128, slab * 128 + 128
            queries = head_rows(qt_ref[low:high, columns], h)
            scores = nn(mixed_ref[rows, WIDE + low : WIDE + high], queries)
            probs = jnp.where(allowed, jnp.exp(scores - stat_ref[h : h + 1, columns]), 0.0)
            keep = (lane // HD) == (h % 2)
            value = nn(probs.astype(jnp.bfloat16), jnp.where(keep, grad_ref[columns, low:high], 0.0))
            if h == NH - 1 and NH % 2 == 1:
                grad_rows = jnp.concatenate(
                    [gradt_ref[h * HD : (h + 1) * HD, columns], jnp.zeros((HD, size), jnp.bfloat16)],
                    axis=0,
                )
            else:
                grad_rows = head_rows(gradt_ref[low:high, columns], h)
            grad_probs = nn(mixed_ref[rows, 2 * WIDE + low : 2 * WIDE + high], grad_rows)
            grad_scores = (probs * (grad_probs - delta_ref[h : h + 1, columns])).astype(
                jnp.bfloat16
            )
            key_term = nn(grad_scores, jnp.where(keep, mixed_ref[columns, low:high], 0.0))
            grad_values[slab] = value if grad_values[slab] is None else grad_values[slab] + value
            grad_keys[slab] = key_term if grad_keys[slab] is None else grad_keys[slab] + key_term
            dqt_ref[h * HD : (h + 1) * HD, columns] += nn(
                kt_ref[h * HD : (h + 1) * HD, rows], grad_scores
            )
        return grad_keys + grad_values

    def key_block(turn, carry):
        key = count - 1 - turn
        for copy in loads(key):
            copy.wait()
        prepare_block(key)
        base = pl.multiple_of(key * BK, BK)
        rows = pl.ds(base, BK)
        upper = terms(base, half, base, BQ, True)
        lower = terms(pl.multiple_of(base + half, half), half, pl.multiple_of(base + half, half), half, True)
        state = tuple(jnp.concatenate([a, b], axis=0) for a, b in zip(upper, lower))

        def query_block(block, state):
            fresh = terms(base, BK, pl.multiple_of(block * BQ, BQ), BQ, False)
            return tuple(a + b for a, b in zip(state, fresh))

        stop = jnp.minimum(segment_stop(ends, base + BK - 1, tokens), ends[-1])
        state = lax.fori_loop(key + 1, (stop - 1) // BQ + 1, query_block, state)
        for slab in range(SLABS):
            low = slab * 128
            gmixed_ref[rows, WIDE + low : WIDE + low + 128] = (
                state[slab] * HD ** (-0.5)
            ).astype(jnp.bfloat16)
            gmixed_ref[rows, 2 * WIDE + low : 2 * WIDE + low + 128] = state[SLABS + slab].astype(
                jnp.bfloat16
            )
        leave(key, 1).start()
        return carry

    def padded_block(key, carry):
        for copy in loads(key):
            copy.wait()
        rows = pl.ds(pl.multiple_of(key * BK, BK), BK)
        gmixed_ref[rows, WIDE:] = jnp.zeros((BK, 2 * WIDE), jnp.bfloat16)
        leave(key, 1).start()
        return carry

    lax.fori_loop(count, blocks, padded_block, 0)
    lax.fori_loop(0, count, key_block, 0)
    for block in range(blocks):
        rows = pl.ds(block * BQ, BQ)
        for slab in range(SLABS):
            low = slab * 128
            gmixed_ref[rows, low : low + 128] = (
                (dqt_ref[low : low + 128, rows] * HD ** (-0.5)).T.astype(jnp.bfloat16)
            )
        leave(block, 0).start()
    for block in range(blocks):
        leave(block, 0).wait()
        leave(block, 1).wait()


def attend_back(lengths, mixed, out, stat, gradt):
    tokens = mixed.shape[0]
    vm = pl.BlockSpec(memory_space=pltpu.VMEM)
    hbm = pl.BlockSpec(memory_space=pltpu.HBM)
    return pl.pallas_call(
        attend_back_kernel,
        out_shape=jax.ShapeDtypeStruct((tokens, 3 * WIDE), jnp.bfloat16),
        in_specs=[pl.BlockSpec(memory_space=pltpu.SMEM), hbm, hbm, vm, hbm],
        out_specs=hbm,
        scratch_shapes=[
            pltpu.VMEM(mixed.shape, jnp.bfloat16),
            pltpu.VMEM(out.shape, jnp.bfloat16),
            pltpu.VMEM(gradt.shape, jnp.bfloat16),
            pltpu.VMEM(mixed.shape, jnp.bfloat16),
            pltpu.VMEM((WIDE, tokens), jnp.bfloat16),
            pltpu.VMEM((WIDE, tokens), jnp.bfloat16),
            pltpu.VMEM((tokens, WIDE), jnp.bfloat16),
            pltpu.VMEM((8, tokens), jnp.float32),
            pltpu.VMEM((WIDE, tokens), jnp.float32),
            pltpu.SemaphoreType.DMA((3, tokens // BQ)),
            pltpu.SemaphoreType.DMA((2, tokens // BQ)),
        ],
        compiler_params=pltpu.CompilerParams(vmem_limit_bytes=VMEM_LIMIT),
        cost_estimate=pl.CostEstimate(
            flops=20 * tokens * tokens * NH * HD,
            bytes_accessed=32 * tokens * WIDE,
            transcendentals=tokens * tokens,
        ),
        name="attend_back",
    )(lengths, mixed, out, stat, gradt)


class Copies:
    def __init__(self, send, recv):
        self.send, self.recv, self.made, self.started = send, recv, 0, []

    def plan(self, source, target, device):
        index = self.made
        self.made += 1
        return pltpu.make_async_remote_copy(
            src_ref=source,
            dst_ref=target,
            send_sem=self.send.at[index],
            recv_sem=self.recv.at[index],
            device_id=device,
            device_id_type=MESH,
        )

    def begin(self, copy, condition=None):
        self.started.append((copy, condition))
        when(condition, copy.start)

    def start(self, source, target, device):
        copy = self.plan(source, target, device)
        self.begin(copy)
        return copy

    def finish(self):
        for copy, condition in self.started:
            when(condition, copy.wait_send)


class Several:
    def __init__(self, copies):
        self.copies = copies

    def start(self):
        for copy in self.copies:
            copy.start()

    def wait(self):
        for copy in self.copies:
            copy.wait()


def when(condition, action):
    if condition is None:
        action()
    else:
        pl.when(condition)(action)


def greet(devices):
    barrier = pltpu.get_barrier_semaphore()
    for device, condition in devices:
        when(
            condition,
            lambda device=device: pl.semaphore_signal(
                barrier, inc=1, device_id=device, device_id_type=MESH
            ),
        )
    present = [1 if condition is None else condition.astype(jnp.int32) for _, condition in devices]
    pl.semaphore_wait(barrier, sum(present))


class Place:
    def __init__(self, line):
        self.dp = dp = lax.axis_index("dp")
        self.tensor = tensor = lax.axis_index("tensor")
        self.spot, self.side = spot, side = dp // 2, dp % 2
        self.chip, self.core = tensor // 2, tensor % 2
        self.has_up, self.has_down = spot + 1 < line, spot > 0
        self.up = (jnp.minimum(spot + 1, line - 1) * 2 + side, tensor)
        self.down = (jnp.maximum(spot - 1, 0) * 2 + side, tensor)
        self.across = (spot * 2 + 1 - side, tensor)
        self.mate = (dp, tensor + 1 - 2 * (tensor % 2))
        self.far = (dp, (tensor + 2) % 4)
        self.corner = (dp, 3 - tensor)

    def everyone(self):
        return [
            (self.mate, None), (self.far, None), (self.corner, None), (self.across, None),
            (self.up, self.has_up), (self.down, self.has_down),
        ]


def comm_call(kernel, name, outputs, inputs, in_specs, out_specs, copies, cid, scratch=(), local=1, limit=VMEM_LIMIT):
    return pl.pallas_call(
        kernel,
        out_shape=outputs,
        in_specs=in_specs,
        out_specs=out_specs,
        scratch_shapes=list(scratch)
        + [
            pltpu.SemaphoreType.DMA((copies,)),
            pltpu.SemaphoreType.DMA((copies,)),
            pltpu.SemaphoreType.DMA((local,)),
        ],
        compiler_params=pltpu.CompilerParams(
            collective_id=cid, has_side_effects=True, vmem_limit_bytes=limit
        ),
        name=name,
    )(*inputs)


def one_hot(rows, columns, shift, limit):
    lane = lax.broadcasted_iota(jnp.int32, (rows, columns), 0)
    spot = lax.broadcasted_iota(jnp.int32, (rows, columns), 1)
    return ((spot == lane + shift) & (lane < limit)).astype(LOW)


def gather_inputs(tokens, thoughts, positions, cotangent, fc, proj, qkv, out, vectors, n_dp):
    line = n_dp // 2
    hops = line - 1
    rows, width = tokens.shape
    latents = thoughts.shape[0]
    window = rows // latents
    shard = fc.shape[0]
    half_rows = rows // 2
    share = width // (n_dp * 4)

    def kernel(
        pos_ref, tokens_in, thoughts_in, cot_ref, fc_in, proj_in, qkv_in, out_in, *refs
    ):
        given = (fc_in, tokens_in, thoughts_in, proj_in, qkv_in, out_in) + refs[: len(vectors)]
        (
            normed_out, mixed_out, mix_out, fc_near, fc_side, fc_far, proj_near, cot_out, out_out,
            hidden_out, vec_out, pos_out,
            hidden_ref, mix_ref, vec_ref, tile,
            land, mix_land, tiles, tile_land, normed, mixed, out_turned,
            *held, arrive, send, recv, local,
        ) = refs[len(vectors) :]
        arrivals = [
            pltpu.make_async_copy(given[i], held[i], arrive.at[i]) for i in range(len(given))
        ]
        for copy in arrivals:
            copy.start()
        fc_ref, tokens_ref, thoughts_ref, proj_ref, qkv_ref, out_ref = held[:6]
        vec_refs = held[6:]
        at = Place(line)
        dp, tensor, spot, side = at.dp, at.tensor, at.spot, at.side
        mate_row, far_row, corner_row = at.mate[1], at.far[1], at.corner[1]
        greet(at.everyone())
        copies = Copies(send, recv)
        MIX, FC, PROJ, VEC = range(4)
        own = [mix_ref, fc_ref, proj_ref, tiles.at[dp]]

        def seat(item, position):
            if item == MIX:
                return mix_land.at[position * 2 + side]
            if item == FC:
                return fc_near.at[position]
            if item == PROJ:
                return proj_near.at[position]
            return tiles.at[position * 2 + side]

        def plan(item, hop):
            above, below = jnp.maximum(spot - hop, 0), jnp.minimum(spot + hop, line - 1)
            came_up = jnp.maximum(spot - 1 - hop, 0)
            came_down = jnp.minimum(spot + 1 + hop, line - 1)
            made = {
                "up": copies.plan(
                    own[item] if hop == 0 else seat(item, above), seat(item, above), at.up
                ),
                "down": copies.plan(
                    own[item] if hop == 0 else seat(item, below), seat(item, below), at.down
                ),
                "onward": [],
            }
            for position in (came_up, came_down):
                onward = []
                if item in (MIX, VEC):
                    onward.append(copies.plan(seat(item, position), seat(item, position), at.across))
                if item == FC:
                    onward.append(copies.plan(fc_near.at[position], fc_side.at[position], at.across))
                    onward.append(copies.plan(fc_near.at[position], fc_far.at[position], at.far))
                made["onward"].append(onward)
            return made

        plans = [[plan(item, hop) for hop in range(hops)] for item in range(4)]

        def launch(item):
            copies.begin(plans[item][0]["up"], at.has_up)
            copies.begin(plans[item][0]["down"], at.has_down)

        def handle(item, hop):
            made = plans[item][hop]
            for way, key, comes, goes in (
                (0, "up", spot - 1 - hop >= 0, at.has_up),
                (1, "down", spot + 1 + hop < line, at.has_down),
            ):
                when(comes, made[key].wait_recv)
                if hop + 1 < hops:
                    copies.begin(plans[item][hop + 1][key], comes & goes)
                for copy in made["onward"][way]:
                    copies.begin(copy, comes)

        def settle(item):
            for hop in range(hops):
                for way, comes in ((0, spot - 1 - hop >= 0), (1, spot + 1 + hop < line)):
                    for copy in plans[item][hop]["onward"][way]:
                        when(comes, copy.wait_recv)

        stays = []

        def stay(source, target):
            copy = pltpu.make_async_copy(source, target, local.at[len(stays)])
            copy.start()
            stays.append(copy)
            return copy

        parts = [pl.ds(0, half_rows), pl.ds(half_rows, half_rows)]
        arrivals[0].wait()
        launch(FC)
        fc_sides = [copies.start(fc_ref, fc_side.at[spot], at.across)]
        cot_made = copies.start(cot_ref, cot_out, at.mate)
        for copy in arrivals[6:]:
            copy.wait()
        tile[...] = jnp.zeros_like(tile)
        row = 0
        for ref in vec_refs:
            count, size = ref.shape
            tile[row : row + count, 0:size] = ref[...].astype(F32)
            row += count
        vec_ref[...] = tile[...].astype(LOW)
        vec_made = [
            copies.start(vec_ref, tile_land.at[i], device)
            for i, device in enumerate((at.mate, at.far, at.corner))
        ]
        arrivals[1].wait()
        arrivals[2].wait()
        pos_row = lax.broadcasted_iota(jnp.int32, (latents, 128), 0)
        places = jnp.zeros((latents, 128), jnp.int32)
        for w in range(latents):
            places = jnp.where(pos_row == w, pos_ref[w], places)
            span = pl.ds(w * window, window)
            here = lax.broadcasted_iota(jnp.int32, (window, 1), 0) == pos_ref[w] - w * window
            hidden_ref[span] = jnp.where(
                here, thoughts_ref[w : w + 1].astype(F32), tokens_ref[span].astype(F32)
            ).astype(LOW)
        pos_out[...] = places
        far_made = [
            copies.start(hidden_ref.at[part], land.at[2, part], at.far) for part in parts
        ]
        mate_made = copies.start(hidden_ref, land.at[1], at.mate)
        fc_sides.append(copies.start(fc_ref, fc_far.at[spot], at.far))
        for copy in arrivals[3:6]:
            copy.wait()
        turned = qkv_ref[...].astype(F32).T
        extra = out_ref[...].astype(F32)
        pieces = []
        for p in range(3):
            for h in range(NH):
                low = (h * 3 + p) * HD
                pieces.append(turned[low : low + HD])
            pieces.append(extra[p * HD : (p + 1) * HD])
        mix_ref[...] = jnp.concatenate(pieces, axis=0).T.astype(LOW)
        launch(MIX)
        mix_side = copies.start(mix_ref, mix_land.at[dp], at.across)
        stay(hidden_ref, hidden_out)
        stay(fc_ref, fc_near.at[spot])
        stay(proj_ref, proj_near.at[spot])
        mix_land[dp] = mix_ref[...]
        for copy in vec_made:
            copy.wait_recv()
        merged = jnp.zeros((VEC_ROWS, 128), F32)
        bias_rows = jnp.zeros((VEC_ROWS, 128), F32)
        row_ids = lax.broadcasted_iota(jnp.int32, (VEC_ROWS, 128), 0)
        for i, index in enumerate((tensor, mate_row, far_row, corner_row)):
            tile = vec_ref[...] if i == 0 else tile_land[i - 1]
            merged += nn(tile, one_hot(128, 128, index * share, share))
            bias_rows = jnp.where(row_ids == 8 + index, tile[8:9].astype(F32), bias_rows)
        tiles[dp] = jnp.where(row_ids < 8, merged, bias_rows).astype(LOW)
        launch(VEC)
        vec_side = copies.start(tiles.at[dp], tiles.at[dp], at.across)

        def norm_rows(source, index):
            @pl.loop(0, rows // 128)
            def _(i):
                span = pl.ds(pl.multiple_of(i * 128, 128), 128)
                normed[index, span] = normalize(source[span].astype(F32))[0].astype(LOW)

            stay(normed.at[index], normed_out.at[index])

        def relay(i):
            far_made[i].wait_recv()
            return copies.start(land.at[2, parts[i]], land.at[3, parts[i]], at.mate)

        def mix_rows(index):
            @pl.loop(0, rows // 256)
            def _(i):
                span = pl.ds(pl.multiple_of(i * 256, 256), 256)
                turned = normed[index, span].astype(F32) * whole[0:1] + whole[1:2]
                weight = mix_land[...].reshape(width, width)
                mixed[index, span] = (nn(turned.astype(LOW), weight) + bias).astype(LOW)

            stay(mixed.at[index], mixed_out.at[index])

        norm_rows(hidden_ref, tensor)
        relayed = []
        for step in range(hops + 2):
            for item, hop in ((MIX, step), (VEC, step), (FC, step - 1), (PROJ, step - 2)):
                if 0 <= hop < hops:
                    handle(item, hop)
            if step == 0:
                launch(PROJ)
                mate_made.wait_recv()
                norm_rows(land.at[1], mate_row)
                relayed.append(relay(0))
            if step == 1:
                relayed.append(relay(1))
                norm_rows(land.at[2], far_row)
            if step == hops:
                mix_side.wait_recv()
                vec_side.wait_recv()
                settle(MIX)
                settle(VEC)
                whole = jnp.zeros((VEC_ROWS, width), F32)
                for i in range(n_dp):
                    whole += nn(tiles[i], one_hot(128, width, i * shard, shard))
                vec_out[...] = whole
                for i, block in enumerate((tensor, far_row)):
                    vec_out[12 + i : 13 + i] = units_row(whole[8:12], block, n_dp)
                lane = lax.broadcasted_iota(jnp.int32, (width, WIDE), 0)
                column = lax.broadcasted_iota(jnp.int32, (width, WIDE), 1)
                pick = (lane == column + tensor * (NH * HD)) & (column < NH * HD)
                picked = nn(whole.astype(LOW), pick.astype(LOW))
                bias = jnp.concatenate(
                    [picked[2:3], jnp.zeros((1, WIDE), F32), picked[3:4]], axis=1
                )
                mix_rows(tensor)
                mix_rows(mate_row)
                mix_rows(far_row)
                for copy in relayed:
                    copy.wait_recv()
                norm_rows(land.at[3], corner_row)
                mix_rows(corner_row)
                stay(mix_land, mix_out)
                weight = mix_land[...].reshape(width, width)
                for part in range(3):
                    low = part * WIDE + WIDE - 128
                    turned = weight[:, low : low + 128].T
                    out_turned[part * HD : (part + 1) * HD] = turned[128 - HD :]
                stay(out_turned, out_out)
        settle(FC)
        for copy in fc_sides:
            copy.wait_recv()
        cot_made.wait_recv()
        copies.finish()
        for copy in stays:
            copy.wait()

    low = lambda *shape: jax.ShapeDtypeStruct(shape, LOW)
    outputs = (
        low(4, rows, width), low(4, rows, width), low(n_dp, shard, width),
        low(line, shard, width), low(line, shard, width), low(line, shard, width),
        low(line, shard, width), low(rows, width), low(NH * HD, width), low(rows, width),
        jax.ShapeDtypeStruct((VEC_ROWS, width), F32),
        jax.ShapeDtypeStruct((latents, 128), jnp.int32),
    )
    scratch = [
        pltpu.VMEM((rows, width), LOW),
        pltpu.VMEM((shard, 3 * WIDE), LOW),
        pltpu.VMEM((VEC_ROWS, 128), LOW),
        pltpu.VMEM((VEC_ROWS, 128), F32),
        pltpu.VMEM((4, rows, width), LOW),
        pltpu.VMEM((n_dp, shard, width), LOW),
        pltpu.VMEM((n_dp, VEC_ROWS, 128), LOW),
        pltpu.VMEM((3, VEC_ROWS, 128), LOW),
        pltpu.VMEM((4, rows, width), LOW),
        pltpu.VMEM((4, rows, width), LOW),
        pltpu.VMEM((NH * HD, width), LOW),
    ]
    given = (fc, tokens, thoughts, proj, qkv, out, *vectors)
    scratch += [pltpu.VMEM(x.shape, x.dtype) for x in given]
    scratch.append(pltpu.SemaphoreType.DMA((len(given),)))
    return comm_call(
        kernel,
        "gather_inputs",
        outputs,
        (positions, tokens, thoughts, cotangent, fc, proj, qkv, out, *vectors),
        [SM] + [ANY] * (7 + len(vectors)),
        (ANY,) * 10 + (VM, VM),
        3 + 2 + 1 + 2 + 2 + 1 + 2 + hops * (2 * 4 + 2 * 4),
        0,
        scratch=scratch,
        local=3 + 8 + 2,
    )


def after_attention(attended, out_own, out_far, hidden, vec_all, n_dp, cid):
    head_width, slots = attended.shape
    rows, width = hidden.shape
    half_rows = rows // 2

    def kernel(
        heads_in, own_in, far_in, hidden_in, vec_ref,
        both_out, middle_out, two_out,
        heads_ref, own_ref, far_ref, hidden_ref,
        land, part, part_low, part_land, two, send, recv, local,
    ):
        loads = [
            pltpu.make_async_copy(source, target, local.at[5 + i])
            for i, (source, target) in enumerate(
                (
                    (heads_in, heads_ref), (own_in, own_ref), (far_in, far_ref),
                    (hidden_in, hidden_ref),
                )
            )
        ]
        for copy in loads:
            copy.start()
        at = Place(n_dp // 2)
        greet([(at.far, None), (at.mate, None)])
        copies = Copies(send, recv)
        cores = (at.core, 1 - at.core)
        made = [None, None]
        for i in (1, 0):
            theirs = pl.multiple_of(((1 - at.chip) * 2 + cores[i]) * rows, rows)
            made[i] = copies.start(heads_in.at[:, pl.ds(theirs, rows)], land.at[i], at.far)
        stays = []

        def stay(source, target):
            stays.append(pltpu.make_async_copy(source, target, local.at[len(stays)]))
            stays[-1].start()

        spans = []
        for copy in loads:
            copy.wait()
        for i in range(2):
            ours = pl.multiple_of((at.chip * 2 + cores[i]) * rows, rows)
            spans.append(pl.ds(ours, rows))
            stay(heads_ref.at[:, spans[i]], both_out.at[0, :, i * rows : (i + 1) * rows])
            part[i] = tn(heads_ref[:, spans[i]], own_ref[...])
        sums = None
        for i in (1, 0):
            made[i].wait_recv()
            stay(land.at[i], both_out.at[1, :, i * rows : (i + 1) * rows])
            part[i] += tn(land[i], far_ref[...])
            if i == 1:
                part_low[...] = part[1].astype(LOW)
                sums = copies.start(part_low, part_land, at.mate)
        sums.wait_recv()
        mated = []
        for piece in range(2):

            @pl.loop(0, half_rows // 128)
            def _(i):
                span = pl.ds(pl.multiple_of(piece * half_rows + i * 128, 128), 128)
                middle = (
                    hidden_ref[span].astype(F32)
                    + part[0, span]
                    + part_land[span].astype(F32)
                    + vec_ref[4:5]
                )
                middle_out[span] = middle
                two[span] = (normalize(middle)[0] * vec_ref[5:6] + vec_ref[6:7]).astype(LOW)

            span = pl.ds(piece * half_rows, half_rows)
            mated.append(copies.start(two.at[span], two_out.at[1, span], at.mate))
        stay(two, two_out.at[0])
        for copy in mated:
            copy.wait_recv()
        copies.finish()
        for copy in stays:
            copy.wait()

    return comm_call(
        kernel,
        "after_attention",
        (
            jax.ShapeDtypeStruct((2, head_width, 2 * rows), LOW),
            jax.ShapeDtypeStruct((rows, width), F32),
            jax.ShapeDtypeStruct((2, rows, width), LOW),
        ),
        (attended, out_own, out_far, hidden, vec_all),
        [ANY] * 4 + [VM],
        (ANY, VM, ANY),
        5,
        cid,
        scratch=[pltpu.VMEM(x.shape, x.dtype) for x in (attended, out_own, out_far, hidden)]
        + [
            pltpu.VMEM((2, head_width, rows), LOW),
            pltpu.VMEM((2, rows, width), F32),
            pltpu.VMEM((rows, width), LOW),
            pltpu.VMEM((rows, width), LOW),
            pltpu.VMEM((rows, width), LOW),
        ],
        local=9,
    )


def before_attention_back(
    lengths, two, middle, cotangent, both, out_own, out_far, vec_all, pairs, n_dp, cid
):
    _, rows, width = two.shape
    head_width = out_own.shape[0]
    half_rows = rows // 2

    def kernel(
        lengths_ref, two_in, middle_in, cot_in, both_in, own_in, far_in, vec_ref,
        one_a, one_b, two_a, two_b,
        heads_out, grad_out, own_out, far_out, vec_out, sum_one, sum_two,
        two_ref, middle_ref, cot_ref, both_ref, own_ref, far_ref,
        two_land, mid, stay_heads, sent_heads, held, send, recv, local,
    ):
        at = Place(n_dp // 2)
        greet([(at.far, None), (at.mate, None)])
        copies = Copies(send, recv)
        halves = [pl.ds(0, half_rows), pl.ds(half_rows, half_rows)]
        loads = [
            pltpu.make_async_copy(ref, held.at[i], local.at[2 + i])
            for i, ref in enumerate((one_a, one_b, two_a, two_b))
        ]
        early = [
            pltpu.make_async_copy(source, target, local.at[6 + i])
            for i, (source, target) in enumerate(
                (
                    (two_in.at[0], two_ref), (middle_in, middle_ref), (cot_in, cot_ref),
                    (far_in, far_ref), (own_in, own_ref), (both_in, both_ref),
                )
            )
        ]
        sums = [copies.start(two_in.at[1, span], two_land.at[span], at.mate) for span in halves]
        for copy in early + loads:
            copy.start()
        vec_out[...] = jnp.zeros_like(vec_out)
        first_row = at.tensor * rows
        live = ends_of(lengths_ref)[-1]
        mated = []
        for copy in early:
            copy.wait()
        for piece in range(2):
            sums[piece].wait_recv()

            @pl.loop(0, half_rows // 128)
            def _(i):
                start = pl.multiple_of(piece * half_rows + i * 128, 128)
                span = pl.ds(start, 128)
                grad = two_ref[span].astype(F32) + two_land[span].astype(F32)
                normed, inverse = normalize(middle_ref[span])
                ids = first_row + start + lax.broadcasted_iota(jnp.int32, (128, 1), 0)
                final = jnp.where(ids < live, cot_ref[span].astype(F32), 0.0)
                total = final + norm_back(normed, inverse, grad, vec_ref[5:6])
                grad_out[span] = total
                mid[0, span] = total.astype(LOW)
                for row, term in ((4, total), (5, normed * grad), (6, grad), (7, final)):
                    vec_out[row : row + 1] += jnp.sum(term, axis=0, keepdims=True)

            mated.append(copies.start(mid.at[0, halves[piece]], mid.at[1, halves[piece]], at.mate))
        cores = (at.core, 1 - at.core)
        made, stays = [], []
        for i in range(2):
            if i == 1:
                for copy in mated:
                    copy.wait_recv()
            ours = pl.ds(pl.multiple_of((at.chip * 2 + cores[i]) * rows, rows), rows)
            sent_heads[i] = nt(far_ref[...], mid[i]).astype(LOW)
            made.append(copies.start(sent_heads.at[i], heads_out.at[:, ours], at.far))
            stay_heads[i] = nt(own_ref[...], mid[i]).astype(LOW)
            stays.append(
                pltpu.make_async_copy(stay_heads.at[i], heads_out.at[:, ours], local.at[i])
            )
            stays[-1].start()
        grads = mid[...].reshape(2 * rows, width)
        own_out[...] = nn(both_ref[0], grads).astype(LOW)
        far_out[...] = nn(both_ref[1], grads).astype(LOW)
        for copy in loads:
            copy.wait()
        sum_one[...] = (held[0].astype(F32) + held[1].astype(F32)).astype(LOW)
        sum_two[...] = (held[2].astype(F32) + held[3].astype(F32)).astype(LOW)
        for copy in made:
            copy.wait_recv()
        copies.finish()
        for copy in stays:
            copy.wait()

    return comm_call(
        kernel,
        "before_attention_back",
        (
            jax.ShapeDtypeStruct((head_width, 4 * rows), LOW),
            jax.ShapeDtypeStruct((rows, width), F32),
            jax.ShapeDtypeStruct((head_width, width), LOW),
            jax.ShapeDtypeStruct((head_width, width), LOW),
            jax.ShapeDtypeStruct((VEC_ROWS, width), F32),
            jax.ShapeDtypeStruct(pairs[0].shape, LOW),
            jax.ShapeDtypeStruct(pairs[0].shape, LOW),
        ),
        (lengths, two, middle, cotangent, both, out_own, out_far, vec_all, *pairs),
        [SM] + [ANY] * 6 + [VM] + [ANY] * 4,
        (ANY,) + (VM,) * 6,
        6,
        cid,
        scratch=[pltpu.VMEM((rows, width), LOW)]
        + [pltpu.VMEM(x.shape, x.dtype) for x in (middle, cotangent, both, out_own, out_far)]
        + [
            pltpu.VMEM((rows, width), LOW),
            pltpu.VMEM((2, rows, width), LOW),
            pltpu.VMEM((2, head_width, rows), LOW),
            pltpu.VMEM((2, head_width, rows), LOW),
            pltpu.VMEM((4,) + pairs[0].shape, LOW),
        ],
        local=12,
    )


def finish_grads(lengths, arrays, n_dp, cid):
    part_rows = arrays["hidden"].shape[0] // 4
    flat, shapes = [], {}
    for name, array in arrays.items():
        pieces = array if isinstance(array, tuple) else (array,)
        flat += [(name, i, piece) for i, piece in enumerate(pieces)]
        lead = sum(piece.shape[0] for piece in pieces)
        shapes[name] = ((lead,) + pieces[0].shape[1:], pieces[0].dtype)
    kept = [name for name in arrays if name != "out_far"]
    line = n_dp // 2
    shard = arrays["mix"].shape[1]
    rows, width = arrays["hidden"].shape
    group = 4 * rows
    latents = arrays["positions"].shape[0]
    window = rows // latents
    far_end = line - 1
    slots = [(distance, way) for distance in range(far_end, 0, -1) for way in (0, 1)] + [(0, 0)]
    last = len(slots) - 1
    share = width // (n_dp * 4)
    FC, PROJ, MIX, VEC = range(4)

    def kernel(lengths_ref, *refs):
        refs = list(refs)

        def take(number):
            taken = refs[:number]
            del refs[:number]
            return taken

        sources = take(len(flat))
        out_source = sources[[name for name, _, _ in flat].index("out_far")]
        fc_out, proj_out, mix_out, vec_out, tokens_out, thoughts_out, block_out = take(7)
        held = dict(zip(kept, take(len(kept))))
        cross_send, cross_land = [None, None] + take(2), [None, None] + take(2)
        hop_send, hop_land = take(4), take(4)
        (
            part, mate_land, far_send, far_land, last_land, total, vec_mine, vec_land, vec_near,
            plain_sum, column_sum, out_land, tokens_kept, thoughts_kept, block_kept, send, recv,
            local,
        ) = refs
        out = [fc_out, proj_out, mix_out, None]
        at = Place(line)
        tensor, spot, side = at.tensor, at.spot, at.side
        mate_row, far_row, corner_row = at.mate[1], at.far[1], at.corner[1]
        copies = Copies(send, recv)
        loads = {}
        held["out_far"] = out_land
        for k, (name, i, piece) in enumerate(flat):
            if name != "out_far":
                target = held[name]
                if isinstance(arrays[name], tuple):
                    first = 0 if i == 0 else arrays[name][0].shape[0]
                    target = target.at[first : first + piece.shape[0]]
                copy = pltpu.make_async_copy(sources[k], target, local.at[k])
                loads.setdefault(name, Several([])).copies.append(copy)

        def load(*group):
            for name in group:
                loads[name].start()

        load("fc_near", "fc_near_side", "fc_cross", "proj_near", "proj_near_far", "proj_cross")
        load("grad_mixed", "mix")
        greet(at.everyone())

        def block_of(slot):
            distance, way = slots[slot]
            if way == 0:
                return jnp.minimum(spot + distance, far_end), spot + distance < line
            return jnp.maximum(spot - distance, 0), spot - distance >= 0

        crosses, hops = [], []
        for slot in range(len(slots)):
            block, _ = block_of(slot)
            crosses.append(
                {
                    i: copies.plan(cross_send[i].at[block], cross_land[i].at[block], at.across)
                    for i in (MIX, VEC)
                }
            )
            if slot < last:
                hops.append(
                    [
                        copies.plan(
                            hop_send[i].at[slot],
                            hop_land[i].at[slot],
                            (at.up, at.down)[slots[slot][1]],
                        )
                        for i in range(4)
                    ]
                )

        def cross(distance, items):
            for slot in range(len(slots)):
                if slots[slot][0] == distance:
                    for i in items:
                        copies.begin(crosses[slot][i], block_of(slot)[1])

        terms = (
            ("fc_near", "fc_near_side", "fc_cross"),
            ("proj_near", "proj_near_far", "proj_cross"),
        )

        def own_term(i, block):
            if i in (FC, PROJ):
                return sum(held[name][block].astype(F32) for name in terms[i])
            if i == MIX:
                return total[block * 2 + side].astype(F32)
            return vec_near[block * 2 + side]

        def handle(slot, i):
            block, inside = block_of(slot)
            behind = (at.has_down, at.has_up)[slots[slot][1]]
            outer = slot - 2

            def work():
                value = own_term(i, block)
                if i in (MIX, VEC):
                    crosses[slot][i].wait_recv()
                    value = value + cross_land[i][block].astype(F32)
                if outer < 0:
                    hop_send[i][slot] = value.astype(hop_send[i].dtype)
                    return

                @pl.when(behind)
                def _():
                    hops[outer][i].wait_recv()
                    hop_send[i][slot] = (value + hop_land[i][outer].astype(F32)).astype(
                        hop_send[i].dtype
                    )

                @pl.when(jnp.logical_not(behind))
                def _():
                    hop_send[i][slot] = value.astype(hop_send[i].dtype)

            when(inside, work)
            copies.begin(hops[slot][i], inside)

        def handle_all(distance, items):
            for slot in range(last):
                if slots[slot][0] == distance:
                    for i in items:
                        handle(slot, i)

        def close(i, target):
            value = own_term(i, spot)
            if i in (MIX, VEC):
                crosses[last][i].wait_recv()
                value = value + cross_land[i][spot].astype(F32)
            target[...] = value
            for way, behind in enumerate((at.has_down, at.has_up)):

                def add(way=way):
                    hops[last - 2 + way][i].wait_recv()
                    target[...] += hop_land[i][last - 2 + way].astype(F32)

                when(behind, add)

        for name in ("fc_near", "fc_near_side", "fc_cross", "proj_near", "proj_near_far", "proj_cross"):
            loads[name].wait()
        out_made = copies.start(out_source, out_land, at.far)
        handle_all(far_end, (FC, PROJ))
        load("group", "out_own", "vec_all", "vec_part", "bias_own", "bias_far")
        load("last", "hidden", "grad_middle", "middle", "positions")
        loads["grad_mixed"].wait()
        loads["mix"].wait()

        def row_part(index):
            @pl.loop(0, rows // 256)
            def _(i):
                span = pl.ds(pl.multiple_of(i * 256, 256), 256)
                weight = held["mix"][...].reshape(width, width)
                part[index, span] = nt(held["grad_mixed"][index, span], weight).astype(LOW)

        for name in ("group", "out_own", "vec_all", "vec_part", "bias_own", "bias_far"):
            loads[name].wait()

        plain_sum[...] = jnp.zeros_like(plain_sum)
        column_sum[...] = jnp.zeros_like(column_sum)

        @pl.loop(0, group // 256)
        def _(i):
            block, start = i // (rows // 256), (i % (rows // 256)) * 256
            span = pl.ds(pl.multiple_of(start, 256), 256)
            grad = held["grad_mixed"][block, span]
            plain_sum[...] += tn(held["group"][block, span], grad)
            column_sum[...] += jnp.sum(grad.astype(F32), axis=0, keepdims=True)

        row_part(corner_row)
        mate_far = copies.start(part.at[corner_row], mate_land.at[1], at.mate)
        row_part(mate_row)
        mate_own = copies.start(part.at[mate_row], mate_land.at[0], at.mate)
        if far_end > 1:
            handle_all(far_end - 1, (FC, PROJ))
        out_made.wait_recv()
        plain, columns = plain_sum[...], column_sum[...]
        turned = held["vec_all"][...].T
        weight = held["mix"][...].reshape(width, width).astype(F32)
        gain_grad = jnp.sum(plain * weight, axis=1, keepdims=True)
        shift_grad = jnp.sum(weight * columns, axis=1, keepdims=True)
        scaled = plain * turned[:, 0:1] + turned[:, 1:2] * columns
        extras = []
        out_sum = held["out_own"][...].astype(F32) + held["out_far"][...].astype(F32)
        for p in range(3):
            piece = out_sum[p * HD : (p + 1) * HD]
            extras.append(jnp.zeros((width, WIDE - 128), F32))
            extras.append(jnp.concatenate([jnp.zeros((128 - HD, width), F32), piece], axis=0).T)
        scaled = scaled + jnp.concatenate(extras, axis=1)
        for k in range(n_dp):
            total[k] = scaled[k * shard : (k + 1) * shard].astype(LOW)
        for block in range(line):
            cross_send[MIX][block] = total[block * 2 + 1 - side]
        cross(far_end, [MIX])
        cross(far_end - 1, [MIX])
        row_part(far_row)
        mate_far.wait_recv()
        far_made = []

        def send_far(count):
            for i in range(len(far_made), min(len(far_made) + count, 8)):
                span = pl.ds(i * (part_rows // 2), part_rows // 2)
                far_send[span] = (
                    mate_land[1, span].astype(F32) + part[far_row, span].astype(F32)
                ).astype(LOW)
                far_made.append(copies.start(far_send.at[span], far_land.at[span], at.far))

        send_far(2)
        row_part(tensor)
        send_far(1)
        loads["last"].wait()
        last_copy = copies.start(held["last"].at[1], last_land, at.mate)
        vec_mine[...] = held["vec_part"][...]
        norm_grads = jnp.concatenate(
            [gain_grad, shift_grad, jnp.zeros((width, 6), F32)], axis=1
        ).T
        vec_mine[0:2] = norm_grads[0:2]
        vec_mine[8:12] = units_rows_back(held["bias_own"][...], tensor, n_dp) + units_rows_back(
            held["bias_far"][...], far_row, n_dp
        )
        vec_lane = lax.broadcasted_iota(jnp.int32, (1, width), 1)
        in_part = (vec_lane >= tensor * (NH * HD)) & (vec_lane < (tensor + 1) * (NH * HD))
        for row, low in ((2, 0), (3, 2 * WIDE)):
            line_up = jnp.concatenate([columns[:, low : low + WIDE]] + [columns[:, 0:WIDE]] * 2, axis=1)
            placed = jnp.zeros((1, width), F32)
            for t in range(4):
                shifted = pltpu.roll(line_up, t * NH * HD, 1)
                placed = jnp.where(tensor == t, shifted, placed)
            vec_mine[row : row + 1] = jnp.where(in_part, placed, 0.0)
        vec_made = [
            copies.start(vec_mine, vec_land.at[i], device)
            for i, device in enumerate((at.mate, at.far, at.corner))
        ]
        handle_all(far_end, [MIX])
        if far_end >= 2:
            cross(far_end - 2, [MIX])
        send_far(2)
        for distance in range(far_end - 2, 0, -1):
            handle_all(distance, (FC, PROJ))
        send_far(1)
        for copy in vec_made:
            copy.wait_recv()
        send_far(1)
        vec_sum = vec_mine[...] + vec_land[0] + vec_land[1] + vec_land[2]
        for k in range(n_dp):
            vec_near[k] = pltpu.roll(vec_sum, (width - k * shard) % width, 1)[:, 0:128]
        for block in range(line):
            cross_send[VEC][block] = vec_near[block * 2 + 1 - side]
        cross(far_end, [VEC])
        cross(far_end - 1, [VEC])
        send_far(8)
        live = ends_of(lengths_ref)[-1]
        stays = []

        def close_rows(i):
            if i == 0:
                for name in ("hidden", "grad_middle", "middle", "positions"):
                    loads[name].wait()
                last_copy.wait_recv()
                mate_own.wait_recv()
            far_made[2 * i].wait_recv()
            far_made[2 * i + 1].wait_recv()
            span = pl.ds(i * part_rows, part_rows)
            ids = tensor * rows + i * part_rows + lax.broadcasted_iota(
                jnp.int32, (part_rows, 1), 0
            )
            final = (
                held["middle"][span]
                + held["last"][0, span].astype(F32)
                + last_land[span].astype(F32)
                + held["vec_all"][7:8]
            )
            block_kept[span] = jnp.where(ids < live, final, 0.0).astype(LOW)
            grad = (
                part[tensor, span].astype(F32)
                + mate_land[0, span].astype(F32)
                + far_land[span].astype(F32)
            )
            normed, inverse = normalize(held["hidden"][span].astype(F32))
            grad = held["grad_middle"][span] + norm_back(
                normed, inverse, grad, held["vec_all"][0:1]
            )
            for w in range(part_rows // window):
                index = i * (part_rows // window) + w
                here = (
                    lax.broadcasted_iota(jnp.int32, (window, 1), 0)
                    == held["positions"][index : index + 1, 0:1] - index * window
                )
                piece = grad[w * window : (w + 1) * window]
                tokens_kept[pl.ds(index * window, window)] = jnp.where(here, 0.0, piece)
                thoughts_kept[index : index + 1] = jnp.sum(
                    jnp.where(here, piece, 0.0), axis=0, keepdims=True
                )
            moves = [(tokens_kept.at[span], tokens_out.at[span])]
            moves.append((block_kept.at[span], block_out.at[span]))
            if i == 3:
                moves.append((thoughts_kept, thoughts_out))
            for kept_ref, out_ref in moves:
                stays.append(
                    pltpu.make_async_copy(kept_ref, out_ref, local.at[len(flat) + len(stays)])
                )
                stays[-1].start()

        done = 0
        for distance in range(far_end, 0, -1):
            items = (MIX, VEC) if distance < far_end else (VEC,)
            handle_all(distance, items)
            if distance >= 2:
                cross(distance - 2, items)
            if distance <= 3:
                close_rows(done)
                done += 1
        for i in range(done, 4):
            close_rows(i)
        for i in (FC, PROJ, MIX):
            close(i, out[i])
        close(VEC, vec_out)
        copies.finish()
        for copy in stays:
            copy.wait()

    f32 = lambda *shape: jax.ShapeDtypeStruct(shape, F32)
    outputs = (
        f32(shard, width), f32(shard, width), f32(shard, width), f32(VEC_ROWS, 128),
        f32(rows, width), f32(latents, width), jax.ShapeDtypeStruct((rows, width), LOW),
    )
    scratch = [pltpu.VMEM(*shapes[name]) for name in kept]
    for number, wide in ((line, 1), (line, 1), (last, 3), (last, 3)):
        scratch += [pltpu.VMEM((number, shard, width), LOW)] * wide
        scratch.append(pltpu.VMEM((number, VEC_ROWS, 128), F32))
    scratch += [
        pltpu.VMEM((4, rows, width), LOW),
        pltpu.VMEM((2, rows, width), LOW),
        pltpu.VMEM((rows, width), LOW),
        pltpu.VMEM((rows, width), LOW),
        pltpu.VMEM((rows, width), LOW),
        pltpu.VMEM((n_dp, shard, width), LOW),
        pltpu.VMEM((VEC_ROWS, width), F32),
        pltpu.VMEM((3, VEC_ROWS, width), F32),
        pltpu.VMEM((n_dp, VEC_ROWS, 128), F32),
        pltpu.VMEM((width, width), F32),
        pltpu.VMEM((1, width), F32),
        pltpu.VMEM(arrays["out_far"].shape, LOW),
        pltpu.VMEM((rows, width), F32),
        pltpu.VMEM((latents, width), F32),
        pltpu.VMEM((rows, width), LOW),
    ]
    return comm_call(
        kernel,
        "finish_grads",
        outputs,
        (lengths, *(piece for _, _, piece in flat)),
        [SM] + [ANY] * len(flat),
        (VM,) * 4 + (ANY,) * 3,
        (last + 1) * 2 + last * 4 + 1 + 2 + 8 + 3 + 1,
        cid,
        scratch=scratch,
        local=len(flat) + 9,
    )


def unit_kernel(add, line, bias_row, lengths_ref, *refs):
    refs = list(refs)
    rows_ref, grad_own, grad_mate = refs[:3]
    pieces, vec_ref = refs[3:7], refs[7]
    refs = refs[8:]
    if add:
        last_in, two_in = refs[:2]
        refs = refs[2:]
    last_ref, two_ref, fc_near, fc_side, proj_one, proj_two, proj_side, bias_grad_ref = refs[:8]
    fc_all, proj_all, fc_sum, proj_sum = refs[8:]
    step = pl.program_id(0)
    side, tensor = lax.axis_index("dp") % 2, lax.axis_index("tensor")
    live = ends_of(lengths_ref)[-1]

    @pl.when(step == 0)
    def _():
        for full, near, across in ((fc_all, *pieces[:2]), (proj_all, *pieces[2:])):
            for i in range(line):
                full[2 * i + side] = near[i]
                full[2 * i + 1 - side] = across[i]
        fc_sum[...] = jnp.zeros_like(fc_sum)
        proj_sum[...] = jnp.zeros_like(proj_sum)
        bias_grad_ref[...] = jnp.zeros_like(bias_grad_ref)

    count, width = rows_ref.shape
    half = pl.num_programs(0) // 2
    block = jnp.where(step < half, tensor, tensor + 1 - 2 * (tensor % 2))
    first = block * (half * count) + (step % half) * count
    alive = first + lax.broadcasted_iota(jnp.int32, (count, 1), 0) < live
    rows = rows_ref[...]
    grad = jnp.where(step < half, grad_own[...], grad_mate[...])
    grad = jnp.where(alive, grad, jnp.zeros_like(grad))
    fc = fc_all[...].reshape(width, -1)
    proj = proj_all[...].reshape(width, -1)
    inner = nn(rows, fc) + vec_ref[bias_row : bias_row + 1]
    square = inner * inner
    bend = jnp.tanh(GELU_SCALE * inner * (1.0 + GELU_CUBE * square))
    half = 0.5 * (1.0 + bend)
    activated = (inner * half).astype(LOW)
    slope = half + 0.5 * inner * (1.0 - bend * bend) * GELU_SCALE * (1.0 + 3.0 * GELU_CUBE * square)
    grad_inner = (nn(grad, proj) * slope).astype(LOW)
    last = nt(activated, proj)
    two = nt(grad_inner, fc)
    if add:
        last, two = last + last_in[...], two + two_in[...]
    last_ref[...] = last.astype(last_ref.dtype)
    two_ref[...] = two.astype(two_ref.dtype)
    fc_sum[...] += tn(rows, grad_inner)
    proj_sum[...] += tn(grad, activated)
    bias_grad_ref[...] += jnp.sum(grad_inner.astype(F32), axis=0, keepdims=True)

    @pl.when(step == pl.num_programs(0) - 1)
    def _():
        shard = fc_near.shape[1]
        split = line // 2
        near_seats = (
            [fc_near.at[i] for i in range(line)],
            [proj_one.at[i] for i in range(split)] + [proj_two.at[i] for i in range(line - split)],
        )
        for sums, near, across in (
            (fc_sum, near_seats[0], fc_side), (proj_sum, near_seats[1], proj_side),
        ):
            for i in range(line):
                even = sums[2 * i * shard : (2 * i + 1) * shard].astype(LOW)
                odd = sums[(2 * i + 1) * shard : (2 * i + 2) * shard].astype(LOW)
                near[i][...] = jnp.where(side == 0, even, odd)
                across[i] = jnp.where(side == 0, odd, even)


def units_both_ways(lengths, rows, grad, mate_grad, pieces, vec_all, bias_row, before):
    count, width = rows.shape
    line, shard, units = pieces[0].shape
    half = count // ROW_TILE // 2
    leads = (line, line, line // 2, line - line // 2, line)
    tile = pl.BlockSpec((ROW_TILE, width), lambda i: (i, 0))
    fixed = lambda shape: pl.BlockSpec(shape, lambda i: (0,) * len(shape))
    add = before is not None
    kind = LOW if add else F32
    return pl.pallas_call(
        functools.partial(unit_kernel, add, line, bias_row),
        grid=(count // ROW_TILE,),
        out_shape=(
            jax.ShapeDtypeStruct((count, width), kind),
            jax.ShapeDtypeStruct((count, width), kind),
        )
        + tuple(jax.ShapeDtypeStruct((k, shard, units), LOW) for k in leads)
        + (jax.ShapeDtypeStruct((1, units), F32),        ),
        in_specs=[
            SM,
            tile,
            pl.BlockSpec((ROW_TILE, width), lambda i: (jnp.minimum(i, half - 1), 0)),
            pl.BlockSpec((ROW_TILE, width), lambda i: (jnp.maximum(i - half, 0), 0)),
        ]
        + [fixed((line, shard, units))] * 4
        + [fixed(vec_all.shape)]
        + [tile] * (2 if add else 0),
        out_specs=(tile, tile)
        + tuple(fixed((k, shard, units)) for k in leads)
        + (fixed((1, units)),),
        scratch_shapes=[pltpu.VMEM((2 * line, shard, units), LOW)] * 2
        + [pltpu.VMEM((width, units), F32)] * 2,
        compiler_params=pltpu.CompilerParams(
            dimension_semantics=("arbitrary",), vmem_limit_bytes=VMEM_LIMIT
        ),
        cost_estimate=pl.CostEstimate(
            flops=12 * count * width * units,
            bytes_accessed=24 * count * width,
            transcendentals=count * units,
        ),
        name="units_second" if add else "units_first",
    )(lengths, rows, grad, mate_grad, *pieces, vec_all, *(before or ()))


def split_grads(mix_grad, vec, through, share):
    shard, width = mix_grad.shape
    head_width = NH * HD
    count = len(through)
    pieces_of = []
    for i, array in enumerate(through):
        size = 128 if array.shape[0] % 128 == 0 else array.shape[0]
        pieces_of += [(i, row, size) for row in range(0, array.shape[0], size)]

    def kernel(mix_ref, vec_ref, *refs):
        given, (qkv_out, out_out), refs = refs[:count], refs[count : count + 2], refs[count + 2 :]
        small, passed, held, sems = refs[:8], refs[8 : 8 + count], refs[8 + count : -1], refs[-1]
        ins, outs = [], []
        for i, row, size in pieces_of:
            span = pl.ds(row, size)
            ins.append(
                pltpu.make_async_copy(
                    given[i].at[span], held[i].at[span], sems.at[0, len(ins)]
                )
            )
            outs.append(
                pltpu.make_async_copy(
                    held[i].at[span], passed[i].at[span], sems.at[1, len(outs)]
                )
            )
        for copy in ins:
            copy.start()
        for i in range(len(ins)):
            ins[i].wait()
            outs[i].start()
        tensor = lax.axis_index("tensor")
        turned = mix_ref[...].T
        pieces = []
        for h in range(NH):
            for part in range(3):
                low = part * WIDE + h * HD
                pieces.append(turned[low : low + HD])
        qkv_out[...] = jnp.concatenate(pieces, axis=0).T
        for part in range(3):
            low = part * WIDE + head_width
            out_out[part * HD : (part + 1) * HD] = turned[low : low + HD]
        rows = vec_ref[0:8]
        moved = rows
        for i in range(1, 4):
            moved = jnp.where(tensor == i, pltpu.roll(rows, 128 - i * share, 1), moved)
        for i, row in enumerate((0, 1, 4, 5, 6, 7)):
            small[i][...] = moved[row : row + 1, 0:share]
        small[6][...] = moved[2:4, 0:share]
        small[7][...] = vec_ref[pl.ds(8 + tensor, 1)][:, 0:shard]
        for copy in outs:
            copy.wait()

    f32 = lambda *shape: jax.ShapeDtypeStruct(shape, F32)
    return pl.pallas_call(
        kernel,
        out_shape=(f32(shard, 3 * head_width), f32(head_width, shard))
        + (f32(1, share),) * 6
        + (f32(2, share), f32(1, shard))
        + tuple(jax.ShapeDtypeStruct(x.shape, x.dtype) for x in through),
        in_specs=[VM] * 2 + [ANY] * count,
        out_specs=(VM,) * 10 + (ANY,) * count,
        scratch_shapes=[pltpu.VMEM(x.shape, x.dtype) for x in through]
        + [pltpu.SemaphoreType.DMA((2, len(pieces_of)))],
        compiler_params=pltpu.CompilerParams(vmem_limit_bytes=VMEM_LIMIT),
        name="split_grads",
    )(mix_grad, vec, *through)


def by_tensor(row, step, index):
    moved = row
    for i in range(1, 4):
        moved = jnp.where(index == i, pltpu.roll(row, (i * step) % row.shape[1], 1), moved)
    return moved


def units_row(rows, block, n_dp):
    width = rows.shape[1]
    shard, step = width // n_dp, n_dp // 4
    lane = lax.broadcasted_iota(jnp.int32, (1, width), 1) // shard
    base = by_tensor(rows, width - step * shard, block)
    total = jnp.zeros((1, width), F32)
    for j in range(n_dp):
        moved = pltpu.roll(base[j % 4 : j % 4 + 1], (j - j // 4) * shard, 1)
        total = jnp.where(lane == j, moved, total)
    return total


def units_rows_back(row, block, n_dp):
    width = row.shape[1]
    shard, step = width // n_dp, n_dp // 4
    lane = lax.broadcasted_iota(jnp.int32, (1, width), 1) // shard
    rows = [jnp.zeros((1, width), F32) for _ in range(4)]
    for j in range(n_dp):
        moved = pltpu.roll(row, (width - (j - j // 4) * shard) % width, 1)
        rows[j % 4] = jnp.where(lane == j // 4, moved, rows[j % 4])
    return by_tensor(jnp.concatenate(rows, axis=0), step * shard, block)


def normalize(values):
    center = jnp.mean(values, axis=-1, keepdims=True)
    offset = values - center
    spread = jnp.mean(offset * offset, axis=-1, keepdims=True)
    inverse = lax.rsqrt(spread + EPSILON)
    return offset * inverse, inverse


def norm_back(normed, inverse, grad, gain):
    scaled = grad * gain
    center = jnp.mean(scaled, axis=-1, keepdims=True)
    along = jnp.mean(scaled * normed, axis=-1, keepdims=True)
    return inverse * (scaled - center - normed * along)


def product(equation, left, right):
    return jnp.einsum(equation, left, right, preferred_element_type=F32)


def per_device(
    tokens,
    thoughts,
    positions,
    lengths,
    attn_norm_gain,
    attn_norm_shift,
    qkv_weight,
    qv_bias,
    attn_out_weight,
    attn_out_bias,
    mlp_norm_gain,
    mlp_norm_shift,
    fc_weight,
    fc_bias,
    proj_weight,
    proj_bias,
    cotangent,
):
    n_dp = lax.axis_size("dp")
    n_tensor = lax.axis_size("tensor")
    rows, width = tokens.shape
    slots = rows * n_tensor
    swap_far = [(i, (i + 2) % n_tensor) for i in range(n_tensor)]

    share = width // (n_dp * n_tensor)
    small = [
        attn_norm_gain[None], attn_norm_shift[None], qv_bias, attn_out_bias[None],
        mlp_norm_gain[None], mlp_norm_shift[None], proj_bias[None], fc_bias[None],
    ]
    (
        group_low, mixed, mix_all, fc_near, fc_side, fc_far_near, proj_near, mate_grad, out_own,
        hidden, vec_all, places,
    ) = gather_inputs(
        tokens, thoughts, positions, cotangent, fc_weight, proj_weight.T, qkv_weight,
        attn_out_weight, small, n_dp,
    )
    mixed = mixed.reshape(slots, -1)
    swap_side = [(i, i + 1 - 2 * (i % 2)) for i in range(n_dp)]
    out_far = lax.ppermute(out_own, "tensor", swap_far)
    proj_far_near = lax.ppermute(proj_near, "tensor", swap_far)
    fc_far_side = lax.ppermute(fc_far_near, "dp", swap_side)
    attended, stats = attend(lengths, mixed)
    sent, out_far, proj_far_near, fc_far_side = lax.optimization_barrier(
        (attended, out_far, proj_far_near, fc_far_side)
    )
    proj_far_side = lax.ppermute(proj_far_near, "dp", swap_side)
    both, middle, chip_two = after_attention(
        sent, out_own, out_far, hidden, vec_all, n_dp, 1
    )
    chip_two, proj_far_side, proj_sent = lax.optimization_barrier(
        (chip_two, proj_far_side, proj_near)
    )
    proj_side = lax.ppermute(proj_sent, "dp", swap_side)
    chip_two = chip_two.reshape(2 * rows, width)

    first = units_both_ways(
        lengths, chip_two, cotangent, mate_grad,
        (fc_far_near, fc_far_side, proj_far_near, proj_far_side), vec_all, 13, None,
    )
    far_fc_near, far_fc_side, far_proj_one, far_proj_two, far_proj_side, far_fc_bias = first[2:]
    proj_side_far = lax.ppermute(far_proj_side, "tensor", swap_far)
    fc_far_side_in = lax.ppermute(far_fc_side, "dp", swap_side)
    second = units_both_ways(
        lengths, chip_two, cotangent, mate_grad, (fc_near, fc_side, proj_near, proj_side), vec_all, 12,
        first[:2],
    )
    last_part, grad_two_part, fc_near_grad, fc_side_grad, proj_one, proj_two, proj_side_grad = second[:7]
    far_proj_one, grad_two_part = lax.optimization_barrier((far_proj_one, grad_two_part))
    proj_one_far = lax.ppermute(far_proj_one, "tensor", swap_far)
    fc_near_side_in = lax.ppermute(fc_side_grad, "dp", swap_side)
    grad_heads, grad_middle, grad_out, far_out, vec_part, fc_cross, proj_cross = before_attention_back(
        lengths, grad_two_part.reshape(2, rows, width), middle, cotangent, both, out_own, out_far,
        vec_all, (far_fc_near, fc_far_side_in, proj_side_grad, proj_side_far), n_dp, 2,
    )
    grad_heads, fc_cross, proj_cross, far_proj_two, proj_one_far = lax.optimization_barrier(
        (grad_heads, fc_cross, proj_cross, far_proj_two, proj_one_far)
    )
    fc_cross = lax.ppermute(fc_cross, "tensor", swap_far)
    proj_cross = lax.ppermute(proj_cross, "dp", swap_side)
    proj_two_far = lax.ppermute(far_proj_two, "tensor", swap_far)
    last_low = last_part.reshape(2, rows, width)

    grad_mixed = attend_back(lengths, mixed, attended, stats, grad_heads)
    arrays = {
        "fc_near": fc_near_grad, "fc_near_side": fc_near_side_in, "fc_cross": fc_cross,
        "proj_near": (proj_one, proj_two), "proj_near_far": (proj_one_far, proj_two_far),
        "proj_cross": proj_cross,
        "grad_mixed": grad_mixed.reshape(n_tensor, rows, width), "mix": mix_all,
        "last": last_low, "group": group_low,
        "out_own": grad_out, "out_far": far_out,
        "vec_all": vec_all, "vec_part": vec_part, "bias_own": second[7], "bias_far": far_fc_bias,
        "hidden": hidden, "grad_middle": grad_middle, "middle": middle, "positions": places,
    }
    fc_grad, proj_grad, mix_grad, vec, grad_tokens, grad_thoughts, block_out = finish_grads(
        lengths, arrays, n_dp, 8
    )
    parts = split_grads(
        mix_grad, vec, (fc_grad, proj_grad, grad_tokens, grad_thoughts, block_out), share
    )
    qkv_grad, out_grad = parts[:2]
    gain_one, shift_one, out_bias, gain_two, shift_two, last_bias = [p[0] for p in parts[2:8]]
    query_value, hidden_bias = parts[8], parts[9][0]
    fc_grad, proj_grad, grad_tokens, grad_thoughts, block_out = parts[10:]
    return (
        block_out,
        grad_tokens,
        grad_thoughts,
        gain_one,
        shift_one,
        qkv_grad,
        query_value,
        out_grad,
        out_bias,
        gain_two,
        shift_two,
        fc_grad,
        hidden_bias,
        proj_grad.T,
        last_bias,
    )


def solution(mesh):
    rows = P(("dp", "tensor"), None)
    line = P(("dp", "tensor"))
    in_specs = (
        rows, rows, line, P("dp", None), line, line, P("dp", "tensor"),
        P(None, ("dp", "tensor")), P("tensor", "dp"), line, line, line,
        P("dp", "tensor"), line, P("tensor", "dp"), line, rows,
    )
    out_specs = (
        rows, rows, rows, line, line, P("dp", "tensor"), P(None, ("dp", "tensor")),
        P("tensor", "dp"), line, line, line, P("dp", "tensor"), line, P("tensor", "dp"), line,
    )
    return jax.shard_map(
        per_device, mesh=mesh, in_specs=in_specs, out_specs=out_specs, check_vma=False
    )
```

```python
import functools
import math

import jax
import jax.numpy as jnp
from jax import lax
from jax.experimental import pallas as pl
from jax.experimental.pallas import tpu as pltpu
from jax.sharding import PartitionSpec as P

H = 12
HD = 64
FF = 3072
SEQ_DEV = 3
EPSILON = 1e-05
MASKED = -1e30
NH = 3
SLABS = 2
WIDE = SLABS * 128
BQ = 512
BK = 512
SUMMED = HD + 16
VEC_ROWS = 16
VMEM_LIMIT = 67043328
ROW_TILE = 256
GELU_SCALE = math.sqrt(2.0 / math.pi)
GELU_CUBE = 0.044715
MESH = pl.DeviceIdType.MESH
ANY = pl.BlockSpec(memory_space=pltpu.HBM)
VM = pl.BlockSpec(memory_space=pltpu.VMEM)
SM = pl.BlockSpec(memory_space=pltpu.SMEM)
LOW = jnp.bfloat16
F32 = jnp.float32


def nn(a, b):
    return lax.dot_general(a, b, (((1,), (0,)), ((), ())), preferred_element_type=jnp.float32)


def nt(a, b):
    return lax.dot_general(a, b, (((1,), (1,)), ((), ())), preferred_element_type=jnp.float32)


def tn(a, b):
    return lax.dot_general(a, b, (((0,), (0,)), ((), ())), preferred_element_type=jnp.float32)


def head_rows(slab, head):
    half = slab[(head % 2) * HD : (head % 2 + 1) * HD]
    zero = jnp.zeros_like(half)
    return jnp.concatenate([half, zero] if head % 2 == 0 else [zero, half], axis=0)


def ends_of(lengths_ref):
    ends = [lengths_ref[0, 0]]
    for i in range(1, SEQ_DEV):
        ends.append(ends[-1] + lengths_ref[0, i])
    return ends


def segment_start(ends, slots):
    start = jnp.zeros_like(slots)
    for i in range(SEQ_DEV):
        start = jnp.where(slots >= ends[i], ends[i], start)
    return start


def segment_stop(ends, slot, slots):
    stop = slots
    for i in reversed(range(SEQ_DEV)):
        stop = jnp.where(slot < ends[i], ends[i], stop)
    return stop


def attend_kernel(
    lengths_ref, mixed_in, out_ref, stat_ref, mixed_ref, qt_ref, vt_ref, sems
):
    tokens = mixed_ref.shape[0]
    ends = ends_of(lengths_ref)
    count = (ends[-1] + BQ - 1) // BQ
    half = BQ // 2

    def load(block):
        rows = pl.ds(pl.multiple_of(block * BQ, BQ), BQ)
        return pltpu.make_async_copy(mixed_in.at[rows], mixed_ref.at[rows], sems.at[block])

    for block in range(tokens // BQ):
        load(block).start()
    for h in range(NH):
        vt_ref[h * SUMMED + HD : (h + 1) * SUMMED] = jnp.ones((SUMMED - HD, tokens), jnp.bfloat16)

    def step(rows, keys, columns, queries, first, causal, state):
        size = queries[0].shape[1]
        slots = first + lax.broadcasted_iota(jnp.int32, (1, size), 1)
        start = segment_start(ends, slots)
        key_ids = rows + lax.broadcasted_iota(jnp.int32, (keys, size), 0)
        allowed = key_ids >= start
        if causal:
            allowed = allowed & (key_ids <= slots)
        span = pl.ds(rows, keys)
        result = []
        for h in range(NH):
            peak, acc = state[h]
            low = WIDE + (h // 2) * 128
            scores = nn(mixed_ref[span, low : low + 128], queries[h])
            scores = jnp.where(allowed, scores, MASKED)
            fresh = jnp.maximum(peak, jnp.max(scores, axis=0, keepdims=True))
            weight = jnp.exp(scores - fresh)
            decay = jnp.exp(peak - fresh)
            values = vt_ref[h * SUMMED : (h + 1) * SUMMED, span]
            acc = acc * decay + nn(values, weight.astype(jnp.bfloat16))
            result.append((fresh, acc))
        return tuple(result)

    def query_block(block, carry):
        first = pl.multiple_of(block * BQ, BQ)
        columns = pl.ds(first, BQ)
        load(block).wait()
        for slab in range(SLABS):
            low = slab * 128
            qt_ref[low : low + 128] = (mixed_ref[columns, low : low + 128] * HD ** (-0.5)).T
            turned = mixed_ref[columns, 2 * WIDE + low : 2 * WIDE + low + 128].T
            for h in range(2 * slab, min(2 * slab + 2, NH)):
                piece = turned[(h % 2) * HD : (h % 2 + 1) * HD]
                vt_ref[h * SUMMED : h * SUMMED + HD, columns] = piece
        queries = [head_rows(qt_ref[(h // 2) * 128 : (h // 2 + 1) * 128], h) for h in range(NH)]

        def key_block(key, state):
            return step(pl.multiple_of(key * BK, BK), BK, columns, queries, first, False, state)

        empty = tuple(
            (
                jnp.full((1, BQ), MASKED, jnp.float32),
                jnp.zeros((SUMMED, BQ), jnp.float32),
            )
            for _ in range(NH)
        )
        state = lax.fori_loop(segment_start(ends, first) // BK, block, key_block, empty)
        for side, keys in ((0, half), (1, BQ)):
            piece = slice(side * half, (side + 1) * half)
            final = step(
                first, keys, columns, [q[:, piece] for q in queries], first + side * half, True,
                tuple(tuple(x[:, piece] for x in one) for one in state),
            )
            for h in range(NH):
                peak, acc = final[h]
                total = acc[HD : HD + 1]
                place_here = pl.ds(pl.multiple_of(first + side * half, half), half)
                out_ref[h * HD : (h + 1) * HD, place_here] = (acc[:HD] / total).astype(
                    jnp.bfloat16
                )
                stat_ref[h : h + 1, place_here] = peak + jnp.log(total)
        return carry

    lax.fori_loop(0, count, query_block, 0)

    def padded_block(block, carry):
        load(block).wait()
        columns = pl.ds(pl.multiple_of(block * BQ, BQ), BQ)
        out_ref[:, columns] = jnp.zeros((out_ref.shape[0], BQ), jnp.bfloat16)
        return carry

    lax.fori_loop(count, tokens // BQ, padded_block, 0)


def attend(lengths, mixed):
    tokens = mixed.shape[0]
    vm = pl.BlockSpec(memory_space=pltpu.VMEM)
    return pl.pallas_call(
        attend_kernel,
        out_shape=(
            jax.ShapeDtypeStruct((NH * HD, tokens), jnp.bfloat16),
            jax.ShapeDtypeStruct((8, tokens), jnp.float32),
        ),
        in_specs=[pl.BlockSpec(memory_space=pltpu.SMEM), pl.BlockSpec(memory_space=pltpu.HBM)],
        out_specs=(vm, vm),
        scratch_shapes=[
            pltpu.VMEM(mixed.shape, mixed.dtype),
            pltpu.VMEM((WIDE, BQ), jnp.bfloat16),
            pltpu.VMEM((NH * SUMMED, tokens), jnp.bfloat16),
            pltpu.SemaphoreType.DMA((tokens // BQ,)),
        ],
        compiler_params=pltpu.CompilerParams(vmem_limit_bytes=VMEM_LIMIT),
        cost_estimate=pl.CostEstimate(
            flops=8 * tokens * tokens * NH * HD,
            bytes_accessed=16 * tokens * WIDE,
            transcendentals=tokens * tokens,
        ),
        name="attend",
    )(lengths, mixed)


def attend_back_kernel(
    lengths_ref, mixed_in, out_in, stat_ref, gradt_in,
    gmixed_out, mixed_ref, out_ref, gradt_ref, gmixed_ref, qt_ref, kt_ref, grad_ref, delta_ref,
    dqt_ref, sems, out_sems
):
    tokens = mixed_ref.shape[0]
    blocks = tokens // BQ
    ends = ends_of(lengths_ref)
    count = (ends[-1] + BK - 1) // BK
    half = BQ // 2

    def loads(block):
        rows = pl.ds(pl.multiple_of(block * BQ, BQ), BQ)
        return (
            pltpu.make_async_copy(mixed_in.at[rows], mixed_ref.at[rows], sems.at[0, block]),
            pltpu.make_async_copy(out_in.at[:, rows], out_ref.at[:, rows], sems.at[1, block]),
            pltpu.make_async_copy(gradt_in.at[:, rows], gradt_ref.at[:, rows], sems.at[2, block]),
        )

    def leave(block, part):
        rows = pl.ds(pl.multiple_of(block * BQ, BQ), BQ)
        lanes = pl.ds(0, WIDE) if part == 0 else pl.ds(WIDE, 2 * WIDE)
        return pltpu.make_async_copy(
            gmixed_ref.at[rows, lanes], gmixed_out.at[rows, lanes], out_sems.at[part, block]
        )

    for block in reversed(range(blocks)):
        for copy in loads(block):
            copy.start()
    dqt_ref[...] = jnp.zeros_like(dqt_ref)

    def prepare_block(block):
        rows = pl.ds(pl.multiple_of(block * BQ, BQ), BQ)
        for slab in range(SLABS):
            low = slab * 128
            qt_ref[low : low + 128, rows] = (
                mixed_ref[rows, low : low + 128] * HD ** (-0.5)
            ).T
            kt_ref[low : low + 128, rows] = mixed_ref[rows, WIDE + low : WIDE + low + 128].T
        grad_ref[rows, 0:128] = gradt_ref[0:128, rows].T
        grad_ref[rows, 128:256] = jnp.concatenate(
            [gradt_ref[128:192, rows], jnp.zeros((64, BQ), jnp.bfloat16)], axis=0
        ).T
        for h in range(NH):
            product = gradt_ref[h * HD : (h + 1) * HD, rows].astype(jnp.float32) * out_ref[
                h * HD : (h + 1) * HD, rows
            ].astype(jnp.float32)
            delta_ref[h : h + 1, rows] = jnp.sum(product, axis=0, keepdims=True)

    def terms(base, keys, first, size, causal):
        rows, columns = pl.ds(base, keys), pl.ds(first, size)
        slots = first + lax.broadcasted_iota(jnp.int32, (1, size), 1)
        key_ids = base + lax.broadcasted_iota(jnp.int32, (keys, size), 0)
        allowed = key_ids >= segment_start(ends, slots)
        if causal:
            allowed = allowed & (key_ids <= slots)
        lane = lax.broadcasted_iota(jnp.int32, (size, 128), 1)
        grad_keys, grad_values = [None] * SLABS, [None] * SLABS
        for h in range(NH):
            slab = h // 2
            low, high = slab * 128, slab * 128 + 128
            queries = head_rows(qt_ref[low:high, columns], h)
            scores = nn(mixed_ref[rows, WIDE + low : WIDE + high], queries)
            probs = jnp.where(allowed, jnp.exp(scores - stat_ref[h : h + 1, columns]), 0.0)
            keep = (lane // HD) == (h % 2)
            value = nn(probs.astype(jnp.bfloat16), jnp.where(keep, grad_ref[columns, low:high], 0.0))
            if h == NH - 1 and NH % 2 == 1:
                grad_rows = jnp.concatenate(
                    [gradt_ref[h * HD : (h + 1) * HD, columns], jnp.zeros((HD, size), jnp.bfloat16)],
                    axis=0,
                )
            else:
                grad_rows = head_rows(gradt_ref[low:high, columns], h)
            grad_probs = nn(mixed_ref[rows, 2 * WIDE + low : 2 * WIDE + high], grad_rows)
            grad_scores = (probs * (grad_probs - delta_ref[h : h + 1, columns])).astype(
                jnp.bfloat16
            )
            key_term = nn(grad_scores, jnp.where(keep, mixed_ref[columns, low:high], 0.0))
            grad_values[slab] = value if grad_values[slab] is None else grad_values[slab] + value
            grad_keys[slab] = key_term if grad_keys[slab] is None else grad_keys[slab] + key_term
            dqt_ref[h * HD : (h + 1) * HD, columns] += nn(
                kt_ref[h * HD : (h + 1) * HD, rows], grad_scores
            )
        return grad_keys + grad_values

    def key_block(turn, carry):
        key = count - 1 - turn
        for copy in loads(key):
            copy.wait()
        prepare_block(key)
        base = pl.multiple_of(key * BK, BK)
        rows = pl.ds(base, BK)
        upper = terms(base, half, base, BQ, True)
        lower = terms(pl.multiple_of(base + half, half), half, pl.multiple_of(base + half, half), half, True)
        state = tuple(jnp.concatenate([a, b], axis=0) for a, b in zip(upper, lower))

        def query_block(block, state):
            fresh = terms(base, BK, pl.multiple_of(block * BQ, BQ), BQ, False)
            return tuple(a + b for a, b in zip(state, fresh))

        stop = jnp.minimum(segment_stop(ends, base + BK - 1, tokens), ends[-1])
        state = lax.fori_loop(key + 1, (stop - 1) // BQ + 1, query_block, state)
        for slab in range(SLABS):
            low = slab * 128
            gmixed_ref[rows, WIDE + low : WIDE + low + 128] = (
                state[slab] * HD ** (-0.5)
            ).astype(jnp.bfloat16)
            gmixed_ref[rows, 2 * WIDE + low : 2 * WIDE + low + 128] = state[SLABS + slab].astype(
                jnp.bfloat16
            )
        leave(key, 1).start()
        return carry

    def padded_block(key, carry):
        for copy in loads(key):
            copy.wait()
        rows = pl.ds(pl.multiple_of(key * BK, BK), BK)
        gmixed_ref[rows, WIDE:] = jnp.zeros((BK, 2 * WIDE), jnp.bfloat16)
        leave(key, 1).start()
        return carry

    lax.fori_loop(count, blocks, padded_block, 0)
    lax.fori_loop(0, count, key_block, 0)
    for block in range(blocks):
        rows = pl.ds(block * BQ, BQ)
        for slab in range(SLABS):
            low = slab * 128
            gmixed_ref[rows, low : low + 128] = (
                (dqt_ref[low : low + 128, rows] * HD ** (-0.5)).T.astype(jnp.bfloat16)
            )
        leave(block, 0).start()
    for block in range(blocks):
        leave(block, 0).wait()
        leave(block, 1).wait()


def attend_back(lengths, mixed, out, stat, gradt):
    tokens = mixed.shape[0]
    vm = pl.BlockSpec(memory_space=pltpu.VMEM)
    hbm = pl.BlockSpec(memory_space=pltpu.HBM)
    return pl.pallas_call(
        attend_back_kernel,
        out_shape=jax.ShapeDtypeStruct((tokens, 3 * WIDE), jnp.bfloat16),
        in_specs=[pl.BlockSpec(memory_space=pltpu.SMEM), hbm, hbm, vm, hbm],
        out_specs=hbm,
        scratch_shapes=[
            pltpu.VMEM(mixed.shape, jnp.bfloat16),
            pltpu.VMEM(out.shape, jnp.bfloat16),
            pltpu.VMEM(gradt.shape, jnp.bfloat16),
            pltpu.VMEM(mixed.shape, jnp.bfloat16),
            pltpu.VMEM((WIDE, tokens), jnp.bfloat16),
            pltpu.VMEM((WIDE, tokens), jnp.bfloat16),
            pltpu.VMEM((tokens, WIDE), jnp.bfloat16),
            pltpu.VMEM((8, tokens), jnp.float32),
            pltpu.VMEM((WIDE, tokens), jnp.float32),
            pltpu.SemaphoreType.DMA((3, tokens // BQ)),
            pltpu.SemaphoreType.DMA((2, tokens // BQ)),
        ],
        compiler_params=pltpu.CompilerParams(vmem_limit_bytes=VMEM_LIMIT),
        cost_estimate=pl.CostEstimate(
            flops=20 * tokens * tokens * NH * HD,
            bytes_accessed=32 * tokens * WIDE,
            transcendentals=tokens * tokens,
        ),
        name="attend_back",
    )(lengths, mixed, out, stat, gradt)


class Copies:
    def __init__(self, send, recv):
        self.send, self.recv, self.made, self.started = send, recv, 0, []

    def plan(self, source, target, device):
        index = self.made
        self.made += 1
        return pltpu.make_async_remote_copy(
            src_ref=source,
            dst_ref=target,
            send_sem=self.send.at[index],
            recv_sem=self.recv.at[index],
            device_id=device,
            device_id_type=MESH,
        )

    def begin(self, copy, condition=None):
        self.started.append((copy, condition))
        when(condition, copy.start)

    def start(self, source, target, device):
        copy = self.plan(source, target, device)
        self.begin(copy)
        return copy

    def finish(self):
        for copy, condition in self.started:
            when(condition, copy.wait_send)


class Several:
    def __init__(self, copies):
        self.copies = copies

    def start(self):
        for copy in self.copies:
            copy.start()

    def wait(self):
        for copy in self.copies:
            copy.wait()


def when(condition, action):
    if condition is None:
        action()
    else:
        pl.when(condition)(action)


def greet(devices):
    barrier = pltpu.get_barrier_semaphore()
    for device, condition in devices:
        when(
            condition,
            lambda device=device: pl.semaphore_signal(
                barrier, inc=1, device_id=device, device_id_type=MESH
            ),
        )
    present = [1 if condition is None else condition.astype(jnp.int32) for _, condition in devices]
    pl.semaphore_wait(barrier, sum(present))


class Place:
    def __init__(self, line):
        self.dp = dp = lax.axis_index("dp")
        self.tensor = tensor = lax.axis_index("tensor")
        self.spot, self.side = spot, side = dp // 2, dp % 2
        self.chip, self.core = tensor // 2, tensor % 2
        self.has_up, self.has_down = spot + 1 < line, spot > 0
        self.up = (jnp.minimum(spot + 1, line - 1) * 2 + side, tensor)
        self.down = (jnp.maximum(spot - 1, 0) * 2 + side, tensor)
        self.across = (spot * 2 + 1 - side, tensor)
        self.mate = (dp, tensor + 1 - 2 * (tensor % 2))
        self.far = (dp, (tensor + 2) % 4)
        self.corner = (dp, 3 - tensor)

    def everyone(self):
        return [
            (self.mate, None), (self.far, None), (self.corner, None), (self.across, None),
            (self.up, self.has_up), (self.down, self.has_down),
        ]


def comm_call(kernel, name, outputs, inputs, in_specs, out_specs, copies, cid, scratch=(), local=1, limit=VMEM_LIMIT):
    return pl.pallas_call(
        kernel,
        out_shape=outputs,
        in_specs=in_specs,
        out_specs=out_specs,
        scratch_shapes=list(scratch)
        + [
            pltpu.SemaphoreType.DMA((copies,)),
            pltpu.SemaphoreType.DMA((copies,)),
            pltpu.SemaphoreType.DMA((local,)),
        ],
        compiler_params=pltpu.CompilerParams(
            collective_id=cid, has_side_effects=True, vmem_limit_bytes=limit
        ),
        name=name,
    )(*inputs)


def one_hot(rows, columns, shift, limit):
    lane = lax.broadcasted_iota(jnp.int32, (rows, columns), 0)
    spot = lax.broadcasted_iota(jnp.int32, (rows, columns), 1)
    return ((spot == lane + shift) & (lane < limit)).astype(LOW)


def gather_inputs(tokens, thoughts, positions, cotangent, fc, proj, qkv, out, vectors, n_dp):
    line = n_dp // 2
    hops = line - 1
    rows, width = tokens.shape
    latents = thoughts.shape[0]
    window = rows // latents
    shard = fc.shape[0]
    half_rows = rows // 2
    share = width // (n_dp * 4)

    def kernel(
        pos_ref, tokens_in, thoughts_in, cot_ref, fc_in, proj_in, qkv_in, out_in, *refs
    ):
        given = (fc_in, tokens_in, thoughts_in, proj_in, qkv_in, out_in) + refs[: len(vectors)]
        (
            normed_out, mixed_out, mix_out, fc_near, fc_side, fc_far, proj_near, cot_out, out_out,
            hidden_out, vec_out, pos_out,
            hidden_ref, mix_ref, vec_ref, tile,
            land, mix_land, tiles, tile_land, normed, mixed, out_turned,
            *held, arrive, send, recv, local,
        ) = refs[len(vectors) :]
        arrivals = [
            pltpu.make_async_copy(given[i], held[i], arrive.at[i]) for i in range(len(given))
        ]
        for copy in arrivals:
            copy.start()
        fc_ref, tokens_ref, thoughts_ref, proj_ref, qkv_ref, out_ref = held[:6]
        vec_refs = held[6:]
        at = Place(line)
        dp, tensor, spot, side = at.dp, at.tensor, at.spot, at.side
        mate_row, far_row, corner_row = at.mate[1], at.far[1], at.corner[1]
        greet(at.everyone())
        copies = Copies(send, recv)
        MIX, FC, PROJ, VEC = range(4)
        own = [mix_ref, fc_ref, proj_ref, tiles.at[dp]]

        def seat(item, position):
            if item == MIX:
                return mix_land.at[position * 2 + side]
            if item == FC:
                return fc_near.at[position]
            if item == PROJ:
                return proj_near.at[position]
            return tiles.at[position * 2 + side]

        def plan(item, hop):
            above, below = jnp.maximum(spot - hop, 0), jnp.minimum(spot + hop, line - 1)
            came_up = jnp.maximum(spot - 1 - hop, 0)
            came_down = jnp.minimum(spot + 1 + hop, line - 1)
            made = {
                "up": copies.plan(
                    own[item] if hop == 0 else seat(item, above), seat(item, above), at.up
                ),
                "down": copies.plan(
                    own[item] if hop == 0 else seat(item, below), seat(item, below), at.down
                ),
                "onward": [],
            }
            for position in (came_up, came_down):
                onward = []
                if item in (MIX, VEC):
                    onward.append(copies.plan(seat(item, position), seat(item, position), at.across))
                if item == FC:
                    onward.append(copies.plan(fc_near.at[position], fc_side.at[position], at.across))
                    onward.append(copies.plan(fc_near.at[position], fc_far.at[position], at.far))
                made["onward"].append(onward)
            return made

        plans = [[plan(item, hop) for hop in range(hops)] for item in range(4)]

        def launch(item):
            copies.begin(plans[item][0]["up"], at.has_up)
            copies.begin(plans[item][0]["down"], at.has_down)

        def handle(item, hop):
            made = plans[item][hop]
            for way, key, comes, goes in (
                (0, "up", spot - 1 - hop >= 0, at.has_up),
                (1, "down", spot + 1 + hop < line, at.has_down),
            ):
                when(comes, made[key].wait_recv)
                if hop + 1 < hops:
                    copies.begin(plans[item][hop + 1][key], comes & goes)
                for copy in made["onward"][way]:
                    copies.begin(copy, comes)

        def settle(item):
            for hop in range(hops):
                for way, comes in ((0, spot - 1 - hop >= 0), (1, spot + 1 + hop < line)):
                    for copy in plans[item][hop]["onward"][way]:
                        when(comes, copy.wait_recv)

        stays = []

        def stay(source, target):
            copy = pltpu.make_async_copy(source, target, local.at[len(stays)])
            copy.start()
            stays.append(copy)
            return copy

        parts = [pl.ds(0, half_rows), pl.ds(half_rows, half_rows)]
        arrivals[0].wait()
        launch(FC)
        fc_sides = [copies.start(fc_ref, fc_side.at[spot], at.across)]
        cot_made = copies.start(cot_ref, cot_out, at.mate)
        for copy in arrivals[6:]:
            copy.wait()
        tile[...] = jnp.zeros_like(tile)
        row = 0
        for ref in vec_refs:
            count, size = ref.shape
            tile[row : row + count, 0:size] = ref[...].astype(F32)
            row += count
        vec_ref[...] = tile[...].astype(LOW)
        vec_made = [
            copies.start(vec_ref, tile_land.at[i], device)
            for i, device in enumerate((at.mate, at.far, at.corner))
        ]
        arrivals[1].wait()
        arrivals[2].wait()
        pos_row = lax.broadcasted_iota(jnp.int32, (latents, 128), 0)
        places = jnp.zeros((latents, 128), jnp.int32)
        for w in range(latents):
            places = jnp.where(pos_row == w, pos_ref[w], places)
            span = pl.ds(w * window, window)
            here = lax.broadcasted_iota(jnp.int32, (window, 1), 0) == pos_ref[w] - w * window
            hidden_ref[span] = jnp.where(
                here, thoughts_ref[w : w + 1].astype(F32), tokens_ref[span].astype(F32)
            ).astype(LOW)
        pos_out[...] = places
        far_made = [
            copies.start(hidden_ref.at[part], land.at[2, part], at.far) for part in parts
        ]
        mate_made = copies.start(hidden_ref, land.at[1], at.mate)
        fc_sides.append(copies.start(fc_ref, fc_far.at[spot], at.far))
        for copy in arrivals[3:6]:
            copy.wait()
        turned = qkv_ref[...].astype(F32).T
        extra = out_ref[...].astype(F32)
        pieces = []
        for p in range(3):
            for h in range(NH):
                low = (h * 3 + p) * HD
                pieces.append(turned[low : low + HD])
            pieces.append(extra[p * HD : (p + 1) * HD])
        mix_ref[...] = jnp.concatenate(pieces, axis=0).T.astype(LOW)
        launch(MIX)
        mix_side = copies.start(mix_ref, mix_land.at[dp], at.across)
        stay(hidden_ref, hidden_out)
        stay(fc_ref, fc_near.at[spot])
        stay(proj_ref, proj_near.at[spot])
        mix_land[dp] = mix_ref[...]
        for copy in vec_made:
            copy.wait_recv()
        merged = jnp.zeros((VEC_ROWS, 128), F32)
        bias_rows = jnp.zeros((VEC_ROWS, 128), F32)
        row_ids = lax.broadcasted_iota(jnp.int32, (VEC_ROWS, 128), 0)
        for i, index in enumerate((tensor, mate_row, far_row, corner_row)):
            tile = vec_ref[...] if i == 0 else tile_land[i - 1]
            merged += nn(tile, one_hot(128, 128, index * share, share))
            bias_rows = jnp.where(row_ids == 8 + index, tile[8:9].astype(F32), bias_rows)
        tiles[dp] = jnp.where(row_ids < 8, merged, bias_rows).astype(LOW)
        launch(VEC)
        vec_side = copies.start(tiles.at[dp], tiles.at[dp], at.across)

        def norm_rows(source, index):
            @pl.loop(0, rows // 128)
            def _(i):
                span = pl.ds(pl.multiple_of(i * 128, 128), 128)
                normed[index, span] = normalize(source[span].astype(F32))[0].astype(LOW)

            stay(normed.at[index], normed_out.at[index])

        def relay(i):
            far_made[i].wait_recv()
            return copies.start(land.at[2, parts[i]], land.at[3, parts[i]], at.mate)

        def mix_rows(index):
            @pl.loop(0, rows // 256)
            def _(i):
                span = pl.ds(pl.multiple_of(i * 256, 256), 256)
                turned = normed[index, span].astype(F32) * whole[0:1] + whole[1:2]
                weight = mix_land[...].reshape(width, width)
                mixed[index, span] = (nn(turned.astype(LOW), weight) + bias).astype(LOW)

            stay(mixed.at[index], mixed_out.at[index])

        norm_rows(hidden_ref, tensor)
        relayed = []
        for step in range(hops + 2):
            for item, hop in ((MIX, step), (VEC, step), (FC, step - 1), (PROJ, step - 2)):
                if 0 <= hop < hops:
                    handle(item, hop)
            if step == 0:
                launch(PROJ)
                mate_made.wait_recv()
                norm_rows(land.at[1], mate_row)
                relayed.append(relay(0))
            if step == 1:
                relayed.append(relay(1))
                norm_rows(land.at[2], far_row)
            if step == hops:
                mix_side.wait_recv()
                vec_side.wait_recv()
                settle(MIX)
                settle(VEC)
                whole = jnp.zeros((VEC_ROWS, width), F32)
                for i in range(n_dp):
                    whole += nn(tiles[i], one_hot(128, width, i * shard, shard))
                vec_out[...] = whole
                for i, block in enumerate((tensor, far_row)):
                    vec_out[12 + i : 13 + i] = units_row(whole[8:12], block, n_dp)
                lane = lax.broadcasted_iota(jnp.int32, (width, WIDE), 0)
                column = lax.broadcasted_iota(jnp.int32, (width, WIDE), 1)
                pick = (lane == column + tensor * (NH * HD)) & (column < NH * HD)
                picked = nn(whole.astype(LOW), pick.astype(LOW))
                bias = jnp.concatenate(
                    [picked[2:3], jnp.zeros((1, WIDE), F32), picked[3:4]], axis=1
                )
                mix_rows(tensor)
                mix_rows(mate_row)
                mix_rows(far_row)
                for copy in relayed:
                    copy.wait_recv()
                norm_rows(land.at[3], corner_row)
                mix_rows(corner_row)
                stay(mix_land, mix_out)
                weight = mix_land[...].reshape(width, width)
                for part in range(3):
                    low = part * WIDE + WIDE - 128
                    turned = weight[:, low : low + 128].T
                    out_turned[part * HD : (part + 1) * HD] = turned[128 - HD :]
                stay(out_turned, out_out)
        settle(FC)
        for copy in fc_sides:
            copy.wait_recv()
        cot_made.wait_recv()
        copies.finish()
        for copy in stays:
            copy.wait()

    low = lambda *shape: jax.ShapeDtypeStruct(shape, LOW)
    outputs = (
        low(4, rows, width), low(4, rows, width), low(n_dp, shard, width),
        low(line, shard, width), low(line, shard, width), low(line, shard, width),
        low(line, shard, width), low(rows, width), low(NH * HD, width), low(rows, width),
        jax.ShapeDtypeStruct((VEC_ROWS, width), F32),
        jax.ShapeDtypeStruct((latents, 128), jnp.int32),
    )
    scratch = [
        pltpu.VMEM((rows, width), LOW),
        pltpu.VMEM((shard, 3 * WIDE), LOW),
        pltpu.VMEM((VEC_ROWS, 128), LOW),
        pltpu.VMEM((VEC_ROWS, 128), F32),
        pltpu.VMEM((4, rows, width), LOW),
        pltpu.VMEM((n_dp, shard, width), LOW),
        pltpu.VMEM((n_dp, VEC_ROWS, 128), LOW),
        pltpu.VMEM((3, VEC_ROWS, 128), LOW),
        pltpu.VMEM((4, rows, width), LOW),
        pltpu.VMEM((4, rows, width), LOW),
        pltpu.VMEM((NH * HD, width), LOW),
    ]
    given = (fc, tokens, thoughts, proj, qkv, out, *vectors)
    scratch += [pltpu.VMEM(x.shape, x.dtype) for x in given]
    scratch.append(pltpu.SemaphoreType.DMA((len(given),)))
    return comm_call(
        kernel,
        "gather_inputs",
        outputs,
        (positions, tokens, thoughts, cotangent, fc, proj, qkv, out, *vectors),
        [SM] + [ANY] * (7 + len(vectors)),
        (ANY,) * 10 + (VM, VM),
        3 + 2 + 1 + 2 + 2 + 1 + 2 + hops * (2 * 4 + 2 * 4),
        0,
        scratch=scratch,
        local=3 + 8 + 2,
    )


def after_attention(attended, out_own, out_far, hidden, vec_all, n_dp, cid):
    head_width, slots = attended.shape
    rows, width = hidden.shape
    half_rows = rows // 2

    def kernel(
        heads_in, own_in, far_in, hidden_in, vec_ref,
        both_out, middle_out, two_out,
        heads_ref, own_ref, far_ref, hidden_ref,
        land, part, part_low, part_land, two, send, recv, local,
    ):
        loads = [
            pltpu.make_async_copy(source, target, local.at[5 + i])
            for i, (source, target) in enumerate(
                (
                    (heads_in, heads_ref), (own_in, own_ref), (far_in, far_ref),
                    (hidden_in, hidden_ref),
                )
            )
        ]
        for copy in loads:
            copy.start()
        at = Place(n_dp // 2)
        greet([(at.far, None), (at.mate, None)])
        copies = Copies(send, recv)
        cores = (at.core, 1 - at.core)
        made = [None, None]
        for i in (1, 0):
            theirs = pl.multiple_of(((1 - at.chip) * 2 + cores[i]) * rows, rows)
            made[i] = copies.start(heads_in.at[:, pl.ds(theirs, rows)], land.at[i], at.far)
        stays = []

        def stay(source, target):
            stays.append(pltpu.make_async_copy(source, target, local.at[len(stays)]))
            stays[-1].start()

        spans = []
        for copy in loads:
            copy.wait()
        for i in range(2):
            ours = pl.multiple_of((at.chip * 2 + cores[i]) * rows, rows)
            spans.append(pl.ds(ours, rows))
            stay(heads_ref.at[:, spans[i]], both_out.at[0, :, i * rows : (i + 1) * rows])
            part[i] = tn(heads_ref[:, spans[i]], own_ref[...])
        sums = None
        for i in (1, 0):
            made[i].wait_recv()
            stay(land.at[i], both_out.at[1, :, i * rows : (i + 1) * rows])
            part[i] += tn(land[i], far_ref[...])
            if i == 1:
                part_low[...] = part[1].astype(LOW)
                sums = copies.start(part_low, part_land, at.mate)
        sums.wait_recv()
        mated = []
        for piece in range(2):

            @pl.loop(0, half_rows // 128)
            def _(i):
                span = pl.ds(pl.multiple_of(piece * half_rows + i * 128, 128), 128)
                middle = (
                    hidden_ref[span].astype(F32)
                    + part[0, span]
                    + part_land[span].astype(F32)
                    + vec_ref[4:5]
                )
                middle_out[span] = middle
                two[span] = (normalize(middle)[0] * vec_ref[5:6] + vec_ref[6:7]).astype(LOW)

            span = pl.ds(piece * half_rows, half_rows)
            mated.append(copies.start(two.at[span], two_out.at[1, span], at.mate))
        stay(two, two_out.at[0])
        for copy in mated:
            copy.wait_recv()
        copies.finish()
        for copy in stays:
            copy.wait()

    return comm_call(
        kernel,
        "after_attention",
        (
            jax.ShapeDtypeStruct((2, head_width, 2 * rows), LOW),
            jax.ShapeDtypeStruct((rows, width), F32),
            jax.ShapeDtypeStruct((2, rows, width), LOW),
        ),
        (attended, out_own, out_far, hidden, vec_all),
        [ANY] * 4 + [VM],
        (ANY, VM, ANY),
        5,
        cid,
        scratch=[pltpu.VMEM(x.shape, x.dtype) for x in (attended, out_own, out_far, hidden)]
        + [
            pltpu.VMEM((2, head_width, rows), LOW),
            pltpu.VMEM((2, rows, width), F32),
            pltpu.VMEM((rows, width), LOW),
            pltpu.VMEM((rows, width), LOW),
            pltpu.VMEM((rows, width), LOW),
        ],
        local=9,
    )


def before_attention_back(
    lengths, two, middle, cotangent, both, out_own, out_far, vec_all, pairs, n_dp, cid
):
    _, rows, width = two.shape
    head_width = out_own.shape[0]
    half_rows = rows // 2

    def kernel(
        lengths_ref, two_in, middle_in, cot_in, both_in, own_in, far_in, vec_ref,
        one_a, one_b, two_a, two_b,
        heads_out, grad_out, own_out, far_out, vec_out, sum_one, sum_two,
        two_ref, middle_ref, cot_ref, both_ref, own_ref, far_ref,
        two_land, mid, stay_heads, sent_heads, held, send, recv, local,
    ):
        at = Place(n_dp // 2)
        greet([(at.far, None), (at.mate, None)])
        copies = Copies(send, recv)
        halves = [pl.ds(0, half_rows), pl.ds(half_rows, half_rows)]
        loads = [
            pltpu.make_async_copy(ref, held.at[i], local.at[2 + i])
            for i, ref in enumerate((one_a, one_b, two_a, two_b))
        ]
        early = [
            pltpu.make_async_copy(source, target, local.at[6 + i])
            for i, (source, target) in enumerate(
                (
                    (two_in.at[0], two_ref), (middle_in, middle_ref), (cot_in, cot_ref),
                    (far_in, far_ref), (own_in, own_ref), (both_in, both_ref),
                )
            )
        ]
        sums = [copies.start(two_in.at[1, span], two_land.at[span], at.mate) for span in halves]
        for copy in early + loads:
            copy.start()
        vec_out[...] = jnp.zeros_like(vec_out)
        first_row = at.tensor * rows
        live = ends_of(lengths_ref)[-1]
        mated = []
        for copy in early:
            copy.wait()
        for piece in range(2):
            sums[piece].wait_recv()

            @pl.loop(0, half_rows // 128)
            def _(i):
                start = pl.multiple_of(piece * half_rows + i * 128, 128)
                span = pl.ds(start, 128)
                grad = two_ref[span].astype(F32) + two_land[span].astype(F32)
                normed, inverse = normalize(middle_ref[span])
                ids = first_row + start + lax.broadcasted_iota(jnp.int32, (128, 1), 0)
                final = jnp.where(ids < live, cot_ref[span].astype(F32), 0.0)
                total = final + norm_back(normed, inverse, grad, vec_ref[5:6])
                grad_out[span] = total
                mid[0, span] = total.astype(LOW)
                for row, term in ((4, total), (5, normed * grad), (6, grad), (7, final)):
                    vec_out[row : row + 1] += jnp.sum(term, axis=0, keepdims=True)

            mated.append(copies.start(mid.at[0, halves[piece]], mid.at[1, halves[piece]], at.mate))
        cores = (at.core, 1 - at.core)
        made, stays = [], []
        for i in range(2):
            if i == 1:
                for copy in mated:
                    copy.wait_recv()
            ours = pl.ds(pl.multiple_of((at.chip * 2 + cores[i]) * rows, rows), rows)
            sent_heads[i] = nt(far_ref[...], mid[i]).astype(LOW)
            made.append(copies.start(sent_heads.at[i], heads_out.at[:, ours], at.far))
            stay_heads[i] = nt(own_ref[...], mid[i]).astype(LOW)
            stays.append(
                pltpu.make_async_copy(stay_heads.at[i], heads_out.at[:, ours], local.at[i])
            )
            stays[-1].start()
        grads = mid[...].reshape(2 * rows, width)
        own_out[...] = nn(both_ref[0], grads).astype(LOW)
        far_out[...] = nn(both_ref[1], grads).astype(LOW)
        for copy in loads:
            copy.wait()
        sum_one[...] = (held[0].astype(F32) + held[1].astype(F32)).astype(LOW)
        sum_two[...] = (held[2].astype(F32) + held[3].astype(F32)).astype(LOW)
        for copy in made:
            copy.wait_recv()
        copies.finish()
        for copy in stays:
            copy.wait()

    return comm_call(
        kernel,
        "before_attention_back",
        (
            jax.ShapeDtypeStruct((head_width, 4 * rows), LOW),
            jax.ShapeDtypeStruct((rows, width), F32),
            jax.ShapeDtypeStruct((head_width, width), LOW),
            jax.ShapeDtypeStruct((head_width, width), LOW),
            jax.ShapeDtypeStruct((VEC_ROWS, width), F32),
            jax.ShapeDtypeStruct(pairs[0].shape, LOW),
            jax.ShapeDtypeStruct(pairs[0].shape, LOW),
        ),
        (lengths, two, middle, cotangent, both, out_own, out_far, vec_all, *pairs),
        [SM] + [ANY] * 6 + [VM] + [ANY] * 4,
        (ANY,) + (VM,) * 6,
        6,
        cid,
        scratch=[pltpu.VMEM((rows, width), LOW)]
        + [pltpu.VMEM(x.shape, x.dtype) for x in (middle, cotangent, both, out_own, out_far)]
        + [
            pltpu.VMEM((rows, width), LOW),
            pltpu.VMEM((2, rows, width), LOW),
            pltpu.VMEM((2, head_width, rows), LOW),
            pltpu.VMEM((2, head_width, rows), LOW),
            pltpu.VMEM((4,) + pairs[0].shape, LOW),
        ],
        local=12,
    )


def finish_grads(lengths, arrays, n_dp, cid):
    part_rows = arrays["hidden"].shape[0] // 4
    flat, shapes = [], {}
    for name, array in arrays.items():
        pieces = array if isinstance(array, tuple) else (array,)
        flat += [(name, i, piece) for i, piece in enumerate(pieces)]
        lead = sum(piece.shape[0] for piece in pieces)
        shapes[name] = ((lead,) + pieces[0].shape[1:], pieces[0].dtype)
    kept = [name for name in arrays if name != "out_far"]
    line = n_dp // 2
    shard = arrays["mix"].shape[1]
    rows, width = arrays["hidden"].shape
    group = 4 * rows
    latents = arrays["positions"].shape[0]
    window = rows // latents
    far_end = line - 1
    slots = [(distance, way) for distance in range(far_end, 0, -1) for way in (0, 1)] + [(0, 0)]
    last = len(slots) - 1
    share = width // (n_dp * 4)
    FC, PROJ, MIX, VEC = range(4)

    def kernel(lengths_ref, *refs):
        refs = list(refs)

        def take(number):
            taken = refs[:number]
            del refs[:number]
            return taken

        sources = take(len(flat))
        out_source = sources[[name for name, _, _ in flat].index("out_far")]
        fc_out, proj_out, mix_out, vec_out, tokens_out, thoughts_out, block_out = take(7)
        held = dict(zip(kept, take(len(kept))))
        cross_send, cross_land = [None, None] + take(2), [None, None] + take(2)
        hop_send, hop_land = take(4), take(4)
        (
            part, mate_land, far_send, far_land, last_land, total, vec_mine, vec_land, vec_near,
            plain_sum, column_sum, out_land, tokens_kept, thoughts_kept, block_kept, send, recv,
            local,
        ) = refs
        out = [fc_out, proj_out, mix_out, None]
        at = Place(line)
        tensor, spot, side = at.tensor, at.spot, at.side
        mate_row, far_row, corner_row = at.mate[1], at.far[1], at.corner[1]
        copies = Copies(send, recv)
        loads = {}
        held["out_far"] = out_land
        for k, (name, i, piece) in enumerate(flat):
            if name != "out_far":
                target = held[name]
                if isinstance(arrays[name], tuple):
                    first = 0 if i == 0 else arrays[name][0].shape[0]
                    target = target.at[first : first + piece.shape[0]]
                copy = pltpu.make_async_copy(sources[k], target, local.at[k])
                loads.setdefault(name, Several([])).copies.append(copy)

        def load(*group):
            for name in group:
                loads[name].start()

        load("fc_near", "fc_near_side", "fc_cross", "proj_near", "proj_near_far", "proj_cross")
        load("grad_mixed", "mix")
        greet(at.everyone())

        def block_of(slot):
            distance, way = slots[slot]
            if way == 0:
                return jnp.minimum(spot + distance, far_end), spot + distance < line
            return jnp.maximum(spot - distance, 0), spot - distance >= 0

        crosses, hops = [], []
        for slot in range(len(slots)):
            block, _ = block_of(slot)
            crosses.append(
                {
                    i: copies.plan(cross_send[i].at[block], cross_land[i].at[block], at.across)
                    for i in (MIX, VEC)
                }
            )
            if slot < last:
                hops.append(
                    [
                        copies.plan(
                            hop_send[i].at[slot],
                            hop_land[i].at[slot],
                            (at.up, at.down)[slots[slot][1]],
                        )
                        for i in range(4)
                    ]
                )

        def cross(distance, items):
            for slot in range(len(slots)):
                if slots[slot][0] == distance:
                    for i in items:
                        copies.begin(crosses[slot][i], block_of(slot)[1])

        terms = (
            ("fc_near", "fc_near_side", "fc_cross"),
            ("proj_near", "proj_near_far", "proj_cross"),
        )

        def own_term(i, block):
            if i in (FC, PROJ):
                return sum(held[name][block].astype(F32) for name in terms[i])
            if i == MIX:
                return total[block * 2 + side].astype(F32)
            return vec_near[block * 2 + side]

        def handle(slot, i):
            block, inside = block_of(slot)
            behind = (at.has_down, at.has_up)[slots[slot][1]]
            outer = slot - 2

            def work():
                value = own_term(i, block)
                if i in (MIX, VEC):
                    crosses[slot][i].wait_recv()
                    value = value + cross_land[i][block].astype(F32)
                if outer < 0:
                    hop_send[i][slot] = value.astype(hop_send[i].dtype)
                    return

                @pl.when(behind)
                def _():
                    hops[outer][i].wait_recv()
                    hop_send[i][slot] = (value + hop_land[i][outer].astype(F32)).astype(
                        hop_send[i].dtype
                    )

                @pl.when(jnp.logical_not(behind))
                def _():
                    hop_send[i][slot] = value.astype(hop_send[i].dtype)

            when(inside, work)
            copies.begin(hops[slot][i], inside)

        def handle_all(distance, items):
            for slot in range(last):
                if slots[slot][0] == distance:
                    for i in items:
                        handle(slot, i)

        def close(i, target):
            value = own_term(i, spot)
            if i in (MIX, VEC):
                crosses[last][i].wait_recv()
                value = value + cross_land[i][spot].astype(F32)
            target[...] = value
            for way, behind in enumerate((at.has_down, at.has_up)):

                def add(way=way):
                    hops[last - 2 + way][i].wait_recv()
                    target[...] += hop_land[i][last - 2 + way].astype(F32)

                when(behind, add)

        for name in ("fc_near", "fc_near_side", "fc_cross", "proj_near", "proj_near_far", "proj_cross"):
            loads[name].wait()
        out_made = copies.start(out_source, out_land, at.far)
        handle_all(far_end, (FC, PROJ))
        load("group", "out_own", "vec_all", "vec_part", "bias_own", "bias_far")
        load("last", "hidden", "grad_middle", "middle", "positions")
        loads["grad_mixed"].wait()
        loads["mix"].wait()

        def row_part(index):
            @pl.loop(0, rows // 256)
            def _(i):
                span = pl.ds(pl.multiple_of(i * 256, 256), 256)
                weight = held["mix"][...].reshape(width, width)
                part[index, span] = nt(held["grad_mixed"][index, span], weight).astype(LOW)

        for name in ("group", "out_own", "vec_all", "vec_part", "bias_own", "bias_far"):
            loads[name].wait()

        plain_sum[...] = jnp.zeros_like(plain_sum)
        column_sum[...] = jnp.zeros_like(column_sum)

        @pl.loop(0, group // 256)
        def _(i):
            block, start = i // (rows // 256), (i % (rows // 256)) * 256
            span = pl.ds(pl.multiple_of(start, 256), 256)
            grad = held["grad_mixed"][block, span]
            plain_sum[...] += tn(held["group"][block, span], grad)
            column_sum[...] += jnp.sum(grad.astype(F32), axis=0, keepdims=True)

        row_part(corner_row)
        mate_far = copies.start(part.at[corner_row], mate_land.at[1], at.mate)
        row_part(mate_row)
        mate_own = copies.start(part.at[mate_row], mate_land.at[0], at.mate)
        if far_end > 1:
            handle_all(far_end - 1, (FC, PROJ))
        out_made.wait_recv()
        plain, columns = plain_sum[...], column_sum[...]
        turned = held["vec_all"][...].T
        weight = held["mix"][...].reshape(width, width).astype(F32)
        gain_grad = jnp.sum(plain * weight, axis=1, keepdims=True)
        shift_grad = jnp.sum(weight * columns, axis=1, keepdims=True)
        scaled = plain * turned[:, 0:1] + turned[:, 1:2] * columns
        extras = []
        out_sum = held["out_own"][...].astype(F32) + held["out_far"][...].astype(F32)
        for p in range(3):
            piece = out_sum[p * HD : (p + 1) * HD]
            extras.append(jnp.zeros((width, WIDE - 128), F32))
            extras.append(jnp.concatenate([jnp.zeros((128 - HD, width), F32), piece], axis=0).T)
        scaled = scaled + jnp.concatenate(extras, axis=1)
        for k in range(n_dp):
            total[k] = scaled[k * shard : (k + 1) * shard].astype(LOW)
        for block in range(line):
            cross_send[MIX][block] = total[block * 2 + 1 - side]
        cross(far_end, [MIX])
        cross(far_end - 1, [MIX])
        row_part(far_row)
        mate_far.wait_recv()
        far_made = []

        def send_far(count):
            for i in range(len(far_made), min(len(far_made) + count, 8)):
                span = pl.ds(i * (part_rows // 2), part_rows // 2)
                far_send[span] = (
                    mate_land[1, span].astype(F32) + part[far_row, span].astype(F32)
                ).astype(LOW)
                far_made.append(copies.start(far_send.at[span], far_land.at[span], at.far))

        send_far(2)
        row_part(tensor)
        send_far(1)
        loads["last"].wait()
        last_copy = copies.start(held["last"].at[1], last_land, at.mate)
        vec_mine[...] = held["vec_part"][...]
        norm_grads = jnp.concatenate(
            [gain_grad, shift_grad, jnp.zeros((width, 6), F32)], axis=1
        ).T
        vec_mine[0:2] = norm_grads[0:2]
        vec_mine[8:12] = units_rows_back(held["bias_own"][...], tensor, n_dp) + units_rows_back(
            held["bias_far"][...], far_row, n_dp
        )
        vec_lane = lax.broadcasted_iota(jnp.int32, (1, width), 1)
        in_part = (vec_lane >= tensor * (NH * HD)) & (vec_lane < (tensor + 1) * (NH * HD))
        for row, low in ((2, 0), (3, 2 * WIDE)):
            line_up = jnp.concatenate([columns[:, low : low + WIDE]] + [columns[:, 0:WIDE]] * 2, axis=1)
            placed = jnp.zeros((1, width), F32)
            for t in range(4):
                shifted = pltpu.roll(line_up, t * NH * HD, 1)
                placed = jnp.where(tensor == t, shifted, placed)
            vec_mine[row : row + 1] = jnp.where(in_part, placed, 0.0)
        vec_made = [
            copies.start(vec_mine, vec_land.at[i], device)
            for i, device in enumerate((at.mate, at.far, at.corner))
        ]
        handle_all(far_end, [MIX])
        if far_end >= 2:
            cross(far_end - 2, [MIX])
        send_far(2)
        for distance in range(far_end - 2, 0, -1):
            handle_all(distance, (FC, PROJ))
        send_far(1)
        for copy in vec_made:
            copy.wait_recv()
        send_far(1)
        vec_sum = vec_mine[...] + vec_land[0] + vec_land[1] + vec_land[2]
        for k in range(n_dp):
            vec_near[k] = pltpu.roll(vec_sum, (width - k * shard) % width, 1)[:, 0:128]
        for block in range(line):
            cross_send[VEC][block] = vec_near[block * 2 + 1 - side]
        cross(far_end, [VEC])
        cross(far_end - 1, [VEC])
        send_far(8)
        live = ends_of(lengths_ref)[-1]
        stays = []

        def close_rows(i):
            if i == 0:
                for name in ("hidden", "grad_middle", "middle", "positions"):
                    loads[name].wait()
                last_copy.wait_recv()
                mate_own.wait_recv()
            far_made[2 * i].wait_recv()
            far_made[2 * i + 1].wait_recv()
            span = pl.ds(i * part_rows, part_rows)
            ids = tensor * rows + i * part_rows + lax.broadcasted_iota(
                jnp.int32, (part_rows, 1), 0
            )
            final = (
                held["middle"][span]
                + held["last"][0, span].astype(F32)
                + last_land[span].astype(F32)
                + held["vec_all"][7:8]
            )
            block_kept[span] = jnp.where(ids < live, final, 0.0).astype(LOW)
            grad = (
                part[tensor, span].astype(F32)
                + mate_land[0, span].astype(F32)
                + far_land[span].astype(F32)
            )
            normed, inverse = normalize(held["hidden"][span].astype(F32))
            grad = held["grad_middle"][span] + norm_back(
                normed, inverse, grad, held["vec_all"][0:1]
            )
            for w in range(part_rows // window):
                index = i * (part_rows // window) + w
                here = (
                    lax.broadcasted_iota(jnp.int32, (window, 1), 0)
                    == held["positions"][index : index + 1, 0:1] - index * window
                )
                piece = grad[w * window : (w + 1) * window]
                tokens_kept[pl.ds(index * window, window)] = jnp.where(here, 0.0, piece)
                thoughts_kept[index : index + 1] = jnp.sum(
                    jnp.where(here, piece, 0.0), axis=0, keepdims=True
                )
            moves = [(tokens_kept.at[span], tokens_out.at[span])]
            moves.append((block_kept.at[span], block_out.at[span]))
            if i == 3:
                moves.append((thoughts_kept, thoughts_out))
            for kept_ref, out_ref in moves:
                stays.append(
                    pltpu.make_async_copy(kept_ref, out_ref, local.at[len(flat) + len(stays)])
                )
                stays[-1].start()

        done = 0
        for distance in range(far_end, 0, -1):
            items = (MIX, VEC) if distance < far_end else (VEC,)
            handle_all(distance, items)
            if distance >= 2:
                cross(distance - 2, items)
            if distance <= 3:
                close_rows(done)
                done += 1
        for i in range(done, 4):
            close_rows(i)
        for i in (FC, PROJ, MIX):
            close(i, out[i])
        close(VEC, vec_out)
        copies.finish()
        for copy in stays:
            copy.wait()

    f32 = lambda *shape: jax.ShapeDtypeStruct(shape, F32)
    outputs = (
        f32(shard, width), f32(shard, width), f32(shard, width), f32(VEC_ROWS, 128),
        f32(rows, width), f32(latents, width), jax.ShapeDtypeStruct((rows, width), LOW),
    )
    scratch = [pltpu.VMEM(*shapes[name]) for name in kept]
    for number, wide in ((line, 1), (line, 1), (last, 3), (last, 3)):
        scratch += [pltpu.VMEM((number, shard, width), LOW)] * wide
        scratch.append(pltpu.VMEM((number, VEC_ROWS, 128), F32))
    scratch += [
        pltpu.VMEM((4, rows, width), LOW),
        pltpu.VMEM((2, rows, width), LOW),
        pltpu.VMEM((rows, width), LOW),
        pltpu.VMEM((rows, width), LOW),
        pltpu.VMEM((rows, width), LOW),
        pltpu.VMEM((n_dp, shard, width), LOW),
        pltpu.VMEM((VEC_ROWS, width), F32),
        pltpu.VMEM((3, VEC_ROWS, width), F32),
        pltpu.VMEM((n_dp, VEC_ROWS, 128), F32),
        pltpu.VMEM((width, width), F32),
        pltpu.VMEM((1, width), F32),
        pltpu.VMEM(arrays["out_far"].shape, LOW),
        pltpu.VMEM((rows, width), F32),
        pltpu.VMEM((latents, width), F32),
        pltpu.VMEM((rows, width), LOW),
    ]
    return comm_call(
        kernel,
        "finish_grads",
        outputs,
        (lengths, *(piece for _, _, piece in flat)),
        [SM] + [ANY] * len(flat),
        (VM,) * 4 + (ANY,) * 3,
        (last + 1) * 2 + last * 4 + 1 + 2 + 8 + 3 + 1,
        cid,
        scratch=scratch,
        local=len(flat) + 9,
    )


def unit_kernel(add, line, bias_row, lengths_ref, *refs):
    refs = list(refs)
    rows_ref, grad_own, grad_mate = refs[:3]
    pieces, vec_ref = refs[3:7], refs[7]
    refs = refs[8:]
    if add:
        last_in, two_in = refs[:2]
        refs = refs[2:]
    last_ref, two_ref, fc_near, fc_side, proj_one, proj_two, proj_side, bias_grad_ref = refs[:8]
    fc_all, proj_all, fc_sum, proj_sum = refs[8:]
    step = pl.program_id(0)
    side, tensor = lax.axis_index("dp") % 2, lax.axis_index("tensor")
    live = ends_of(lengths_ref)[-1]

    @pl.when(step == 0)
    def _():
        for full, near, across in ((fc_all, *pieces[:2]), (proj_all, *pieces[2:])):
            for i in range(line):
                full[2 * i + side] = near[i]
                full[2 * i + 1 - side] = across[i]
        fc_sum[...] = jnp.zeros_like(fc_sum)
        proj_sum[...] = jnp.zeros_like(proj_sum)
        bias_grad_ref[...] = jnp.zeros_like(bias_grad_ref)

    count, width = rows_ref.shape
    half = pl.num_programs(0) // 2
    block = jnp.where(step < half, tensor, tensor + 1 - 2 * (tensor % 2))
    first = block * (half * count) + (step % half) * count
    alive = first + lax.broadcasted_iota(jnp.int32, (count, 1), 0) < live
    rows = rows_ref[...]
    grad = jnp.where(step < half, grad_own[...], grad_mate[...])
    grad = jnp.where(alive, grad, jnp.zeros_like(grad))
    fc = fc_all[...].reshape(width, -1)
    proj = proj_all[...].reshape(width, -1)
    inner = nn(rows, fc) + vec_ref[bias_row : bias_row + 1]
    square = inner * inner
    bend = jnp.tanh(GELU_SCALE * inner * (1.0 + GELU_CUBE * square))
    half = 0.5 * (1.0 + bend)
    activated = (inner * half).astype(LOW)
    slope = half + 0.5 * inner * (1.0 - bend * bend) * GELU_SCALE * (1.0 + 3.0 * GELU_CUBE * square)
    grad_inner = (nn(grad, proj) * slope).astype(LOW)
    last = nt(activated, proj)
    two = nt(grad_inner, fc)
    if add:
        last, two = last + last_in[...], two + two_in[...]
    last_ref[...] = last.astype(last_ref.dtype)
    two_ref[...] = two.astype(two_ref.dtype)
    fc_sum[...] += tn(rows, grad_inner)
    proj_sum[...] += tn(grad, activated)
    bias_grad_ref[...] += jnp.sum(grad_inner.astype(F32), axis=0, keepdims=True)

    @pl.when(step == pl.num_programs(0) - 1)
    def _():
        shard = fc_near.shape[1]
        split = line // 2
        near_seats = (
            [fc_near.at[i] for i in range(line)],
            [proj_one.at[i] for i in range(split)] + [proj_two.at[i] for i in range(line - split)],
        )
        for sums, near, across in (
            (fc_sum, near_seats[0], fc_side), (proj_sum, near_seats[1], proj_side),
        ):
            for i in range(line):
                even = sums[2 * i * shard : (2 * i + 1) * shard].astype(LOW)
                odd = sums[(2 * i + 1) * shard : (2 * i + 2) * shard].astype(LOW)
                near[i][...] = jnp.where(side == 0, even, odd)
                across[i] = jnp.where(side == 0, odd, even)


def units_both_ways(lengths, rows, grad, mate_grad, pieces, vec_all, bias_row, before):
    count, width = rows.shape
    line, shard, units = pieces[0].shape
    half = count // ROW_TILE // 2
    leads = (line, line, line // 2, line - line // 2, line)
    tile = pl.BlockSpec((ROW_TILE, width), lambda i: (i, 0))
    fixed = lambda shape: pl.BlockSpec(shape, lambda i: (0,) * len(shape))
    add = before is not None
    kind = LOW if add else F32
    return pl.pallas_call(
        functools.partial(unit_kernel, add, line, bias_row),
        grid=(count // ROW_TILE,),
        out_shape=(
            jax.ShapeDtypeStruct((count, width), kind),
            jax.ShapeDtypeStruct((count, width), kind),
        )
        + tuple(jax.ShapeDtypeStruct((k, shard, units), LOW) for k in leads)
        + (jax.ShapeDtypeStruct((1, units), F32),        ),
        in_specs=[
            SM,
            tile,
            pl.BlockSpec((ROW_TILE, width), lambda i: (jnp.minimum(i, half - 1), 0)),
            pl.BlockSpec((ROW_TILE, width), lambda i: (jnp.maximum(i - half, 0), 0)),
        ]
        + [fixed((line, shard, units))] * 4
        + [fixed(vec_all.shape)]
        + [tile] * (2 if add else 0),
        out_specs=(tile, tile)
        + tuple(fixed((k, shard, units)) for k in leads)
        + (fixed((1, units)),),
        scratch_shapes=[pltpu.VMEM((2 * line, shard, units), LOW)] * 2
        + [pltpu.VMEM((width, units), F32)] * 2,
        compiler_params=pltpu.CompilerParams(
            dimension_semantics=("arbitrary",), vmem_limit_bytes=VMEM_LIMIT
        ),
        cost_estimate=pl.CostEstimate(
            flops=12 * count * width * units,
            bytes_accessed=24 * count * width,
            transcendentals=count * units,
        ),
        name="units_second" if add else "units_first",
    )(lengths, rows, grad, mate_grad, *pieces, vec_all, *(before or ()))


def split_grads(mix_grad, vec, through, share):
    shard, width = mix_grad.shape
    head_width = NH * HD
    count = len(through)
    pieces_of = []
    for i, array in enumerate(through):
        size = 128 if array.shape[0] % 128 == 0 else array.shape[0]
        pieces_of += [(i, row, size) for row in range(0, array.shape[0], size)]

    def kernel(mix_ref, vec_ref, *refs):
        given, (qkv_out, out_out), refs = refs[:count], refs[count : count + 2], refs[count + 2 :]
        small, passed, held, sems = refs[:8], refs[8 : 8 + count], refs[8 + count : -1], refs[-1]
        ins, outs = [], []
        for i, row, size in pieces_of:
            span = pl.ds(row, size)
            ins.append(
                pltpu.make_async_copy(
                    given[i].at[span], held[i].at[span], sems.at[0, len(ins)]
                )
            )
            outs.append(
                pltpu.make_async_copy(
                    held[i].at[span], passed[i].at[span], sems.at[1, len(outs)]
                )
            )
        for copy in ins:
            copy.start()
        for i in range(len(ins)):
            ins[i].wait()
            outs[i].start()
        tensor = lax.axis_index("tensor")
        turned = mix_ref[...].T
        pieces = []
        for h in range(NH):
            for part in range(3):
                low = part * WIDE + h * HD
                pieces.append(turned[low : low + HD])
        qkv_out[...] = jnp.concatenate(pieces, axis=0).T
        for part in range(3):
            low = part * WIDE + head_width
            out_out[part * HD : (part + 1) * HD] = turned[low : low + HD]
        rows = vec_ref[0:8]
        moved = rows
        for i in range(1, 4):
            moved = jnp.where(tensor == i, pltpu.roll(rows, 128 - i * share, 1), moved)
        for i, row in enumerate((0, 1, 4, 5, 6, 7)):
            small[i][...] = moved[row : row + 1, 0:share]
        small[6][...] = moved[2:4, 0:share]
        small[7][...] = vec_ref[pl.ds(8 + tensor, 1)][:, 0:shard]
        for copy in outs:
            copy.wait()

    f32 = lambda *shape: jax.ShapeDtypeStruct(shape, F32)
    return pl.pallas_call(
        kernel,
        out_shape=(f32(shard, 3 * head_width), f32(head_width, shard))
        + (f32(1, share),) * 6
        + (f32(2, share), f32(1, shard))
        + tuple(jax.ShapeDtypeStruct(x.shape, x.dtype) for x in through),
        in_specs=[VM] * 2 + [ANY] * count,
        out_specs=(VM,) * 10 + (ANY,) * count,
        scratch_shapes=[pltpu.VMEM(x.shape, x.dtype) for x in through]
        + [pltpu.SemaphoreType.DMA((2, len(pieces_of)))],
        compiler_params=pltpu.CompilerParams(vmem_limit_bytes=VMEM_LIMIT),
        name="split_grads",
    )(mix_grad, vec, *through)


def by_tensor(row, step, index):
    moved = row
    for i in range(1, 4):
        moved = jnp.where(index == i, pltpu.roll(row, (i * step) % row.shape[1], 1), moved)
    return moved


def units_row(rows, block, n_dp):
    width = rows.shape[1]
    shard, step = width // n_dp, n_dp // 4
    lane = lax.broadcasted_iota(jnp.int32, (1, width), 1) // shard
    base = by_tensor(rows, width - step * shard, block)
    total = jnp.zeros((1, width), F32)
    for j in range(n_dp):
        moved = pltpu.roll(base[j % 4 : j % 4 + 1], (j - j // 4) * shard, 1)
        total = jnp.where(lane == j, moved, total)
    return total


def units_rows_back(row, block, n_dp):
    width = row.shape[1]
    shard, step = width // n_dp, n_dp // 4
    lane = lax.broadcasted_iota(jnp.int32, (1, width), 1) // shard
    rows = [jnp.zeros((1, width), F32) for _ in range(4)]
    for j in range(n_dp):
        moved = pltpu.roll(row, (width - (j - j // 4) * shard) % width, 1)
        rows[j % 4] = jnp.where(lane == j // 4, moved, rows[j % 4])
    return by_tensor(jnp.concatenate(rows, axis=0), step * shard, block)


def normalize(values):
    center = jnp.mean(values, axis=-1, keepdims=True)
    offset = values - center
    spread = jnp.mean(offset * offset, axis=-1, keepdims=True)
    inverse = lax.rsqrt(spread + EPSILON)
    return offset * inverse, inverse


def norm_back(normed, inverse, grad, gain):
    scaled = grad * gain
    center = jnp.mean(scaled, axis=-1, keepdims=True)
    along = jnp.mean(scaled * normed, axis=-1, keepdims=True)
    return inverse * (scaled - center - normed * along)


def product(equation, left, right):
    return jnp.einsum(equation, left, right, preferred_element_type=F32)


def per_device(
    tokens,
    thoughts,
    positions,
    lengths,
    attn_norm_gain,
    attn_norm_shift,
    qkv_weight,
    qv_bias,
    attn_out_weight,
    attn_out_bias,
    mlp_norm_gain,
    mlp_norm_shift,
    fc_weight,
    fc_bias,
    proj_weight,
    proj_bias,
    cotangent,
):
    n_dp = lax.axis_size("dp")
    n_tensor = lax.axis_size("tensor")
    rows, width = tokens.shape
    slots = rows * n_tensor
    swap_far = [(i, (i + 2) % n_tensor) for i in range(n_tensor)]

    share = width // (n_dp * n_tensor)
    small = [
        attn_norm_gain[None], attn_norm_shift[None], qv_bias, attn_out_bias[None],
        mlp_norm_gain[None], mlp_norm_shift[None], proj_bias[None], fc_bias[None],
    ]
    (
        group_low, mixed, mix_all, fc_near, fc_side, fc_far_near, proj_near, mate_grad, out_own,
        hidden, vec_all, places,
    ) = gather_inputs(
        tokens, thoughts, positions, cotangent, fc_weight, proj_weight.T, qkv_weight,
        attn_out_weight, small, n_dp,
    )
    mixed = mixed.reshape(slots, -1)
    swap_side = [(i, i + 1 - 2 * (i % 2)) for i in range(n_dp)]
    out_far = lax.ppermute(out_own, "tensor", swap_far)
    proj_far_near = lax.ppermute(proj_near, "tensor", swap_far)
    fc_far_side = lax.ppermute(fc_far_near, "dp", swap_side)
    attended, stats = attend(lengths, mixed)
    sent, out_far, proj_far_near, fc_far_side = lax.optimization_barrier(
        (attended, out_far, proj_far_near, fc_far_side)
    )
    proj_far_side = lax.ppermute(proj_far_near, "dp", swap_side)
    both, middle, chip_two = after_attention(
        sent, out_own, out_far, hidden, vec_all, n_dp, 1
    )
    chip_two, proj_far_side, proj_sent = lax.optimization_barrier(
        (chip_two, proj_far_side, proj_near)
    )
    proj_side = lax.ppermute(proj_sent, "dp", swap_side)
    chip_two = chip_two.reshape(2 * rows, width)

    first = units_both_ways(
        lengths, chip_two, cotangent, mate_grad,
        (fc_far_near, fc_far_side, proj_far_near, proj_far_side), vec_all, 13, None,
    )
    far_fc_near, far_fc_side, far_proj_one, far_proj_two, far_proj_side, far_fc_bias = first[2:]
    proj_side_far = lax.ppermute(far_proj_side, "tensor", swap_far)
    fc_far_side_in = lax.ppermute(far_fc_side, "dp", swap_side)
    second = units_both_ways(
        lengths, chip_two, cotangent, mate_grad, (fc_near, fc_side, proj_near, proj_side), vec_all, 12,
        first[:2],
    )
    last_part, grad_two_part, fc_near_grad, fc_side_grad, proj_one, proj_two, proj_side_grad = second[:7]
    far_proj_one, grad_two_part = lax.optimization_barrier((far_proj_one, grad_two_part))
    proj_one_far = lax.ppermute(far_proj_one, "tensor", swap_far)
    fc_near_side_in = lax.ppermute(fc_side_grad, "dp", swap_side)
    grad_heads, grad_middle, grad_out, far_out, vec_part, fc_cross, proj_cross = before_attention_back(
        lengths, grad_two_part.reshape(2, rows, width), middle, cotangent, both, out_own, out_far,
        vec_all, (far_fc_near, fc_far_side_in, proj_side_grad, proj_side_far), n_dp, 2,
    )
    grad_heads, fc_cross, proj_cross, far_proj_two, proj_one_far = lax.optimization_barrier(
        (grad_heads, fc_cross, proj_cross, far_proj_two, proj_one_far)
    )
    fc_cross = lax.ppermute(fc_cross, "tensor", swap_far)
    proj_cross = lax.ppermute(proj_cross, "dp", swap_side)
    proj_two_far = lax.ppermute(far_proj_two, "tensor", swap_far)
    last_low = last_part.reshape(2, rows, width)

    grad_mixed = attend_back(lengths, mixed, attended, stats, grad_heads)
    arrays = {
        "fc_near": fc_near_grad, "fc_near_side": fc_near_side_in, "fc_cross": fc_cross,
        "proj_near": (proj_one, proj_two), "proj_near_far": (proj_one_far, proj_two_far),
        "proj_cross": proj_cross,
        "grad_mixed": grad_mixed.reshape(n_tensor, rows, width), "mix": mix_all,
        "last": last_low, "group": group_low,
        "out_own": grad_out, "out_far": far_out,
        "vec_all": vec_all, "vec_part": vec_part, "bias_own": second[7], "bias_far": far_fc_bias,
        "hidden": hidden, "grad_middle": grad_middle, "middle": middle, "positions": places,
    }
    fc_grad, proj_grad, mix_grad, vec, grad_tokens, grad_thoughts, block_out = finish_grads(
        lengths, arrays, n_dp, 8
    )
    parts = split_grads(
        mix_grad, vec, (fc_grad, proj_grad, grad_tokens, grad_thoughts, block_out), share
    )
    qkv_grad, out_grad = parts[:2]
    gain_one, shift_one, out_bias, gain_two, shift_two, last_bias = [p[0] for p in parts[2:8]]
    query_value, hidden_bias = parts[8], parts[9][0]
    fc_grad, proj_grad, grad_tokens, grad_thoughts, block_out = parts[10:]
    return (
        block_out,
        grad_tokens,
        grad_thoughts,
        gain_one,
        shift_one,
        qkv_grad,
        query_value,
        out_grad,
        out_bias,
        gain_two,
        shift_two,
        fc_grad,
        hidden_bias,
        proj_grad.T,
        last_bias,
    )


def solution(mesh):
    rows = P(("dp", "tensor"), None)
    line = P(("dp", "tensor"))
    in_specs = (
        rows, rows, line, P("dp", None), line, line, P("dp", "tensor"),
        P(None, ("dp", "tensor")), P("tensor", "dp"), line, line, line,
        P("dp", "tensor"), line, P("tensor", "dp"), line, rows,
    )
    out_specs = (
        rows, rows, rows, line, line, P("dp", "tensor"), P(None, ("dp", "tensor")),
        P("tensor", "dp"), line, line, line, P("dp", "tensor"), line, P("tensor", "dp"), line,
    )
    return jax.shard_map(
        per_device, mesh=mesh, in_specs=in_specs, out_specs=out_specs, check_vma=False
    )
```

```python
import functools
import math

import jax
import jax.numpy as jnp
from jax import lax
from jax.experimental import pallas as pl
from jax.experimental.pallas import tpu as pltpu
from jax.sharding import PartitionSpec as P

H = 12
HD = 64
FF = 3072
SEQ_DEV = 3
EPSILON = 1e-05
MASKED = -1e30
NH = 3
SLABS = 2
WIDE = SLABS * 128
BQ = 512
BK = 512
SUMMED = HD + 16
VEC_ROWS = 16
VMEM_LIMIT = 67043328
ROW_TILE = 256
GELU_SCALE = math.sqrt(2.0 / math.pi)
GELU_CUBE = 0.044715
MESH = pl.DeviceIdType.MESH
ANY = pl.BlockSpec(memory_space=pltpu.HBM)
VM = pl.BlockSpec(memory_space=pltpu.VMEM)
SM = pl.BlockSpec(memory_space=pltpu.SMEM)
LOW = jnp.bfloat16
F32 = jnp.float32


def nn(a, b):
    return lax.dot_general(a, b, (((1,), (0,)), ((), ())), preferred_element_type=jnp.float32)


def nt(a, b):
    return lax.dot_general(a, b, (((1,), (1,)), ((), ())), preferred_element_type=jnp.float32)


def tn(a, b):
    return lax.dot_general(a, b, (((0,), (0,)), ((), ())), preferred_element_type=jnp.float32)


def head_rows(slab, head):
    half = slab[(head % 2) * HD : (head % 2 + 1) * HD]
    zero = jnp.zeros_like(half)
    return jnp.concatenate([half, zero] if head % 2 == 0 else [zero, half], axis=0)


def ends_of(lengths_ref):
    ends = [lengths_ref[0, 0]]
    for i in range(1, SEQ_DEV):
        ends.append(ends[-1] + lengths_ref[0, i])
    return ends


def segment_start(ends, slots):
    start = jnp.zeros_like(slots)
    for i in range(SEQ_DEV):
        start = jnp.where(slots >= ends[i], ends[i], start)
    return start


def segment_stop(ends, slot, slots):
    stop = slots
    for i in reversed(range(SEQ_DEV)):
        stop = jnp.where(slot < ends[i], ends[i], stop)
    return stop


def attend_kernel(
    lengths_ref, mixed_in, out_ref, stat_ref, mixed_ref, qt_ref, vt_ref, sems
):
    tokens = mixed_ref.shape[0]
    ends = ends_of(lengths_ref)
    count = (ends[-1] + BQ - 1) // BQ
    half = BQ // 2

    def load(block):
        rows = pl.ds(pl.multiple_of(block * BQ, BQ), BQ)
        return pltpu.make_async_copy(mixed_in.at[rows], mixed_ref.at[rows], sems.at[block])

    for block in range(tokens // BQ):
        load(block).start()
    for h in range(NH):
        vt_ref[h * SUMMED + HD : (h + 1) * SUMMED] = jnp.ones((SUMMED - HD, tokens), jnp.bfloat16)

    def step(rows, keys, columns, queries, first, causal, state):
        size = queries[0].shape[1]
        slots = first + lax.broadcasted_iota(jnp.int32, (1, size), 1)
        start = segment_start(ends, slots)
        key_ids = rows + lax.broadcasted_iota(jnp.int32, (keys, size), 0)
        allowed = key_ids >= start
        if causal:
            allowed = allowed & (key_ids <= slots)
        span = pl.ds(rows, keys)
        result = []
        for h in range(NH):
            peak, acc = state[h]
            low = WIDE + (h // 2) * 128
            scores = nn(mixed_ref[span, low : low + 128], queries[h])
            scores = jnp.where(allowed, scores, MASKED)
            fresh = jnp.maximum(peak, jnp.max(scores, axis=0, keepdims=True))
            weight = jnp.exp(scores - fresh)
            decay = jnp.exp(peak - fresh)
            values = vt_ref[h * SUMMED : (h + 1) * SUMMED, span]
            acc = acc * decay + nn(values, weight.astype(jnp.bfloat16))
            result.append((fresh, acc))
        return tuple(result)

    def query_block(block, carry):
        first = pl.multiple_of(block * BQ, BQ)
        columns = pl.ds(first, BQ)
        load(block).wait()
        for slab in range(SLABS):
            low = slab * 128
            qt_ref[low : low + 128] = (mixed_ref[columns, low : low + 128] * HD ** (-0.5)).T
            turned = mixed_ref[columns, 2 * WIDE + low : 2 * WIDE + low + 128].T
            for h in range(2 * slab, min(2 * slab + 2, NH)):
                piece = turned[(h % 2) * HD : (h % 2 + 1) * HD]
                vt_ref[h * SUMMED : h * SUMMED + HD, columns] = piece
        queries = [head_rows(qt_ref[(h // 2) * 128 : (h // 2 + 1) * 128], h) for h in range(NH)]

        def key_block(key, state):
            return step(pl.multiple_of(key * BK, BK), BK, columns, queries, first, False, state)

        empty = tuple(
            (
                jnp.full((1, BQ), MASKED, jnp.float32),
                jnp.zeros((SUMMED, BQ), jnp.float32),
            )
            for _ in range(NH)
        )
        state = lax.fori_loop(segment_start(ends, first) // BK, block, key_block, empty)
        for side, keys in ((0, half), (1, BQ)):
            piece = slice(side * half, (side + 1) * half)
            final = step(
                first, keys, columns, [q[:, piece] for q in queries], first + side * half, True,
                tuple(tuple(x[:, piece] for x in one) for one in state),
            )
            for h in range(NH):
                peak, acc = final[h]
                total = acc[HD : HD + 1]
                place_here = pl.ds(pl.multiple_of(first + side * half, half), half)
                out_ref[h * HD : (h + 1) * HD, place_here] = (acc[:HD] / total).astype(
                    jnp.bfloat16
                )
                stat_ref[h : h + 1, place_here] = peak + jnp.log(total)
        return carry

    lax.fori_loop(0, count, query_block, 0)

    def padded_block(block, carry):
        load(block).wait()
        columns = pl.ds(pl.multiple_of(block * BQ, BQ), BQ)
        out_ref[:, columns] = jnp.zeros((out_ref.shape[0], BQ), jnp.bfloat16)
        return carry

    lax.fori_loop(count, tokens // BQ, padded_block, 0)


def attend(lengths, mixed):
    tokens = mixed.shape[0]
    vm = pl.BlockSpec(memory_space=pltpu.VMEM)
    return pl.pallas_call(
        attend_kernel,
        out_shape=(
            jax.ShapeDtypeStruct((NH * HD, tokens), jnp.bfloat16),
            jax.ShapeDtypeStruct((8, tokens), jnp.float32),
        ),
        in_specs=[pl.BlockSpec(memory_space=pltpu.SMEM), pl.BlockSpec(memory_space=pltpu.HBM)],
        out_specs=(vm, vm),
        scratch_shapes=[
            pltpu.VMEM(mixed.shape, mixed.dtype),
            pltpu.VMEM((WIDE, BQ), jnp.bfloat16),
            pltpu.VMEM((NH * SUMMED, tokens), jnp.bfloat16),
            pltpu.SemaphoreType.DMA((tokens // BQ,)),
        ],
        compiler_params=pltpu.CompilerParams(vmem_limit_bytes=VMEM_LIMIT),
        cost_estimate=pl.CostEstimate(
            flops=8 * tokens * tokens * NH * HD,
            bytes_accessed=16 * tokens * WIDE,
            transcendentals=tokens * tokens,
        ),
        name="attend",
    )(lengths, mixed)


def attend_back_kernel(
    lengths_ref, mixed_in, out_in, stat_ref, gradt_in,
    gmixed_out, mixed_ref, out_ref, gradt_ref, gmixed_ref, qt_ref, kt_ref, grad_ref, delta_ref,
    dqt_ref, sems, out_sems
):
    tokens = mixed_ref.shape[0]
    blocks = tokens // BQ
    ends = ends_of(lengths_ref)
    count = (ends[-1] + BK - 1) // BK
    half = BQ // 2

    def loads(block):
        rows = pl.ds(pl.multiple_of(block * BQ, BQ), BQ)
        return (
            pltpu.make_async_copy(mixed_in.at[rows], mixed_ref.at[rows], sems.at[0, block]),
            pltpu.make_async_copy(out_in.at[:, rows], out_ref.at[:, rows], sems.at[1, block]),
            pltpu.make_async_copy(gradt_in.at[:, rows], gradt_ref.at[:, rows], sems.at[2, block]),
        )

    def leave(block, part):
        rows = pl.ds(pl.multiple_of(block * BQ, BQ), BQ)
        lanes = pl.ds(0, WIDE) if part == 0 else pl.ds(WIDE, 2 * WIDE)
        return pltpu.make_async_copy(
            gmixed_ref.at[rows, lanes], gmixed_out.at[rows, lanes], out_sems.at[part, block]
        )

    for block in reversed(range(blocks)):
        for copy in loads(block):
            copy.start()
    dqt_ref[...] = jnp.zeros_like(dqt_ref)

    def prepare_block(block):
        rows = pl.ds(pl.multiple_of(block * BQ, BQ), BQ)
        for slab in range(SLABS):
            low = slab * 128
            qt_ref[low : low + 128, rows] = (
                mixed_ref[rows, low : low + 128] * HD ** (-0.5)
            ).T
            kt_ref[low : low + 128, rows] = mixed_ref[rows, WIDE + low : WIDE + low + 128].T
        grad_ref[rows, 0:128] = gradt_ref[0:128, rows].T
        grad_ref[rows, 128:256] = jnp.concatenate(
            [gradt_ref[128:192, rows], jnp.zeros((64, BQ), jnp.bfloat16)], axis=0
        ).T
        for h in range(NH):
            product = gradt_ref[h * HD : (h + 1) * HD, rows].astype(jnp.float32) * out_ref[
                h * HD : (h + 1) * HD, rows
            ].astype(jnp.float32)
            delta_ref[h : h + 1, rows] = jnp.sum(product, axis=0, keepdims=True)

    def terms(base, keys, first, size, causal):
        rows, columns = pl.ds(base, keys), pl.ds(first, size)
        slots = first + lax.broadcasted_iota(jnp.int32, (1, size), 1)
        key_ids = base + lax.broadcasted_iota(jnp.int32, (keys, size), 0)
        allowed = key_ids >= segment_start(ends, slots)
        if causal:
            allowed = allowed & (key_ids <= slots)
        lane = lax.broadcasted_iota(jnp.int32, (size, 128), 1)
        grad_keys, grad_values = [None] * SLABS, [None] * SLABS
        for h in range(NH):
            slab = h // 2
            low, high = slab * 128, slab * 128 + 128
            queries = head_rows(qt_ref[low:high, columns], h)
            scores = nn(mixed_ref[rows, WIDE + low : WIDE + high], queries)
            probs = jnp.where(allowed, jnp.exp(scores - stat_ref[h : h + 1, columns]), 0.0)
            keep = (lane // HD) == (h % 2)
            value = nn(probs.astype(jnp.bfloat16), jnp.where(keep, grad_ref[columns, low:high], 0.0))
            if h == NH - 1 and NH % 2 == 1:
                grad_rows = jnp.concatenate(
                    [gradt_ref[h * HD : (h + 1) * HD, columns], jnp.zeros((HD, size), jnp.bfloat16)],
                    axis=0,
                )
            else:
                grad_rows = head_rows(gradt_ref[low:high, columns], h)
            grad_probs = nn(mixed_ref[rows, 2 * WIDE + low : 2 * WIDE + high], grad_rows)
            grad_scores = (probs * (grad_probs - delta_ref[h : h + 1, columns])).astype(
                jnp.bfloat16
            )
            key_term = nn(grad_scores, jnp.where(keep, mixed_ref[columns, low:high], 0.0))
            grad_values[slab] = value if grad_values[slab] is None else grad_values[slab] + value
            grad_keys[slab] = key_term if grad_keys[slab] is None else grad_keys[slab] + key_term
            dqt_ref[h * HD : (h + 1) * HD, columns] += nn(
                kt_ref[h * HD : (h + 1) * HD, rows], grad_scores
            )
        return grad_keys + grad_values

    def key_block(turn, carry):
        key = count - 1 - turn
        for copy in loads(key):
            copy.wait()
        prepare_block(key)
        base = pl.multiple_of(key * BK, BK)
        rows = pl.ds(base, BK)
        upper = terms(base, half, base, BQ, True)
        lower = terms(pl.multiple_of(base + half, half), half, pl.multiple_of(base + half, half), half, True)
        state = tuple(jnp.concatenate([a, b], axis=0) for a, b in zip(upper, lower))

        def query_block(block, state):
            fresh = terms(base, BK, pl.multiple_of(block * BQ, BQ), BQ, False)
            return tuple(a + b for a, b in zip(state, fresh))

        stop = jnp.minimum(segment_stop(ends, base + BK - 1, tokens), ends[-1])
        state = lax.fori_loop(key + 1, (stop - 1) // BQ + 1, query_block, state)
        for slab in range(SLABS):
            low = slab * 128
            gmixed_ref[rows, WIDE + low : WIDE + low + 128] = (
                state[slab] * HD ** (-0.5)
            ).astype(jnp.bfloat16)
            gmixed_ref[rows, 2 * WIDE + low : 2 * WIDE + low + 128] = state[SLABS + slab].astype(
                jnp.bfloat16
            )
        leave(key, 1).start()
        return carry

    def padded_block(key, carry):
        for copy in loads(key):
            copy.wait()
        rows = pl.ds(pl.multiple_of(key * BK, BK), BK)
        gmixed_ref[rows, WIDE:] = jnp.zeros((BK, 2 * WIDE), jnp.bfloat16)
        leave(key, 1).start()
        return carry

    lax.fori_loop(count, blocks, padded_block, 0)
    lax.fori_loop(0, count, key_block, 0)
    for block in range(blocks):
        rows = pl.ds(block * BQ, BQ)
        for slab in range(SLABS):
            low = slab * 128
            gmixed_ref[rows, low : low + 128] = (
                (dqt_ref[low : low + 128, rows] * HD ** (-0.5)).T.astype(jnp.bfloat16)
            )
        leave(block, 0).start()
    for block in range(blocks):
        leave(block, 0).wait()
        leave(block, 1).wait()


def attend_back(lengths, mixed, out, stat, gradt):
    tokens = mixed.shape[0]
    vm = pl.BlockSpec(memory_space=pltpu.VMEM)
    hbm = pl.BlockSpec(memory_space=pltpu.HBM)
    return pl.pallas_call(
        attend_back_kernel,
        out_shape=jax.ShapeDtypeStruct((tokens, 3 * WIDE), jnp.bfloat16),
        in_specs=[pl.BlockSpec(memory_space=pltpu.SMEM), hbm, hbm, vm, hbm],
        out_specs=hbm,
        scratch_shapes=[
            pltpu.VMEM(mixed.shape, jnp.bfloat16),
            pltpu.VMEM(out.shape, jnp.bfloat16),
            pltpu.VMEM(gradt.shape, jnp.bfloat16),
            pltpu.VMEM(mixed.shape, jnp.bfloat16),
            pltpu.VMEM((WIDE, tokens), jnp.bfloat16),
            pltpu.VMEM((WIDE, tokens), jnp.bfloat16),
            pltpu.VMEM((tokens, WIDE), jnp.bfloat16),
            pltpu.VMEM((8, tokens), jnp.float32),
            pltpu.VMEM((WIDE, tokens), jnp.float32),
            pltpu.SemaphoreType.DMA((3, tokens // BQ)),
            pltpu.SemaphoreType.DMA((2, tokens // BQ)),
        ],
        compiler_params=pltpu.CompilerParams(vmem_limit_bytes=VMEM_LIMIT),
        cost_estimate=pl.CostEstimate(
            flops=20 * tokens * tokens * NH * HD,
            bytes_accessed=32 * tokens * WIDE,
            transcendentals=tokens * tokens,
        ),
        name="attend_back",
    )(lengths, mixed, out, stat, gradt)


class Copies:
    def __init__(self, send, recv):
        self.send, self.recv, self.made, self.started = send, recv, 0, []

    def plan(self, source, target, device):
        index = self.made
        self.made += 1
        return pltpu.make_async_remote_copy(
            src_ref=source,
            dst_ref=target,
            send_sem=self.send.at[index],
            recv_sem=self.recv.at[index],
            device_id=device,
            device_id_type=MESH,
        )

    def begin(self, copy, condition=None):
        self.started.append((copy, condition))
        when(condition, copy.start)

    def start(self, source, target, device):
        copy = self.plan(source, target, device)
        self.begin(copy)
        return copy

    def finish(self):
        for copy, condition in self.started:
            when(condition, copy.wait_send)


class Several:
    def __init__(self, copies):
        self.copies = copies

    def start(self):
        for copy in self.copies:
            copy.start()

    def wait(self):
        for copy in self.copies:
            copy.wait()


def when(condition, action):
    if condition is None:
        action()
    else:
        pl.when(condition)(action)


def greet(devices):
    barrier = pltpu.get_barrier_semaphore()
    for device, condition in devices:
        when(
            condition,
            lambda device=device: pl.semaphore_signal(
                barrier, inc=1, device_id=device, device_id_type=MESH
            ),
        )
    present = [1 if condition is None else condition.astype(jnp.int32) for _, condition in devices]
    pl.semaphore_wait(barrier, sum(present))


class Place:
    def __init__(self, line):
        self.dp = dp = lax.axis_index("dp")
        self.tensor = tensor = lax.axis_index("tensor")
        self.spot, self.side = spot, side = dp // 2, dp % 2
        self.chip, self.core = tensor // 2, tensor % 2
        self.has_up, self.has_down = spot + 1 < line, spot > 0
        self.up = (jnp.minimum(spot + 1, line - 1) * 2 + side, tensor)
        self.down = (jnp.maximum(spot - 1, 0) * 2 + side, tensor)
        self.across = (spot * 2 + 1 - side, tensor)
        self.mate = (dp, tensor + 1 - 2 * (tensor % 2))
        self.far = (dp, (tensor + 2) % 4)
        self.corner = (dp, 3 - tensor)

    def everyone(self):
        return [
            (self.mate, None), (self.far, None), (self.corner, None), (self.across, None),
            (self.up, self.has_up), (self.down, self.has_down),
        ]


def comm_call(kernel, name, outputs, inputs, in_specs, out_specs, copies, cid, scratch=(), local=1, limit=VMEM_LIMIT):
    return pl.pallas_call(
        kernel,
        out_shape=outputs,
        in_specs=in_specs,
        out_specs=out_specs,
        scratch_shapes=list(scratch)
        + [
            pltpu.SemaphoreType.DMA((copies,)),
            pltpu.SemaphoreType.DMA((copies,)),
            pltpu.SemaphoreType.DMA((local,)),
        ],
        compiler_params=pltpu.CompilerParams(
            collective_id=cid, has_side_effects=True, vmem_limit_bytes=limit
        ),
        name=name,
    )(*inputs)


def one_hot(rows, columns, shift, limit):
    lane = lax.broadcasted_iota(jnp.int32, (rows, columns), 0)
    spot = lax.broadcasted_iota(jnp.int32, (rows, columns), 1)
    return ((spot == lane + shift) & (lane < limit)).astype(LOW)


def gather_inputs(tokens, thoughts, positions, cotangent, fc, proj, qkv, out, vectors, n_dp):
    line = n_dp // 2
    hops = line - 1
    rows, width = tokens.shape
    latents = thoughts.shape[0]
    window = rows // latents
    shard = fc.shape[0]
    half_rows = rows // 2
    share = width // (n_dp * 4)

    def kernel(
        pos_ref, tokens_in, thoughts_in, cot_ref, fc_in, proj_in, qkv_in, out_in, *refs
    ):
        given = (fc_in, tokens_in, thoughts_in, proj_in, qkv_in, out_in) + refs[: len(vectors)]
        (
            normed_out, mixed_out, mix_out, fc_near, fc_side, fc_far, proj_near, cot_out, out_out,
            hidden_out, vec_out, pos_out,
            hidden_ref, mix_ref, vec_ref, tile,
            land, mix_land, tiles, tile_land, normed, mixed, out_turned,
            *held, arrive, send, recv, local,
        ) = refs[len(vectors) :]
        arrivals = [
            pltpu.make_async_copy(given[i], held[i], arrive.at[i]) for i in range(len(given))
        ]
        for copy in arrivals:
            copy.start()
        fc_ref, tokens_ref, thoughts_ref, proj_ref, qkv_ref, out_ref = held[:6]
        vec_refs = held[6:]
        at = Place(line)
        dp, tensor, spot, side = at.dp, at.tensor, at.spot, at.side
        mate_row, far_row, corner_row = at.mate[1], at.far[1], at.corner[1]
        greet(at.everyone())
        copies = Copies(send, recv)
        MIX, FC, PROJ, VEC = range(4)
        own = [mix_ref, fc_ref, proj_ref, tiles.at[dp]]

        def seat(item, position):
            if item == MIX:
                return mix_land.at[position * 2 + side]
            if item == FC:
                return fc_near.at[position]
            if item == PROJ:
                return proj_near.at[position]
            return tiles.at[position * 2 + side]

        def plan(item, hop):
            above, below = jnp.maximum(spot - hop, 0), jnp.minimum(spot + hop, line - 1)
            came_up = jnp.maximum(spot - 1 - hop, 0)
            came_down = jnp.minimum(spot + 1 + hop, line - 1)
            made = {
                "up": copies.plan(
                    own[item] if hop == 0 else seat(item, above), seat(item, above), at.up
                ),
                "down": copies.plan(
                    own[item] if hop == 0 else seat(item, below), seat(item, below), at.down
                ),
                "onward": [],
            }
            for position in (came_up, came_down):
                onward = []
                if item in (MIX, VEC):
                    onward.append(copies.plan(seat(item, position), seat(item, position), at.across))
                if item == FC:
                    onward.append(copies.plan(fc_near.at[position], fc_side.at[position], at.across))
                    onward.append(copies.plan(fc_near.at[position], fc_far.at[position], at.far))
                made["onward"].append(onward)
            return made

        plans = [[plan(item, hop) for hop in range(hops)] for item in range(4)]

        def launch(item):
            copies.begin(plans[item][0]["up"], at.has_up)
            copies.begin(plans[item][0]["down"], at.has_down)

        def handle(item, hop):
            made = plans[item][hop]
            for way, key, comes, goes in (
                (0, "up", spot - 1 - hop >= 0, at.has_up),
                (1, "down", spot + 1 + hop < line, at.has_down),
            ):
                when(comes, made[key].wait_recv)
                if hop + 1 < hops:
                    copies.begin(plans[item][hop + 1][key], comes & goes)
                for copy in made["onward"][way]:
                    copies.begin(copy, comes)

        def settle(item):
            for hop in range(hops):
                for way, comes in ((0, spot - 1 - hop >= 0), (1, spot + 1 + hop < line)):
                    for copy in plans[item][hop]["onward"][way]:
                        when(comes, copy.wait_recv)

        stays = []

        def stay(source, target):
            copy = pltpu.make_async_copy(source, target, local.at[len(stays)])
            copy.start()
            stays.append(copy)
            return copy

        parts = [pl.ds(0, half_rows), pl.ds(half_rows, half_rows)]
        arrivals[0].wait()
        launch(FC)
        fc_sides = [copies.start(fc_ref, fc_side.at[spot], at.across)]
        cot_made = copies.start(cot_ref, cot_out, at.mate)
        for copy in arrivals[6:]:
            copy.wait()
        tile[...] = jnp.zeros_like(tile)
        row = 0
        for ref in vec_refs:
            count, size = ref.shape
            tile[row : row + count, 0:size] = ref[...].astype(F32)
            row += count
        vec_ref[...] = tile[...].astype(LOW)
        vec_made = [
            copies.start(vec_ref, tile_land.at[i], device)
            for i, device in enumerate((at.mate, at.far, at.corner))
        ]
        arrivals[1].wait()
        arrivals[2].wait()
        pos_row = lax.broadcasted_iota(jnp.int32, (latents, 128), 0)
        places = jnp.zeros((latents, 128), jnp.int32)
        for w in range(latents):
            places = jnp.where(pos_row == w, pos_ref[w], places)
            span = pl.ds(w * window, window)
            here = lax.broadcasted_iota(jnp.int32, (window, 1), 0) == pos_ref[w] - w * window
            hidden_ref[span] = jnp.where(
                here, thoughts_ref[w : w + 1].astype(F32), tokens_ref[span].astype(F32)
            ).astype(LOW)
        pos_out[...] = places
        far_made = [
            copies.start(hidden_ref.at[part], land.at[2, part], at.far) for part in parts
        ]
        mate_made = copies.start(hidden_ref, land.at[1], at.mate)
        fc_sides.append(copies.start(fc_ref, fc_far.at[spot], at.far))
        for copy in arrivals[3:6]:
            copy.wait()
        turned = qkv_ref[...].astype(F32).T
        extra = out_ref[...].astype(F32)
        pieces = []
        for p in range(3):
            for h in range(NH):
                low = (h * 3 + p) * HD
                pieces.append(turned[low : low + HD])
            pieces.append(extra[p * HD : (p + 1) * HD])
        mix_ref[...] = jnp.concatenate(pieces, axis=0).T.astype(LOW)
        launch(MIX)
        mix_side = copies.start(mix_ref, mix_land.at[dp], at.across)
        stay(hidden_ref, hidden_out)
        stay(fc_ref, fc_near.at[spot])
        stay(proj_ref, proj_near.at[spot])
        mix_land[dp] = mix_ref[...]
        for copy in vec_made:
            copy.wait_recv()
        merged = jnp.zeros((VEC_ROWS, 128), F32)
        bias_rows = jnp.zeros((VEC_ROWS, 128), F32)
        row_ids = lax.broadcasted_iota(jnp.int32, (VEC_ROWS, 128), 0)
        for i, index in enumerate((tensor, mate_row, far_row, corner_row)):
            tile = vec_ref[...] if i == 0 else tile_land[i - 1]
            merged += nn(tile, one_hot(128, 128, index * share, share))
            bias_rows = jnp.where(row_ids == 8 + index, tile[8:9].astype(F32), bias_rows)
        tiles[dp] = jnp.where(row_ids < 8, merged, bias_rows).astype(LOW)
        launch(VEC)
        vec_side = copies.start(tiles.at[dp], tiles.at[dp], at.across)

        def norm_rows(source, index):
            @pl.loop(0, rows // 128)
            def _(i):
                span = pl.ds(pl.multiple_of(i * 128, 128), 128)
                normed[index, span] = normalize(source[span].astype(F32))[0].astype(LOW)

            stay(normed.at[index], normed_out.at[index])

        def relay(i):
            far_made[i].wait_recv()
            return copies.start(land.at[2, parts[i]], land.at[3, parts[i]], at.mate)

        def mix_rows(index):
            @pl.loop(0, rows // 256)
            def _(i):
                span = pl.ds(pl.multiple_of(i * 256, 256), 256)
                turned = normed[index, span].astype(F32) * whole[0:1] + whole[1:2]
                weight = mix_land[...].reshape(width, width)
                mixed[index, span] = (nn(turned.astype(LOW), weight) + bias).astype(LOW)

            stay(mixed.at[index], mixed_out.at[index])

        norm_rows(hidden_ref, tensor)
        relayed = []
        for step in range(hops + 2):
            for item, hop in ((MIX, step), (VEC, step), (FC, step - 1), (PROJ, step - 2)):
                if 0 <= hop < hops:
                    handle(item, hop)
            if step == 0:
                launch(PROJ)
                mate_made.wait_recv()
                norm_rows(land.at[1], mate_row)
                relayed.append(relay(0))
            if step == 1:
                relayed.append(relay(1))
                norm_rows(land.at[2], far_row)
            if step == hops:
                mix_side.wait_recv()
                vec_side.wait_recv()
                settle(MIX)
                settle(VEC)
                whole = jnp.zeros((VEC_ROWS, width), F32)
                for i in range(n_dp):
                    whole += nn(tiles[i], one_hot(128, width, i * shard, shard))
                vec_out[...] = whole
                for i, block in enumerate((tensor, far_row)):
                    vec_out[12 + i : 13 + i] = units_row(whole[8:12], block, n_dp)
                lane = lax.broadcasted_iota(jnp.int32, (width, WIDE), 0)
                column = lax.broadcasted_iota(jnp.int32, (width, WIDE), 1)
                pick = (lane == column + tensor * (NH * HD)) & (column < NH * HD)
                picked = nn(whole.astype(LOW), pick.astype(LOW))
                bias = jnp.concatenate(
                    [picked[2:3], jnp.zeros((1, WIDE), F32), picked[3:4]], axis=1
                )
                mix_rows(tensor)
                mix_rows(mate_row)
                mix_rows(far_row)
                for copy in relayed:
                    copy.wait_recv()
                norm_rows(land.at[3], corner_row)
                mix_rows(corner_row)
                stay(mix_land, mix_out)
                weight = mix_land[...].reshape(width, width)
                for part in range(3):
                    low = part * WIDE + WIDE - 128
                    turned = weight[:, low : low + 128].T
                    out_turned[part * HD : (part + 1) * HD] = turned[128 - HD :]
                stay(out_turned, out_out)
        settle(FC)
        for copy in fc_sides:
            copy.wait_recv()
        cot_made.wait_recv()
        copies.finish()
        for copy in stays:
            copy.wait()

    low = lambda *shape: jax.ShapeDtypeStruct(shape, LOW)
    outputs = (
        low(4, rows, width), low(4, rows, width), low(n_dp, shard, width),
        low(line, shard, width), low(line, shard, width), low(line, shard, width),
        low(line, shard, width), low(rows, width), low(NH * HD, width), low(rows, width),
        jax.ShapeDtypeStruct((VEC_ROWS, width), F32),
        jax.ShapeDtypeStruct((latents, 128), jnp.int32),
    )
    scratch = [
        pltpu.VMEM((rows, width), LOW),
        pltpu.VMEM((shard, 3 * WIDE), LOW),
        pltpu.VMEM((VEC_ROWS, 128), LOW),
        pltpu.VMEM((VEC_ROWS, 128), F32),
        pltpu.VMEM((4, rows, width), LOW),
        pltpu.VMEM((n_dp, shard, width), LOW),
        pltpu.VMEM((n_dp, VEC_ROWS, 128), LOW),
        pltpu.VMEM((3, VEC_ROWS, 128), LOW),
        pltpu.VMEM((4, rows, width), LOW),
        pltpu.VMEM((4, rows, width), LOW),
        pltpu.VMEM((NH * HD, width), LOW),
    ]
    given = (fc, tokens, thoughts, proj, qkv, out, *vectors)
    scratch += [pltpu.VMEM(x.shape, x.dtype) for x in given]
    scratch.append(pltpu.SemaphoreType.DMA((len(given),)))
    return comm_call(
        kernel,
        "gather_inputs",
        outputs,
        (positions, tokens, thoughts, cotangent, fc, proj, qkv, out, *vectors),
        [SM] + [ANY] * (7 + len(vectors)),
        (ANY,) * 10 + (VM, VM),
        3 + 2 + 1 + 2 + 2 + 1 + 2 + hops * (2 * 4 + 2 * 4),
        0,
        scratch=scratch,
        local=3 + 8 + 2,
    )


def after_attention(attended, out_own, out_far, hidden, vec_all, n_dp, cid):
    head_width, slots = attended.shape
    rows, width = hidden.shape
    half_rows = rows // 2

    def kernel(
        heads_in, own_in, far_in, hidden_in, vec_ref,
        both_out, middle_out, two_out,
        heads_ref, own_ref, far_ref, hidden_ref,
        land, part, part_low, part_land, two, send, recv, local,
    ):
        loads = [
            pltpu.make_async_copy(source, target, local.at[5 + i])
            for i, (source, target) in enumerate(
                (
                    (heads_in, heads_ref), (own_in, own_ref), (far_in, far_ref),
                    (hidden_in, hidden_ref),
                )
            )
        ]
        for copy in loads:
            copy.start()
        at = Place(n_dp // 2)
        greet([(at.far, None), (at.mate, None)])
        copies = Copies(send, recv)
        cores = (at.core, 1 - at.core)
        made = [None, None]
        for i in (1, 0):
            theirs = pl.multiple_of(((1 - at.chip) * 2 + cores[i]) * rows, rows)
            made[i] = copies.start(heads_in.at[:, pl.ds(theirs, rows)], land.at[i], at.far)
        stays = []

        def stay(source, target):
            stays.append(pltpu.make_async_copy(source, target, local.at[len(stays)]))
            stays[-1].start()

        spans = []
        for copy in loads:
            copy.wait()
        for i in range(2):
            ours = pl.multiple_of((at.chip * 2 + cores[i]) * rows, rows)
            spans.append(pl.ds(ours, rows))
            stay(heads_ref.at[:, spans[i]], both_out.at[0, :, i * rows : (i + 1) * rows])
            part[i] = tn(heads_ref[:, spans[i]], own_ref[...])
        sums = None
        for i in (1, 0):
            made[i].wait_recv()
            stay(land.at[i], both_out.at[1, :, i * rows : (i + 1) * rows])
            part[i] += tn(land[i], far_ref[...])
            if i == 1:
                part_low[...] = part[1].astype(LOW)
                sums = copies.start(part_low, part_land, at.mate)
        sums.wait_recv()
        mated = []
        for piece in range(2):

            @pl.loop(0, half_rows // 128)
            def _(i):
                span = pl.ds(pl.multiple_of(piece * half_rows + i * 128, 128), 128)
                middle = (
                    hidden_ref[span].astype(F32)
                    + part[0, span]
                    + part_land[span].astype(F32)
                    + vec_ref[4:5]
                )
                middle_out[span] = middle
                two[span] = (normalize(middle)[0] * vec_ref[5:6] + vec_ref[6:7]).astype(LOW)

            span = pl.ds(piece * half_rows, half_rows)
            mated.append(copies.start(two.at[span], two_out.at[1, span], at.mate))
        stay(two, two_out.at[0])
        for copy in mated:
            copy.wait_recv()
        copies.finish()
        for copy in stays:
            copy.wait()

    return comm_call(
        kernel,
        "after_attention",
        (
            jax.ShapeDtypeStruct((2, head_width, 2 * rows), LOW),
            jax.ShapeDtypeStruct((rows, width), F32),
            jax.ShapeDtypeStruct((2, rows, width), LOW),
        ),
        (attended, out_own, out_far, hidden, vec_all),
        [ANY] * 4 + [VM],
        (ANY, VM, ANY),
        5,
        cid,
        scratch=[pltpu.VMEM(x.shape, x.dtype) for x in (attended, out_own, out_far, hidden)]
        + [
            pltpu.VMEM((2, head_width, rows), LOW),
            pltpu.VMEM((2, rows, width), F32),
            pltpu.VMEM((rows, width), LOW),
            pltpu.VMEM((rows, width), LOW),
            pltpu.VMEM((rows, width), LOW),
        ],
        local=9,
    )


def before_attention_back(
    lengths, two, middle, cotangent, both, out_own, out_far, vec_all, pairs, n_dp, cid
):
    _, rows, width = two.shape
    head_width = out_own.shape[0]
    half_rows = rows // 2

    def kernel(
        lengths_ref, two_in, middle_in, cot_in, both_in, own_in, far_in, vec_ref,
        one_a, one_b, two_a, two_b,
        heads_out, grad_out, own_out, far_out, vec_out, sum_one, sum_two,
        two_ref, middle_ref, cot_ref, both_ref, own_ref, far_ref,
        two_land, mid, stay_heads, sent_heads, held, send, recv, local,
    ):
        at = Place(n_dp // 2)
        greet([(at.far, None), (at.mate, None)])
        copies = Copies(send, recv)
        halves = [pl.ds(0, half_rows), pl.ds(half_rows, half_rows)]
        loads = [
            pltpu.make_async_copy(ref, held.at[i], local.at[2 + i])
            for i, ref in enumerate((one_a, one_b, two_a, two_b))
        ]
        early = [
            pltpu.make_async_copy(source, target, local.at[6 + i])
            for i, (source, target) in enumerate(
                (
                    (two_in.at[0], two_ref), (middle_in, middle_ref), (cot_in, cot_ref),
                    (far_in, far_ref), (own_in, own_ref), (both_in, both_ref),
                )
            )
        ]
        sums = [copies.start(two_in.at[1, span], two_land.at[span], at.mate) for span in halves]
        for copy in early + loads:
            copy.start()
        vec_out[...] = jnp.zeros_like(vec_out)
        first_row = at.tensor * rows
        live = ends_of(lengths_ref)[-1]
        mated = []
        for copy in early:
            copy.wait()
        for piece in range(2):
            sums[piece].wait_recv()

            @pl.loop(0, half_rows // 128)
            def _(i):
                start = pl.multiple_of(piece * half_rows + i * 128, 128)
                span = pl.ds(start, 128)
                grad = two_ref[span].astype(F32) + two_land[span].astype(F32)
                normed, inverse = normalize(middle_ref[span])
                ids = first_row + start + lax.broadcasted_iota(jnp.int32, (128, 1), 0)
                final = jnp.where(ids < live, cot_ref[span].astype(F32), 0.0)
                total = final + norm_back(normed, inverse, grad, vec_ref[5:6])
                grad_out[span] = total
                mid[0, span] = total.astype(LOW)
                for row, term in ((4, total), (5, normed * grad), (6, grad), (7, final)):
                    vec_out[row : row + 1] += jnp.sum(term, axis=0, keepdims=True)

            mated.append(copies.start(mid.at[0, halves[piece]], mid.at[1, halves[piece]], at.mate))
        cores = (at.core, 1 - at.core)
        made, stays = [], []
        for i in range(2):
            if i == 1:
                for copy in mated:
                    copy.wait_recv()
            ours = pl.ds(pl.multiple_of((at.chip * 2 + cores[i]) * rows, rows), rows)
            sent_heads[i] = nt(far_ref[...], mid[i]).astype(LOW)
            made.append(copies.start(sent_heads.at[i], heads_out.at[:, ours], at.far))
            stay_heads[i] = nt(own_ref[...], mid[i]).astype(LOW)
            stays.append(
                pltpu.make_async_copy(stay_heads.at[i], heads_out.at[:, ours], local.at[i])
            )
            stays[-1].start()
        grads = mid[...].reshape(2 * rows, width)
        own_out[...] = nn(both_ref[0], grads).astype(LOW)
        far_out[...] = nn(both_ref[1], grads).astype(LOW)
        for copy in loads:
            copy.wait()
        sum_one[...] = (held[0].astype(F32) + held[1].astype(F32)).astype(LOW)
        sum_two[...] = (held[2].astype(F32) + held[3].astype(F32)).astype(LOW)
        for copy in made:
            copy.wait_recv()
        copies.finish()
        for copy in stays:
            copy.wait()

    return comm_call(
        kernel,
        "before_attention_back",
        (
            jax.ShapeDtypeStruct((head_width, 4 * rows), LOW),
            jax.ShapeDtypeStruct((rows, width), F32),
            jax.ShapeDtypeStruct((head_width, width), LOW),
            jax.ShapeDtypeStruct((head_width, width), LOW),
            jax.ShapeDtypeStruct((VEC_ROWS, width), F32),
            jax.ShapeDtypeStruct(pairs[0].shape, LOW),
            jax.ShapeDtypeStruct(pairs[0].shape, LOW),
        ),
        (lengths, two, middle, cotangent, both, out_own, out_far, vec_all, *pairs),
        [SM] + [ANY] * 6 + [VM] + [ANY] * 4,
        (ANY,) + (VM,) * 6,
        6,
        cid,
        scratch=[pltpu.VMEM((rows, width), LOW)]
        + [pltpu.VMEM(x.shape, x.dtype) for x in (middle, cotangent, both, out_own, out_far)]
        + [
            pltpu.VMEM((rows, width), LOW),
            pltpu.VMEM((2, rows, width), LOW),
            pltpu.VMEM((2, head_width, rows), LOW),
            pltpu.VMEM((2, head_width, rows), LOW),
            pltpu.VMEM((4,) + pairs[0].shape, LOW),
        ],
        local=12,
    )


def finish_grads(lengths, arrays, n_dp, cid):
    part_rows = arrays["hidden"].shape[0] // 4
    flat, shapes = [], {}
    for name, array in arrays.items():
        pieces = array if isinstance(array, tuple) else (array,)
        flat += [(name, i, piece) for i, piece in enumerate(pieces)]
        lead = sum(piece.shape[0] for piece in pieces)
        shapes[name] = ((lead,) + pieces[0].shape[1:], pieces[0].dtype)
    kept = [name for name in arrays if name != "out_far"]
    line = n_dp // 2
    shard = arrays["mix"].shape[1]
    rows, width = arrays["hidden"].shape
    group = 4 * rows
    latents = arrays["positions"].shape[0]
    window = rows // latents
    far_end = line - 1
    slots = [(distance, way) for distance in range(far_end, 0, -1) for way in (0, 1)] + [(0, 0)]
    last = len(slots) - 1
    share = width // (n_dp * 4)
    FC, PROJ, MIX, VEC = range(4)

    def kernel(lengths_ref, *refs):
        refs = list(refs)

        def take(number):
            taken = refs[:number]
            del refs[:number]
            return taken

        sources = take(len(flat))
        out_source = sources[[name for name, _, _ in flat].index("out_far")]
        fc_out, proj_out, mix_out, vec_out, tokens_out, thoughts_out, block_out = take(7)
        held = dict(zip(kept, take(len(kept))))
        cross_send, cross_land = [None, None] + take(2), [None, None] + take(2)
        hop_send, hop_land = take(4), take(4)
        (
            part, mate_land, far_send, far_land, last_land, total, vec_mine, vec_land, vec_near,
            plain_sum, column_sum, out_land, tokens_kept, thoughts_kept, block_kept, send, recv,
            local,
        ) = refs
        out = [fc_out, proj_out, mix_out, None]
        at = Place(line)
        tensor, spot, side = at.tensor, at.spot, at.side
        mate_row, far_row, corner_row = at.mate[1], at.far[1], at.corner[1]
        copies = Copies(send, recv)
        loads = {}
        held["out_far"] = out_land
        for k, (name, i, piece) in enumerate(flat):
            if name != "out_far":
                target = held[name]
                if isinstance(arrays[name], tuple):
                    first = 0 if i == 0 else arrays[name][0].shape[0]
                    target = target.at[first : first + piece.shape[0]]
                copy = pltpu.make_async_copy(sources[k], target, local.at[k])
                loads.setdefault(name, Several([])).copies.append(copy)

        def load(*group):
            for name in group:
                loads[name].start()

        load("fc_near", "fc_near_side", "fc_cross", "proj_near", "proj_near_far", "proj_cross")
        load("grad_mixed", "mix")
        greet(at.everyone())

        def block_of(slot):
            distance, way = slots[slot]
            if way == 0:
                return jnp.minimum(spot + distance, far_end), spot + distance < line
            return jnp.maximum(spot - distance, 0), spot - distance >= 0

        crosses, hops = [], []
        for slot in range(len(slots)):
            block, _ = block_of(slot)
            crosses.append(
                {
                    i: copies.plan(cross_send[i].at[block], cross_land[i].at[block], at.across)
                    for i in (MIX, VEC)
                }
            )
            if slot < last:
                hops.append(
                    [
                        copies.plan(
                            hop_send[i].at[slot],
                            hop_land[i].at[slot],
                            (at.up, at.down)[slots[slot][1]],
                        )
                        for i in range(4)
                    ]
                )

        def cross(distance, items):
            for slot in range(len(slots)):
                if slots[slot][0] == distance:
                    for i in items:
                        copies.begin(crosses[slot][i], block_of(slot)[1])

        terms = (
            ("fc_near", "fc_near_side", "fc_cross"),
            ("proj_near", "proj_near_far", "proj_cross"),
        )

        def own_term(i, block):
            if i in (FC, PROJ):
                return sum(held[name][block].astype(F32) for name in terms[i])
            if i == MIX:
                return total[block * 2 + side].astype(F32)
            return vec_near[block * 2 + side]

        def handle(slot, i):
            block, inside = block_of(slot)
            behind = (at.has_down, at.has_up)[slots[slot][1]]
            outer = slot - 2

            def work():
                value = own_term(i, block)
                if i in (MIX, VEC):
                    crosses[slot][i].wait_recv()
                    value = value + cross_land[i][block].astype(F32)
                if outer < 0:
                    hop_send[i][slot] = value.astype(hop_send[i].dtype)
                    return

                @pl.when(behind)
                def _():
                    hops[outer][i].wait_recv()
                    hop_send[i][slot] = (value + hop_land[i][outer].astype(F32)).astype(
                        hop_send[i].dtype
                    )

                @pl.when(jnp.logical_not(behind))
                def _():
                    hop_send[i][slot] = value.astype(hop_send[i].dtype)

            when(inside, work)
            copies.begin(hops[slot][i], inside)

        def handle_all(distance, items):
            for slot in range(last):
                if slots[slot][0] == distance:
                    for i in items:
                        handle(slot, i)

        def close(i, target):
            value = own_term(i, spot)
            if i in (MIX, VEC):
                crosses[last][i].wait_recv()
                value = value + cross_land[i][spot].astype(F32)
            target[...] = value
            for way, behind in enumerate((at.has_down, at.has_up)):

                def add(way=way):
                    hops[last - 2 + way][i].wait_recv()
                    target[...] += hop_land[i][last - 2 + way].astype(F32)

                when(behind, add)

        for name in ("fc_near", "fc_near_side", "fc_cross", "proj_near", "proj_near_far", "proj_cross"):
            loads[name].wait()
        out_made = copies.start(out_source, out_land, at.far)
        handle_all(far_end, (FC, PROJ))
        load("group", "out_own", "vec_all", "vec_part", "bias_own", "bias_far")
        load("last", "hidden", "grad_middle", "middle", "positions")
        loads["grad_mixed"].wait()
        loads["mix"].wait()

        def row_part(index):
            @pl.loop(0, rows // 256)
            def _(i):
                span = pl.ds(pl.multiple_of(i * 256, 256), 256)
                weight = held["mix"][...].reshape(width, width)
                part[index, span] = nt(held["grad_mixed"][index, span], weight).astype(LOW)

        for name in ("group", "out_own", "vec_all", "vec_part", "bias_own", "bias_far"):
            loads[name].wait()

        plain_sum[...] = jnp.zeros_like(plain_sum)
        column_sum[...] = jnp.zeros_like(column_sum)

        @pl.loop(0, group // 256)
        def _(i):
            block, start = i // (rows // 256), (i % (rows // 256)) * 256
            span = pl.ds(pl.multiple_of(start, 256), 256)
            grad = held["grad_mixed"][block, span]
            plain_sum[...] += tn(held["group"][block, span], grad)
            column_sum[...] += jnp.sum(grad.astype(F32), axis=0, keepdims=True)

        row_part(corner_row)
        mate_far = copies.start(part.at[corner_row], mate_land.at[1], at.mate)
        row_part(mate_row)
        mate_own = copies.start(part.at[mate_row], mate_land.at[0], at.mate)
        if far_end > 1:
            handle_all(far_end - 1, (FC, PROJ))
        out_made.wait_recv()
        plain, columns = plain_sum[...], column_sum[...]
        turned = held["vec_all"][...].T
        weight = held["mix"][...].reshape(width, width).astype(F32)
        gain_grad = jnp.sum(plain * weight, axis=1, keepdims=True)
        shift_grad = jnp.sum(weight * columns, axis=1, keepdims=True)
        scaled = plain * turned[:, 0:1] + turned[:, 1:2] * columns
        extras = []
        out_sum = held["out_own"][...].astype(F32) + held["out_far"][...].astype(F32)
        for p in range(3):
            piece = out_sum[p * HD : (p + 1) * HD]
            extras.append(jnp.zeros((width, WIDE - 128), F32))
            extras.append(jnp.concatenate([jnp.zeros((128 - HD, width), F32), piece], axis=0).T)
        scaled = scaled + jnp.concatenate(extras, axis=1)
        for k in range(n_dp):
            total[k] = scaled[k * shard : (k + 1) * shard].astype(LOW)
        for block in range(line):
            cross_send[MIX][block] = total[block * 2 + 1 - side]
        cross(far_end, [MIX])
        cross(far_end - 1, [MIX])
        row_part(far_row)
        mate_far.wait_recv()
        far_made = []

        def send_far(count):
            for i in range(len(far_made), min(len(far_made) + count, 8)):
                span = pl.ds(i * (part_rows // 2), part_rows // 2)
                far_send[span] = (
                    mate_land[1, span].astype(F32) + part[far_row, span].astype(F32)
                ).astype(LOW)
                far_made.append(copies.start(far_send.at[span], far_land.at[span], at.far))

        send_far(2)
        row_part(tensor)
        send_far(1)
        loads["last"].wait()
        last_copy = copies.start(held["last"].at[1], last_land, at.mate)
        vec_mine[...] = held["vec_part"][...]
        norm_grads = jnp.concatenate(
            [gain_grad, shift_grad, jnp.zeros((width, 6), F32)], axis=1
        ).T
        vec_mine[0:2] = norm_grads[0:2]
        vec_mine[8:12] = units_rows_back(held["bias_own"][...], tensor, n_dp) + units_rows_back(
            held["bias_far"][...], far_row, n_dp
        )
        vec_lane = lax.broadcasted_iota(jnp.int32, (1, width), 1)
        in_part = (vec_lane >= tensor * (NH * HD)) & (vec_lane < (tensor + 1) * (NH * HD))
        for row, low in ((2, 0), (3, 2 * WIDE)):
            line_up = jnp.concatenate([columns[:, low : low + WIDE]] + [columns[:, 0:WIDE]] * 2, axis=1)
            placed = jnp.zeros((1, width), F32)
            for t in range(4):
                shifted = pltpu.roll(line_up, t * NH * HD, 1)
                placed = jnp.where(tensor == t, shifted, placed)
            vec_mine[row : row + 1] = jnp.where(in_part, placed, 0.0)
        vec_made = [
            copies.start(vec_mine, vec_land.at[i], device)
            for i, device in enumerate((at.mate, at.far, at.corner))
        ]
        handle_all(far_end, [MIX])
        if far_end >= 2:
            cross(far_end - 2, [MIX])
        send_far(2)
        for distance in range(far_end - 2, 0, -1):
            handle_all(distance, (FC, PROJ))
        send_far(1)
        for copy in vec_made:
            copy.wait_recv()
        send_far(1)
        vec_sum = vec_mine[...] + vec_land[0] + vec_land[1] + vec_land[2]
        for k in range(n_dp):
            vec_near[k] = pltpu.roll(vec_sum, (width - k * shard) % width, 1)[:, 0:128]
        for block in range(line):
            cross_send[VEC][block] = vec_near[block * 2 + 1 - side]
        cross(far_end, [VEC])
        cross(far_end - 1, [VEC])
        send_far(8)
        live = ends_of(lengths_ref)[-1]
        stays = []

        def close_rows(i):
            if i == 0:
                for name in ("hidden", "grad_middle", "middle", "positions"):
                    loads[name].wait()
                last_copy.wait_recv()
                mate_own.wait_recv()
            far_made[2 * i].wait_recv()
            far_made[2 * i + 1].wait_recv()
            span = pl.ds(i * part_rows, part_rows)
            ids = tensor * rows + i * part_rows + lax.broadcasted_iota(
                jnp.int32, (part_rows, 1), 0
            )
            final = (
                held["middle"][span]
                + held["last"][0, span].astype(F32)
                + last_land[span].astype(F32)
                + held["vec_all"][7:8]
            )
            block_kept[span] = jnp.where(ids < live, final, 0.0).astype(LOW)
            grad = (
                part[tensor, span].astype(F32)
                + mate_land[0, span].astype(F32)
                + far_land[span].astype(F32)
            )
            normed, inverse = normalize(held["hidden"][span].astype(F32))
            grad = held["grad_middle"][span] + norm_back(
                normed, inverse, grad, held["vec_all"][0:1]
            )
            for w in range(part_rows // window):
                index = i * (part_rows // window) + w
                here = (
                    lax.broadcasted_iota(jnp.int32, (window, 1), 0)
                    == held["positions"][index : index + 1, 0:1] - index * window
                )
                piece = grad[w * window : (w + 1) * window]
                tokens_kept[pl.ds(index * window, window)] = jnp.where(here, 0.0, piece)
                thoughts_kept[index : index + 1] = jnp.sum(
                    jnp.where(here, piece, 0.0), axis=0, keepdims=True
                )
            moves = [(tokens_kept.at[span], tokens_out.at[span])]
            moves.append((block_kept.at[span], block_out.at[span]))
            if i == 3:
                moves.append((thoughts_kept, thoughts_out))
            for kept_ref, out_ref in moves:
                stays.append(
                    pltpu.make_async_copy(kept_ref, out_ref, local.at[len(flat) + len(stays)])
                )
                stays[-1].start()

        done = 0
        for distance in range(far_end, 0, -1):
            items = (MIX, VEC) if distance < far_end else (VEC,)
            handle_all(distance, items)
            if distance >= 2:
                cross(distance - 2, items)
            if distance <= 3:
                close_rows(done)
                done += 1
        for i in range(done, 4):
            close_rows(i)
        for i in (FC, PROJ, MIX):
            close(i, out[i])
        close(VEC, vec_out)
        copies.finish()
        for copy in stays:
            copy.wait()

    f32 = lambda *shape: jax.ShapeDtypeStruct(shape, F32)
    outputs = (
        f32(shard, width), f32(shard, width), f32(shard, width), f32(VEC_ROWS, 128),
        f32(rows, width), f32(latents, width), jax.ShapeDtypeStruct((rows, width), LOW),
    )
    scratch = [pltpu.VMEM(*shapes[name]) for name in kept]
    for number, wide in ((line, 1), (line, 1), (last, 3), (last, 3)):
        scratch += [pltpu.VMEM((number, shard, width), LOW)] * wide
        scratch.append(pltpu.VMEM((number, VEC_ROWS, 128), F32))
    scratch += [
        pltpu.VMEM((4, rows, width), LOW),
        pltpu.VMEM((2, rows, width), LOW),
        pltpu.VMEM((rows, width), LOW),
        pltpu.VMEM((rows, width), LOW),
        pltpu.VMEM((rows, width), LOW),
        pltpu.VMEM((n_dp, shard, width), LOW),
        pltpu.VMEM((VEC_ROWS, width), F32),
        pltpu.VMEM((3, VEC_ROWS, width), F32),
        pltpu.VMEM((n_dp, VEC_ROWS, 128), F32),
        pltpu.VMEM((width, width), F32),
        pltpu.VMEM((1, width), F32),
        pltpu.VMEM(arrays["out_far"].shape, LOW),
        pltpu.VMEM((rows, width), F32),
        pltpu.VMEM((latents, width), F32),
        pltpu.VMEM((rows, width), LOW),
    ]
    return comm_call(
        kernel,
        "finish_grads",
        outputs,
        (lengths, *(piece for _, _, piece in flat)),
        [SM] + [ANY] * len(flat),
        (VM,) * 4 + (ANY,) * 3,
        (last + 1) * 2 + last * 4 + 1 + 2 + 8 + 3 + 1,
        cid,
        scratch=scratch,
        local=len(flat) + 9,
    )


def unit_kernel(add, line, bias_row, lengths_ref, *refs):
    refs = list(refs)
    rows_ref, grad_own, grad_mate = refs[:3]
    pieces, vec_ref = refs[3:7], refs[7]
    refs = refs[8:]
    if add:
        last_in, two_in = refs[:2]
        refs = refs[2:]
    last_ref, two_ref, fc_near, fc_side, proj_one, proj_two, proj_side, bias_grad_ref = refs[:8]
    fc_all, proj_all, fc_sum, proj_sum = refs[8:]
    step = pl.program_id(0)
    side, tensor = lax.axis_index("dp") % 2, lax.axis_index("tensor")
    live = ends_of(lengths_ref)[-1]

    @pl.when(step == 0)
    def _():
        for full, near, across in ((fc_all, *pieces[:2]), (proj_all, *pieces[2:])):
            for i in range(line):
                full[2 * i + side] = near[i]
                full[2 * i + 1 - side] = across[i]
        fc_sum[...] = jnp.zeros_like(fc_sum)
        proj_sum[...] = jnp.zeros_like(proj_sum)
        bias_grad_ref[...] = jnp.zeros_like(bias_grad_ref)

    count, width = rows_ref.shape
    half = pl.num_programs(0) // 2
    block = jnp.where(step < half, tensor, tensor + 1 - 2 * (tensor % 2))
    first = block * (half * count) + (step % half) * count
    alive = first + lax.broadcasted_iota(jnp.int32, (count, 1), 0) < live
    rows = rows_ref[...]
    grad = jnp.where(step < half, grad_own[...], grad_mate[...])
    grad = jnp.where(alive, grad, jnp.zeros_like(grad))
    fc = fc_all[...].reshape(width, -1)
    proj = proj_all[...].reshape(width, -1)
    inner = nn(rows, fc) + vec_ref[bias_row : bias_row + 1]
    square = inner * inner
    bend = jnp.tanh(GELU_SCALE * inner * (1.0 + GELU_CUBE * square))
    half = 0.5 * (1.0 + bend)
    activated = (inner * half).astype(LOW)
    slope = half + 0.5 * inner * (1.0 - bend * bend) * GELU_SCALE * (1.0 + 3.0 * GELU_CUBE * square)
    grad_inner = (nn(grad, proj) * slope).astype(LOW)
    last = nt(activated, proj)
    two = nt(grad_inner, fc)
    if add:
        last, two = last + last_in[...], two + two_in[...]
    last_ref[...] = last.astype(last_ref.dtype)
    two_ref[...] = two.astype(two_ref.dtype)
    fc_sum[...] += tn(rows, grad_inner)
    proj_sum[...] += tn(grad, activated)
    bias_grad_ref[...] += jnp.sum(grad_inner.astype(F32), axis=0, keepdims=True)

    @pl.when(step == pl.num_programs(0) - 1)
    def _():
        shard = fc_near.shape[1]
        split = line // 2
        near_seats = (
            [fc_near.at[i] for i in range(line)],
            [proj_one.at[i] for i in range(split)] + [proj_two.at[i] for i in range(line - split)],
        )
        for sums, near, across in (
            (fc_sum, near_seats[0], fc_side), (proj_sum, near_seats[1], proj_side),
        ):
            for i in range(line):
                even = sums[2 * i * shard : (2 * i + 1) * shard].astype(LOW)
                odd = sums[(2 * i + 1) * shard : (2 * i + 2) * shard].astype(LOW)
                near[i][...] = jnp.where(side == 0, even, odd)
                across[i] = jnp.where(side == 0, odd, even)


def units_both_ways(lengths, rows, grad, mate_grad, pieces, vec_all, bias_row, before):
    count, width = rows.shape
    line, shard, units = pieces[0].shape
    half = count // ROW_TILE // 2
    leads = (line, line, line // 2, line - line // 2, line)
    tile = pl.BlockSpec((ROW_TILE, width), lambda i: (i, 0))
    fixed = lambda shape: pl.BlockSpec(shape, lambda i: (0,) * len(shape))
    add = before is not None
    return pl.pallas_call(
        functools.partial(unit_kernel, add, line, bias_row),
        grid=(count // ROW_TILE,),
        out_shape=(
            jax.ShapeDtypeStruct((count, width), LOW),
            jax.ShapeDtypeStruct((count, width), LOW),
        )
        + tuple(jax.ShapeDtypeStruct((k, shard, units), LOW) for k in leads)
        + (jax.ShapeDtypeStruct((1, units), F32),        ),
        in_specs=[
            SM,
            tile,
            pl.BlockSpec((ROW_TILE, width), lambda i: (jnp.minimum(i, half - 1), 0)),
            pl.BlockSpec((ROW_TILE, width), lambda i: (jnp.maximum(i - half, 0), 0)),
        ]
        + [fixed((line, shard, units))] * 4
        + [fixed(vec_all.shape)]
        + [tile] * (2 if add else 0),
        out_specs=(tile, tile)
        + tuple(fixed((k, shard, units)) for k in leads)
        + (fixed((1, units)),),
        scratch_shapes=[pltpu.VMEM((2 * line, shard, units), LOW)] * 2
        + [pltpu.VMEM((width, units), F32)] * 2,
        compiler_params=pltpu.CompilerParams(
            dimension_semantics=("arbitrary",), vmem_limit_bytes=VMEM_LIMIT
        ),
        cost_estimate=pl.CostEstimate(
            flops=12 * count * width * units,
            bytes_accessed=24 * count * width,
            transcendentals=count * units,
        ),
        name="units_second" if add else "units_first",
    )(lengths, rows, grad, mate_grad, *pieces, vec_all, *(before or ()))


def split_grads(mix_grad, vec, through, share):
    shard, width = mix_grad.shape
    head_width = NH * HD
    count = len(through)
    pieces_of = []
    for i, array in enumerate(through):
        size = 128 if array.shape[0] % 128 == 0 else array.shape[0]
        pieces_of += [(i, row, size) for row in range(0, array.shape[0], size)]

    def kernel(mix_ref, vec_ref, *refs):
        given, (qkv_out, out_out), refs = refs[:count], refs[count : count + 2], refs[count + 2 :]
        small, passed, held, sems = refs[:8], refs[8 : 8 + count], refs[8 + count : -1], refs[-1]
        ins, outs = [], []
        for i, row, size in pieces_of:
            span = pl.ds(row, size)
            ins.append(
                pltpu.make_async_copy(
                    given[i].at[span], held[i].at[span], sems.at[0, len(ins)]
                )
            )
            outs.append(
                pltpu.make_async_copy(
                    held[i].at[span], passed[i].at[span], sems.at[1, len(outs)]
                )
            )
        for copy in ins:
            copy.start()
        for i in range(len(ins)):
            ins[i].wait()
            outs[i].start()
        tensor = lax.axis_index("tensor")
        turned = mix_ref[...].T
        pieces = []
        for h in range(NH):
            for part in range(3):
                low = part * WIDE + h * HD
                pieces.append(turned[low : low + HD])
        qkv_out[...] = jnp.concatenate(pieces, axis=0).T
        for part in range(3):
            low = part * WIDE + head_width
            out_out[part * HD : (part + 1) * HD] = turned[low : low + HD]
        rows = vec_ref[0:8]
        moved = rows
        for i in range(1, 4):
            moved = jnp.where(tensor == i, pltpu.roll(rows, 128 - i * share, 1), moved)
        for i, row in enumerate((0, 1, 4, 5, 6, 7)):
            small[i][...] = moved[row : row + 1, 0:share]
        small[6][...] = moved[2:4, 0:share]
        small[7][...] = vec_ref[pl.ds(8 + tensor, 1)][:, 0:shard]
        for copy in outs:
            copy.wait()

    f32 = lambda *shape: jax.ShapeDtypeStruct(shape, F32)
    return pl.pallas_call(
        kernel,
        out_shape=(f32(shard, 3 * head_width), f32(head_width, shard))
        + (f32(1, share),) * 6
        + (f32(2, share), f32(1, shard))
        + tuple(jax.ShapeDtypeStruct(x.shape, x.dtype) for x in through),
        in_specs=[VM] * 2 + [ANY] * count,
        out_specs=(VM,) * 10 + (ANY,) * count,
        scratch_shapes=[pltpu.VMEM(x.shape, x.dtype) for x in through]
        + [pltpu.SemaphoreType.DMA((2, len(pieces_of)))],
        compiler_params=pltpu.CompilerParams(vmem_limit_bytes=VMEM_LIMIT),
        name="split_grads",
    )(mix_grad, vec, *through)


def by_tensor(row, step, index):
    moved = row
    for i in range(1, 4):
        moved = jnp.where(index == i, pltpu.roll(row, (i * step) % row.shape[1], 1), moved)
    return moved


def units_row(rows, block, n_dp):
    width = rows.shape[1]
    shard, step = width // n_dp, n_dp // 4
    lane = lax.broadcasted_iota(jnp.int32, (1, width), 1) // shard
    base = by_tensor(rows, width - step * shard, block)
    total = jnp.zeros((1, width), F32)
    for j in range(n_dp):
        moved = pltpu.roll(base[j % 4 : j % 4 + 1], (j - j // 4) * shard, 1)
        total = jnp.where(lane == j, moved, total)
    return total


def units_rows_back(row, block, n_dp):
    width = row.shape[1]
    shard, step = width // n_dp, n_dp // 4
    lane = lax.broadcasted_iota(jnp.int32, (1, width), 1) // shard
    rows = [jnp.zeros((1, width), F32) for _ in range(4)]
    for j in range(n_dp):
        moved = pltpu.roll(row, (width - (j - j // 4) * shard) % width, 1)
        rows[j % 4] = jnp.where(lane == j // 4, moved, rows[j % 4])
    return by_tensor(jnp.concatenate(rows, axis=0), step * shard, block)


def normalize(values):
    center = jnp.mean(values, axis=-1, keepdims=True)
    offset = values - center
    spread = jnp.mean(offset * offset, axis=-1, keepdims=True)
    inverse = lax.rsqrt(spread + EPSILON)
    return offset * inverse, inverse


def norm_back(normed, inverse, grad, gain):
    scaled = grad * gain
    center = jnp.mean(scaled, axis=-1, keepdims=True)
    along = jnp.mean(scaled * normed, axis=-1, keepdims=True)
    return inverse * (scaled - center - normed * along)


def product(equation, left, right):
    return jnp.einsum(equation, left, right, preferred_element_type=F32)


def per_device(
    tokens,
    thoughts,
    positions,
    lengths,
    attn_norm_gain,
    attn_norm_shift,
    qkv_weight,
    qv_bias,
    attn_out_weight,
    attn_out_bias,
    mlp_norm_gain,
    mlp_norm_shift,
    fc_weight,
    fc_bias,
    proj_weight,
    proj_bias,
    cotangent,
):
    n_dp = lax.axis_size("dp")
    n_tensor = lax.axis_size("tensor")
    rows, width = tokens.shape
    slots = rows * n_tensor
    swap_far = [(i, (i + 2) % n_tensor) for i in range(n_tensor)]

    share = width // (n_dp * n_tensor)
    small = [
        attn_norm_gain[None], attn_norm_shift[None], qv_bias, attn_out_bias[None],
        mlp_norm_gain[None], mlp_norm_shift[None], proj_bias[None], fc_bias[None],
    ]
    (
        group_low, mixed, mix_all, fc_near, fc_side, fc_far_near, proj_near, mate_grad, out_own,
        hidden, vec_all, places,
    ) = gather_inputs(
        tokens, thoughts, positions, cotangent, fc_weight, proj_weight.T, qkv_weight,
        attn_out_weight, small, n_dp,
    )
    mixed = mixed.reshape(slots, -1)
    swap_side = [(i, i + 1 - 2 * (i % 2)) for i in range(n_dp)]
    out_far = lax.ppermute(out_own, "tensor", swap_far)
    proj_far_near = lax.ppermute(proj_near, "tensor", swap_far)
    fc_far_side = lax.ppermute(fc_far_near, "dp", swap_side)
    attended, stats = attend(lengths, mixed)
    sent, out_far, proj_far_near, fc_far_side = lax.optimization_barrier(
        (attended, out_far, proj_far_near, fc_far_side)
    )
    proj_far_side = lax.ppermute(proj_far_near, "dp", swap_side)
    both, middle, chip_two = after_attention(
        sent, out_own, out_far, hidden, vec_all, n_dp, 1
    )
    chip_two, proj_far_side, proj_sent = lax.optimization_barrier(
        (chip_two, proj_far_side, proj_near)
    )
    proj_side = lax.ppermute(proj_sent, "dp", swap_side)
    chip_two = chip_two.reshape(2 * rows, width)

    first = units_both_ways(
        lengths, chip_two, cotangent, mate_grad,
        (fc_far_near, fc_far_side, proj_far_near, proj_far_side), vec_all, 13, None,
    )
    far_fc_near, far_fc_side, far_proj_one, far_proj_two, far_proj_side, far_fc_bias = first[2:]
    proj_side_far = lax.ppermute(far_proj_side, "tensor", swap_far)
    fc_far_side_in = lax.ppermute(far_fc_side, "dp", swap_side)
    second = units_both_ways(
        lengths, chip_two, cotangent, mate_grad, (fc_near, fc_side, proj_near, proj_side), vec_all, 12,
        first[:2],
    )
    last_part, grad_two_part, fc_near_grad, fc_side_grad, proj_one, proj_two, proj_side_grad = second[:7]
    far_proj_one, grad_two_part = lax.optimization_barrier((far_proj_one, grad_two_part))
    proj_one_far = lax.ppermute(far_proj_one, "tensor", swap_far)
    fc_near_side_in = lax.ppermute(fc_side_grad, "dp", swap_side)
    grad_heads, grad_middle, grad_out, far_out, vec_part, fc_cross, proj_cross = before_attention_back(
        lengths, grad_two_part.reshape(2, rows, width), middle, cotangent, both, out_own, out_far,
        vec_all, (far_fc_near, fc_far_side_in, proj_side_grad, proj_side_far), n_dp, 2,
    )
    grad_heads, fc_cross, proj_cross, far_proj_two, proj_one_far = lax.optimization_barrier(
        (grad_heads, fc_cross, proj_cross, far_proj_two, proj_one_far)
    )
    fc_cross = lax.ppermute(fc_cross, "tensor", swap_far)
    proj_cross = lax.ppermute(proj_cross, "dp", swap_side)
    proj_two_far = lax.ppermute(far_proj_two, "tensor", swap_far)
    last_low = last_part.reshape(2, rows, width)

    grad_mixed = attend_back(lengths, mixed, attended, stats, grad_heads)
    arrays = {
        "fc_near": fc_near_grad, "fc_near_side": fc_near_side_in, "fc_cross": fc_cross,
        "proj_near": (proj_one, proj_two), "proj_near_far": (proj_one_far, proj_two_far),
        "proj_cross": proj_cross,
        "grad_mixed": grad_mixed.reshape(n_tensor, rows, width), "mix": mix_all,
        "last": last_low, "group": group_low,
        "out_own": grad_out, "out_far": far_out,
        "vec_all": vec_all, "vec_part": vec_part, "bias_own": second[7], "bias_far": far_fc_bias,
        "hidden": hidden, "grad_middle": grad_middle, "middle": middle, "positions": places,
    }
    fc_grad, proj_grad, mix_grad, vec, grad_tokens, grad_thoughts, block_out = finish_grads(
        lengths, arrays, n_dp, 8
    )
    parts = split_grads(
        mix_grad, vec, (fc_grad, proj_grad, grad_tokens, grad_thoughts, block_out), share
    )
    qkv_grad, out_grad = parts[:2]
    gain_one, shift_one, out_bias, gain_two, shift_two, last_bias = [p[0] for p in parts[2:8]]
    query_value, hidden_bias = parts[8], parts[9][0]
    fc_grad, proj_grad, grad_tokens, grad_thoughts, block_out = parts[10:]
    return (
        block_out,
        grad_tokens,
        grad_thoughts,
        gain_one,
        shift_one,
        qkv_grad,
        query_value,
        out_grad,
        out_bias,
        gain_two,
        shift_two,
        fc_grad,
        hidden_bias,
        proj_grad.T,
        last_bias,
    )


def solution(mesh):
    rows = P(("dp", "tensor"), None)
    line = P(("dp", "tensor"))
    in_specs = (
        rows, rows, line, P("dp", None), line, line, P("dp", "tensor"),
        P(None, ("dp", "tensor")), P("tensor", "dp"), line, line, line,
        P("dp", "tensor"), line, P("tensor", "dp"), line, rows,
    )
    out_specs = (
        rows, rows, rows, line, line, P("dp", "tensor"), P(None, ("dp", "tensor")),
        P("tensor", "dp"), line, line, line, P("dp", "tensor"), line, P("tensor", "dp"), line,
    )
    return jax.shard_map(
        per_device, mesh=mesh, in_specs=in_specs, out_specs=out_specs, check_vma=False
    )
```

```python
import functools
import math

import jax
import jax.numpy as jnp
from jax import lax
from jax.experimental import pallas as pl
from jax.experimental.pallas import tpu as pltpu
from jax.sharding import PartitionSpec as P

H = 12
HD = 64
FF = 3072
SEQ_DEV = 3
EPSILON = 1e-05
MASKED = -1e30
NH = 3
SLABS = 2
WIDE = SLABS * 128
BQ = 512
BK = 512
SUMMED = HD + 16
VEC_ROWS = 16
VMEM_LIMIT = 67043328
ROW_TILE = 256
GELU_SCALE = math.sqrt(2.0 / math.pi)
GELU_CUBE = 0.044715
MESH = pl.DeviceIdType.MESH
ANY = pl.BlockSpec(memory_space=pltpu.HBM)
VM = pl.BlockSpec(memory_space=pltpu.VMEM)
SM = pl.BlockSpec(memory_space=pltpu.SMEM)
LOW = jnp.bfloat16
F32 = jnp.float32


def nn(a, b):
    return lax.dot_general(a, b, (((1,), (0,)), ((), ())), preferred_element_type=jnp.float32)


def nt(a, b):
    return lax.dot_general(a, b, (((1,), (1,)), ((), ())), preferred_element_type=jnp.float32)


def tn(a, b):
    return lax.dot_general(a, b, (((0,), (0,)), ((), ())), preferred_element_type=jnp.float32)


def head_rows(slab, head):
    half = slab[(head % 2) * HD : (head % 2 + 1) * HD]
    zero = jnp.zeros_like(half)
    return jnp.concatenate([half, zero] if head % 2 == 0 else [zero, half], axis=0)


def ends_of(lengths_ref):
    ends = [lengths_ref[0, 0]]
    for i in range(1, SEQ_DEV):
        ends.append(ends[-1] + lengths_ref[0, i])
    return ends


def segment_start(ends, slots):
    start = jnp.zeros_like(slots)
    for i in range(SEQ_DEV):
        start = jnp.where(slots >= ends[i], ends[i], start)
    return start


def segment_stop(ends, slot, slots):
    stop = slots
    for i in reversed(range(SEQ_DEV)):
        stop = jnp.where(slot < ends[i], ends[i], stop)
    return stop


def attend_kernel(
    lengths_ref, mixed_in, out_ref, stat_ref, mixed_ref, qt_ref, vt_ref, sems
):
    tokens = mixed_ref.shape[0]
    ends = ends_of(lengths_ref)
    count = (ends[-1] + BQ - 1) // BQ
    half = BQ // 2

    def load(block):
        rows = pl.ds(pl.multiple_of(block * BQ, BQ), BQ)
        return pltpu.make_async_copy(mixed_in.at[rows], mixed_ref.at[rows], sems.at[block])

    for block in range(tokens // BQ):
        load(block).start()
    for h in range(NH):
        vt_ref[h * SUMMED + HD : (h + 1) * SUMMED] = jnp.ones((SUMMED - HD, tokens), jnp.bfloat16)

    def step(rows, keys, columns, queries, first, causal, state):
        size = queries[0].shape[1]
        slots = first + lax.broadcasted_iota(jnp.int32, (1, size), 1)
        start = segment_start(ends, slots)
        key_ids = rows + lax.broadcasted_iota(jnp.int32, (keys, size), 0)
        allowed = key_ids >= start
        if causal:
            allowed = allowed & (key_ids <= slots)
        span = pl.ds(rows, keys)
        result = []
        for h in range(NH):
            peak, acc = state[h]
            low = WIDE + (h // 2) * 128
            scores = nn(mixed_ref[span, low : low + 128], queries[h])
            scores = jnp.where(allowed, scores, MASKED)
            fresh = jnp.maximum(peak, jnp.max(scores, axis=0, keepdims=True))
            weight = jnp.exp(scores - fresh)
            decay = jnp.exp(peak - fresh)
            values = vt_ref[h * SUMMED : (h + 1) * SUMMED, span]
            acc = acc * decay + nn(values, weight.astype(jnp.bfloat16))
            result.append((fresh, acc))
        return tuple(result)

    def query_block(block, carry):
        first = pl.multiple_of(block * BQ, BQ)
        columns = pl.ds(first, BQ)
        load(block).wait()
        for slab in range(SLABS):
            low = slab * 128
            qt_ref[low : low + 128] = (mixed_ref[columns, low : low + 128] * HD ** (-0.5)).T
            turned = mixed_ref[columns, 2 * WIDE + low : 2 * WIDE + low + 128].T
            for h in range(2 * slab, min(2 * slab + 2, NH)):
                piece = turned[(h % 2) * HD : (h % 2 + 1) * HD]
                vt_ref[h * SUMMED : h * SUMMED + HD, columns] = piece
        queries = [head_rows(qt_ref[(h // 2) * 128 : (h // 2 + 1) * 128], h) for h in range(NH)]

        def key_block(key, state):
            return step(pl.multiple_of(key * BK, BK), BK, columns, queries, first, False, state)

        empty = tuple(
            (
                jnp.full((1, BQ), MASKED, jnp.float32),
                jnp.zeros((SUMMED, BQ), jnp.float32),
            )
            for _ in range(NH)
        )
        state = lax.fori_loop(segment_start(ends, first) // BK, block, key_block, empty)
        for side, keys in ((0, half), (1, BQ)):
            piece = slice(side * half, (side + 1) * half)
            final = step(
                first, keys, columns, [q[:, piece] for q in queries], first + side * half, True,
                tuple(tuple(x[:, piece] for x in one) for one in state),
            )
            for h in range(NH):
                peak, acc = final[h]
                total = acc[HD : HD + 1]
                place_here = pl.ds(pl.multiple_of(first + side * half, half), half)
                out_ref[h * HD : (h + 1) * HD, place_here] = (acc[:HD] / total).astype(
                    jnp.bfloat16
                )
                stat_ref[h : h + 1, place_here] = peak + jnp.log(total)
        return carry

    lax.fori_loop(0, count, query_block, 0)

    def padded_block(block, carry):
        load(block).wait()
        columns = pl.ds(pl.multiple_of(block * BQ, BQ), BQ)
        out_ref[:, columns] = jnp.zeros((out_ref.shape[0], BQ), jnp.bfloat16)
        return carry

    lax.fori_loop(count, tokens // BQ, padded_block, 0)


def attend(lengths, mixed):
    tokens = mixed.shape[0]
    vm = pl.BlockSpec(memory_space=pltpu.VMEM)
    return pl.pallas_call(
        attend_kernel,
        out_shape=(
            jax.ShapeDtypeStruct((NH * HD, tokens), jnp.bfloat16),
            jax.ShapeDtypeStruct((8, tokens), jnp.float32),
        ),
        in_specs=[pl.BlockSpec(memory_space=pltpu.SMEM), pl.BlockSpec(memory_space=pltpu.HBM)],
        out_specs=(vm, vm),
        scratch_shapes=[
            pltpu.VMEM(mixed.shape, mixed.dtype),
            pltpu.VMEM((WIDE, BQ), jnp.bfloat16),
            pltpu.VMEM((NH * SUMMED, tokens), jnp.bfloat16),
            pltpu.SemaphoreType.DMA((tokens // BQ,)),
        ],
        compiler_params=pltpu.CompilerParams(vmem_limit_bytes=VMEM_LIMIT),
        cost_estimate=pl.CostEstimate(
            flops=8 * tokens * tokens * NH * HD,
            bytes_accessed=16 * tokens * WIDE,
            transcendentals=tokens * tokens,
        ),
        name="attend",
    )(lengths, mixed)


def attend_back_kernel(
    lengths_ref, mixed_in, out_in, stat_ref, gradt_in,
    gmixed_out, mixed_ref, out_ref, gradt_ref, gmixed_ref, qt_ref, kt_ref, grad_ref, delta_ref,
    dqt_ref, sems, out_sems
):
    tokens = mixed_ref.shape[0]
    blocks = tokens // BQ
    ends = ends_of(lengths_ref)
    count = (ends[-1] + BK - 1) // BK
    half = BQ // 2

    def loads(block):
        rows = pl.ds(pl.multiple_of(block * BQ, BQ), BQ)
        return (
            pltpu.make_async_copy(mixed_in.at[rows], mixed_ref.at[rows], sems.at[0, block]),
            pltpu.make_async_copy(out_in.at[:, rows], out_ref.at[:, rows], sems.at[1, block]),
            pltpu.make_async_copy(gradt_in.at[:, rows], gradt_ref.at[:, rows], sems.at[2, block]),
        )

    def leave(block, part):
        rows = pl.ds(pl.multiple_of(block * BQ, BQ), BQ)
        lanes = pl.ds(0, WIDE) if part == 0 else pl.ds(WIDE, 2 * WIDE)
        return pltpu.make_async_copy(
            gmixed_ref.at[rows, lanes], gmixed_out.at[rows, lanes], out_sems.at[part, block]
        )

    for block in reversed(range(blocks)):
        for copy in loads(block):
            copy.start()
    dqt_ref[...] = jnp.zeros_like(dqt_ref)

    def prepare_block(block):
        rows = pl.ds(pl.multiple_of(block * BQ, BQ), BQ)
        for slab in range(SLABS):
            low = slab * 128
            qt_ref[low : low + 128, rows] = (
                mixed_ref[rows, low : low + 128] * HD ** (-0.5)
            ).T
            kt_ref[low : low + 128, rows] = mixed_ref[rows, WIDE + low : WIDE + low + 128].T
        grad_ref[rows, 0:128] = gradt_ref[0:128, rows].T
        grad_ref[rows, 128:256] = jnp.concatenate(
            [gradt_ref[128:192, rows], jnp.zeros((64, BQ), jnp.bfloat16)], axis=0
        ).T
        for h in range(NH):
            product = gradt_ref[h * HD : (h + 1) * HD, rows].astype(jnp.float32) * out_ref[
                h * HD : (h + 1) * HD, rows
            ].astype(jnp.float32)
            delta_ref[h : h + 1, rows] = jnp.sum(product, axis=0, keepdims=True)

    def terms(base, keys, first, size, causal):
        rows, columns = pl.ds(base, keys), pl.ds(first, size)
        slots = first + lax.broadcasted_iota(jnp.int32, (1, size), 1)
        key_ids = base + lax.broadcasted_iota(jnp.int32, (keys, size), 0)
        allowed = key_ids >= segment_start(ends, slots)
        if causal:
            allowed = allowed & (key_ids <= slots)
        lane = lax.broadcasted_iota(jnp.int32, (size, 128), 1)
        grad_keys, grad_values = [None] * SLABS, [None] * SLABS
        for h in range(NH):
            slab = h // 2
            low, high = slab * 128, slab * 128 + 128
            queries = head_rows(qt_ref[low:high, columns], h)
            scores = nn(mixed_ref[rows, WIDE + low : WIDE + high], queries)
            probs = jnp.where(allowed, jnp.exp(scores - stat_ref[h : h + 1, columns]), 0.0)
            keep = (lane // HD) == (h % 2)
            value = nn(probs.astype(jnp.bfloat16), jnp.where(keep, grad_ref[columns, low:high], 0.0))
            if h == NH - 1 and NH % 2 == 1:
                grad_rows = jnp.concatenate(
                    [gradt_ref[h * HD : (h + 1) * HD, columns], jnp.zeros((HD, size), jnp.bfloat16)],
                    axis=0,
                )
            else:
                grad_rows = head_rows(gradt_ref[low:high, columns], h)
            grad_probs = nn(mixed_ref[rows, 2 * WIDE + low : 2 * WIDE + high], grad_rows)
            grad_scores = (probs * (grad_probs - delta_ref[h : h + 1, columns])).astype(
                jnp.bfloat16
            )
            key_term = nn(grad_scores, jnp.where(keep, mixed_ref[columns, low:high], 0.0))
            grad_values[slab] = value if grad_values[slab] is None else grad_values[slab] + value
            grad_keys[slab] = key_term if grad_keys[slab] is None else grad_keys[slab] + key_term
            dqt_ref[h * HD : (h + 1) * HD, columns] += nn(
                kt_ref[h * HD : (h + 1) * HD, rows], grad_scores
            )
        return grad_keys + grad_values

    def key_block(turn, carry):
        key = count - 1 - turn
        for copy in loads(key):
            copy.wait()
        prepare_block(key)
        base = pl.multiple_of(key * BK, BK)
        rows = pl.ds(base, BK)
        upper = terms(base, half, base, BQ, True)
        lower = terms(pl.multiple_of(base + half, half), half, pl.multiple_of(base + half, half), half, True)
        state = tuple(jnp.concatenate([a, b], axis=0) for a, b in zip(upper, lower))

        def query_block(block, state):
            fresh = terms(base, BK, pl.multiple_of(block * BQ, BQ), BQ, False)
            return tuple(a + b for a, b in zip(state, fresh))

        stop = jnp.minimum(segment_stop(ends, base + BK - 1, tokens), ends[-1])
        state = lax.fori_loop(key + 1, (stop - 1) // BQ + 1, query_block, state)
        for slab in range(SLABS):
            low = slab * 128
            gmixed_ref[rows, WIDE + low : WIDE + low + 128] = (
                state[slab] * HD ** (-0.5)
            ).astype(jnp.bfloat16)
            gmixed_ref[rows, 2 * WIDE + low : 2 * WIDE + low + 128] = state[SLABS + slab].astype(
                jnp.bfloat16
            )
        leave(key, 1).start()
        return carry

    def padded_block(key, carry):
        for copy in loads(key):
            copy.wait()
        rows = pl.ds(pl.multiple_of(key * BK, BK), BK)
        gmixed_ref[rows, WIDE:] = jnp.zeros((BK, 2 * WIDE), jnp.bfloat16)
        leave(key, 1).start()
        return carry

    lax.fori_loop(count, blocks, padded_block, 0)
    lax.fori_loop(0, count, key_block, 0)
    for block in range(blocks):
        rows = pl.ds(block * BQ, BQ)
        for slab in range(SLABS):
            low = slab * 128
            gmixed_ref[rows, low : low + 128] = (
                (dqt_ref[low : low + 128, rows] * HD ** (-0.5)).T.astype(jnp.bfloat16)
            )
        leave(block, 0).start()
    for block in range(blocks):
        leave(block, 0).wait()
        leave(block, 1).wait()


def attend_back(lengths, mixed, out, stat, gradt):
    tokens = mixed.shape[0]
    vm = pl.BlockSpec(memory_space=pltpu.VMEM)
    hbm = pl.BlockSpec(memory_space=pltpu.HBM)
    return pl.pallas_call(
        attend_back_kernel,
        out_shape=jax.ShapeDtypeStruct((tokens, 3 * WIDE), jnp.bfloat16),
        in_specs=[pl.BlockSpec(memory_space=pltpu.SMEM), hbm, hbm, vm, hbm],
        out_specs=hbm,
        scratch_shapes=[
            pltpu.VMEM(mixed.shape, jnp.bfloat16),
            pltpu.VMEM(out.shape, jnp.bfloat16),
            pltpu.VMEM(gradt.shape, jnp.bfloat16),
            pltpu.VMEM(mixed.shape, jnp.bfloat16),
            pltpu.VMEM((WIDE, tokens), jnp.bfloat16),
            pltpu.VMEM((WIDE, tokens), jnp.bfloat16),
            pltpu.VMEM((tokens, WIDE), jnp.bfloat16),
            pltpu.VMEM((8, tokens), jnp.float32),
            pltpu.VMEM((WIDE, tokens), jnp.float32),
            pltpu.SemaphoreType.DMA((3, tokens // BQ)),
            pltpu.SemaphoreType.DMA((2, tokens // BQ)),
        ],
        compiler_params=pltpu.CompilerParams(vmem_limit_bytes=VMEM_LIMIT),
        cost_estimate=pl.CostEstimate(
            flops=20 * tokens * tokens * NH * HD,
            bytes_accessed=32 * tokens * WIDE,
            transcendentals=tokens * tokens,
        ),
        name="attend_back",
    )(lengths, mixed, out, stat, gradt)


class Copies:
    def __init__(self, send, recv):
        self.send, self.recv, self.made, self.started = send, recv, 0, []

    def plan(self, source, target, device):
        index = self.made
        self.made += 1
        return pltpu.make_async_remote_copy(
            src_ref=source,
            dst_ref=target,
            send_sem=self.send.at[index],
            recv_sem=self.recv.at[index],
            device_id=device,
            device_id_type=MESH,
        )

    def begin(self, copy, condition=None):
        self.started.append((copy, condition))
        when(condition, copy.start)

    def start(self, source, target, device):
        copy = self.plan(source, target, device)
        self.begin(copy)
        return copy

    def finish(self):
        for copy, condition in self.started:
            when(condition, copy.wait_send)


class Several:
    def __init__(self, copies):
        self.copies = copies

    def start(self):
        for copy in self.copies:
            copy.start()

    def wait(self):
        for copy in self.copies:
            copy.wait()


def when(condition, action):
    if condition is None:
        action()
    else:
        pl.when(condition)(action)


def greet(devices):
    barrier = pltpu.get_barrier_semaphore()
    for device, condition in devices:
        when(
            condition,
            lambda device=device: pl.semaphore_signal(
                barrier, inc=1, device_id=device, device_id_type=MESH
            ),
        )
    present = [1 if condition is None else condition.astype(jnp.int32) for _, condition in devices]
    pl.semaphore_wait(barrier, sum(present))


class Place:
    def __init__(self, line):
        self.dp = dp = lax.axis_index("dp")
        self.tensor = tensor = lax.axis_index("tensor")
        self.spot, self.side = spot, side = dp // 2, dp % 2
        self.chip, self.core = tensor // 2, tensor % 2
        self.has_up, self.has_down = spot + 1 < line, spot > 0
        self.up = (jnp.minimum(spot + 1, line - 1) * 2 + side, tensor)
        self.down = (jnp.maximum(spot - 1, 0) * 2 + side, tensor)
        self.across = (spot * 2 + 1 - side, tensor)
        self.mate = (dp, tensor + 1 - 2 * (tensor % 2))
        self.far = (dp, (tensor + 2) % 4)
        self.corner = (dp, 3 - tensor)

    def everyone(self):
        return [
            (self.mate, None), (self.far, None), (self.corner, None), (self.across, None),
            (self.up, self.has_up), (self.down, self.has_down),
        ]


def comm_call(kernel, name, outputs, inputs, in_specs, out_specs, copies, cid, scratch=(), local=1, limit=VMEM_LIMIT):
    return pl.pallas_call(
        kernel,
        out_shape=outputs,
        in_specs=in_specs,
        out_specs=out_specs,
        scratch_shapes=list(scratch)
        + [
            pltpu.SemaphoreType.DMA((copies,)),
            pltpu.SemaphoreType.DMA((copies,)),
            pltpu.SemaphoreType.DMA((local,)),
        ],
        compiler_params=pltpu.CompilerParams(
            collective_id=cid, has_side_effects=True, vmem_limit_bytes=limit
        ),
        name=name,
    )(*inputs)


def one_hot(rows, columns, shift, limit):
    lane = lax.broadcasted_iota(jnp.int32, (rows, columns), 0)
    spot = lax.broadcasted_iota(jnp.int32, (rows, columns), 1)
    return ((spot == lane + shift) & (lane < limit)).astype(LOW)


def gather_inputs(tokens, thoughts, positions, cotangent, fc, proj, qkv, out, vectors, n_dp):
    line = n_dp // 2
    hops = line - 1
    rows, width = tokens.shape
    latents = thoughts.shape[0]
    window = rows // latents
    shard = fc.shape[0]
    half_rows = rows // 2
    share = width // (n_dp * 4)

    def kernel(
        pos_ref, tokens_in, thoughts_in, cot_ref, fc_in, proj_in, qkv_in, out_in, *refs
    ):
        given = (fc_in, tokens_in, thoughts_in, proj_in, qkv_in, out_in) + refs[: len(vectors)]
        (
            normed_out, mixed_out, mix_out, fc_near, fc_side, fc_far, proj_near, cot_out, out_out,
            out_far_out,
            hidden_out, vec_out, pos_out,
            hidden_ref, mix_ref, vec_ref, tile,
            land, mix_land, tiles, tile_land, normed, mixed, out_turned,
            *held, arrive, send, recv, local,
        ) = refs[len(vectors) :]
        arrivals = [
            pltpu.make_async_copy(given[i], held[i], arrive.at[i]) for i in range(len(given))
        ]
        for copy in arrivals:
            copy.start()
        fc_ref, tokens_ref, thoughts_ref, proj_ref, qkv_ref, out_ref = held[:6]
        vec_refs = held[6:]
        at = Place(line)
        dp, tensor, spot, side = at.dp, at.tensor, at.spot, at.side
        mate_row, far_row, corner_row = at.mate[1], at.far[1], at.corner[1]
        greet(at.everyone())
        copies = Copies(send, recv)
        MIX, FC, PROJ, VEC = range(4)
        own = [mix_ref, fc_ref, proj_ref, tiles.at[dp]]

        def seat(item, position):
            if item == MIX:
                return mix_land.at[position * 2 + side]
            if item == FC:
                return fc_near.at[position]
            if item == PROJ:
                return proj_near.at[position]
            return tiles.at[position * 2 + side]

        def plan(item, hop):
            above, below = jnp.maximum(spot - hop, 0), jnp.minimum(spot + hop, line - 1)
            came_up = jnp.maximum(spot - 1 - hop, 0)
            came_down = jnp.minimum(spot + 1 + hop, line - 1)
            made = {
                "up": copies.plan(
                    own[item] if hop == 0 else seat(item, above), seat(item, above), at.up
                ),
                "down": copies.plan(
                    own[item] if hop == 0 else seat(item, below), seat(item, below), at.down
                ),
                "onward": [],
            }
            for position in (came_up, came_down):
                onward = []
                if item in (MIX, VEC):
                    onward.append(copies.plan(seat(item, position), seat(item, position), at.across))
                if item == FC:
                    onward.append(copies.plan(fc_near.at[position], fc_side.at[position], at.across))
                    onward.append(copies.plan(fc_near.at[position], fc_far.at[position], at.far))
                made["onward"].append(onward)
            return made

        plans = [[plan(item, hop) for hop in range(hops)] for item in range(4)]

        def launch(item):
            copies.begin(plans[item][0]["up"], at.has_up)
            copies.begin(plans[item][0]["down"], at.has_down)

        def handle(item, hop):
            made = plans[item][hop]
            for way, key, comes, goes in (
                (0, "up", spot - 1 - hop >= 0, at.has_up),
                (1, "down", spot + 1 + hop < line, at.has_down),
            ):
                when(comes, made[key].wait_recv)
                if hop + 1 < hops:
                    copies.begin(plans[item][hop + 1][key], comes & goes)
                for copy in made["onward"][way]:
                    copies.begin(copy, comes)

        def settle(item):
            for hop in range(hops):
                for way, comes in ((0, spot - 1 - hop >= 0), (1, spot + 1 + hop < line)):
                    for copy in plans[item][hop]["onward"][way]:
                        when(comes, copy.wait_recv)

        stays = []

        def stay(source, target):
            copy = pltpu.make_async_copy(source, target, local.at[len(stays)])
            copy.start()
            stays.append(copy)
            return copy

        parts = [pl.ds(0, half_rows), pl.ds(half_rows, half_rows)]
        arrivals[0].wait()
        launch(FC)
        fc_sides = [copies.start(fc_ref, fc_side.at[spot], at.across)]
        cot_made = copies.start(cot_ref, cot_out, at.mate)
        for copy in arrivals[6:]:
            copy.wait()
        tile[...] = jnp.zeros_like(tile)
        row = 0
        for ref in vec_refs:
            count, size = ref.shape
            tile[row : row + count, 0:size] = ref[...].astype(F32)
            row += count
        vec_ref[...] = tile[...].astype(LOW)
        vec_made = [
            copies.start(vec_ref, tile_land.at[i], device)
            for i, device in enumerate((at.mate, at.far, at.corner))
        ]
        arrivals[1].wait()
        arrivals[2].wait()
        pos_row = lax.broadcasted_iota(jnp.int32, (latents, 128), 0)
        places = jnp.zeros((latents, 128), jnp.int32)
        for w in range(latents):
            places = jnp.where(pos_row == w, pos_ref[w], places)
            span = pl.ds(w * window, window)
            here = lax.broadcasted_iota(jnp.int32, (window, 1), 0) == pos_ref[w] - w * window
            hidden_ref[span] = jnp.where(
                here, thoughts_ref[w : w + 1].astype(F32), tokens_ref[span].astype(F32)
            ).astype(LOW)
        pos_out[...] = places
        far_made = [
            copies.start(hidden_ref.at[part], land.at[2, part], at.far) for part in parts
        ]
        mate_made = copies.start(hidden_ref, land.at[1], at.mate)
        fc_sides.append(copies.start(fc_ref, fc_far.at[spot], at.far))
        for copy in arrivals[3:6]:
            copy.wait()
        turned = qkv_ref[...].astype(F32).T
        extra = out_ref[...].astype(F32)
        pieces = []
        for p in range(3):
            for h in range(NH):
                low = (h * 3 + p) * HD
                pieces.append(turned[low : low + HD])
            pieces.append(extra[p * HD : (p + 1) * HD])
        mix_ref[...] = jnp.concatenate(pieces, axis=0).T.astype(LOW)
        launch(MIX)
        mix_side = copies.start(mix_ref, mix_land.at[dp], at.across)
        stay(hidden_ref, hidden_out)
        stay(fc_ref, fc_near.at[spot])
        stay(proj_ref, proj_near.at[spot])
        mix_land[dp] = mix_ref[...]
        for copy in vec_made:
            copy.wait_recv()
        merged = jnp.zeros((VEC_ROWS, 128), F32)
        bias_rows = jnp.zeros((VEC_ROWS, 128), F32)
        row_ids = lax.broadcasted_iota(jnp.int32, (VEC_ROWS, 128), 0)
        for i, index in enumerate((tensor, mate_row, far_row, corner_row)):
            tile = vec_ref[...] if i == 0 else tile_land[i - 1]
            merged += nn(tile, one_hot(128, 128, index * share, share))
            bias_rows = jnp.where(row_ids == 8 + index, tile[8:9].astype(F32), bias_rows)
        tiles[dp] = jnp.where(row_ids < 8, merged, bias_rows).astype(LOW)
        launch(VEC)
        vec_side = copies.start(tiles.at[dp], tiles.at[dp], at.across)

        def norm_rows(source, index):
            @pl.loop(0, rows // 128)
            def _(i):
                span = pl.ds(pl.multiple_of(i * 128, 128), 128)
                normed[index, span] = normalize(source[span].astype(F32))[0].astype(LOW)

            stay(normed.at[index], normed_out.at[index])

        def relay(i):
            far_made[i].wait_recv()
            return copies.start(land.at[2, parts[i]], land.at[3, parts[i]], at.mate)

        def mix_rows(index):
            @pl.loop(0, rows // 256)
            def _(i):
                span = pl.ds(pl.multiple_of(i * 256, 256), 256)
                turned = normed[index, span].astype(F32) * whole[0:1] + whole[1:2]
                weight = mix_land[...].reshape(width, width)
                mixed[index, span] = (nn(turned.astype(LOW), weight) + bias).astype(LOW)

            stay(mixed.at[index], mixed_out.at[index])

        norm_rows(hidden_ref, tensor)
        relayed = []
        for step in range(hops + 2):
            for item, hop in ((MIX, step), (VEC, step), (FC, step - 1), (PROJ, step - 2)):
                if 0 <= hop < hops:
                    handle(item, hop)
            if step == 0:
                launch(PROJ)
                mate_made.wait_recv()
                norm_rows(land.at[1], mate_row)
                relayed.append(relay(0))
            if step == 1:
                relayed.append(relay(1))
                norm_rows(land.at[2], far_row)
            if step == hops:
                mix_side.wait_recv()
                vec_side.wait_recv()
                settle(MIX)
                settle(VEC)
                whole = jnp.zeros((VEC_ROWS, width), F32)
                for i in range(n_dp):
                    whole += nn(tiles[i], one_hot(128, width, i * shard, shard))
                vec_out[...] = whole
                for i, block in enumerate((tensor, far_row)):
                    vec_out[12 + i : 13 + i] = units_row(whole[8:12], block, n_dp)
                lane = lax.broadcasted_iota(jnp.int32, (width, WIDE), 0)
                column = lax.broadcasted_iota(jnp.int32, (width, WIDE), 1)
                pick = (lane == column + tensor * (NH * HD)) & (column < NH * HD)
                picked = nn(whole.astype(LOW), pick.astype(LOW))
                bias = jnp.concatenate(
                    [picked[2:3], jnp.zeros((1, WIDE), F32), picked[3:4]], axis=1
                )
                mix_rows(tensor)
                mix_rows(mate_row)
                mix_rows(far_row)
                for copy in relayed:
                    copy.wait_recv()
                norm_rows(land.at[3], corner_row)
                mix_rows(corner_row)
                stay(mix_land, mix_out)
                weight = mix_land[...].reshape(width, width)
                for part in range(3):
                    low = part * WIDE + WIDE - 128
                    turned = weight[:, low : low + 128].T
                    out_turned[part * HD : (part + 1) * HD] = turned[128 - HD :]
                stay(out_turned, out_out)
                out_made = copies.start(out_turned, out_far_out, at.far)
        settle(FC)
        out_made.wait_recv()
        for copy in fc_sides:
            copy.wait_recv()
        cot_made.wait_recv()
        copies.finish()
        for copy in stays:
            copy.wait()

    low = lambda *shape: jax.ShapeDtypeStruct(shape, LOW)
    outputs = (
        low(4, rows, width), low(4, rows, width), low(n_dp, shard, width),
        low(line, shard, width), low(line, shard, width), low(line, shard, width),
        low(line, shard, width), low(rows, width), low(NH * HD, width), low(NH * HD, width),
        low(rows, width),
        jax.ShapeDtypeStruct((VEC_ROWS, width), F32),
        jax.ShapeDtypeStruct((latents, 128), jnp.int32),
    )
    scratch = [
        pltpu.VMEM((rows, width), LOW),
        pltpu.VMEM((shard, 3 * WIDE), LOW),
        pltpu.VMEM((VEC_ROWS, 128), LOW),
        pltpu.VMEM((VEC_ROWS, 128), F32),
        pltpu.VMEM((4, rows, width), LOW),
        pltpu.VMEM((n_dp, shard, width), LOW),
        pltpu.VMEM((n_dp, VEC_ROWS, 128), LOW),
        pltpu.VMEM((3, VEC_ROWS, 128), LOW),
        pltpu.VMEM((4, rows, width), LOW),
        pltpu.VMEM((4, rows, width), LOW),
        pltpu.VMEM((NH * HD, width), LOW),
    ]
    given = (fc, tokens, thoughts, proj, qkv, out, *vectors)
    scratch += [pltpu.VMEM(x.shape, x.dtype) for x in given]
    scratch.append(pltpu.SemaphoreType.DMA((len(given),)))
    return comm_call(
        kernel,
        "gather_inputs",
        outputs,
        (positions, tokens, thoughts, cotangent, fc, proj, qkv, out, *vectors),
        [SM] + [ANY] * (7 + len(vectors)),
        (ANY,) * 11 + (VM, VM),
        3 + 2 + 1 + 2 + 2 + 1 + 2 + 1 + hops * (2 * 4 + 2 * 4),
        0,
        scratch=scratch,
        local=3 + 8 + 2,
    )


def after_attention(attended, out_own, out_far, hidden, vec_all, n_dp, cid):
    head_width, slots = attended.shape
    rows, width = hidden.shape
    half_rows = rows // 2

    def kernel(
        heads_in, own_in, far_in, hidden_in, vec_ref,
        both_out, middle_out, two_out,
        heads_ref, own_ref, far_ref, hidden_ref,
        land, part, part_low, part_land, two, send, recv, local,
    ):
        loads = [
            pltpu.make_async_copy(source, target, local.at[5 + i])
            for i, (source, target) in enumerate(
                (
                    (heads_in, heads_ref), (own_in, own_ref), (far_in, far_ref),
                    (hidden_in, hidden_ref),
                )
            )
        ]
        for copy in loads:
            copy.start()
        at = Place(n_dp // 2)
        greet([(at.far, None), (at.mate, None)])
        copies = Copies(send, recv)
        cores = (at.core, 1 - at.core)
        made = [None, None]
        for i in (1, 0):
            theirs = pl.multiple_of(((1 - at.chip) * 2 + cores[i]) * rows, rows)
            made[i] = copies.start(heads_in.at[:, pl.ds(theirs, rows)], land.at[i], at.far)
        stays = []

        def stay(source, target):
            stays.append(pltpu.make_async_copy(source, target, local.at[len(stays)]))
            stays[-1].start()

        spans = []
        for copy in loads:
            copy.wait()
        for i in range(2):
            ours = pl.multiple_of((at.chip * 2 + cores[i]) * rows, rows)
            spans.append(pl.ds(ours, rows))
            stay(heads_ref.at[:, spans[i]], both_out.at[0, :, i * rows : (i + 1) * rows])
            part[i] = tn(heads_ref[:, spans[i]], own_ref[...])
        sums = None
        for i in (1, 0):
            made[i].wait_recv()
            stay(land.at[i], both_out.at[1, :, i * rows : (i + 1) * rows])
            part[i] += tn(land[i], far_ref[...])
            if i == 1:
                part_low[...] = part[1].astype(LOW)
                sums = copies.start(part_low, part_land, at.mate)
        sums.wait_recv()
        mated = []
        for piece in range(2):

            @pl.loop(0, half_rows // 128)
            def _(i):
                span = pl.ds(pl.multiple_of(piece * half_rows + i * 128, 128), 128)
                middle = (
                    hidden_ref[span].astype(F32)
                    + part[0, span]
                    + part_land[span].astype(F32)
                    + vec_ref[4:5]
                )
                middle_out[span] = middle
                two[span] = (normalize(middle)[0] * vec_ref[5:6] + vec_ref[6:7]).astype(LOW)

            span = pl.ds(piece * half_rows, half_rows)
            mated.append(copies.start(two.at[span], two_out.at[1, span], at.mate))
        stay(two, two_out.at[0])
        for copy in mated:
            copy.wait_recv()
        copies.finish()
        for copy in stays:
            copy.wait()

    return comm_call(
        kernel,
        "after_attention",
        (
            jax.ShapeDtypeStruct((2, head_width, 2 * rows), LOW),
            jax.ShapeDtypeStruct((rows, width), F32),
            jax.ShapeDtypeStruct((2, rows, width), LOW),
        ),
        (attended, out_own, out_far, hidden, vec_all),
        [ANY] * 4 + [VM],
        (ANY, VM, ANY),
        5,
        cid,
        scratch=[pltpu.VMEM(x.shape, x.dtype) for x in (attended, out_own, out_far, hidden)]
        + [
            pltpu.VMEM((2, head_width, rows), LOW),
            pltpu.VMEM((2, rows, width), F32),
            pltpu.VMEM((rows, width), LOW),
            pltpu.VMEM((rows, width), LOW),
            pltpu.VMEM((rows, width), LOW),
        ],
        local=9,
    )


def before_attention_back(
    lengths, two, middle, cotangent, both, out_own, out_far, vec_all, pairs, n_dp, cid
):
    _, rows, width = two.shape
    head_width = out_own.shape[0]
    half_rows = rows // 2

    def kernel(
        lengths_ref, two_in, middle_in, cot_in, both_in, own_in, far_in, vec_ref,
        one_a, one_b, two_a, two_b,
        heads_out, grad_out, own_out, far_out, vec_out, sum_one, sum_two,
        two_ref, middle_ref, cot_ref, both_ref, own_ref, far_ref,
        two_land, mid, stay_heads, sent_heads, held, send, recv, local,
    ):
        at = Place(n_dp // 2)
        greet([(at.far, None), (at.mate, None)])
        copies = Copies(send, recv)
        halves = [pl.ds(0, half_rows), pl.ds(half_rows, half_rows)]
        loads = [
            pltpu.make_async_copy(ref, held.at[i], local.at[2 + i])
            for i, ref in enumerate((one_a, one_b, two_a, two_b))
        ]
        early = [
            pltpu.make_async_copy(source, target, local.at[6 + i])
            for i, (source, target) in enumerate(
                (
                    (two_in.at[0], two_ref), (middle_in, middle_ref), (cot_in, cot_ref),
                    (far_in, far_ref), (own_in, own_ref), (both_in, both_ref),
                )
            )
        ]
        sums = [copies.start(two_in.at[1, span], two_land.at[span], at.mate) for span in halves]
        for copy in early + loads:
            copy.start()
        vec_out[...] = jnp.zeros_like(vec_out)
        first_row = at.tensor * rows
        live = ends_of(lengths_ref)[-1]
        mated = []
        for copy in early:
            copy.wait()
        for piece in range(2):
            sums[piece].wait_recv()

            @pl.loop(0, half_rows // 128)
            def _(i):
                start = pl.multiple_of(piece * half_rows + i * 128, 128)
                span = pl.ds(start, 128)
                grad = two_ref[span].astype(F32) + two_land[span].astype(F32)
                normed, inverse = normalize(middle_ref[span])
                ids = first_row + start + lax.broadcasted_iota(jnp.int32, (128, 1), 0)
                final = jnp.where(ids < live, cot_ref[span].astype(F32), 0.0)
                total = final + norm_back(normed, inverse, grad, vec_ref[5:6])
                grad_out[span] = total
                mid[0, span] = total.astype(LOW)
                for row, term in ((4, total), (5, normed * grad), (6, grad), (7, final)):
                    vec_out[row : row + 1] += jnp.sum(term, axis=0, keepdims=True)

            mated.append(copies.start(mid.at[0, halves[piece]], mid.at[1, halves[piece]], at.mate))
        cores = (at.core, 1 - at.core)
        made, stays = [], []
        for i in range(2):
            if i == 1:
                for copy in mated:
                    copy.wait_recv()
            ours = pl.ds(pl.multiple_of((at.chip * 2 + cores[i]) * rows, rows), rows)
            sent_heads[i] = nt(far_ref[...], mid[i]).astype(LOW)
            made.append(copies.start(sent_heads.at[i], heads_out.at[:, ours], at.far))
            stay_heads[i] = nt(own_ref[...], mid[i]).astype(LOW)
            stays.append(
                pltpu.make_async_copy(stay_heads.at[i], heads_out.at[:, ours], local.at[i])
            )
            stays[-1].start()
        grads = mid[...].reshape(2 * rows, width)
        own_out[...] = nn(both_ref[0], grads).astype(LOW)
        far_out[...] = nn(both_ref[1], grads).astype(LOW)
        for copy in loads:
            copy.wait()
        sum_one[...] = (held[0].astype(F32) + held[1].astype(F32)).astype(LOW)
        sum_two[...] = (held[2].astype(F32) + held[3].astype(F32)).astype(LOW)
        for copy in made:
            copy.wait_recv()
        copies.finish()
        for copy in stays:
            copy.wait()

    return comm_call(
        kernel,
        "before_attention_back",
        (
            jax.ShapeDtypeStruct((head_width, 4 * rows), LOW),
            jax.ShapeDtypeStruct((rows, width), F32),
            jax.ShapeDtypeStruct((head_width, width), LOW),
            jax.ShapeDtypeStruct((head_width, width), LOW),
            jax.ShapeDtypeStruct((VEC_ROWS, width), F32),
            jax.ShapeDtypeStruct(pairs[0].shape, LOW),
            jax.ShapeDtypeStruct(pairs[0].shape, LOW),
        ),
        (lengths, two, middle, cotangent, both, out_own, out_far, vec_all, *pairs),
        [SM] + [ANY] * 6 + [VM] + [ANY] * 4,
        (ANY,) + (VM,) * 6,
        6,
        cid,
        scratch=[pltpu.VMEM((rows, width), LOW)]
        + [pltpu.VMEM(x.shape, x.dtype) for x in (middle, cotangent, both, out_own, out_far)]
        + [
            pltpu.VMEM((rows, width), LOW),
            pltpu.VMEM((2, rows, width), LOW),
            pltpu.VMEM((2, head_width, rows), LOW),
            pltpu.VMEM((2, head_width, rows), LOW),
            pltpu.VMEM((4,) + pairs[0].shape, LOW),
        ],
        local=12,
    )


def finish_grads(lengths, arrays, n_dp, cid):
    part_rows = arrays["hidden"].shape[0] // 4
    flat, shapes = [], {}
    for name, array in arrays.items():
        pieces = array if isinstance(array, tuple) else (array,)
        flat += [(name, i, piece) for i, piece in enumerate(pieces)]
        lead = sum(piece.shape[0] for piece in pieces)
        shapes[name] = ((lead,) + pieces[0].shape[1:], pieces[0].dtype)
    kept = [name for name in arrays if name != "out_far"]
    line = n_dp // 2
    shard = arrays["mix"].shape[1]
    rows, width = arrays["hidden"].shape
    group = 4 * rows
    latents = arrays["positions"].shape[0]
    window = rows // latents
    far_end = line - 1
    slots = [(distance, way) for distance in range(far_end, 0, -1) for way in (0, 1)] + [(0, 0)]
    last = len(slots) - 1
    share = width // (n_dp * 4)
    FC, PROJ, MIX, VEC = range(4)

    def kernel(lengths_ref, *refs):
        refs = list(refs)

        def take(number):
            taken = refs[:number]
            del refs[:number]
            return taken

        sources = take(len(flat))
        out_source = sources[[name for name, _, _ in flat].index("out_far")]
        fc_out, proj_out, mix_out, vec_out, tokens_out, thoughts_out, block_out = take(7)
        held = dict(zip(kept, take(len(kept))))
        cross_send, cross_land = [None, None] + take(2), [None, None] + take(2)
        hop_send, hop_land = take(4), take(4)
        (
            part, mate_land, far_send, far_land, last_land, total, vec_mine, vec_land, vec_near,
            plain_sum, column_sum, out_land, tokens_kept, thoughts_kept, block_kept, send, recv,
            local,
        ) = refs
        out = [fc_out, proj_out, mix_out, None]
        at = Place(line)
        tensor, spot, side = at.tensor, at.spot, at.side
        mate_row, far_row, corner_row = at.mate[1], at.far[1], at.corner[1]
        copies = Copies(send, recv)
        loads = {}
        held["out_far"] = out_land
        for k, (name, i, piece) in enumerate(flat):
            if name != "out_far":
                target = held[name]
                if isinstance(arrays[name], tuple):
                    first = 0 if i == 0 else arrays[name][0].shape[0]
                    target = target.at[first : first + piece.shape[0]]
                copy = pltpu.make_async_copy(sources[k], target, local.at[k])
                loads.setdefault(name, Several([])).copies.append(copy)

        def load(*group):
            for name in group:
                loads[name].start()

        load("fc_near", "fc_near_side", "fc_cross", "proj_near", "proj_near_far", "proj_cross")
        load("grad_mixed", "mix")
        greet(at.everyone())

        def block_of(slot):
            distance, way = slots[slot]
            if way == 0:
                return jnp.minimum(spot + distance, far_end), spot + distance < line
            return jnp.maximum(spot - distance, 0), spot - distance >= 0

        crosses, hops = [], []
        for slot in range(len(slots)):
            block, _ = block_of(slot)
            crosses.append(
                {
                    i: copies.plan(cross_send[i].at[block], cross_land[i].at[block], at.across)
                    for i in (MIX, VEC)
                }
            )
            if slot < last:
                hops.append(
                    [
                        copies.plan(
                            hop_send[i].at[slot],
                            hop_land[i].at[slot],
                            (at.up, at.down)[slots[slot][1]],
                        )
                        for i in range(4)
                    ]
                )

        def cross(distance, items):
            for slot in range(len(slots)):
                if slots[slot][0] == distance:
                    for i in items:
                        copies.begin(crosses[slot][i], block_of(slot)[1])

        terms = (
            ("fc_near", "fc_near_side", "fc_cross"),
            ("proj_near", "proj_near_far", "proj_cross"),
        )

        def own_term(i, block):
            if i in (FC, PROJ):
                return sum(held[name][block].astype(F32) for name in terms[i])
            if i == MIX:
                return total[block * 2 + side].astype(F32)
            return vec_near[block * 2 + side]

        def handle(slot, i):
            block, inside = block_of(slot)
            behind = (at.has_down, at.has_up)[slots[slot][1]]
            outer = slot - 2

            def work():
                value = own_term(i, block)
                if i in (MIX, VEC):
                    crosses[slot][i].wait_recv()
                    value = value + cross_land[i][block].astype(F32)
                if outer < 0:
                    hop_send[i][slot] = value.astype(hop_send[i].dtype)
                    return

                @pl.when(behind)
                def _():
                    hops[outer][i].wait_recv()
                    hop_send[i][slot] = (value + hop_land[i][outer].astype(F32)).astype(
                        hop_send[i].dtype
                    )

                @pl.when(jnp.logical_not(behind))
                def _():
                    hop_send[i][slot] = value.astype(hop_send[i].dtype)

            when(inside, work)
            copies.begin(hops[slot][i], inside)

        def handle_all(distance, items):
            for slot in range(last):
                if slots[slot][0] == distance:
                    for i in items:
                        handle(slot, i)

        def close(i, target):
            value = own_term(i, spot)
            if i in (MIX, VEC):
                crosses[last][i].wait_recv()
                value = value + cross_land[i][spot].astype(F32)
            target[...] = value
            for way, behind in enumerate((at.has_down, at.has_up)):

                def add(way=way):
                    hops[last - 2 + way][i].wait_recv()
                    target[...] += hop_land[i][last - 2 + way].astype(F32)

                when(behind, add)

        for name in ("fc_near", "fc_near_side", "fc_cross", "proj_near", "proj_near_far", "proj_cross"):
            loads[name].wait()
        out_made = copies.start(out_source, out_land, at.far)
        handle_all(far_end, (FC, PROJ))
        load("group", "out_own", "vec_all", "vec_part", "bias_own", "bias_far")
        load("last", "hidden", "grad_middle", "middle", "positions")
        loads["grad_mixed"].wait()
        loads["mix"].wait()

        def row_part(index):
            @pl.loop(0, rows // 256)
            def _(i):
                span = pl.ds(pl.multiple_of(i * 256, 256), 256)
                weight = held["mix"][...].reshape(width, width)
                part[index, span] = nt(held["grad_mixed"][index, span], weight).astype(LOW)

        for name in ("group", "out_own", "vec_all", "vec_part", "bias_own", "bias_far"):
            loads[name].wait()

        plain_sum[...] = jnp.zeros_like(plain_sum)
        column_sum[...] = jnp.zeros_like(column_sum)

        @pl.loop(0, group // 256)
        def _(i):
            block, start = i // (rows // 256), (i % (rows // 256)) * 256
            span = pl.ds(pl.multiple_of(start, 256), 256)
            grad = held["grad_mixed"][block, span]
            plain_sum[...] += tn(held["group"][block, span], grad)
            column_sum[...] += jnp.sum(grad.astype(F32), axis=0, keepdims=True)

        row_part(corner_row)
        mate_far = copies.start(part.at[corner_row], mate_land.at[1], at.mate)
        row_part(mate_row)
        mate_own = copies.start(part.at[mate_row], mate_land.at[0], at.mate)
        if far_end > 1:
            handle_all(far_end - 1, (FC, PROJ))
        out_made.wait_recv()
        plain, columns = plain_sum[...], column_sum[...]
        turned = held["vec_all"][...].T
        weight = held["mix"][...].reshape(width, width).astype(F32)
        gain_grad = jnp.sum(plain * weight, axis=1, keepdims=True)
        shift_grad = jnp.sum(weight * columns, axis=1, keepdims=True)
        scaled = plain * turned[:, 0:1] + turned[:, 1:2] * columns
        extras = []
        out_sum = held["out_own"][...].astype(F32) + held["out_far"][...].astype(F32)
        for p in range(3):
            piece = out_sum[p * HD : (p + 1) * HD]
            extras.append(jnp.zeros((width, WIDE - 128), F32))
            extras.append(jnp.concatenate([jnp.zeros((128 - HD, width), F32), piece], axis=0).T)
        scaled = scaled + jnp.concatenate(extras, axis=1)
        for k in range(n_dp):
            total[k] = scaled[k * shard : (k + 1) * shard].astype(LOW)
        for block in range(line):
            cross_send[MIX][block] = total[block * 2 + 1 - side]
        cross(far_end, [MIX])
        cross(far_end - 1, [MIX])
        row_part(far_row)
        mate_far.wait_recv()
        far_made = []

        def send_far(count):
            for i in range(len(far_made), min(len(far_made) + count, 8)):
                span = pl.ds(i * (part_rows // 2), part_rows // 2)
                far_send[span] = (
                    mate_land[1, span].astype(F32) + part[far_row, span].astype(F32)
                ).astype(LOW)
                far_made.append(copies.start(far_send.at[span], far_land.at[span], at.far))

        send_far(2)
        row_part(tensor)
        send_far(1)
        loads["last"].wait()
        last_copy = copies.start(held["last"].at[1], last_land, at.mate)
        vec_mine[...] = held["vec_part"][...]
        norm_grads = jnp.concatenate(
            [gain_grad, shift_grad, jnp.zeros((width, 6), F32)], axis=1
        ).T
        vec_mine[0:2] = norm_grads[0:2]
        vec_mine[8:12] = units_rows_back(held["bias_own"][...], tensor, n_dp) + units_rows_back(
            held["bias_far"][...], far_row, n_dp
        )
        vec_lane = lax.broadcasted_iota(jnp.int32, (1, width), 1)
        in_part = (vec_lane >= tensor * (NH * HD)) & (vec_lane < (tensor + 1) * (NH * HD))
        for row, low in ((2, 0), (3, 2 * WIDE)):
            line_up = jnp.concatenate([columns[:, low : low + WIDE]] + [columns[:, 0:WIDE]] * 2, axis=1)
            placed = jnp.zeros((1, width), F32)
            for t in range(4):
                shifted = pltpu.roll(line_up, t * NH * HD, 1)
                placed = jnp.where(tensor == t, shifted, placed)
            vec_mine[row : row + 1] = jnp.where(in_part, placed, 0.0)
        vec_made = [
            copies.start(vec_mine, vec_land.at[i], device)
            for i, device in enumerate((at.mate, at.far, at.corner))
        ]
        handle_all(far_end, [MIX])
        if far_end >= 2:
            cross(far_end - 2, [MIX])
        send_far(2)
        for distance in range(far_end - 2, 0, -1):
            handle_all(distance, (FC, PROJ))
        send_far(1)
        for copy in vec_made:
            copy.wait_recv()
        send_far(1)
        vec_sum = vec_mine[...] + vec_land[0] + vec_land[1] + vec_land[2]
        for k in range(n_dp):
            vec_near[k] = pltpu.roll(vec_sum, (width - k * shard) % width, 1)[:, 0:128]
        for block in range(line):
            cross_send[VEC][block] = vec_near[block * 2 + 1 - side]
        cross(far_end, [VEC])
        cross(far_end - 1, [VEC])
        send_far(8)
        live = ends_of(lengths_ref)[-1]
        stays = []

        def close_rows(i):
            if i == 0:
                for name in ("hidden", "grad_middle", "middle", "positions"):
                    loads[name].wait()
                last_copy.wait_recv()
                mate_own.wait_recv()
            far_made[2 * i].wait_recv()
            far_made[2 * i + 1].wait_recv()
            span = pl.ds(i * part_rows, part_rows)
            ids = tensor * rows + i * part_rows + lax.broadcasted_iota(
                jnp.int32, (part_rows, 1), 0
            )
            final = (
                held["middle"][span]
                + held["last"][0, span].astype(F32)
                + last_land[span].astype(F32)
                + held["vec_all"][7:8]
            )
            block_kept[span] = jnp.where(ids < live, final, 0.0).astype(LOW)
            grad = (
                part[tensor, span].astype(F32)
                + mate_land[0, span].astype(F32)
                + far_land[span].astype(F32)
            )
            normed, inverse = normalize(held["hidden"][span].astype(F32))
            grad = held["grad_middle"][span] + norm_back(
                normed, inverse, grad, held["vec_all"][0:1]
            )
            for w in range(part_rows // window):
                index = i * (part_rows // window) + w
                here = (
                    lax.broadcasted_iota(jnp.int32, (window, 1), 0)
                    == held["positions"][index : index + 1, 0:1] - index * window
                )
                piece = grad[w * window : (w + 1) * window]
                tokens_kept[pl.ds(index * window, window)] = jnp.where(here, 0.0, piece)
                thoughts_kept[index : index + 1] = jnp.sum(
                    jnp.where(here, piece, 0.0), axis=0, keepdims=True
                )
            moves = [(tokens_kept.at[span], tokens_out.at[span])]
            moves.append((block_kept.at[span], block_out.at[span]))
            if i == 3:
                moves.append((thoughts_kept, thoughts_out))
            for kept_ref, out_ref in moves:
                stays.append(
                    pltpu.make_async_copy(kept_ref, out_ref, local.at[len(flat) + len(stays)])
                )
                stays[-1].start()

        done = 0
        for distance in range(far_end, 0, -1):
            items = (MIX, VEC) if distance < far_end else (VEC,)
            handle_all(distance, items)
            if distance >= 2:
                cross(distance - 2, items)
            if distance <= 3:
                close_rows(done)
                done += 1
        for i in range(done, 4):
            close_rows(i)
        for i in (FC, PROJ, MIX):
            close(i, out[i])
        close(VEC, vec_out)
        copies.finish()
        for copy in stays:
            copy.wait()

    f32 = lambda *shape: jax.ShapeDtypeStruct(shape, F32)
    outputs = (
        f32(shard, width), f32(shard, width), f32(shard, width), f32(VEC_ROWS, 128),
        f32(rows, width), f32(latents, width), jax.ShapeDtypeStruct((rows, width), LOW),
    )
    scratch = [pltpu.VMEM(*shapes[name]) for name in kept]
    for number, wide in ((line, 1), (line, 1), (last, 3), (last, 3)):
        scratch += [pltpu.VMEM((number, shard, width), LOW)] * wide
        scratch.append(pltpu.VMEM((number, VEC_ROWS, 128), F32))
    scratch += [
        pltpu.VMEM((4, rows, width), LOW),
        pltpu.VMEM((2, rows, width), LOW),
        pltpu.VMEM((rows, width), LOW),
        pltpu.VMEM((rows, width), LOW),
        pltpu.VMEM((rows, width), LOW),
        pltpu.VMEM((n_dp, shard, width), LOW),
        pltpu.VMEM((VEC_ROWS, width), F32),
        pltpu.VMEM((3, VEC_ROWS, width), F32),
        pltpu.VMEM((n_dp, VEC_ROWS, 128), F32),
        pltpu.VMEM((width, width), F32),
        pltpu.VMEM((1, width), F32),
        pltpu.VMEM(arrays["out_far"].shape, LOW),
        pltpu.VMEM((rows, width), F32),
        pltpu.VMEM((latents, width), F32),
        pltpu.VMEM((rows, width), LOW),
    ]
    return comm_call(
        kernel,
        "finish_grads",
        outputs,
        (lengths, *(piece for _, _, piece in flat)),
        [SM] + [ANY] * len(flat),
        (VM,) * 4 + (ANY,) * 3,
        (last + 1) * 2 + last * 4 + 1 + 2 + 8 + 3 + 1,
        cid,
        scratch=scratch,
        local=len(flat) + 9,
    )


def unit_kernel(add, line, bias_row, lengths_ref, *refs):
    refs = list(refs)
    rows_ref, grad_own, grad_mate = refs[:3]
    pieces, vec_ref = refs[3:7], refs[7]
    refs = refs[8:]
    if add:
        last_in, two_in = refs[:2]
        refs = refs[2:]
    last_ref, two_ref, fc_near, fc_side, proj_one, proj_two, proj_side, bias_grad_ref = refs[:8]
    fc_all, proj_all, fc_sum, proj_sum = refs[8:]
    step = pl.program_id(0)
    side, tensor = lax.axis_index("dp") % 2, lax.axis_index("tensor")
    live = ends_of(lengths_ref)[-1]

    @pl.when(step == 0)
    def _():
        for full, near, across in ((fc_all, *pieces[:2]), (proj_all, *pieces[2:])):
            for i in range(line):
                full[2 * i + side] = near[i]
                full[2 * i + 1 - side] = across[i]
        fc_sum[...] = jnp.zeros_like(fc_sum)
        proj_sum[...] = jnp.zeros_like(proj_sum)
        bias_grad_ref[...] = jnp.zeros_like(bias_grad_ref)

    count, width = rows_ref.shape
    half = pl.num_programs(0) // 2
    block = jnp.where(step < half, tensor, tensor + 1 - 2 * (tensor % 2))
    first = block * (half * count) + (step % half) * count
    alive = first + lax.broadcasted_iota(jnp.int32, (count, 1), 0) < live
    rows = rows_ref[...]
    grad = jnp.where(step < half, grad_own[...], grad_mate[...])
    grad = jnp.where(alive, grad, jnp.zeros_like(grad))
    fc = fc_all[...].reshape(width, -1)
    proj = proj_all[...].reshape(width, -1)
    inner = nn(rows, fc) + vec_ref[bias_row : bias_row + 1]
    square = inner * inner
    bend = jnp.tanh(GELU_SCALE * inner * (1.0 + GELU_CUBE * square))
    half = 0.5 * (1.0 + bend)
    activated = (inner * half).astype(LOW)
    slope = half + 0.5 * inner * (1.0 - bend * bend) * GELU_SCALE * (1.0 + 3.0 * GELU_CUBE * square)
    grad_inner = (nn(grad, proj) * slope).astype(LOW)
    last = nt(activated, proj)
    two = nt(grad_inner, fc)
    if add:
        last, two = last + last_in[...], two + two_in[...]
    last_ref[...] = last.astype(last_ref.dtype)
    two_ref[...] = two.astype(two_ref.dtype)
    fc_sum[...] += tn(rows, grad_inner)
    proj_sum[...] += tn(grad, activated)
    bias_grad_ref[...] += jnp.sum(grad_inner.astype(F32), axis=0, keepdims=True)

    @pl.when(step == pl.num_programs(0) - 1)
    def _():
        shard = fc_near.shape[1]
        split = line // 2
        near_seats = (
            [fc_near.at[i] for i in range(line)],
            [proj_one.at[i] for i in range(split)] + [proj_two.at[i] for i in range(line - split)],
        )
        for sums, near, across in (
            (fc_sum, near_seats[0], fc_side), (proj_sum, near_seats[1], proj_side),
        ):
            for i in range(line):
                even = sums[2 * i * shard : (2 * i + 1) * shard].astype(LOW)
                odd = sums[(2 * i + 1) * shard : (2 * i + 2) * shard].astype(LOW)
                near[i][...] = jnp.where(side == 0, even, odd)
                across[i] = jnp.where(side == 0, odd, even)


def units_both_ways(lengths, rows, grad, mate_grad, pieces, vec_all, bias_row, before):
    count, width = rows.shape
    line, shard, units = pieces[0].shape
    half = count // ROW_TILE // 2
    leads = (line, line, line // 2, line - line // 2, line)
    tile = pl.BlockSpec((ROW_TILE, width), lambda i: (i, 0))
    fixed = lambda shape: pl.BlockSpec(shape, lambda i: (0,) * len(shape))
    add = before is not None
    kind = LOW if add else F32
    return pl.pallas_call(
        functools.partial(unit_kernel, add, line, bias_row),
        grid=(count // ROW_TILE,),
        out_shape=(
            jax.ShapeDtypeStruct((count, width), kind),
            jax.ShapeDtypeStruct((count, width), kind),
        )
        + tuple(jax.ShapeDtypeStruct((k, shard, units), LOW) for k in leads)
        + (jax.ShapeDtypeStruct((1, units), F32),        ),
        in_specs=[
            SM,
            tile,
            pl.BlockSpec((ROW_TILE, width), lambda i: (jnp.minimum(i, half - 1), 0)),
            pl.BlockSpec((ROW_TILE, width), lambda i: (jnp.maximum(i - half, 0), 0)),
        ]
        + [fixed((line, shard, units))] * 4
        + [fixed(vec_all.shape)]
        + [tile] * (2 if add else 0),
        out_specs=(tile, tile)
        + tuple(fixed((k, shard, units)) for k in leads)
        + (fixed((1, units)),),
        scratch_shapes=[pltpu.VMEM((2 * line, shard, units), LOW)] * 2
        + [pltpu.VMEM((width, units), F32)] * 2,
        compiler_params=pltpu.CompilerParams(
            dimension_semantics=("arbitrary",), vmem_limit_bytes=VMEM_LIMIT
        ),
        cost_estimate=pl.CostEstimate(
            flops=12 * count * width * units,
            bytes_accessed=24 * count * width,
            transcendentals=count * units,
        ),
        name="units_second" if add else "units_first",
    )(lengths, rows, grad, mate_grad, *pieces, vec_all, *(before or ()))


def split_grads(mix_grad, vec, through, share):
    shard, width = mix_grad.shape
    head_width = NH * HD
    count = len(through)
    pieces_of = []
    for i, array in enumerate(through):
        size = 128 if array.shape[0] % 128 == 0 else array.shape[0]
        pieces_of += [(i, row, size) for row in range(0, array.shape[0], size)]

    def kernel(mix_ref, vec_ref, *refs):
        given, (qkv_out, out_out), refs = refs[:count], refs[count : count + 2], refs[count + 2 :]
        small, passed, held, sems = refs[:8], refs[8 : 8 + count], refs[8 + count : -1], refs[-1]
        ins, outs = [], []
        for i, row, size in pieces_of:
            span = pl.ds(row, size)
            ins.append(
                pltpu.make_async_copy(
                    given[i].at[span], held[i].at[span], sems.at[0, len(ins)]
                )
            )
            outs.append(
                pltpu.make_async_copy(
                    held[i].at[span], passed[i].at[span], sems.at[1, len(outs)]
                )
            )
        for copy in ins:
            copy.start()
        for i in range(len(ins)):
            ins[i].wait()
            outs[i].start()
        tensor = lax.axis_index("tensor")
        turned = mix_ref[...].T
        pieces = []
        for h in range(NH):
            for part in range(3):
                low = part * WIDE + h * HD
                pieces.append(turned[low : low + HD])
        qkv_out[...] = jnp.concatenate(pieces, axis=0).T
        for part in range(3):
            low = part * WIDE + head_width
            out_out[part * HD : (part + 1) * HD] = turned[low : low + HD]
        rows = vec_ref[0:8]
        moved = rows
        for i in range(1, 4):
            moved = jnp.where(tensor == i, pltpu.roll(rows, 128 - i * share, 1), moved)
        for i, row in enumerate((0, 1, 4, 5, 6, 7)):
            small[i][...] = moved[row : row + 1, 0:share]
        small[6][...] = moved[2:4, 0:share]
        small[7][...] = vec_ref[pl.ds(8 + tensor, 1)][:, 0:shard]
        for copy in outs:
            copy.wait()

    f32 = lambda *shape: jax.ShapeDtypeStruct(shape, F32)
    return pl.pallas_call(
        kernel,
        out_shape=(f32(shard, 3 * head_width), f32(head_width, shard))
        + (f32(1, share),) * 6
        + (f32(2, share), f32(1, shard))
        + tuple(jax.ShapeDtypeStruct(x.shape, x.dtype) for x in through),
        in_specs=[VM] * 2 + [ANY] * count,
        out_specs=(VM,) * 10 + (ANY,) * count,
        scratch_shapes=[pltpu.VMEM(x.shape, x.dtype) for x in through]
        + [pltpu.SemaphoreType.DMA((2, len(pieces_of)))],
        compiler_params=pltpu.CompilerParams(vmem_limit_bytes=VMEM_LIMIT),
        name="split_grads",
    )(mix_grad, vec, *through)


def by_tensor(row, step, index):
    moved = row
    for i in range(1, 4):
        moved = jnp.where(index == i, pltpu.roll(row, (i * step) % row.shape[1], 1), moved)
    return moved


def units_row(rows, block, n_dp):
    width = rows.shape[1]
    shard, step = width // n_dp, n_dp // 4
    lane = lax.broadcasted_iota(jnp.int32, (1, width), 1) // shard
    base = by_tensor(rows, width - step * shard, block)
    total = jnp.zeros((1, width), F32)
    for j in range(n_dp):
        moved = pltpu.roll(base[j % 4 : j % 4 + 1], (j - j // 4) * shard, 1)
        total = jnp.where(lane == j, moved, total)
    return total


def units_rows_back(row, block, n_dp):
    width = row.shape[1]
    shard, step = width // n_dp, n_dp // 4
    lane = lax.broadcasted_iota(jnp.int32, (1, width), 1) // shard
    rows = [jnp.zeros((1, width), F32) for _ in range(4)]
    for j in range(n_dp):
        moved = pltpu.roll(row, (width - (j - j // 4) * shard) % width, 1)
        rows[j % 4] = jnp.where(lane == j // 4, moved, rows[j % 4])
    return by_tensor(jnp.concatenate(rows, axis=0), step * shard, block)


def normalize(values):
    center = jnp.mean(values, axis=-1, keepdims=True)
    offset = values - center
    spread = jnp.mean(offset * offset, axis=-1, keepdims=True)
    inverse = lax.rsqrt(spread + EPSILON)
    return offset * inverse, inverse


def norm_back(normed, inverse, grad, gain):
    scaled = grad * gain
    center = jnp.mean(scaled, axis=-1, keepdims=True)
    along = jnp.mean(scaled * normed, axis=-1, keepdims=True)
    return inverse * (scaled - center - normed * along)


def product(equation, left, right):
    return jnp.einsum(equation, left, right, preferred_element_type=F32)


def per_device(
    tokens,
    thoughts,
    positions,
    lengths,
    attn_norm_gain,
    attn_norm_shift,
    qkv_weight,
    qv_bias,
    attn_out_weight,
    attn_out_bias,
    mlp_norm_gain,
    mlp_norm_shift,
    fc_weight,
    fc_bias,
    proj_weight,
    proj_bias,
    cotangent,
):
    n_dp = lax.axis_size("dp")
    n_tensor = lax.axis_size("tensor")
    rows, width = tokens.shape
    slots = rows * n_tensor
    swap_far = [(i, (i + 2) % n_tensor) for i in range(n_tensor)]

    share = width // (n_dp * n_tensor)
    small = [
        attn_norm_gain[None], attn_norm_shift[None], qv_bias, attn_out_bias[None],
        mlp_norm_gain[None], mlp_norm_shift[None], proj_bias[None], fc_bias[None],
    ]
    (
        group_low, mixed, mix_all, fc_near, fc_side, fc_far_near, proj_near, mate_grad, out_own,
        out_far, hidden, vec_all, places,
    ) = gather_inputs(
        tokens, thoughts, positions, cotangent, fc_weight, proj_weight.T, qkv_weight,
        attn_out_weight, small, n_dp,
    )
    mixed = mixed.reshape(slots, -1)
    swap_side = [(i, i + 1 - 2 * (i % 2)) for i in range(n_dp)]
    proj_far_near = lax.ppermute(proj_near, "tensor", swap_far)
    fc_far_side = lax.ppermute(fc_far_near, "dp", swap_side)
    attended, stats = attend(lengths, mixed)
    sent, proj_far_near, fc_far_side = lax.optimization_barrier(
        (attended, proj_far_near, fc_far_side)
    )
    proj_far_side = lax.ppermute(proj_far_near, "dp", swap_side)
    both, middle, chip_two = after_attention(
        sent, out_own, out_far, hidden, vec_all, n_dp, 1
    )
    chip_two, proj_far_side, proj_sent = lax.optimization_barrier(
        (chip_two, proj_far_side, proj_near)
    )
    proj_side = lax.ppermute(proj_sent, "dp", swap_side)
    chip_two = chip_two.reshape(2 * rows, width)

    first = units_both_ways(
        lengths, chip_two, cotangent, mate_grad,
        (fc_far_near, fc_far_side, proj_far_near, proj_far_side), vec_all, 13, None,
    )
    far_fc_near, far_fc_side, far_proj_one, far_proj_two, far_proj_side, far_fc_bias = first[2:]
    proj_side_far = lax.ppermute(far_proj_side, "tensor", swap_far)
    fc_far_side_in = lax.ppermute(far_fc_side, "dp", swap_side)
    second = units_both_ways(
        lengths, chip_two, cotangent, mate_grad, (fc_near, fc_side, proj_near, proj_side), vec_all, 12,
        first[:2],
    )
    last_part, grad_two_part, fc_near_grad, fc_side_grad, proj_one, proj_two, proj_side_grad = second[:7]
    far_proj_one, grad_two_part = lax.optimization_barrier((far_proj_one, grad_two_part))
    proj_one_far = lax.ppermute(far_proj_one, "tensor", swap_far)
    fc_near_side_in = lax.ppermute(fc_side_grad, "dp", swap_side)
    grad_heads, grad_middle, grad_out, far_out, vec_part, fc_cross, proj_cross = before_attention_back(
        lengths, grad_two_part.reshape(2, rows, width), middle, cotangent, both, out_own, out_far,
        vec_all, (far_fc_near, fc_far_side_in, proj_side_grad, proj_side_far), n_dp, 2,
    )
    grad_heads, fc_cross, proj_cross, far_proj_two, proj_one_far = lax.optimization_barrier(
        (grad_heads, fc_cross, proj_cross, far_proj_two, proj_one_far)
    )
    fc_cross = lax.ppermute(fc_cross, "tensor", swap_far)
    proj_cross = lax.ppermute(proj_cross, "dp", swap_side)
    proj_two_far = lax.ppermute(far_proj_two, "tensor", swap_far)
    last_low = last_part.reshape(2, rows, width)

    grad_mixed = attend_back(lengths, mixed, attended, stats, grad_heads)
    arrays = {
        "fc_near": fc_near_grad, "fc_near_side": fc_near_side_in, "fc_cross": fc_cross,
        "proj_near": (proj_one, proj_two), "proj_near_far": (proj_one_far, proj_two_far),
        "proj_cross": proj_cross,
        "grad_mixed": grad_mixed.reshape(n_tensor, rows, width), "mix": mix_all,
        "last": last_low, "group": group_low,
        "out_own": grad_out, "out_far": far_out,
        "vec_all": vec_all, "vec_part": vec_part, "bias_own": second[7], "bias_far": far_fc_bias,
        "hidden": hidden, "grad_middle": grad_middle, "middle": middle, "positions": places,
    }
    fc_grad, proj_grad, mix_grad, vec, grad_tokens, grad_thoughts, block_out = finish_grads(
        lengths, arrays, n_dp, 8
    )
    parts = split_grads(
        mix_grad, vec, (fc_grad, proj_grad, grad_tokens, grad_thoughts, block_out), share
    )
    qkv_grad, out_grad = parts[:2]
    gain_one, shift_one, out_bias, gain_two, shift_two, last_bias = [p[0] for p in parts[2:8]]
    query_value, hidden_bias = parts[8], parts[9][0]
    fc_grad, proj_grad, grad_tokens, grad_thoughts, block_out = parts[10:]
    return (
        block_out,
        grad_tokens,
        grad_thoughts,
        gain_one,
        shift_one,
        qkv_grad,
        query_value,
        out_grad,
        out_bias,
        gain_two,
        shift_two,
        fc_grad,
        hidden_bias,
        proj_grad.T,
        last_bias,
    )


def solution(mesh):
    rows = P(("dp", "tensor"), None)
    line = P(("dp", "tensor"))
    in_specs = (
        rows, rows, line, P("dp", None), line, line, P("dp", "tensor"),
        P(None, ("dp", "tensor")), P("tensor", "dp"), line, line, line,
        P("dp", "tensor"), line, P("tensor", "dp"), line, rows,
    )
    out_specs = (
        rows, rows, rows, line, line, P("dp", "tensor"), P(None, ("dp", "tensor")),
        P("tensor", "dp"), line, line, line, P("dp", "tensor"), line, P("tensor", "dp"), line,
    )
    return jax.shard_map(
        per_device, mesh=mesh, in_specs=in_specs, out_specs=out_specs, check_vma=False
    )
```
